32 devices in a mesh: dp: 8 (over y, x, core), mp: 4 (over z).
Axes of the slice: x: 2, y: 2, z: 4, core: 2. Of those that a mesh axis runs over, the one named last changes fastest.
Arguments:
- clean_patches: float32 [32, 12, 1024], P('dp'), may hold values from -1 to 1
- noise_patches: float32 [32, 12, 1024], P('dp'), may hold values from -6 to 6
- timesteps: int32 [32], P('dp'), may hold values from 0 to 999
- present_mask: int32 [32, 1024], P('dp'), may hold values from 0 to 1, as said below
- copy_widein: bfloat16 [1024, 10, 1024], P(None, None, 'mp'), may hold values from -0.1875 to 0.1875
- copy_narrowin: bfloat16 [512, 3, 1024], P(None, None, 'mp'), may hold values from -0.25 to 0.25
- copy_wideout: bfloat16 [6, 1024, 1024], P(None, 'mp')
- copy_narrowout: bfloat16 [1024, 512], P('mp'), may hold values from -1.5 to 1.5
- copy_latents: bfloat16 [128, 1024], replicated, may hold values from -3 to 3
- copy_gains: bfloat16 [11, 512], replicated, may hold values from 0.5 to 1.5
- copy_pixels: bfloat16 [2, 12, 512], replicated
- master_widein: float32 [1024, 10, 1024], P('dp', None, 'mp'), may hold values from -0.1875 to 0.1875
- first_widein: float32 [1024, 10, 1024], P('dp', None, 'mp'), may hold values from -1.8e-05 to 1.8e-05
- second_widein: float32 [1024, 10, 1024], P('dp', None, 'mp'), may hold values from 4.5e-12 to 7.2e-11
- master_narrowin: float32 [512, 3, 1024], P('dp', None, 'mp'), may hold values from -0.25 to 0.25
- first_narrowin: float32 [512, 3, 1024], P('dp', None, 'mp'), may hold values from -1.8e-05 to 1.8e-05
- second_narrowin: float32 [512, 3, 1024], P('dp', None, 'mp'), may hold values from 4.5e-12 to 7.2e-11
- master_wideout: float32 [6, 1024, 1024], P(None, 'mp', 'dp')
- first_wideout: float32 [6, 1024, 1024], P(None, 'mp', 'dp'), may hold values from -1.8e-05 to 1.8e-05
- second_wideout: float32 [6, 1024, 1024], P(None, 'mp', 'dp'), may hold values from 4.5e-12 to 7.2e-11
- master_narrowout: float32 [1024, 512], P('mp', 'dp'), may hold values from -1.5 to 1.5
- first_narrowout: float32 [1024, 512], P('mp', 'dp'), may hold values from -1.8e-05 to 1.8e-05
- second_narrowout: float32 [1024, 512], P('mp', 'dp'), may hold values from 4.5e-12 to 7.2e-11
- master_latents: float32 [128, 1024], P(None, 'dp'), may hold values from -3 to 3
- first_latents: float32 [128, 1024], P(None, 'dp'), may hold values from -1.7883438e-06 to 1.7883438e-06
- second_latents: float32 [128, 1024], P(None, 'dp'), may hold values from 8.8838144e-14 to 3.5535257e-13
- master_gains: float32 [11, 512], P(None, 'dp'), may hold values from 0.5 to 1.5
- first_gains: float32 [11, 512], P(None, 'dp'), may hold values from -6e-05 to 6e-05
- second_gains: float32 [11, 512], P(None, 'dp'), may hold values from 5e-11 to 8e-10
- master_pixels: float32 [2, 12, 512], P(None, None, 'dp')
- first_pixels: float32 [2, 12, 512], P(None, None, 'dp'), may hold values from -6e-05 to 6e-05
- second_pixels: float32 [2, 12, 512], P(None, None, 'dp'), may hold values from 5e-11 to 8e-10
Outputs:
- loss_value: float32 [], replicated
- grad_norm: float32 [], replicated
- updated_widein: float32 [1024, 10, 1024], P('dp', None, 'mp')
- moment_widein: float32 [1024, 10, 1024], P('dp', None, 'mp')
- square_widein: float32 [1024, 10, 1024], P('dp', None, 'mp')
- updated_narrowin: float32 [512, 3, 1024], P('dp', None, 'mp')
- moment_narrowin: float32 [512, 3, 1024], P('dp', None, 'mp')
- square_narrowin: float32 [512, 3, 1024], P('dp', None, 'mp')
- updated_wideout: float32 [6, 1024, 1024], P(None, 'mp', 'dp')
- moment_wideout: float32 [6, 1024, 1024], P(None, 'mp', 'dp')
- square_wideout: float32 [6, 1024, 1024], P(None, 'mp', 'dp')
- updated_narrowout: float32 [1024, 512], P('mp', 'dp')
- moment_narrowout: float32 [1024, 512], P('mp', 'dp')
- square_narrowout: float32 [1024, 512], P('mp', 'dp')
- updated_latents: float32 [128, 1024], P(None, 'dp')
- moment_latents: float32 [128, 1024], P(None, 'dp')
- square_latents: float32 [128, 1024], P(None, 'dp')
- updated_gains: float32 [11, 512], P(None, 'dp')
- moment_gains: float32 [11, 512], P(None, 'dp')
- square_gains: float32 [11, 512], P(None, 'dp')
- updated_pixels: float32 [2, 12, 512], P(None, None, 'dp')
- moment_pixels: float32 [2, 12, 512], P(None, None, 'dp')
- square_pixels: float32 [2, 12, 512], P(None, None, 'dp')
The draws below stay inside these ranges and needn't reach their ends.
Inputs may be any that keep to these rules, and one draw needn't show every extreme that they name: `present_mask`: every image has at least one present patch.
All inputs are finite; a program needn't handle non-finite values.
Results may differ from the reference program's by a relative error of at most 0.0035.
Values sent between devices are 32-bit elements; how exact they have to be, the bound alone decides.
A program may use at most 256 MiB of HBM per device.

```python
import math
import jax
import jax.numpy as jnp
from jax import lax

D_LAT = 1024
D_IF = 512
HEADS = 16
HEAD_DIM = 64
LATENTS = 128
PATCHES = 1024
PIX = 12
NSTEPS = 1000
STEP = 10
IMAGES = 32


def draw_present_mask(key, part):
    level = jax.random.randint(jax.random.fold_in(key, 11), (IMAGES, PATCHES), 0, 4)
    chosen = jax.random.randint(jax.random.fold_in(key, 12), (IMAGES, 1), 0, PATCHES)
    column = jnp.arange(PATCHES, dtype=jnp.int32)[None, :]
    return jnp.where((level != 0) | (column == chosen), 1, 0).astype(jnp.int32)


def output_scaled(key):
    values = jax.random.normal(key, (6, D_LAT, D_LAT), jnp.float32)
    attention_scale = (D_LAT // 64) ** (-0.5)
    feed_scale = 1.6 * (4 * D_LAT) ** (-0.5)
    scales = jnp.concatenate([jnp.full((2, 1, 1), attention_scale, jnp.float32), jnp.full((4, 1, 1), feed_scale, jnp.float32)])
    return values * scales


def pixel_scaled(key):
    values = jax.random.normal(key, (2, PIX, D_IF), jnp.float32)
    scales = jnp.concatenate([jnp.full((1, 1, 1), PIX ** (-0.5), jnp.float32), jnp.full((1, 1, 1), D_IF ** (-0.5), jnp.float32)])
    return values * scales


def draw_copy_wideout(key, part):
    return output_scaled(jax.random.fold_in(key, 21)).astype(jnp.bfloat16)


def draw_master_wideout(key, part):
    return output_scaled(jax.random.fold_in(key, 22))


def draw_copy_pixels(key, part):
    return pixel_scaled(jax.random.fold_in(key, 31)).astype(jnp.bfloat16)


def draw_master_pixels(key, part):
    return pixel_scaled(jax.random.fold_in(key, 32))


def set_ends(values, own_key, low, high):
    longest = values.shape.index(max(values.shape))
    spots = []
    for shift in (0, 1):
        where = [jax.random.randint(jax.random.fold_in(own_key, axis), (), 0, length) for axis, length in enumerate(values.shape)]
        where[longest] = (where[longest] + shift) % values.shape[longest]
        spots.append(tuple(where))
    return values.at[spots[0]].set(low).at[spots[1]].set(high)


def shard_levels(own_key, shape, split, smallest, top_value):
    factor_of, own = 1.0, jax.random.fold_in(own_key, 6)
    for position, shards_of in split:
        draws = jnp.exp(jax.random.uniform(jax.random.fold_in(own, position), (shards_of,), jnp.float32, smallest / len(split), top_value / len(split)))
        factor_of = factor_of * jnp.repeat(draws, shape[position] // shards_of).reshape([-1 if axis == position else 1 for axis in range(len(shape))])
    return factor_of


def bell_draw(key, shape, spread, bound, shards=(), held_as=jnp.bfloat16):
    values = spread * jax.random.normal(key, shape, jnp.float32)
    if shards:
        values = values * shard_levels(key, shape, shards, -0.22, 0.18)
    return jnp.clip(values, -bound, bound).astype(held_as)


def setup_inputs(seed: int = 0) -> dict:
    arg_keys = jax.random.split(jax.random.key(seed), 33)
    return {
        "clean_patches": jnp.clip(jax.random.uniform(arg_keys[0], (IMAGES, PIX, PATCHES), jnp.float32, -1.0, 1.0) * shard_levels(arg_keys[0], (IMAGES, PIX, PATCHES), ((0, 8),), -0.4, 0.0), -1.0, 1.0),
        "noise_patches": bell_draw(arg_keys[1], (IMAGES, PIX, PATCHES), 1.0, 6.0, ((0, 8),), jnp.float32),
        "timesteps": set_ends(jax.random.randint(arg_keys[2], (IMAGES,), 0, NSTEPS), jax.random.fold_in(arg_keys[2], 1), 0, NSTEPS - 1).astype(jnp.int32),
        "present_mask": draw_present_mask(jax.random.fold_in(arg_keys[32], 71), 0),
        "copy_widein": bell_draw(arg_keys[4], (D_LAT, 10, D_LAT), D_LAT ** -0.5, 0.1875, ((2, 4),)),
        "copy_narrowin": bell_draw(arg_keys[5], (D_IF, 3, D_LAT), D_IF ** -0.5, 0.25, ((2, 4),)),
        "copy_wideout": draw_copy_wideout(jax.random.fold_in(arg_keys[32], 71), 0),
        "copy_narrowout": bell_draw(arg_keys[7], (D_LAT, D_IF), (D_LAT // 64) ** -0.5, 1.5, ((0, 4),)),
        "copy_latents": bell_draw(arg_keys[8], (LATENTS, D_LAT), 0.5, 3.0),
        "copy_gains": jnp.clip(1.0 + 0.1 * jax.random.normal(arg_keys[9], (11, D_IF), jnp.float32), 0.5, 1.5).astype(jnp.bfloat16),
        "copy_pixels": draw_copy_pixels(jax.random.fold_in(arg_keys[32], 71), 0),
        "master_widein": bell_draw(arg_keys[11], (D_LAT, 10, D_LAT), D_LAT ** -0.5, 0.1875, ((0, 8), (2, 4)), jnp.float32),
        "first_widein": bell_draw(arg_keys[12], (D_LAT, 10, D_LAT), (3e-6), 1.8000000636675395e-05, ((0, 8), (2, 4)), jnp.float32),
        "second_widein": jnp.clip(jnp.exp(math.log(7.200000318174915e-11) - 2.7725887 * jax.random.uniform(arg_keys[13], (D_LAT, 10, D_LAT), jnp.float32) ** shard_levels(arg_keys[13], (D_LAT, 10, D_LAT), ((0, 8), (2, 4)), -0.2, 0.2)), 4.500000198859322e-12, 7.200000318174915e-11),
        "master_narrowin": bell_draw(arg_keys[14], (D_IF, 3, D_LAT), D_IF ** -0.5, 0.25, ((0, 8), (2, 4)), jnp.float32),
        "first_narrowin": bell_draw(arg_keys[15], (D_IF, 3, D_LAT), (3e-6), 1.8000000636675395e-05, ((0, 8), (2, 4)), jnp.float32),
        "second_narrowin": jnp.clip(jnp.exp(math.log(7.200000318174915e-11) - 2.7725887 * jax.random.uniform(arg_keys[16], (D_IF, 3, D_LAT), jnp.float32) ** shard_levels(arg_keys[16], (D_IF, 3, D_LAT), ((0, 8), (2, 4)), -0.2, 0.2)), 4.500000198859322e-12, 7.200000318174915e-11),
        "master_wideout": draw_master_wideout(jax.random.fold_in(arg_keys[32], 71), 0),
        "first_wideout": bell_draw(arg_keys[18], (6, D_LAT, D_LAT), (3e-6), 1.8000000636675395e-05, ((1, 4), (2, 8)), jnp.float32),
        "second_wideout": jnp.clip(jnp.exp(math.log(7.200000318174915e-11) - 2.7725887 * jax.random.uniform(arg_keys[19], (6, D_LAT, D_LAT), jnp.float32) ** shard_levels(arg_keys[19], (6, D_LAT, D_LAT), ((1, 4), (2, 8)), -0.2, 0.2)), 4.500000198859322e-12, 7.200000318174915e-11),
        "master_narrowout": bell_draw(arg_keys[20], (D_LAT, D_IF), (D_LAT // 64) ** -0.5, 1.5, ((0, 4), (1, 8)), jnp.float32),
        "first_narrowout": bell_draw(arg_keys[21], (D_LAT, D_IF), (3e-6), 1.8000000636675395e-05, ((0, 4), (1, 8)), jnp.float32),
        "second_narrowout": jnp.clip(jnp.exp(math.log(7.200000318174915e-11) - 2.7725887 * jax.random.uniform(arg_keys[22], (D_LAT, D_IF), jnp.float32) ** shard_levels(arg_keys[22], (D_LAT, D_IF), ((0, 4), (1, 8)), -0.2, 0.2)), 4.500000198859322e-12, 7.200000318174915e-11),
        "master_latents": bell_draw(arg_keys[23], (LATENTS, D_LAT), 0.5, 3.0, ((1, 8),), jnp.float32),
        "first_latents": bell_draw(arg_keys[24], (LATENTS, D_LAT), (0.0013 / (16 * D_LAT * D_LAT + 4 * D_IF * D_LAT + LATENTS * D_LAT + (11 + 2 * PIX) * D_IF) ** 0.5), 1.7883437521959422e-06, ((1, 8),), jnp.float32),
        "second_latents": jnp.clip(jnp.exp(math.log(3.5535257462276926e-13) - 1.3862944 * jax.random.uniform(arg_keys[25], (LATENTS, D_LAT), jnp.float32) ** shard_levels(arg_keys[25], (LATENTS, D_LAT), ((1, 8),), -0.2, 0.2)), 8.883814365569231e-14, 3.5535257462276926e-13),
        "master_gains": jnp.clip(1.0 + 0.1 * jax.random.normal(arg_keys[26], (11, D_IF), jnp.float32), 0.5, 1.5),
        "first_gains": bell_draw(arg_keys[27], (11, D_IF), (1e-5), 5.999999848427251e-05, ((1, 8),), jnp.float32),
        "second_gains": jnp.clip(jnp.exp(math.log(8.000000106811456e-10) - 2.7725887 * jax.random.uniform(arg_keys[28], (11, D_IF), jnp.float32) ** shard_levels(arg_keys[28], (11, D_IF), ((1, 8),), -0.2, 0.2)), 5.00000006675716e-11, 8.000000106811456e-10),
        "master_pixels": draw_master_pixels(jax.random.fold_in(arg_keys[32], 71), 0),
        "first_pixels": bell_draw(arg_keys[30], (2, PIX, D_IF), (1e-5), 5.999999848427251e-05, ((2, 8),), jnp.float32),
        "second_pixels": jnp.clip(jnp.exp(math.log(8.000000106811456e-10) - 2.7725887 * jax.random.uniform(arg_keys[31], (2, PIX, D_IF), jnp.float32) ** shard_levels(arg_keys[31], (2, PIX, D_IF), ((2, 8),), -0.2, 0.2)), 5.00000006675716e-11, 8.000000106811456e-10),
    }


precise = lax.Precision.HIGHEST
clip_level = 0.01
learning_rate = 0.05
weight_decay = 0.1
adam_beta = 0.5
adam_eps = 1e-08

@jax.custom_vjp
def low(v):
    return lax.optimization_barrier(v.astype(jnp.bfloat16)).astype(jnp.float32)

@jax.custom_vjp
def low_back(v):
    return v

def low_keep(v):
    return (low(v), None)

def low_pass(kept, grad):
    return (grad,)

def back_keep(v):
    return (v, None)

def back_low(kept, grad):
    return (low(grad),)
low.defvjp(low_keep, low_pass)
low_back.defvjp(back_keep, back_low)

def rounded(values):
    return low(low_back(values))

def layer_norm(values, gain):
    centered = values - lax.optimization_barrier(jnp.mean(values, -1, keepdims=True))
    return centered * lax.rsqrt(lax.optimization_barrier(jnp.mean(centered * centered, -1, keepdims=True)) + 1e-05) * gain

def positions():
    place = jnp.arange(PATCHES, dtype=jnp.float32)[:, None]
    index = jnp.arange(D_IF // 2, dtype=jnp.float32)[None, :]
    angle = place * jnp.exp(-math.log(10000.0) * 2.0 * index / D_IF)
    return jnp.concatenate([jnp.sin(angle), jnp.cos(angle)], -1)

def split_heads(values):
    return values.reshape(values.shape[0], HEADS, HEAD_DIM)

def attend(queries, keys, values, keep_mask):
    scores = jnp.einsum('qhd,khd->hqk', split_heads(queries), split_heads(keys), precision=precise) * HEAD_DIM ** (-0.5)
    if keep_mask is not None:
        scores = jnp.where(keep_mask[None, None, :] > 0, scores, -1e+30)
    scores = low_back(scores)
    probs = jax.nn.softmax(scores, axis=-1)
    output = jnp.einsum('hqk,khd->qhd', low(probs), split_heads(values), precision=precise)
    return rounded(output.reshape(output.shape[0], HEADS * HEAD_DIM))

def image_loss(params, noisy, keep_mask, noise, weight):
    widein, narrowin, wideout, narrowout, latents, gains, pixels = params

    def wide_gain(index):
        return gains[2 * index:2 * index + 2].reshape(D_LAT)
    interface = jnp.einsum('cp,cd->pd', noisy, pixels[0], precision=precise) + positions()
    normed = low(layer_norm(latents, wide_gain(0)))
    side = low(layer_norm(interface, gains[8]))
    query = rounded(jnp.dot(normed, widein[:, 0], precision=precise))
    pairs = rounded(jnp.einsum('pd,dsc->psc', side, narrowin[:, 0:2], precision=precise))
    output = attend(query, pairs[:, 0], pairs[:, 1], keep_mask)
    latent_one = latents + low_back(jnp.dot(output, wideout[0], precision=precise))
    normed = low(layer_norm(latent_one, wide_gain(1)))
    triple = rounded(jnp.einsum('ld,dsc->lsc', normed, widein[:, 1:4], precision=precise))
    output = attend(triple[:, 0], triple[:, 1], triple[:, 2], None)
    latent_two = latent_one + low_back(jnp.dot(output, wideout[1], precision=precise))
    normed = low(layer_norm(latent_two, wide_gain(2)))
    hidden = low_back(jnp.einsum('ld,dsc->lsc', normed, widein[:, 4:8], precision=precise))
    active = low(jax.nn.gelu(hidden, approximate=False))
    latent_three = latent_two + low_back(jnp.einsum('lsc,scd->ld', active, wideout[2:6], precision=precise))
    normed = low(layer_norm(latent_three, wide_gain(3)))
    side = low(layer_norm(interface, gains[9]))
    query = rounded(jnp.dot(side, narrowin[:, 2], precision=precise))
    pairs = rounded(jnp.einsum('ld,dsc->lsc', normed, widein[:, 8:10], precision=precise))
    output = attend(query, pairs[:, 0], pairs[:, 1], None)
    outer = interface + low_back(jnp.dot(output, narrowout, precision=precise))
    final = low(layer_norm(outer, gains[10]))
    predicted = low_back(jnp.einsum('pd,cd->cp', final, pixels[1], precision=precise))
    diff = predicted - noise
    return weight * jnp.sum(keep_mask[None, :] * diff * diff)

def adam_update(master, first, second, gradient, scale):
    clipped = gradient * scale
    moment = adam_beta * first + (1.0 - adam_beta) * clipped
    square = adam_beta * second + (1.0 - adam_beta) * clipped * clipped
    fixed_first = moment / (1.0 - adam_beta ** STEP)
    fixed_second = square / (1.0 - adam_beta ** STEP)
    updated = master - learning_rate * (fixed_first / (jnp.sqrt(fixed_second) + adam_eps) + weight_decay * master)
    return (updated, moment, square)

def reference(clean_patches, noise_patches, timesteps, present_mask, copy_widein, copy_narrowin, copy_wideout, copy_narrowout, copy_latents, copy_gains, copy_pixels, master_widein, first_widein, second_widein, master_narrowin, first_narrowin, second_narrowin, master_wideout, first_wideout, second_wideout, master_narrowout, first_narrowout, second_narrowout, master_latents, first_latents, second_latents, master_gains, first_gains, second_gains, master_pixels, first_pixels, second_pixels):
    signal = jnp.cos(0.5 * math.pi * (timesteps.astype(jnp.float32) + 0.5) / NSTEPS) ** 2
    noisy = jnp.sqrt(signal)[:, None, None] * clean_patches + jnp.sqrt(1.0 - signal)[:, None, None] * noise_patches
    loss_weight = 0.5 + signal
    keep_float = present_mask.astype(jnp.float32)
    weight_total = jnp.sum(loss_weight * PIX * lax.optimization_barrier(jnp.sum(keep_float, 1)))
    copies = (copy_widein, copy_narrowin, copy_wideout, copy_narrowout, copy_latents, copy_gains, copy_pixels)
    params = tuple((item.astype(jnp.float32) for item in copies))
    checked = jax.checkpoint(image_loss)

    def total(*weights):

        def one_image(carry, item):
            return (carry + checked(weights, item[0], item[1], item[2], item[3]), None)
        summed, unused = lax.scan(one_image, jnp.zeros((), jnp.float32), (noisy, keep_float, noise_patches, loss_weight))
        return summed / weight_total
    loss_value, pullback = jax.vjp(total, *params)
    grads = pullback(jnp.ones((), jnp.float32))
    grad_norm = jnp.sqrt(sum((jnp.sum(item * item) for item in grads)))
    scale = clip_level / jnp.maximum(grad_norm, clip_level)
    states = ((master_widein, first_widein, second_widein), (master_narrowin, first_narrowin, second_narrowin), (master_wideout, first_wideout, second_wideout), (master_narrowout, first_narrowout, second_narrowout), (master_latents, first_latents, second_latents), (master_gains, first_gains, second_gains), (master_pixels, first_pixels, second_pixels))
    results = []
    for state, gradient in zip(states, grads):
        results.extend(adam_update(state[0], state[1], state[2], gradient, scale))
    return (loss_value, grad_norm, results[0], results[1], results[2], results[3], results[4], results[5], results[6], results[7], results[8], results[9], results[10], results[11], results[12], results[13], results[14], results[15], results[16], results[17], results[18], results[19], results[20])
```

```python
from functools import partial
import math

import jax
import jax.numpy as jnp
from jax import lax
from jax.experimental import pallas as pl
from jax.experimental.pallas import tpu as pltpu
from jax.sharding import PartitionSpec as P

HEAD_DIM = 64
PIX = 12
NSTEPS = 1000
STEP = 10


precise = lax.Precision.HIGHEST
clip_level = 0.01
learning_rate = 0.05
weight_decay = 0.1
adam_beta = 0.5
adam_eps = 1e-08


def layer_norm(values, gain):
    centered = values - jnp.mean(values, -1, keepdims=True)
    scale = lax.rsqrt(jnp.mean(centered * centered, -1, keepdims=True) + 1e-05)
    normed = centered * scale
    return (normed * gain, (normed, scale))


def norm_back(upstream, gain, stats):
    normed, scale = stats
    inner = upstream * gain
    values = scale * (
        inner
        - jnp.mean(inner, -1, keepdims=True)
        - normed * jnp.mean(inner * normed, -1, keepdims=True)
    )
    gain_grad = jnp.sum((upstream * normed).reshape(-1, normed.shape[-1]), 0)
    return (values, gain_grad)


def positions(count, width):
    place = jnp.arange(count, dtype=jnp.float32)[:, None]
    index = jnp.arange(width // 2, dtype=jnp.float32)[None, :]
    angle = place * jnp.exp(-math.log(10000.0) * 2.0 * index / width)
    return jnp.concatenate([jnp.sin(angle), jnp.cos(angle)], -1)


def split_heads(values):
    return values.reshape(values.shape[:-1] + (values.shape[-1] // HEAD_DIM, HEAD_DIM))


def attend_scores(queries, keys, keep_mask):
    scores = jnp.einsum(
        "bqhe,bkhe->bhqk",
        split_heads(queries),
        split_heads(keys),
        preferred_element_type=jnp.float32,
    ) * HEAD_DIM ** (-0.5)
    if keep_mask is not None:
        scores = jnp.where(keep_mask[:, None, None, :] > 0, scores, -1e30)
    return scores


def attend_forward(queries, keys, values, keep_mask):
    scores = attend_scores(queries, keys, keep_mask)
    top = jnp.max(scores, -1, keepdims=True)
    log_total = top + jnp.log(jnp.sum(jnp.exp(scores - top), -1, keepdims=True))
    probs = jnp.exp(scores - log_total).astype(jnp.bfloat16)
    output = jnp.einsum(
        "bhqk,bkhe->bqhe", probs, split_heads(values), preferred_element_type=jnp.float32
    )
    return (output.reshape(queries.shape).astype(jnp.bfloat16), log_total)


def attend_back(queries, keys, values, keep_mask, log_total, upstream):
    scores = attend_scores(queries, keys, keep_mask)
    probs = jnp.exp(scores - log_total)
    value_grad = jnp.einsum(
        "bhqk,bqhe->bkhe",
        probs.astype(jnp.bfloat16),
        split_heads(upstream),
        preferred_element_type=jnp.float32,
    )
    prob_grad = jnp.einsum(
        "bqhe,bkhe->bhqk",
        split_heads(upstream),
        split_heads(values),
        preferred_element_type=jnp.float32,
    )
    score_grad = (probs * (prob_grad - jnp.sum(prob_grad * probs, -1, keepdims=True))).astype(
        jnp.bfloat16
    )
    query_grad = jnp.einsum(
        "bhqk,bkhe->bqhe", score_grad, split_heads(keys), preferred_element_type=jnp.float32
    ) * HEAD_DIM ** (-0.5)
    key_grad = jnp.einsum(
        "bhqk,bqhe->bkhe", score_grad, split_heads(queries), preferred_element_type=jnp.float32
    ) * HEAD_DIM ** (-0.5)
    return (
        query_grad.reshape(queries.shape).astype(jnp.bfloat16),
        key_grad.reshape(keys.shape),
        value_grad.reshape(values.shape),
    )


MESH_ID = pl.DeviceIdType.MESH
VMEM_SPEC = pl.BlockSpec(memory_space=pltpu.VMEM)
CHUNKS = 32


def remote(source, target, send_sem, recv_sem, device):
    return pltpu.make_async_remote_copy(
        src_ref=source,
        dst_ref=target,
        send_sem=send_sem,
        recv_sem=recv_sem,
        device_id=device,
        device_id_type=MESH_ID,
    )


def greet_line(place, count):
    barrier = pltpu.get_barrier_semaphore()
    below, above = {"mp": place - 1}, {"mp": place + 1}

    @pl.when(place > 0)
    def _():
        pl.semaphore_signal(barrier, inc=1, device_id=below, device_id_type=MESH_ID)

    @pl.when(place < count - 1)
    def _():
        pl.semaphore_signal(barrier, inc=1, device_id=above, device_id_type=MESH_ID)

    inside = jnp.logical_and(place > 0, place < count - 1)

    @pl.when(inside)
    def _():
        pl.semaphore_wait(barrier, 2)

    @pl.when(jnp.logical_not(inside))
    def _():
        pl.semaphore_wait(barrier, 1)


def line_sum_kernel(
    count,
    part_ref,
    base_ref,
    out_ref,
    inner,
    from_away,
    from_toward,
    toward_send,
    away_send,
    away_recv,
    toward_recv,
):
    place = lax.axis_index("mp")
    half = count // 2
    low_side = place < half
    toward = {"mp": jnp.where(low_side, place + 1, place - 1)}
    away = {"mp": jnp.where(low_side, place - 1, place + 1)}
    middle = jnp.logical_or(place == half - 1, place == half)
    outermost = jnp.logical_or(place == 0, place == count - 1)
    chunks = toward_send.shape[0]
    rows = part_ref.shape[0] // chunks
    greet_line(place, count)

    def window(step):
        return pl.ds(pl.multiple_of(step * rows, rows), rows)

    def push(step, source, inside):
        target = from_toward if inside else from_away
        recv = toward_recv if inside else away_recv
        return remote(
            source.at[window(step)],
            target.at[window(step)],
            toward_send.at[step],
            recv.at[step],
            toward,
        )

    def back(step, source):
        return remote(
            source.at[window(step)],
            from_toward.at[window(step)],
            away_send.at[step],
            toward_recv.at[step],
            away,
        )

    def gather_in(step):
        push(step, part_ref, False).wait_recv()
        inner[window(step)] = part_ref[window(step)] + from_away[window(step)]

    @pl.when(outermost)
    def _():
        def leave(step, carry):
            push(step, part_ref, False).start()
            return carry

        lax.fori_loop(0, chunks, leave, 0)

        def arrive(step, carry):
            push(step, part_ref, True).wait_recv()
            out_ref[window(step)] = from_toward[window(step)] + base_ref[window(step)]
            push(step, part_ref, False).wait_send()
            return carry

        lax.fori_loop(0, chunks, arrive, 0)

    lag = 2

    @pl.when(middle)
    def _():
        def finish(step):
            push(step, inner, True).wait_recv()
            push(step, inner, True).wait_send()
            total = inner[window(step)] + from_toward[window(step)]
            inner[window(step)] = total
            back(step, inner).start()
            out_ref[window(step)] = total + base_ref[window(step)]

        def first(step, carry):
            gather_in(step)
            push(step, inner, True).start()
            return carry

        def both(step, carry):
            first(step, carry)
            finish(step - lag)
            return carry

        def last(step, carry):
            finish(step)
            return carry

        def drain(step, carry):
            back(step, inner).wait_send()
            return carry

        lax.fori_loop(0, lag, first, 0)
        lax.fori_loop(lag, chunks, both, 0)
        lax.fori_loop(chunks - lag, chunks, last, 0)
        lax.fori_loop(0, chunks, drain, 0)

    if count > 4:

        @pl.when(jnp.logical_not(jnp.logical_or(middle, outermost)))
        def _():
            def inwards(step, carry):
                gather_in(step)
                push(step, inner, False).start()
                return carry

            def outwards(step, carry):
                push(step, inner, True).wait_recv()
                back(step, from_toward).start()
                out_ref[window(step)] = from_toward[window(step)] + base_ref[window(step)]
                return carry

            def drain(step, carry):
                push(step, inner, False).wait_send()
                back(step, from_toward).wait_send()
                return carry

            lax.fori_loop(0, chunks, inwards, 0)
            lax.fori_loop(0, chunks, outwards, 0)
            lax.fori_loop(0, chunks, drain, 0)


def line_sum(part, base, call_id):
    shape = part.shape
    part = part.reshape(-1, shape[-1])
    rows, width = part.shape
    buffer = pltpu.VMEM((rows, width), jnp.float32)
    sems = pltpu.SemaphoreType.DMA((CHUNKS,))
    out = pl.pallas_call(
        partial(line_sum_kernel, lax.axis_size("mp")),
        out_shape=jax.ShapeDtypeStruct((rows, width), jnp.float32),
        in_specs=[VMEM_SPEC] * 2,
        out_specs=VMEM_SPEC,
        scratch_shapes=[buffer] * 3 + [sems] * 4,
        compiler_params=pltpu.CompilerParams(
            collective_id=call_id, has_side_effects=True, vmem_limit_bytes=24 << 20
        ),
        cost_estimate=pl.CostEstimate(
            flops=4 * rows * width, bytes_accessed=16 * rows * width, transcendentals=0
        ),
    )(part, base.reshape(part.shape))
    return out.reshape(shape)


def line_scatter_kernel(
    count, part_ref, out_ref, up_acc, down_acc, from_below, from_above, up_send, down_send, up_recv, down_recv
):
    place = lax.axis_index("mp")
    steps = up_send.shape[1]
    block = part_ref.shape[0] // count
    rows = block // steps
    below, above = {"mp": place - 1}, {"mp": place + 1}
    greet_line(place, count)

    def window(owner, step):
        return pl.ds(pl.multiple_of(owner * block + step * rows, rows), rows)

    def up(owner, step, source):
        where = window(owner, step)
        return remote(
            source.at[where], from_below.at[where], up_send.at[owner, step], up_recv.at[owner, step], above
        )

    def down(owner, step, source):
        where = window(owner, step)
        return remote(
            source.at[where], from_above.at[where], down_send.at[owner, step], down_recv.at[owner, step], below
        )

    def up_turn(index):
        owner, step = count - 1 - index // steps, lax.rem(index, steps)

        @pl.when(jnp.logical_and(owner > place, place == 0))
        def _():
            up(owner, step, part_ref).start()

        @pl.when(jnp.logical_and(owner > place, place > 0))
        def _():
            up(owner, step, part_ref).wait_recv()
            where = window(owner, step)
            up_acc[where] = part_ref[where] + from_below[where]
            up(owner, step, up_acc).start()

    def down_turn(index):
        owner, step = index // steps, lax.rem(index, steps)

        @pl.when(jnp.logical_and(owner < place, place == count - 1))
        def _():
            down(owner, step, part_ref).start()

        @pl.when(jnp.logical_and(owner < place, place < count - 1))
        def _():
            down(owner, step, part_ref).wait_recv()
            where = window(owner, step)
            down_acc[where] = part_ref[where] + from_above[where]
            down(owner, step, down_acc).start()

    turns, lag = count * steps, steps

    def staggered(first, second):
        def begin(index, carry):
            first(index)
            return carry

        def both(index, carry):
            first(index)
            second(index - lag)
            return carry

        def end(index, carry):
            second(index)
            return carry

        lax.fori_loop(0, lag, begin, 0)
        lax.fori_loop(lag, turns, both, 0)
        lax.fori_loop(turns - lag, turns, end, 0)

    @pl.when(place < count // 2)
    def _():
        staggered(up_turn, down_turn)

    @pl.when(place >= count // 2)
    def _():
        staggered(down_turn, up_turn)

    def settle(step, carry):
        where = window(place, step)
        mine = pl.ds(pl.multiple_of(step * rows, rows), rows)
        out_ref[mine] = part_ref[where]

        @pl.when(place > 0)
        def _():
            up(place, step, part_ref).wait_recv()
            out_ref[mine] += from_below[where]

        @pl.when(place < count - 1)
        def _():
            down(place, step, part_ref).wait_recv()
            out_ref[mine] += from_above[where]

        return carry

    lax.fori_loop(0, steps, settle, 0)

    def drain(index, carry):
        owner, step = index // steps, lax.rem(index, steps)

        @pl.when(owner > place)
        def _():
            up(owner, step, part_ref).wait_send()

        @pl.when(owner < place)
        def _():
            down(owner, step, part_ref).wait_send()

        return carry

    lax.fori_loop(0, count * steps, drain, 0)


def line_scatter(part, call_id):
    rows, width = part.shape
    count = lax.axis_size("mp")
    steps = 8
    buffer = pltpu.VMEM((rows, width), jnp.float32)
    sems = pltpu.SemaphoreType.DMA((count, steps))
    return pl.pallas_call(
        partial(line_scatter_kernel, count),
        out_shape=jax.ShapeDtypeStruct((rows // count, width), jnp.float32),
        in_specs=[VMEM_SPEC],
        out_specs=VMEM_SPEC,
        scratch_shapes=[buffer] * 4 + [sems] * 4,
        compiler_params=pltpu.CompilerParams(
            collective_id=call_id, has_side_effects=True, vmem_limit_bytes=24 << 20
        ),
        cost_estimate=pl.CostEstimate(
            flops=2 * rows * width, bytes_accessed=8 * rows * width, transcendentals=0
        ),
    )(part)


def line_gather_kernel(count, own_ref, out_ref, up_send, down_send, up_recv, down_recv):
    place = lax.axis_index("mp")
    steps = up_send.shape[1]
    block = own_ref.shape[0]
    rows = block // steps
    below, above = {"mp": place - 1}, {"mp": place + 1}
    greet_line(place, count)

    def window(owner, step):
        return pl.ds(pl.multiple_of(owner * block + step * rows, rows), rows)

    def up(owner, step):
        part = out_ref.at[window(owner, step)]
        return remote(part, part, up_send.at[owner, step], up_recv.at[owner, step], above)

    def down(owner, step):
        part = out_ref.at[window(owner, step)]
        return remote(part, part, down_send.at[owner, step], down_recv.at[owner, step], below)

    def begin(step, carry):
        out_ref[window(place, step)] = own_ref[pl.ds(pl.multiple_of(step * rows, rows), rows)]

        @pl.when(place < count - 1)
        def _():
            up(place, step).start()

        @pl.when(place > 0)
        def _():
            down(place, step).start()

        return carry

    lax.fori_loop(0, steps, begin, 0)

    def pass_on(index, carry):
        away, step = 1 + index // steps, lax.rem(index, steps)

        @pl.when(place - away >= 0)
        def _():
            up(place - away, step).wait_recv()

        @pl.when(jnp.logical_and(place - away >= 0, place < count - 1))
        def _():
            up(place - away, step).start()

        @pl.when(place + away < count)
        def _():
            down(place + away, step).wait_recv()

        @pl.when(jnp.logical_and(place + away < count, place > 0))
        def _():
            down(place + away, step).start()

        return carry

    lax.fori_loop(0, (count - 1) * steps, pass_on, 0)

    def drain(index, carry):
        owner, step = index // steps, lax.rem(index, steps)

        @pl.when(jnp.logical_and(owner <= place, place < count - 1))
        def _():
            up(owner, step).wait_send()

        @pl.when(jnp.logical_and(owner >= place, place > 0))
        def _():
            down(owner, step).wait_send()

        return carry

    lax.fori_loop(0, count * steps, drain, 0)


def line_gather(own, call_id):
    rows, width = own.shape
    count = lax.axis_size("mp")
    steps = 8
    sems = pltpu.SemaphoreType.DMA((count, steps))
    return pl.pallas_call(
        partial(line_gather_kernel, count),
        out_shape=jax.ShapeDtypeStruct((rows * count, width), jnp.float32),
        in_specs=[VMEM_SPEC],
        out_specs=VMEM_SPEC,
        scratch_shapes=[sems] * 4,
        compiler_params=pltpu.CompilerParams(
            collective_id=call_id, has_side_effects=True, vmem_limit_bytes=16 << 20
        ),
        cost_estimate=pl.CostEstimate(
            flops=rows * width, bytes_accessed=8 * rows * width * count, transcendentals=0
        ),
    )(own)


def mesh_sum_kernel(axes, tile_ref, out_ref, held, send_sem, recv_sem):
    barrier = pltpu.get_barrier_semaphore()
    places = {name: lax.axis_index(name) for name, _ in axes}

    def peer(name, count, step):
        return {name: lax.rem(places[name] + step, count)}

    for name, count in axes:

        def greet(step, carry, name=name, count=count):
            pl.semaphore_signal(
                barrier, inc=1, device_id=peer(name, count, step), device_id_type=MESH_ID
            )
            return carry

        lax.fori_loop(1, count, greet, 0)
    pl.semaphore_wait(barrier, sum(count - 1 for _, count in axes))
    value = tile_ref[...]
    first = 0
    for name, count in axes:
        place = places[name]
        held[first + place] = value

        def copy(step, slot, name=name, count=count, first=first, place=place):
            return remote(
                held.at[first + place],
                held.at[first + slot],
                send_sem.at[first + step],
                recv_sem.at[first + slot],
                peer(name, count, step),
            )

        def send(step, carry, copy=copy, place=place):
            copy(step, place).start()
            return carry

        def take(step, carry, copy=copy, count=count, place=place):
            copy(step, lax.rem(place + step, count)).wait_recv()
            return carry

        def add(slot, carry, first=first):
            return carry + held[first + slot]

        def drain(step, carry, copy=copy, place=place):
            copy(step, place).wait_send()
            return carry

        lax.fori_loop(1, count, send, 0)
        lax.fori_loop(1, count, take, 0)
        value = lax.fori_loop(1, count, add, held[first])
        lax.fori_loop(1, count, drain, 0)
        first += count
    out_ref[...] = value


def mesh_sum(tile, names, call_id):
    axes = [(name, lax.axis_size(name)) for name in names]
    slots = sum(count for _, count in axes)
    return pl.pallas_call(
        partial(mesh_sum_kernel, axes),
        out_shape=jax.ShapeDtypeStruct(tile.shape, jnp.float32),
        in_specs=[VMEM_SPEC],
        out_specs=VMEM_SPEC,
        scratch_shapes=[
            pltpu.VMEM((slots,) + tile.shape, jnp.float32),
            pltpu.SemaphoreType.DMA((slots,)),
            pltpu.SemaphoreType.DMA((slots,)),
        ],
        compiler_params=pltpu.CompilerParams(collective_id=call_id, has_side_effects=True),
    )(tile)


def adam_update(master, first, second, gradient, scale):
    clipped = gradient * scale
    moment = adam_beta * first + (1.0 - adam_beta) * clipped
    square = adam_beta * second + (1.0 - adam_beta) * clipped * clipped
    fixed_first = moment / (1.0 - adam_beta**STEP)
    fixed_second = square / (1.0 - adam_beta**STEP)
    updated = master - learning_rate * (
        fixed_first / (jnp.sqrt(fixed_second) + adam_eps) + weight_decay * master
    )
    return (updated, moment, square)


def body(
    clean_patches,
    noise_patches,
    timesteps,
    present_mask,
    copy_widein,
    copy_narrowin,
    copy_wideout,
    copy_narrowout,
    copy_latents,
    copy_gains,
    copy_pixels,
    master_widein,
    first_widein,
    second_widein,
    master_narrowin,
    first_narrowin,
    second_narrowin,
    master_wideout,
    first_wideout,
    second_wideout,
    master_narrowout,
    first_narrowout,
    second_narrowout,
    master_latents,
    first_latents,
    second_latents,
    master_gains,
    first_gains,
    second_gains,
    master_pixels,
    first_pixels,
    second_pixels,
):
    images = clean_patches.shape[0]
    patches = clean_patches.shape[2]
    count_mp, count_dp = lax.axis_size("mp"), lax.axis_size("dp")
    mp_index, dp_index = lax.axis_index("mp"), lax.axis_index("dp")
    lead = (mp_index == 0).astype(jnp.float32)
    latents, d_lat = copy_latents.shape
    d_if = copy_gains.shape[1]
    local = copy_widein.shape[2]
    sharers = max(1, count_mp // images)
    own_images = max(1, images // count_mp)
    own_patches, own_latents = patches // sharers, latents // sharers
    first_image = mp_index * own_images // sharers
    share = lax.rem(mp_index, sharers)

    def dp_piece(values, axis):
        size = values.shape[axis] // count_dp
        return lax.dynamic_slice_in_dim(values, dp_index * size, size, axis).astype(jnp.float32)

    key_piece = dp_piece(copy_widein[:, 8], 0)
    value_piece = dp_piece(copy_widein[:, 9], 0)
    query_piece = dp_piece(copy_narrowin[:, 2], 0)
    out_piece = dp_piece(copy_narrowout, 1).T
    gathered = lax.all_gather(
        jnp.concatenate([key_piece, value_piece, query_piece, out_piece], 0), ("mp", "dp")
    ).reshape(count_mp, count_dp, -1, local)
    nothing = jnp.where(timesteps[0] > 0, 0.0, -0.0)
    gathered = gathered + nothing
    edges = [0, d_lat, 2 * d_lat, 2 * d_lat + d_if, 2 * d_lat + 2 * d_if]
    write_key_weight, write_value_weight, write_query_weight, write_out_weight = (
        gathered[:, :, low // count_dp : high // count_dp]
        .reshape(count_mp, high - low, local)
        .astype(jnp.bfloat16)
        for low, high in zip(edges[:-1], edges[1:])
    )

    signal = jnp.cos(0.5 * math.pi * (timesteps.astype(jnp.float32) + 0.5) / NSTEPS) ** 2
    noisy = (
        jnp.sqrt(signal)[:, None, None] * clean_patches
        + jnp.sqrt(1.0 - signal)[:, None, None] * noise_patches
    )
    loss_weight = 0.5 + signal
    keep_float = present_mask.astype(jnp.float32)
    weight_here = jnp.sum(loss_weight * PIX * jnp.sum(keep_float, 1))
    weight_total = mesh_sum(jnp.full((8, 128), weight_here), ("dp",), 1)[0, 0]
    gain_rows = copy_gains.astype(jnp.float32)

    def wide_gain(index):
        return gain_rows[2 * index : 2 * index + 2].reshape(-1)

    pixel_rows = copy_pixels.astype(jnp.float32)
    interface = jnp.einsum("bcp,cd->bpd", noisy, pixel_rows[0], precision=precise) + positions(
        noisy.shape[2], pixel_rows.shape[2]
    )
    latent_zero = copy_latents.astype(jnp.float32)
    read_norm, read_stats = layer_norm(latent_zero, wide_gain(0))
    read_low = read_norm.astype(jnp.bfloat16)
    side_norm, side_stats = layer_norm(interface, gain_rows[8])
    side_low = side_norm.astype(jnp.bfloat16)
    read_query = jnp.einsum(
        "ld,dc->lc", read_low, copy_widein[:, 0], preferred_element_type=jnp.float32
    ).astype(jnp.bfloat16)
    read_query = jnp.broadcast_to(read_query[None], (images,) + read_query.shape)
    read_key = jnp.einsum(
        "bpd,dc->bpc", side_low, copy_narrowin[:, 0], preferred_element_type=jnp.float32
    ).astype(jnp.bfloat16)
    read_value = jnp.einsum(
        "bpd,dc->bpc", side_low, copy_narrowin[:, 1], preferred_element_type=jnp.float32
    ).astype(jnp.bfloat16)
    read_out, read_total = attend_forward(read_query, read_key, read_value, present_mask)
    latent_one = line_sum(
        jnp.einsum("blc,cd->bld", read_out, copy_wideout[0], preferred_element_type=jnp.float32),
        jnp.broadcast_to(latent_zero[None], (images, latents, d_lat)),
        2,
    )
    self_norm, self_stats = layer_norm(latent_one, wide_gain(1))
    self_low = self_norm.astype(jnp.bfloat16)
    self_triple = jnp.einsum(
        "bld,dsc->blsc", self_low, copy_widein[:, 1:4], preferred_element_type=jnp.float32
    ).astype(jnp.bfloat16)
    self_out, self_total = attend_forward(
        self_triple[:, :, 0], self_triple[:, :, 1], self_triple[:, :, 2], None
    )
    latent_two = line_sum(
        jnp.einsum("blc,cd->bld", self_out, copy_wideout[1], preferred_element_type=jnp.float32),
        latent_one,
        3,
    )
    feed_norm, feed_stats = layer_norm(latent_two, wide_gain(2))
    feed_low = feed_norm.astype(jnp.bfloat16)
    hidden = jnp.einsum(
        "bld,dsc->blsc", feed_low, copy_widein[:, 4:8], preferred_element_type=jnp.float32
    )
    active, gelu_pull = jax.vjp(partial(jax.nn.gelu, approximate=False), hidden)
    active_low = active.astype(jnp.bfloat16)
    feed_partial = jnp.einsum(
        "blsc,scd->bld", active_low, copy_wideout[2:6], preferred_element_type=jnp.float32
    )

    def own_rows(values):
        values = values.reshape((images * sharers, own_latents) + values.shape[2:])
        return lax.dynamic_slice_in_dim(values, mp_index * own_images, own_images, 0)

    latent_three = own_rows(latent_two) + line_scatter(
        feed_partial.reshape(-1, d_lat), 4
    ).reshape(own_images, own_latents, d_lat)
    write_norm, write_stats = layer_norm(latent_three, wide_gain(3))
    write_low = write_norm.astype(jnp.bfloat16)

    def own_tokens(values, axis):
        values = lax.dynamic_slice_in_dim(values, first_image, own_images, 0)
        return lax.dynamic_slice_in_dim(values, share * own_patches, own_patches, axis)

    own_interface = own_tokens(interface, 1)
    own_noisy, own_noise = own_tokens(noisy, 2), own_tokens(noise_patches, 2)
    own_keep = own_tokens(keep_float, 1)
    own_weight = lax.dynamic_slice_in_dim(loss_weight, first_image, own_images, 0)

    outer_norm, outer_stats = layer_norm(own_interface, gain_rows[9])
    outer_low = outer_norm.astype(jnp.bfloat16)

    def join(spec, values, weight):
        product = jnp.einsum(spec, values, weight, preferred_element_type=jnp.float32)
        return product.astype(jnp.bfloat16).reshape(product.shape[:2] + (-1,))

    def image_rows(values):
        if sharers == 1:
            return values
        whole = lax.all_gather(values.astype(jnp.float32), "mp", axis=0, tiled=True)
        whole = whole + nothing
        whole = whole.reshape(images, latents, d_lat).astype(jnp.bfloat16)
        return lax.dynamic_slice_in_dim(whole, first_image, own_images, 0)

    write_query = join("bpd,mdc->bpmc", outer_low, write_query_weight)
    write_key = image_rows(join("bld,mdc->blmc", write_low, write_key_weight))
    write_value = image_rows(join("bld,mdc->blmc", write_low, write_value_weight))
    write_out, write_total = attend_forward(write_query, write_key, write_value, None)
    write_split = write_out.reshape(write_out.shape[:2] + (count_mp, local))
    outer = own_interface + jnp.einsum(
        "bpmc,mdc->bpd", write_split, write_out_weight, preferred_element_type=jnp.float32
    )
    final_norm, final_stats = layer_norm(outer, gain_rows[10])
    final_low = final_norm.astype(jnp.bfloat16)
    predicted = jnp.einsum(
        "bpd,cd->bcp", final_low, copy_pixels[1], preferred_element_type=jnp.float32
    )
    difference = predicted - own_noise
    masked = own_weight[:, None, None] * own_keep[:, None, :] * difference
    loss_local = jnp.sum(masked * difference)
    predict_grad = (2.0 * masked / weight_total).astype(jnp.bfloat16)
    head_grad = jnp.einsum(
        "bcp,bpd->cd", predict_grad, final_low, preferred_element_type=jnp.float32
    )
    final_grad = jnp.einsum(
        "bcp,cd->bpd", predict_grad, copy_pixels[1], preferred_element_type=jnp.float32
    )
    outer_grad, gain_final = norm_back(final_grad, gain_rows[10], final_stats)
    branch_low = outer_grad.astype(jnp.bfloat16)
    narrowout_grad = jnp.einsum(
        "bpd,bpmc->mdc", branch_low, write_split, preferred_element_type=jnp.float32
    )
    write_upstream = join("bpd,mdc->bpmc", branch_low, write_out_weight)
    query_grad, key_grad, value_grad = attend_back(
        write_query, write_key, write_value, None, write_total, write_upstream
    )
    query_split = query_grad.reshape(query_grad.shape[:2] + (count_mp, local))
    write_query_grad = jnp.einsum(
        "bpd,bpmc->mdc", outer_low, query_split, preferred_element_type=jnp.float32
    )
    outer_part = jnp.einsum(
        "bpmc,mdc->bpd", query_split, write_query_weight, preferred_element_type=jnp.float32
    )

    def row_grad(values):
        if sharers > 1:
            whole = jnp.zeros((images, latents, d_lat), jnp.float32)
            whole = lax.dynamic_update_slice_in_dim(whole, values, first_image, 0)
            values = lax.psum_scatter(
                whole.reshape(images * sharers, own_latents, d_lat),
                "mp",
                scatter_dimension=0,
                tiled=True,
            )
        values = values.astype(jnp.bfloat16)
        return values.reshape(values.shape[:2] + (count_mp, local))

    key_grad, value_grad = row_grad(key_grad), row_grad(value_grad)
    write_key_grad = jnp.einsum(
        "bld,blmc->mdc", write_low, key_grad, preferred_element_type=jnp.float32
    )
    write_value_grad = jnp.einsum(
        "bld,blmc->mdc", write_low, value_grad, preferred_element_type=jnp.float32
    )
    write_part = jnp.einsum(
        "blmc,mdc->bld", key_grad, write_key_weight, preferred_element_type=jnp.float32
    ) + jnp.einsum(
        "blmc,mdc->bld", value_grad, write_value_weight, preferred_element_type=jnp.float32
    )
    own_grad, gain_write = norm_back(write_part, wide_gain(3), write_stats)
    latent_grad = line_gather(own_grad.reshape(-1, d_lat), 5).reshape(latent_one.shape)
    outer_back, gain_outer = norm_back(outer_part, gain_rows[9], outer_stats)

    def pieces(values, groups):
        return values.reshape(groups, -1, local)

    def both_pieces(values):
        values = values.reshape(count_mp, count_dp, -1, local)
        return jnp.swapaxes(values, 0, 1)

    write_joined = jnp.concatenate(
        [
            both_pieces(item)
            for item in (write_key_grad, write_value_grad, write_query_grad, narrowout_grad)
        ],
        2,
    )
    write_share = lax.psum_scatter(
        lax.psum_scatter(write_joined, "dp", scatter_dimension=0), "mp", scatter_dimension=0
    )

    def dp_scatter(items):
        joined = jnp.concatenate([pieces(item, count_dp) for item in items], 1)
        return lax.psum_scatter(joined, "dp", scatter_dimension=0)

    branch_low = latent_grad.astype(jnp.bfloat16)
    down_grad = [
        jnp.einsum(
            "bld,blc->dc", branch_low, active_low[:, :, slot], preferred_element_type=jnp.float32
        )
        for slot in range(4)
    ]
    active_grad = jnp.einsum(
        "bld,scd->blsc", branch_low, copy_wideout[2:6], preferred_element_type=jnp.float32
    )
    hidden_grad = gelu_pull(active_grad)[0].astype(jnp.bfloat16)
    up_grad = [
        jnp.einsum(
            "bld,blc->dc", feed_low, hidden_grad[:, :, slot], preferred_element_type=jnp.float32
        )
        for slot in range(4)
    ]
    feed_part = jnp.einsum(
        "blsc,dsc->bld", hidden_grad, copy_widein[:, 4:8], preferred_element_type=jnp.float32
    )
    feed_share = dp_scatter(up_grad + down_grad)
    latent_part, gain_feed = norm_back(feed_part, wide_gain(2), feed_stats)
    latent_grad = line_sum(latent_part, latent_grad, 6)
    branch_low = latent_grad.astype(jnp.bfloat16)
    self_out_grad = jnp.einsum(
        "bld,blc->dc", branch_low, self_out, preferred_element_type=jnp.float32
    )
    self_upstream = jnp.einsum(
        "bld,cd->blc", branch_low, copy_wideout[1], preferred_element_type=jnp.float32
    ).astype(jnp.bfloat16)
    triple_grad = [
        item.astype(jnp.bfloat16)
        for item in attend_back(
            self_triple[:, :, 0],
            self_triple[:, :, 1],
            self_triple[:, :, 2],
            None,
            self_total,
            self_upstream,
        )
    ]
    self_in_grad = [
        jnp.einsum("bld,blc->dc", self_low, item, preferred_element_type=jnp.float32)
        for item in triple_grad
    ]
    self_part = jnp.einsum(
        "blsc,dsc->bld",
        jnp.stack(triple_grad, 2),
        copy_widein[:, 1:4],
        preferred_element_type=jnp.float32,
    )
    self_share = dp_scatter(self_in_grad + [self_out_grad])
    latent_part, gain_self = norm_back(self_part, wide_gain(1), self_stats)
    latent_grad = line_sum(latent_part, latent_grad, 7)
    branch_low = latent_grad.astype(jnp.bfloat16)
    read_out_grad = jnp.einsum(
        "bld,blc->dc", branch_low, read_out, preferred_element_type=jnp.float32
    )
    read_upstream = jnp.einsum(
        "bld,cd->blc", branch_low, copy_wideout[0], preferred_element_type=jnp.float32
    ).astype(jnp.bfloat16)
    query_grad, key_grad, value_grad = (
        item.astype(jnp.bfloat16)
        for item in attend_back(
            read_query, read_key, read_value, present_mask, read_total, read_upstream
        )
    )
    read_query_grad = jnp.einsum(
        "ld,blc->dc", read_low, query_grad, preferred_element_type=jnp.float32
    )
    read_part = jnp.einsum(
        "blc,dc->bld", query_grad, copy_widein[:, 0], preferred_element_type=jnp.float32
    )
    normed, scale = read_stats
    latent_part, gain_read = norm_back(
        read_part, wide_gain(0), (normed[None], scale[None])
    )
    latent_total = jnp.sum(lead * latent_grad + latent_part, 0)
    read_key_grad = jnp.einsum(
        "bpd,bpc->dc", side_low, key_grad, preferred_element_type=jnp.float32
    )
    read_value_grad = jnp.einsum(
        "bpd,bpc->dc", side_low, value_grad, preferred_element_type=jnp.float32
    )
    side_part = jnp.einsum(
        "bpc,dc->bpd", key_grad, copy_narrowin[:, 0], preferred_element_type=jnp.float32
    ) + jnp.einsum(
        "bpc,dc->bpd", value_grad, copy_narrowin[:, 1], preferred_element_type=jnp.float32
    )
    side_back, gain_side = norm_back(side_part, gain_rows[8], side_stats)
    embed_grad = jnp.einsum("bcp,bpd->cd", noisy, side_back, precision=precise) + jnp.einsum(
        "bcp,bpd->cd", own_noisy, outer_grad + outer_back, precision=precise
    )
    gains_grad = jnp.concatenate(
        [
            gain_read.reshape(2, -1),
            gain_self.reshape(2, -1),
            gain_feed.reshape(2, -1),
            gain_write.reshape(2, -1),
            gain_side[None],
            gain_outer[None],
            gain_final[None],
        ],
        0,
    )

    def dp_columns(values):
        values = values.reshape(-1, count_dp, values.shape[-1] // count_dp)
        return jnp.swapaxes(values, 0, 1).reshape(count_dp, -1)

    small_parts = [
        dp_columns(item)
        for item in (latent_total, gains_grad, embed_grad, head_grad)
    ]
    small_sizes = [item.shape[1] for item in small_parts]
    small = jnp.concatenate(small_parts, 1)
    fill = -small.shape[1] % (8 * local)
    small = jnp.pad(small, ((0, 0), (0, fill))).reshape(count_dp, -1, local)
    read_joined = jnp.concatenate(
        [
            pieces(item, count_dp)
            for item in (read_query_grad, read_key_grad, read_value_grad, read_out_grad)
        ]
        + [small],
        1,
    )
    read_share = lax.psum_scatter(read_joined, "dp", scatter_dimension=0)
    lat_rows, if_rows = d_lat // count_dp, d_if // count_dp
    small_share = lax.psum(read_share[2 * lat_rows + 2 * if_rows :], "mp")
    small_flat = small_share.reshape(-1)
    latents_grad, gains_grad, embed_grad, head_grad = (
        small_flat[sum(small_sizes[:i]) : sum(small_sizes[: i + 1])].reshape(rows, -1)
        for i, rows in enumerate((latents, gains_grad.shape[0], PIX, PIX))
    )
    pixels_grad = jnp.stack([embed_grad, head_grad], 0)

    def cut(share, index, rows, start=0):
        return share[start + index * rows : start + (index + 1) * rows]

    widein_grad = jnp.stack(
        [cut(read_share, 0, lat_rows)]
        + [cut(self_share, i, lat_rows) for i in range(3)]
        + [cut(feed_share, i, lat_rows) for i in range(4)]
        + [cut(write_share, i, lat_rows) for i in range(2)],
        1,
    )
    narrowin_grad = jnp.stack(
        [
            cut(read_share, 0, if_rows, lat_rows),
            cut(read_share, 1, if_rows, lat_rows),
            cut(write_share, 0, if_rows, 2 * lat_rows),
        ],
        1,
    )
    wideout_grad = jnp.stack(
        [
            cut(read_share, 0, lat_rows, lat_rows + 2 * if_rows).T,
            cut(self_share, 3, lat_rows).T,
        ]
        + [cut(feed_share, 4 + i, lat_rows).T for i in range(4)],
        0,
    )
    narrowout_grad = cut(write_share, 1, if_rows, 2 * lat_rows).T
    shares = (
        widein_grad,
        narrowin_grad,
        wideout_grad,
        narrowout_grad,
        latents_grad,
        gains_grad,
        pixels_grad,
    )
    split_square = sum((jnp.sum(item * item) for item in shares[:4]))
    copied_square = sum((jnp.sum(item * item) for item in shares[4:]))
    lane = lax.broadcasted_iota(jnp.int32, (8, 128), 1)
    totals = mesh_sum(
        jnp.where(lane == 0, split_square + lead * copied_square, loss_local), ("dp", "mp"), 8
    )
    square_total, loss_total = totals[0, 0], totals[0, 1]
    grad_norm = jnp.sqrt(square_total)
    loss_value = loss_total / weight_total
    scale = clip_level / jnp.maximum(grad_norm, clip_level)
    states = (
        (master_widein, first_widein, second_widein),
        (master_narrowin, first_narrowin, second_narrowin),
        (master_wideout, first_wideout, second_wideout),
        (master_narrowout, first_narrowout, second_narrowout),
        (master_latents, first_latents, second_latents),
        (master_gains, first_gains, second_gains),
        (master_pixels, first_pixels, second_pixels),
    )
    results = []
    for state, gradient in zip(states, shares):
        results.extend(adam_update(state[0], state[1], state[2], gradient, scale))
    return (
        loss_value,
        grad_norm,
        results[0],
        results[1],
        results[2],
        results[3],
        results[4],
        results[5],
        results[6],
        results[7],
        results[8],
        results[9],
        results[10],
        results[11],
        results[12],
        results[13],
        results[14],
        results[15],
        results[16],
        results[17],
        results[18],
        results[19],
        results[20],
    )


def solution(mesh):
    in_specs = (
        P("dp", None, None),
        P("dp", None, None),
        P("dp"),
        P("dp", None),
        P(None, None, "mp"),
        P(None, None, "mp"),
        P(None, "mp", None),
        P("mp", None),
        P(),
        P(),
        P(),
        P("dp", None, "mp"),
        P("dp", None, "mp"),
        P("dp", None, "mp"),
        P("dp", None, "mp"),
        P("dp", None, "mp"),
        P("dp", None, "mp"),
        P(None, "mp", "dp"),
        P(None, "mp", "dp"),
        P(None, "mp", "dp"),
        P("mp", "dp"),
        P("mp", "dp"),
        P("mp", "dp"),
        P(None, "dp"),
        P(None, "dp"),
        P(None, "dp"),
        P(None, "dp"),
        P(None, "dp"),
        P(None, "dp"),
        P(None, None, "dp"),
        P(None, None, "dp"),
        P(None, None, "dp"),
    )
    out_specs = (
        P(),
        P(),
        P("dp", None, "mp"),
        P("dp", None, "mp"),
        P("dp", None, "mp"),
        P("dp", None, "mp"),
        P("dp", None, "mp"),
        P("dp", None, "mp"),
        P(None, "mp", "dp"),
        P(None, "mp", "dp"),
        P(None, "mp", "dp"),
        P("mp", "dp"),
        P("mp", "dp"),
        P("mp", "dp"),
        P(None, "dp"),
        P(None, "dp"),
        P(None, "dp"),
        P(None, "dp"),
        P(None, "dp"),
        P(None, "dp"),
        P(None, None, "dp"),
        P(None, None, "dp"),
        P(None, None, "dp"),
    )
    return jax.shard_map(body, mesh=mesh, in_specs=in_specs, out_specs=out_specs, check_vma=False)
```

```python
from functools import partial
import math

import jax
import jax.numpy as jnp
from jax import lax
from jax.experimental import pallas as pl
from jax.experimental.pallas import tpu as pltpu
from jax.sharding import PartitionSpec as P

HEAD_DIM = 64
PIX = 12
NSTEPS = 1000
STEP = 10


precise = lax.Precision.HIGHEST
clip_level = 0.01
learning_rate = 0.05
weight_decay = 0.1
adam_beta = 0.5
adam_eps = 1e-08


def layer_norm(values, gain):
    centered = values - jnp.mean(values, -1, keepdims=True)
    scale = lax.rsqrt(jnp.mean(centered * centered, -1, keepdims=True) + 1e-05)
    normed = centered * scale
    return (normed * gain, (normed, scale))


def norm_back(upstream, gain, stats):
    normed, scale = stats
    inner = upstream * gain
    values = scale * (
        inner
        - jnp.mean(inner, -1, keepdims=True)
        - normed * jnp.mean(inner * normed, -1, keepdims=True)
    )
    gain_grad = jnp.sum((upstream * normed).reshape(-1, normed.shape[-1]), 0)
    return (values, gain_grad)


def positions(count, width):
    place = jnp.arange(count, dtype=jnp.float32)[:, None]
    index = jnp.arange(width // 2, dtype=jnp.float32)[None, :]
    angle = place * jnp.exp(-math.log(10000.0) * 2.0 * index / width)
    return jnp.concatenate([jnp.sin(angle), jnp.cos(angle)], -1)


def split_heads(values):
    return values.reshape(values.shape[:-1] + (values.shape[-1] // HEAD_DIM, HEAD_DIM))


def attend_scores(queries, keys, keep_mask):
    scores = jnp.einsum(
        "bqhe,bkhe->bhqk",
        split_heads(queries),
        split_heads(keys),
        preferred_element_type=jnp.float32,
    ) * HEAD_DIM ** (-0.5)
    if keep_mask is not None:
        scores = jnp.where(keep_mask[:, None, None, :] > 0, scores, -1e30)
    return scores


def attend_forward(queries, keys, values, keep_mask):
    scores = attend_scores(queries, keys, keep_mask)
    top = jnp.max(scores, -1, keepdims=True)
    log_total = top + jnp.log(jnp.sum(jnp.exp(scores - top), -1, keepdims=True))
    probs = jnp.exp(scores - log_total).astype(jnp.bfloat16)
    output = jnp.einsum(
        "bhqk,bkhe->bqhe", probs, split_heads(values), preferred_element_type=jnp.float32
    )
    return (output.reshape(queries.shape).astype(jnp.bfloat16), log_total)


def attend_back(queries, keys, values, keep_mask, log_total, upstream):
    scores = attend_scores(queries, keys, keep_mask)
    probs = jnp.exp(scores - log_total)
    value_grad = jnp.einsum(
        "bhqk,bqhe->bkhe",
        probs.astype(jnp.bfloat16),
        split_heads(upstream),
        preferred_element_type=jnp.float32,
    )
    prob_grad = jnp.einsum(
        "bqhe,bkhe->bhqk",
        split_heads(upstream),
        split_heads(values),
        preferred_element_type=jnp.float32,
    )
    score_grad = (probs * (prob_grad - jnp.sum(prob_grad * probs, -1, keepdims=True))).astype(
        jnp.bfloat16
    )
    query_grad = jnp.einsum(
        "bhqk,bkhe->bqhe", score_grad, split_heads(keys), preferred_element_type=jnp.float32
    ) * HEAD_DIM ** (-0.5)
    key_grad = jnp.einsum(
        "bhqk,bqhe->bkhe", score_grad, split_heads(queries), preferred_element_type=jnp.float32
    ) * HEAD_DIM ** (-0.5)
    return (
        query_grad.reshape(queries.shape).astype(jnp.bfloat16),
        key_grad.reshape(keys.shape),
        value_grad.reshape(values.shape),
    )


MESH_ID = pl.DeviceIdType.MESH
VMEM_SPEC = pl.BlockSpec(memory_space=pltpu.VMEM)
CHUNKS = 32
VMEM_LIMIT = 56 << 20


def remote(source, target, send_sem, recv_sem, device):
    return pltpu.make_async_remote_copy(
        src_ref=source,
        dst_ref=target,
        send_sem=send_sem,
        recv_sem=recv_sem,
        device_id=device,
        device_id_type=MESH_ID,
    )


class PieceSums:
    def __init__(self, count, items, outs, scratch):
        self.count, self.items, self.outs = count, items, outs
        self.bits = count.bit_length() - 1
        self.place = lax.axis_index("dp") if items else None
        self.held = []
        for index in range(len(items)):
            self.held.append(scratch[index * (self.bits + 2) : (index + 1) * (self.bits + 2)])

    @staticmethod
    def scratch(count, shapes):
        bits = count.bit_length() - 1
        result = []
        for rows, width in shapes:
            result.append(pltpu.VMEM((count // 2, rows, width), jnp.float32))
            for phase in range(2, bits + 1):
                result.append(
                    pltpu.VMEM((2 * (count >> phase), rows // 2, width), jnp.float32)
                )
            copies = count // 2 + 2 * sum(count >> phase for phase in range(2, bits + 1))
            result += [pltpu.SemaphoreType.DMA((copies,))] * 2
        return result

    def peers(self):
        return [{"dp": self.place ^ (1 << bit)} for bit in range(self.bits)] if self.items else []

    def order(self, half):
        later = list(range(1, self.bits))
        turn = half * (len(later) // 2)
        return later[turn:] + later[:turn]

    def first_copy(self, index, piece):
        item, held = self.items[index], self.held[index]
        other = 1 - (self.place & 1)
        return remote(
            item.at[2 * piece + other],
            held[0].at[piece],
            held[-2].at[piece],
            held[-1].at[piece],
            {"dp": self.place ^ 1},
        )

    def member(self, half, phase, entry, flip):
        bits = self.order(half)
        settled, now, rest = bits[: phase - 2], bits[phase - 2], bits[phase - 1 :]
        piece = 0
        for bit in settled:
            piece = piece | (self.place & (1 << bit))
        own = self.place & (1 << now)
        piece = piece | ((own ^ (1 << now)) if flip else own)
        for position, bit in enumerate(rest):
            if (entry >> position) & 1:
                piece = piece | (1 << bit)
        return piece >> 1

    def later_copy(self, index, half, phase, entry):
        held = self.held[index]
        rows = self.items[index].shape[1] // 2
        size = self.count >> phase
        sem = self.count // 2 + 2 * sum(self.count >> p for p in range(2, phase)) + half * size + entry
        return remote(
            held[0].at[self.member(half, phase, entry, True), pl.ds(half * rows, rows)],
            held[phase - 1].at[half * size + entry],
            held[-2].at[sem],
            held[-1].at[sem],
            {"dp": self.place ^ (1 << self.order(half)[phase - 2])},
        )

    def entries(self, phase):
        return [
            (index, half, entry)
            for index in range(len(self.items))
            for half in range(2)
            for entry in range(self.count >> phase)
        ]

    def begin(self):
        for index in range(len(self.items)):
            for piece in range(self.count // 2):
                self.first_copy(index, piece).start()

    def send(self, phase):
        for index, half, entry in self.entries(phase):
            self.later_copy(index, half, phase, entry).start()

    def advance(self, phase):
        if not self.items:
            return
        if phase == 1:
            own = self.place & 1
            for index, item in enumerate(self.items):
                total = self.held[index][0]
                for piece in range(self.count // 2):
                    self.first_copy(index, piece).wait_recv()
                    add_rows(total.at[piece], total.at[piece], item.at[2 * piece + own])
        else:
            for index, half, entry in self.entries(phase):
                self.later_copy(index, half, phase, entry).wait_recv()
                held, rows = self.held[index], self.items[index].shape[1] // 2
                where = pl.ds(half * rows, rows)
                came = held[phase - 1].at[half * (self.count >> phase) + entry]
                kept = held[0].at[self.member(half, phase, entry, False), where]
                if phase == self.bits:
                    add_rows(self.outs[index].at[where], kept, came)
                else:
                    add_rows(kept, kept, came)
        if phase < self.bits:
            self.send(phase + 1)

    def finish(self):
        for index in range(len(self.items)):
            for piece in range(self.count // 2):
                self.first_copy(index, piece).wait_send()
        for phase in range(2, self.bits + 1):
            for index, half, entry in self.entries(phase):
                self.later_copy(index, half, phase, entry).wait_send()

    def moments(self, total):
        if not self.items:
            return [(0, total, None)]
        marks, low = [], 0
        for phase in range(1, self.bits + 1):
            share = (1 - 0.5 ** (phase - 1)) / (1 - 0.5 ** (self.bits - 1))
            high = total if phase == self.bits else int(total * (0.22 + 0.78 * share))
            marks.append((low, high, phase))
            low = high
        return marks


def add_rows(target, left, right):
    rows, width = target.shape
    step = math.gcd(rows, max(8, 8192 // width))

    def one(index, carry):
        where = pl.ds(pl.multiple_of(index * step, step), step)
        target[where] = left[where] + right[where]
        return carry

    lax.fori_loop(0, rows // step, one, 0)


def greet(place, count, others=()):
    barrier = pltpu.get_barrier_semaphore()
    below, above = {"mp": place - 1}, {"mp": place + 1}

    @pl.when(place > 0)
    def _():
        pl.semaphore_signal(barrier, inc=1, device_id=below, device_id_type=MESH_ID)

    @pl.when(place < count - 1)
    def _():
        pl.semaphore_signal(barrier, inc=1, device_id=above, device_id_type=MESH_ID)

    for other in others:
        pl.semaphore_signal(barrier, inc=1, device_id=other, device_id_type=MESH_ID)
    inside = jnp.logical_and(place > 0, place < count - 1)

    @pl.when(inside)
    def _():
        pl.semaphore_wait(barrier, 2 + len(others))

    @pl.when(jnp.logical_not(inside))
    def _():
        pl.semaphore_wait(barrier, 1 + len(others))


def line_sum_kernel(count, count_dp, extra, part_ref, base_ref, *refs):
    items, out_ref, outs = refs[:extra], refs[extra], refs[extra + 1 : 2 * extra + 1]
    inner, from_away, from_toward = refs[2 * extra + 1 : 2 * extra + 4]
    toward_send, away_send, away_recv, toward_recv = refs[2 * extra + 4 : 2 * extra + 8]
    sums = PieceSums(count_dp, items, outs, refs[2 * extra + 8 :])
    place = lax.axis_index("mp")
    half = count // 2
    low_side = place < half
    toward = {"mp": jnp.where(low_side, place + 1, place - 1)}
    away = {"mp": jnp.where(low_side, place - 1, place + 1)}
    middle = jnp.logical_or(place == half - 1, place == half)
    outermost = jnp.logical_or(place == 0, place == count - 1)
    chunks = toward_send.shape[0]
    rows = part_ref.shape[0] // chunks
    greet(place, count, sums.peers())
    sums.begin()

    def window(step):
        return pl.ds(pl.multiple_of(step * rows, rows), rows)

    def push(step, source, inside):
        target = from_toward if inside else from_away
        recv = toward_recv if inside else away_recv
        return remote(
            source.at[window(step)],
            target.at[window(step)],
            toward_send.at[step],
            recv.at[step],
            toward,
        )

    def back(step, source):
        return remote(
            source.at[window(step)],
            from_toward.at[window(step)],
            away_send.at[step],
            toward_recv.at[step],
            away,
        )

    def gather_in(step):
        push(step, part_ref, False).wait_recv()
        inner[window(step)] = part_ref[window(step)] + from_away[window(step)]

    @pl.when(outermost)
    def _():
        def leave(step, carry):
            push(step, part_ref, False).start()
            return carry

        lax.fori_loop(0, chunks, leave, 0)

        def arrive(step, carry):
            push(step, part_ref, True).wait_recv()
            out_ref[window(step)] = from_toward[window(step)] + base_ref[window(step)]
            push(step, part_ref, False).wait_send()
            return carry

        for low, high, phase in sums.moments(chunks):
            lax.fori_loop(low, high, arrive, 0)
            sums.advance(phase)

    lag = 2

    @pl.when(middle)
    def _():
        def finish(step):
            push(step, inner, True).wait_recv()
            push(step, inner, True).wait_send()
            total = inner[window(step)] + from_toward[window(step)]
            inner[window(step)] = total
            back(step, inner).start()
            out_ref[window(step)] = total + base_ref[window(step)]

        def first(step, carry):
            gather_in(step)
            push(step, inner, True).start()
            return carry

        def both(step, carry):
            first(step, carry)
            finish(step - lag)
            return carry

        def last(step, carry):
            finish(step)
            return carry

        def drain(step, carry):
            back(step, inner).wait_send()
            return carry

        lax.fori_loop(0, lag, first, 0)
        for low, high, phase in sums.moments(chunks):
            lax.fori_loop(max(low, lag), high, both, 0)
            if high == chunks:
                lax.fori_loop(chunks - lag, chunks, last, 0)
            sums.advance(phase)
        lax.fori_loop(0, chunks, drain, 0)

    if count > 4:

        @pl.when(jnp.logical_not(jnp.logical_or(middle, outermost)))
        def _():
            def inwards(step, carry):
                gather_in(step)
                push(step, inner, False).start()
                return carry

            def outwards(step, carry):
                push(step, inner, True).wait_recv()
                back(step, from_toward).start()
                out_ref[window(step)] = from_toward[window(step)] + base_ref[window(step)]
                return carry

            def drain(step, carry):
                push(step, inner, False).wait_send()
                back(step, from_toward).wait_send()
                return carry

            lax.fori_loop(0, chunks, inwards, 0)
            for low, high, phase in sums.moments(chunks):
                lax.fori_loop(low, high, outwards, 0)
                sums.advance(phase)
            lax.fori_loop(0, chunks, drain, 0)

    sums.finish()


def piece_shapes(items):
    count = lax.axis_size("dp")
    items = [item.reshape(count, -1, item.shape[-1]) for item in items]
    shapes = [item.shape[1:] for item in items]
    return items, shapes, [jax.ShapeDtypeStruct(shape, jnp.float32) for shape in shapes]


def line_sum(part, base, call_id, items=()):
    shape = part.shape
    items, shapes, shares = piece_shapes(items)
    extra = len(items)
    part = part.reshape(-1, shape[-1])
    rows, width = part.shape
    buffer = pltpu.VMEM((rows, width), jnp.float32)
    sems = pltpu.SemaphoreType.DMA((CHUNKS,))
    results = pl.pallas_call(
        partial(line_sum_kernel, lax.axis_size("mp"), lax.axis_size("dp"), extra),
        out_shape=[jax.ShapeDtypeStruct((rows, width), jnp.float32)] + shares,
        in_specs=[VMEM_SPEC] * (2 + extra),
        out_specs=[VMEM_SPEC] * (1 + extra),
        scratch_shapes=[buffer] * 3
        + [sems] * 4
        + PieceSums.scratch(lax.axis_size("dp"), shapes),
        compiler_params=pltpu.CompilerParams(
            collective_id=call_id, has_side_effects=True, vmem_limit_bytes=VMEM_LIMIT
        ),
        cost_estimate=pl.CostEstimate(
            flops=4 * rows * width, bytes_accessed=350 * rows * width, transcendentals=0
        ),
    )(part, base.reshape(part.shape), *items)
    return results[0].reshape(shape), results[1:]


def line_scatter_kernel(
    count, part_ref, out_ref, up_acc, down_acc, from_below, from_above, up_send, down_send, up_recv, down_recv
):
    place = lax.axis_index("mp")
    steps = up_send.shape[1]
    block = part_ref.shape[0] // count
    rows = block // steps
    below, above = {"mp": place - 1}, {"mp": place + 1}
    greet(place, count)

    def window(owner, step):
        return pl.ds(pl.multiple_of(owner * block + step * rows, rows), rows)

    def up(owner, step, source):
        where = window(owner, step)
        return remote(
            source.at[where], from_below.at[where], up_send.at[owner, step], up_recv.at[owner, step], above
        )

    def down(owner, step, source):
        where = window(owner, step)
        return remote(
            source.at[where], from_above.at[where], down_send.at[owner, step], down_recv.at[owner, step], below
        )

    def up_turn(index):
        owner, step = count - 1 - index // steps, lax.rem(index, steps)

        @pl.when(jnp.logical_and(owner > place, place == 0))
        def _():
            up(owner, step, part_ref).start()

        @pl.when(jnp.logical_and(owner > place, place > 0))
        def _():
            up(owner, step, part_ref).wait_recv()
            where = window(owner, step)
            up_acc[where] = part_ref[where] + from_below[where]
            up(owner, step, up_acc).start()

    def down_turn(index):
        owner, step = index // steps, lax.rem(index, steps)

        @pl.when(jnp.logical_and(owner < place, place == count - 1))
        def _():
            down(owner, step, part_ref).start()

        @pl.when(jnp.logical_and(owner < place, place < count - 1))
        def _():
            down(owner, step, part_ref).wait_recv()
            where = window(owner, step)
            down_acc[where] = part_ref[where] + from_above[where]
            down(owner, step, down_acc).start()

    turns, lag = count * steps, steps

    def staggered(first, second):
        def begin(index, carry):
            first(index)
            return carry

        def both(index, carry):
            first(index)
            second(index - lag)
            return carry

        def end(index, carry):
            second(index)
            return carry

        lax.fori_loop(0, lag, begin, 0)
        lax.fori_loop(lag, turns, both, 0)
        lax.fori_loop(turns - lag, turns, end, 0)

    @pl.when(place < count // 2)
    def _():
        staggered(up_turn, down_turn)

    @pl.when(place >= count // 2)
    def _():
        staggered(down_turn, up_turn)

    def settle(step, carry):
        where = window(place, step)
        mine = pl.ds(pl.multiple_of(step * rows, rows), rows)
        out_ref[mine] = part_ref[where]

        @pl.when(place > 0)
        def _():
            up(place, step, part_ref).wait_recv()
            out_ref[mine] += from_below[where]

        @pl.when(place < count - 1)
        def _():
            down(place, step, part_ref).wait_recv()
            out_ref[mine] += from_above[where]

        return carry

    lax.fori_loop(0, steps, settle, 0)

    def drain(index, carry):
        owner, step = index // steps, lax.rem(index, steps)

        @pl.when(owner > place)
        def _():
            up(owner, step, part_ref).wait_send()

        @pl.when(owner < place)
        def _():
            down(owner, step, part_ref).wait_send()

        return carry

    lax.fori_loop(0, count * steps, drain, 0)


def line_scatter(part, call_id):
    rows, width = part.shape
    count = lax.axis_size("mp")
    steps = 8
    buffer = pltpu.VMEM((rows, width), jnp.float32)
    sems = pltpu.SemaphoreType.DMA((count, steps))
    return pl.pallas_call(
        partial(line_scatter_kernel, count),
        out_shape=jax.ShapeDtypeStruct((rows // count, width), jnp.float32),
        in_specs=[VMEM_SPEC],
        out_specs=VMEM_SPEC,
        scratch_shapes=[buffer] * 4 + [sems] * 4,
        compiler_params=pltpu.CompilerParams(
            collective_id=call_id, has_side_effects=True, vmem_limit_bytes=24 << 20
        ),
        cost_estimate=pl.CostEstimate(
            flops=2 * rows * width, bytes_accessed=230 * rows * width, transcendentals=0
        ),
    )(part)


def line_gather_kernel(count, count_dp, extra, own_ref, *refs):
    items, out_ref, outs = refs[:extra], refs[extra], refs[extra + 1 : 2 * extra + 1]
    up_send, down_send, up_recv, down_recv = refs[2 * extra + 1 : 2 * extra + 5]
    sums = PieceSums(count_dp, items, outs, refs[2 * extra + 5 :])
    place = lax.axis_index("mp")
    steps = up_send.shape[1]
    block = own_ref.shape[0]
    rows = block // steps
    below, above = {"mp": place - 1}, {"mp": place + 1}
    greet(place, count, sums.peers())
    sums.begin()

    def window(owner, step):
        return pl.ds(pl.multiple_of(owner * block + step * rows, rows), rows)

    def up(owner, step):
        part = out_ref.at[window(owner, step)]
        return remote(part, part, up_send.at[owner, step], up_recv.at[owner, step], above)

    def down(owner, step):
        part = out_ref.at[window(owner, step)]
        return remote(part, part, down_send.at[owner, step], down_recv.at[owner, step], below)

    def begin(step, carry):
        out_ref[window(place, step)] = own_ref[pl.ds(pl.multiple_of(step * rows, rows), rows)]

        @pl.when(place < count - 1)
        def _():
            up(place, step).start()

        @pl.when(place > 0)
        def _():
            down(place, step).start()

        return carry

    lax.fori_loop(0, steps, begin, 0)

    def pass_on(index, carry):
        away, step = 1 + index // steps, lax.rem(index, steps)

        @pl.when(place - away >= 0)
        def _():
            up(place - away, step).wait_recv()

        @pl.when(jnp.logical_and(place - away >= 0, place < count - 1))
        def _():
            up(place - away, step).start()

        @pl.when(place + away < count)
        def _():
            down(place + away, step).wait_recv()

        @pl.when(jnp.logical_and(place + away < count, place > 0))
        def _():
            down(place + away, step).start()

        return carry

    for low, high, phase in sums.moments((count - 1) * steps):
        lax.fori_loop(low, high, pass_on, 0)
        sums.advance(phase)

    def drain(index, carry):
        owner, step = index // steps, lax.rem(index, steps)

        @pl.when(jnp.logical_and(owner <= place, place < count - 1))
        def _():
            up(owner, step).wait_send()

        @pl.when(jnp.logical_and(owner >= place, place > 0))
        def _():
            down(owner, step).wait_send()

        return carry

    lax.fori_loop(0, count * steps, drain, 0)
    sums.finish()


def line_gather(own, call_id, items=()):
    rows, width = own.shape
    count = lax.axis_size("mp")
    steps = 8
    sems = pltpu.SemaphoreType.DMA((count, steps))
    items, shapes, shares = piece_shapes(items)
    extra = len(items)
    results = pl.pallas_call(
        partial(line_gather_kernel, count, lax.axis_size("dp"), extra),
        out_shape=[jax.ShapeDtypeStruct((rows * count, width), jnp.float32)] + shares,
        in_specs=[VMEM_SPEC] * (1 + extra),
        out_specs=[VMEM_SPEC] * (1 + extra),
        scratch_shapes=[sems] * 4 + PieceSums.scratch(lax.axis_size("dp"), shapes),
        compiler_params=pltpu.CompilerParams(
            collective_id=call_id, has_side_effects=True, vmem_limit_bytes=VMEM_LIMIT
        ),
        cost_estimate=pl.CostEstimate(
            flops=rows * width, bytes_accessed=250 * rows * width * count, transcendentals=0
        ),
    )(own, *items)
    return results[0], results[1:]


def piece_sums_kernel(count_dp, extra, *refs):
    sums = PieceSums(count_dp, refs[:extra], refs[extra : 2 * extra], refs[2 * extra :])
    barrier = pltpu.get_barrier_semaphore()
    for other in sums.peers():
        pl.semaphore_signal(barrier, inc=1, device_id=other, device_id_type=MESH_ID)
    pl.semaphore_wait(barrier, len(sums.peers()))
    sums.begin()
    for phase in range(1, sums.bits + 1):
        sums.advance(phase)
    sums.finish()


def piece_sums(items, call_id):
    items, shapes, shares = piece_shapes(items)
    return pl.pallas_call(
        partial(piece_sums_kernel, lax.axis_size("dp"), len(items)),
        out_shape=shares,
        in_specs=[VMEM_SPEC] * len(items),
        out_specs=[VMEM_SPEC] * len(items),
        scratch_shapes=PieceSums.scratch(lax.axis_size("dp"), shapes),
        compiler_params=pltpu.CompilerParams(
            collective_id=call_id, has_side_effects=True, vmem_limit_bytes=VMEM_LIMIT
        ),
    )(*items)


def mesh_sum_kernel(axes, tile_ref, out_ref, held, send_sem, recv_sem):
    barrier = pltpu.get_barrier_semaphore()
    places = {name: lax.axis_index(name) for name, _ in axes}

    def peer(name, count, step):
        return {name: lax.rem(places[name] + step, count)}

    for name, count in axes:

        def greet(step, carry, name=name, count=count):
            pl.semaphore_signal(
                barrier, inc=1, device_id=peer(name, count, step), device_id_type=MESH_ID
            )
            return carry

        lax.fori_loop(1, count, greet, 0)
    pl.semaphore_wait(barrier, sum(count - 1 for _, count in axes))
    value = tile_ref[...]
    first = 0
    for name, count in axes:
        place = places[name]
        held[first + place] = value

        def copy(step, slot, name=name, count=count, first=first, place=place):
            return remote(
                held.at[first + place],
                held.at[first + slot],
                send_sem.at[first + step],
                recv_sem.at[first + slot],
                peer(name, count, step),
            )

        def send(step, carry, copy=copy, place=place):
            copy(step, place).start()
            return carry

        def take(step, carry, copy=copy, count=count, place=place):
            copy(step, lax.rem(place + step, count)).wait_recv()
            return carry

        def add(slot, carry, first=first):
            return carry + held[first + slot]

        def drain(step, carry, copy=copy, place=place):
            copy(step, place).wait_send()
            return carry

        lax.fori_loop(1, count, send, 0)
        lax.fori_loop(1, count, take, 0)
        value = lax.fori_loop(1, count, add, held[first])
        lax.fori_loop(1, count, drain, 0)
        first += count
    out_ref[...] = value


def mesh_sum(tile, names, call_id):
    axes = [(name, lax.axis_size(name)) for name in names]
    slots = sum(count for _, count in axes)
    return pl.pallas_call(
        partial(mesh_sum_kernel, axes),
        out_shape=jax.ShapeDtypeStruct(tile.shape, jnp.float32),
        in_specs=[VMEM_SPEC],
        out_specs=VMEM_SPEC,
        scratch_shapes=[
            pltpu.VMEM((slots,) + tile.shape, jnp.float32),
            pltpu.SemaphoreType.DMA((slots,)),
            pltpu.SemaphoreType.DMA((slots,)),
        ],
        compiler_params=pltpu.CompilerParams(collective_id=call_id, has_side_effects=True),
    )(tile)


def adam_update(master, first, second, gradient, scale):
    clipped = gradient * scale
    moment = adam_beta * first + (1.0 - adam_beta) * clipped
    square = adam_beta * second + (1.0 - adam_beta) * clipped * clipped
    fixed_first = moment / (1.0 - adam_beta**STEP)
    fixed_second = square / (1.0 - adam_beta**STEP)
    updated = master - learning_rate * (
        fixed_first / (jnp.sqrt(fixed_second) + adam_eps) + weight_decay * master
    )
    return (updated, moment, square)


def body(
    clean_patches,
    noise_patches,
    timesteps,
    present_mask,
    copy_widein,
    copy_narrowin,
    copy_wideout,
    copy_narrowout,
    copy_latents,
    copy_gains,
    copy_pixels,
    master_widein,
    first_widein,
    second_widein,
    master_narrowin,
    first_narrowin,
    second_narrowin,
    master_wideout,
    first_wideout,
    second_wideout,
    master_narrowout,
    first_narrowout,
    second_narrowout,
    master_latents,
    first_latents,
    second_latents,
    master_gains,
    first_gains,
    second_gains,
    master_pixels,
    first_pixels,
    second_pixels,
):
    images = clean_patches.shape[0]
    patches = clean_patches.shape[2]
    count_mp, count_dp = lax.axis_size("mp"), lax.axis_size("dp")
    mp_index, dp_index = lax.axis_index("mp"), lax.axis_index("dp")
    lead = (mp_index == 0).astype(jnp.float32)
    latents, d_lat = copy_latents.shape
    d_if = copy_gains.shape[1]
    local = copy_widein.shape[2]
    sharers = max(1, count_mp // images)
    own_images = max(1, images // count_mp)
    own_patches, own_latents = patches // sharers, latents // sharers
    first_image = mp_index * own_images // sharers
    share = lax.rem(mp_index, sharers)

    def dp_piece(values, axis):
        size = values.shape[axis] // count_dp
        return lax.dynamic_slice_in_dim(values, dp_index * size, size, axis).astype(jnp.float32)

    key_piece = dp_piece(copy_widein[:, 8], 0)
    value_piece = dp_piece(copy_widein[:, 9], 0)
    query_piece = dp_piece(copy_narrowin[:, 2], 0)
    out_piece = dp_piece(copy_narrowout, 1).T
    gathered = lax.all_gather(
        jnp.concatenate([key_piece, value_piece, query_piece, out_piece], 0), "mp"
    )
    gathered = lax.all_gather(gathered, "dp")
    nothing = jnp.where(timesteps[0] > 0, 0.0, -0.0)
    gathered = gathered + nothing
    edges = [0, d_lat, 2 * d_lat, 2 * d_lat + d_if, 2 * d_lat + 2 * d_if]
    write_key_weight, write_value_weight, write_query_weight, write_out_weight = (
        jnp.swapaxes(gathered[:, :, low // count_dp : high // count_dp], 1, 2)
        .reshape(high - low, count_mp * local)
        .astype(jnp.bfloat16)
        for low, high in zip(edges[:-1], edges[1:])
    )

    signal = jnp.cos(0.5 * math.pi * (timesteps.astype(jnp.float32) + 0.5) / NSTEPS) ** 2
    noisy = (
        jnp.sqrt(signal)[:, None, None] * clean_patches
        + jnp.sqrt(1.0 - signal)[:, None, None] * noise_patches
    )
    loss_weight = 0.5 + signal
    keep_float = present_mask.astype(jnp.float32)
    weight_here = jnp.sum(loss_weight * PIX * jnp.sum(keep_float, 1))
    weight_total = mesh_sum(jnp.full((8, 128), weight_here), ("dp",), 1)[0, 0]
    gain_rows = copy_gains.astype(jnp.float32)

    def wide_gain(index):
        return gain_rows[2 * index : 2 * index + 2].reshape(-1)

    pixel_rows = copy_pixels.astype(jnp.float32)
    interface = jnp.einsum("bcp,cd->bpd", noisy, pixel_rows[0], precision=precise) + positions(
        noisy.shape[2], pixel_rows.shape[2]
    )
    latent_zero = copy_latents.astype(jnp.float32)
    read_norm, read_stats = layer_norm(latent_zero, wide_gain(0))
    read_low = read_norm.astype(jnp.bfloat16)
    side_norm, side_stats = layer_norm(interface, gain_rows[8])
    side_low = side_norm.astype(jnp.bfloat16)
    read_query = jnp.einsum(
        "ld,dc->lc", read_low, copy_widein[:, 0], preferred_element_type=jnp.float32
    ).astype(jnp.bfloat16)
    read_query = jnp.broadcast_to(read_query[None], (images,) + read_query.shape)
    read_key = jnp.einsum(
        "bpd,dc->bpc", side_low, copy_narrowin[:, 0], preferred_element_type=jnp.float32
    ).astype(jnp.bfloat16)
    read_value = jnp.einsum(
        "bpd,dc->bpc", side_low, copy_narrowin[:, 1], preferred_element_type=jnp.float32
    ).astype(jnp.bfloat16)
    read_out, read_total = attend_forward(read_query, read_key, read_value, present_mask)
    latent_one = line_sum(
        jnp.einsum("blc,cd->bld", read_out, copy_wideout[0], preferred_element_type=jnp.float32),
        jnp.broadcast_to(latent_zero[None], (images, latents, d_lat)),
        2,
    )[0]
    self_norm, self_stats = layer_norm(latent_one, wide_gain(1))
    self_low = self_norm.astype(jnp.bfloat16)
    self_triple = jnp.einsum(
        "bld,dsc->blsc", self_low, copy_widein[:, 1:4], preferred_element_type=jnp.float32
    ).astype(jnp.bfloat16)
    self_out, self_total = attend_forward(
        self_triple[:, :, 0], self_triple[:, :, 1], self_triple[:, :, 2], None
    )
    latent_two = line_sum(
        jnp.einsum("blc,cd->bld", self_out, copy_wideout[1], preferred_element_type=jnp.float32),
        latent_one,
        3,
    )[0]
    feed_norm, feed_stats = layer_norm(latent_two, wide_gain(2))
    feed_low = feed_norm.astype(jnp.bfloat16)
    hidden = jnp.einsum(
        "bld,dsc->blsc", feed_low, copy_widein[:, 4:8], preferred_element_type=jnp.float32
    )
    active, gelu_pull = jax.vjp(partial(jax.nn.gelu, approximate=False), hidden)
    active_low = active.astype(jnp.bfloat16)
    feed_partial = jnp.einsum(
        "blsc,scd->bld", active_low, copy_wideout[2:6], preferred_element_type=jnp.float32
    )

    def own_rows(values):
        values = values.reshape((images * sharers, own_latents) + values.shape[2:])
        return lax.dynamic_slice_in_dim(values, mp_index * own_images, own_images, 0)

    latent_three = own_rows(latent_two) + line_scatter(
        feed_partial.reshape(-1, d_lat), 4
    ).reshape(own_images, own_latents, d_lat)
    write_norm, write_stats = layer_norm(latent_three, wide_gain(3))
    write_low = write_norm.astype(jnp.bfloat16)

    def own_tokens(values, axis):
        values = lax.dynamic_slice_in_dim(values, first_image, own_images, 0)
        return lax.dynamic_slice_in_dim(values, share * own_patches, own_patches, axis)

    own_interface = own_tokens(interface, 1)
    own_noisy, own_noise = own_tokens(noisy, 2), own_tokens(noise_patches, 2)
    own_keep = own_tokens(keep_float, 1)
    own_weight = lax.dynamic_slice_in_dim(loss_weight, first_image, own_images, 0)

    outer_norm, outer_stats = layer_norm(own_interface, gain_rows[9])
    outer_low = outer_norm.astype(jnp.bfloat16)

    def join(spec, values, weight):
        product = jnp.einsum(spec, values, weight, preferred_element_type=jnp.float32)
        return product.astype(jnp.bfloat16)

    def image_rows(values):
        if sharers == 1:
            return values
        whole = lax.all_gather(values.astype(jnp.float32), "mp", axis=0, tiled=True)
        whole = whole + nothing
        whole = whole.reshape(images, latents, d_lat).astype(jnp.bfloat16)
        return lax.dynamic_slice_in_dim(whole, first_image, own_images, 0)

    write_query = join("bpd,dc->bpc", outer_low, write_query_weight)
    write_key = image_rows(join("bld,dc->blc", write_low, write_key_weight))
    write_value = image_rows(join("bld,dc->blc", write_low, write_value_weight))
    write_out, write_total = attend_forward(write_query, write_key, write_value, None)
    outer = own_interface + jnp.einsum(
        "bpc,dc->bpd", write_out, write_out_weight, preferred_element_type=jnp.float32
    )
    final_norm, final_stats = layer_norm(outer, gain_rows[10])
    final_low = final_norm.astype(jnp.bfloat16)
    predicted = jnp.einsum(
        "bpd,cd->bcp", final_low, copy_pixels[1], preferred_element_type=jnp.float32
    )
    difference = predicted - own_noise
    masked = own_weight[:, None, None] * own_keep[:, None, :] * difference
    loss_local = jnp.sum(masked * difference)
    predict_grad = (2.0 * masked / weight_total).astype(jnp.bfloat16)
    head_grad = jnp.einsum(
        "bcp,bpd->cd", predict_grad, final_low, preferred_element_type=jnp.float32
    )
    final_grad = jnp.einsum(
        "bcp,cd->bpd", predict_grad, copy_pixels[1], preferred_element_type=jnp.float32
    )
    outer_grad, gain_final = norm_back(final_grad, gain_rows[10], final_stats)
    branch_low = outer_grad.astype(jnp.bfloat16)
    narrowout_grad = jnp.einsum(
        "bpd,bpc->dc", branch_low, write_out, preferred_element_type=jnp.float32
    )
    write_upstream = join("bpd,dc->bpc", branch_low, write_out_weight)
    query_grad, key_grad, value_grad = attend_back(
        write_query, write_key, write_value, None, write_total, write_upstream
    )
    write_query_grad = jnp.einsum(
        "bpd,bpc->dc", outer_low, query_grad, preferred_element_type=jnp.float32
    )
    outer_part = jnp.einsum(
        "bpc,dc->bpd", query_grad, write_query_weight, preferred_element_type=jnp.float32
    )

    def row_grad(values):
        if sharers > 1:
            whole = jnp.zeros((images, latents, d_lat), jnp.float32)
            whole = lax.dynamic_update_slice_in_dim(whole, values, first_image, 0)
            values = lax.psum_scatter(
                whole.reshape(images * sharers, own_latents, d_lat),
                "mp",
                scatter_dimension=0,
                tiled=True,
            )
        return values.astype(jnp.bfloat16)

    key_grad, value_grad = row_grad(key_grad), row_grad(value_grad)
    write_key_grad = jnp.einsum(
        "bld,blc->dc", write_low, key_grad, preferred_element_type=jnp.float32
    )
    write_value_grad = jnp.einsum(
        "bld,blc->dc", write_low, value_grad, preferred_element_type=jnp.float32
    )
    write_part = jnp.einsum(
        "blc,dc->bld", key_grad, write_key_weight, preferred_element_type=jnp.float32
    ) + jnp.einsum(
        "blc,dc->bld", value_grad, write_value_weight, preferred_element_type=jnp.float32
    )
    own_grad, gain_write = norm_back(write_part, wide_gain(3), write_stats)
    outer_back, gain_outer = norm_back(outer_part, gain_rows[9], outer_stats)

    latent_grad, (key_share, query_share) = line_gather(
        own_grad.reshape(-1, d_lat), 5, [write_key_grad, write_query_grad]
    )
    latent_grad = latent_grad.reshape(latent_one.shape)
    outer_back, gain_outer = norm_back(outer_part, gain_rows[9], outer_stats)

    branch_low = latent_grad.astype(jnp.bfloat16)
    down_grad = [
        jnp.einsum(
            "bld,blc->dc", branch_low, active_low[:, :, slot], preferred_element_type=jnp.float32
        )
        for slot in range(4)
    ]
    active_grad = jnp.einsum(
        "bld,scd->blsc", branch_low, copy_wideout[2:6], preferred_element_type=jnp.float32
    )
    hidden_grad = gelu_pull(active_grad)[0].astype(jnp.bfloat16)
    up_grad = [
        jnp.einsum(
            "bld,blc->dc", feed_low, hidden_grad[:, :, slot], preferred_element_type=jnp.float32
        )
        for slot in range(4)
    ]
    feed_part = jnp.einsum(
        "blsc,dsc->bld", hidden_grad, copy_widein[:, 4:8], preferred_element_type=jnp.float32
    )
    latent_part, gain_feed = norm_back(feed_part, wide_gain(2), feed_stats)
    latent_grad, five_shares = line_sum(
        latent_part, latent_grad, 6, [write_value_grad, narrowout_grad] + up_grad[:2]
    )
    branch_low = latent_grad.astype(jnp.bfloat16)
    self_out_grad = jnp.einsum(
        "bld,blc->dc", branch_low, self_out, preferred_element_type=jnp.float32
    )
    self_upstream = jnp.einsum(
        "bld,cd->blc", branch_low, copy_wideout[1], preferred_element_type=jnp.float32
    ).astype(jnp.bfloat16)
    triple_grad = [
        item.astype(jnp.bfloat16)
        for item in attend_back(
            self_triple[:, :, 0],
            self_triple[:, :, 1],
            self_triple[:, :, 2],
            None,
            self_total,
            self_upstream,
        )
    ]
    self_in_grad = [
        jnp.einsum("bld,blc->dc", self_low, item, preferred_element_type=jnp.float32)
        for item in triple_grad
    ]
    self_part = jnp.einsum(
        "blsc,dsc->bld",
        jnp.stack(triple_grad, 2),
        copy_widein[:, 1:4],
        preferred_element_type=jnp.float32,
    )
    latent_part, gain_self = norm_back(self_part, wide_gain(1), self_stats)
    latent_grad, six_shares = line_sum(
        latent_part, latent_grad, 7, up_grad[2:] + down_grad + self_in_grad[:2]
    )
    write_share = jnp.concatenate([key_share, five_shares[0], query_share, five_shares[1]], 0)
    write_share = lax.optimization_barrier((write_share, latent_grad))[0]
    write_share = lax.psum_scatter(write_share, "mp", scatter_dimension=1, tiled=True)
    branch_low = latent_grad.astype(jnp.bfloat16)
    read_out_grad = jnp.einsum(
        "bld,blc->dc", branch_low, read_out, preferred_element_type=jnp.float32
    )
    read_upstream = jnp.einsum(
        "bld,cd->blc", branch_low, copy_wideout[0], preferred_element_type=jnp.float32
    ).astype(jnp.bfloat16)
    query_grad, key_grad, value_grad = (
        item.astype(jnp.bfloat16)
        for item in attend_back(
            read_query, read_key, read_value, present_mask, read_total, read_upstream
        )
    )
    read_query_grad = jnp.einsum(
        "ld,blc->dc", read_low, query_grad, preferred_element_type=jnp.float32
    )
    read_part = jnp.einsum(
        "blc,dc->bld", query_grad, copy_widein[:, 0], preferred_element_type=jnp.float32
    )
    normed, scale = read_stats
    latent_part, gain_read = norm_back(
        read_part, wide_gain(0), (normed[None], scale[None])
    )
    latent_total = jnp.sum(lead * latent_grad + latent_part, 0)
    read_key_grad = jnp.einsum(
        "bpd,bpc->dc", side_low, key_grad, preferred_element_type=jnp.float32
    )
    read_value_grad = jnp.einsum(
        "bpd,bpc->dc", side_low, value_grad, preferred_element_type=jnp.float32
    )
    side_part = jnp.einsum(
        "bpc,dc->bpd", key_grad, copy_narrowin[:, 0], preferred_element_type=jnp.float32
    ) + jnp.einsum(
        "bpc,dc->bpd", value_grad, copy_narrowin[:, 1], preferred_element_type=jnp.float32
    )
    side_back, gain_side = norm_back(side_part, gain_rows[8], side_stats)
    embed_grad = jnp.einsum("bcp,bpd->cd", noisy, side_back, precision=precise) + jnp.einsum(
        "bcp,bpd->cd", own_noisy, outer_grad + outer_back, precision=precise
    )
    gains_grad = jnp.concatenate(
        [
            gain_read.reshape(2, -1),
            gain_self.reshape(2, -1),
            gain_feed.reshape(2, -1),
            gain_write.reshape(2, -1),
            gain_side[None],
            gain_outer[None],
            gain_final[None],
        ],
        0,
    )

    def dp_columns(values):
        values = values.reshape(-1, count_dp, values.shape[-1] // count_dp)
        return jnp.swapaxes(values, 0, 1).reshape(count_dp, -1)

    small_parts = [
        dp_columns(item)
        for item in (latent_total, gains_grad, embed_grad, head_grad)
    ]
    small_sizes = [item.shape[1] for item in small_parts]
    small = jnp.concatenate(small_parts, 1)
    fill = -small.shape[1] % (16 * local)
    small = jnp.pad(small, ((0, 0), (0, fill))).reshape(-1, local)
    last_shares = piece_sums(
        [
            self_in_grad[2],
            self_out_grad,
            read_query_grad,
            read_key_grad,
            read_value_grad,
            read_out_grad,
            small,
        ],
        9,
    )
    lat_rows, if_rows = d_lat // count_dp, d_if // count_dp
    small_share = mesh_sum(last_shares[6], ("mp",), 10)
    small_flat = small_share.reshape(-1)
    latents_grad, gains_grad, embed_grad, head_grad = (
        small_flat[sum(small_sizes[:i]) : sum(small_sizes[: i + 1])].reshape(rows, -1)
        for i, rows in enumerate((latents, gains_grad.shape[0], PIX, PIX))
    )
    pixels_grad = jnp.stack([embed_grad, head_grad], 0)

    def cut(share, index, rows, start=0):
        return share[start + index * rows : start + (index + 1) * rows]

    widein_grad = jnp.stack(
        [last_shares[2], six_shares[6], six_shares[7], last_shares[0]]
        + list(five_shares[2:])
        + list(six_shares[:2])
        + [cut(write_share, i, lat_rows) for i in range(2)],
        1,
    )
    narrowin_grad = jnp.stack(
        [last_shares[3], last_shares[4], cut(write_share, 0, if_rows, 2 * lat_rows)], 1
    )
    wideout_grad = jnp.stack(
        [last_shares[5].T, last_shares[1].T] + [item.T for item in six_shares[2:6]], 0
    )
    narrowout_grad = cut(write_share, 1, if_rows, 2 * lat_rows).T
    shares = (
        widein_grad,
        narrowin_grad,
        wideout_grad,
        narrowout_grad,
        latents_grad,
        gains_grad,
        pixels_grad,
    )
    split_square = sum((jnp.sum(item * item) for item in shares[:4]))
    copied_square = sum((jnp.sum(item * item) for item in shares[4:]))
    lane = lax.broadcasted_iota(jnp.int32, (8, 128), 1)
    totals = mesh_sum(
        jnp.where(lane == 0, split_square + lead * copied_square, loss_local), ("dp", "mp"), 8
    )
    square_total, loss_total = totals[0, 0], totals[0, 1]
    grad_norm = jnp.sqrt(square_total)
    loss_value = loss_total / weight_total
    scale = clip_level / jnp.maximum(grad_norm, clip_level)
    states = (
        (master_widein, first_widein, second_widein),
        (master_narrowin, first_narrowin, second_narrowin),
        (master_wideout, first_wideout, second_wideout),
        (master_narrowout, first_narrowout, second_narrowout),
        (master_latents, first_latents, second_latents),
        (master_gains, first_gains, second_gains),
        (master_pixels, first_pixels, second_pixels),
    )
    results = []
    for state, gradient in zip(states, shares):
        results.extend(adam_update(state[0], state[1], state[2], gradient, scale))
    return (
        loss_value,
        grad_norm,
        results[0],
        results[1],
        results[2],
        results[3],
        results[4],
        results[5],
        results[6],
        results[7],
        results[8],
        results[9],
        results[10],
        results[11],
        results[12],
        results[13],
        results[14],
        results[15],
        results[16],
        results[17],
        results[18],
        results[19],
        results[20],
    )


def solution(mesh):
    in_specs = (
        P("dp", None, None),
        P("dp", None, None),
        P("dp"),
        P("dp", None),
        P(None, None, "mp"),
        P(None, None, "mp"),
        P(None, "mp", None),
        P("mp", None),
        P(),
        P(),
        P(),
        P("dp", None, "mp"),
        P("dp", None, "mp"),
        P("dp", None, "mp"),
        P("dp", None, "mp"),
        P("dp", None, "mp"),
        P("dp", None, "mp"),
        P(None, "mp", "dp"),
        P(None, "mp", "dp"),
        P(None, "mp", "dp"),
        P("mp", "dp"),
        P("mp", "dp"),
        P("mp", "dp"),
        P(None, "dp"),
        P(None, "dp"),
        P(None, "dp"),
        P(None, "dp"),
        P(None, "dp"),
        P(None, "dp"),
        P(None, None, "dp"),
        P(None, None, "dp"),
        P(None, None, "dp"),
    )
    out_specs = (
        P(),
        P(),
        P("dp", None, "mp"),
        P("dp", None, "mp"),
        P("dp", None, "mp"),
        P("dp", None, "mp"),
        P("dp", None, "mp"),
        P("dp", None, "mp"),
        P(None, "mp", "dp"),
        P(None, "mp", "dp"),
        P(None, "mp", "dp"),
        P("mp", "dp"),
        P("mp", "dp"),
        P("mp", "dp"),
        P(None, "dp"),
        P(None, "dp"),
        P(None, "dp"),
        P(None, "dp"),
        P(None, "dp"),
        P(None, "dp"),
        P(None, None, "dp"),
        P(None, None, "dp"),
        P(None, None, "dp"),
    )
    return jax.shard_map(body, mesh=mesh, in_specs=in_specs, out_specs=out_specs, check_vma=False)
```

```python
from functools import partial
import math

import jax
import jax.numpy as jnp
from jax import lax
from jax.experimental import pallas as pl
from jax.experimental.pallas import tpu as pltpu
from jax.sharding import PartitionSpec as P

HEAD_DIM = 64
PIX = 12
NSTEPS = 1000
STEP = 10


precise = lax.Precision.HIGHEST
clip_level = 0.01
learning_rate = 0.05
weight_decay = 0.1
adam_beta = 0.5
adam_eps = 1e-08


def layer_norm(values, gain):
    centered = values - jnp.mean(values, -1, keepdims=True)
    scale = lax.rsqrt(jnp.mean(centered * centered, -1, keepdims=True) + 1e-05)
    normed = centered * scale
    return (normed * gain, (normed, scale))


def norm_back(upstream, gain, stats):
    normed, scale = stats
    inner = upstream * gain
    values = scale * (
        inner
        - jnp.mean(inner, -1, keepdims=True)
        - normed * jnp.mean(inner * normed, -1, keepdims=True)
    )
    gain_grad = jnp.sum((upstream * normed).reshape(-1, normed.shape[-1]), 0)
    return (values, gain_grad)


def positions(count, width):
    place = jnp.arange(count, dtype=jnp.float32)[:, None]
    index = jnp.arange(width // 2, dtype=jnp.float32)[None, :]
    angle = place * jnp.exp(-math.log(10000.0) * 2.0 * index / width)
    return jnp.concatenate([jnp.sin(angle), jnp.cos(angle)], -1)


def split_heads(values):
    return values.reshape(values.shape[:-1] + (values.shape[-1] // HEAD_DIM, HEAD_DIM))


def attend_scores(queries, keys, keep_mask):
    scores = jnp.einsum(
        "bqhe,bkhe->bhqk",
        split_heads(queries),
        split_heads(keys),
        preferred_element_type=jnp.float32,
    ) * HEAD_DIM ** (-0.5)
    if keep_mask is not None:
        scores = jnp.where(keep_mask[:, None, None, :] > 0, scores, -1e30)
    return scores


def attend_forward(queries, keys, values, keep_mask):
    scores = attend_scores(queries, keys, keep_mask)
    top = jnp.max(scores, -1, keepdims=True)
    log_total = top + jnp.log(jnp.sum(jnp.exp(scores - top), -1, keepdims=True))
    probs = jnp.exp(scores - log_total).astype(jnp.bfloat16)
    output = jnp.einsum(
        "bhqk,bkhe->bqhe", probs, split_heads(values), preferred_element_type=jnp.float32
    )
    return (output.reshape(queries.shape).astype(jnp.bfloat16), log_total)


def attend_back(queries, keys, values, keep_mask, log_total, upstream):
    scores = attend_scores(queries, keys, keep_mask)
    probs = jnp.exp(scores - log_total)
    value_grad = jnp.einsum(
        "bhqk,bqhe->bkhe",
        probs.astype(jnp.bfloat16),
        split_heads(upstream),
        preferred_element_type=jnp.float32,
    )
    prob_grad = jnp.einsum(
        "bqhe,bkhe->bhqk",
        split_heads(upstream),
        split_heads(values),
        preferred_element_type=jnp.float32,
    )
    score_grad = (probs * (prob_grad - jnp.sum(prob_grad * probs, -1, keepdims=True))).astype(
        jnp.bfloat16
    )
    query_grad = jnp.einsum(
        "bhqk,bkhe->bqhe", score_grad, split_heads(keys), preferred_element_type=jnp.float32
    ) * HEAD_DIM ** (-0.5)
    key_grad = jnp.einsum(
        "bhqk,bqhe->bkhe", score_grad, split_heads(queries), preferred_element_type=jnp.float32
    ) * HEAD_DIM ** (-0.5)
    return (
        query_grad.reshape(queries.shape).astype(jnp.bfloat16),
        key_grad.reshape(keys.shape),
        value_grad.reshape(values.shape),
    )


MESH_ID = pl.DeviceIdType.MESH
VMEM_SPEC = pl.BlockSpec(memory_space=pltpu.VMEM)
CHUNKS = 32
VMEM_LIMIT = 56 << 20


def remote(source, target, send_sem, recv_sem, device):
    return pltpu.make_async_remote_copy(
        src_ref=source,
        dst_ref=target,
        send_sem=send_sem,
        recv_sem=recv_sem,
        device_id=device,
        device_id_type=MESH_ID,
    )


class PieceSums:
    def __init__(self, count, items, outs, scratch):
        self.count, self.items, self.outs = count, items, outs
        self.bits = count.bit_length() - 1
        self.place = lax.axis_index("dp") if items else None
        self.held = []
        for index in range(len(items)):
            self.held.append(scratch[index * (self.bits + 2) : (index + 1) * (self.bits + 2)])

    @staticmethod
    def scratch(count, shapes):
        bits = count.bit_length() - 1
        result = []
        for rows, width in shapes:
            result.append(pltpu.VMEM((count // 2, rows, width), jnp.float32))
            for phase in range(2, bits + 1):
                result.append(
                    pltpu.VMEM((2 * (count >> phase), rows // 2, width), jnp.float32)
                )
            copies = count // 2 + 2 * sum(count >> phase for phase in range(2, bits + 1))
            result += [pltpu.SemaphoreType.DMA((copies,))] * 2
        return result

    def peers(self):
        return [{"dp": self.place ^ (1 << bit)} for bit in range(self.bits)] if self.items else []

    def order(self, half):
        later = list(range(1, self.bits))
        turn = half * (len(later) // 2)
        return later[turn:] + later[:turn]

    def first_copy(self, index, piece):
        item, held = self.items[index], self.held[index]
        other = 1 - (self.place & 1)
        return remote(
            item.at[2 * piece + other],
            held[0].at[piece],
            held[-2].at[piece],
            held[-1].at[piece],
            {"dp": self.place ^ 1},
        )

    def member(self, half, phase, entry, flip):
        bits = self.order(half)
        settled, now, rest = bits[: phase - 2], bits[phase - 2], bits[phase - 1 :]
        piece = 0
        for bit in settled:
            piece = piece | (self.place & (1 << bit))
        own = self.place & (1 << now)
        piece = piece | ((own ^ (1 << now)) if flip else own)
        for position, bit in enumerate(rest):
            if (entry >> position) & 1:
                piece = piece | (1 << bit)
        return piece >> 1

    def later_copy(self, index, half, phase, entry):
        held = self.held[index]
        rows = self.items[index].shape[1] // 2
        size = self.count >> phase
        sem = self.count // 2 + 2 * sum(self.count >> p for p in range(2, phase)) + half * size + entry
        return remote(
            held[0].at[self.member(half, phase, entry, True), pl.ds(half * rows, rows)],
            held[phase - 1].at[half * size + entry],
            held[-2].at[sem],
            held[-1].at[sem],
            {"dp": self.place ^ (1 << self.order(half)[phase - 2])},
        )

    def entries(self, phase):
        return [
            (index, half, entry)
            for index in range(len(self.items))
            for half in range(2)
            for entry in range(self.count >> phase)
        ]

    def begin(self):
        for index in range(len(self.items)):
            for piece in range(self.count // 2):
                self.first_copy(index, piece).start()

    def send(self, phase):
        for index, half, entry in self.entries(phase):
            self.later_copy(index, half, phase, entry).start()

    def advance(self, phase):
        if not self.items:
            return
        if phase == 1:
            own = self.place & 1
            for index, item in enumerate(self.items):
                total = self.held[index][0]
                for piece in range(self.count // 2):
                    self.first_copy(index, piece).wait_recv()
                    add_rows(total.at[piece], total.at[piece], item.at[2 * piece + own])
        else:
            for index, half, entry in self.entries(phase):
                self.later_copy(index, half, phase, entry).wait_recv()
                held, rows = self.held[index], self.items[index].shape[1] // 2
                where = pl.ds(half * rows, rows)
                came = held[phase - 1].at[half * (self.count >> phase) + entry]
                kept = held[0].at[self.member(half, phase, entry, False), where]
                if phase == self.bits:
                    add_rows(self.outs[index].at[where], kept, came)
                else:
                    add_rows(kept, kept, came)
        if phase < self.bits:
            self.send(phase + 1)

    def finish(self):
        for index in range(len(self.items)):
            for piece in range(self.count // 2):
                self.first_copy(index, piece).wait_send()
        for phase in range(2, self.bits + 1):
            for index, half, entry in self.entries(phase):
                self.later_copy(index, half, phase, entry).wait_send()

    def moments(self, total):
        if not self.items:
            return [(0, total, None)]
        marks, low = [], 0
        for phase in range(1, self.bits + 1):
            share = (1 - 0.5 ** (phase - 1)) / (1 - 0.5 ** (self.bits - 1))
            high = total if phase == self.bits else int(total * (0.22 + 0.78 * share))
            marks.append((low, high, phase))
            low = high
        return marks


def add_rows(target, left, right):
    rows, width = target.shape
    step = math.gcd(rows, max(8, 8192 // width))

    def one(index, carry):
        where = pl.ds(pl.multiple_of(index * step, step), step)
        target[where] = left[where] + right[where]
        return carry

    lax.fori_loop(0, rows // step, one, 0)


class Spread:
    def __init__(self, name, count, held, send_sem, recv_sem):
        self.name, self.count, self.held = name, count, held
        self.send_sem, self.recv_sem = send_sem, recv_sem
        self.place = lax.axis_index(name)

    @staticmethod
    def scratch(count, shape):
        sems = pltpu.SemaphoreType.DMA((count,))
        return [pltpu.VMEM((count,) + shape, jnp.float32), sems, sems]

    def peer(self, step):
        return {self.name: lax.rem(self.place + step, self.count)}

    def copy(self, step, slot):
        return remote(
            self.held.at[slot],
            self.held.at[slot],
            self.send_sem.at[step],
            self.recv_sem.at[slot],
            self.peer(step),
        )

    def each(self, action):
        def one(step, carry):
            action(step)
            return carry

        lax.fori_loop(1, self.count, one, 0)

    def start(self):
        self.each(lambda step: self.copy(step, self.place).start())

    def take(self):
        self.each(lambda step: self.copy(step, lax.rem(self.place + step, self.count)).wait_recv())

    def finish(self):
        self.each(lambda step: self.copy(step, self.place).wait_send())

    def total(self):
        return lax.fori_loop(
            1, self.count, lambda slot, carry: carry + self.held[slot], self.held[0]
        )


class Convert:
    def __init__(self, count_mp, steps, blocks, outs, buffer, sems):
        self.count_mp, self.blocks, self.outs = count_mp, blocks, outs
        self.buffer, self.sems = buffer, sems
        self.number = blocks.shape[0]
        self.each = -(-self.number // steps)

    @staticmethod
    def scratch(block):
        return [pltpu.VMEM((3,) + block, jnp.float32), pltpu.SemaphoreType.DMA((3,))]

    def copy(self, index):
        slot = lax.rem(index, 3)
        return pltpu.make_async_copy(
            self.blocks.at[index], self.buffer.at[slot], self.sems.at[slot]
        )

    def begin(self):
        self.copy(0).start()
        self.copy(1).start()

    def one(self, index):
        self.copy(index).wait()

        @pl.when(index + 2 < self.number)
        def _():
            self.copy(index + 2).start()

        block = self.buffer.at[lax.rem(index, 3)]
        local = block.shape[1]
        columns = pl.ds(pl.multiple_of(lax.rem(index, self.count_mp) * local, local), local)
        low = 0
        for out in self.outs:
            rows = out.shape[0] * self.count_mp // self.number
            where = pl.ds(pl.multiple_of(index // self.count_mp * rows, rows), rows)
            out[where, columns] = block[pl.ds(low, rows)].astype(jnp.bfloat16)
            low += rows

    def step(self, index):
        for entry in range(self.each):
            self.one(index * self.each + entry)


def signal_all(barrier, others):
    for other in others:
        pl.semaphore_signal(barrier, inc=1, device_id=other, device_id_type=MESH_ID)


def greet(place, count, others=()):
    barrier = pltpu.get_barrier_semaphore()
    below, above = {"mp": place - 1}, {"mp": place + 1}

    @pl.when(place > 0)
    def _():
        pl.semaphore_signal(barrier, inc=1, device_id=below, device_id_type=MESH_ID)

    @pl.when(place < count - 1)
    def _():
        pl.semaphore_signal(barrier, inc=1, device_id=above, device_id_type=MESH_ID)

    signal_all(barrier, others)
    inside = jnp.logical_and(place > 0, place < count - 1)

    @pl.when(inside)
    def _():
        pl.semaphore_wait(barrier, 2 + len(others))

    @pl.when(jnp.logical_not(inside))
    def _():
        pl.semaphore_wait(barrier, 1 + len(others))


def line_sum_kernel(count, count_dp, extra, tiled, converted, *refs):
    refs = list(refs)

    def pull(number):
        taken = refs[:number]
        del refs[:number]
        return taken

    part_ref, base_ref = pull(2)
    items, tile, blocks = pull(extra), pull(tiled), pull(min(1, converted))
    (out_ref,) = pull(1)
    outs, tile_out, wide = pull(extra), pull(tiled), pull(converted)
    inner, from_away, from_toward, toward_send, away_send, away_recv, toward_recv = pull(7)
    chunks = toward_send.shape[0]
    spread = Spread("dp", count_dp, *pull(3)) if tiled else None
    convert = Convert(count, chunks, blocks[0], wide, *pull(2)) if converted else None
    sums = PieceSums(count_dp, items, outs, refs)
    place = lax.axis_index("mp")
    half = count // 2
    low_side = place < half
    toward = {"mp": jnp.where(low_side, place + 1, place - 1)}
    away = {"mp": jnp.where(low_side, place - 1, place + 1)}
    middle = jnp.logical_or(place == half - 1, place == half)
    outermost = jnp.logical_or(place == 0, place == count - 1)
    rows = part_ref.shape[0] // chunks
    others = [spread.peer(step) for step in range(1, count_dp)] if tiled else sums.peers()
    if tiled:
        spread.held[spread.place] = tile[0][...]
    greet(place, count, others)
    if tiled:
        spread.start()
    if converted:
        convert.begin()
    sums.begin()

    def window(step):
        return pl.ds(pl.multiple_of(step * rows, rows), rows)

    def push(step, source, inside):
        target = from_toward if inside else from_away
        recv = toward_recv if inside else away_recv
        return remote(
            source.at[window(step)],
            target.at[window(step)],
            toward_send.at[step],
            recv.at[step],
            toward,
        )

    def back(step, source):
        return remote(
            source.at[window(step)],
            from_toward.at[window(step)],
            away_send.at[step],
            toward_recv.at[step],
            away,
        )

    def gather_in(step):
        push(step, part_ref, False).wait_recv()
        inner[window(step)] = part_ref[window(step)] + from_away[window(step)]

    @pl.when(outermost)
    def _():
        def leave(step, carry):
            push(step, part_ref, False).start()
            return carry

        lax.fori_loop(0, chunks, leave, 0)

        def arrive(step, carry):
            push(step, part_ref, True).wait_recv()
            out_ref[window(step)] = from_toward[window(step)] + base_ref[window(step)]
            push(step, part_ref, False).wait_send()
            if converted:
                convert.step(step)
            return carry

        for low, high, phase in sums.moments(chunks):
            lax.fori_loop(low, high, arrive, 0)
            sums.advance(phase)

    lag = 2

    @pl.when(middle)
    def _():
        def finish(step):
            push(step, inner, True).wait_recv()
            push(step, inner, True).wait_send()
            total = inner[window(step)] + from_toward[window(step)]
            inner[window(step)] = total
            back(step, inner).start()
            out_ref[window(step)] = total + base_ref[window(step)]

        def first(step, carry):
            gather_in(step)
            push(step, inner, True).start()
            if converted:
                convert.step(step)
            return carry

        def both(step, carry):
            first(step, carry)
            finish(step - lag)
            return carry

        def last(step, carry):
            finish(step)
            return carry

        def drain(step, carry):
            back(step, inner).wait_send()
            return carry

        lax.fori_loop(0, lag, first, 0)
        for low, high, phase in sums.moments(chunks):
            lax.fori_loop(max(low, lag), high, both, 0)
            if high == chunks:
                lax.fori_loop(chunks - lag, chunks, last, 0)
            sums.advance(phase)
        lax.fori_loop(0, chunks, drain, 0)

    if count > 4:

        @pl.when(jnp.logical_not(jnp.logical_or(middle, outermost)))
        def _():
            def inwards(step, carry):
                gather_in(step)
                push(step, inner, False).start()
                return carry

            def outwards(step, carry):
                push(step, inner, True).wait_recv()
                back(step, from_toward).start()
                out_ref[window(step)] = from_toward[window(step)] + base_ref[window(step)]
                if converted:
                    convert.step(step)
                return carry

            def drain(step, carry):
                push(step, inner, False).wait_send()
                back(step, from_toward).wait_send()
                return carry

            lax.fori_loop(0, chunks, inwards, 0)
            for low, high, phase in sums.moments(chunks):
                lax.fori_loop(low, high, outwards, 0)
                sums.advance(phase)
            lax.fori_loop(0, chunks, drain, 0)

    sums.finish()
    if tiled:
        spread.take()
        tile_out[0][...] = spread.total()
        spread.finish()


def room(*groups):
    total = 8 << 20
    for group in groups:
        for item in group:
            if hasattr(item, "shape") and hasattr(item, "dtype"):
                total += math.prod(item.shape) * jnp.dtype(item.dtype).itemsize
    return min(total, VMEM_LIMIT)


def room_of(scratch):
    return [
        jax.ShapeDtypeStruct(item.shape, item.dtype)
        for item in scratch
        if getattr(item, "dtype", None) in (jnp.float32, jnp.bfloat16)
    ]


def piece_shapes(items):
    count = lax.axis_size("dp")
    items = [item.reshape(count, -1, item.shape[-1]) for item in items]
    shapes = [item.shape[1:] for item in items]
    return items, shapes, [jax.ShapeDtypeStruct(shape, jnp.float32) for shape in shapes]


def line_sum(part, base, call_id, items=(), tile=None, blocks=None):
    shape = part.shape
    items, shapes, shares = piece_shapes(items)
    count, count_dp = lax.axis_size("mp"), lax.axis_size("dp")
    part = part.reshape(-1, shape[-1])
    rows, width = part.shape
    buffer = pltpu.VMEM((rows, width), jnp.float32)
    sems = pltpu.SemaphoreType.DMA((CHUNKS,))
    inputs, specs = [part, base.reshape(part.shape), *items], [VMEM_SPEC] * (2 + len(items))
    outs = [jax.ShapeDtypeStruct((rows, width), jnp.float32)] + shares
    scratch = [buffer] * 3 + [sems] * 4
    if tile is not None:
        inputs.append(tile)
        specs.append(VMEM_SPEC)
        outs.append(jax.ShapeDtypeStruct(tile.shape, jnp.float32))
        scratch += Spread.scratch(count_dp, tile.shape)
    sizes = []
    if blocks is not None:
        blocks, sizes = blocks
        outs += [
            jax.ShapeDtypeStruct((size, count * blocks.shape[2]), jnp.bfloat16) for size in sizes
        ]
        scratch += Convert.scratch(blocks.shape[1:])
    scratch += PieceSums.scratch(count_dp, shapes)
    limit = room(inputs, outs, room_of(scratch))
    if blocks is not None:
        inputs.append(blocks)
        specs.append(pl.BlockSpec(memory_space=pl.ANY))
    results = pl.pallas_call(
        partial(line_sum_kernel, count, count_dp, len(items), int(tile is not None), len(sizes)),
        out_shape=outs,
        in_specs=specs,
        out_specs=[VMEM_SPEC] * len(outs),
        scratch_shapes=scratch,
        compiler_params=pltpu.CompilerParams(
            collective_id=call_id, has_side_effects=True, vmem_limit_bytes=limit
        ),
        cost_estimate=pl.CostEstimate(
            flops=4 * rows * width, bytes_accessed=350 * rows * width, transcendentals=0
        ),
    )(*inputs)
    return results[0].reshape(shape), results[1:]


class LineScatter:
    def __init__(self, count, part, out, buffers, sems):
        self.count, self.part, self.out = count, part, out
        self.up_acc, self.down_acc, self.from_below, self.from_above = buffers
        self.up_send, self.down_send, self.up_recv, self.down_recv = sems
        self.place = lax.axis_index("mp")
        self.steps = self.up_send.shape[1]
        self.block = part.shape[0] // count
        self.rows = self.block // self.steps

    @staticmethod
    def scratch(count, shape, steps):
        sems = pltpu.SemaphoreType.DMA((count, steps))
        return [pltpu.VMEM(shape, jnp.float32)] * 4 + [sems] * 4

    def window(self, owner, step):
        return pl.ds(pl.multiple_of(owner * self.block + step * self.rows, self.rows), self.rows)

    def up(self, owner, step, source):
        where = self.window(owner, step)
        return remote(
            source.at[where],
            self.from_below.at[where],
            self.up_send.at[owner, step],
            self.up_recv.at[owner, step],
            {"mp": self.place + 1},
        )

    def down(self, owner, step, source):
        where = self.window(owner, step)
        return remote(
            source.at[where],
            self.from_above.at[where],
            self.down_send.at[owner, step],
            self.down_recv.at[owner, step],
            {"mp": self.place - 1},
        )

    def up_turn(self, index):
        place, part = self.place, self.part
        owner, step = self.count - 1 - index // self.steps, lax.rem(index, self.steps)

        @pl.when(jnp.logical_and(owner > place, place == 0))
        def _():
            self.up(owner, step, part).start()

        @pl.when(jnp.logical_and(owner > place, place > 0))
        def _():
            self.up(owner, step, part).wait_recv()
            where = self.window(owner, step)
            self.up_acc[where] = part[where] + self.from_below[where]
            self.up(owner, step, self.up_acc).start()

    def down_turn(self, index):
        place, part, count = self.place, self.part, self.count
        owner, step = index // self.steps, lax.rem(index, self.steps)

        @pl.when(jnp.logical_and(owner < place, place == count - 1))
        def _():
            self.down(owner, step, part).start()

        @pl.when(jnp.logical_and(owner < place, place < count - 1))
        def _():
            self.down(owner, step, part).wait_recv()
            where = self.window(owner, step)
            self.down_acc[where] = part[where] + self.from_above[where]
            self.down(owner, step, self.down_acc).start()

    def run(self, pause=None):
        turns, lag = self.count * self.steps, self.steps

        def staggered(first, second):
            def begin(index, carry):
                first(index)
                return carry

            def both(index, carry):
                first(index)
                second(index - lag)
                return carry

            def end(index, carry):
                second(index)
                return carry

            lax.fori_loop(0, lag, begin, 0)
            if pause is not None:
                pause()
            lax.fori_loop(lag, turns, both, 0)
            lax.fori_loop(turns - lag, turns, end, 0)

        @pl.when(self.place < self.count // 2)
        def _():
            staggered(self.up_turn, self.down_turn)

        @pl.when(self.place >= self.count // 2)
        def _():
            staggered(self.down_turn, self.up_turn)

    def settle(self):
        place, rows = self.place, self.rows

        def one(step, carry):
            where = self.window(place, step)
            mine = pl.ds(pl.multiple_of(step * rows, rows), rows)
            self.out[mine] = self.part[where]

            @pl.when(place > 0)
            def _():
                self.up(place, step, self.part).wait_recv()
                self.out[mine] += self.from_below[where]

            @pl.when(place < self.count - 1)
            def _():
                self.down(place, step, self.part).wait_recv()
                self.out[mine] += self.from_above[where]

            return carry

        lax.fori_loop(0, self.steps, one, 0)

    def finish(self):
        place = self.place

        def one(index, carry):
            owner, step = index // self.steps, lax.rem(index, self.steps)

            @pl.when(owner > place)
            def _():
                self.up(owner, step, self.part).wait_send()

            @pl.when(owner < place)
            def _():
                self.down(owner, step, self.part).wait_send()

            return carry

        lax.fori_loop(0, self.count * self.steps, one, 0)


def line_scatter_kernel(count, part_ref, out_ref, *scratch):
    scatter = LineScatter(count, part_ref, out_ref, scratch[:4], scratch[4:])
    greet(scatter.place, count)
    scatter.run()
    scatter.settle()
    scatter.finish()


def line_scatter(part, call_id):
    rows, width = part.shape
    count = lax.axis_size("mp")
    steps = 8
    return pl.pallas_call(
        partial(line_scatter_kernel, count),
        out_shape=jax.ShapeDtypeStruct((rows // count, width), jnp.float32),
        in_specs=[VMEM_SPEC],
        out_specs=VMEM_SPEC,
        scratch_shapes=LineScatter.scratch(count, (rows, width), steps),
        compiler_params=pltpu.CompilerParams(
            collective_id=call_id, has_side_effects=True, vmem_limit_bytes=24 << 20
        ),
        cost_estimate=pl.CostEstimate(
            flops=2 * rows * width, bytes_accessed=230 * rows * width, transcendentals=0
        ),
    )(part)


def line_gather_kernel(count, count_dp, extra, own_ref, *refs):
    items, out_ref, outs = refs[:extra], refs[extra], refs[extra + 1 : 2 * extra + 1]
    up_send, down_send, up_recv, down_recv = refs[2 * extra + 1 : 2 * extra + 5]
    sums = PieceSums(count_dp, items, outs, refs[2 * extra + 5 :])
    place = lax.axis_index("mp")
    steps = up_send.shape[1]
    block = own_ref.shape[0]
    rows = block // steps
    below, above = {"mp": place - 1}, {"mp": place + 1}
    greet(place, count, sums.peers())
    sums.begin()

    def window(owner, step):
        return pl.ds(pl.multiple_of(owner * block + step * rows, rows), rows)

    def up(owner, step):
        part = out_ref.at[window(owner, step)]
        return remote(part, part, up_send.at[owner, step], up_recv.at[owner, step], above)

    def down(owner, step):
        part = out_ref.at[window(owner, step)]
        return remote(part, part, down_send.at[owner, step], down_recv.at[owner, step], below)

    def begin(step, carry):
        out_ref[window(place, step)] = own_ref[pl.ds(pl.multiple_of(step * rows, rows), rows)]

        @pl.when(place < count - 1)
        def _():
            up(place, step).start()

        @pl.when(place > 0)
        def _():
            down(place, step).start()

        return carry

    lax.fori_loop(0, steps, begin, 0)

    def pass_on(index, carry):
        away, step = 1 + index // steps, lax.rem(index, steps)

        @pl.when(place - away >= 0)
        def _():
            up(place - away, step).wait_recv()

        @pl.when(jnp.logical_and(place - away >= 0, place < count - 1))
        def _():
            up(place - away, step).start()

        @pl.when(place + away < count)
        def _():
            down(place + away, step).wait_recv()

        @pl.when(jnp.logical_and(place + away < count, place > 0))
        def _():
            down(place + away, step).start()

        return carry

    for low, high, phase in sums.moments((count - 1) * steps):
        lax.fori_loop(low, high, pass_on, 0)
        sums.advance(phase)

    def drain(index, carry):
        owner, step = index // steps, lax.rem(index, steps)

        @pl.when(jnp.logical_and(owner <= place, place < count - 1))
        def _():
            up(owner, step).wait_send()

        @pl.when(jnp.logical_and(owner >= place, place > 0))
        def _():
            down(owner, step).wait_send()

        return carry

    lax.fori_loop(0, count * steps, drain, 0)
    sums.finish()


def line_gather(own, call_id, items=()):
    rows, width = own.shape
    count, count_dp = lax.axis_size("mp"), lax.axis_size("dp")
    steps = 8
    sems = pltpu.SemaphoreType.DMA((count, steps))
    items, shapes, shares = piece_shapes(items)
    extra = len(items)
    scratch = PieceSums.scratch(count_dp, shapes)
    limit = room(items, shares, room_of(scratch)) + 2 * rows * count * width * 4
    results = pl.pallas_call(
        partial(line_gather_kernel, count, count_dp, extra),
        out_shape=[jax.ShapeDtypeStruct((rows * count, width), jnp.float32)] + shares,
        in_specs=[VMEM_SPEC] * (1 + extra),
        out_specs=[VMEM_SPEC] * (1 + extra),
        scratch_shapes=[sems] * 4 + scratch,
        compiler_params=pltpu.CompilerParams(
            collective_id=call_id, has_side_effects=True, vmem_limit_bytes=limit
        ),
        cost_estimate=pl.CostEstimate(
            flops=rows * width, bytes_accessed=250 * rows * width * count, transcendentals=0
        ),
    )(own, *items)
    return results[0], results[1:]


def adam_update(master, first, second, gradient, scale):
    clipped = gradient * scale
    moment = adam_beta * first + (1.0 - adam_beta) * clipped
    square = adam_beta * second + (1.0 - adam_beta) * clipped * clipped
    fixed_first = moment / (1.0 - adam_beta**STEP)
    fixed_second = square / (1.0 - adam_beta**STEP)
    updated = master - learning_rate * (
        fixed_first / (jnp.sqrt(fixed_second) + adam_eps) + weight_decay * master
    )
    return (updated, moment, square)


def sum_rows(values):
    return jnp.sum(values.reshape(-1, 8, values.shape[-1]), 0)


def closing_kernel(count, count_dp, sizes, *refs):
    refs = list(refs)

    def pull(number):
        taken = refs[:number]
        del refs[:number]
        return taken

    number, finished, states = sizes
    items, (columns, tile), done = pull(number), pull(2), pull(finished)
    state_in, state_out, (stats,) = pull(states), pull(states), pull(1)
    shares = pull(number)
    sums = PieceSums(count_dp, items, shares, pull(number * (count_dp.bit_length() + 1)))
    (write_share,) = pull(1)
    scatter = LineScatter(count, columns, write_share, pull(4), pull(4))
    small = [Spread("mp", count, *pull(3)) for _ in range(2)]
    over_dp, over_mp = Spread("dp", count_dp, *pull(3)), Spread("mp", count, *pull(3))
    held, (turned, in_sems, out_sems) = pull(states), pull(3)

    barrier = pltpu.get_barrier_semaphore()
    others = [over_dp.peer(step) for step in range(1, count_dp)]
    others += [over_mp.peer(step) for step in range(1, count)]
    signal_all(barrier, others)
    loads = [
        pltpu.make_async_copy(source, target, in_sems.at[index])
        for index, (source, target) in enumerate(zip(state_in, held))
    ]
    for load in loads:
        load.start()
    pl.semaphore_wait(barrier, len(others))

    sums.begin()
    scatter.run(lambda: sums.advance(1))
    for phase in range(2, sums.bits + 1):
        sums.advance(phase)
    for spread, share in zip(small, shares[-2:]):
        spread.held[spread.place] = share[...]
        spread.start()
    scatter.settle()

    self_in_2, self_out, read_query, read_key, read_value, read_out = shares[:6]
    self_in_0, self_in_1 = done[:2]
    up, down = done[2:6], done[6:10]
    lat_rows, if_rows = self_out.shape[0], read_key.shape[0]
    write_key, write_value = (write_share.at[pl.ds(i * lat_rows, lat_rows)] for i in range(2))
    write_query, write_out = (
        write_share.at[pl.ds(2 * lat_rows + i * if_rows, if_rows)] for i in range(2)
    )
    for index, share in enumerate([read_out, self_out] + down):
        turned[index] = share[...].T
    split = [read_query, read_key, read_value, read_out, self_in_0, self_in_1, self_in_2, self_out]
    square = sum(sum_rows(ref[...] * ref[...]) for ref in split + up + down + [write_share])
    for spread in small:
        spread.take()
    latents, rest = (spread.total() for spread in small)
    lead = (over_mp.place == 0).astype(jnp.float32)
    local = jnp.sum(square) + lead * (
        jnp.sum(sum_rows(latents * latents)) + jnp.sum(sum_rows(rest * rest))
    )
    lane = lax.broadcasted_iota(jnp.int32, (8, 128), 1)
    value = jnp.where(lane == 0, local, tile[...])
    for spread in (over_dp, over_mp):
        spread.held[spread.place] = value
        spread.start()
        spread.take()
        value = spread.total()
    norm = jnp.sqrt(value)
    stats[...] = jnp.where(lane == 0, norm, value)
    first = jnp.logical_and(lane == 0, lax.broadcasted_iota(jnp.int32, (8, 128), 0) == 0)
    scale = jnp.sum(jnp.where(first, clip_level / jnp.maximum(norm, clip_level), 0.0))

    def update(kind, at, gradient):
        refs = held[3 * kind : 3 * kind + 3]
        results = adam_update(refs[0][at], refs[1][at], refs[2][at], gradient, scale)
        for ref, result in zip(refs, results):
            ref[at] = result

    def update_rows(kind, slot, gradient):
        rows, width = gradient.shape
        step = math.gcd(rows, max(8, 8192 // width))

        def one(index, carry):
            where = pl.ds(pl.multiple_of(index * step, step), step)
            at = (where,) if slot is None else (slot, where)
            update(kind, at, gradient[where])
            return carry

        lax.fori_loop(0, rows // step, one, 0)

    def store(kind):
        for index in range(3 * kind, 3 * kind + 3):
            pltpu.make_async_copy(held[index], state_out[index], out_sems.at[index]).start()

    for load in loads:
        load.wait()
    wide = [read_query, self_in_0, self_in_1, self_in_2] + up + [write_key, write_value]
    for slot, gradient in enumerate(wide):
        update_rows(0, slot, gradient)
    store(0)
    for slot in range(turned.shape[0]):
        update_rows(2, slot, turned.at[slot])
    store(2)
    for slot, gradient in enumerate([read_key, read_value, write_query]):
        update_rows(1, slot, gradient)
    store(1)
    update_rows(3, None, write_out)
    store(3)
    update(4, (slice(None),), latents)
    store(4)
    gains, lanes = held[15].shape
    update(5, (slice(None),), rest[:gains, :lanes])
    store(5)
    for slot in range(2):
        low = 16 * (slot + 1)
        update(6, (slot,), rest[low : low + PIX, :lanes])
    store(6)
    sums.finish()
    scatter.finish()
    for spread in small + [over_dp, over_mp]:
        spread.finish()
    for index in range(states):
        pltpu.make_async_copy(held[index], state_out[index], out_sems.at[index]).wait()


def closing(items, columns, tile, done, states, call_id):
    items, shapes, shares = piece_shapes(items)
    count, count_dp = lax.axis_size("mp"), lax.axis_size("dp")
    shares = [pltpu.VMEM(item.shape, jnp.float32) for item in shares]
    held = [pltpu.VMEM(item.shape, jnp.float32) for item in states]
    turned = (6,) + done[0].shape[::-1]
    state_sems = pltpu.SemaphoreType.DMA((len(states),))
    scratch = (
        shares
        + PieceSums.scratch(count_dp, shapes)
        + [pltpu.VMEM((columns.shape[0] // count, columns.shape[1]), jnp.float32)]
        + LineScatter.scratch(count, columns.shape, 4)
        + Spread.scratch(count, tuple(shares[-2].shape))
        + Spread.scratch(count, tuple(shares[-1].shape))
        + Spread.scratch(count_dp, tile.shape)
        + Spread.scratch(count, tile.shape)
        + held
        + [pltpu.VMEM(turned, jnp.float32), state_sems, state_sems]
    )
    here = [*items, columns, tile, *done]
    any_spec = pl.BlockSpec(memory_space=pl.ANY)
    results = pl.pallas_call(
        partial(closing_kernel, count, count_dp, (len(items), len(done), len(states))),
        out_shape=[jax.ShapeDtypeStruct(item.shape, jnp.float32) for item in states]
        + [jax.ShapeDtypeStruct((8, 128), jnp.float32)],
        in_specs=[VMEM_SPEC] * len(here) + [any_spec] * len(states),
        out_specs=[any_spec] * len(states) + [VMEM_SPEC],
        scratch_shapes=scratch,
        compiler_params=pltpu.CompilerParams(
            collective_id=call_id,
            has_side_effects=True,
            vmem_limit_bytes=room(here, room_of(scratch)),
        ),
    )(*here, *states)
    return results[:-1], results[-1]


def body(
    clean_patches,
    noise_patches,
    timesteps,
    present_mask,
    copy_widein,
    copy_narrowin,
    copy_wideout,
    copy_narrowout,
    copy_latents,
    copy_gains,
    copy_pixels,
    master_widein,
    first_widein,
    second_widein,
    master_narrowin,
    first_narrowin,
    second_narrowin,
    master_wideout,
    first_wideout,
    second_wideout,
    master_narrowout,
    first_narrowout,
    second_narrowout,
    master_latents,
    first_latents,
    second_latents,
    master_gains,
    first_gains,
    second_gains,
    master_pixels,
    first_pixels,
    second_pixels,
):
    images = clean_patches.shape[0]
    patches = clean_patches.shape[2]
    count_mp, count_dp = lax.axis_size("mp"), lax.axis_size("dp")
    mp_index, dp_index = lax.axis_index("mp"), lax.axis_index("dp")
    lead = (mp_index == 0).astype(jnp.float32)
    latents, d_lat = copy_latents.shape
    d_if = copy_gains.shape[1]
    local = copy_widein.shape[2]
    sharers = max(1, count_mp // images)
    own_images = max(1, images // count_mp)
    own_patches, own_latents = patches // sharers, latents // sharers
    first_image = mp_index * own_images // sharers
    share = lax.rem(mp_index, sharers)

    def dp_piece(values, axis):
        size = values.shape[axis] // count_dp
        return lax.dynamic_slice_in_dim(values, dp_index * size, size, axis).astype(jnp.float32)

    key_piece = dp_piece(copy_widein[:, 8], 0)
    value_piece = dp_piece(copy_widein[:, 9], 0)
    query_piece = dp_piece(copy_narrowin[:, 2], 0)
    out_piece = dp_piece(copy_narrowout, 1).T
    gathered = lax.all_gather(
        jnp.concatenate([key_piece, value_piece, query_piece, out_piece], 0), "mp"
    )

    signal = jnp.cos(0.5 * math.pi * (timesteps.astype(jnp.float32) + 0.5) / NSTEPS) ** 2
    noisy = (
        jnp.sqrt(signal)[:, None, None] * clean_patches
        + jnp.sqrt(1.0 - signal)[:, None, None] * noise_patches
    )
    loss_weight = 0.5 + signal
    keep_float = present_mask.astype(jnp.float32)
    weight_here = jnp.sum(loss_weight * PIX * jnp.sum(keep_float, 1))
    gain_rows = copy_gains.astype(jnp.float32)

    def wide_gain(index):
        return gain_rows[2 * index : 2 * index + 2].reshape(-1)

    pixel_rows = copy_pixels.astype(jnp.float32)
    interface = jnp.einsum("bcp,cd->bpd", noisy, pixel_rows[0], precision=precise) + positions(
        noisy.shape[2], pixel_rows.shape[2]
    )
    latent_zero = copy_latents.astype(jnp.float32)
    read_norm, read_stats = layer_norm(latent_zero, wide_gain(0))
    read_low = read_norm.astype(jnp.bfloat16)
    side_norm, side_stats = layer_norm(interface, gain_rows[8])
    side_low = side_norm.astype(jnp.bfloat16)
    read_query = jnp.einsum(
        "ld,dc->lc", read_low, copy_widein[:, 0], preferred_element_type=jnp.float32
    ).astype(jnp.bfloat16)
    read_query = jnp.broadcast_to(read_query[None], (images,) + read_query.shape)
    read_key = jnp.einsum(
        "bpd,dc->bpc", side_low, copy_narrowin[:, 0], preferred_element_type=jnp.float32
    ).astype(jnp.bfloat16)
    read_value = jnp.einsum(
        "bpd,dc->bpc", side_low, copy_narrowin[:, 1], preferred_element_type=jnp.float32
    ).astype(jnp.bfloat16)
    read_out, read_total = attend_forward(read_query, read_key, read_value, present_mask)
    read_part = jnp.einsum(
        "blc,cd->bld", read_out, copy_wideout[0], preferred_element_type=jnp.float32
    )
    gathered, read_part = lax.optimization_barrier((gathered, read_part))
    gathered = lax.all_gather(gathered, "dp").reshape(count_dp * count_mp, -1, local)
    latent_one, (weight_tile,) = line_sum(
        read_part,
        jnp.broadcast_to(latent_zero[None], (images, latents, d_lat)),
        2,
        tile=jnp.full((8, 128), weight_here),
    )
    weight_total = weight_tile[0, 0]
    self_norm, self_stats = layer_norm(latent_one, wide_gain(1))
    self_low = self_norm.astype(jnp.bfloat16)
    self_triple = jnp.einsum(
        "bld,dsc->blsc", self_low, copy_widein[:, 1:4], preferred_element_type=jnp.float32
    ).astype(jnp.bfloat16)
    self_out, self_total = attend_forward(
        self_triple[:, :, 0], self_triple[:, :, 1], self_triple[:, :, 2], None
    )
    latent_two, write_weights = line_sum(
        jnp.einsum("blc,cd->bld", self_out, copy_wideout[1], preferred_element_type=jnp.float32),
        latent_one,
        3,
        blocks=(gathered, [d_lat, d_lat, d_if, d_if]),
    )
    write_key_weight, write_value_weight, write_query_weight, write_out_weight = write_weights
    feed_norm, feed_stats = layer_norm(latent_two, wide_gain(2))
    feed_low = feed_norm.astype(jnp.bfloat16)
    hidden = jnp.einsum(
        "bld,dsc->blsc", feed_low, copy_widein[:, 4:8], preferred_element_type=jnp.float32
    )
    active, gelu_pull = jax.vjp(partial(jax.nn.gelu, approximate=False), hidden)
    active_low = active.astype(jnp.bfloat16)
    feed_partial = jnp.einsum(
        "blsc,scd->bld", active_low, copy_wideout[2:6], preferred_element_type=jnp.float32
    )

    def own_rows(values):
        values = values.reshape((images * sharers, own_latents) + values.shape[2:])
        return lax.dynamic_slice_in_dim(values, mp_index * own_images, own_images, 0)

    latent_three = own_rows(latent_two) + line_scatter(
        feed_partial.reshape(-1, d_lat), 4
    ).reshape(own_images, own_latents, d_lat)
    write_norm, write_stats = layer_norm(latent_three, wide_gain(3))
    write_low = write_norm.astype(jnp.bfloat16)

    def own_tokens(values, axis):
        values = lax.dynamic_slice_in_dim(values, first_image, own_images, 0)
        return lax.dynamic_slice_in_dim(values, share * own_patches, own_patches, axis)

    own_interface = own_tokens(interface, 1)
    own_noisy, own_noise = own_tokens(noisy, 2), own_tokens(noise_patches, 2)
    own_keep = own_tokens(keep_float, 1)
    own_weight = lax.dynamic_slice_in_dim(loss_weight, first_image, own_images, 0)

    outer_norm, outer_stats = layer_norm(own_interface, gain_rows[9])
    outer_low = outer_norm.astype(jnp.bfloat16)

    def join(spec, values, weight):
        product = jnp.einsum(spec, values, weight, preferred_element_type=jnp.float32)
        return product.astype(jnp.bfloat16)

    def image_rows(values):
        if sharers == 1:
            return values
        nothing = jnp.where(timesteps[0] > 0, 0.0, -0.0)
        whole = lax.all_gather(values.astype(jnp.float32), "mp", axis=0, tiled=True)
        whole = whole + nothing
        whole = whole.reshape(images, latents, d_lat).astype(jnp.bfloat16)
        return lax.dynamic_slice_in_dim(whole, first_image, own_images, 0)

    write_query = join("bpd,dc->bpc", outer_low, write_query_weight)
    write_key = image_rows(join("bld,dc->blc", write_low, write_key_weight))
    write_value = image_rows(join("bld,dc->blc", write_low, write_value_weight))
    write_out, write_total = attend_forward(write_query, write_key, write_value, None)
    outer = own_interface + jnp.einsum(
        "bpc,dc->bpd", write_out, write_out_weight, preferred_element_type=jnp.float32
    )
    final_norm, final_stats = layer_norm(outer, gain_rows[10])
    final_low = final_norm.astype(jnp.bfloat16)
    predicted = jnp.einsum(
        "bpd,cd->bcp", final_low, copy_pixels[1], preferred_element_type=jnp.float32
    )
    difference = predicted - own_noise
    masked = own_weight[:, None, None] * own_keep[:, None, :] * difference
    loss_local = jnp.sum(masked * difference)
    predict_grad = (2.0 * masked / weight_total).astype(jnp.bfloat16)
    head_grad = jnp.einsum(
        "bcp,bpd->cd", predict_grad, final_low, preferred_element_type=jnp.float32
    )
    final_grad = jnp.einsum(
        "bcp,cd->bpd", predict_grad, copy_pixels[1], preferred_element_type=jnp.float32
    )
    outer_grad, gain_final = norm_back(final_grad, gain_rows[10], final_stats)
    branch_low = outer_grad.astype(jnp.bfloat16)
    narrowout_grad = jnp.einsum(
        "bpd,bpc->dc", branch_low, write_out, preferred_element_type=jnp.float32
    )
    write_upstream = join("bpd,dc->bpc", branch_low, write_out_weight)
    query_grad, key_grad, value_grad = attend_back(
        write_query, write_key, write_value, None, write_total, write_upstream
    )
    write_query_grad = jnp.einsum(
        "bpd,bpc->dc", outer_low, query_grad, preferred_element_type=jnp.float32
    )
    outer_part = jnp.einsum(
        "bpc,dc->bpd", query_grad, write_query_weight, preferred_element_type=jnp.float32
    )

    def row_grad(values):
        if sharers > 1:
            whole = jnp.zeros((images, latents, d_lat), jnp.float32)
            whole = lax.dynamic_update_slice_in_dim(whole, values, first_image, 0)
            values = lax.psum_scatter(
                whole.reshape(images * sharers, own_latents, d_lat),
                "mp",
                scatter_dimension=0,
                tiled=True,
            )
        return values.astype(jnp.bfloat16)

    key_grad, value_grad = row_grad(key_grad), row_grad(value_grad)
    write_key_grad = jnp.einsum(
        "bld,blc->dc", write_low, key_grad, preferred_element_type=jnp.float32
    )
    write_value_grad = jnp.einsum(
        "bld,blc->dc", write_low, value_grad, preferred_element_type=jnp.float32
    )
    write_part = jnp.einsum(
        "blc,dc->bld", key_grad, write_key_weight, preferred_element_type=jnp.float32
    ) + jnp.einsum(
        "blc,dc->bld", value_grad, write_value_weight, preferred_element_type=jnp.float32
    )
    own_grad, gain_write = norm_back(write_part, wide_gain(3), write_stats)
    outer_back, gain_outer = norm_back(outer_part, gain_rows[9], outer_stats)

    latent_grad, (key_share, query_share) = line_gather(
        own_grad.reshape(-1, d_lat), 5, [write_key_grad, write_query_grad]
    )
    latent_grad = latent_grad.reshape(latent_one.shape)
    outer_back, gain_outer = norm_back(outer_part, gain_rows[9], outer_stats)

    branch_low = latent_grad.astype(jnp.bfloat16)
    down_grad = [
        jnp.einsum(
            "bld,blc->dc", branch_low, active_low[:, :, slot], preferred_element_type=jnp.float32
        )
        for slot in range(4)
    ]
    active_grad = jnp.einsum(
        "bld,scd->blsc", branch_low, copy_wideout[2:6], preferred_element_type=jnp.float32
    )
    hidden_grad = gelu_pull(active_grad)[0].astype(jnp.bfloat16)
    up_grad = [
        jnp.einsum(
            "bld,blc->dc", feed_low, hidden_grad[:, :, slot], preferred_element_type=jnp.float32
        )
        for slot in range(4)
    ]
    feed_part = jnp.einsum(
        "blsc,dsc->bld", hidden_grad, copy_widein[:, 4:8], preferred_element_type=jnp.float32
    )
    latent_part, gain_feed = norm_back(feed_part, wide_gain(2), feed_stats)
    latent_grad, five_shares = line_sum(
        latent_part, latent_grad, 6, [write_value_grad, narrowout_grad] + up_grad[:2]
    )
    branch_low = latent_grad.astype(jnp.bfloat16)
    self_out_grad = jnp.einsum(
        "bld,blc->dc", branch_low, self_out, preferred_element_type=jnp.float32
    )
    self_upstream = jnp.einsum(
        "bld,cd->blc", branch_low, copy_wideout[1], preferred_element_type=jnp.float32
    ).astype(jnp.bfloat16)
    triple_grad = [
        item.astype(jnp.bfloat16)
        for item in attend_back(
            self_triple[:, :, 0],
            self_triple[:, :, 1],
            self_triple[:, :, 2],
            None,
            self_total,
            self_upstream,
        )
    ]
    self_in_grad = [
        jnp.einsum("bld,blc->dc", self_low, item, preferred_element_type=jnp.float32)
        for item in triple_grad
    ]
    self_part = jnp.einsum(
        "blsc,dsc->bld",
        jnp.stack(triple_grad, 2),
        copy_widein[:, 1:4],
        preferred_element_type=jnp.float32,
    )
    latent_part, gain_self = norm_back(self_part, wide_gain(1), self_stats)
    latent_grad, six_shares = line_sum(
        latent_part, latent_grad, 7, up_grad[2:] + down_grad + self_in_grad[:2]
    )
    write_share = jnp.concatenate([key_share, five_shares[0], query_share, five_shares[1]], 0)
    write_columns = jnp.concatenate(jnp.split(write_share, count_mp, 1), 0)
    branch_low = latent_grad.astype(jnp.bfloat16)
    read_out_grad = jnp.einsum(
        "bld,blc->dc", branch_low, read_out, preferred_element_type=jnp.float32
    )
    read_upstream = jnp.einsum(
        "bld,cd->blc", branch_low, copy_wideout[0], preferred_element_type=jnp.float32
    ).astype(jnp.bfloat16)
    query_grad, key_grad, value_grad = (
        item.astype(jnp.bfloat16)
        for item in attend_back(
            read_query, read_key, read_value, present_mask, read_total, read_upstream
        )
    )
    read_query_grad = jnp.einsum(
        "ld,blc->dc", read_low, query_grad, preferred_element_type=jnp.float32
    )
    read_part = jnp.einsum(
        "blc,dc->bld", query_grad, copy_widein[:, 0], preferred_element_type=jnp.float32
    )
    normed, scale = read_stats
    latent_part, gain_read = norm_back(
        read_part, wide_gain(0), (normed[None], scale[None])
    )
    latent_total = jnp.sum(lead * latent_grad + latent_part, 0)
    read_key_grad = jnp.einsum(
        "bpd,bpc->dc", side_low, key_grad, preferred_element_type=jnp.float32
    )
    read_value_grad = jnp.einsum(
        "bpd,bpc->dc", side_low, value_grad, preferred_element_type=jnp.float32
    )
    side_part = jnp.einsum(
        "bpc,dc->bpd", key_grad, copy_narrowin[:, 0], preferred_element_type=jnp.float32
    ) + jnp.einsum(
        "bpc,dc->bpd", value_grad, copy_narrowin[:, 1], preferred_element_type=jnp.float32
    )
    side_back, gain_side = norm_back(side_part, gain_rows[8], side_stats)
    embed_grad = jnp.einsum("bcp,bpd->cd", noisy, side_back, precision=precise) + jnp.einsum(
        "bcp,bpd->cd", own_noisy, outer_grad + outer_back, precision=precise
    )
    gains_grad = jnp.concatenate(
        [
            gain_read.reshape(2, -1),
            gain_self.reshape(2, -1),
            gain_feed.reshape(2, -1),
            gain_write.reshape(2, -1),
            gain_side[None],
            gain_outer[None],
            gain_final[None],
        ],
        0,
    )

    def dp_pieces(values):
        values = values.reshape(values.shape[0], count_dp, -1)
        return jnp.swapaxes(values, 0, 1)

    low_rows = [gains_grad, embed_grad, head_grad]
    low_rows = [jnp.pad(item, ((0, 16 - item.shape[0]), (0, 0))) for item in low_rows]
    rest = dp_pieces(jnp.concatenate(low_rows, 0))
    rest = jnp.pad(rest, ((0, 0), (0, 0), (0, 128 - rest.shape[2])))
    latents_item = dp_pieces(latent_total)

    states = (
        *(jnp.swapaxes(item, 0, 1) for item in (master_widein, first_widein, second_widein)),
        *(jnp.swapaxes(item, 0, 1) for item in (master_narrowin, first_narrowin, second_narrowin)),
        master_wideout,
        first_wideout,
        second_wideout,
        *(item.T for item in (master_narrowout, first_narrowout, second_narrowout)),
        master_latents,
        first_latents,
        second_latents,
        master_gains,
        first_gains,
        second_gains,
        master_pixels,
        first_pixels,
        second_pixels,
    )
    results, stats = closing(
        [
            self_in_grad[2],
            self_out_grad,
            read_query_grad,
            read_key_grad,
            read_value_grad,
            read_out_grad,
            latents_item.reshape(-1, latents_item.shape[2]),
            rest.reshape(-1, rest.shape[2]),
        ],
        write_columns,
        jnp.full((8, 128), loss_local),
        [*six_shares[6:8], *five_shares[2:], *six_shares[:6]],
        states,
        8,
    )
    results = [
        jnp.swapaxes(item, 0, 1) if index < 6 or 9 <= index < 12 else item
        for index, item in enumerate(results)
    ]
    return (stats[0, 1] / weight_total, stats[0, 0], *results)


def solution(mesh):
    in_specs = (
        P("dp", None, None),
        P("dp", None, None),
        P("dp"),
        P("dp", None),
        P(None, None, "mp"),
        P(None, None, "mp"),
        P(None, "mp", None),
        P("mp", None),
        P(),
        P(),
        P(),
        P("dp", None, "mp"),
        P("dp", None, "mp"),
        P("dp", None, "mp"),
        P("dp", None, "mp"),
        P("dp", None, "mp"),
        P("dp", None, "mp"),
        P(None, "mp", "dp"),
        P(None, "mp", "dp"),
        P(None, "mp", "dp"),
        P("mp", "dp"),
        P("mp", "dp"),
        P("mp", "dp"),
        P(None, "dp"),
        P(None, "dp"),
        P(None, "dp"),
        P(None, "dp"),
        P(None, "dp"),
        P(None, "dp"),
        P(None, None, "dp"),
        P(None, None, "dp"),
        P(None, None, "dp"),
    )
    out_specs = (
        P(),
        P(),
        P("dp", None, "mp"),
        P("dp", None, "mp"),
        P("dp", None, "mp"),
        P("dp", None, "mp"),
        P("dp", None, "mp"),
        P("dp", None, "mp"),
        P(None, "mp", "dp"),
        P(None, "mp", "dp"),
        P(None, "mp", "dp"),
        P("mp", "dp"),
        P("mp", "dp"),
        P("mp", "dp"),
        P(None, "dp"),
        P(None, "dp"),
        P(None, "dp"),
        P(None, "dp"),
        P(None, "dp"),
        P(None, "dp"),
        P(None, None, "dp"),
        P(None, None, "dp"),
        P(None, None, "dp"),
    )
    return jax.shard_map(body, mesh=mesh, in_specs=in_specs, out_specs=out_specs, check_vma=False)
```

```python
from functools import partial
import math

import jax
import jax.numpy as jnp
import numpy as np
from jax import lax
from jax.experimental import pallas as pl
from jax.experimental.pallas import tpu as pltpu
from jax.sharding import PartitionSpec as P

HEAD_DIM = 64
PIX = 12
NSTEPS = 1000
STEP = 10


precise = lax.Precision.HIGHEST
clip_level = 0.01
learning_rate = 0.05
weight_decay = 0.1
adam_beta = 0.5
adam_eps = 1e-08


def layer_norm(values, gain):
    centered = values - jnp.mean(values, -1, keepdims=True)
    scale = lax.rsqrt(jnp.mean(centered * centered, -1, keepdims=True) + 1e-05)
    normed = centered * scale
    return (normed * gain, (normed, scale))


def norm_back(upstream, gain, stats):
    normed, scale = stats
    inner = upstream * gain
    values = scale * (
        inner
        - jnp.mean(inner, -1, keepdims=True)
        - normed * jnp.mean(inner * normed, -1, keepdims=True)
    )
    gain_grad = jnp.sum((upstream * normed).reshape(-1, normed.shape[-1]), 0)
    return (values, gain_grad)


def position_table(count, width):
    place = np.arange(count, dtype=np.float64)[:, None]
    angle = place * 10000.0 ** (-2.0 * np.arange(width // 2) / width)
    return jnp.asarray(np.concatenate([np.sin(angle), np.cos(angle)], -1), jnp.float32)


def positions(count, width):
    place = jnp.arange(count, dtype=jnp.float32)[:, None]
    index = jnp.arange(width // 2, dtype=jnp.float32)[None, :]
    angle = place * jnp.exp(-math.log(10000.0) * 2.0 * index / width)
    return jnp.concatenate([jnp.sin(angle), jnp.cos(angle)], -1)


def split_heads(values):
    return values.reshape(values.shape[:-1] + (values.shape[-1] // HEAD_DIM, HEAD_DIM))


def attend_scores(queries, keys, keep_mask):
    scores = jnp.einsum(
        "bqhe,bkhe->bhqk",
        split_heads(queries),
        split_heads(keys),
        preferred_element_type=jnp.float32,
    ) * HEAD_DIM ** (-0.5)
    if keep_mask is not None:
        scores = jnp.where(keep_mask[:, None, None, :] > 0, scores, -1e30)
    return scores


def attend_forward(queries, keys, values, keep_mask):
    scores = attend_scores(queries, keys, keep_mask)
    top = jnp.max(scores, -1, keepdims=True)
    log_total = top + jnp.log(jnp.sum(jnp.exp(scores - top), -1, keepdims=True))
    probs = jnp.exp(scores - log_total).astype(jnp.bfloat16)
    output = jnp.einsum(
        "bhqk,bkhe->bqhe", probs, split_heads(values), preferred_element_type=jnp.float32
    )
    return (output.reshape(queries.shape).astype(jnp.bfloat16), log_total)


def attend_back(queries, keys, values, keep_mask, log_total, upstream):
    scores = attend_scores(queries, keys, keep_mask)
    probs = jnp.exp(scores - log_total)
    value_grad = jnp.einsum(
        "bhqk,bqhe->bkhe",
        probs.astype(jnp.bfloat16),
        split_heads(upstream),
        preferred_element_type=jnp.float32,
    )
    prob_grad = jnp.einsum(
        "bqhe,bkhe->bhqk",
        split_heads(upstream),
        split_heads(values),
        preferred_element_type=jnp.float32,
    )
    score_grad = (probs * (prob_grad - jnp.sum(prob_grad * probs, -1, keepdims=True))).astype(
        jnp.bfloat16
    )
    query_grad = jnp.einsum(
        "bhqk,bkhe->bqhe", score_grad, split_heads(keys), preferred_element_type=jnp.float32
    ) * HEAD_DIM ** (-0.5)
    key_grad = jnp.einsum(
        "bhqk,bqhe->bkhe", score_grad, split_heads(queries), preferred_element_type=jnp.float32
    ) * HEAD_DIM ** (-0.5)
    return (
        query_grad.reshape(queries.shape).astype(jnp.bfloat16),
        key_grad.reshape(keys.shape),
        value_grad.reshape(values.shape),
    )


MESH_ID = pl.DeviceIdType.MESH
VMEM_SPEC = pl.BlockSpec(memory_space=pltpu.VMEM)
CHUNKS = 32
VMEM_LIMIT = 56 << 20


def remote(source, target, send_sem, recv_sem, device):
    return pltpu.make_async_remote_copy(
        src_ref=source,
        dst_ref=target,
        send_sem=send_sem,
        recv_sem=recv_sem,
        device_id=device,
        device_id_type=MESH_ID,
    )


class PieceSums:
    def __init__(self, count, items, outs, scratch):
        self.count, self.items, self.outs = count, items, outs
        self.bits = count.bit_length() - 1
        self.place = lax.axis_index("dp") if items else None
        self.held = []
        for index in range(len(items)):
            self.held.append(scratch[index * (self.bits + 2) : (index + 1) * (self.bits + 2)])

    @staticmethod
    def scratch(count, shapes):
        bits = count.bit_length() - 1
        result = []
        for rows, width in shapes:
            result.append(pltpu.VMEM((count // 2, rows, width), jnp.float32))
            for phase in range(2, bits + 1):
                result.append(
                    pltpu.VMEM((2 * (count >> phase), rows // 2, width), jnp.float32)
                )
            copies = count // 2 + 2 * sum(count >> phase for phase in range(2, bits + 1))
            result += [pltpu.SemaphoreType.DMA((copies,))] * 2
        return result

    def peers(self):
        return [{"dp": self.place ^ (1 << bit)} for bit in range(self.bits)] if self.items else []

    def order(self, half):
        later = list(range(1, self.bits))
        turn = half * (len(later) // 2)
        return later[turn:] + later[:turn]

    def first_copy(self, index, piece):
        item, held = self.items[index], self.held[index]
        other = 1 - (self.place & 1)
        return remote(
            item.at[2 * piece + other],
            held[0].at[piece],
            held[-2].at[piece],
            held[-1].at[piece],
            {"dp": self.place ^ 1},
        )

    def member(self, half, phase, entry, flip):
        bits = self.order(half)
        settled, now, rest = bits[: phase - 2], bits[phase - 2], bits[phase - 1 :]
        piece = 0
        for bit in settled:
            piece = piece | (self.place & (1 << bit))
        own = self.place & (1 << now)
        piece = piece | ((own ^ (1 << now)) if flip else own)
        for position, bit in enumerate(rest):
            if (entry >> position) & 1:
                piece = piece | (1 << bit)
        return piece >> 1

    def later_copy(self, index, half, phase, entry):
        held = self.held[index]
        rows = self.items[index].shape[1] // 2
        size = self.count >> phase
        sem = self.count // 2 + 2 * sum(self.count >> p for p in range(2, phase)) + half * size + entry
        return remote(
            held[0].at[self.member(half, phase, entry, True), pl.ds(half * rows, rows)],
            held[phase - 1].at[half * size + entry],
            held[-2].at[sem],
            held[-1].at[sem],
            {"dp": self.place ^ (1 << self.order(half)[phase - 2])},
        )

    def entries(self, phase):
        return [
            (index, half, entry)
            for index in range(len(self.items))
            for half in range(2)
            for entry in range(self.count >> phase)
        ]

    def begin(self):
        for index in range(len(self.items)):
            for piece in range(self.count // 2):
                self.first_copy(index, piece).start()

    def send(self, phase):
        for index, half, entry in self.entries(phase):
            self.later_copy(index, half, phase, entry).start()

    def advance(self, phase):
        if not self.items:
            return
        if phase == 1:
            own = self.place & 1
            for index, item in enumerate(self.items):
                total = self.held[index][0]
                for piece in range(self.count // 2):
                    self.first_copy(index, piece).wait_recv()
                    add_rows(total.at[piece], total.at[piece], item.at[2 * piece + own])
        else:
            for index, half, entry in self.entries(phase):
                self.later_copy(index, half, phase, entry).wait_recv()
                held, rows = self.held[index], self.items[index].shape[1] // 2
                where = pl.ds(half * rows, rows)
                came = held[phase - 1].at[half * (self.count >> phase) + entry]
                kept = held[0].at[self.member(half, phase, entry, False), where]
                if phase == self.bits:
                    add_rows(self.outs[index].at[where], kept, came)
                else:
                    add_rows(kept, kept, came)
        if phase < self.bits:
            self.send(phase + 1)

    def finish(self):
        for index in range(len(self.items)):
            for piece in range(self.count // 2):
                self.first_copy(index, piece).wait_send()
        for phase in range(2, self.bits + 1):
            for index, half, entry in self.entries(phase):
                self.later_copy(index, half, phase, entry).wait_send()

    def moments(self, total):
        if not self.items:
            return [(0, total, None)]
        marks, low = [], 0
        for phase in range(1, self.bits + 1):
            share = (1 - 0.5 ** (phase - 1)) / (1 - 0.5 ** (self.bits - 1))
            high = total if phase == self.bits else int(total * (0.22 + 0.78 * share))
            marks.append((low, high, phase))
            low = high
        return marks


def add_rows(target, left, right):
    rows, width = target.shape
    step = math.gcd(rows, max(8, 8192 // width))

    def one(index, carry):
        where = pl.ds(pl.multiple_of(index * step, step), step)
        target[where] = left[where] + right[where]
        return carry

    lax.fori_loop(0, rows // step, one, 0)


class Spread:
    def __init__(self, name, count, held, send_sem, recv_sem):
        self.name, self.count, self.held = name, count, held
        self.send_sem, self.recv_sem = send_sem, recv_sem
        self.place = lax.axis_index(name)

    @staticmethod
    def scratch(count, shape):
        sems = pltpu.SemaphoreType.DMA((count,))
        return [pltpu.VMEM((count,) + shape, jnp.float32), sems, sems]

    def peer(self, step):
        return {self.name: lax.rem(self.place + step, self.count)}

    def copy(self, step, slot):
        return remote(
            self.held.at[slot],
            self.held.at[slot],
            self.send_sem.at[step],
            self.recv_sem.at[slot],
            self.peer(step),
        )

    def each(self, action):
        def one(step, carry):
            action(step)
            return carry

        lax.fori_loop(1, self.count, one, 0)

    def start(self):
        self.each(lambda step: self.copy(step, self.place).start())

    def take(self):
        self.each(lambda step: self.copy(step, lax.rem(self.place + step, self.count)).wait_recv())

    def finish(self):
        self.each(lambda step: self.copy(step, self.place).wait_send())

    def total(self):
        return lax.fori_loop(
            1, self.count, lambda slot, carry: carry + self.held[slot], self.held[0]
        )


class Convert:
    def __init__(self, count_mp, steps, blocks, outs, buffer, sems):
        self.count_mp, self.blocks, self.outs = count_mp, blocks, outs
        self.buffer, self.sems = buffer, sems
        self.number = blocks.shape[0]
        self.each = -(-self.number // steps)

    @staticmethod
    def scratch(block):
        return [pltpu.VMEM((3,) + block, jnp.float32), pltpu.SemaphoreType.DMA((3,))]

    def copy(self, index):
        slot = lax.rem(index, 3)
        return pltpu.make_async_copy(
            self.blocks.at[index], self.buffer.at[slot], self.sems.at[slot]
        )

    def begin(self):
        self.copy(0).start()
        self.copy(1).start()

    def one(self, index):
        self.copy(index).wait()

        @pl.when(index + 2 < self.number)
        def _():
            self.copy(index + 2).start()

        block = self.buffer.at[lax.rem(index, 3)]
        local = block.shape[1]
        columns = pl.ds(pl.multiple_of(lax.rem(index, self.count_mp) * local, local), local)
        low = 0
        for out in self.outs:
            rows = out.shape[0] * self.count_mp // self.number
            where = pl.ds(pl.multiple_of(index // self.count_mp * rows, rows), rows)
            out[where, columns] = block[pl.ds(low, rows)].astype(jnp.bfloat16)
            low += rows

    def step(self, index):
        for entry in range(self.each):
            self.one(index * self.each + entry)


def signal_all(barrier, others):
    for other in others:
        pl.semaphore_signal(barrier, inc=1, device_id=other, device_id_type=MESH_ID)


def greet(place, count, others=()):
    barrier = pltpu.get_barrier_semaphore()
    below, above = {"mp": place - 1}, {"mp": place + 1}

    @pl.when(place > 0)
    def _():
        pl.semaphore_signal(barrier, inc=1, device_id=below, device_id_type=MESH_ID)

    @pl.when(place < count - 1)
    def _():
        pl.semaphore_signal(barrier, inc=1, device_id=above, device_id_type=MESH_ID)

    signal_all(barrier, others)
    inside = jnp.logical_and(place > 0, place < count - 1)

    @pl.when(inside)
    def _():
        pl.semaphore_wait(barrier, 2 + len(others))

    @pl.when(jnp.logical_not(inside))
    def _():
        pl.semaphore_wait(barrier, 1 + len(others))


def views(refs):
    result = []
    for ref in refs:
        result += [ref] if len(ref.shape) == 3 else [ref.at[slot] for slot in range(ref.shape[0])]
    return result


def line_sum_kernel(count, count_dp, extra, tiled, converted, *refs):
    refs = list(refs)

    def pull(number):
        taken = refs[:number]
        del refs[:number]
        return taken

    part_ref, base_ref = pull(2)
    items, tile, blocks = views(pull(extra)), pull(tiled), pull(min(1, converted))
    (out_ref,) = pull(1)
    outs, tile_out, wide = pull(len(items)), pull(tiled), pull(converted)
    inner, from_away, from_toward, toward_send, away_send, away_recv, toward_recv = pull(7)
    chunks = toward_send.shape[0]
    spread = Spread("dp", count_dp, *pull(3)) if tiled else None
    convert = Convert(count, chunks, blocks[0], wide, *pull(2)) if converted else None
    sums = PieceSums(count_dp, items, outs, refs)
    place = lax.axis_index("mp")
    half = count // 2
    low_side = place < half
    toward = {"mp": jnp.where(low_side, place + 1, place - 1)}
    away = {"mp": jnp.where(low_side, place - 1, place + 1)}
    middle = jnp.logical_or(place == half - 1, place == half)
    outermost = jnp.logical_or(place == 0, place == count - 1)
    rows = part_ref.shape[0] // chunks
    others = [spread.peer(step) for step in range(1, count_dp)] if tiled else sums.peers()
    if tiled:
        spread.held[spread.place] = tile[0][...]
    greet(place, count, others)
    if tiled:
        spread.start()
    if converted:
        convert.begin()
    sums.begin()

    def window(step):
        return pl.ds(pl.multiple_of(step * rows, rows), rows)

    def push(step, source, inside):
        target = from_toward if inside else from_away
        recv = toward_recv if inside else away_recv
        return remote(
            source.at[window(step)],
            target.at[window(step)],
            toward_send.at[step],
            recv.at[step],
            toward,
        )

    def back(step, source):
        return remote(
            source.at[window(step)],
            from_toward.at[window(step)],
            away_send.at[step],
            toward_recv.at[step],
            away,
        )

    def gather_in(step):
        push(step, part_ref, False).wait_recv()
        inner[window(step)] = part_ref[window(step)] + from_away[window(step)]

    @pl.when(outermost)
    def _():
        def leave(step, carry):
            push(step, part_ref, False).start()
            return carry

        lax.fori_loop(0, chunks, leave, 0)

        def arrive(step, carry):
            push(step, part_ref, True).wait_recv()
            out_ref[window(step)] = from_toward[window(step)] + base_ref[window(step)]
            push(step, part_ref, False).wait_send()
            if converted:
                convert.step(step)
            return carry

        for low, high, phase in sums.moments(chunks):
            lax.fori_loop(low, high, arrive, 0)
            sums.advance(phase)

    lag = 2

    @pl.when(middle)
    def _():
        def finish(step):
            push(step, inner, True).wait_recv()
            push(step, inner, True).wait_send()
            total = inner[window(step)] + from_toward[window(step)]
            inner[window(step)] = total
            back(step, inner).start()
            out_ref[window(step)] = total + base_ref[window(step)]

        def first(step, carry):
            gather_in(step)
            push(step, inner, True).start()
            if converted:
                convert.step(step)
            return carry

        def both(step, carry):
            first(step, carry)
            finish(step - lag)
            return carry

        def last(step, carry):
            finish(step)
            return carry

        def drain(step, carry):
            back(step, inner).wait_send()
            return carry

        lax.fori_loop(0, lag, first, 0)
        for low, high, phase in sums.moments(chunks):
            lax.fori_loop(max(low, lag), high, both, 0)
            if high == chunks:
                lax.fori_loop(chunks - lag, chunks, last, 0)
            sums.advance(phase)
        lax.fori_loop(0, chunks, drain, 0)

    if count > 4:

        @pl.when(jnp.logical_not(jnp.logical_or(middle, outermost)))
        def _():
            def inwards(step, carry):
                gather_in(step)
                push(step, inner, False).start()
                return carry

            def outwards(step, carry):
                push(step, inner, True).wait_recv()
                back(step, from_toward).start()
                out_ref[window(step)] = from_toward[window(step)] + base_ref[window(step)]
                if converted:
                    convert.step(step)
                return carry

            def drain(step, carry):
                push(step, inner, False).wait_send()
                back(step, from_toward).wait_send()
                return carry

            lax.fori_loop(0, chunks, inwards, 0)
            for low, high, phase in sums.moments(chunks):
                lax.fori_loop(low, high, outwards, 0)
                sums.advance(phase)
            lax.fori_loop(0, chunks, drain, 0)

    sums.finish()
    if tiled:
        spread.take()
        tile_out[0][...] = spread.total()
        spread.finish()


def room(*groups):
    total = 8 << 20
    for group in groups:
        for item in group:
            if hasattr(item, "shape") and hasattr(item, "dtype"):
                total += math.prod(item.shape) * jnp.dtype(item.dtype).itemsize
    return min(total, VMEM_LIMIT)


def room_of(scratch):
    return [
        jax.ShapeDtypeStruct(item.shape, item.dtype)
        for item in scratch
        if getattr(item, "dtype", None) in (jnp.float32, jnp.bfloat16)
    ]


def piece_shapes(items):
    count = lax.axis_size("dp")
    items = [item.reshape(item.shape[:-2] + (count, -1, item.shape[-1])) for item in items]
    shapes = []
    for item in items:
        shapes += [item.shape[-2:]] * (item.shape[0] if item.ndim == 4 else 1)
    return items, shapes, [jax.ShapeDtypeStruct(shape, jnp.float32) for shape in shapes]


def line_sum(part, base, call_id, items=(), tile=None, blocks=None):
    shape = part.shape
    items, shapes, shares = piece_shapes(items)
    count, count_dp = lax.axis_size("mp"), lax.axis_size("dp")
    part = part.reshape(-1, shape[-1])
    rows, width = part.shape
    buffer = pltpu.VMEM((rows, width), jnp.float32)
    sems = pltpu.SemaphoreType.DMA((CHUNKS,))
    inputs, specs = [part, base.reshape(part.shape), *items], [VMEM_SPEC] * (2 + len(items))
    outs = [jax.ShapeDtypeStruct((rows, width), jnp.float32)] + shares
    scratch = [buffer] * 3 + [sems] * 4
    if tile is not None:
        inputs.append(tile)
        specs.append(VMEM_SPEC)
        outs.append(jax.ShapeDtypeStruct(tile.shape, jnp.float32))
        scratch += Spread.scratch(count_dp, tile.shape)
    sizes = []
    if blocks is not None:
        blocks, sizes = blocks
        outs += [
            jax.ShapeDtypeStruct((size, count * blocks.shape[2]), jnp.bfloat16) for size in sizes
        ]
        scratch += Convert.scratch(blocks.shape[1:])
    scratch += PieceSums.scratch(count_dp, shapes)
    limit = room(inputs, outs, room_of(scratch))
    if blocks is not None:
        inputs.append(blocks)
        specs.append(pl.BlockSpec(memory_space=pl.ANY))
    results = pl.pallas_call(
        partial(line_sum_kernel, count, count_dp, len(items), int(tile is not None), len(sizes)),
        out_shape=outs,
        in_specs=specs,
        out_specs=[VMEM_SPEC] * len(outs),
        scratch_shapes=scratch,
        compiler_params=pltpu.CompilerParams(
            collective_id=call_id, has_side_effects=True, vmem_limit_bytes=limit
        ),
        cost_estimate=pl.CostEstimate(
            flops=4 * rows * width, bytes_accessed=350 * rows * width, transcendentals=0
        ),
    )(*inputs)
    return results[0].reshape(shape), results[1:]


class LineScatter:
    def __init__(self, count, part, out, buffers, sems):
        self.count, self.part, self.out = count, part, out
        self.up_acc, self.down_acc, self.from_below, self.from_above = buffers
        self.up_send, self.down_send, self.up_recv, self.down_recv = sems
        self.place = lax.axis_index("mp")
        self.steps = self.up_send.shape[1]
        self.block = part.shape[0] // count
        self.rows = self.block // self.steps

    @staticmethod
    def scratch(count, shape, steps):
        sems = pltpu.SemaphoreType.DMA((count, steps))
        return [pltpu.VMEM(shape, jnp.float32)] * 4 + [sems] * 4

    def window(self, owner, step):
        return pl.ds(pl.multiple_of(owner * self.block + step * self.rows, self.rows), self.rows)

    def up(self, owner, step, source):
        where = self.window(owner, step)
        return remote(
            source.at[where],
            self.from_below.at[where],
            self.up_send.at[owner, step],
            self.up_recv.at[owner, step],
            {"mp": self.place + 1},
        )

    def down(self, owner, step, source):
        where = self.window(owner, step)
        return remote(
            source.at[where],
            self.from_above.at[where],
            self.down_send.at[owner, step],
            self.down_recv.at[owner, step],
            {"mp": self.place - 1},
        )

    def up_turn(self, index):
        place, part = self.place, self.part
        owner, step = self.count - 1 - index // self.steps, lax.rem(index, self.steps)

        @pl.when(jnp.logical_and(owner > place, place == 0))
        def _():
            self.up(owner, step, part).start()

        @pl.when(jnp.logical_and(owner > place, place > 0))
        def _():
            self.up(owner, step, part).wait_recv()
            where = self.window(owner, step)
            self.up_acc[where] = part[where] + self.from_below[where]
            self.up(owner, step, self.up_acc).start()

    def down_turn(self, index):
        place, part, count = self.place, self.part, self.count
        owner, step = index // self.steps, lax.rem(index, self.steps)

        @pl.when(jnp.logical_and(owner < place, place == count - 1))
        def _():
            self.down(owner, step, part).start()

        @pl.when(jnp.logical_and(owner < place, place < count - 1))
        def _():
            self.down(owner, step, part).wait_recv()
            where = self.window(owner, step)
            self.down_acc[where] = part[where] + self.from_above[where]
            self.down(owner, step, self.down_acc).start()

    def run(self, pause=None):
        turns, lag = self.count * self.steps, self.steps

        def staggered(first, second):
            def begin(index, carry):
                first(index)
                return carry

            def both(index, carry):
                first(index)
                second(index - lag)
                return carry

            def end(index, carry):
                second(index)
                return carry

            lax.fori_loop(0, lag, begin, 0)
            if pause is not None:
                pause()
            lax.fori_loop(lag, turns, both, 0)
            lax.fori_loop(turns - lag, turns, end, 0)

        @pl.when(self.place < self.count // 2)
        def _():
            staggered(self.up_turn, self.down_turn)

        @pl.when(self.place >= self.count // 2)
        def _():
            staggered(self.down_turn, self.up_turn)

    def settle(self):
        place, rows = self.place, self.rows

        def one(step, carry):
            where = self.window(place, step)
            mine = pl.ds(pl.multiple_of(step * rows, rows), rows)
            self.out[mine] = self.part[where]

            @pl.when(place > 0)
            def _():
                self.up(place, step, self.part).wait_recv()
                self.out[mine] += self.from_below[where]

            @pl.when(place < self.count - 1)
            def _():
                self.down(place, step, self.part).wait_recv()
                self.out[mine] += self.from_above[where]

            return carry

        lax.fori_loop(0, self.steps, one, 0)

    def finish(self):
        place = self.place

        def one(index, carry):
            owner, step = index // self.steps, lax.rem(index, self.steps)

            @pl.when(owner > place)
            def _():
                self.up(owner, step, self.part).wait_send()

            @pl.when(owner < place)
            def _():
                self.down(owner, step, self.part).wait_send()

            return carry

        lax.fori_loop(0, self.count * self.steps, one, 0)


def line_scatter_kernel(count, part_ref, out_ref, *scratch):
    scatter = LineScatter(count, part_ref, out_ref, scratch[:4], scratch[4:])
    greet(scatter.place, count)
    scatter.run()
    scatter.settle()
    scatter.finish()


def line_scatter(part, call_id):
    rows, width = part.shape
    count = lax.axis_size("mp")
    steps = 8
    return pl.pallas_call(
        partial(line_scatter_kernel, count),
        out_shape=jax.ShapeDtypeStruct((rows // count, width), jnp.float32),
        in_specs=[VMEM_SPEC],
        out_specs=VMEM_SPEC,
        scratch_shapes=LineScatter.scratch(count, (rows, width), steps),
        compiler_params=pltpu.CompilerParams(
            collective_id=call_id, has_side_effects=True, vmem_limit_bytes=24 << 20
        ),
        cost_estimate=pl.CostEstimate(
            flops=2 * rows * width, bytes_accessed=230 * rows * width, transcendentals=0
        ),
    )(part)


def line_gather_kernel(count, count_dp, extra, own_ref, *refs):
    items, out_ref, refs = views(refs[:extra]), refs[extra], refs[extra + 1 :]
    outs, refs = refs[: len(items)], refs[len(items) :]
    up_send, down_send, up_recv, down_recv = refs[:4]
    sums = PieceSums(count_dp, items, outs, refs[4:])
    place = lax.axis_index("mp")
    steps = up_send.shape[1]
    block = own_ref.shape[0]
    rows = block // steps
    below, above = {"mp": place - 1}, {"mp": place + 1}
    greet(place, count, sums.peers())
    sums.begin()

    def window(owner, step):
        return pl.ds(pl.multiple_of(owner * block + step * rows, rows), rows)

    def up(owner, step):
        part = out_ref.at[window(owner, step)]
        return remote(part, part, up_send.at[owner, step], up_recv.at[owner, step], above)

    def down(owner, step):
        part = out_ref.at[window(owner, step)]
        return remote(part, part, down_send.at[owner, step], down_recv.at[owner, step], below)

    def begin(step, carry):
        out_ref[window(place, step)] = own_ref[pl.ds(pl.multiple_of(step * rows, rows), rows)]

        @pl.when(place < count - 1)
        def _():
            up(place, step).start()

        @pl.when(place > 0)
        def _():
            down(place, step).start()

        return carry

    lax.fori_loop(0, steps, begin, 0)

    def pass_on(index, carry):
        away, step = 1 + index // steps, lax.rem(index, steps)

        @pl.when(place - away >= 0)
        def _():
            up(place - away, step).wait_recv()

        @pl.when(jnp.logical_and(place - away >= 0, place < count - 1))
        def _():
            up(place - away, step).start()

        @pl.when(place + away < count)
        def _():
            down(place + away, step).wait_recv()

        @pl.when(jnp.logical_and(place + away < count, place > 0))
        def _():
            down(place + away, step).start()

        return carry

    for low, high, phase in sums.moments((count - 1) * steps):
        lax.fori_loop(low, high, pass_on, 0)
        sums.advance(phase)

    def drain(index, carry):
        owner, step = index // steps, lax.rem(index, steps)

        @pl.when(jnp.logical_and(owner <= place, place < count - 1))
        def _():
            up(owner, step).wait_send()

        @pl.when(jnp.logical_and(owner >= place, place > 0))
        def _():
            down(owner, step).wait_send()

        return carry

    lax.fori_loop(0, count * steps, drain, 0)
    sums.finish()


def line_gather(own, call_id, items=()):
    rows, width = own.shape
    count, count_dp = lax.axis_size("mp"), lax.axis_size("dp")
    steps = 8
    sems = pltpu.SemaphoreType.DMA((count, steps))
    items, shapes, shares = piece_shapes(items)
    extra = len(items)
    scratch = PieceSums.scratch(count_dp, shapes)
    limit = room(items, shares, room_of(scratch)) + 2 * rows * count * width * 4
    results = pl.pallas_call(
        partial(line_gather_kernel, count, count_dp, extra),
        out_shape=[jax.ShapeDtypeStruct((rows * count, width), jnp.float32)] + shares,
        in_specs=[VMEM_SPEC] * (1 + extra),
        out_specs=[VMEM_SPEC] * (1 + len(shares)),
        scratch_shapes=[sems] * 4 + scratch,
        compiler_params=pltpu.CompilerParams(
            collective_id=call_id, has_side_effects=True, vmem_limit_bytes=limit
        ),
        cost_estimate=pl.CostEstimate(
            flops=rows * width, bytes_accessed=250 * rows * width * count, transcendentals=0
        ),
    )(own, *items)
    return results[0], results[1:]


def dot(left, right, left_dim=1, right_dim=0):
    return lax.dot_general(
        left, right, (((left_dim,), (right_dim,)), ((), ())), preferred_element_type=jnp.float32
    )


def head_mask(width, copies):
    lane = lax.broadcasted_iota(jnp.int32, (1, width), 1)
    return [lane // HEAD_DIM == head for head in range(copies)]


def spread_heads(values):
    masks = head_mask(values.shape[1], values.shape[1] // HEAD_DIM)
    return jnp.concatenate([jnp.where(mask, values, jnp.zeros_like(values)) for mask in masks], 0)


def join_heads(values, heads):
    rows = values.shape[0] // heads
    masks = head_mask(values.shape[1], heads)
    return sum(
        jnp.where(mask, values[head * rows : (head + 1) * rows], 0.0)
        for head, mask in enumerate(masks)
    )


def split_three(values):
    first = values.astype(jnp.bfloat16)
    left = values - first.astype(jnp.float32)
    second = left.astype(jnp.bfloat16)
    third = (left - second.astype(jnp.float32)).astype(jnp.bfloat16)
    return first, second, third


def norm_rows(values):
    centered = values - jnp.mean(values, -1, keepdims=True)
    scale = lax.rsqrt(jnp.mean(centered * centered, -1, keepdims=True) + 1e-05)
    return centered * scale, scale


def norm_rows_back(upstream, gain, normed, scale):
    inner = upstream * gain
    return scale * (
        inner
        - jnp.mean(inner, -1, keepdims=True)
        - normed * jnp.mean(inner * normed, -1, keepdims=True)
    )


def embed(noisy, pixels, place):
    stacked = jnp.concatenate(split_three(noisy), 0)
    return dot(stacked, jnp.concatenate([pixels] * 3, 0), 0, 0) + place


def read_forward_kernel(
    noisy_ref,
    keep_ref,
    place_ref,
    pixels_ref,
    latents_ref,
    wide_gain_ref,
    gain_ref,
    query_weight_ref,
    pair_weight_ref,
    out_weight_ref,
    part_ref,
    pairs_ref,
    output_ref,
    total_ref,
    queries_ref,
):
    heads = query_weight_ref.shape[2] // HEAD_DIM

    @pl.when(pl.program_id(0) == 0)
    def _():
        normed, _ = norm_rows(latents_ref[...].astype(jnp.float32))
        low = (normed * wide_gain_ref[...]).astype(jnp.bfloat16)
        queries = dot(low, query_weight_ref[0]).astype(jnp.bfloat16)
        queries_ref[...] = spread_heads(queries * jnp.bfloat16(HEAD_DIM ** (-0.5)))

    normed, _ = norm_rows(embed(noisy_ref[0], pixels_ref[...], place_ref[...]))
    side = (normed * gain_ref[...]).astype(jnp.bfloat16)
    keys = dot(side, pair_weight_ref[0]).astype(jnp.bfloat16)
    values = dot(side, pair_weight_ref[1]).astype(jnp.bfloat16)
    pairs_ref[0, 0] = keys
    pairs_ref[0, 1] = values
    scores = dot(keys, queries_ref[...], 1, 1)
    scores = jnp.where(keep_ref[0] > 0, scores, -1e30)
    top = jnp.max(scores, 0, keepdims=True)
    grown = jnp.exp(scores - top)
    summed = jnp.sum(grown, 0, keepdims=True)
    total_ref[0] = top + jnp.log(summed)
    probs = (grown / summed).astype(jnp.bfloat16)
    output = join_heads(dot(probs, values, 0, 0), heads).astype(jnp.bfloat16)
    output_ref[0] = output
    part_ref[...] = dot(output, out_weight_ref[0])


def whole(shape):
    return pl.BlockSpec(shape, lambda b: (0,) * len(shape))


def each(shape):
    return pl.BlockSpec((1,) + shape, lambda b: (b,) + (0,) * len(shape))


def slot_of(shape, slot):
    return pl.BlockSpec(shape, lambda b: (slot,) + (0,) * (len(shape) - 1))


def read_forward(noisy, keep, place, pixels, latents, wide_gain, gain, wide, narrow, wideout):
    images, _, patches = noisy.shape
    count, d_lat = latents.shape
    d_if, local = narrow.shape[1:]
    stacked = local // HEAD_DIM * count
    return pl.pallas_call(
        read_forward_kernel,
        grid=(images,),
        out_shape=[
            jax.ShapeDtypeStruct((images * count, d_lat), jnp.float32),
            jax.ShapeDtypeStruct((images, 2, patches, local), jnp.bfloat16),
            jax.ShapeDtypeStruct((images, count, local), jnp.bfloat16),
            jax.ShapeDtypeStruct((images, 1, stacked), jnp.float32),
            jax.ShapeDtypeStruct((stacked, local), jnp.bfloat16),
        ],
        in_specs=[
            each(noisy.shape[1:]),
            each((patches, 1)),
            whole((patches, d_if)),
            whole(pixels.shape),
            whole(latents.shape),
            whole((1, d_lat)),
            whole((1, d_if)),
            slot_of((1, d_lat, local), 0),
            slot_of((2, d_if, local), 0),
            slot_of((1, local, d_lat), 0),
        ],
        out_specs=[
            pl.BlockSpec((count, d_lat), lambda b: (b, 0)),
            each((2, patches, local)),
            each((count, local)),
            each((1, stacked)),
            whole((stacked, local)),
        ],
        compiler_params=pltpu.CompilerParams(vmem_limit_bytes=40 << 20),
        cost_estimate=pl.CostEstimate(
            flops=10**10, bytes_accessed=30 * 10**6, transcendentals=2 * 10**6
        ),
    )(noisy, keep, place, pixels, latents, wide_gain, gain, wide, narrow, wideout)


def read_backward_kernel(
    noisy_ref,
    keep_ref,
    place_ref,
    pixels_ref,
    latents_ref,
    wide_gain_ref,
    gain_ref,
    query_weight_ref,
    pair_weight_ref,
    out_weight_ref,
    pairs_ref,
    output_ref,
    total_ref,
    queries_ref,
    grad_ref,
    lead_ref,
    query_grad_ref,
    key_grad_ref,
    value_grad_ref,
    out_grad_ref,
    latents_grad_ref,
    wide_gain_grad_ref,
    gain_grad_ref,
    embed_grad_ref,
    low_ref,
    returned_ref,
):
    step, steps = pl.program_id(0), pl.num_programs(0)
    heads = query_weight_ref.shape[2] // HEAD_DIM

    @pl.when(step == 0)
    def _():
        normed, _ = norm_rows(latents_ref[...].astype(jnp.float32))
        low_ref[...] = (normed * wide_gain_ref[...]).astype(jnp.bfloat16)
        for ref in (
            query_grad_ref,
            key_grad_ref,
            value_grad_ref,
            out_grad_ref,
            latents_grad_ref,
            gain_grad_ref,
            embed_grad_ref,
            returned_ref,
        ):
            ref[...] = jnp.zeros_like(ref)

    normed, scale = norm_rows(embed(noisy_ref[0], pixels_ref[...], place_ref[...]))
    side = (normed * gain_ref[...]).astype(jnp.bfloat16)
    keys, values, queries = pairs_ref[0, 0], pairs_ref[0, 1], queries_ref[...]
    branch = grad_ref[...].astype(jnp.bfloat16)
    latents_grad_ref[...] += lead_ref[...] * grad_ref[...]
    out_grad_ref[...] += dot(branch, output_ref[0], 0, 0)
    upstream = spread_heads(dot(branch, out_weight_ref[0], 1, 1).astype(jnp.bfloat16))
    scores = dot(keys, queries, 1, 1)
    scores = jnp.where(keep_ref[0] > 0, scores, -1e30)
    probs = jnp.exp(scores - total_ref[0])
    value_grad = dot(probs.astype(jnp.bfloat16), upstream).astype(jnp.bfloat16)
    prob_grad = dot(values, upstream, 1, 1)
    inner = jnp.sum(prob_grad * probs, 0, keepdims=True)
    score_grad = (probs * (prob_grad - inner)).astype(jnp.bfloat16)
    key_grad = dot(score_grad, queries).astype(jnp.bfloat16)
    query_grad = join_heads(dot(score_grad, keys, 0, 0), heads) * HEAD_DIM ** (-0.5)
    query_grad = query_grad.astype(jnp.bfloat16)
    query_grad_ref[...] += dot(low_ref[...], query_grad, 0, 0)
    returned_ref[...] += dot(query_grad, query_weight_ref[0], 1, 1)
    key_grad_ref[...] += dot(side, key_grad, 0, 0)
    value_grad_ref[...] += dot(side, value_grad, 0, 0)
    side_grad = dot(key_grad, pair_weight_ref[0], 1, 1) + dot(value_grad, pair_weight_ref[1], 1, 1)
    gain_grad_ref[...] += jnp.sum(side_grad * normed, 0, keepdims=True)
    back = norm_rows_back(side_grad, gain_ref[...], normed, scale)
    embed_grad_ref[...] += embed_back(noisy_ref[0], back)

    @pl.when(step == steps - 1)
    def _():
        normed, scale = norm_rows(latents_ref[...].astype(jnp.float32))
        returned = returned_ref[...]
        wide_gain_grad_ref[...] = jnp.sum(returned * normed, 0, keepdims=True)
        latents_grad_ref[...] += norm_rows_back(returned, wide_gain_ref[...], normed, scale)


def embed_back(noisy, back):
    first, second, _ = split_three(noisy)
    high = back.astype(jnp.bfloat16)
    low = (back - high.astype(jnp.float32)).astype(jnp.bfloat16)
    rows = noisy.shape[0]
    both = dot(jnp.concatenate([first, second], 0), high)
    return both[:rows] + both[rows:] + dot(first, low)


def read_backward(
    noisy,
    keep,
    place,
    pixels,
    latents,
    wide_gain,
    gain,
    wide,
    narrow,
    wideout,
    pairs,
    output,
    total,
    queries,
    grad,
    lead,
):
    images, rows, patches = noisy.shape
    count, d_lat = latents.shape
    d_if, local = narrow.shape[1:]
    stacked = local // HEAD_DIM * count
    results = [
        (d_lat, local),
        (d_if, local),
        (d_if, local),
        (d_lat, local),
        (count, d_lat),
        (1, d_lat),
        (1, d_if),
        (rows, d_if),
    ]
    return pl.pallas_call(
        read_backward_kernel,
        grid=(images,),
        out_shape=[jax.ShapeDtypeStruct(shape, jnp.float32) for shape in results],
        in_specs=[
            each(noisy.shape[1:]),
            each((patches, 1)),
            whole((patches, d_if)),
            whole(pixels.shape),
            whole(latents.shape),
            whole((1, d_lat)),
            whole((1, d_if)),
            slot_of((1, d_lat, local), 0),
            slot_of((2, d_if, local), 0),
            slot_of((1, local, d_lat), 0),
            each((2, patches, local)),
            each((count, local)),
            each((1, stacked)),
            whole((stacked, local)),
            pl.BlockSpec((count, d_lat), lambda b: (b, 0)),
            whole((1, 1)),
        ],
        out_specs=[whole(shape) for shape in results],
        scratch_shapes=[
            pltpu.VMEM((count, d_lat), jnp.bfloat16),
            pltpu.VMEM((count, d_lat), jnp.float32),
        ],
        compiler_params=pltpu.CompilerParams(vmem_limit_bytes=48 << 20),
        cost_estimate=pl.CostEstimate(
            flops=2 * 10**10, bytes_accessed=30 * 10**6, transcendentals=2 * 10**6
        ),
    )(
        noisy,
        keep,
        place,
        pixels,
        latents,
        wide_gain,
        gain,
        wide,
        narrow,
        wideout,
        pairs,
        output,
        total,
        queries,
        grad,
        lead,
    )


def rows_of(rows, width):
    return pl.BlockSpec((rows, width), lambda b: (b, 0))


def attend_few(keys, values, queries):
    scores = dot(keys, queries, 1, 1)
    top = jnp.max(scores, 0, keepdims=True)
    grown = jnp.exp(scores - top)
    summed = jnp.sum(grown, 0, keepdims=True)
    probs = (grown / summed).astype(jnp.bfloat16)
    return dot(probs, values, 0, 0), top + jnp.log(summed)


def scaled_heads(queries):
    return spread_heads(queries * jnp.bfloat16(HEAD_DIM ** (-0.5)))


def self_forward_kernel(
    latent_ref, gain_ref, q_ref, k_ref, v_ref, out_weight_ref, part_ref, triple_ref, output_ref, total_ref, low_ref
):
    heads = q_ref.shape[2] // HEAD_DIM
    normed, _ = norm_rows(latent_ref[...])
    low = (normed * gain_ref[...]).astype(jnp.bfloat16)
    low_ref[...] = low
    queries, keys, values = (dot(low, ref[0]).astype(jnp.bfloat16) for ref in (q_ref, k_ref, v_ref))
    for index, item in enumerate((queries, keys, values)):
        triple_ref[0, index] = item
    output, total_ref[0] = attend_few(keys, values, scaled_heads(queries))
    output = join_heads(output, heads).astype(jnp.bfloat16)
    output_ref[0] = output
    part_ref[...] = dot(output, out_weight_ref[0])


def self_forward(latent, gain, wide, wideout, images):
    total, d_lat = latent.shape
    count, local = total // images, wide.shape[2]
    stacked = local // HEAD_DIM * count
    return pl.pallas_call(
        self_forward_kernel,
        grid=(images,),
        out_shape=[
            jax.ShapeDtypeStruct((total, d_lat), jnp.float32),
            jax.ShapeDtypeStruct((images, 3, count, local), jnp.bfloat16),
            jax.ShapeDtypeStruct((images, count, local), jnp.bfloat16),
            jax.ShapeDtypeStruct((images, 1, stacked), jnp.float32),
            jax.ShapeDtypeStruct((total, d_lat), jnp.bfloat16),
        ],
        in_specs=[rows_of(count, d_lat), whole((1, d_lat))]
        + [slot_of((1, d_lat, local), slot) for slot in (1, 2, 3)]
        + [slot_of((1, local, d_lat), 1)],
        out_specs=[
            rows_of(count, d_lat),
            each((3, count, local)),
            each((count, local)),
            each((1, stacked)),
            rows_of(count, d_lat),
        ],
        compiler_params=pltpu.CompilerParams(vmem_limit_bytes=20 << 20),
        cost_estimate=pl.CostEstimate(
            flops=3 * 10**9, bytes_accessed=12 * 10**6, transcendentals=3 * 10**5
        ),
    )(latent, gain, wide, wide, wide, wideout)


def self_backward_kernel(
    grad_ref,
    latent_ref,
    gain_ref,
    q_ref,
    k_ref,
    v_ref,
    out_weight_ref,
    triple_ref,
    output_ref,
    total_ref,
    low_ref,
    part_ref,
    q_grad_ref,
    k_grad_ref,
    v_grad_ref,
    out_grad_ref,
    gain_grad_ref,
    branches,
    outputs,
    grads,
    lows,
):
    step, steps = pl.program_id(0), pl.num_programs(0)
    heads = q_ref.shape[2] // HEAD_DIM
    count = grad_ref.shape[0]
    mine = pl.ds(pl.multiple_of(step * count, count), count)
    normed, scale = norm_rows(latent_ref[...])
    branch = grad_ref[...].astype(jnp.bfloat16)
    branches[mine] = branch
    outputs[mine] = output_ref[0]
    lows[mine] = low_ref[...]
    upstream = spread_heads(dot(branch, out_weight_ref[0], 1, 1).astype(jnp.bfloat16))
    keys, values = triple_ref[0, 1], triple_ref[0, 2]
    queries = scaled_heads(triple_ref[0, 0])
    probs = jnp.exp(dot(keys, queries, 1, 1) - total_ref[0])
    value_grad = dot(probs.astype(jnp.bfloat16), upstream).astype(jnp.bfloat16)
    prob_grad = dot(values, upstream, 1, 1)
    inner = jnp.sum(prob_grad * probs, 0, keepdims=True)
    score_grad = (probs * (prob_grad - inner)).astype(jnp.bfloat16)
    key_grad = dot(score_grad, queries).astype(jnp.bfloat16)
    query_grad = join_heads(dot(score_grad, keys, 0, 0), heads) * HEAD_DIM ** (-0.5)
    query_grad = query_grad.astype(jnp.bfloat16)
    part = (
        dot(query_grad, q_ref[0], 1, 1)
        + dot(key_grad, k_ref[0], 1, 1)
        + dot(value_grad, v_ref[0], 1, 1)
    )
    for index, item in enumerate((query_grad, key_grad, value_grad)):
        grads[index, mine] = item
    gain_part = jnp.sum(part * normed, 0, keepdims=True)
    gain_grad_ref[...] = gain_part + jnp.where(step == 0, 0.0, gain_grad_ref[...])
    part_ref[...] = norm_rows_back(part, gain_ref[...], normed, scale)

    @pl.when(step == steps - 1)
    def _():
        turned = lows[...].T
        for index, ref in enumerate((q_grad_ref, k_grad_ref, v_grad_ref)):
            ref[...] = dot(turned, grads[index])
        out_grad_ref[...] = dot(branches[...], outputs[...], 0, 0)


def self_backward(grad, latent, gain, wide, wideout, triple, output, total, low):
    rows, d_lat = latent.shape
    images, _, count, local = triple.shape
    stacked = local // HEAD_DIM * count
    weight = jax.ShapeDtypeStruct((d_lat, local), jnp.float32)
    return pl.pallas_call(
        self_backward_kernel,
        grid=(images,),
        out_shape=[jax.ShapeDtypeStruct((rows, d_lat), jnp.float32)]
        + [weight] * 4
        + [jax.ShapeDtypeStruct((1, d_lat), jnp.float32)],
        in_specs=[rows_of(count, d_lat), rows_of(count, d_lat), whole((1, d_lat))]
        + [slot_of((1, d_lat, local), slot) for slot in (1, 2, 3)]
        + [
            slot_of((1, local, d_lat), 1),
            each((3, count, local)),
            each((count, local)),
            each((1, stacked)),
            rows_of(count, d_lat),
        ],
        out_specs=[rows_of(count, d_lat)] + [whole((d_lat, local))] * 4 + [whole((1, d_lat))],
        scratch_shapes=[
            pltpu.VMEM((rows, d_lat), jnp.bfloat16),
            pltpu.VMEM((rows, local), jnp.bfloat16),
            pltpu.VMEM((3, rows, local), jnp.bfloat16),
            pltpu.VMEM((rows, d_lat), jnp.bfloat16),
        ],
        compiler_params=pltpu.CompilerParams(vmem_limit_bytes=28 << 20),
        cost_estimate=pl.CostEstimate(
            flops=6 * 10**9, bytes_accessed=16 * 10**6, transcendentals=3 * 10**5
        ),
    )(grad, latent, gain, wide, wide, wide, wideout, triple, output, total, low)


def feed_forward_kernel(
    latent_ref, gain_ref, up_ref, down_ref, part_ref, active_ref, slope_ref, low_ref
):
    @pl.when(pl.program_id(0) == 0)
    def _():
        normed, _ = norm_rows(latent_ref[...])
        low_ref[...] = (normed * gain_ref[...]).astype(jnp.bfloat16)

    hidden = dot(low_ref[...], up_ref[0])
    share = 0.5 * (1.0 + lax.erf(hidden * math.sqrt(0.5)))
    density = jnp.exp(-0.5 * hidden * hidden) * (1.0 / math.sqrt(2.0 * math.pi))
    active = (hidden * share).astype(jnp.bfloat16)
    active_ref[0] = active
    slope_ref[0] = share + hidden * density
    part = dot(active, down_ref[0])

    @pl.when(pl.program_id(0) == 0)
    def _():
        part_ref[...] = part

    @pl.when(pl.program_id(0) > 0)
    def _():
        part_ref[...] += part


def feed_forward(latent, gain, wide, wideout):
    rows, d_lat = latent.shape
    local = wide.shape[2]
    return pl.pallas_call(
        feed_forward_kernel,
        grid=(4,),
        out_shape=[
            jax.ShapeDtypeStruct((rows, d_lat), jnp.float32),
            jax.ShapeDtypeStruct((4, rows, local), jnp.bfloat16),
            jax.ShapeDtypeStruct((4, rows, local), jnp.float32),
            jax.ShapeDtypeStruct((rows, d_lat), jnp.bfloat16),
        ],
        in_specs=[
            whole((rows, d_lat)),
            whole((1, d_lat)),
            pl.BlockSpec((1, d_lat, local), lambda s: (4 + s, 0, 0)),
            pl.BlockSpec((1, local, d_lat), lambda s: (2 + s, 0, 0)),
        ],
        out_specs=[
            whole((rows, d_lat)),
            each((rows, local)),
            each((rows, local)),
            whole((rows, d_lat)),
        ],
        compiler_params=pltpu.CompilerParams(vmem_limit_bytes=24 << 20),
        cost_estimate=pl.CostEstimate(
            flops=4 * 10**9, bytes_accessed=14 * 10**6, transcendentals=10**6
        ),
    )(latent, gain, wide, wideout)


def feed_backward_kernel(
    grad_ref,
    latent_ref,
    gain_ref,
    up_ref,
    down_ref,
    active_ref,
    slope_ref,
    low_ref,
    part_ref,
    up_first_ref,
    up_last_ref,
    down_grad_ref,
    gain_grad_ref,
    branch,
    branch_turned,
    low_turned,
    total,
):
    step, steps = pl.program_id(0), pl.num_programs(0)

    @pl.when(step == 0)
    def _():
        low = grad_ref[...].astype(jnp.bfloat16)
        branch[...] = low
        branch_turned[...] = low.T
        low_turned[...] = low_ref[...].T
        total[...] = jnp.zeros_like(total)

    active_grad = dot(branch[...], down_ref[0], 1, 1)
    hidden_grad = (active_grad * slope_ref[0]).astype(jnp.bfloat16)
    down_grad_ref[0] = dot(branch_turned[...], active_ref[0])
    total[...] += dot(hidden_grad, up_ref[0], 1, 1)
    up_grad = dot(low_turned[...], hidden_grad)

    @pl.when(step < 2)
    def _():
        up_first_ref[0] = up_grad

    @pl.when(step >= 2)
    def _():
        up_last_ref[0] = up_grad

    @pl.when(step == steps - 1)
    def _():
        normed, scale = norm_rows(latent_ref[...])
        part = total[...]
        gain_grad_ref[...] = jnp.sum(part * normed, 0, keepdims=True)
        part_ref[...] = norm_rows_back(part, gain_ref[...], normed, scale)


def feed_backward(grad, latent, gain, wide, wideout, active, slope, low):
    rows, d_lat = latent.shape
    local = wide.shape[2]
    return pl.pallas_call(
        feed_backward_kernel,
        grid=(4,),
        out_shape=[
            jax.ShapeDtypeStruct((rows, d_lat), jnp.float32),
            jax.ShapeDtypeStruct((2, d_lat, local), jnp.float32),
            jax.ShapeDtypeStruct((2, d_lat, local), jnp.float32),
            jax.ShapeDtypeStruct((4, d_lat, local), jnp.float32),
            jax.ShapeDtypeStruct((1, d_lat), jnp.float32),
        ],
        in_specs=[
            whole((rows, d_lat)),
            whole((rows, d_lat)),
            whole((1, d_lat)),
            pl.BlockSpec((1, d_lat, local), lambda s: (4 + s, 0, 0)),
            pl.BlockSpec((1, local, d_lat), lambda s: (2 + s, 0, 0)),
            each((rows, local)),
            each((rows, local)),
            whole((rows, d_lat)),
        ],
        out_specs=[
            whole((rows, d_lat)),
            pl.BlockSpec((1, d_lat, local), lambda s: (jnp.minimum(s, 1), 0, 0)),
            pl.BlockSpec((1, d_lat, local), lambda s: (jnp.maximum(s - 2, 0), 0, 0)),
            each((d_lat, local)),
            whole((1, d_lat)),
        ],
        scratch_shapes=[
            pltpu.VMEM((rows, d_lat), jnp.bfloat16),
            pltpu.VMEM((d_lat, rows), jnp.bfloat16),
            pltpu.VMEM((d_lat, rows), jnp.bfloat16),
            pltpu.VMEM((rows, d_lat), jnp.float32),
        ],
        compiler_params=pltpu.CompilerParams(vmem_limit_bytes=36 << 20),
        cost_estimate=pl.CostEstimate(
            flops=9 * 10**9, bytes_accessed=26 * 10**6, transcendentals=0
        ),
    )(grad, latent, gain, wide, wideout, active, slope, low)


def adam_update(master, first, second, gradient, scale):
    clipped = gradient * scale
    moment = adam_beta * first + (1.0 - adam_beta) * clipped
    square = adam_beta * second + (1.0 - adam_beta) * clipped * clipped
    fixed_first = moment / (1.0 - adam_beta**STEP)
    fixed_second = square / (1.0 - adam_beta**STEP)
    updated = master - learning_rate * (
        fixed_first / (jnp.sqrt(fixed_second) + adam_eps) + weight_decay * master
    )
    return (updated, moment, square)


def sum_rows(values):
    return jnp.sum(values.reshape(-1, 8, values.shape[-1]), 0)


def closing_kernel(count, count_dp, sizes, *refs):
    refs = list(refs)

    def pull(number):
        taken = refs[:number]
        del refs[:number]
        return taken

    number, finished = sizes
    items, (columns, tile), done = pull(number), pull(2), pull(finished)
    wide_out, narrow_out, turned_out, last_out, latents_out, rest_out, stats = pull(7)
    shares = pull(number)
    sums = PieceSums(count_dp, items, shares, pull(number * (count_dp.bit_length() + 1)))
    (write_share,) = pull(1)
    scatter = LineScatter(count, columns, write_share, pull(4), pull(4))
    small = [Spread("mp", count, *pull(3)) for _ in range(2)]
    over_dp, over_mp = Spread("dp", count_dp, *pull(3)), Spread("mp", count, *pull(3))

    barrier = pltpu.get_barrier_semaphore()
    others = [over_dp.peer(step) for step in range(1, count_dp)]
    others += [over_mp.peer(step) for step in range(1, count)]
    signal_all(barrier, others)
    pl.semaphore_wait(barrier, len(others))

    sums.begin()
    scatter.run(lambda: sums.advance(1))
    for phase in range(2, sums.bits + 1):
        sums.advance(phase)
    for spread, share in zip(small, shares[-2:]):
        spread.held[spread.place] = share[...]
        spread.start()
    scatter.settle()

    self_in_2, self_out, read_query, read_key, read_value, read_out = shares[:6]
    self_in_0, self_in_1 = done[:2]
    up, down = done[2:6], done[6:10]
    lat_rows, if_rows = self_out.shape[0], read_key.shape[0]
    write_key, write_value = (write_share.at[pl.ds(i * lat_rows, lat_rows)] for i in range(2))
    write_query, write_out = (
        write_share.at[pl.ds(2 * lat_rows + i * if_rows, if_rows)] for i in range(2)
    )
    square = 0.0

    def keep(out, gradient, turn=False):
        nonlocal square
        value = gradient[...]
        square = square + sum_rows(value * value)
        out[...] = value.T if turn else value

    wide = [read_query, self_in_0, self_in_1, self_in_2] + up + [write_key, write_value]
    for slot, gradient in enumerate(wide):
        keep(wide_out.at[slot], gradient)
    for slot, gradient in enumerate([read_key, read_value, write_query]):
        keep(narrow_out.at[slot], gradient)
    for slot, gradient in enumerate([read_out, self_out] + down):
        keep(turned_out.at[slot], gradient, True)
    keep(last_out, write_out)
    for spread in small:
        spread.take()
    latents, rest = (spread.total() for spread in small)
    latents_out[...] = latents
    rest_out[...] = rest
    lead = (over_mp.place == 0).astype(jnp.float32)
    local = jnp.sum(square) + lead * (
        jnp.sum(sum_rows(latents * latents)) + jnp.sum(sum_rows(rest * rest))
    )
    lane = lax.broadcasted_iota(jnp.int32, (8, 128), 1)
    value = jnp.where(lane == 0, local, tile[...])
    for spread in (over_dp, over_mp):
        spread.held[spread.place] = value
        spread.start()
        spread.take()
        value = spread.total()
    stats[...] = jnp.where(lane == 0, jnp.sqrt(value), value)
    sums.finish()
    scatter.finish()
    for spread in small + [over_dp, over_mp]:
        spread.finish()


def closing(items, columns, tile, done, call_id):
    items, shapes, shares = piece_shapes(items)
    count, count_dp = lax.axis_size("mp"), lax.axis_size("dp")
    lat_rows, local = done[0].shape
    if_rows = shapes[3][0]
    outs = [
        (10, lat_rows, local),
        (3, if_rows, local),
        (6, local, lat_rows),
        (if_rows, local),
        shapes[-2],
        shapes[-1],
        (8, 128),
    ]
    outs = [jax.ShapeDtypeStruct(shape, jnp.float32) for shape in outs]
    shares = [pltpu.VMEM(item.shape, jnp.float32) for item in shares]
    scratch = (
        shares
        + PieceSums.scratch(count_dp, shapes)
        + [pltpu.VMEM((columns.shape[0] // count, columns.shape[1]), jnp.float32)]
        + LineScatter.scratch(count, columns.shape, 4)
        + Spread.scratch(count, tuple(shapes[-2]))
        + Spread.scratch(count, tuple(shapes[-1]))
        + Spread.scratch(count_dp, tile.shape)
        + Spread.scratch(count, tile.shape)
    )
    here = [*items, columns, tile, *done]
    return pl.pallas_call(
        partial(closing_kernel, count, count_dp, (len(items), len(done))),
        out_shape=outs,
        in_specs=[VMEM_SPEC] * len(here),
        out_specs=[VMEM_SPEC] * len(outs),
        scratch_shapes=scratch,
        compiler_params=pltpu.CompilerParams(
            collective_id=call_id,
            has_side_effects=True,
            vmem_limit_bytes=room(here, outs, room_of(scratch)),
        ),
        cost_estimate=pl.CostEstimate(
            flops=10**7, bytes_accessed=150 * 10**6, transcendentals=0
        ),
    )(*here)


def clip_scale(norm):
    return clip_level / jnp.maximum(norm, clip_level)


def update_kernel(kinds, stats, *refs):
    gradients, refs = refs[:kinds], refs[kinds:]
    states, outs, held = (refs[index * 3 * kinds : (index + 1) * 3 * kinds] for index in range(3))
    sems = refs[9 * kinds]
    lane = lax.broadcasted_iota(jnp.int32, (8, 128), 1)
    first = jnp.logical_and(lane == 0, lax.broadcasted_iota(jnp.int32, (8, 128), 0) == 0)
    scale = jnp.sum(jnp.where(first, clip_scale(stats[...]), 0.0))
    copies = []

    def update(kind, at, gradient):
        refs = [3 * kind + index for index in range(3)]
        results = adam_update(*(states[index][at] for index in refs), gradient, scale)
        for index, result in zip(refs, results):
            held[index][at] = result

    def send(kind, slot):
        for index in range(3 * kind, 3 * kind + 3):
            source, target = held[index], outs[index]
            if slot is not None:
                source, target = source.at[slot], target.at[slot]
            copies.append(pltpu.make_async_copy(source, target, sems.at[len(copies)]))
            copies[-1].start()

    for kind, gradient in enumerate(gradients):
        slots = range(gradient.shape[0]) if len(gradient.shape) == 3 else [None]
        for slot in slots:
            rows, width = states[3 * kind].shape[-2:]
            step = math.gcd(rows, max(8, 8192 // width)) if rows % 8 == 0 else rows
            source = gradient if slot is None else gradient.at[slot]

            def one(index, carry, kind=kind, slot=slot, source=source, step=step, width=width):
                where = pl.ds(pl.multiple_of(index * step, step), step)
                update(kind, (where,) if slot is None else (slot, where), source[where, :width])
                return carry

            lax.fori_loop(0, rows // step, one, 0)
            send(kind, slot)
    for copy in copies:
        copy.wait()


def update_states(stats, gradients, states):
    kinds = len(gradients)
    hbm = pl.BlockSpec(memory_space=pltpu.HBM)
    outs = [jax.ShapeDtypeStruct(item.shape, jnp.float32) for item in states]
    copies = sum(3 * (item.shape[0] if item.ndim == 3 else 1) for item in gradients)
    return pl.pallas_call(
        partial(update_kernel, kinds),
        out_shape=outs,
        in_specs=[VMEM_SPEC] * (1 + kinds + len(states)),
        out_specs=[hbm] * len(states),
        scratch_shapes=[pltpu.VMEM(item.shape, jnp.float32) for item in states]
        + [pltpu.SemaphoreType.DMA((copies,))],
        compiler_params=pltpu.CompilerParams(
            vmem_limit_bytes=room(gradients, states, outs)
        ),
        cost_estimate=pl.CostEstimate(
            flops=2 * 10**7, bytes_accessed=14 * 10**6, transcendentals=0
        ),
    )(stats, *gradients, *states)


def body(
    clean_patches,
    noise_patches,
    timesteps,
    present_mask,
    copy_widein,
    copy_narrowin,
    copy_wideout,
    copy_narrowout,
    copy_latents,
    copy_gains,
    copy_pixels,
    master_widein,
    first_widein,
    second_widein,
    master_narrowin,
    first_narrowin,
    second_narrowin,
    master_wideout,
    first_wideout,
    second_wideout,
    master_narrowout,
    first_narrowout,
    second_narrowout,
    master_latents,
    first_latents,
    second_latents,
    master_gains,
    first_gains,
    second_gains,
    master_pixels,
    first_pixels,
    second_pixels,
):
    images = clean_patches.shape[0]
    patches = clean_patches.shape[2]
    count_mp, count_dp = lax.axis_size("mp"), lax.axis_size("dp")
    mp_index, dp_index = lax.axis_index("mp"), lax.axis_index("dp")
    lead = (mp_index == 0).astype(jnp.float32)
    latents, d_lat = copy_latents.shape
    d_if = copy_gains.shape[1]
    local = copy_widein.shape[2]
    sharers = max(1, count_mp // images)
    own_images = max(1, images // count_mp)
    own_patches, own_latents = patches // sharers, latents // sharers
    first_image = mp_index * own_images // sharers
    share = lax.rem(mp_index, sharers)

    def dp_piece(values, axis):
        size = values.shape[axis] // count_dp
        return lax.dynamic_slice_in_dim(values, dp_index * size, size, axis).astype(jnp.float32)

    key_piece = dp_piece(copy_widein[:, 8], 0)
    value_piece = dp_piece(copy_widein[:, 9], 0)
    query_piece = dp_piece(copy_narrowin[:, 2], 0)
    out_piece = dp_piece(copy_narrowout, 1).T
    gathered = lax.all_gather(
        jnp.concatenate([key_piece, value_piece, query_piece, out_piece], 0), "mp"
    )

    signal = jnp.cos(0.5 * math.pi * (timesteps.astype(jnp.float32) + 0.5) / NSTEPS) ** 2
    noisy = (
        jnp.sqrt(signal)[:, None, None] * clean_patches
        + jnp.sqrt(1.0 - signal)[:, None, None] * noise_patches
    )
    loss_weight = 0.5 + signal
    keep_float = present_mask.astype(jnp.float32)
    weight_here = jnp.sum(loss_weight * PIX * jnp.sum(keep_float, 1))
    gain_rows = copy_gains.astype(jnp.float32)

    def wide_gain(index):
        return gain_rows[2 * index : 2 * index + 2].reshape(-1)

    wide_in = jnp.swapaxes(copy_widein, 0, 1)
    narrow_in = jnp.swapaxes(copy_narrowin, 0, 1)
    place = position_table(patches, d_if)
    read_args = (
        jnp.pad(noisy, ((0, 0), (0, 16 - PIX), (0, 0))),
        keep_float[:, :, None],
        place,
        jnp.pad(copy_pixels[0], ((0, 16 - PIX), (0, 0))),
        copy_latents,
        wide_gain(0)[None],
        gain_rows[8:9],
        wide_in,
        narrow_in,
        copy_wideout,
    )
    read_part, *read_kept = read_forward(*read_args)
    gathered, read_part = lax.optimization_barrier((gathered, read_part))
    gathered = lax.all_gather(gathered, "dp").reshape(count_dp * count_mp, -1, local)
    latent_zero = copy_latents.astype(jnp.float32)
    latent_base = jnp.broadcast_to(latent_zero[None], (images, latents, d_lat))
    latent_one, (weight_tile,) = line_sum(
        read_part, latent_base.reshape(-1, d_lat), 2, tile=jnp.full((8, 128), weight_here)
    )
    weight_total = weight_tile[0, 0]
    self_part, *self_kept = self_forward(
        latent_one, wide_gain(1)[None], wide_in, copy_wideout, images
    )
    latent_two, write_weights = line_sum(
        self_part, latent_one, 3, blocks=(gathered, [d_lat, d_lat, d_if, d_if])
    )
    write_key_weight, write_value_weight, write_query_weight, write_out_weight = write_weights
    feed_part, *feed_kept = feed_forward(latent_two, wide_gain(2)[None], wide_in, copy_wideout)
    own_two = lax.dynamic_slice_in_dim(
        latent_two, mp_index * (own_images * own_latents), own_images * own_latents, 0
    )
    latent_three = (own_two + line_scatter(feed_part, 4)).reshape(own_images, own_latents, d_lat)
    write_norm, write_stats = layer_norm(latent_three, wide_gain(3))
    write_low = write_norm.astype(jnp.bfloat16)

    def own_tokens(values, axis):
        values = lax.dynamic_slice_in_dim(values, first_image, own_images, 0)
        return lax.dynamic_slice_in_dim(values, share * own_patches, own_patches, axis)

    own_noisy, own_noise = own_tokens(noisy, 2), own_tokens(noise_patches, 2)
    own_interface = jnp.einsum(
        "bcp,cd->bpd", own_noisy, copy_pixels[0].astype(jnp.float32), precision=precise
    ) + lax.dynamic_slice_in_dim(place, share * own_patches, own_patches, 0)
    own_keep = own_tokens(keep_float, 1)
    own_weight = lax.dynamic_slice_in_dim(loss_weight, first_image, own_images, 0)

    outer_norm, outer_stats = layer_norm(own_interface, gain_rows[9])
    outer_low = outer_norm.astype(jnp.bfloat16)

    def join(spec, values, weight):
        product = jnp.einsum(spec, values, weight, preferred_element_type=jnp.float32)
        return product.astype(jnp.bfloat16)

    def image_rows(values):
        if sharers == 1:
            return values
        nothing = jnp.where(timesteps[0] > 0, 0.0, -0.0)
        whole = lax.all_gather(values.astype(jnp.float32), "mp", axis=0, tiled=True)
        whole = whole + nothing
        whole = whole.reshape(images, latents, d_lat).astype(jnp.bfloat16)
        return lax.dynamic_slice_in_dim(whole, first_image, own_images, 0)

    write_query = join("bpd,dc->bpc", outer_low, write_query_weight)
    write_key = image_rows(join("bld,dc->blc", write_low, write_key_weight))
    write_value = image_rows(join("bld,dc->blc", write_low, write_value_weight))
    write_out, write_total = attend_forward(write_query, write_key, write_value, None)
    outer = own_interface + jnp.einsum(
        "bpc,dc->bpd", write_out, write_out_weight, preferred_element_type=jnp.float32
    )
    final_norm, final_stats = layer_norm(outer, gain_rows[10])
    final_low = final_norm.astype(jnp.bfloat16)
    predicted = jnp.einsum(
        "bpd,cd->bcp", final_low, copy_pixels[1], preferred_element_type=jnp.float32
    )
    difference = predicted - own_noise
    masked = own_weight[:, None, None] * own_keep[:, None, :] * difference
    loss_local = jnp.sum(masked * difference)
    predict_grad = (2.0 * masked / weight_total).astype(jnp.bfloat16)
    head_grad = jnp.einsum(
        "bcp,bpd->cd", predict_grad, final_low, preferred_element_type=jnp.float32
    )
    final_grad = jnp.einsum(
        "bcp,cd->bpd", predict_grad, copy_pixels[1], preferred_element_type=jnp.float32
    )
    outer_grad, gain_final = norm_back(final_grad, gain_rows[10], final_stats)
    branch_low = outer_grad.astype(jnp.bfloat16)
    narrowout_grad = jnp.einsum(
        "bpd,bpc->dc", branch_low, write_out, preferred_element_type=jnp.float32
    )
    write_upstream = join("bpd,dc->bpc", branch_low, write_out_weight)
    query_grad, key_grad, value_grad = attend_back(
        write_query, write_key, write_value, None, write_total, write_upstream
    )
    write_query_grad = jnp.einsum(
        "bpd,bpc->dc", outer_low, query_grad, preferred_element_type=jnp.float32
    )
    outer_part = jnp.einsum(
        "bpc,dc->bpd", query_grad, write_query_weight, preferred_element_type=jnp.float32
    )

    def row_grad(values):
        if sharers > 1:
            whole = jnp.zeros((images, latents, d_lat), jnp.float32)
            whole = lax.dynamic_update_slice_in_dim(whole, values, first_image, 0)
            values = lax.psum_scatter(
                whole.reshape(images * sharers, own_latents, d_lat),
                "mp",
                scatter_dimension=0,
                tiled=True,
            )
        return values.astype(jnp.bfloat16)

    key_grad, value_grad = row_grad(key_grad), row_grad(value_grad)
    write_key_grad = jnp.einsum(
        "bld,blc->dc", write_low, key_grad, preferred_element_type=jnp.float32
    )
    write_value_grad = jnp.einsum(
        "bld,blc->dc", write_low, value_grad, preferred_element_type=jnp.float32
    )
    write_part = jnp.einsum(
        "blc,dc->bld", key_grad, write_key_weight, preferred_element_type=jnp.float32
    ) + jnp.einsum(
        "blc,dc->bld", value_grad, write_value_weight, preferred_element_type=jnp.float32
    )
    own_grad, gain_write = norm_back(write_part, wide_gain(3), write_stats)
    outer_back, gain_outer = norm_back(outer_part, gain_rows[9], outer_stats)

    latent_grad, (key_share, query_share) = line_gather(
        own_grad.reshape(-1, d_lat), 5, [write_key_grad, write_query_grad]
    )
    outer_back, gain_outer = norm_back(outer_part, gain_rows[9], outer_stats)

    latent_grad, (key_share, query_share) = line_gather(
        own_grad.reshape(-1, d_lat), 5, [write_key_grad, write_query_grad]
    )
    latent_grad = latent_grad.reshape(latent_one.shape)
    outer_back, gain_outer = norm_back(outer_part, gain_rows[9], outer_stats)

    latent_part, up_first, up_last, down_grad, gain_feed = feed_backward(
        latent_grad, latent_two, wide_gain(2)[None], wide_in, copy_wideout, *feed_kept
    )
    latent_grad, five_shares = line_sum(
        latent_part, latent_grad, 6, [write_value_grad, narrowout_grad, up_first]
    )
    latent_part, self_query_grad, self_key_grad, self_value_grad, self_out_grad, gain_self = (
        self_backward(latent_grad, latent_one, wide_gain(1)[None], wide_in, copy_wideout, *self_kept)
    )
    latent_grad, six_shares = line_sum(
        latent_part, latent_grad, 7, [up_last, down_grad, self_query_grad, self_key_grad]
    )
    write_share = jnp.concatenate([key_share, five_shares[0], query_share, five_shares[1]], 0)
    write_columns = jnp.concatenate(jnp.split(write_share, count_mp, 1), 0)
    (
        read_query_grad,
        read_key_grad,
        read_value_grad,
        read_out_grad,
        latent_total,
        gain_read,
        gain_side,
        side_embed,
    ) = read_backward(*read_args, *read_kept, latent_grad, lead.reshape(1, 1))
    embed_grad = side_embed[:PIX] + jnp.einsum(
        "bcp,bpd->cd", own_noisy, outer_grad + outer_back, precision=precise
    )
    gains_grad = jnp.concatenate(
        [
            gain_read.reshape(2, -1),
            gain_self.reshape(2, -1),
            gain_feed.reshape(2, -1),
            gain_write.reshape(2, -1),
            gain_side,
            gain_outer[None],
            gain_final[None],
        ],
        0,
    )

    def dp_pieces(values):
        values = values.reshape(values.shape[0], count_dp, -1)
        return jnp.swapaxes(values, 0, 1)

    low_rows = [gains_grad, embed_grad, head_grad]
    low_rows = [jnp.pad(item, ((0, 16 - item.shape[0]), (0, 0))) for item in low_rows]
    rest = dp_pieces(jnp.concatenate(low_rows, 0))
    rest = jnp.pad(rest, ((0, 0), (0, 0), (0, 128 - rest.shape[2])))
    latents_item = dp_pieces(latent_total)

    *gradients, rest_grad, stats = closing(
        [
            self_value_grad,
            self_out_grad,
            read_query_grad,
            read_key_grad,
            read_value_grad,
            read_out_grad,
            latents_item.reshape(-1, latents_item.shape[2]),
            rest.reshape(-1, rest.shape[2]),
        ],
        write_columns,
        jnp.full((8, 128), loss_local),
        [*six_shares[6:8], *five_shares[2:], *six_shares[:6]],
        8,
    )
    states = (
        *(jnp.swapaxes(item, 0, 1) for item in (master_widein, first_widein, second_widein)),
        *(jnp.swapaxes(item, 0, 1) for item in (master_narrowin, first_narrowin, second_narrowin)),
        master_wideout,
        first_wideout,
        second_wideout,
        *(item.T for item in (master_narrowout, first_narrowout, second_narrowout)),
        master_latents,
        first_latents,
        second_latents,
        master_gains,
        first_gains,
        second_gains,
    )
    results = update_states(stats, [*gradients, rest_grad], states)
    results = [
        jnp.swapaxes(item, 0, 1) if index < 6 or 9 <= index < 12 else item
        for index, item in enumerate(results)
    ]
    lanes = master_pixels.shape[2]
    pixels_grad = jnp.stack([rest_grad[16 : 16 + PIX, :lanes], rest_grad[32 : 32 + PIX, :lanes]])
    results += adam_update(
        master_pixels, first_pixels, second_pixels, pixels_grad, clip_scale(stats[0, 0])
    )
    return (stats[0, 1] / weight_total, stats[0, 0], *results)


def solution(mesh):
    in_specs = (
        P("dp", None, None),
        P("dp", None, None),
        P("dp"),
        P("dp", None),
        P(None, None, "mp"),
        P(None, None, "mp"),
        P(None, "mp", None),
        P("mp", None),
        P(),
        P(),
        P(),
        P("dp", None, "mp"),
        P("dp", None, "mp"),
        P("dp", None, "mp"),
        P("dp", None, "mp"),
        P("dp", None, "mp"),
        P("dp", None, "mp"),
        P(None, "mp", "dp"),
        P(None, "mp", "dp"),
        P(None, "mp", "dp"),
        P("mp", "dp"),
        P("mp", "dp"),
        P("mp", "dp"),
        P(None, "dp"),
        P(None, "dp"),
        P(None, "dp"),
        P(None, "dp"),
        P(None, "dp"),
        P(None, "dp"),
        P(None, None, "dp"),
        P(None, None, "dp"),
        P(None, None, "dp"),
    )
    out_specs = (
        P(),
        P(),
        P("dp", None, "mp"),
        P("dp", None, "mp"),
        P("dp", None, "mp"),
        P("dp", None, "mp"),
        P("dp", None, "mp"),
        P("dp", None, "mp"),
        P(None, "mp", "dp"),
        P(None, "mp", "dp"),
        P(None, "mp", "dp"),
        P("mp", "dp"),
        P("mp", "dp"),
        P("mp", "dp"),
        P(None, "dp"),
        P(None, "dp"),
        P(None, "dp"),
        P(None, "dp"),
        P(None, "dp"),
        P(None, "dp"),
        P(None, None, "dp"),
        P(None, None, "dp"),
        P(None, None, "dp"),
    )
    return jax.shard_map(body, mesh=mesh, in_specs=in_specs, out_specs=out_specs, check_vma=False)
```

```python
from functools import partial
import math

import jax
import jax.numpy as jnp
import numpy as np
from jax import lax
from jax.experimental import pallas as pl
from jax.experimental.pallas import tpu as pltpu
from jax.sharding import PartitionSpec as P

HEAD_DIM = 64
PIX = 12
NSTEPS = 1000
STEP = 10


precise = lax.Precision.HIGHEST
clip_level = 0.01
learning_rate = 0.05
weight_decay = 0.1
adam_beta = 0.5
adam_eps = 1e-08


def layer_norm(values, gain):
    centered = values - jnp.mean(values, -1, keepdims=True)
    scale = lax.rsqrt(jnp.mean(centered * centered, -1, keepdims=True) + 1e-05)
    normed = centered * scale
    return (normed * gain, (normed, scale))


def norm_back(upstream, gain, stats):
    normed, scale = stats
    inner = upstream * gain
    values = scale * (
        inner
        - jnp.mean(inner, -1, keepdims=True)
        - normed * jnp.mean(inner * normed, -1, keepdims=True)
    )
    gain_grad = jnp.sum((upstream * normed).reshape(-1, normed.shape[-1]), 0)
    return (values, gain_grad)


def position_table(count, width):
    place = np.arange(count, dtype=np.float64)[:, None]
    angle = place * 10000.0 ** (-2.0 * np.arange(width // 2) / width)
    return jnp.asarray(np.concatenate([np.sin(angle), np.cos(angle)], -1), jnp.float32)


def positions(count, width):
    place = jnp.arange(count, dtype=jnp.float32)[:, None]
    index = jnp.arange(width // 2, dtype=jnp.float32)[None, :]
    angle = place * jnp.exp(-math.log(10000.0) * 2.0 * index / width)
    return jnp.concatenate([jnp.sin(angle), jnp.cos(angle)], -1)


def split_heads(values):
    return values.reshape(values.shape[:-1] + (values.shape[-1] // HEAD_DIM, HEAD_DIM))


def attend_scores(queries, keys, keep_mask):
    scores = jnp.einsum(
        "bqhe,bkhe->bhqk",
        split_heads(queries),
        split_heads(keys),
        preferred_element_type=jnp.float32,
    ) * HEAD_DIM ** (-0.5)
    if keep_mask is not None:
        scores = jnp.where(keep_mask[:, None, None, :] > 0, scores, -1e30)
    return scores


def attend_forward(queries, keys, values, keep_mask):
    scores = attend_scores(queries, keys, keep_mask)
    top = jnp.max(scores, -1, keepdims=True)
    log_total = top + jnp.log(jnp.sum(jnp.exp(scores - top), -1, keepdims=True))
    probs = jnp.exp(scores - log_total).astype(jnp.bfloat16)
    output = jnp.einsum(
        "bhqk,bkhe->bqhe", probs, split_heads(values), preferred_element_type=jnp.float32
    )
    return (output.reshape(queries.shape).astype(jnp.bfloat16), log_total)


def attend_back(queries, keys, values, keep_mask, log_total, upstream):
    scores = attend_scores(queries, keys, keep_mask)
    probs = jnp.exp(scores - log_total)
    value_grad = jnp.einsum(
        "bhqk,bqhe->bkhe",
        probs.astype(jnp.bfloat16),
        split_heads(upstream),
        preferred_element_type=jnp.float32,
    )
    prob_grad = jnp.einsum(
        "bqhe,bkhe->bhqk",
        split_heads(upstream),
        split_heads(values),
        preferred_element_type=jnp.float32,
    )
    score_grad = (probs * (prob_grad - jnp.sum(prob_grad * probs, -1, keepdims=True))).astype(
        jnp.bfloat16
    )
    query_grad = jnp.einsum(
        "bhqk,bkhe->bqhe", score_grad, split_heads(keys), preferred_element_type=jnp.float32
    ) * HEAD_DIM ** (-0.5)
    key_grad = jnp.einsum(
        "bhqk,bqhe->bkhe", score_grad, split_heads(queries), preferred_element_type=jnp.float32
    ) * HEAD_DIM ** (-0.5)
    return (
        query_grad.reshape(queries.shape).astype(jnp.bfloat16),
        key_grad.reshape(keys.shape),
        value_grad.reshape(values.shape),
    )


MESH_ID = pl.DeviceIdType.MESH
HBM_SPEC = pl.BlockSpec(memory_space=pltpu.HBM)
VMEM_SPEC = pl.BlockSpec(memory_space=pltpu.VMEM)
CHUNKS = 32
VMEM_LIMIT = 56 << 20


def in_hbm(values):
    return pltpu.with_memory_space_constraint(values, pltpu.HBM)


def remote(source, target, send_sem, recv_sem, device):
    return pltpu.make_async_remote_copy(
        src_ref=source,
        dst_ref=target,
        send_sem=send_sem,
        recv_sem=recv_sem,
        device_id=device,
        device_id_type=MESH_ID,
    )


class PieceSums:
    def __init__(self, count, items, outs, scratch):
        self.count, self.items, self.outs = count, items, outs
        self.bits = count.bit_length() - 1
        self.place = lax.axis_index("dp") if items else None
        self.held = []
        for index in range(len(items)):
            self.held.append(scratch[index * (self.bits + 2) : (index + 1) * (self.bits + 2)])

    @staticmethod
    def scratch(count, shapes):
        bits = count.bit_length() - 1
        result = []
        for rows, width in shapes:
            result.append(pltpu.VMEM((count // 2, rows, width), jnp.float32))
            for phase in range(2, bits + 1):
                result.append(
                    pltpu.VMEM((2 * (count >> phase), rows // 2, width), jnp.float32)
                )
            copies = count // 2 + 2 * sum(count >> phase for phase in range(2, bits + 1))
            result += [pltpu.SemaphoreType.DMA((copies,))] * 2
        return result

    def peers(self):
        return [{"dp": self.place ^ (1 << bit)} for bit in range(self.bits)] if self.items else []

    def order(self, half):
        later = list(range(1, self.bits))
        turn = half * (len(later) // 2)
        return later[turn:] + later[:turn]

    def first_copy(self, index, piece):
        item, held = self.items[index], self.held[index]
        other = 1 - (self.place & 1)
        return remote(
            item.at[2 * piece + other],
            held[0].at[piece],
            held[-2].at[piece],
            held[-1].at[piece],
            {"dp": self.place ^ 1},
        )

    def member(self, half, phase, entry, flip):
        bits = self.order(half)
        settled, now, rest = bits[: phase - 2], bits[phase - 2], bits[phase - 1 :]
        piece = 0
        for bit in settled:
            piece = piece | (self.place & (1 << bit))
        own = self.place & (1 << now)
        piece = piece | ((own ^ (1 << now)) if flip else own)
        for position, bit in enumerate(rest):
            if (entry >> position) & 1:
                piece = piece | (1 << bit)
        return piece >> 1

    def later_copy(self, index, half, phase, entry):
        held = self.held[index]
        rows = self.items[index].shape[1] // 2
        size = self.count >> phase
        sem = self.count // 2 + 2 * sum(self.count >> p for p in range(2, phase)) + half * size + entry
        return remote(
            held[0].at[self.member(half, phase, entry, True), pl.ds(half * rows, rows)],
            held[phase - 1].at[half * size + entry],
            held[-2].at[sem],
            held[-1].at[sem],
            {"dp": self.place ^ (1 << self.order(half)[phase - 2])},
        )

    def entries(self, phase):
        return [
            (index, half, entry)
            for index in range(len(self.items))
            for half in range(2)
            for entry in range(self.count >> phase)
        ]

    def begin(self):
        for index in range(len(self.items)):
            for piece in range(self.count // 2):
                self.first_copy(index, piece).start()

    def send(self, phase):
        for index, half, entry in self.entries(phase):
            self.later_copy(index, half, phase, entry).start()

    def advance(self, phase):
        if not self.items:
            return
        if phase == 1:
            own = self.place & 1
            for index, item in enumerate(self.items):
                total = self.held[index][0]
                for piece in range(self.count // 2):
                    self.first_copy(index, piece).wait_recv()
                    add_rows(total.at[piece], total.at[piece], item.at[2 * piece + own])
        else:
            for index, half, entry in self.entries(phase):
                self.later_copy(index, half, phase, entry).wait_recv()
                held, rows = self.held[index], self.items[index].shape[1] // 2
                where = pl.ds(half * rows, rows)
                came = held[phase - 1].at[half * (self.count >> phase) + entry]
                kept = held[0].at[self.member(half, phase, entry, False), where]
                if phase == self.bits:
                    add_rows(self.outs[index].at[where], kept, came)
                else:
                    add_rows(kept, kept, came)
        if phase < self.bits:
            self.send(phase + 1)

    def finish(self):
        for index in range(len(self.items)):
            for piece in range(self.count // 2):
                self.first_copy(index, piece).wait_send()
        for phase in range(2, self.bits + 1):
            for index, half, entry in self.entries(phase):
                self.later_copy(index, half, phase, entry).wait_send()

    def moments(self, total):
        if not self.items:
            return [(0, total, None)]
        marks, low = [], 0
        for phase in range(1, self.bits + 1):
            share = (1 - 0.5 ** (phase - 1)) / (1 - 0.5 ** (self.bits - 1))
            high = total if phase == self.bits else int(total * (0.22 + 0.78 * share))
            marks.append((low, high, phase))
            low = high
        return marks


def add_rows(target, left, right):
    rows, width = target.shape
    step = math.gcd(rows, max(8, 8192 // width))

    def one(index, carry):
        where = pl.ds(pl.multiple_of(index * step, step), step)
        target[where] = left[where] + right[where]
        return carry

    lax.fori_loop(0, rows // step, one, 0)


class Spread:
    def __init__(self, name, count, held, send_sem, recv_sem):
        self.name, self.count, self.held = name, count, held
        self.send_sem, self.recv_sem = send_sem, recv_sem
        self.place = lax.axis_index(name)

    @staticmethod
    def scratch(count, shape):
        sems = pltpu.SemaphoreType.DMA((count,))
        return [pltpu.VMEM((count,) + shape, jnp.float32), sems, sems]

    def peer(self, step):
        return {self.name: lax.rem(self.place + step, self.count)}

    def copy(self, step, slot):
        return remote(
            self.held.at[slot],
            self.held.at[slot],
            self.send_sem.at[step],
            self.recv_sem.at[slot],
            self.peer(step),
        )

    def each(self, action):
        def one(step, carry):
            action(step)
            return carry

        lax.fori_loop(1, self.count, one, 0)

    def start(self):
        self.each(lambda step: self.copy(step, self.place).start())

    def take(self):
        self.each(lambda step: self.copy(step, lax.rem(self.place + step, self.count)).wait_recv())

    def finish(self):
        self.each(lambda step: self.copy(step, self.place).wait_send())

    def total(self):
        return lax.fori_loop(
            1, self.count, lambda slot, carry: carry + self.held[slot], self.held[0]
        )


class Convert:
    def __init__(self, count_mp, steps, blocks, outs, buffer, sems):
        self.count_mp, self.blocks, self.outs = count_mp, blocks, outs
        self.buffer, self.sems = buffer, sems
        self.number = blocks.shape[0]
        self.each = -(-self.number // steps)

    @staticmethod
    def scratch(block):
        return [pltpu.VMEM((3,) + block, jnp.float32), pltpu.SemaphoreType.DMA((3,))]

    def copy(self, index):
        slot = lax.rem(index, 3)
        return pltpu.make_async_copy(
            self.blocks.at[index], self.buffer.at[slot], self.sems.at[slot]
        )

    def begin(self):
        self.copy(0).start()
        self.copy(1).start()

    def one(self, index):
        self.copy(index).wait()

        @pl.when(index + 2 < self.number)
        def _():
            self.copy(index + 2).start()

        block = self.buffer.at[lax.rem(index, 3)]
        local = block.shape[1]
        columns = pl.ds(pl.multiple_of(lax.rem(index, self.count_mp) * local, local), local)
        low = 0
        for out in self.outs:
            rows = out.shape[0] * self.count_mp // self.number
            where = pl.ds(pl.multiple_of(index // self.count_mp * rows, rows), rows)
            out[where, columns] = block[pl.ds(low, rows)].astype(jnp.bfloat16)
            low += rows

    def step(self, index):
        for entry in range(self.each):
            self.one(index * self.each + entry)


def signal_all(barrier, others):
    for other in others:
        pl.semaphore_signal(barrier, inc=1, device_id=other, device_id_type=MESH_ID)


class Stage:
    def __init__(self, sources, held, in_sems, results, targets, out_sems):
        self.loads = [
            pltpu.make_async_copy(source, target, in_sems.at[index])
            for index, (source, target) in enumerate(zip(sources, held))
        ]
        self.stores = [
            pltpu.make_async_copy(source, target, out_sems.at[index])
            for index, (source, target) in enumerate(zip(results, targets))
        ]
        self.stored = []

    def start(self):
        for load in self.loads:
            load.start()

    def wait(self, *indices):
        for index in indices or range(len(self.loads)):
            self.loads[index].wait()

    def store(self, *indices):
        for index in indices:
            self.stores[index].start()
            self.stored.append(index)

    def finish(self):
        self.store(*(index for index in range(len(self.stores)) if index not in self.stored))
        for store in self.stores:
            store.wait()


def staged_kernel(body, counts, *refs):
    refs = list(refs)

    def pull(number):
        taken = refs[:number]
        del refs[:number]
        return taken

    number, raw, results = counts
    sources, raws, targets = pull(number), pull(raw), pull(results)
    held, outs, (in_sems, out_sems) = pull(number), pull(results), pull(2)
    stage = Stage(sources, held, in_sems, outs, targets, out_sems)
    stage.start()
    body(stage, held, raws, outs, refs)
    stage.finish()


def staged(body, inputs, outs, scratch, flops, raw=(), call_id=None, length=0):
    copies = [pltpu.VMEM(item.shape, item.dtype) for item in (*inputs, *outs)]
    sems = [pltpu.SemaphoreType.DMA((max(1, len(group)),)) for group in (inputs, outs)]
    needed = sum(
        math.prod(item.shape) * jnp.dtype(item.dtype).itemsize
        for item in copies + list(scratch)
        if getattr(item, "dtype", None) in (jnp.float32, jnp.bfloat16)
    )
    params = {} if call_id is None else {"collective_id": call_id, "has_side_effects": True}
    results = pl.pallas_call(
        partial(staged_kernel, body, (len(inputs), len(raw), len(outs))),
        out_shape=[pltpu.HBM(item.shape, item.dtype) for item in outs],
        in_specs=[HBM_SPEC] * (len(inputs) + len(raw)),
        out_specs=[HBM_SPEC] * len(outs),
        scratch_shapes=copies + sems + list(scratch),
        compiler_params=pltpu.CompilerParams(vmem_limit_bytes=needed + (6 << 20), **params),
        cost_estimate=pl.CostEstimate(
            flops=flops, bytes_accessed=length * 3_500_000, transcendentals=0
        ),
    )(*(in_hbm(item) for item in (*inputs, *raw)))
    return list(results)


def greet(place, count, others=()):
    barrier = pltpu.get_barrier_semaphore()
    below, above = {"mp": place - 1}, {"mp": place + 1}

    @pl.when(place > 0)
    def _():
        pl.semaphore_signal(barrier, inc=1, device_id=below, device_id_type=MESH_ID)

    @pl.when(place < count - 1)
    def _():
        pl.semaphore_signal(barrier, inc=1, device_id=above, device_id_type=MESH_ID)

    signal_all(barrier, others)
    inside = jnp.logical_and(place > 0, place < count - 1)

    @pl.when(inside)
    def _():
        pl.semaphore_wait(barrier, 2 + len(others))

    @pl.when(jnp.logical_not(inside))
    def _():
        pl.semaphore_wait(barrier, 1 + len(others))


def views(refs, base=3):
    result = []
    for ref in refs:
        if len(ref.shape) == base:
            result.append(ref)
        else:
            result += [ref.at[slot] for slot in range(ref.shape[0])]
    return result


def line_sum_kernel(count, count_dp, extra, tiled, stage, held, blocks, results, scratch):
    refs = list(scratch)

    def pull(number):
        taken = refs[:number]
        del refs[:number]
        return taken

    part_ref, base_ref, tile = held[0], held[1], held[2 + extra :]
    items, outs = views(held[2 : 2 + extra]), views(results[1 : 1 + extra], 2)
    out_ref, tile_out = results[0], results[1 + extra : 1 + extra + tiled]
    wide = results[1 + extra + tiled :]
    converted = len(wide)
    inner, from_away, from_toward, toward_send, away_send, away_recv, toward_recv = pull(7)
    chunks = toward_send.shape[0]
    spread = Spread("dp", count_dp, *pull(3)) if tiled else None
    convert = Convert(count, chunks, blocks[0], wide, *pull(2)) if converted else None
    sums = PieceSums(count_dp, items, outs, refs)
    place = lax.axis_index("mp")
    half = count // 2
    low_side = place < half
    toward = {"mp": jnp.where(low_side, place + 1, place - 1)}
    away = {"mp": jnp.where(low_side, place - 1, place + 1)}
    middle = jnp.logical_or(place == half - 1, place == half)
    outermost = jnp.logical_or(place == 0, place == count - 1)
    rows = part_ref.shape[0] // chunks
    others = [spread.peer(step) for step in range(1, count_dp)] if tiled else sums.peers()
    greet(place, count, others)
    stage.wait()
    if tiled:
        spread.held[spread.place] = tile[0][...]
        spread.start()
    if converted:
        convert.begin()
    sums.begin()

    def window(step):
        return pl.ds(pl.multiple_of(step * rows, rows), rows)

    def push(step, source, inside):
        target = from_toward if inside else from_away
        recv = toward_recv if inside else away_recv
        return remote(
            source.at[window(step)],
            target.at[window(step)],
            toward_send.at[step],
            recv.at[step],
            toward,
        )

    def back(step, source):
        return remote(
            source.at[window(step)],
            from_toward.at[window(step)],
            away_send.at[step],
            toward_recv.at[step],
            away,
        )

    def gather_in(step):
        push(step, part_ref, False).wait_recv()
        inner[window(step)] = part_ref[window(step)] + from_away[window(step)]

    @pl.when(outermost)
    def _():
        def leave(step, carry):
            push(step, part_ref, False).start()
            return carry

        lax.fori_loop(0, chunks, leave, 0)

        def arrive(step, carry):
            push(step, part_ref, True).wait_recv()
            out_ref[window(step)] = from_toward[window(step)] + base_ref[window(step)]
            push(step, part_ref, False).wait_send()
            if converted:
                convert.step(step)
            return carry

        for low, high, phase in sums.moments(chunks):
            lax.fori_loop(low, high, arrive, 0)
            sums.advance(phase)

    lag = 2

    @pl.when(middle)
    def _():
        def finish(step):
            push(step, inner, True).wait_recv()
            push(step, inner, True).wait_send()
            total = inner[window(step)] + from_toward[window(step)]
            inner[window(step)] = total
            back(step, inner).start()
            out_ref[window(step)] = total + base_ref[window(step)]

        def first(step, carry):
            gather_in(step)
            push(step, inner, True).start()
            if converted:
                convert.step(step)
            return carry

        def both(step, carry):
            first(step, carry)
            finish(step - lag)
            return carry

        def last(step, carry):
            finish(step)
            return carry

        def drain(step, carry):
            back(step, inner).wait_send()
            return carry

        lax.fori_loop(0, lag, first, 0)
        for low, high, phase in sums.moments(chunks):
            lax.fori_loop(max(low, lag), high, both, 0)
            if high == chunks:
                lax.fori_loop(chunks - lag, chunks, last, 0)
            sums.advance(phase)
        lax.fori_loop(0, chunks, drain, 0)

    if count > 4:

        @pl.when(jnp.logical_not(jnp.logical_or(middle, outermost)))
        def _():
            def inwards(step, carry):
                gather_in(step)
                push(step, inner, False).start()
                return carry

            def outwards(step, carry):
                push(step, inner, True).wait_recv()
                back(step, from_toward).start()
                out_ref[window(step)] = from_toward[window(step)] + base_ref[window(step)]
                if converted:
                    convert.step(step)
                return carry

            def drain(step, carry):
                push(step, inner, False).wait_send()
                back(step, from_toward).wait_send()
                return carry

            lax.fori_loop(0, chunks, inwards, 0)
            for low, high, phase in sums.moments(chunks):
                lax.fori_loop(low, high, outwards, 0)
                sums.advance(phase)
            lax.fori_loop(0, chunks, drain, 0)

    sums.finish()
    if tiled:
        spread.take()
        tile_out[0][...] = spread.total()
        spread.finish()


def piece_shapes(items):
    count = lax.axis_size("dp")
    items = [item.reshape(item.shape[:-2] + (count, -1, item.shape[-1])) for item in items]
    shapes, shares = [], []
    for item in items:
        shapes += [item.shape[-2:]] * (item.shape[0] if item.ndim == 4 else 1)
        shares.append(jax.ShapeDtypeStruct(item.shape[:-3] + item.shape[-2:], jnp.float32))
    return items, shapes, shares


def line_sum(part, base, call_id, items=(), tile=None, blocks=None):
    shape = part.shape
    items, shapes, shares = piece_shapes(items)
    count, count_dp = lax.axis_size("mp"), lax.axis_size("dp")
    rows, width = part.shape
    buffer = pltpu.VMEM((rows, width), jnp.float32)
    sems = pltpu.SemaphoreType.DMA((CHUNKS,))
    inputs, raw = [part, base, *items], []
    outs = [jax.ShapeDtypeStruct((rows, width), jnp.float32)] + shares
    scratch = [buffer] * 3 + [sems] * 4
    if tile is not None:
        inputs.append(tile)
        outs.append(jax.ShapeDtypeStruct(tile.shape, jnp.float32))
        scratch += Spread.scratch(count_dp, tile.shape)
    if blocks is not None:
        blocks, sizes = blocks
        raw.append(blocks)
        outs += [
            jax.ShapeDtypeStruct((size, count * blocks.shape[2]), jnp.bfloat16) for size in sizes
        ]
        scratch += Convert.scratch(blocks.shape[1:])
    scratch += PieceSums.scratch(count_dp, shapes)
    results = staged(
        partial(line_sum_kernel, count, count_dp, len(items), int(tile is not None)),
        inputs,
        outs,
        scratch,
        4 * rows * width,
        raw,
        call_id,
        55,
    )
    return results[0], results[1:]


class LineScatter:
    def __init__(self, count, part, out, buffers, sems):
        self.count, self.part, self.out = count, part, out
        self.up_acc, self.down_acc, self.from_below, self.from_above = buffers
        self.up_send, self.down_send, self.up_recv, self.down_recv = sems
        self.place = lax.axis_index("mp")
        self.steps = self.up_send.shape[1]
        self.block = part.shape[0] // count
        self.rows = self.block // self.steps

    @staticmethod
    def scratch(count, shape, steps):
        sems = pltpu.SemaphoreType.DMA((count, steps))
        return [pltpu.VMEM(shape, jnp.float32)] * 4 + [sems] * 4

    def window(self, owner, step):
        return pl.ds(pl.multiple_of(owner * self.block + step * self.rows, self.rows), self.rows)

    def up(self, owner, step, source):
        where = self.window(owner, step)
        return remote(
            source.at[where],
            self.from_below.at[where],
            self.up_send.at[owner, step],
            self.up_recv.at[owner, step],
            {"mp": self.place + 1},
        )

    def down(self, owner, step, source):
        where = self.window(owner, step)
        return remote(
            source.at[where],
            self.from_above.at[where],
            self.down_send.at[owner, step],
            self.down_recv.at[owner, step],
            {"mp": self.place - 1},
        )

    def up_turn(self, index):
        place, part = self.place, self.part
        owner, step = self.count - 1 - index // self.steps, lax.rem(index, self.steps)

        @pl.when(jnp.logical_and(owner > place, place == 0))
        def _():
            self.up(owner, step, part).start()

        @pl.when(jnp.logical_and(owner > place, place > 0))
        def _():
            self.up(owner, step, part).wait_recv()
            where = self.window(owner, step)
            self.up_acc[where] = part[where] + self.from_below[where]
            self.up(owner, step, self.up_acc).start()

    def down_turn(self, index):
        place, part, count = self.place, self.part, self.count
        owner, step = index // self.steps, lax.rem(index, self.steps)

        @pl.when(jnp.logical_and(owner < place, place == count - 1))
        def _():
            self.down(owner, step, part).start()

        @pl.when(jnp.logical_and(owner < place, place < count - 1))
        def _():
            self.down(owner, step, part).wait_recv()
            where = self.window(owner, step)
            self.down_acc[where] = part[where] + self.from_above[where]
            self.down(owner, step, self.down_acc).start()

    def run(self, pause=None):
        turns, lag = self.count * self.steps, self.steps

        def staggered(first, second):
            def begin(index, carry):
                first(index)
                return carry

            def both(index, carry):
                first(index)
                second(index - lag)
                return carry

            def end(index, carry):
                second(index)
                return carry

            lax.fori_loop(0, lag, begin, 0)
            if pause is not None:
                pause()
            lax.fori_loop(lag, turns, both, 0)
            lax.fori_loop(turns - lag, turns, end, 0)

        @pl.when(self.place < self.count // 2)
        def _():
            staggered(self.up_turn, self.down_turn)

        @pl.when(self.place >= self.count // 2)
        def _():
            staggered(self.down_turn, self.up_turn)

    def settle(self):
        place, rows = self.place, self.rows

        def one(step, carry):
            where = self.window(place, step)
            mine = pl.ds(pl.multiple_of(step * rows, rows), rows)
            self.out[mine] = self.part[where]

            @pl.when(place > 0)
            def _():
                self.up(place, step, self.part).wait_recv()
                self.out[mine] += self.from_below[where]

            @pl.when(place < self.count - 1)
            def _():
                self.down(place, step, self.part).wait_recv()
                self.out[mine] += self.from_above[where]

            return carry

        lax.fori_loop(0, self.steps, one, 0)

    def finish(self):
        place = self.place

        def one(index, carry):
            owner, step = index // self.steps, lax.rem(index, self.steps)

            @pl.when(owner > place)
            def _():
                self.up(owner, step, self.part).wait_send()

            @pl.when(owner < place)
            def _():
                self.down(owner, step, self.part).wait_send()

            return carry

        lax.fori_loop(0, self.count * self.steps, one, 0)


def line_scatter_kernel(count, stage, held, raws, results, scratch):
    scatter = LineScatter(count, held[0], results[0], scratch[:4], scratch[4:])
    greet(scatter.place, count)
    stage.wait()
    scatter.run()
    scatter.settle()
    scatter.finish()


def line_scatter(part, call_id):
    rows, width = part.shape
    count = lax.axis_size("mp")
    (result,) = staged(
        partial(line_scatter_kernel, count),
        [part],
        [jax.ShapeDtypeStruct((rows // count, width), jnp.float32)],
        LineScatter.scratch(count, (rows, width), 8),
        2 * rows * width,
        call_id=call_id,
        length=33,
    )
    return result


def line_gather_kernel(count, count_dp, extra, stage, held, raws, results, scratch):
    own_ref, out_ref = held[0], results[0]
    items, outs = views(held[1:]), views(results[1:], 2)
    up_send, down_send, up_recv, down_recv = scratch[:4]
    sums = PieceSums(count_dp, items, outs, scratch[4:])
    place = lax.axis_index("mp")
    steps = up_send.shape[1]
    block = own_ref.shape[0]
    rows = block // steps
    below, above = {"mp": place - 1}, {"mp": place + 1}
    greet(place, count, sums.peers())
    stage.wait()
    sums.begin()

    def window(owner, step):
        return pl.ds(pl.multiple_of(owner * block + step * rows, rows), rows)

    def up(owner, step):
        part = out_ref.at[window(owner, step)]
        return remote(part, part, up_send.at[owner, step], up_recv.at[owner, step], above)

    def down(owner, step):
        part = out_ref.at[window(owner, step)]
        return remote(part, part, down_send.at[owner, step], down_recv.at[owner, step], below)

    def begin(step, carry):
        out_ref[window(place, step)] = own_ref[pl.ds(pl.multiple_of(step * rows, rows), rows)]

        @pl.when(place < count - 1)
        def _():
            up(place, step).start()

        @pl.when(place > 0)
        def _():
            down(place, step).start()

        return carry

    lax.fori_loop(0, steps, begin, 0)

    def pass_on(index, carry):
        away, step = 1 + index // steps, lax.rem(index, steps)

        @pl.when(place - away >= 0)
        def _():
            up(place - away, step).wait_recv()

        @pl.when(jnp.logical_and(place - away >= 0, place < count - 1))
        def _():
            up(place - away, step).start()

        @pl.when(place + away < count)
        def _():
            down(place + away, step).wait_recv()

        @pl.when(jnp.logical_and(place + away < count, place > 0))
        def _():
            down(place + away, step).start()

        return carry

    for low, high, phase in sums.moments((count - 1) * steps):
        lax.fori_loop(low, high, pass_on, 0)
        sums.advance(phase)

    def drain(index, carry):
        owner, step = index // steps, lax.rem(index, steps)

        @pl.when(jnp.logical_and(owner <= place, place < count - 1))
        def _():
            up(owner, step).wait_send()

        @pl.when(jnp.logical_and(owner >= place, place > 0))
        def _():
            down(owner, step).wait_send()

        return carry

    lax.fori_loop(0, count * steps, drain, 0)
    sums.finish()


def line_gather(own, call_id, items=()):
    rows, width = own.shape
    count, count_dp = lax.axis_size("mp"), lax.axis_size("dp")
    sems = pltpu.SemaphoreType.DMA((count, 8))
    items, shapes, shares = piece_shapes(items)
    results = staged(
        partial(line_gather_kernel, count, count_dp, len(items)),
        [own, *items],
        [jax.ShapeDtypeStruct((rows * count, width), jnp.float32)] + shares,
        [sems] * 4 + PieceSums.scratch(count_dp, shapes),
        rows * width,
        call_id=call_id,
        length=38,
    )
    return results[0], results[1:]


def dot(left, right, left_dim=1, right_dim=0):
    return lax.dot_general(
        left, right, (((left_dim,), (right_dim,)), ((), ())), preferred_element_type=jnp.float32
    )


def head_mask(width, copies):
    lane = lax.broadcasted_iota(jnp.int32, (1, width), 1)
    return [lane // HEAD_DIM == head for head in range(copies)]


def spread_heads(values):
    masks = head_mask(values.shape[1], values.shape[1] // HEAD_DIM)
    return jnp.concatenate([jnp.where(mask, values, jnp.zeros_like(values)) for mask in masks], 0)


def join_heads(values, heads):
    rows = values.shape[0] // heads
    masks = head_mask(values.shape[1], heads)
    return sum(
        jnp.where(mask, values[head * rows : (head + 1) * rows], 0.0)
        for head, mask in enumerate(masks)
    )


def split_three(values):
    first = values.astype(jnp.bfloat16)
    left = values - first.astype(jnp.float32)
    second = left.astype(jnp.bfloat16)
    third = (left - second.astype(jnp.float32)).astype(jnp.bfloat16)
    return first, second, third


def norm_rows(values):
    centered = values - jnp.mean(values, -1, keepdims=True)
    scale = lax.rsqrt(jnp.mean(centered * centered, -1, keepdims=True) + 1e-05)
    return centered * scale, scale


def norm_rows_back(upstream, gain, normed, scale):
    inner = upstream * gain
    return scale * (
        inner
        - jnp.mean(inner, -1, keepdims=True)
        - normed * jnp.mean(inner * normed, -1, keepdims=True)
    )


def embed(noisy, pixels, place):
    stacked = jnp.concatenate(split_three(noisy), 0)
    return dot(stacked, jnp.concatenate([pixels] * 3, 0), 0, 0) + place


def read_forward_kernel(
    noisy_ref,
    keep_ref,
    place_ref,
    pixels_ref,
    latents_ref,
    wide_gain_ref,
    gain_ref,
    query_weight_ref,
    pair_weight_ref,
    out_weight_ref,
    part_ref,
    pairs_ref,
    output_ref,
    total_ref,
    queries_ref,
):
    heads = query_weight_ref.shape[2] // HEAD_DIM

    @pl.when(pl.program_id(0) == 0)
    def _():
        normed, _ = norm_rows(latents_ref[...].astype(jnp.float32))
        low = (normed * wide_gain_ref[...]).astype(jnp.bfloat16)
        queries = dot(low, query_weight_ref[0]).astype(jnp.bfloat16)
        queries_ref[...] = spread_heads(queries * jnp.bfloat16(HEAD_DIM ** (-0.5)))

    normed, _ = norm_rows(embed(noisy_ref[0], pixels_ref[...], place_ref[...]))
    side = (normed * gain_ref[...]).astype(jnp.bfloat16)
    keys = dot(side, pair_weight_ref[0]).astype(jnp.bfloat16)
    values = dot(side, pair_weight_ref[1]).astype(jnp.bfloat16)
    pairs_ref[0, 0] = keys
    pairs_ref[0, 1] = values
    scores = dot(keys, queries_ref[...], 1, 1)
    scores = jnp.where(keep_ref[0] > 0, scores, -1e30)
    top = jnp.max(scores, 0, keepdims=True)
    grown = jnp.exp(scores - top)
    summed = jnp.sum(grown, 0, keepdims=True)
    total_ref[0] = top + jnp.log(summed)
    probs = (grown / summed).astype(jnp.bfloat16)
    output = join_heads(dot(probs, values, 0, 0), heads).astype(jnp.bfloat16)
    output_ref[0] = output
    part_ref[...] = dot(output, out_weight_ref[0])


def whole(shape):
    return pl.BlockSpec(shape, lambda b: (0,) * len(shape))


def each(shape):
    return pl.BlockSpec((1,) + shape, lambda b: (b,) + (0,) * len(shape))


def slot_of(shape, slot):
    return pl.BlockSpec(shape, lambda b: (slot,) + (0,) * (len(shape) - 1))


def read_forward(noisy, keep, place, pixels, latents, wide_gain, gain, wide, narrow, wideout):
    images, _, patches = noisy.shape
    count, d_lat = latents.shape
    d_if, local = narrow.shape[1:]
    stacked = local // HEAD_DIM * count
    return pl.pallas_call(
        read_forward_kernel,
        grid=(images,),
        out_shape=[
            pltpu.HBM((images * count, d_lat), jnp.float32),
            pltpu.HBM((images, 2, patches, local), jnp.bfloat16),
            pltpu.HBM((images, count, local), jnp.bfloat16),
            pltpu.HBM((images, 1, stacked), jnp.float32),
            pltpu.HBM((stacked, local), jnp.bfloat16),
        ],
        in_specs=[
            each(noisy.shape[1:]),
            each((patches, 1)),
            whole((patches, d_if)),
            whole(pixels.shape),
            whole(latents.shape),
            whole((1, d_lat)),
            whole((1, d_if)),
            slot_of((1, d_lat, local), 0),
            slot_of((2, d_if, local), 0),
            slot_of((1, local, d_lat), 0),
        ],
        out_specs=[
            pl.BlockSpec((count, d_lat), lambda b: (b, 0)),
            each((2, patches, local)),
            each((count, local)),
            each((1, stacked)),
            whole((stacked, local)),
        ],
        compiler_params=pltpu.CompilerParams(vmem_limit_bytes=40 << 20),
        cost_estimate=pl.CostEstimate(
            flops=10**10, bytes_accessed=30 * 10**6, transcendentals=2 * 10**6
        ),
    )(*map(in_hbm, (noisy, keep, place, pixels, latents, wide_gain, gain, wide, narrow, wideout)))


def read_backward_kernel(
    noisy_ref,
    keep_ref,
    place_ref,
    pixels_ref,
    latents_ref,
    wide_gain_ref,
    gain_ref,
    query_weight_ref,
    pair_weight_ref,
    out_weight_ref,
    pairs_ref,
    output_ref,
    total_ref,
    queries_ref,
    grad_ref,
    lead_ref,
    wide_grad_ref,
    narrow_grad_ref,
    latents_grad_ref,
    wide_gain_grad_ref,
    gain_grad_ref,
    embed_grad_ref,
    low_ref,
    returned_ref,
):
    step, steps = pl.program_id(0), pl.num_programs(0)
    heads = query_weight_ref.shape[2] // HEAD_DIM

    @pl.when(step == 0)
    def _():
        normed, _ = norm_rows(latents_ref[...].astype(jnp.float32))
        low_ref[...] = (normed * wide_gain_ref[...]).astype(jnp.bfloat16)
        for ref in (
            wide_grad_ref,
            narrow_grad_ref,
            latents_grad_ref,
            gain_grad_ref,
            embed_grad_ref,
            returned_ref,
        ):
            ref[...] = jnp.zeros_like(ref)

    normed, scale = norm_rows(embed(noisy_ref[0], pixels_ref[...], place_ref[...]))
    side = (normed * gain_ref[...]).astype(jnp.bfloat16)
    keys, values, queries = pairs_ref[0, 0], pairs_ref[0, 1], queries_ref[...]
    branch = grad_ref[...].astype(jnp.bfloat16)
    latents_grad_ref[...] += lead_ref[...] * grad_ref[...]
    wide_grad_ref[1] += dot(branch, output_ref[0], 0, 0)
    upstream = spread_heads(dot(branch, out_weight_ref[0], 1, 1).astype(jnp.bfloat16))
    scores = dot(keys, queries, 1, 1)
    scores = jnp.where(keep_ref[0] > 0, scores, -1e30)
    probs = jnp.exp(scores - total_ref[0])
    value_grad = dot(probs.astype(jnp.bfloat16), upstream).astype(jnp.bfloat16)
    prob_grad = dot(values, upstream, 1, 1)
    inner = jnp.sum(prob_grad * probs, 0, keepdims=True)
    score_grad = (probs * (prob_grad - inner)).astype(jnp.bfloat16)
    key_grad = dot(score_grad, queries).astype(jnp.bfloat16)
    query_grad = join_heads(dot(score_grad, keys, 0, 0), heads) * HEAD_DIM ** (-0.5)
    query_grad = query_grad.astype(jnp.bfloat16)
    wide_grad_ref[0] += dot(low_ref[...], query_grad, 0, 0)
    returned_ref[...] += dot(query_grad, query_weight_ref[0], 1, 1)
    narrow_grad_ref[0] += dot(side, key_grad, 0, 0)
    narrow_grad_ref[1] += dot(side, value_grad, 0, 0)
    side_grad = dot(key_grad, pair_weight_ref[0], 1, 1) + dot(value_grad, pair_weight_ref[1], 1, 1)
    gain_grad_ref[...] += jnp.sum(side_grad * normed, 0, keepdims=True)
    back = norm_rows_back(side_grad, gain_ref[...], normed, scale)
    embed_grad_ref[...] += embed_back(noisy_ref[0], back)

    @pl.when(step == steps - 1)
    def _():
        normed, scale = norm_rows(latents_ref[...].astype(jnp.float32))
        returned = returned_ref[...]
        wide_gain_grad_ref[...] = jnp.sum(returned * normed, 0, keepdims=True)
        latents_grad_ref[...] += norm_rows_back(returned, wide_gain_ref[...], normed, scale)


def embed_back(noisy, back):
    first, second, _ = split_three(noisy)
    high = back.astype(jnp.bfloat16)
    low = (back - high.astype(jnp.float32)).astype(jnp.bfloat16)
    rows = noisy.shape[0]
    both = dot(jnp.concatenate([first, second], 0), high)
    return both[:rows] + both[rows:] + dot(first, low)


def read_backward(
    noisy,
    keep,
    place,
    pixels,
    latents,
    wide_gain,
    gain,
    wide,
    narrow,
    wideout,
    pairs,
    output,
    total,
    queries,
    grad,
    lead,
):
    images, rows, patches = noisy.shape
    count, d_lat = latents.shape
    d_if, local = narrow.shape[1:]
    stacked = local // HEAD_DIM * count
    results = [
        (2, d_lat, local),
        (2, d_if, local),
        (count, d_lat),
        (1, d_lat),
        (1, d_if),
        (rows, d_if),
    ]
    return pl.pallas_call(
        read_backward_kernel,
        grid=(images,),
        out_shape=[pltpu.HBM(shape, jnp.float32) for shape in results],
        in_specs=[
            each(noisy.shape[1:]),
            each((patches, 1)),
            whole((patches, d_if)),
            whole(pixels.shape),
            whole(latents.shape),
            whole((1, d_lat)),
            whole((1, d_if)),
            slot_of((1, d_lat, local), 0),
            slot_of((2, d_if, local), 0),
            slot_of((1, local, d_lat), 0),
            each((2, patches, local)),
            each((count, local)),
            each((1, stacked)),
            whole((stacked, local)),
            pl.BlockSpec((count, d_lat), lambda b: (b, 0)),
            whole((1, 1)),
        ],
        out_specs=[whole(shape) for shape in results],
        scratch_shapes=[
            pltpu.VMEM((count, d_lat), jnp.bfloat16),
            pltpu.VMEM((count, d_lat), jnp.float32),
        ],
        compiler_params=pltpu.CompilerParams(vmem_limit_bytes=48 << 20),
        cost_estimate=pl.CostEstimate(
            flops=2 * 10**10, bytes_accessed=30 * 10**6, transcendentals=2 * 10**6
        ),
    )(*map(in_hbm, (noisy,
        keep,
        place,
        pixels,
        latents,
        wide_gain,
        gain,
        wide,
        narrow,
        wideout,
        pairs,
        output,
        total,
        queries,
        grad,
        lead)))


def rows_of(rows, width):
    return pl.BlockSpec((rows, width), lambda b: (b, 0))


def attend_few(keys, values, queries):
    scores = dot(keys, queries, 1, 1)
    top = jnp.max(scores, 0, keepdims=True)
    grown = jnp.exp(scores - top)
    summed = jnp.sum(grown, 0, keepdims=True)
    probs = (grown / summed).astype(jnp.bfloat16)
    return dot(probs, values, 0, 0), top + jnp.log(summed)


def scaled_heads(queries):
    return spread_heads(queries * jnp.bfloat16(HEAD_DIM ** (-0.5)))


def self_forward_kernel(
    latent_ref, gain_ref, q_ref, k_ref, v_ref, out_weight_ref, part_ref, triple_ref, output_ref, total_ref, low_ref
):
    heads = q_ref.shape[2] // HEAD_DIM
    normed, _ = norm_rows(latent_ref[...])
    low = (normed * gain_ref[...]).astype(jnp.bfloat16)
    low_ref[...] = low
    queries, keys, values = (dot(low, ref[0]).astype(jnp.bfloat16) for ref in (q_ref, k_ref, v_ref))
    for index, item in enumerate((queries, keys, values)):
        triple_ref[0, index] = item
    output, total_ref[0] = attend_few(keys, values, scaled_heads(queries))
    output = join_heads(output, heads).astype(jnp.bfloat16)
    output_ref[0] = output
    part_ref[...] = dot(output, out_weight_ref[0])


def self_forward(latent, gain, wide, wideout, images):
    total, d_lat = latent.shape
    count, local = total // images, wide.shape[2]
    stacked = local // HEAD_DIM * count
    return pl.pallas_call(
        self_forward_kernel,
        grid=(images,),
        out_shape=[
            pltpu.HBM((total, d_lat), jnp.float32),
            pltpu.HBM((images, 3, count, local), jnp.bfloat16),
            pltpu.HBM((images, count, local), jnp.bfloat16),
            pltpu.HBM((images, 1, stacked), jnp.float32),
            pltpu.HBM((total, d_lat), jnp.bfloat16),
        ],
        in_specs=[rows_of(count, d_lat), whole((1, d_lat))]
        + [slot_of((1, d_lat, local), slot) for slot in (1, 2, 3)]
        + [slot_of((1, local, d_lat), 1)],
        out_specs=[
            rows_of(count, d_lat),
            each((3, count, local)),
            each((count, local)),
            each((1, stacked)),
            rows_of(count, d_lat),
        ],
        compiler_params=pltpu.CompilerParams(vmem_limit_bytes=20 << 20),
        cost_estimate=pl.CostEstimate(
            flops=3 * 10**9, bytes_accessed=12 * 10**6, transcendentals=3 * 10**5
        ),
    )(*map(in_hbm, (latent, gain, wide, wide, wide, wideout)))


def self_backward_kernel(
    grad_ref,
    latent_ref,
    gain_ref,
    q_ref,
    k_ref,
    v_ref,
    out_weight_ref,
    triple_ref,
    output_ref,
    total_ref,
    low_ref,
    part_ref,
    first_ref,
    last_ref,
    gain_grad_ref,
    branches,
    outputs,
    grads,
    lows,
):
    step, steps = pl.program_id(0), pl.num_programs(0)
    heads = q_ref.shape[2] // HEAD_DIM
    count = grad_ref.shape[0]
    mine = pl.ds(pl.multiple_of(step * count, count), count)
    normed, scale = norm_rows(latent_ref[...])
    branch = grad_ref[...].astype(jnp.bfloat16)
    branches[mine] = branch
    outputs[mine] = output_ref[0]
    lows[mine] = low_ref[...]
    upstream = spread_heads(dot(branch, out_weight_ref[0], 1, 1).astype(jnp.bfloat16))
    keys, values = triple_ref[0, 1], triple_ref[0, 2]
    queries = scaled_heads(triple_ref[0, 0])
    probs = jnp.exp(dot(keys, queries, 1, 1) - total_ref[0])
    value_grad = dot(probs.astype(jnp.bfloat16), upstream).astype(jnp.bfloat16)
    prob_grad = dot(values, upstream, 1, 1)
    inner = jnp.sum(prob_grad * probs, 0, keepdims=True)
    score_grad = (probs * (prob_grad - inner)).astype(jnp.bfloat16)
    key_grad = dot(score_grad, queries).astype(jnp.bfloat16)
    query_grad = join_heads(dot(score_grad, keys, 0, 0), heads) * HEAD_DIM ** (-0.5)
    query_grad = query_grad.astype(jnp.bfloat16)
    part = (
        dot(query_grad, q_ref[0], 1, 1)
        + dot(key_grad, k_ref[0], 1, 1)
        + dot(value_grad, v_ref[0], 1, 1)
    )
    for index, item in enumerate((query_grad, key_grad, value_grad)):
        grads[index, mine] = item
    gain_part = jnp.sum(part * normed, 0, keepdims=True)
    gain_grad_ref[...] = gain_part + jnp.where(step == 0, 0.0, gain_grad_ref[...])
    part_ref[...] = norm_rows_back(part, gain_ref[...], normed, scale)

    @pl.when(step == steps - 1)
    def _():
        turned = lows[...].T
        first_ref[0] = dot(turned, grads[0])
        first_ref[1] = dot(turned, grads[1])
        last_ref[0] = dot(turned, grads[2])
        last_ref[1] = dot(branches[...], outputs[...], 0, 0)


def self_backward(grad, latent, gain, wide, wideout, triple, output, total, low):
    rows, d_lat = latent.shape
    images, _, count, local = triple.shape
    stacked = local // HEAD_DIM * count
    weight = pltpu.HBM((2, d_lat, local), jnp.float32)
    return pl.pallas_call(
        self_backward_kernel,
        grid=(images,),
        out_shape=[pltpu.HBM((rows, d_lat), jnp.float32)]
        + [weight] * 2
        + [pltpu.HBM((1, d_lat), jnp.float32)],
        in_specs=[rows_of(count, d_lat), rows_of(count, d_lat), whole((1, d_lat))]
        + [slot_of((1, d_lat, local), slot) for slot in (1, 2, 3)]
        + [
            slot_of((1, local, d_lat), 1),
            each((3, count, local)),
            each((count, local)),
            each((1, stacked)),
            rows_of(count, d_lat),
        ],
        out_specs=[rows_of(count, d_lat)] + [whole((2, d_lat, local))] * 2 + [whole((1, d_lat))],
        scratch_shapes=[
            pltpu.VMEM((rows, d_lat), jnp.bfloat16),
            pltpu.VMEM((rows, local), jnp.bfloat16),
            pltpu.VMEM((3, rows, local), jnp.bfloat16),
            pltpu.VMEM((rows, d_lat), jnp.bfloat16),
        ],
        compiler_params=pltpu.CompilerParams(vmem_limit_bytes=28 << 20),
        cost_estimate=pl.CostEstimate(
            flops=6 * 10**9, bytes_accessed=16 * 10**6, transcendentals=3 * 10**5
        ),
    )(*map(in_hbm, (grad, latent, gain, wide, wide, wide, wideout, triple, output, total, low)))


def feed_forward_kernel(
    latent_ref, gain_ref, up_ref, down_ref, part_ref, active_ref, slope_ref, low_ref
):
    @pl.when(pl.program_id(0) == 0)
    def _():
        normed, _ = norm_rows(latent_ref[...])
        low_ref[...] = (normed * gain_ref[...]).astype(jnp.bfloat16)

    hidden = dot(low_ref[...], up_ref[0])
    share = 0.5 * (1.0 + lax.erf(hidden * math.sqrt(0.5)))
    density = jnp.exp(-0.5 * hidden * hidden) * (1.0 / math.sqrt(2.0 * math.pi))
    active = (hidden * share).astype(jnp.bfloat16)
    active_ref[0] = active
    slope_ref[0] = share + hidden * density
    part = dot(active, down_ref[0])

    @pl.when(pl.program_id(0) == 0)
    def _():
        part_ref[...] = part

    @pl.when(pl.program_id(0) > 0)
    def _():
        part_ref[...] += part


def feed_forward(latent, gain, wide, wideout):
    rows, d_lat = latent.shape
    local = wide.shape[2]
    return pl.pallas_call(
        feed_forward_kernel,
        grid=(4,),
        out_shape=[
            pltpu.HBM((rows, d_lat), jnp.float32),
            pltpu.HBM((4, rows, local), jnp.bfloat16),
            pltpu.HBM((4, rows, local), jnp.float32),
            pltpu.HBM((rows, d_lat), jnp.bfloat16),
        ],
        in_specs=[
            whole((rows, d_lat)),
            whole((1, d_lat)),
            pl.BlockSpec((1, d_lat, local), lambda s: (4 + s, 0, 0)),
            pl.BlockSpec((1, local, d_lat), lambda s: (2 + s, 0, 0)),
        ],
        out_specs=[
            whole((rows, d_lat)),
            each((rows, local)),
            each((rows, local)),
            whole((rows, d_lat)),
        ],
        compiler_params=pltpu.CompilerParams(vmem_limit_bytes=24 << 20),
        cost_estimate=pl.CostEstimate(
            flops=4 * 10**9, bytes_accessed=14 * 10**6, transcendentals=10**6
        ),
    )(*map(in_hbm, (latent, gain, wide, wideout)))


def feed_backward_kernel(
    grad_ref,
    latent_ref,
    gain_ref,
    up_ref,
    down_ref,
    active_ref,
    slope_ref,
    low_ref,
    part_ref,
    up_first_ref,
    up_last_ref,
    down_grad_ref,
    gain_grad_ref,
    branch,
    branch_turned,
    low_turned,
    total,
):
    step, steps = pl.program_id(0), pl.num_programs(0)

    @pl.when(step == 0)
    def _():
        low = grad_ref[...].astype(jnp.bfloat16)
        branch[...] = low
        branch_turned[...] = low.T
        low_turned[...] = low_ref[...].T
        total[...] = jnp.zeros_like(total)

    active_grad = dot(branch[...], down_ref[0], 1, 1)
    hidden_grad = (active_grad * slope_ref[0]).astype(jnp.bfloat16)
    down_grad_ref[0] = dot(branch_turned[...], active_ref[0])
    total[...] += dot(hidden_grad, up_ref[0], 1, 1)
    up_grad = dot(low_turned[...], hidden_grad)

    @pl.when(step < 2)
    def _():
        up_first_ref[0] = up_grad

    @pl.when(step >= 2)
    def _():
        up_last_ref[0] = up_grad

    @pl.when(step == steps - 1)
    def _():
        normed, scale = norm_rows(latent_ref[...])
        part = total[...]
        gain_grad_ref[...] = jnp.sum(part * normed, 0, keepdims=True)
        part_ref[...] = norm_rows_back(part, gain_ref[...], normed, scale)


def feed_backward(grad, latent, gain, wide, wideout, active, slope, low):
    rows, d_lat = latent.shape
    local = wide.shape[2]
    return pl.pallas_call(
        feed_backward_kernel,
        grid=(4,),
        out_shape=[
            pltpu.HBM((rows, d_lat), jnp.float32),
            pltpu.HBM((2, d_lat, local), jnp.float32),
            pltpu.HBM((2, d_lat, local), jnp.float32),
            pltpu.HBM((4, d_lat, local), jnp.float32),
            pltpu.HBM((1, d_lat), jnp.float32),
        ],
        in_specs=[
            whole((rows, d_lat)),
            whole((rows, d_lat)),
            whole((1, d_lat)),
            pl.BlockSpec((1, d_lat, local), lambda s: (4 + s, 0, 0)),
            pl.BlockSpec((1, local, d_lat), lambda s: (2 + s, 0, 0)),
            each((rows, local)),
            each((rows, local)),
            whole((rows, d_lat)),
        ],
        out_specs=[
            whole((rows, d_lat)),
            pl.BlockSpec((1, d_lat, local), lambda s: (jnp.minimum(s, 1), 0, 0)),
            pl.BlockSpec((1, d_lat, local), lambda s: (jnp.maximum(s - 2, 0), 0, 0)),
            each((d_lat, local)),
            whole((1, d_lat)),
        ],
        scratch_shapes=[
            pltpu.VMEM((rows, d_lat), jnp.bfloat16),
            pltpu.VMEM((d_lat, rows), jnp.bfloat16),
            pltpu.VMEM((d_lat, rows), jnp.bfloat16),
            pltpu.VMEM((rows, d_lat), jnp.float32),
        ],
        compiler_params=pltpu.CompilerParams(vmem_limit_bytes=36 << 20),
        cost_estimate=pl.CostEstimate(
            flops=9 * 10**9, bytes_accessed=26 * 10**6, transcendentals=0
        ),
    )(*map(in_hbm, (grad, latent, gain, wide, wideout, active, slope, low)))


def write_kernel(stage, held, raws, results, scratch):
    (
        scalars_ref,
        latent_ref,
        noisy_ref,
        noise_ref,
        keep_ref,
        place_ref,
        pixels_ref,
        wide_gain_ref,
        gain_ref,
        key_weight_ref,
        value_weight_ref,
        query_weight_ref,
        out_weight_ref,
    ) = held
    (
        latent_grad_ref,
        key_grad_ref,
        value_grad_ref,
        query_grad_ref,
        out_grad_ref,
        wide_gain_grad_ref,
        gain_grad_ref,
        embed_grad_ref,
        head_grad_ref,
        loss_ref,
    ) = results
    queries, outputs, upstream, query_grads, normed_ref, scale_ref = scratch
    stage.wait(*range(9))
    patches, width = queries.shape
    group = 4 * HEAD_DIM
    groups = width // group
    latents = latent_ref.shape[0]
    rows = 4 * latents
    weight, weight_total = scalars_ref[:1, :1], scalars_ref[:1, 1:2]

    latent_normed, latent_scale = norm_rows(latent_ref[...])
    latent_low = (latent_normed * wide_gain_ref[...]).astype(jnp.bfloat16)
    interface = embed(noisy_ref[...], pixels_ref[0], place_ref[...])
    normed, scale = norm_rows(interface)
    normed_ref[...] = normed
    scale_ref[...] = scale
    outer_low = (normed * gain_ref[1:2]).astype(jnp.bfloat16)
    stage.wait(9, 10)
    keys = dot(latent_low, key_weight_ref[...]).astype(jnp.bfloat16)
    values = dot(latent_low, value_weight_ref[...]).astype(jnp.bfloat16)
    stage.wait(11, 12)
    queries[...] = dot(outer_low, query_weight_ref[...]).astype(jnp.bfloat16)

    def part(values, index):
        return values[:, index * group : (index + 1) * group]

    def by_head(values):
        return values.reshape(4, latents, patches)

    def group_probs(index):
        scores = by_head(dot(scaled_heads(part(keys, index)), part(queries, index), 1, 1))
        grown = jnp.exp(scores - jnp.max(scores, 1, keepdims=True))
        return grown / jnp.sum(grown, 1, keepdims=True)

    for index in range(groups):
        probs = group_probs(index).reshape(rows, patches).astype(jnp.bfloat16)
        output = dot(probs, spread_heads(part(values, index)), 0, 0)
        outputs[:, index * group : (index + 1) * group] = output.astype(jnp.bfloat16)

    outer = interface + dot(outputs[...], out_weight_ref[...], 1, 1)
    final_normed, final_scale = norm_rows(outer)
    final_low = (final_normed * gain_ref[2:3]).astype(jnp.bfloat16)
    head = pixels_ref[1]
    difference = dot(head, final_low, 1, 1) - noise_ref[...]
    masked = weight * keep_ref[...] * difference
    loss_ref[...] = jnp.full(loss_ref.shape, jnp.sum(masked * difference))
    predict_grad = (2.0 * masked / weight_total).astype(jnp.bfloat16)
    head_grad_ref[...] = dot(predict_grad, final_low)
    final_grad = dot(predict_grad, head, 0, 0)
    gain_final = jnp.sum(final_grad * final_normed, 0, keepdims=True)
    outer_grad = norm_rows_back(final_grad, gain_ref[2:3], final_normed, final_scale)
    branch = outer_grad.astype(jnp.bfloat16)
    out_grad_ref[...] = dot(branch, outputs[...], 0, 0)
    stage.store(4)
    upstream[...] = dot(branch, out_weight_ref[...]).astype(jnp.bfloat16)

    key_grads, value_grads = [], []
    for index in range(groups):
        probs = group_probs(index)
        low = probs.reshape(rows, patches).astype(jnp.bfloat16)
        above = part(upstream, index)
        value_grads.append(join_heads(dot(low, above), 4).astype(jnp.bfloat16))
        prob_grad = by_head(dot(spread_heads(part(values, index)), above, 1, 1))
        inner = jnp.sum(prob_grad * probs, 1, keepdims=True)
        score_grad = (probs * (prob_grad - inner)).reshape(rows, patches).astype(jnp.bfloat16)
        key_grad = join_heads(dot(score_grad, part(queries, index)), 4) * HEAD_DIM ** (-0.5)
        key_grads.append(key_grad.astype(jnp.bfloat16))
        query_grad = dot(score_grad, scaled_heads(part(keys, index)), 0, 0)
        query_grads[:, index * group : (index + 1) * group] = query_grad.astype(jnp.bfloat16)
    key_grad, value_grad = (jnp.concatenate(item, 1) for item in (key_grads, value_grads))

    turned = latent_low.T
    key_grad_ref[...] = dot(turned, key_grad)
    value_grad_ref[...] = dot(turned, value_grad)
    stage.store(1, 2)
    latent_part = dot(key_grad, key_weight_ref[...], 1, 1) + dot(
        value_grad, value_weight_ref[...], 1, 1
    )
    wide_gain_grad_ref[...] = jnp.sum(latent_part * latent_normed, 0, keepdims=True)
    latent_grad_ref[...] = norm_rows_back(
        latent_part, wide_gain_ref[...], latent_normed, latent_scale
    )
    normed, scale = normed_ref[...], scale_ref[...]
    outer_low = (normed * gain_ref[1:2]).astype(jnp.bfloat16)
    query_grad_ref[...] = dot(outer_low, query_grads[...], 0, 0)
    stage.store(3)
    outer_part = dot(query_grads[...], query_weight_ref[...], 1, 1)
    gain_outer = jnp.sum(outer_part * normed, 0, keepdims=True)
    gain_grad_ref[...] = jnp.concatenate([gain_outer, gain_final], 0)
    back = outer_grad + norm_rows_back(outer_part, gain_ref[1:2], normed, scale)
    embed_grad_ref[...] = embed_back(noisy_ref[...], back)


def write_stage(
    scalars, latent, noisy, noise, keep, place, pixels, wide_gain, gains, weights
):
    latents, d_lat = latent.shape
    rows, patches = noisy.shape
    d_if = place.shape[1]
    width = weights[0].shape[1]
    results = [
        (latents, d_lat),
        (d_lat, width),
        (d_lat, width),
        (d_if, width),
        (d_if, width),
        (1, d_lat),
        (2, d_if),
        (rows, d_if),
        (rows, d_if),
        (8, 128),
    ]
    wide = pltpu.VMEM((patches, width), jnp.bfloat16)
    return staged(
        write_kernel,
        [scalars, latent, noisy, noise, keep, place, pixels, wide_gain, gains, *weights],
        [jax.ShapeDtypeStruct(shape, jnp.float32) for shape in results],
        [wide] * 4
        + [pltpu.VMEM((patches, d_if), jnp.float32), pltpu.VMEM((patches, 1), jnp.float32)],
        15 * 10**9,
        length=27,
    )


def adam_update(master, first, second, gradient, scale):
    clipped = gradient * scale
    moment = adam_beta * first + (1.0 - adam_beta) * clipped
    square = adam_beta * second + (1.0 - adam_beta) * clipped * clipped
    fixed_first = moment / (1.0 - adam_beta**STEP)
    fixed_second = square / (1.0 - adam_beta**STEP)
    updated = master - learning_rate * (
        fixed_first / (jnp.sqrt(fixed_second) + adam_eps) + weight_decay * master
    )
    return (updated, moment, square)


def sum_rows(values):
    return jnp.sum(values.reshape(-1, 8, values.shape[-1]), 0)


def closing_kernel(count, count_dp, number, stage, held, raws, results, scratch):
    refs = list(scratch)

    def pull(number):
        taken = refs[:number]
        del refs[:number]
        return taken

    items, (columns, tile), done = views(held[:number]), held[number : number + 2], held[number + 2 :]
    done = views(done, 2)
    number = len(items)
    wide_out, narrow_out, turned_out, last_out, latents_out, rest_out, stats = results
    shares = pull(number)
    sums = PieceSums(count_dp, items, shares, pull(number * (count_dp.bit_length() + 1)))
    (write_share,) = pull(1)
    scatter = LineScatter(count, columns, write_share, pull(4), pull(4))
    small = [Spread("mp", count, *pull(3)) for _ in range(2)]
    over_dp, over_mp = Spread("dp", count_dp, *pull(3)), Spread("mp", count, *pull(3))

    barrier = pltpu.get_barrier_semaphore()
    others = [over_dp.peer(step) for step in range(1, count_dp)]
    others += [over_mp.peer(step) for step in range(1, count)]
    signal_all(barrier, others)
    pl.semaphore_wait(barrier, len(others))
    stage.wait()

    sums.begin()
    scatter.run(lambda: sums.advance(1))
    for phase in range(2, sums.bits + 1):
        sums.advance(phase)
    for spread, share in zip(small, shares[-2:]):
        spread.held[spread.place] = share[...]
        spread.start()
    scatter.settle()

    self_in_2, self_out, read_query, read_out, read_key, read_value = shares[:6]
    self_in_0, self_in_1 = done[:2]
    up, down = done[2:6], done[6:10]
    lat_rows, if_rows = self_out.shape[0], read_key.shape[0]
    write_key, write_value = (write_share.at[pl.ds(i * lat_rows, lat_rows)] for i in range(2))
    write_query, write_out = (
        write_share.at[pl.ds(2 * lat_rows + i * if_rows, if_rows)] for i in range(2)
    )
    square = 0.0

    def keep(out, gradient, turn=False):
        nonlocal square
        value = gradient[...]
        square = square + sum_rows(value * value)
        out[...] = value.T if turn else value

    wide = [read_query, self_in_0, self_in_1, self_in_2] + up + [write_key, write_value]
    for slot, gradient in enumerate(wide):
        keep(wide_out.at[slot], gradient)
    for slot, gradient in enumerate([read_key, read_value, write_query]):
        keep(narrow_out.at[slot], gradient)
    for slot, gradient in enumerate([read_out, self_out] + down):
        keep(turned_out.at[slot], gradient, True)
    keep(last_out, write_out)
    stage.store(0, 1, 2, 3)
    for spread in small:
        spread.take()
    latents, rest = (spread.total() for spread in small)
    latents_out[...] = latents
    rest_out[...] = rest
    lead = (over_mp.place == 0).astype(jnp.float32)
    local = jnp.sum(square) + lead * (
        jnp.sum(sum_rows(latents * latents)) + jnp.sum(sum_rows(rest * rest))
    )
    lane = lax.broadcasted_iota(jnp.int32, (8, 128), 1)
    value = jnp.where(lane == 0, local, tile[...])
    for spread in (over_dp, over_mp):
        spread.held[spread.place] = value
        spread.start()
        spread.take()
        value = spread.total()
    stats[...] = jnp.where(lane == 0, jnp.sqrt(value), value)
    sums.finish()
    scatter.finish()
    for spread in small + [over_dp, over_mp]:
        spread.finish()


def closing(items, columns, tile, done, call_id):
    items, shapes, shares = piece_shapes(items)
    count, count_dp = lax.axis_size("mp"), lax.axis_size("dp")
    lat_rows, local = done[0].shape[1:]
    if_rows = shapes[4][0]
    outs = [
        (10, lat_rows, local),
        (3, if_rows, local),
        (6, local, lat_rows),
        (if_rows, local),
        shapes[-2],
        shapes[-1],
        (8, 128),
    ]
    outs = [jax.ShapeDtypeStruct(shape, jnp.float32) for shape in outs]
    shares = [pltpu.VMEM(shape, jnp.float32) for shape in shapes]
    scratch = (
        shares
        + PieceSums.scratch(count_dp, shapes)
        + [pltpu.VMEM((columns.shape[0] // count, columns.shape[1]), jnp.float32)]
        + LineScatter.scratch(count, columns.shape, 4)
        + Spread.scratch(count, tuple(shapes[-2]))
        + Spread.scratch(count, tuple(shapes[-1]))
        + Spread.scratch(count_dp, tile.shape)
        + Spread.scratch(count, tile.shape)
    )
    return staged(
        partial(closing_kernel, count, count_dp, len(items)),
        [*items, columns, tile, *done],
        outs,
        scratch,
        10**7,
        call_id=call_id,
        length=50,
    )


def clip_scale(norm):
    return clip_level / jnp.maximum(norm, clip_level)


def update_kernel(kinds, *refs):
    number = 3 * kinds
    sources, states, refs = refs[: 1 + kinds], refs[1 + kinds :][:number], refs[1 + kinds + number :]
    outs, local, refs = refs[:number], refs[number:][: 1 + kinds], refs[number + 1 + kinds :]
    local_sems, held, (in_sems, out_sems) = refs[0], refs[1 : 1 + number], refs[1 + number :]
    stats, gradients = local[0], local[1:]
    firsts = [
        pltpu.make_async_copy(source, target, local_sems.at[index])
        for index, (source, target) in enumerate(zip(sources, local))
    ]
    for first in firsts:
        first.start()
    lane = lax.broadcasted_iota(jnp.int32, (8, 128), 1)
    corner = jnp.logical_and(lane == 0, lax.broadcasted_iota(jnp.int32, (8, 128), 0) == 0)
    loads, copies = [], []
    pieces = []
    for kind, gradient in enumerate(gradients):
        slots = range(gradient.shape[0]) if len(gradient.shape) == 3 else [None]
        pieces += [(kind, slot) for slot in slots]

    def at(ref, slot):
        return ref if slot is None else ref.at[slot]

    for kind, slot in pieces:
        for index in range(3 * kind, 3 * kind + 3):
            source, target = at(states[index], slot), at(held[index], slot)
            loads.append(pltpu.make_async_copy(source, target, in_sems.at[len(loads)]))
            loads[-1].start()
    for load in firsts:
        load.wait()
    scale = jnp.sum(jnp.where(corner, clip_scale(stats[...]), 0.0))
    for order, (kind, slot) in enumerate(pieces):
        for load in loads[3 * order : 3 * order + 3]:
            load.wait()
        refs = [at(held[index], slot) for index in range(3 * kind, 3 * kind + 3)]
        source = at(gradients[kind], slot)
        rows, width = refs[0].shape
        step = math.gcd(rows, max(8, 8192 // width)) if rows % 8 == 0 else rows

        def one(index, carry, refs=refs, source=source, step=step, width=width):
            where = pl.ds(pl.multiple_of(index * step, step), step)
            state = [ref[where] for ref in refs]
            for ref, result in zip(refs, adam_update(*state, source[where, :width], scale)):
                ref[where] = result
            return carry

        lax.fori_loop(0, rows // step, one, 0)
        for index in range(3 * kind, 3 * kind + 3):
            source, target = at(held[index], slot), at(outs[index], slot)
            copies.append(pltpu.make_async_copy(source, target, out_sems.at[len(copies)]))
            copies[-1].start()
    for copy in copies:
        copy.wait()


def update_states(stats, gradients, states):
    kinds = len(gradients)
    copies = sum(3 * (item.shape[0] if item.ndim == 3 else 1) for item in gradients)
    sems = pltpu.SemaphoreType.DMA((copies,))
    return pl.pallas_call(
        partial(update_kernel, kinds),
        out_shape=[pltpu.HBM(item.shape, item.dtype) for item in states],
        in_specs=[HBM_SPEC] * (1 + kinds + len(states)),
        out_specs=[HBM_SPEC] * len(states),
        scratch_shapes=[pltpu.VMEM(item.shape, jnp.float32) for item in (stats, *gradients)]
        + [pltpu.SemaphoreType.DMA((1 + kinds,))]
        + [pltpu.VMEM(item.shape, jnp.float32) for item in states]
        + [sems] * 2,
        compiler_params=pltpu.CompilerParams(vmem_limit_bytes=24 << 20),
        cost_estimate=pl.CostEstimate(
            flops=2 * 10**7, bytes_accessed=14 * 10**6, transcendentals=0
        ),
    )(*(in_hbm(item) for item in (stats, *gradients, *states)))


def write_apart(
    latent_three,
    own_noisy,
    own_noise,
    own_keep,
    own_weight,
    weight_total,
    place,
    copy_pixels,
    gain,
    gain_rows,
    weights,
    layout,
    timesteps,
):
    write_key_weight, write_value_weight, write_query_weight, write_out_weight = weights
    images, latents, first_image, sharers = layout
    own_images, own_latents, d_lat = latent_three.shape
    write_norm, write_stats = layer_norm(latent_three, gain)
    write_low = write_norm.astype(jnp.bfloat16)

    own_interface = (
        jnp.einsum(
            "bcp,cd->bpd", own_noisy, copy_pixels[0].astype(jnp.float32), precision=precise
        )
        + place
    )

    outer_norm, outer_stats = layer_norm(own_interface, gain_rows[9])
    outer_low = outer_norm.astype(jnp.bfloat16)

    def join(spec, values, weight):
        product = jnp.einsum(spec, values, weight, preferred_element_type=jnp.float32)
        return product.astype(jnp.bfloat16)

    def image_rows(values):
        if sharers == 1:
            return values
        nothing = jnp.where(timesteps[0] > 0, 0.0, -0.0)
        whole = lax.all_gather(values.astype(jnp.float32), "mp", axis=0, tiled=True)
        whole = whole + nothing
        whole = whole.reshape(images, latents, d_lat).astype(jnp.bfloat16)
        return lax.dynamic_slice_in_dim(whole, first_image, own_images, 0)

    write_query = join("bpd,dc->bpc", outer_low, write_query_weight)
    write_key = image_rows(join("bld,dc->blc", write_low, write_key_weight))
    write_value = image_rows(join("bld,dc->blc", write_low, write_value_weight))
    write_out, write_total = attend_forward(write_query, write_key, write_value, None)
    outer = own_interface + jnp.einsum(
        "bpc,dc->bpd", write_out, write_out_weight, preferred_element_type=jnp.float32
    )
    final_norm, final_stats = layer_norm(outer, gain_rows[10])
    final_low = final_norm.astype(jnp.bfloat16)
    predicted = jnp.einsum(
        "bpd,cd->bcp", final_low, copy_pixels[1], preferred_element_type=jnp.float32
    )
    difference = predicted - own_noise
    masked = own_weight[:, None, None] * own_keep[:, None, :] * difference
    loss_local = jnp.sum(masked * difference)
    predict_grad = (2.0 * masked / weight_total).astype(jnp.bfloat16)
    head_grad = jnp.einsum(
        "bcp,bpd->cd", predict_grad, final_low, preferred_element_type=jnp.float32
    )
    final_grad = jnp.einsum(
        "bcp,cd->bpd", predict_grad, copy_pixels[1], preferred_element_type=jnp.float32
    )
    outer_grad, gain_final = norm_back(final_grad, gain_rows[10], final_stats)
    branch_low = outer_grad.astype(jnp.bfloat16)
    narrowout_grad = jnp.einsum(
        "bpd,bpc->dc", branch_low, write_out, preferred_element_type=jnp.float32
    )
    write_upstream = join("bpd,dc->bpc", branch_low, write_out_weight)
    query_grad, key_grad, value_grad = attend_back(
        write_query, write_key, write_value, None, write_total, write_upstream
    )
    write_query_grad = jnp.einsum(
        "bpd,bpc->dc", outer_low, query_grad, preferred_element_type=jnp.float32
    )
    outer_part = jnp.einsum(
        "bpc,dc->bpd", query_grad, write_query_weight, preferred_element_type=jnp.float32
    )

    def row_grad(values):
        if sharers > 1:
            whole = jnp.zeros((images, latents, d_lat), jnp.float32)
            whole = lax.dynamic_update_slice_in_dim(whole, values, first_image, 0)
            values = lax.psum_scatter(
                whole.reshape(images * sharers, own_latents, d_lat),
                "mp",
                scatter_dimension=0,
                tiled=True,
            )
        return values.astype(jnp.bfloat16)

    key_grad, value_grad = row_grad(key_grad), row_grad(value_grad)
    write_key_grad = jnp.einsum(
        "bld,blc->dc", write_low, key_grad, preferred_element_type=jnp.float32
    )
    write_value_grad = jnp.einsum(
        "bld,blc->dc", write_low, value_grad, preferred_element_type=jnp.float32
    )
    write_part = jnp.einsum(
        "blc,dc->bld", key_grad, write_key_weight, preferred_element_type=jnp.float32
    ) + jnp.einsum(
        "blc,dc->bld", value_grad, write_value_weight, preferred_element_type=jnp.float32
    )
    own_grad, gain_write = norm_back(write_part, gain, write_stats)
    outer_back, gain_outer = norm_back(outer_part, gain_rows[9], outer_stats)
    embed_grad = jnp.einsum(
        "bcp,bpd->cd", own_noisy, outer_grad + outer_back, precision=precise
    )
    return (
        own_grad,
        write_key_grad,
        write_value_grad,
        write_query_grad,
        narrowout_grad,
        gain_write,
        gain_outer,
        gain_final,
        embed_grad,
        head_grad,
        loss_local,
    )


def body(
    clean_patches,
    noise_patches,
    timesteps,
    present_mask,
    copy_widein,
    copy_narrowin,
    copy_wideout,
    copy_narrowout,
    copy_latents,
    copy_gains,
    copy_pixels,
    master_widein,
    first_widein,
    second_widein,
    master_narrowin,
    first_narrowin,
    second_narrowin,
    master_wideout,
    first_wideout,
    second_wideout,
    master_narrowout,
    first_narrowout,
    second_narrowout,
    master_latents,
    first_latents,
    second_latents,
    master_gains,
    first_gains,
    second_gains,
    master_pixels,
    first_pixels,
    second_pixels,
):
    images = clean_patches.shape[0]
    patches = clean_patches.shape[2]
    count_mp, count_dp = lax.axis_size("mp"), lax.axis_size("dp")
    mp_index, dp_index = lax.axis_index("mp"), lax.axis_index("dp")
    lead = (mp_index == 0).astype(jnp.float32)
    latents, d_lat = copy_latents.shape
    d_if = copy_gains.shape[1]
    local = copy_widein.shape[2]
    sharers = max(1, count_mp // images)
    own_images = max(1, images // count_mp)
    own_patches, own_latents = patches // sharers, latents // sharers
    first_image = mp_index * own_images // sharers
    share = lax.rem(mp_index, sharers)

    def dp_piece(values, axis):
        size = values.shape[axis] // count_dp
        return lax.dynamic_slice_in_dim(values, dp_index * size, size, axis).astype(jnp.float32)

    key_piece = dp_piece(copy_widein[:, 8], 0)
    value_piece = dp_piece(copy_widein[:, 9], 0)
    query_piece = dp_piece(copy_narrowin[:, 2], 0)
    out_piece = dp_piece(copy_narrowout, 1).T
    gathered = lax.all_gather(
        jnp.concatenate([key_piece, value_piece, query_piece, out_piece], 0), "mp"
    )

    signal = jnp.cos(0.5 * math.pi * (timesteps.astype(jnp.float32) + 0.5) / NSTEPS) ** 2
    noisy = (
        jnp.sqrt(signal)[:, None, None] * clean_patches
        + jnp.sqrt(1.0 - signal)[:, None, None] * noise_patches
    )
    loss_weight = 0.5 + signal
    keep_float = present_mask.astype(jnp.float32)
    weight_here = jnp.sum(loss_weight * PIX * jnp.sum(keep_float, 1))
    gain_rows = copy_gains.astype(jnp.float32)

    def wide_gain(index):
        return gain_rows[2 * index : 2 * index + 2].reshape(-1)

    wide_in = in_hbm(jnp.swapaxes(copy_widein, 0, 1))
    narrow_in = in_hbm(jnp.swapaxes(copy_narrowin, 0, 1))
    wide_out = in_hbm(copy_wideout)
    place = position_table(patches, d_if)
    noisy_rows, pixel_rows, noise_rows = (
        jnp.pad(item, ((0, 0), (0, 16 - PIX), (0, 0)))
        for item in (noisy, copy_pixels, noise_patches)
    )
    read_args = (
        noisy_rows,
        keep_float[:, :, None],
        place,
        pixel_rows[0],
        copy_latents,
        wide_gain(0)[None],
        gain_rows[8:9],
        wide_in,
        narrow_in,
        wide_out,
    )
    read_part, *read_kept = read_forward(*read_args)
    gathered, read_part = lax.optimization_barrier((gathered, read_part))
    gathered = lax.all_gather(gathered, "dp").reshape(count_dp * count_mp, -1, local)
    latent_zero = copy_latents.astype(jnp.float32)
    latent_base = jnp.broadcast_to(latent_zero[None], (images, latents, d_lat))
    latent_one, (weight_tile,) = line_sum(
        read_part, latent_base.reshape(-1, d_lat), 2, tile=jnp.full((8, 128), weight_here)
    )
    weight_total = weight_tile[0, 0]
    self_part, *self_kept = self_forward(
        latent_one, wide_gain(1)[None], wide_in, wide_out, images
    )
    latent_two, write_weights = line_sum(
        self_part, latent_one, 3, blocks=(gathered, [d_lat, d_lat, d_if, d_if])
    )
    feed_part, *feed_kept = feed_forward(latent_two, wide_gain(2)[None], wide_in, wide_out)
    own_two = lax.dynamic_slice_in_dim(
        latent_two, mp_index * (own_images * own_latents), own_images * own_latents, 0
    )
    latent_three = (own_two + line_scatter(feed_part, 4)).reshape(own_images, own_latents, d_lat)
    def own_tokens(values, axis):
        values = lax.dynamic_slice_in_dim(values, first_image, own_images, 0)
        return lax.dynamic_slice_in_dim(values, share * own_patches, own_patches, axis)

    own_weight = lax.dynamic_slice_in_dim(loss_weight, first_image, own_images, 0)
    if sharers == 1 and own_images == 1:
        (
            own_grad,
            write_key_grad,
            write_value_grad,
            write_query_grad,
            narrowout_grad,
            gain_write,
            gain_pair,
            own_embed,
            head_grad,
            loss_tile,
        ) = write_stage(
            jnp.pad(jnp.stack([own_weight[0], weight_total])[None], ((0, 7), (0, 126))),
            latent_three[0],
            own_tokens(noisy_rows, 2)[0],
            own_tokens(noise_rows, 2)[0],
            own_tokens(keep_float, 1),
            place,
            pixel_rows,
            wide_gain(3)[None],
            gain_rows[8:11],
            write_weights,
        )
        gain_outer, gain_final = gain_pair[0], gain_pair[1]
        head_grad, own_embed = head_grad[:PIX], own_embed[:PIX]
        loss_local = loss_tile[0, 0]
    else:
        (
            own_grad,
            write_key_grad,
            write_value_grad,
            write_query_grad,
            narrowout_grad,
            gain_write,
            gain_outer,
            gain_final,
            own_embed,
            head_grad,
            loss_local,
        ) = write_apart(
            latent_three,
            own_tokens(noisy, 2),
            own_tokens(noise_patches, 2),
            own_tokens(keep_float, 1),
            own_weight,
            weight_total,
            lax.dynamic_slice_in_dim(place, share * own_patches, own_patches, 0),
            copy_pixels,
            wide_gain(3),
            gain_rows,
            write_weights,
            (images, latents, first_image, sharers),
            timesteps,
        )
    latent_grad, (key_share, query_share) = line_gather(
        own_grad.reshape(-1, d_lat), 5, [write_key_grad, write_query_grad]
    )
    latent_grad = latent_grad.reshape(latent_one.shape)

    latent_part, up_first, up_last, down_grad, gain_feed = feed_backward(
        latent_grad, latent_two, wide_gain(2)[None], wide_in, wide_out, *feed_kept
    )
    latent_grad, five_shares = line_sum(
        latent_part, latent_grad, 6, [write_value_grad, narrowout_grad, up_first]
    )
    latent_part, self_first, self_last, gain_self = self_backward(
        latent_grad, latent_one, wide_gain(1)[None], wide_in, wide_out, *self_kept
    )
    latent_grad, six_shares = line_sum(
        latent_part, latent_grad, 7, [up_last, down_grad, self_first]
    )
    write_share = jnp.concatenate([key_share, five_shares[0], query_share, five_shares[1]], 0)
    write_columns = jnp.concatenate(jnp.split(write_share, count_mp, 1), 0)
    read_wide, read_narrow, latent_total, gain_read, gain_side, side_embed = read_backward(
        *read_args, *read_kept, latent_grad, lead.reshape(1, 1)
    )
    embed_grad = side_embed[:PIX] + own_embed
    gains_grad = jnp.concatenate(
        [
            gain_read.reshape(2, -1),
            gain_self.reshape(2, -1),
            gain_feed.reshape(2, -1),
            gain_write.reshape(2, -1),
            gain_side,
            gain_outer[None],
            gain_final[None],
        ],
        0,
    )

    def dp_pieces(values):
        values = values.reshape(values.shape[0], count_dp, -1)
        return jnp.swapaxes(values, 0, 1)

    low_rows = [gains_grad, embed_grad, head_grad]
    low_rows = [jnp.pad(item, ((0, 16 - item.shape[0]), (0, 0))) for item in low_rows]
    rest = dp_pieces(jnp.concatenate(low_rows, 0))
    rest = jnp.pad(rest, ((0, 0), (0, 0), (0, 128 - rest.shape[2])))
    latents_item = dp_pieces(latent_total)

    *gradients, rest_grad, stats = closing(
        [
            self_last,
            read_wide,
            read_narrow,
            latents_item.reshape(-1, latents_item.shape[2]),
            rest.reshape(-1, rest.shape[2]),
        ],
        write_columns,
        jnp.full((8, 128), loss_local),
        [six_shares[2], five_shares[2], six_shares[0], six_shares[1]],
        8,
    )
    states = (
        *(jnp.swapaxes(item, 0, 1) for item in (master_widein, first_widein, second_widein)),
        *(jnp.swapaxes(item, 0, 1) for item in (master_narrowin, first_narrowin, second_narrowin)),
        master_wideout,
        first_wideout,
        second_wideout,
        *(item.T for item in (master_narrowout, first_narrowout, second_narrowout)),
        master_latents,
        first_latents,
        second_latents,
        master_gains,
        first_gains,
        second_gains,
    )
    results = update_states(stats, [*gradients, rest_grad], states)
    results = [
        jnp.swapaxes(item, 0, 1) if index < 6 or 9 <= index < 12 else item
        for index, item in enumerate(results)
    ]
    lanes = master_pixels.shape[2]
    pixels_grad = jnp.stack([rest_grad[16 : 16 + PIX, :lanes], rest_grad[32 : 32 + PIX, :lanes]])
    results += adam_update(
        master_pixels, first_pixels, second_pixels, pixels_grad, clip_scale(stats[0, 0])
    )
    return (stats[0, 1] / weight_total, stats[0, 0], *results)


def solution(mesh):
    in_specs = (
        P("dp", None, None),
        P("dp", None, None),
        P("dp"),
        P("dp", None),
        P(None, None, "mp"),
        P(None, None, "mp"),
        P(None, "mp", None),
        P("mp", None),
        P(),
        P(),
        P(),
        P("dp", None, "mp"),
        P("dp", None, "mp"),
        P("dp", None, "mp"),
        P("dp", None, "mp"),
        P("dp", None, "mp"),
        P("dp", None, "mp"),
        P(None, "mp", "dp"),
        P(None, "mp", "dp"),
        P(None, "mp", "dp"),
        P("mp", "dp"),
        P("mp", "dp"),
        P("mp", "dp"),
        P(None, "dp"),
        P(None, "dp"),
        P(None, "dp"),
        P(None, "dp"),
        P(None, "dp"),
        P(None, "dp"),
        P(None, None, "dp"),
        P(None, None, "dp"),
        P(None, None, "dp"),
    )
    out_specs = (
        P(),
        P(),
        P("dp", None, "mp"),
        P("dp", None, "mp"),
        P("dp", None, "mp"),
        P("dp", None, "mp"),
        P("dp", None, "mp"),
        P("dp", None, "mp"),
        P(None, "mp", "dp"),
        P(None, "mp", "dp"),
        P(None, "mp", "dp"),
        P("mp", "dp"),
        P("mp", "dp"),
        P("mp", "dp"),
        P(None, "dp"),
        P(None, "dp"),
        P(None, "dp"),
        P(None, "dp"),
        P(None, "dp"),
        P(None, "dp"),
        P(None, None, "dp"),
        P(None, None, "dp"),
        P(None, None, "dp"),
    )
    return jax.shard_map(body, mesh=mesh, in_specs=in_specs, out_specs=out_specs, check_vma=False)
```

```python
from functools import partial
import math

import jax
import jax.numpy as jnp
import numpy as np
from jax import lax
from jax.experimental import pallas as pl
from jax.experimental.pallas import tpu as pltpu
from jax.sharding import PartitionSpec as P

HEAD_DIM = 64
PIX = 12
NSTEPS = 1000
STEP = 10


precise = lax.Precision.HIGHEST
clip_level = 0.01
learning_rate = 0.05
weight_decay = 0.1
adam_beta = 0.5
adam_eps = 1e-08


def layer_norm(values, gain):
    centered = values - jnp.mean(values, -1, keepdims=True)
    scale = lax.rsqrt(jnp.mean(centered * centered, -1, keepdims=True) + 1e-05)
    normed = centered * scale
    return (normed * gain, (normed, scale))


def norm_back(upstream, gain, stats):
    normed, scale = stats
    inner = upstream * gain
    values = scale * (
        inner
        - jnp.mean(inner, -1, keepdims=True)
        - normed * jnp.mean(inner * normed, -1, keepdims=True)
    )
    gain_grad = jnp.sum((upstream * normed).reshape(-1, normed.shape[-1]), 0)
    return (values, gain_grad)


def position_table(count, width):
    place = np.arange(count, dtype=np.float64)[:, None]
    angle = place * 10000.0 ** (-2.0 * np.arange(width // 2) / width)
    return jnp.asarray(np.concatenate([np.sin(angle), np.cos(angle)], -1), jnp.float32)


def positions(count, width):
    place = jnp.arange(count, dtype=jnp.float32)[:, None]
    index = jnp.arange(width // 2, dtype=jnp.float32)[None, :]
    angle = place * jnp.exp(-math.log(10000.0) * 2.0 * index / width)
    return jnp.concatenate([jnp.sin(angle), jnp.cos(angle)], -1)


def split_heads(values):
    return values.reshape(values.shape[:-1] + (values.shape[-1] // HEAD_DIM, HEAD_DIM))


def attend_scores(queries, keys, keep_mask):
    scores = jnp.einsum(
        "bqhe,bkhe->bhqk",
        split_heads(queries),
        split_heads(keys),
        preferred_element_type=jnp.float32,
    ) * HEAD_DIM ** (-0.5)
    if keep_mask is not None:
        scores = jnp.where(keep_mask[:, None, None, :] > 0, scores, -1e30)
    return scores


def attend_forward(queries, keys, values, keep_mask):
    scores = attend_scores(queries, keys, keep_mask)
    top = jnp.max(scores, -1, keepdims=True)
    log_total = top + jnp.log(jnp.sum(jnp.exp(scores - top), -1, keepdims=True))
    probs = jnp.exp(scores - log_total).astype(jnp.bfloat16)
    output = jnp.einsum(
        "bhqk,bkhe->bqhe", probs, split_heads(values), preferred_element_type=jnp.float32
    )
    return (output.reshape(queries.shape).astype(jnp.bfloat16), log_total)


def attend_back(queries, keys, values, keep_mask, log_total, upstream):
    scores = attend_scores(queries, keys, keep_mask)
    probs = jnp.exp(scores - log_total)
    value_grad = jnp.einsum(
        "bhqk,bqhe->bkhe",
        probs.astype(jnp.bfloat16),
        split_heads(upstream),
        preferred_element_type=jnp.float32,
    )
    prob_grad = jnp.einsum(
        "bqhe,bkhe->bhqk",
        split_heads(upstream),
        split_heads(values),
        preferred_element_type=jnp.float32,
    )
    score_grad = (probs * (prob_grad - jnp.sum(prob_grad * probs, -1, keepdims=True))).astype(
        jnp.bfloat16
    )
    query_grad = jnp.einsum(
        "bhqk,bkhe->bqhe", score_grad, split_heads(keys), preferred_element_type=jnp.float32
    ) * HEAD_DIM ** (-0.5)
    key_grad = jnp.einsum(
        "bhqk,bqhe->bkhe", score_grad, split_heads(queries), preferred_element_type=jnp.float32
    ) * HEAD_DIM ** (-0.5)
    return (
        query_grad.reshape(queries.shape).astype(jnp.bfloat16),
        key_grad.reshape(keys.shape),
        value_grad.reshape(values.shape),
    )


MESH_ID = pl.DeviceIdType.MESH
HBM_SPEC = pl.BlockSpec(memory_space=pltpu.HBM)
VMEM_SPEC = pl.BlockSpec(memory_space=pltpu.VMEM)
CHUNKS = 32
VMEM_LIMIT = 56 << 20


def in_hbm(values):
    return pltpu.with_memory_space_constraint(values, pltpu.HBM)


def in_vmem(values):
    return pltpu.with_memory_space_constraint(values, pltpu.VMEM)


def remote(source, target, send_sem, recv_sem, device):
    return pltpu.make_async_remote_copy(
        src_ref=source,
        dst_ref=target,
        send_sem=send_sem,
        recv_sem=recv_sem,
        device_id=device,
        device_id_type=MESH_ID,
    )


class PieceSums:
    def __init__(self, count, items, outs, scratch):
        self.count, self.items, self.outs = count, items, outs
        self.bits = count.bit_length() - 1
        self.place = lax.axis_index("dp") if items else None
        self.held = []
        for index in range(len(items)):
            self.held.append(scratch[index * (self.bits + 2) : (index + 1) * (self.bits + 2)])

    @staticmethod
    def scratch(count, shapes):
        bits = count.bit_length() - 1
        result = []
        for rows, width in shapes:
            result.append(pltpu.VMEM((count // 2, rows, width), jnp.float32))
            for phase in range(2, bits + 1):
                result.append(
                    pltpu.VMEM((2 * (count >> phase), rows // 2, width), jnp.float32)
                )
            copies = count // 2 + 2 * sum(count >> phase for phase in range(2, bits + 1))
            result += [pltpu.SemaphoreType.DMA((copies,))] * 2
        return result

    def peers(self):
        return [{"dp": self.place ^ (1 << bit)} for bit in range(self.bits)] if self.items else []

    def order(self, half):
        later = list(range(1, self.bits))
        turn = half * (len(later) // 2)
        return later[turn:] + later[:turn]

    def first_copy(self, index, piece):
        item, held = self.items[index], self.held[index]
        other = 1 - (self.place & 1)
        return remote(
            item.at[2 * piece + other],
            held[0].at[piece],
            held[-2].at[piece],
            held[-1].at[piece],
            {"dp": self.place ^ 1},
        )

    def member(self, half, phase, entry, flip):
        bits = self.order(half)
        settled, now, rest = bits[: phase - 2], bits[phase - 2], bits[phase - 1 :]
        piece = 0
        for bit in settled:
            piece = piece | (self.place & (1 << bit))
        own = self.place & (1 << now)
        piece = piece | ((own ^ (1 << now)) if flip else own)
        for position, bit in enumerate(rest):
            if (entry >> position) & 1:
                piece = piece | (1 << bit)
        return piece >> 1

    def later_copy(self, index, half, phase, entry):
        held = self.held[index]
        rows = self.items[index].shape[1] // 2
        size = self.count >> phase
        sem = self.count // 2 + 2 * sum(self.count >> p for p in range(2, phase)) + half * size + entry
        return remote(
            held[0].at[self.member(half, phase, entry, True), pl.ds(half * rows, rows)],
            held[phase - 1].at[half * size + entry],
            held[-2].at[sem],
            held[-1].at[sem],
            {"dp": self.place ^ (1 << self.order(half)[phase - 2])},
        )

    def entries(self, phase):
        return [
            (index, half, entry)
            for index in range(len(self.items))
            for half in range(2)
            for entry in range(self.count >> phase)
        ]

    def begin(self):
        for index in range(len(self.items)):
            for piece in range(self.count // 2):
                self.first_copy(index, piece).start()

    def send(self, phase):
        for index, half, entry in self.entries(phase):
            self.later_copy(index, half, phase, entry).start()

    def advance(self, phase):
        if not self.items:
            return
        if phase == 1:
            own = self.place & 1
            for index, item in enumerate(self.items):
                total = self.held[index][0]
                for piece in range(self.count // 2):
                    self.first_copy(index, piece).wait_recv()
                    add_rows(total.at[piece], total.at[piece], item.at[2 * piece + own])
        else:
            for index, half, entry in self.entries(phase):
                self.later_copy(index, half, phase, entry).wait_recv()
                held, rows = self.held[index], self.items[index].shape[1] // 2
                where = pl.ds(half * rows, rows)
                came = held[phase - 1].at[half * (self.count >> phase) + entry]
                kept = held[0].at[self.member(half, phase, entry, False), where]
                if phase == self.bits:
                    add_rows(self.outs[index].at[where], kept, came)
                else:
                    add_rows(kept, kept, came)
        if phase < self.bits:
            self.send(phase + 1)

    def finish(self):
        for index in range(len(self.items)):
            for piece in range(self.count // 2):
                self.first_copy(index, piece).wait_send()
        for phase in range(2, self.bits + 1):
            for index, half, entry in self.entries(phase):
                self.later_copy(index, half, phase, entry).wait_send()

    def moments(self, total):
        if not self.items:
            return [(0, total, None)]
        marks, low = [], 0
        for phase in range(1, self.bits + 1):
            share = (1 - 0.5 ** (phase - 1)) / (1 - 0.5 ** (self.bits - 1))
            high = total if phase == self.bits else int(total * (0.22 + 0.78 * share))
            marks.append((low, high, phase))
            low = high
        return marks


def add_rows(target, left, right):
    rows, width = target.shape
    step = math.gcd(rows, max(8, 8192 // width))

    def one(index, carry):
        where = pl.ds(pl.multiple_of(index * step, step), step)
        target[where] = left[where] + right[where]
        return carry

    lax.fori_loop(0, rows // step, one, 0)


class Spread:
    def __init__(self, name, count, held, send_sem, recv_sem):
        self.name, self.count, self.held = name, count, held
        self.send_sem, self.recv_sem = send_sem, recv_sem
        self.place = lax.axis_index(name)

    @staticmethod
    def scratch(count, shape):
        sems = pltpu.SemaphoreType.DMA((count,))
        return [pltpu.VMEM((count,) + shape, jnp.float32), sems, sems]

    def peer(self, step):
        return {self.name: lax.rem(self.place + step, self.count)}

    def copy(self, step, slot):
        return remote(
            self.held.at[slot],
            self.held.at[slot],
            self.send_sem.at[step],
            self.recv_sem.at[slot],
            self.peer(step),
        )

    def each(self, action):
        def one(step, carry):
            action(step)
            return carry

        lax.fori_loop(1, self.count, one, 0)

    def start(self):
        self.each(lambda step: self.copy(step, self.place).start())

    def take(self):
        self.each(lambda step: self.copy(step, lax.rem(self.place + step, self.count)).wait_recv())

    def finish(self):
        self.each(lambda step: self.copy(step, self.place).wait_send())

    def total(self):
        return lax.fori_loop(
            1, self.count, lambda slot, carry: carry + self.held[slot], self.held[0]
        )


class Convert:
    def __init__(self, count_mp, steps, blocks, outs, buffer, sems):
        self.count_mp, self.blocks, self.outs = count_mp, blocks, outs
        self.buffer, self.sems = buffer, sems
        self.number = blocks.shape[0]
        self.each = -(-self.number // steps)

    @staticmethod
    def scratch(block):
        return [pltpu.VMEM((3,) + block, jnp.float32), pltpu.SemaphoreType.DMA((3,))]

    def copy(self, index):
        slot = lax.rem(index, 3)
        return pltpu.make_async_copy(
            self.blocks.at[index], self.buffer.at[slot], self.sems.at[slot]
        )

    def begin(self):
        self.copy(0).start()
        self.copy(1).start()

    def one(self, index):
        self.copy(index).wait()

        @pl.when(index + 2 < self.number)
        def _():
            self.copy(index + 2).start()

        block = self.buffer.at[lax.rem(index, 3)]
        local = block.shape[1]
        columns = pl.ds(pl.multiple_of(lax.rem(index, self.count_mp) * local, local), local)
        low = 0
        for out in self.outs:
            rows = out.shape[0] * self.count_mp // self.number
            where = pl.ds(pl.multiple_of(index // self.count_mp * rows, rows), rows)
            out[where, columns] = block[pl.ds(low, rows)].astype(jnp.bfloat16)
            low += rows

    def step(self, index):
        for entry in range(self.each):
            self.one(index * self.each + entry)


def signal_all(barrier, others):
    for other in others:
        pl.semaphore_signal(barrier, inc=1, device_id=other, device_id_type=MESH_ID)


class Stage:
    def __init__(self, sources, held, in_sems, results, targets, out_sems):
        self.loads = [
            pltpu.make_async_copy(source, target, in_sems.at[index])
            for index, (source, target) in enumerate(zip(sources, held))
        ]
        self.stores = [
            pltpu.make_async_copy(source, target, out_sems.at[index])
            for index, (source, target) in enumerate(zip(results, targets))
        ]
        self.stored, self.waited = [], []

    def start(self):
        for load in self.loads:
            load.start()

    def wait(self, *indices):
        for index in indices or range(len(self.loads)):
            if index not in self.waited:
                self.loads[index].wait()
                self.waited.append(index)

    def store(self, *indices):
        for index in indices:
            self.stores[index].start()
            self.stored.append(index)

    def finish(self):
        self.store(*(index for index in range(len(self.stores)) if index not in self.stored))
        for store in self.stores:
            store.wait()


def staged_kernel(body, counts, *refs):
    refs = list(refs)

    def pull(number):
        taken = refs[:number]
        del refs[:number]
        return taken

    close, number, raw, close_outs, results = counts
    near, sources, raws = pull(close), pull(number), pull(raw)
    near_outs, targets, echoes = pull(close_outs), pull(results), pull(close_outs)
    held, outs, (in_sems, out_sems) = pull(number), pull(results), pull(2)
    stage = Stage(
        sources, held, in_sems, [*near_outs, *outs], [*echoes, *targets], out_sems
    )
    stage.start()
    body(stage, [*near, *held], raws, [*near_outs, *outs], refs)
    stage.finish()


def staged(
    body, inputs, outs, scratch, flops, raw=(), call_id=None, length=0, near=(), near_outs=()
):
    copies = [pltpu.VMEM(item.shape, item.dtype) for item in (*inputs, *outs)]
    stores = [*outs, *near_outs]
    sems = [pltpu.SemaphoreType.DMA((max(1, len(group)),)) for group in (inputs, stores)]
    needed = sum(
        math.prod(item.shape) * jnp.dtype(item.dtype).itemsize
        for item in copies + list(scratch)
        if getattr(item, "dtype", None) in (jnp.float32, jnp.bfloat16)
    )
    params = {} if call_id is None else {"collective_id": call_id, "has_side_effects": True}
    counts = (len(near), len(inputs), len(raw), len(near_outs), len(outs))
    results = pl.pallas_call(
        partial(staged_kernel, body, counts),
        out_shape=[pltpu.VMEM(item.shape, item.dtype) for item in near_outs]
        + [pltpu.HBM(item.shape, item.dtype) for item in stores],
        in_specs=[VMEM_SPEC] * len(near) + [HBM_SPEC] * (len(inputs) + len(raw)),
        out_specs=[VMEM_SPEC] * len(near_outs) + [HBM_SPEC] * len(stores),
        scratch_shapes=copies + sems + list(scratch),
        compiler_params=pltpu.CompilerParams(vmem_limit_bytes=needed + (6 << 20), **params),
        cost_estimate=pl.CostEstimate(
            flops=flops, bytes_accessed=length * 3_500_000, transcendentals=0
        ),
    )(*map(in_vmem, near), *map(in_hbm, (*inputs, *raw)))
    return list(results)


def greet(place, count, others=()):
    barrier = pltpu.get_barrier_semaphore()
    below, above = {"mp": place - 1}, {"mp": place + 1}

    @pl.when(place > 0)
    def _():
        pl.semaphore_signal(barrier, inc=1, device_id=below, device_id_type=MESH_ID)

    @pl.when(place < count - 1)
    def _():
        pl.semaphore_signal(barrier, inc=1, device_id=above, device_id_type=MESH_ID)

    signal_all(barrier, others)
    inside = jnp.logical_and(place > 0, place < count - 1)

    @pl.when(inside)
    def _():
        pl.semaphore_wait(barrier, 2 + len(others))

    @pl.when(jnp.logical_not(inside))
    def _():
        pl.semaphore_wait(barrier, 1 + len(others))


def views(refs, base=3):
    result = []
    for ref in refs:
        if len(ref.shape) == base:
            result.append(ref)
        else:
            result += [ref.at[slot] for slot in range(ref.shape[0])]
    return result


def line_sum_kernel(count, count_dp, extra, tiled, stage, held, raws, results, scratch):
    refs = list(scratch)

    def pull(number):
        taken = refs[:number]
        del refs[:number]
        return taken

    part_ref, base_ref, tile = held[0], held[1], held[2 + extra :]
    items, outs = views(held[2 : 2 + extra]), views(results[1 : 1 + extra], 2)
    out_ref, tile_out = results[0], results[1 + extra : 1 + extra + tiled]
    blocks, base_rows = raws, base_ref.shape[0]
    wide = results[1 + extra + tiled :]
    converted = len(wide)
    inner, from_away, from_toward, toward_send, away_send, away_recv, toward_recv = pull(7)
    chunks = toward_send.shape[0]
    spread = Spread("dp", count_dp, *pull(3)) if tiled else None
    convert = Convert(count, chunks, blocks[0], wide, *pull(2)) if converted else None
    sums = PieceSums(count_dp, items, outs, refs)
    place = lax.axis_index("mp")
    half = count // 2
    low_side = place < half
    toward = {"mp": jnp.where(low_side, place + 1, place - 1)}
    away = {"mp": jnp.where(low_side, place - 1, place + 1)}
    middle = jnp.logical_or(place == half - 1, place == half)
    outermost = jnp.logical_or(place == 0, place == count - 1)
    rows = part_ref.shape[0] // chunks
    others = [spread.peer(step) for step in range(1, count_dp)] if tiled else sums.peers()
    greet(place, count, others)

    def window(step):
        return pl.ds(pl.multiple_of(step * rows, rows), rows)

    def put(step, total):
        first = lax.rem(step * rows, base_rows)
        out_ref[window(step)] = total + base_ref[pl.ds(pl.multiple_of(first, rows), rows)]

    def push(step, source, inside):
        target = from_toward if inside else from_away
        recv = toward_recv if inside else away_recv
        return remote(
            source.at[window(step)],
            target.at[window(step)],
            toward_send.at[step],
            recv.at[step],
            toward,
        )

    def back(step, source):
        return remote(
            source.at[window(step)],
            from_toward.at[window(step)],
            away_send.at[step],
            toward_recv.at[step],
            away,
        )

    def gather_in(step):
        push(step, part_ref, False).wait_recv()
        inner[window(step)] = part_ref[window(step)] + from_away[window(step)]

    @pl.when(outermost)
    def _():
        def leave(step, carry):
            push(step, part_ref, False).start()
            return carry

        lax.fori_loop(0, chunks, leave, 0)

    stage.wait()
    if tiled:
        spread.held[spread.place] = tile[0][...]
        spread.start()
    if converted:
        convert.begin()
    sums.begin()

    @pl.when(outermost)
    def _():

        def arrive(step, carry):
            push(step, part_ref, True).wait_recv()
            put(step, from_toward[window(step)])
            push(step, part_ref, False).wait_send()
            if converted:
                convert.step(step)
            return carry

        for low, high, phase in sums.moments(chunks):
            lax.fori_loop(low, high, arrive, 0)
            sums.advance(phase)

    lag = 2

    @pl.when(middle)
    def _():
        def finish(step):
            push(step, inner, True).wait_recv()
            push(step, inner, True).wait_send()
            total = inner[window(step)] + from_toward[window(step)]
            inner[window(step)] = total
            back(step, inner).start()
            put(step, total)

        def first(step, carry):
            gather_in(step)
            push(step, inner, True).start()
            if converted:
                convert.step(step)
            return carry

        def both(step, carry):
            first(step, carry)
            finish(step - lag)
            return carry

        def last(step, carry):
            finish(step)
            return carry

        def drain(step, carry):
            back(step, inner).wait_send()
            return carry

        lax.fori_loop(0, lag, first, 0)
        for low, high, phase in sums.moments(chunks):
            lax.fori_loop(max(low, lag), high, both, 0)
            if high == chunks:
                lax.fori_loop(chunks - lag, chunks, last, 0)
            sums.advance(phase)
        lax.fori_loop(0, chunks, drain, 0)

    if count > 4:

        @pl.when(jnp.logical_not(jnp.logical_or(middle, outermost)))
        def _():
            def inwards(step, carry):
                gather_in(step)
                push(step, inner, False).start()
                return carry

            def outwards(step, carry):
                push(step, inner, True).wait_recv()
                back(step, from_toward).start()
                put(step, from_toward[window(step)])
                if converted:
                    convert.step(step)
                return carry

            def drain(step, carry):
                push(step, inner, False).wait_send()
                back(step, from_toward).wait_send()
                return carry

            lax.fori_loop(0, chunks, inwards, 0)
            for low, high, phase in sums.moments(chunks):
                lax.fori_loop(low, high, outwards, 0)
                sums.advance(phase)
            lax.fori_loop(0, chunks, drain, 0)

    sums.finish()
    if tiled:
        spread.take()
        tile_out[0][...] = spread.total()
        spread.finish()


def piece_shapes(items):
    count = lax.axis_size("dp")
    items = [item.reshape(item.shape[:-2] + (count, -1, item.shape[-1])) for item in items]
    shapes, shares = [], []
    for item in items:
        shapes += [item.shape[-2:]] * (item.shape[0] if item.ndim == 4 else 1)
        shares.append(jax.ShapeDtypeStruct(item.shape[:-3] + item.shape[-2:], jnp.float32))
    return items, shapes, shares


def line_sum(part, base, call_id, items=(), tile=None, blocks=None):
    items, shapes, shares = piece_shapes(items)
    count, count_dp = lax.axis_size("mp"), lax.axis_size("dp")
    rows, width = part.shape
    buffer = pltpu.VMEM((rows, width), jnp.float32)
    sems = pltpu.SemaphoreType.DMA((CHUNKS,))
    inputs, raw = [base, *items], []
    outs = list(shares)
    scratch = [buffer] * 3 + [sems] * 4
    if tile is not None:
        inputs.append(tile)
        outs.append(jax.ShapeDtypeStruct(tile.shape, jnp.float32))
        scratch += Spread.scratch(count_dp, tile.shape)
    if blocks is not None:
        blocks, sizes = blocks
        raw.append(blocks)
        outs += [
            jax.ShapeDtypeStruct((size, count * blocks.shape[2]), jnp.bfloat16) for size in sizes
        ]
        scratch += Convert.scratch(blocks.shape[1:])
    scratch += PieceSums.scratch(count_dp, shapes)
    total = jax.ShapeDtypeStruct((rows, width), jnp.float32)
    results = staged(
        partial(line_sum_kernel, count, count_dp, len(items), int(tile is not None)),
        inputs,
        outs,
        scratch,
        4 * rows * width,
        raw,
        call_id,
        55,
        [part],
        [total],
    )
    return results[0], results[-1], results[1:-1]


class LineScatter:
    def __init__(self, count, part, out, buffers, sems):
        self.count, self.part, self.out = count, part, out
        self.up_acc, self.down_acc, self.from_below, self.from_above = buffers
        self.up_send, self.down_send, self.up_recv, self.down_recv = sems
        self.place = lax.axis_index("mp")
        self.steps = self.up_send.shape[1]
        self.block = part.shape[0] // count
        self.rows = self.block // self.steps

    @staticmethod
    def scratch(count, shape, steps):
        sems = pltpu.SemaphoreType.DMA((count, steps))
        return [pltpu.VMEM(shape, jnp.float32)] * 4 + [sems] * 4

    def window(self, owner, step):
        return pl.ds(pl.multiple_of(owner * self.block + step * self.rows, self.rows), self.rows)

    def up(self, owner, step, source):
        where = self.window(owner, step)
        return remote(
            source.at[where],
            self.from_below.at[where],
            self.up_send.at[owner, step],
            self.up_recv.at[owner, step],
            {"mp": self.place + 1},
        )

    def down(self, owner, step, source):
        where = self.window(owner, step)
        return remote(
            source.at[where],
            self.from_above.at[where],
            self.down_send.at[owner, step],
            self.down_recv.at[owner, step],
            {"mp": self.place - 1},
        )

    def up_turn(self, index):
        place, part = self.place, self.part
        owner, step = self.count - 1 - index // self.steps, lax.rem(index, self.steps)

        @pl.when(jnp.logical_and(owner > place, place == 0))
        def _():
            self.up(owner, step, part).start()

        @pl.when(jnp.logical_and(owner > place, place > 0))
        def _():
            self.up(owner, step, part).wait_recv()
            where = self.window(owner, step)
            self.up_acc[where] = part[where] + self.from_below[where]
            self.up(owner, step, self.up_acc).start()

    def down_turn(self, index):
        place, part, count = self.place, self.part, self.count
        owner, step = index // self.steps, lax.rem(index, self.steps)

        @pl.when(jnp.logical_and(owner < place, place == count - 1))
        def _():
            self.down(owner, step, part).start()

        @pl.when(jnp.logical_and(owner < place, place < count - 1))
        def _():
            self.down(owner, step, part).wait_recv()
            where = self.window(owner, step)
            self.down_acc[where] = part[where] + self.from_above[where]
            self.down(owner, step, self.down_acc).start()

    def run(self, pause=None):
        turns, lag = self.count * self.steps, self.steps

        def staggered(first, second):
            def begin(index, carry):
                first(index)
                return carry

            def both(index, carry):
                first(index)
                second(index - lag)
                return carry

            def end(index, carry):
                second(index)
                return carry

            lax.fori_loop(0, lag, begin, 0)
            if pause is not None:
                pause()
            lax.fori_loop(lag, turns, both, 0)
            lax.fori_loop(turns - lag, turns, end, 0)

        @pl.when(self.place < self.count // 2)
        def _():
            staggered(self.up_turn, self.down_turn)

        @pl.when(self.place >= self.count // 2)
        def _():
            staggered(self.down_turn, self.up_turn)

    def settle(self):
        place, rows = self.place, self.rows

        def one(step, carry):
            where = self.window(place, step)
            mine = pl.ds(pl.multiple_of(step * rows, rows), rows)
            self.out[mine] = self.part[where]

            @pl.when(place > 0)
            def _():
                self.up(place, step, self.part).wait_recv()
                self.out[mine] += self.from_below[where]

            @pl.when(place < self.count - 1)
            def _():
                self.down(place, step, self.part).wait_recv()
                self.out[mine] += self.from_above[where]

            return carry

        lax.fori_loop(0, self.steps, one, 0)

    def finish(self):
        place = self.place

        def one(index, carry):
            owner, step = index // self.steps, lax.rem(index, self.steps)

            @pl.when(owner > place)
            def _():
                self.up(owner, step, self.part).wait_send()

            @pl.when(owner < place)
            def _():
                self.down(owner, step, self.part).wait_send()

            return carry

        lax.fori_loop(0, self.count * self.steps, one, 0)


def line_scatter_kernel(count, stage, held, raws, results, scratch):
    own, sem = scratch[8:]
    scatter = LineScatter(count, held[0], results[0], scratch[:4], scratch[4:8])
    rows = own.shape[0]
    load = pltpu.make_async_copy(
        raws[0].at[pl.ds(pl.multiple_of(scatter.place * rows, rows), rows)], own, sem
    )
    load.start()
    greet(scatter.place, count)
    scatter.run()
    scatter.settle()
    load.wait()
    results[0][...] += own[...]
    scatter.finish()


def line_scatter(part, base, call_id):
    rows, width = part.shape
    count = lax.axis_size("mp")
    own = (rows // count, width)
    (result,) = staged(
        partial(line_scatter_kernel, count),
        [],
        [jax.ShapeDtypeStruct(own, jnp.float32)],
        LineScatter.scratch(count, (rows, width), 8)
        + [pltpu.VMEM(own, jnp.float32), pltpu.SemaphoreType.DMA],
        2 * rows * width,
        [base],
        call_id=call_id,
        length=33,
        near=[part],
    )
    return result


def line_gather_kernel(count, count_dp, extra, stage, held, raws, results, scratch):
    own_ref, out_ref = held[0], results[0]
    items, outs = views(held[1:]), views(results[1:], 2)
    up_send, down_send, up_recv, down_recv = scratch[:4]
    sums = PieceSums(count_dp, items, outs, scratch[4:])
    place = lax.axis_index("mp")
    steps = up_send.shape[1]
    block = own_ref.shape[0]
    rows = block // steps
    below, above = {"mp": place - 1}, {"mp": place + 1}
    greet(place, count, sums.peers())
    stage.wait(0)

    def window(owner, step):
        return pl.ds(pl.multiple_of(owner * block + step * rows, rows), rows)

    def up(owner, step):
        part = out_ref.at[window(owner, step)]
        return remote(part, part, up_send.at[owner, step], up_recv.at[owner, step], above)

    def down(owner, step):
        part = out_ref.at[window(owner, step)]
        return remote(part, part, down_send.at[owner, step], down_recv.at[owner, step], below)

    def begin(step, carry):
        out_ref[window(place, step)] = own_ref[pl.ds(pl.multiple_of(step * rows, rows), rows)]

        @pl.when(place < count - 1)
        def _():
            up(place, step).start()

        @pl.when(place > 0)
        def _():
            down(place, step).start()

        return carry

    lax.fori_loop(0, steps, begin, 0)
    stage.wait(*range(1, len(stage.loads)))
    sums.begin()

    def pass_on(index, carry):
        away, step = 1 + index // steps, lax.rem(index, steps)

        @pl.when(place - away >= 0)
        def _():
            up(place - away, step).wait_recv()

        @pl.when(jnp.logical_and(place - away >= 0, place < count - 1))
        def _():
            up(place - away, step).start()

        @pl.when(place + away < count)
        def _():
            down(place + away, step).wait_recv()

        @pl.when(jnp.logical_and(place + away < count, place > 0))
        def _():
            down(place + away, step).start()

        return carry

    for low, high, phase in sums.moments((count - 1) * steps):
        lax.fori_loop(low, high, pass_on, 0)
        sums.advance(phase)

    def drain(index, carry):
        owner, step = index // steps, lax.rem(index, steps)

        @pl.when(jnp.logical_and(owner <= place, place < count - 1))
        def _():
            up(owner, step).wait_send()

        @pl.when(jnp.logical_and(owner >= place, place > 0))
        def _():
            down(owner, step).wait_send()

        return carry

    lax.fori_loop(0, count * steps, drain, 0)
    sums.finish()


def line_gather(own, call_id, items=()):
    rows, width = own.shape
    count, count_dp = lax.axis_size("mp"), lax.axis_size("dp")
    sems = pltpu.SemaphoreType.DMA((count, 8))
    items, shapes, shares = piece_shapes(items)
    results = staged(
        partial(line_gather_kernel, count, count_dp, len(items)),
        [own, *items],
        shares,
        [sems] * 4 + PieceSums.scratch(count_dp, shapes),
        rows * width,
        call_id=call_id,
        length=38,
        near_outs=[jax.ShapeDtypeStruct((rows * count, width), jnp.float32)],
    )
    return results[0], results[-1], results[1:-1]


def dot(left, right, left_dim=1, right_dim=0):
    return lax.dot_general(
        left, right, (((left_dim,), (right_dim,)), ((), ())), preferred_element_type=jnp.float32
    )


def head_mask(width, copies):
    lane = lax.broadcasted_iota(jnp.int32, (1, width), 1)
    return [lane // HEAD_DIM == head for head in range(copies)]


def spread_heads(values):
    masks = head_mask(values.shape[1], values.shape[1] // HEAD_DIM)
    return jnp.concatenate([jnp.where(mask, values, jnp.zeros_like(values)) for mask in masks], 0)


def join_heads(values, heads):
    rows = values.shape[0] // heads
    masks = head_mask(values.shape[1], heads)
    return sum(
        jnp.where(mask, values[head * rows : (head + 1) * rows], 0.0)
        for head, mask in enumerate(masks)
    )


def split_three(values):
    first = values.astype(jnp.bfloat16)
    left = values - first.astype(jnp.float32)
    second = left.astype(jnp.bfloat16)
    third = (left - second.astype(jnp.float32)).astype(jnp.bfloat16)
    return first, second, third


def norm_rows(values):
    centered = values - jnp.mean(values, -1, keepdims=True)
    scale = lax.rsqrt(jnp.mean(centered * centered, -1, keepdims=True) + 1e-05)
    return centered * scale, scale


def norm_rows_back(upstream, gain, normed, scale):
    inner = upstream * gain
    return scale * (
        inner
        - jnp.mean(inner, -1, keepdims=True)
        - normed * jnp.mean(inner * normed, -1, keepdims=True)
    )


def embed(noisy, pixels, place):
    stacked = jnp.concatenate(split_three(noisy), 0)
    return dot(stacked, jnp.concatenate([pixels] * 3, 0), 0, 0) + place


def read_forward_kernel(
    noisy_ref,
    keep_ref,
    place_ref,
    pixels_ref,
    latents_ref,
    wide_gain_ref,
    gain_ref,
    query_weight_ref,
    pair_weight_ref,
    out_weight_ref,
    part_ref,
    pairs_ref,
    output_ref,
    total_ref,
    queries_ref,
):
    heads = query_weight_ref.shape[2] // HEAD_DIM

    @pl.when(pl.program_id(0) == 0)
    def _():
        normed, _ = norm_rows(latents_ref[...].astype(jnp.float32))
        low = (normed * wide_gain_ref[...]).astype(jnp.bfloat16)
        queries = dot(low, query_weight_ref[0]).astype(jnp.bfloat16)
        queries_ref[...] = spread_heads(queries * jnp.bfloat16(HEAD_DIM ** (-0.5)))

    normed, _ = norm_rows(embed(noisy_ref[0], pixels_ref[...], place_ref[...]))
    side = (normed * gain_ref[...]).astype(jnp.bfloat16)
    keys = dot(side, pair_weight_ref[0]).astype(jnp.bfloat16)
    values = dot(side, pair_weight_ref[1]).astype(jnp.bfloat16)
    pairs_ref[0, 0] = keys
    pairs_ref[0, 1] = values
    scores = dot(keys, queries_ref[...], 1, 1)
    scores = jnp.where(keep_ref[0] > 0, scores, -1e30)
    top = jnp.max(scores, 0, keepdims=True)
    grown = jnp.exp(scores - top)
    summed = jnp.sum(grown, 0, keepdims=True)
    total_ref[0] = top + jnp.log(summed)
    probs = (grown / summed).astype(jnp.bfloat16)
    output = join_heads(dot(probs, values, 0, 0), heads).astype(jnp.bfloat16)
    output_ref[0] = output
    part_ref[...] = dot(output, out_weight_ref[0])


def whole(shape):
    return pl.BlockSpec(shape, lambda b: (0,) * len(shape))


def each(shape):
    return pl.BlockSpec((1,) + shape, lambda b: (b,) + (0,) * len(shape))


def slot_of(shape, slot):
    return pl.BlockSpec(shape, lambda b: (slot,) + (0,) * (len(shape) - 1))


def read_forward(noisy, keep, place, pixels, latents, wide_gain, gain, wide, narrow, wideout):
    images, _, patches = noisy.shape
    count, d_lat = latents.shape
    d_if, local = narrow.shape[1:]
    stacked = local // HEAD_DIM * count
    return pl.pallas_call(
        read_forward_kernel,
        grid=(images,),
        out_shape=[
            pltpu.VMEM((images * count, d_lat), jnp.float32),
            pltpu.HBM((images, 2, patches, local), jnp.bfloat16),
            pltpu.HBM((images, count, local), jnp.bfloat16),
            pltpu.HBM((images, 1, stacked), jnp.float32),
            pltpu.HBM((stacked, local), jnp.bfloat16),
        ],
        in_specs=[
            each(noisy.shape[1:]),
            each((patches, 1)),
            whole((patches, d_if)),
            whole(pixels.shape),
            whole(latents.shape),
            whole((1, d_lat)),
            whole((1, d_if)),
            slot_of((1, d_lat, local), 0),
            slot_of((2, d_if, local), 0),
            slot_of((1, local, d_lat), 0),
        ],
        out_specs=[
            pl.BlockSpec((count, d_lat), lambda b: (b, 0)),
            each((2, patches, local)),
            each((count, local)),
            each((1, stacked)),
            whole((stacked, local)),
        ],
        compiler_params=pltpu.CompilerParams(vmem_limit_bytes=40 << 20),
        cost_estimate=pl.CostEstimate(
            flops=10**10, bytes_accessed=30 * 10**6, transcendentals=2 * 10**6
        ),
    )(in_hbm(noisy), in_hbm(keep), in_hbm(place), in_hbm(pixels), in_hbm(latents), in_hbm(wide_gain), in_hbm(gain), in_hbm(wide), in_hbm(narrow), in_hbm(wideout))


def read_backward_kernel(
    noisy_ref,
    keep_ref,
    place_ref,
    pixels_ref,
    latents_ref,
    wide_gain_ref,
    gain_ref,
    query_weight_ref,
    pair_weight_ref,
    out_weight_ref,
    pairs_ref,
    output_ref,
    total_ref,
    queries_ref,
    grad_ref,
    lead_ref,
    wide_grad_ref,
    narrow_grad_ref,
    latents_grad_ref,
    wide_gain_grad_ref,
    gain_grad_ref,
    embed_grad_ref,
    low_ref,
    returned_ref,
):
    step, steps = pl.program_id(0), pl.num_programs(0)
    heads = query_weight_ref.shape[2] // HEAD_DIM

    @pl.when(step == 0)
    def _():
        normed, _ = norm_rows(latents_ref[...].astype(jnp.float32))
        low_ref[...] = (normed * wide_gain_ref[...]).astype(jnp.bfloat16)
        for ref in (
            wide_grad_ref,
            narrow_grad_ref,
            latents_grad_ref,
            gain_grad_ref,
            embed_grad_ref,
            returned_ref,
        ):
            ref[...] = jnp.zeros_like(ref)

    normed, scale = norm_rows(embed(noisy_ref[0], pixels_ref[...], place_ref[...]))
    side = (normed * gain_ref[...]).astype(jnp.bfloat16)
    keys, values, queries = pairs_ref[0, 0], pairs_ref[0, 1], queries_ref[...]
    branch = grad_ref[...].astype(jnp.bfloat16)
    latents_grad_ref[...] += lead_ref[...] * grad_ref[...]
    wide_grad_ref[1] += dot(branch, output_ref[0], 0, 0)
    upstream = spread_heads(dot(branch, out_weight_ref[0], 1, 1).astype(jnp.bfloat16))
    scores = dot(keys, queries, 1, 1)
    scores = jnp.where(keep_ref[0] > 0, scores, -1e30)
    probs = jnp.exp(scores - total_ref[0])
    value_grad = dot(probs.astype(jnp.bfloat16), upstream).astype(jnp.bfloat16)
    prob_grad = dot(values, upstream, 1, 1)
    inner = jnp.sum(prob_grad * probs, 0, keepdims=True)
    score_grad = (probs * (prob_grad - inner)).astype(jnp.bfloat16)
    key_grad = dot(score_grad, queries).astype(jnp.bfloat16)
    query_grad = join_heads(dot(score_grad, keys, 0, 0), heads) * HEAD_DIM ** (-0.5)
    query_grad = query_grad.astype(jnp.bfloat16)
    wide_grad_ref[0] += dot(low_ref[...], query_grad, 0, 0)
    returned_ref[...] += dot(query_grad, query_weight_ref[0], 1, 1)
    narrow_grad_ref[0] += dot(side, key_grad, 0, 0)
    narrow_grad_ref[1] += dot(side, value_grad, 0, 0)
    side_grad = dot(key_grad, pair_weight_ref[0], 1, 1) + dot(value_grad, pair_weight_ref[1], 1, 1)
    gain_grad_ref[...] += jnp.sum(side_grad * normed, 0, keepdims=True)
    back = norm_rows_back(side_grad, gain_ref[...], normed, scale)
    embed_grad_ref[...] += embed_back(noisy_ref[0], back)

    @pl.when(step == steps - 1)
    def _():
        normed, scale = norm_rows(latents_ref[...].astype(jnp.float32))
        returned = returned_ref[...]
        wide_gain_grad_ref[...] = jnp.sum(returned * normed, 0, keepdims=True)
        latents_grad_ref[...] += norm_rows_back(returned, wide_gain_ref[...], normed, scale)


def embed_back(noisy, back):
    first, second, _ = split_three(noisy)
    high = back.astype(jnp.bfloat16)
    low = (back - high.astype(jnp.float32)).astype(jnp.bfloat16)
    rows = noisy.shape[0]
    both = dot(jnp.concatenate([first, second], 0), high)
    return both[:rows] + both[rows:] + dot(first, low)


def read_backward(
    noisy,
    keep,
    place,
    pixels,
    latents,
    wide_gain,
    gain,
    wide,
    narrow,
    wideout,
    pairs,
    output,
    total,
    queries,
    grad,
    lead,
):
    images, rows, patches = noisy.shape
    count, d_lat = latents.shape
    d_if, local = narrow.shape[1:]
    stacked = local // HEAD_DIM * count
    results = [
        (2, d_lat, local),
        (2, d_if, local),
        (count, d_lat),
        (1, d_lat),
        (1, d_if),
        (rows, d_if),
    ]
    return pl.pallas_call(
        read_backward_kernel,
        grid=(images,),
        out_shape=[pltpu.HBM(shape, jnp.float32) for shape in results],
        in_specs=[
            each(noisy.shape[1:]),
            each((patches, 1)),
            whole((patches, d_if)),
            whole(pixels.shape),
            whole(latents.shape),
            whole((1, d_lat)),
            whole((1, d_if)),
            slot_of((1, d_lat, local), 0),
            slot_of((2, d_if, local), 0),
            slot_of((1, local, d_lat), 0),
            each((2, patches, local)),
            each((count, local)),
            each((1, stacked)),
            whole((stacked, local)),
            pl.BlockSpec((count, d_lat), lambda b: (b, 0)),
            whole((1, 1)),
        ],
        out_specs=[whole(shape) for shape in results],
        scratch_shapes=[
            pltpu.VMEM((count, d_lat), jnp.bfloat16),
            pltpu.VMEM((count, d_lat), jnp.float32),
        ],
        compiler_params=pltpu.CompilerParams(vmem_limit_bytes=48 << 20),
        cost_estimate=pl.CostEstimate(
            flops=2 * 10**10, bytes_accessed=30 * 10**6, transcendentals=2 * 10**6
        ),
    )(in_hbm(noisy), in_hbm(keep), in_hbm(place), in_hbm(pixels), in_hbm(latents), in_hbm(wide_gain), in_hbm(gain), in_hbm(wide), in_hbm(narrow), in_hbm(wideout), in_hbm(pairs), in_hbm(output), in_hbm(total), in_hbm(queries), in_vmem(grad), in_hbm(lead))


def rows_of(rows, width):
    return pl.BlockSpec((rows, width), lambda b: (b, 0))


def attend_few(keys, values, queries):
    scores = dot(keys, queries, 1, 1)
    top = jnp.max(scores, 0, keepdims=True)
    grown = jnp.exp(scores - top)
    summed = jnp.sum(grown, 0, keepdims=True)
    probs = (grown / summed).astype(jnp.bfloat16)
    return dot(probs, values, 0, 0), top + jnp.log(summed)


def scaled_heads(queries):
    return spread_heads(queries * jnp.bfloat16(HEAD_DIM ** (-0.5)))


def self_forward_kernel(
    latent_ref, gain_ref, q_ref, k_ref, v_ref, out_weight_ref, part_ref, triple_ref, output_ref, total_ref, low_ref
):
    heads = q_ref.shape[2] // HEAD_DIM
    normed, _ = norm_rows(latent_ref[...])
    low = (normed * gain_ref[...]).astype(jnp.bfloat16)
    low_ref[...] = low
    queries, keys, values = (dot(low, ref[0]).astype(jnp.bfloat16) for ref in (q_ref, k_ref, v_ref))
    for index, item in enumerate((queries, keys, values)):
        triple_ref[0, index] = item
    output, total_ref[0] = attend_few(keys, values, scaled_heads(queries))
    output = join_heads(output, heads).astype(jnp.bfloat16)
    output_ref[0] = output
    part_ref[...] = dot(output, out_weight_ref[0])


def self_forward(latent, gain, wide, wideout, images):
    total, d_lat = latent.shape
    count, local = total // images, wide.shape[2]
    stacked = local // HEAD_DIM * count
    return pl.pallas_call(
        self_forward_kernel,
        grid=(images,),
        out_shape=[
            pltpu.VMEM((total, d_lat), jnp.float32),
            pltpu.HBM((images, 3, count, local), jnp.bfloat16),
            pltpu.HBM((images, count, local), jnp.bfloat16),
            pltpu.HBM((images, 1, stacked), jnp.float32),
            pltpu.HBM((total, d_lat), jnp.bfloat16),
        ],
        in_specs=[rows_of(count, d_lat), whole((1, d_lat))]
        + [slot_of((1, d_lat, local), slot) for slot in (1, 2, 3)]
        + [slot_of((1, local, d_lat), 1)],
        out_specs=[
            rows_of(count, d_lat),
            each((3, count, local)),
            each((count, local)),
            each((1, stacked)),
            rows_of(count, d_lat),
        ],
        compiler_params=pltpu.CompilerParams(vmem_limit_bytes=20 << 20),
        cost_estimate=pl.CostEstimate(
            flops=3 * 10**9, bytes_accessed=12 * 10**6, transcendentals=3 * 10**5
        ),
    )(in_vmem(latent), in_hbm(gain), in_hbm(wide), in_hbm(wide), in_hbm(wide), in_hbm(wideout))


def self_backward_kernel(
    grad_ref,
    latent_ref,
    gain_ref,
    q_ref,
    k_ref,
    v_ref,
    out_weight_ref,
    triple_ref,
    output_ref,
    total_ref,
    low_ref,
    part_ref,
    first_ref,
    last_ref,
    gain_grad_ref,
    branches,
    outputs,
    grads,
    lows,
):
    step, steps = pl.program_id(0), pl.num_programs(0)
    heads = q_ref.shape[2] // HEAD_DIM
    count = grad_ref.shape[0]
    mine = pl.ds(pl.multiple_of(step * count, count), count)
    normed, scale = norm_rows(latent_ref[...])
    branch = grad_ref[...].astype(jnp.bfloat16)
    branches[mine] = branch
    outputs[mine] = output_ref[0]
    lows[mine] = low_ref[...]
    upstream = spread_heads(dot(branch, out_weight_ref[0], 1, 1).astype(jnp.bfloat16))
    keys, values = triple_ref[0, 1], triple_ref[0, 2]
    queries = scaled_heads(triple_ref[0, 0])
    probs = jnp.exp(dot(keys, queries, 1, 1) - total_ref[0])
    value_grad = dot(probs.astype(jnp.bfloat16), upstream).astype(jnp.bfloat16)
    prob_grad = dot(values, upstream, 1, 1)
    inner = jnp.sum(prob_grad * probs, 0, keepdims=True)
    score_grad = (probs * (prob_grad - inner)).astype(jnp.bfloat16)
    key_grad = dot(score_grad, queries).astype(jnp.bfloat16)
    query_grad = join_heads(dot(score_grad, keys, 0, 0), heads) * HEAD_DIM ** (-0.5)
    query_grad = query_grad.astype(jnp.bfloat16)
    part = (
        dot(query_grad, q_ref[0], 1, 1)
        + dot(key_grad, k_ref[0], 1, 1)
        + dot(value_grad, v_ref[0], 1, 1)
    )
    for index, item in enumerate((query_grad, key_grad, value_grad)):
        grads[index, mine] = item
    gain_part = jnp.sum(part * normed, 0, keepdims=True)
    gain_grad_ref[...] = gain_part + jnp.where(step == 0, 0.0, gain_grad_ref[...])
    part_ref[...] = norm_rows_back(part, gain_ref[...], normed, scale)

    @pl.when(step == steps - 1)
    def _():
        turned = lows[...].T
        first_ref[0] = dot(turned, grads[0])
        first_ref[1] = dot(turned, grads[1])
        last_ref[0] = dot(turned, grads[2])
        last_ref[1] = dot(branches[...], outputs[...], 0, 0)


def self_backward(grad, latent, gain, wide, wideout, triple, output, total, low):
    rows, d_lat = latent.shape
    images, _, count, local = triple.shape
    stacked = local // HEAD_DIM * count
    weight = pltpu.HBM((2, d_lat, local), jnp.float32)
    return pl.pallas_call(
        self_backward_kernel,
        grid=(images,),
        out_shape=[pltpu.VMEM((rows, d_lat), jnp.float32)]
        + [weight] * 2
        + [pltpu.HBM((1, d_lat), jnp.float32)],
        in_specs=[rows_of(count, d_lat), rows_of(count, d_lat), whole((1, d_lat))]
        + [slot_of((1, d_lat, local), slot) for slot in (1, 2, 3)]
        + [
            slot_of((1, local, d_lat), 1),
            each((3, count, local)),
            each((count, local)),
            each((1, stacked)),
            rows_of(count, d_lat),
        ],
        out_specs=[rows_of(count, d_lat)] + [whole((2, d_lat, local))] * 2 + [whole((1, d_lat))],
        scratch_shapes=[
            pltpu.VMEM((rows, d_lat), jnp.bfloat16),
            pltpu.VMEM((rows, local), jnp.bfloat16),
            pltpu.VMEM((3, rows, local), jnp.bfloat16),
            pltpu.VMEM((rows, d_lat), jnp.bfloat16),
        ],
        compiler_params=pltpu.CompilerParams(vmem_limit_bytes=28 << 20),
        cost_estimate=pl.CostEstimate(
            flops=6 * 10**9, bytes_accessed=16 * 10**6, transcendentals=3 * 10**5
        ),
    )(in_vmem(grad), in_hbm(latent), in_hbm(gain), in_hbm(wide), in_hbm(wide), in_hbm(wide), in_hbm(wideout), in_hbm(triple), in_hbm(output), in_hbm(total), in_hbm(low))


def feed_forward_kernel(
    latent_ref, gain_ref, up_ref, down_ref, part_ref, active_ref, slope_ref, low_ref
):
    @pl.when(pl.program_id(0) == 0)
    def _():
        normed, _ = norm_rows(latent_ref[...])
        low_ref[...] = (normed * gain_ref[...]).astype(jnp.bfloat16)

    hidden = dot(low_ref[...], up_ref[0])
    share = 0.5 * (1.0 + lax.erf(hidden * math.sqrt(0.5)))
    density = jnp.exp(-0.5 * hidden * hidden) * (1.0 / math.sqrt(2.0 * math.pi))
    active = (hidden * share).astype(jnp.bfloat16)
    active_ref[0] = active
    slope_ref[0] = share + hidden * density
    part = dot(active, down_ref[0])

    @pl.when(pl.program_id(0) == 0)
    def _():
        part_ref[...] = part

    @pl.when(pl.program_id(0) > 0)
    def _():
        part_ref[...] += part


def feed_forward(latent, gain, wide, wideout):
    rows, d_lat = latent.shape
    local = wide.shape[2]
    return pl.pallas_call(
        feed_forward_kernel,
        grid=(4,),
        out_shape=[
            pltpu.VMEM((rows, d_lat), jnp.float32),
            pltpu.HBM((4, rows, local), jnp.bfloat16),
            pltpu.HBM((4, rows, local), jnp.float32),
            pltpu.HBM((rows, d_lat), jnp.bfloat16),
        ],
        in_specs=[
            whole((rows, d_lat)),
            whole((1, d_lat)),
            pl.BlockSpec((1, d_lat, local), lambda s: (4 + s, 0, 0)),
            pl.BlockSpec((1, local, d_lat), lambda s: (2 + s, 0, 0)),
        ],
        out_specs=[
            whole((rows, d_lat)),
            each((rows, local)),
            each((rows, local)),
            whole((rows, d_lat)),
        ],
        compiler_params=pltpu.CompilerParams(vmem_limit_bytes=24 << 20),
        cost_estimate=pl.CostEstimate(
            flops=4 * 10**9, bytes_accessed=14 * 10**6, transcendentals=10**6
        ),
    )(in_vmem(latent), in_hbm(gain), in_hbm(wide), in_hbm(wideout))


def feed_backward_kernel(
    grad_ref,
    latent_ref,
    gain_ref,
    up_ref,
    down_ref,
    active_ref,
    slope_ref,
    low_ref,
    part_ref,
    up_first_ref,
    up_last_ref,
    down_grad_ref,
    gain_grad_ref,
    branch,
    branch_turned,
    low_turned,
    total,
):
    step, steps = pl.program_id(0), pl.num_programs(0)

    @pl.when(step == 0)
    def _():
        low = grad_ref[...].astype(jnp.bfloat16)
        branch[...] = low
        branch_turned[...] = low.T
        low_turned[...] = low_ref[...].T
        total[...] = jnp.zeros_like(total)

    active_grad = dot(branch[...], down_ref[0], 1, 1)
    hidden_grad = (active_grad * slope_ref[0]).astype(jnp.bfloat16)
    down_grad_ref[0] = dot(branch_turned[...], active_ref[0])
    total[...] += dot(hidden_grad, up_ref[0], 1, 1)
    up_grad = dot(low_turned[...], hidden_grad)

    @pl.when(step < 2)
    def _():
        up_first_ref[0] = up_grad

    @pl.when(step >= 2)
    def _():
        up_last_ref[0] = up_grad

    @pl.when(step == steps - 1)
    def _():
        normed, scale = norm_rows(latent_ref[...])
        part = total[...]
        gain_grad_ref[...] = jnp.sum(part * normed, 0, keepdims=True)
        part_ref[...] = norm_rows_back(part, gain_ref[...], normed, scale)


def feed_backward(grad, latent, gain, wide, wideout, active, slope, low):
    rows, d_lat = latent.shape
    local = wide.shape[2]
    return pl.pallas_call(
        feed_backward_kernel,
        grid=(4,),
        out_shape=[
            pltpu.VMEM((rows, d_lat), jnp.float32),
            pltpu.HBM((2, d_lat, local), jnp.float32),
            pltpu.HBM((2, d_lat, local), jnp.float32),
            pltpu.HBM((4, d_lat, local), jnp.float32),
            pltpu.HBM((1, d_lat), jnp.float32),
        ],
        in_specs=[
            whole((rows, d_lat)),
            whole((rows, d_lat)),
            whole((1, d_lat)),
            pl.BlockSpec((1, d_lat, local), lambda s: (4 + s, 0, 0)),
            pl.BlockSpec((1, local, d_lat), lambda s: (2 + s, 0, 0)),
            each((rows, local)),
            each((rows, local)),
            whole((rows, d_lat)),
        ],
        out_specs=[
            whole((rows, d_lat)),
            pl.BlockSpec((1, d_lat, local), lambda s: (jnp.minimum(s, 1), 0, 0)),
            pl.BlockSpec((1, d_lat, local), lambda s: (jnp.maximum(s - 2, 0), 0, 0)),
            each((d_lat, local)),
            whole((1, d_lat)),
        ],
        scratch_shapes=[
            pltpu.VMEM((rows, d_lat), jnp.bfloat16),
            pltpu.VMEM((d_lat, rows), jnp.bfloat16),
            pltpu.VMEM((d_lat, rows), jnp.bfloat16),
            pltpu.VMEM((rows, d_lat), jnp.float32),
        ],
        compiler_params=pltpu.CompilerParams(vmem_limit_bytes=36 << 20),
        cost_estimate=pl.CostEstimate(
            flops=9 * 10**9, bytes_accessed=26 * 10**6, transcendentals=0
        ),
    )(in_vmem(grad), in_hbm(latent), in_hbm(gain), in_hbm(wide), in_hbm(wideout), in_hbm(active), in_hbm(slope), in_hbm(low))


def write_kernel(stage, held, raws, results, scratch):
    (
        own_weight_ref,
        weight_total_ref,
        latent_ref,
        noisy_ref,
        noise_ref,
        keep_ref,
        place_ref,
        pixels_ref,
        wide_gain_ref,
        gain_ref,
        key_weight_ref,
        value_weight_ref,
        query_weight_ref,
        out_weight_ref,
    ) = held
    (
        latent_grad_ref,
        key_grad_ref,
        value_grad_ref,
        query_grad_ref,
        out_grad_ref,
        wide_gain_grad_ref,
        gain_grad_ref,
        embed_grad_ref,
        head_grad_ref,
        loss_ref,
    ) = results
    queries, outputs, upstream, query_grads, normed_ref, scale_ref = scratch
    stage.wait(*range(10))
    patches, width = queries.shape
    group = 4 * HEAD_DIM
    groups = width // group
    latents = latent_ref.shape[0]
    rows = 4 * latents
    weight, weight_total = own_weight_ref[:1, :1], weight_total_ref[:1, :1]

    latent_normed, latent_scale = norm_rows(latent_ref[...])
    latent_low = (latent_normed * wide_gain_ref[...]).astype(jnp.bfloat16)
    interface = embed(noisy_ref[...], pixels_ref[0], place_ref[...])
    normed, scale = norm_rows(interface)
    normed_ref[...] = normed
    scale_ref[...] = scale
    outer_low = (normed * gain_ref[1:2]).astype(jnp.bfloat16)
    stage.wait(10, 11)
    keys = dot(latent_low, key_weight_ref[...]).astype(jnp.bfloat16)
    values = dot(latent_low, value_weight_ref[...]).astype(jnp.bfloat16)
    stage.wait(12, 13)
    queries[...] = dot(outer_low, query_weight_ref[...]).astype(jnp.bfloat16)

    def part(values, index):
        return values[:, index * group : (index + 1) * group]

    def by_head(values):
        return values.reshape(4, latents, patches)

    def group_probs(index):
        scores = by_head(dot(scaled_heads(part(keys, index)), part(queries, index), 1, 1))
        grown = jnp.exp(scores - jnp.max(scores, 1, keepdims=True))
        return grown / jnp.sum(grown, 1, keepdims=True)

    for index in range(groups):
        probs = group_probs(index).reshape(rows, patches).astype(jnp.bfloat16)
        output = dot(probs, spread_heads(part(values, index)), 0, 0)
        outputs[:, index * group : (index + 1) * group] = output.astype(jnp.bfloat16)

    outer = interface + dot(outputs[...], out_weight_ref[...], 1, 1)
    final_normed, final_scale = norm_rows(outer)
    final_low = (final_normed * gain_ref[2:3]).astype(jnp.bfloat16)
    head = pixels_ref[1]
    difference = dot(head, final_low, 1, 1) - noise_ref[...]
    masked = weight * keep_ref[...] * difference
    loss_ref[...] = jnp.full(loss_ref.shape, jnp.sum(masked * difference))
    predict_grad = (2.0 * masked / weight_total).astype(jnp.bfloat16)
    head_grad_ref[...] = dot(predict_grad, final_low)
    final_grad = dot(predict_grad, head, 0, 0)
    gain_final = jnp.sum(final_grad * final_normed, 0, keepdims=True)
    outer_grad = norm_rows_back(final_grad, gain_ref[2:3], final_normed, final_scale)
    branch = outer_grad.astype(jnp.bfloat16)
    out_grad_ref[...] = dot(branch, outputs[...], 0, 0)
    stage.store(4)
    upstream[...] = dot(branch, out_weight_ref[...]).astype(jnp.bfloat16)

    key_grads, value_grads = [], []
    for index in range(groups):
        probs = group_probs(index)
        low = probs.reshape(rows, patches).astype(jnp.bfloat16)
        above = part(upstream, index)
        value_grads.append(join_heads(dot(low, above), 4).astype(jnp.bfloat16))
        prob_grad = by_head(dot(spread_heads(part(values, index)), above, 1, 1))
        inner = jnp.sum(prob_grad * probs, 1, keepdims=True)
        score_grad = (probs * (prob_grad - inner)).reshape(rows, patches).astype(jnp.bfloat16)
        key_grad = join_heads(dot(score_grad, part(queries, index)), 4) * HEAD_DIM ** (-0.5)
        key_grads.append(key_grad.astype(jnp.bfloat16))
        query_grad = dot(score_grad, scaled_heads(part(keys, index)), 0, 0)
        query_grads[:, index * group : (index + 1) * group] = query_grad.astype(jnp.bfloat16)
    key_grad, value_grad = (jnp.concatenate(item, 1) for item in (key_grads, value_grads))

    turned = latent_low.T
    key_grad_ref[...] = dot(turned, key_grad)
    value_grad_ref[...] = dot(turned, value_grad)
    stage.store(1, 2)
    latent_part = dot(key_grad, key_weight_ref[...], 1, 1) + dot(
        value_grad, value_weight_ref[...], 1, 1
    )
    wide_gain_grad_ref[...] = jnp.sum(latent_part * latent_normed, 0, keepdims=True)
    latent_grad_ref[...] = norm_rows_back(
        latent_part, wide_gain_ref[...], latent_normed, latent_scale
    )
    normed, scale = normed_ref[...], scale_ref[...]
    outer_low = (normed * gain_ref[1:2]).astype(jnp.bfloat16)
    query_grad_ref[...] = dot(outer_low, query_grads[...], 0, 0)
    stage.store(3)
    outer_part = dot(query_grads[...], query_weight_ref[...], 1, 1)
    gain_outer = jnp.sum(outer_part * normed, 0, keepdims=True)
    gain_grad_ref[...] = jnp.concatenate([gain_outer, gain_final], 0)
    back = outer_grad + norm_rows_back(outer_part, gain_ref[1:2], normed, scale)
    embed_grad_ref[...] = embed_back(noisy_ref[...], back)


def write_stage(
    own_weight, weight_total, latent, noisy, noise, keep, place, pixels, wide_gain, gains, weights
):
    latents, d_lat = latent.shape
    rows, patches = noisy.shape
    d_if = place.shape[1]
    width = weights[0].shape[1]
    results = [
        (latents, d_lat),
        (d_lat, width),
        (d_lat, width),
        (d_if, width),
        (d_if, width),
        (1, d_lat),
        (2, d_if),
        (rows, d_if),
        (rows, d_if),
        (8, 128),
    ]
    wide = pltpu.VMEM((patches, width), jnp.bfloat16)
    return staged(
        write_kernel,
        [
            own_weight,
            weight_total,
            latent,
            noisy,
            noise,
            keep,
            place,
            pixels,
            wide_gain,
            gains,
            *weights,
        ],
        [jax.ShapeDtypeStruct(shape, jnp.float32) for shape in results],
        [wide] * 4
        + [pltpu.VMEM((patches, d_if), jnp.float32), pltpu.VMEM((patches, 1), jnp.float32)],
        15 * 10**9,
        length=27,
    )


def adam_update(master, first, second, gradient, scale):
    clipped = gradient * scale
    moment = adam_beta * first + (1.0 - adam_beta) * clipped
    square = adam_beta * second + (1.0 - adam_beta) * clipped * clipped
    fixed_first = moment / (1.0 - adam_beta**STEP)
    fixed_second = square / (1.0 - adam_beta**STEP)
    updated = master - learning_rate * (
        fixed_first / (jnp.sqrt(fixed_second) + adam_eps) + weight_decay * master
    )
    return (updated, moment, square)


def sum_rows(values):
    return jnp.sum(values.reshape(-1, 8, values.shape[-1]), 0)


def closing_kernel(count, count_dp, sizes, stage, held, raws, results, scratch):
    refs, given = list(scratch), list(held)

    def pull(number, source=None):
        source = refs if source is None else source
        taken = source[:number]
        del source[:number]
        return taken

    number, finished = sizes
    items, small_parts = views(pull(number, given)), pull(10, given)
    loss_tile, weight_tile = pull(2, given)
    done = views(pull(finished, given), 2)
    wide_out, narrow_out, turned_out, last_out, latents_out, rest_out, stats = results
    latents_item, rest_item, columns, column_sems = pull(4)
    items += [latents_item, rest_item]
    number = len(items)
    shares = pull(number)
    sums = PieceSums(count_dp, items, shares, pull(number * (count_dp.bit_length() + 1)))
    (write_share,) = pull(1)
    scatter = LineScatter(count, columns, write_share, pull(4), pull(4))
    small = [Spread("mp", count, *pull(3)) for _ in range(2)]
    over_dp, over_mp = Spread("dp", count_dp, *pull(3)), Spread("mp", count, *pull(3))

    column_loads, low = [], 0
    block, local = columns.shape[0] // count, columns.shape[1]
    for source in raws:
        rows = source.shape[0]
        for owner in range(count):
            column_loads.append(
                pltpu.make_async_copy(
                    source.at[:, pl.ds(owner * local, local)],
                    columns.at[pl.ds(owner * block + low, rows)],
                    column_sems.at[len(column_loads)],
                )
            )
        low += rows
    for load in column_loads:
        load.start()
    barrier = pltpu.get_barrier_semaphore()
    others = [over_dp.peer(step) for step in range(1, count_dp)]
    others += [over_mp.peer(step) for step in range(1, count)]
    signal_all(barrier, others)
    stage.wait()
    (latent_total, *gains, gain_side, gain_pair, side_embed, own_embed, head_grad) = small_parts
    d_if = gain_side.shape[1]
    lanes = d_if // count_dp
    width = latents_item.shape[2]
    rest_item[...] = jnp.zeros_like(rest_item)
    rows = []
    for gain in gains:
        rows += [gain[:, :d_if], gain[:, d_if:]]
    rows += [gain_side[...], gain_pair[...]]
    blocks = [(0, jnp.concatenate(rows, 0)), (16, side_embed[...] + own_embed[...]), (32, head_grad[...])]
    for piece in range(count_dp):
        latents_item[piece] = latent_total[:, piece * width : (piece + 1) * width]
        for first, block in blocks:
            rest_item[piece, pl.ds(first, block.shape[0]), :lanes] = block[
                :, piece * lanes : (piece + 1) * lanes
            ]
    pl.semaphore_wait(barrier, len(others))

    sums.begin()
    for load in column_loads:
        load.wait()
    scatter.run(lambda: sums.advance(1))
    for phase in range(2, sums.bits + 1):
        sums.advance(phase)
    for spread, share in zip(small, shares[-2:]):
        spread.held[spread.place] = share[...]
        spread.start()
    scatter.settle()

    self_in_2, self_out, read_query, read_out, read_key, read_value = shares[:6]
    self_in_0, self_in_1 = done[:2]
    up, down = done[2:6], done[6:10]
    lat_rows, if_rows = self_out.shape[0], read_key.shape[0]
    write_key, write_value = (write_share.at[pl.ds(i * lat_rows, lat_rows)] for i in range(2))
    write_query, write_out = (
        write_share.at[pl.ds(2 * lat_rows + i * if_rows, if_rows)] for i in range(2)
    )
    square = 0.0

    def keep(out, gradient, turn=False):
        nonlocal square
        value = gradient[...]
        square = square + sum_rows(value * value)
        out[...] = value.T if turn else value

    wide = [read_query, self_in_0, self_in_1, self_in_2] + up + [write_key, write_value]
    for slot, gradient in enumerate(wide):
        keep(wide_out.at[slot], gradient)
    for slot, gradient in enumerate([read_key, read_value, write_query]):
        keep(narrow_out.at[slot], gradient)
    for slot, gradient in enumerate([read_out, self_out] + down):
        keep(turned_out.at[slot], gradient, True)
    keep(last_out, write_out)
    stage.store(0, 1, 2, 3)
    for spread in small:
        spread.take()
    latents, rest = (spread.total() for spread in small)
    latents_out[...] = latents
    rest_out[...] = rest
    lead = (over_mp.place == 0).astype(jnp.float32)
    local = jnp.sum(square) + lead * (
        jnp.sum(sum_rows(latents * latents)) + jnp.sum(sum_rows(rest * rest))
    )
    lane = lax.broadcasted_iota(jnp.int32, (8, 128), 1)
    value = jnp.where(lane == 0, local, loss_tile[...])
    for spread in (over_dp, over_mp):
        spread.held[spread.place] = value
        spread.start()
        spread.take()
        value = spread.total()
    stats[...] = jnp.where(lane == 0, jnp.sqrt(value), value / weight_tile[...])
    sums.finish()
    scatter.finish()
    for spread in small + [over_dp, over_mp]:
        spread.finish()


def closing(items, small_parts, tiles, done, write_shares, call_id):
    items, shapes, _ = piece_shapes(items)
    count, count_dp = lax.axis_size("mp"), lax.axis_size("dp")
    latents, d_lat = small_parts[0].shape
    lat_rows, local = done[0].shape[1:]
    if_rows = write_shares[2].shape[0]
    extra = [(latents, d_lat // count_dp), (48, 128)]
    block = (sum(item.shape[0] for item in write_shares), local)
    columns = (count * block[0], local)
    outs = [
        (10, lat_rows, local),
        (3, if_rows, local),
        (6, local, lat_rows),
        (if_rows, local),
        *extra,
        (8, 128),
    ]
    shapes = shapes + extra
    scratch = (
        [pltpu.VMEM((count_dp,) + shape, jnp.float32) for shape in extra]
        + [
            pltpu.VMEM(columns, jnp.float32),
            pltpu.SemaphoreType.DMA((count * len(write_shares),)),
        ]
        + [pltpu.VMEM(shape, jnp.float32) for shape in shapes]
        + PieceSums.scratch(count_dp, shapes)
        + [pltpu.VMEM(block, jnp.float32)]
        + LineScatter.scratch(count, columns, 4)
        + Spread.scratch(count, extra[0])
        + Spread.scratch(count, extra[1])
        + Spread.scratch(count_dp, (8, 128))
        + Spread.scratch(count, (8, 128))
    )
    return staged(
        partial(closing_kernel, count, count_dp, (len(items), len(done))),
        [*items, *small_parts, *tiles, *done],
        [jax.ShapeDtypeStruct(shape, jnp.float32) for shape in outs],
        scratch,
        10**7,
        write_shares,
        call_id,
        50,
    )


def clip_scale(norm):
    return clip_level / jnp.maximum(norm, clip_level)


def update_kernel(kinds, *refs):
    number = 3 * (kinds + 1)
    sources, states, refs = refs[: 1 + kinds], refs[1 + kinds :][:number], refs[1 + kinds + number :]
    outs, local, refs = refs[:number], refs[number:][: 1 + kinds], refs[number + 1 + kinds :]
    local_sems, held, (in_sems, out_sems) = refs[0], refs[1 : 1 + number], refs[1 + number :]
    stats, gradients = local[0], local[1:]
    kinds += 1
    firsts = [
        pltpu.make_async_copy(source, target, local_sems.at[index])
        for index, (source, target) in enumerate(zip(sources, local))
    ]
    for first in firsts:
        first.start()
    lane = lax.broadcasted_iota(jnp.int32, (8, 128), 1)
    corner = jnp.logical_and(lane == 0, lax.broadcasted_iota(jnp.int32, (8, 128), 0) == 0)
    loads, copies = [], []
    pieces = []
    for kind, gradient in enumerate(gradients):
        slots = range(gradient.shape[0]) if len(gradient.shape) == 3 else [None]
        pieces += [(kind, slot) for slot in slots]

    def at(ref, slot):
        return ref if slot is None else ref.at[slot]

    for kind, slot in pieces:
        for index in range(3 * kind, 3 * kind + 3):
            source, target = at(states[index], slot), at(held[index], slot)
            loads.append(pltpu.make_async_copy(source, target, in_sems.at[len(loads)]))
            loads[-1].start()
    for load in firsts:
        load.wait()
    scale = jnp.sum(jnp.where(corner, clip_scale(stats[...]), 0.0))
    pixel_loads = [
        pltpu.make_async_copy(states[index], held[index], in_sems.at[len(loads) + index - 18])
        for index in range(18, 21)
    ]
    for load in pixel_loads:
        load.start()
    for order, (kind, slot) in enumerate(pieces):
        for load in loads[3 * order : 3 * order + 3]:
            load.wait()
        refs = [at(held[index], slot) for index in range(3 * kind, 3 * kind + 3)]
        source = at(gradients[kind], slot)
        rows, width = refs[0].shape
        step = math.gcd(rows, max(8, 8192 // width)) if rows % 8 == 0 else rows

        def one(index, carry, refs=refs, source=source, step=step, width=width):
            where = pl.ds(pl.multiple_of(index * step, step), step)
            state = [ref[where] for ref in refs]
            for ref, result in zip(refs, adam_update(*state, source[where, :width], scale)):
                ref[where] = result
            return carry

        lax.fori_loop(0, rows // step, one, 0)
        for index in range(3 * kind, 3 * kind + 3):
            source, target = at(held[index], slot), at(outs[index], slot)
            copies.append(pltpu.make_async_copy(source, target, out_sems.at[len(copies)]))
            copies[-1].start()
    for load in pixel_loads:
        load.wait()
    pixels, rest = held[18:21], gradients[-1]
    for slot in range(2):
        gradient = rest[16 * (slot + 1) : 16 * (slot + 1) + PIX, : pixels[0].shape[2]]
        state = [ref[:, slot, :] for ref in pixels]
        for ref, result in zip(pixels, adam_update(*state, gradient, scale)):
            ref[:, slot, :] = result
    for index in range(18, 21):
        copies.append(pltpu.make_async_copy(held[index], outs[index], out_sems.at[len(copies)]))
        copies[-1].start()
    for copy in copies:
        copy.wait()


def update_states(stats, gradients, states):
    kinds = len(gradients)
    copies = sum(3 * (item.shape[0] if item.ndim == 3 else 1) for item in gradients) + 3
    sems = pltpu.SemaphoreType.DMA((copies,))
    return pl.pallas_call(
        partial(update_kernel, kinds),
        out_shape=[pltpu.HBM(item.shape, item.dtype) for item in states],
        in_specs=[HBM_SPEC] * (1 + kinds + len(states)),
        out_specs=[HBM_SPEC] * len(states),
        scratch_shapes=[pltpu.VMEM(item.shape, jnp.float32) for item in (stats, *gradients)]
        + [pltpu.SemaphoreType.DMA((1 + kinds,))]
        + [pltpu.VMEM(item.shape, jnp.float32) for item in states]
        + [sems] * 2,
        compiler_params=pltpu.CompilerParams(vmem_limit_bytes=24 << 20),
        cost_estimate=pl.CostEstimate(
            flops=2 * 10**7, bytes_accessed=14 * 10**6, transcendentals=0
        ),
    )(*(in_hbm(item) for item in (stats, *gradients, *states)))


def write_apart(
    latent_three,
    own_noisy,
    own_noise,
    own_keep,
    own_weight,
    weight_total,
    place,
    copy_pixels,
    gain,
    gain_rows,
    weights,
    layout,
    timesteps,
):
    write_key_weight, write_value_weight, write_query_weight, write_out_weight = weights
    images, latents, first_image, sharers = layout
    own_images, own_latents, d_lat = latent_three.shape
    write_norm, write_stats = layer_norm(latent_three, gain)
    write_low = write_norm.astype(jnp.bfloat16)

    own_interface = (
        jnp.einsum(
            "bcp,cd->bpd", own_noisy, copy_pixels[0].astype(jnp.float32), precision=precise
        )
        + place
    )

    outer_norm, outer_stats = layer_norm(own_interface, gain_rows[9])
    outer_low = outer_norm.astype(jnp.bfloat16)

    def join(spec, values, weight):
        product = jnp.einsum(spec, values, weight, preferred_element_type=jnp.float32)
        return product.astype(jnp.bfloat16)

    def image_rows(values):
        if sharers == 1:
            return values
        nothing = jnp.where(timesteps[0] > 0, 0.0, -0.0)
        whole = lax.all_gather(values.astype(jnp.float32), "mp", axis=0, tiled=True)
        whole = whole + nothing
        whole = whole.reshape(images, latents, d_lat).astype(jnp.bfloat16)
        return lax.dynamic_slice_in_dim(whole, first_image, own_images, 0)

    write_query = join("bpd,dc->bpc", outer_low, write_query_weight)
    write_key = image_rows(join("bld,dc->blc", write_low, write_key_weight))
    write_value = image_rows(join("bld,dc->blc", write_low, write_value_weight))
    write_out, write_total = attend_forward(write_query, write_key, write_value, None)
    outer = own_interface + jnp.einsum(
        "bpc,dc->bpd", write_out, write_out_weight, preferred_element_type=jnp.float32
    )
    final_norm, final_stats = layer_norm(outer, gain_rows[10])
    final_low = final_norm.astype(jnp.bfloat16)
    predicted = jnp.einsum(
        "bpd,cd->bcp", final_low, copy_pixels[1], preferred_element_type=jnp.float32
    )
    difference = predicted - own_noise
    masked = own_weight[:, None, None] * own_keep[:, None, :] * difference
    loss_local = jnp.sum(masked * difference)
    predict_grad = (2.0 * masked / weight_total).astype(jnp.bfloat16)
    head_grad = jnp.einsum(
        "bcp,bpd->cd", predict_grad, final_low, preferred_element_type=jnp.float32
    )
    final_grad = jnp.einsum(
        "bcp,cd->bpd", predict_grad, copy_pixels[1], preferred_element_type=jnp.float32
    )
    outer_grad, gain_final = norm_back(final_grad, gain_rows[10], final_stats)
    branch_low = outer_grad.astype(jnp.bfloat16)
    narrowout_grad = jnp.einsum(
        "bpd,bpc->dc", branch_low, write_out, preferred_element_type=jnp.float32
    )
    write_upstream = join("bpd,dc->bpc", branch_low, write_out_weight)
    query_grad, key_grad, value_grad = attend_back(
        write_query, write_key, write_value, None, write_total, write_upstream
    )
    write_query_grad = jnp.einsum(
        "bpd,bpc->dc", outer_low, query_grad, preferred_element_type=jnp.float32
    )
    outer_part = jnp.einsum(
        "bpc,dc->bpd", query_grad, write_query_weight, preferred_element_type=jnp.float32
    )

    def row_grad(values):
        if sharers > 1:
            whole = jnp.zeros((images, latents, d_lat), jnp.float32)
            whole = lax.dynamic_update_slice_in_dim(whole, values, first_image, 0)
            values = lax.psum_scatter(
                whole.reshape(images * sharers, own_latents, d_lat),
                "mp",
                scatter_dimension=0,
                tiled=True,
            )
        return values.astype(jnp.bfloat16)

    key_grad, value_grad = row_grad(key_grad), row_grad(value_grad)
    write_key_grad = jnp.einsum(
        "bld,blc->dc", write_low, key_grad, preferred_element_type=jnp.float32
    )
    write_value_grad = jnp.einsum(
        "bld,blc->dc", write_low, value_grad, preferred_element_type=jnp.float32
    )
    write_part = jnp.einsum(
        "blc,dc->bld", key_grad, write_key_weight, preferred_element_type=jnp.float32
    ) + jnp.einsum(
        "blc,dc->bld", value_grad, write_value_weight, preferred_element_type=jnp.float32
    )
    own_grad, gain_write = norm_back(write_part, gain, write_stats)
    outer_back, gain_outer = norm_back(outer_part, gain_rows[9], outer_stats)
    embed_grad = jnp.einsum(
        "bcp,bpd->cd", own_noisy, outer_grad + outer_back, precision=precise
    )
    return (
        own_grad,
        write_key_grad,
        write_value_grad,
        write_query_grad,
        narrowout_grad,
        gain_write,
        gain_outer,
        gain_final,
        embed_grad,
        head_grad,
        loss_local,
    )


def body(
    clean_patches,
    noise_patches,
    timesteps,
    present_mask,
    copy_widein,
    copy_narrowin,
    copy_wideout,
    copy_narrowout,
    copy_latents,
    copy_gains,
    copy_pixels,
    master_widein,
    first_widein,
    second_widein,
    master_narrowin,
    first_narrowin,
    second_narrowin,
    master_wideout,
    first_wideout,
    second_wideout,
    master_narrowout,
    first_narrowout,
    second_narrowout,
    master_latents,
    first_latents,
    second_latents,
    master_gains,
    first_gains,
    second_gains,
    master_pixels,
    first_pixels,
    second_pixels,
):
    images = clean_patches.shape[0]
    patches = clean_patches.shape[2]
    count_mp, count_dp = lax.axis_size("mp"), lax.axis_size("dp")
    mp_index, dp_index = lax.axis_index("mp"), lax.axis_index("dp")
    lead = (mp_index == 0).astype(jnp.float32)
    latents, d_lat = copy_latents.shape
    d_if = copy_gains.shape[1]
    local = copy_widein.shape[2]
    sharers = max(1, count_mp // images)
    own_images = max(1, images // count_mp)
    own_patches, own_latents = patches // sharers, latents // sharers
    first_image = mp_index * own_images // sharers
    share = lax.rem(mp_index, sharers)

    def dp_piece(values, axis):
        size = values.shape[axis] // count_dp
        return lax.dynamic_slice_in_dim(values, dp_index * size, size, axis).astype(jnp.float32)

    key_piece = dp_piece(copy_widein[:, 8], 0)
    value_piece = dp_piece(copy_widein[:, 9], 0)
    query_piece = dp_piece(copy_narrowin[:, 2], 0)
    out_piece = dp_piece(copy_narrowout, 1).T
    gathered = lax.all_gather(
        jnp.concatenate([key_piece, value_piece, query_piece, out_piece], 0), "mp"
    )

    signal = jnp.cos(0.5 * math.pi * (timesteps.astype(jnp.float32) + 0.5) / NSTEPS) ** 2
    noisy = (
        jnp.sqrt(signal)[:, None, None] * clean_patches
        + jnp.sqrt(1.0 - signal)[:, None, None] * noise_patches
    )
    loss_weight = 0.5 + signal
    keep_float = present_mask.astype(jnp.float32)
    weight_here = jnp.sum(loss_weight * PIX * jnp.sum(keep_float, 1))
    gain_rows = copy_gains.astype(jnp.float32)

    def wide_gain(index):
        return gain_rows[2 * index : 2 * index + 2].reshape(-1)

    wide_in = in_hbm(jnp.swapaxes(copy_widein, 0, 1))
    narrow_in = in_hbm(jnp.swapaxes(copy_narrowin, 0, 1))
    wide_out = in_hbm(copy_wideout)
    place = position_table(patches, d_if)
    noisy_rows, pixel_rows, noise_rows = (
        jnp.pad(item, ((0, 0), (0, 16 - PIX), (0, 0)))
        for item in (noisy, copy_pixels, noise_patches)
    )
    read_args = (
        noisy_rows,
        keep_float[:, :, None],
        place,
        pixel_rows[0],
        copy_latents,
        wide_gain(0)[None],
        gain_rows[8:9],
        wide_in,
        narrow_in,
        wide_out,
    )
    read_part, *read_kept = read_forward(*read_args)
    gathered, read_part = lax.optimization_barrier((gathered, read_part))
    gathered = lax.all_gather(gathered, "dp").reshape(count_dp * count_mp, -1, local)
    latent_near, latent_one, (weight_tile,) = line_sum(
        read_part, copy_latents.astype(jnp.float32), 2, tile=jnp.full((8, 128), weight_here)
    )
    self_part, *self_kept = self_forward(
        latent_near, wide_gain(1)[None], wide_in, wide_out, images
    )
    latent_near, latent_two, write_weights = line_sum(
        self_part, latent_one, 3, blocks=(gathered, [d_lat, d_lat, d_if, d_if])
    )
    feed_part, *feed_kept = feed_forward(latent_near, wide_gain(2)[None], wide_in, wide_out)
    latent_three = line_scatter(feed_part, latent_two, 4)
    latent_three = latent_three.reshape(own_images, own_latents, d_lat)

    def own_tokens(values, axis):
        values = lax.dynamic_slice_in_dim(values, first_image, own_images, 0)
        return lax.dynamic_slice_in_dim(values, share * own_patches, own_patches, axis)

    own_weight = lax.dynamic_slice_in_dim(loss_weight, first_image, own_images, 0)
    own_scalar = jnp.broadcast_to(own_weight[0], (8, 128))
    if sharers == 1 and own_images == 1:
        (
            own_grad,
            write_key_grad,
            write_value_grad,
            write_query_grad,
            narrowout_grad,
            gain_write,
            gain_pair,
            own_embed,
            head_grad,
            loss_tile,
        ) = write_stage(
            own_scalar,
            weight_tile,
            latent_three[0],
            own_tokens(noisy_rows, 2)[0],
            own_tokens(noise_rows, 2)[0],
            own_tokens(keep_float, 1),
            place,
            pixel_rows,
            wide_gain(3)[None],
            gain_rows[8:11],
            write_weights,
        )
    else:
        (
            own_grad,
            write_key_grad,
            write_value_grad,
            write_query_grad,
            narrowout_grad,
            gain_write,
            gain_outer,
            gain_final,
            own_embed,
            head_grad,
            loss_local,
        ) = write_apart(
            latent_three,
            own_tokens(noisy, 2),
            own_tokens(noise_patches, 2),
            own_tokens(keep_float, 1),
            own_weight,
            weight_tile[0, 0],
            lax.dynamic_slice_in_dim(place, share * own_patches, own_patches, 0),
            copy_pixels,
            wide_gain(3),
            gain_rows,
            write_weights,
            (images, latents, first_image, sharers),
            timesteps,
        )
        gain_write, gain_pair = gain_write[None], jnp.stack([gain_outer, gain_final])
        own_embed, head_grad = (
            jnp.pad(item, ((0, 16 - PIX), (0, 0))) for item in (own_embed, head_grad)
        )
        loss_tile = jnp.full((8, 128), loss_local)
    latent_near, latent_grad, (key_share, query_share) = line_gather(
        own_grad.reshape(-1, d_lat), 5, [write_key_grad, write_query_grad]
    )
    latent_part, up_first, up_last, down_grad, gain_feed = feed_backward(
        latent_near, latent_two, wide_gain(2)[None], wide_in, wide_out, *feed_kept
    )
    latent_near, latent_grad, five_shares = line_sum(
        latent_part, latent_grad, 6, [write_value_grad, narrowout_grad, up_first]
    )
    latent_part, self_first, self_last, gain_self = self_backward(
        latent_near, latent_one, wide_gain(1)[None], wide_in, wide_out, *self_kept
    )
    latent_near, latent_grad, six_shares = line_sum(
        latent_part, latent_grad, 7, [up_last, down_grad, self_first]
    )
    read_wide, read_narrow, latent_total, gain_read, gain_side, side_embed = read_backward(
        *read_args, *read_kept, latent_near, lead.reshape(1, 1)
    )
    *gradients, stats = closing(
        [self_last, read_wide, read_narrow],
        [
            latent_total,
            gain_read,
            gain_self,
            gain_feed,
            gain_write,
            gain_side,
            gain_pair,
            side_embed,
            own_embed,
            head_grad,
        ],
        [loss_tile, weight_tile],
        [six_shares[2], five_shares[2], six_shares[0], six_shares[1]],
        [key_share, five_shares[0], query_share, five_shares[1]],
        8,
    )
    states = (
        *(jnp.swapaxes(item, 0, 1) for item in (master_widein, first_widein, second_widein)),
        *(jnp.swapaxes(item, 0, 1) for item in (master_narrowin, first_narrowin, second_narrowin)),
        master_wideout,
        first_wideout,
        second_wideout,
        *(item.T for item in (master_narrowout, first_narrowout, second_narrowout)),
        master_latents,
        first_latents,
        second_latents,
        master_gains,
        first_gains,
        second_gains,
        *(jnp.swapaxes(item, 0, 1) for item in (master_pixels, first_pixels, second_pixels)),
    )
    results = update_states(stats, gradients, states)
    results = [
        jnp.swapaxes(item, 0, 1) if index < 6 or 9 <= index < 12 or index >= 18 else item
        for index, item in enumerate(results)
    ]
    return (stats[0, 1], stats[0, 0], *results)


def solution(mesh):
    in_specs = (
        P("dp", None, None),
        P("dp", None, None),
        P("dp"),
        P("dp", None),
        P(None, None, "mp"),
        P(None, None, "mp"),
        P(None, "mp", None),
        P("mp", None),
        P(),
        P(),
        P(),
        P("dp", None, "mp"),
        P("dp", None, "mp"),
        P("dp", None, "mp"),
        P("dp", None, "mp"),
        P("dp", None, "mp"),
        P("dp", None, "mp"),
        P(None, "mp", "dp"),
        P(None, "mp", "dp"),
        P(None, "mp", "dp"),
        P("mp", "dp"),
        P("mp", "dp"),
        P("mp", "dp"),
        P(None, "dp"),
        P(None, "dp"),
        P(None, "dp"),
        P(None, "dp"),
        P(None, "dp"),
        P(None, "dp"),
        P(None, None, "dp"),
        P(None, None, "dp"),
        P(None, None, "dp"),
    )
    out_specs = (
        P(),
        P(),
        P("dp", None, "mp"),
        P("dp", None, "mp"),
        P("dp", None, "mp"),
        P("dp", None, "mp"),
        P("dp", None, "mp"),
        P("dp", None, "mp"),
        P(None, "mp", "dp"),
        P(None, "mp", "dp"),
        P(None, "mp", "dp"),
        P("mp", "dp"),
        P("mp", "dp"),
        P("mp", "dp"),
        P(None, "dp"),
        P(None, "dp"),
        P(None, "dp"),
        P(None, "dp"),
        P(None, "dp"),
        P(None, "dp"),
        P(None, None, "dp"),
        P(None, None, "dp"),
        P(None, None, "dp"),
    )
    return jax.shard_map(body, mesh=mesh, in_specs=in_specs, out_specs=out_specs, check_vma=False)
```

```python
from functools import partial
import math

import jax
import jax.numpy as jnp
import numpy as np
from jax import lax
from jax.experimental import pallas as pl
from jax.experimental.pallas import tpu as pltpu
from jax.sharding import PartitionSpec as P

HEAD_DIM = 64
PIX = 12
NSTEPS = 1000
STEP = 10


precise = lax.Precision.HIGHEST
clip_level = 0.01
learning_rate = 0.05
weight_decay = 0.1
adam_beta = 0.5
adam_eps = 1e-08


def layer_norm(values, gain):
    centered = values - jnp.mean(values, -1, keepdims=True)
    scale = lax.rsqrt(jnp.mean(centered * centered, -1, keepdims=True) + 1e-05)
    normed = centered * scale
    return (normed * gain, (normed, scale))


def norm_back(upstream, gain, stats):
    normed, scale = stats
    inner = upstream * gain
    values = scale * (
        inner
        - jnp.mean(inner, -1, keepdims=True)
        - normed * jnp.mean(inner * normed, -1, keepdims=True)
    )
    gain_grad = jnp.sum((upstream * normed).reshape(-1, normed.shape[-1]), 0)
    return (values, gain_grad)


def position_table(count, width):
    place = np.arange(count, dtype=np.float64)[:, None]
    angle = place * 10000.0 ** (-2.0 * np.arange(width // 2) / width)
    return jnp.asarray(np.concatenate([np.sin(angle), np.cos(angle)], -1), jnp.float32)


def positions(count, width):
    place = jnp.arange(count, dtype=jnp.float32)[:, None]
    index = jnp.arange(width // 2, dtype=jnp.float32)[None, :]
    angle = place * jnp.exp(-math.log(10000.0) * 2.0 * index / width)
    return jnp.concatenate([jnp.sin(angle), jnp.cos(angle)], -1)


def split_heads(values):
    return values.reshape(values.shape[:-1] + (values.shape[-1] // HEAD_DIM, HEAD_DIM))


def attend_scores(queries, keys, keep_mask):
    scores = jnp.einsum(
        "bqhe,bkhe->bhqk",
        split_heads(queries),
        split_heads(keys),
        preferred_element_type=jnp.float32,
    ) * HEAD_DIM ** (-0.5)
    if keep_mask is not None:
        scores = jnp.where(keep_mask[:, None, None, :] > 0, scores, -1e30)
    return scores


def attend_forward(queries, keys, values, keep_mask):
    scores = attend_scores(queries, keys, keep_mask)
    top = jnp.max(scores, -1, keepdims=True)
    log_total = top + jnp.log(jnp.sum(jnp.exp(scores - top), -1, keepdims=True))
    probs = jnp.exp(scores - log_total).astype(jnp.bfloat16)
    output = jnp.einsum(
        "bhqk,bkhe->bqhe", probs, split_heads(values), preferred_element_type=jnp.float32
    )
    return (output.reshape(queries.shape).astype(jnp.bfloat16), log_total)


def attend_back(queries, keys, values, keep_mask, log_total, upstream):
    scores = attend_scores(queries, keys, keep_mask)
    probs = jnp.exp(scores - log_total)
    value_grad = jnp.einsum(
        "bhqk,bqhe->bkhe",
        probs.astype(jnp.bfloat16),
        split_heads(upstream),
        preferred_element_type=jnp.float32,
    )
    prob_grad = jnp.einsum(
        "bqhe,bkhe->bhqk",
        split_heads(upstream),
        split_heads(values),
        preferred_element_type=jnp.float32,
    )
    score_grad = (probs * (prob_grad - jnp.sum(prob_grad * probs, -1, keepdims=True))).astype(
        jnp.bfloat16
    )
    query_grad = jnp.einsum(
        "bhqk,bkhe->bqhe", score_grad, split_heads(keys), preferred_element_type=jnp.float32
    ) * HEAD_DIM ** (-0.5)
    key_grad = jnp.einsum(
        "bhqk,bqhe->bkhe", score_grad, split_heads(queries), preferred_element_type=jnp.float32
    ) * HEAD_DIM ** (-0.5)
    return (
        query_grad.reshape(queries.shape).astype(jnp.bfloat16),
        key_grad.reshape(keys.shape),
        value_grad.reshape(values.shape),
    )


MESH_ID = pl.DeviceIdType.MESH
HBM_SPEC = pl.BlockSpec(memory_space=pltpu.HBM)
VMEM_SPEC = pl.BlockSpec(memory_space=pltpu.VMEM)
CHUNKS = 64
VMEM_LIMIT = 56 << 20


def in_hbm(values):
    return pltpu.with_memory_space_constraint(values, pltpu.HBM)


def in_vmem(values):
    return pltpu.with_memory_space_constraint(values, pltpu.VMEM)


def remote(source, target, send_sem, recv_sem, device):
    return pltpu.make_async_remote_copy(
        src_ref=source,
        dst_ref=target,
        send_sem=send_sem,
        recv_sem=recv_sem,
        device_id=device,
        device_id_type=MESH_ID,
    )


class PieceSums:
    def __init__(self, count, items, outs, scratch):
        self.count, self.items, self.outs = count, items, outs
        self.bits = count.bit_length() - 1
        self.place = lax.axis_index("dp") if items else None
        self.held = []
        for index in range(len(items)):
            self.held.append(scratch[index * (self.bits + 2) : (index + 1) * (self.bits + 2)])

    @staticmethod
    def scratch(count, shapes):
        bits = count.bit_length() - 1
        result = []
        for rows, width in shapes:
            result.append(pltpu.VMEM((count // 2, rows, width), jnp.float32))
            for phase in range(2, bits + 1):
                result.append(
                    pltpu.VMEM((2 * (count >> phase), rows // 2, width), jnp.float32)
                )
            copies = count // 2 + 2 * sum(count >> phase for phase in range(2, bits + 1))
            result += [pltpu.SemaphoreType.DMA((copies,))] * 2
        return result

    def peers(self):
        return [{"dp": self.place ^ (1 << bit)} for bit in range(self.bits)] if self.items else []

    def order(self, half):
        later = list(range(1, self.bits))
        turn = half * (len(later) // 2)
        return later[turn:] + later[:turn]

    def first_copy(self, index, piece):
        item, held = self.items[index], self.held[index]
        other = 1 - (self.place & 1)
        return remote(
            item.at[2 * piece + other],
            held[0].at[piece],
            held[-2].at[piece],
            held[-1].at[piece],
            {"dp": self.place ^ 1},
        )

    def member(self, half, phase, entry, flip):
        bits = self.order(half)
        settled, now, rest = bits[: phase - 2], bits[phase - 2], bits[phase - 1 :]
        piece = 0
        for bit in settled:
            piece = piece | (self.place & (1 << bit))
        own = self.place & (1 << now)
        piece = piece | ((own ^ (1 << now)) if flip else own)
        for position, bit in enumerate(rest):
            if (entry >> position) & 1:
                piece = piece | (1 << bit)
        return piece >> 1

    def later_copy(self, index, half, phase, entry):
        held = self.held[index]
        rows = self.items[index].shape[1] // 2
        size = self.count >> phase
        sem = self.count // 2 + 2 * sum(self.count >> p for p in range(2, phase)) + half * size + entry
        return remote(
            held[0].at[self.member(half, phase, entry, True), pl.ds(half * rows, rows)],
            held[phase - 1].at[half * size + entry],
            held[-2].at[sem],
            held[-1].at[sem],
            {"dp": self.place ^ (1 << self.order(half)[phase - 2])},
        )

    def entries(self, phase):
        return [
            (index, half, entry)
            for index in range(len(self.items))
            for half in range(2)
            for entry in range(self.count >> phase)
        ]

    def begin(self):
        for index in range(len(self.items)):
            for piece in range(self.count // 2):
                self.first_copy(index, piece).start()

    def send(self, phase):
        for index, half, entry in self.entries(phase):
            self.later_copy(index, half, phase, entry).start()

    def advance(self, phase):
        if not self.items:
            return
        if phase == 1:
            own = self.place & 1
            for index, item in enumerate(self.items):
                total = self.held[index][0]
                for piece in range(self.count // 2):
                    self.first_copy(index, piece).wait_recv()
                    add_rows(total.at[piece], total.at[piece], item.at[2 * piece + own])
        else:
            for index, half, entry in self.entries(phase):
                self.later_copy(index, half, phase, entry).wait_recv()
                held, rows = self.held[index], self.items[index].shape[1] // 2
                where = pl.ds(half * rows, rows)
                came = held[phase - 1].at[half * (self.count >> phase) + entry]
                kept = held[0].at[self.member(half, phase, entry, False), where]
                if phase == self.bits:
                    add_rows(self.outs[index].at[where], kept, came)
                else:
                    add_rows(kept, kept, came)
        if phase < self.bits:
            self.send(phase + 1)

    def finish(self):
        for index in range(len(self.items)):
            for piece in range(self.count // 2):
                self.first_copy(index, piece).wait_send()
        for phase in range(2, self.bits + 1):
            for index, half, entry in self.entries(phase):
                self.later_copy(index, half, phase, entry).wait_send()

    def moments(self, total):
        if not self.items:
            return [(0, total, None)]
        marks, low = [], 0
        for phase in range(1, self.bits + 1):
            share = (1 - 0.5 ** (phase - 1)) / (1 - 0.5 ** (self.bits - 1))
            high = total if phase == self.bits else int(total * (0.22 + 0.78 * share))
            marks.append((low, high, phase))
            low = high
        return marks


def add_rows(target, left, right):
    rows, width = target.shape
    step = math.gcd(rows, max(8, 8192 // width))

    def one(index, carry):
        where = pl.ds(pl.multiple_of(index * step, step), step)
        target[where] = left[where] + right[where]
        return carry

    lax.fori_loop(0, rows // step, one, 0)


class Spread:
    def __init__(self, name, count, held, send_sem, recv_sem):
        self.name, self.count, self.held = name, count, held
        self.send_sem, self.recv_sem = send_sem, recv_sem
        self.place = lax.axis_index(name)

    @staticmethod
    def scratch(count, shape):
        sems = pltpu.SemaphoreType.DMA((count,))
        return [pltpu.VMEM((count,) + shape, jnp.float32), sems, sems]

    def peer(self, step):
        return {self.name: lax.rem(self.place + step, self.count)}

    def copy(self, step, slot):
        return remote(
            self.held.at[slot],
            self.held.at[slot],
            self.send_sem.at[step],
            self.recv_sem.at[slot],
            self.peer(step),
        )

    def each(self, action):
        def one(step, carry):
            action(step)
            return carry

        lax.fori_loop(1, self.count, one, 0)

    def start(self):
        self.each(lambda step: self.copy(step, self.place).start())

    def take(self):
        self.each(lambda step: self.copy(step, lax.rem(self.place + step, self.count)).wait_recv())

    def finish(self):
        self.each(lambda step: self.copy(step, self.place).wait_send())

    def total(self):
        return lax.fori_loop(
            1, self.count, lambda slot, carry: carry + self.held[slot], self.held[0]
        )


class Convert:
    def __init__(self, count_mp, steps, blocks, outs, buffer, sems):
        self.count_mp, self.blocks, self.outs = count_mp, blocks, outs
        self.buffer, self.sems = buffer, sems
        self.number = blocks.shape[0]
        self.each, self.stride = max(1, self.number // steps), max(1, steps // self.number)

    @staticmethod
    def scratch(block):
        return [pltpu.VMEM((3,) + block, jnp.float32), pltpu.SemaphoreType.DMA((3,))]

    def copy(self, index):
        slot = lax.rem(index, 3)
        return pltpu.make_async_copy(
            self.blocks.at[index], self.buffer.at[slot], self.sems.at[slot]
        )

    def begin(self):
        self.copy(0).start()
        self.copy(1).start()

    def one(self, index):
        self.copy(index).wait()

        @pl.when(index + 2 < self.number)
        def _():
            self.copy(index + 2).start()

        block = self.buffer.at[lax.rem(index, 3)]
        local = block.shape[1]
        columns = pl.ds(pl.multiple_of(lax.rem(index, self.count_mp) * local, local), local)
        low = 0
        for out in self.outs:
            rows = out.shape[0] * self.count_mp // self.number
            where = pl.ds(pl.multiple_of(index // self.count_mp * rows, rows), rows)
            out[where, columns] = block[pl.ds(low, rows)].astype(jnp.bfloat16)
            low += rows

    def step(self, index):
        @pl.when(lax.rem(index, self.stride) == 0)
        def _():
            for entry in range(self.each):
                self.one(index // self.stride * self.each + entry)


def signal_all(barrier, others):
    for other in others:
        pl.semaphore_signal(barrier, inc=1, device_id=other, device_id_type=MESH_ID)


class Stage:
    def __init__(self, sources, held, in_sems, results, targets, out_sems):
        self.loads = [
            pltpu.make_async_copy(source, target, in_sems.at[index])
            for index, (source, target) in enumerate(zip(sources, held))
        ]
        self.stores = [
            pltpu.make_async_copy(source, target, out_sems.at[index])
            for index, (source, target) in enumerate(zip(results, targets))
        ]
        self.stored, self.waited = [], []

    def start(self):
        for load in self.loads:
            load.start()

    def wait(self, *indices):
        for index in indices or range(len(self.loads)):
            if index not in self.waited:
                self.loads[index].wait()
                self.waited.append(index)

    def store(self, *indices):
        for index in indices:
            self.stores[index].start()
            self.stored.append(index)

    def finish(self):
        self.store(*(index for index in range(len(self.stores)) if index not in self.stored))
        for store in self.stores:
            store.wait()


def staged_kernel(body, counts, *refs):
    refs = list(refs)

    def pull(number):
        taken = refs[:number]
        del refs[:number]
        return taken

    close, number, raw, close_outs, results = counts
    near, sources, raws = pull(close), pull(number), pull(raw)
    near_outs, targets, echoes = pull(close_outs), pull(results), pull(close_outs)
    held, outs, (in_sems, out_sems) = pull(number), pull(results), pull(2)
    stage = Stage(
        sources, held, in_sems, [*near_outs, *outs], [*echoes, *targets], out_sems
    )
    stage.start()
    body(stage, [*near, *held], raws, [*near_outs, *outs], refs)
    stage.finish()


def staged(
    body, inputs, outs, scratch, flops, raw=(), call_id=None, length=0, near=(), near_outs=()
):
    copies = [pltpu.VMEM(item.shape, item.dtype) for item in (*inputs, *outs)]
    stores = [*outs, *near_outs]
    sems = [pltpu.SemaphoreType.DMA((max(1, len(group)),)) for group in (inputs, stores)]
    needed = sum(
        math.prod(item.shape) * jnp.dtype(item.dtype).itemsize
        for item in copies + list(scratch)
        if getattr(item, "dtype", None) in (jnp.float32, jnp.bfloat16)
    )
    params = {} if call_id is None else {"collective_id": call_id, "has_side_effects": True}
    counts = (len(near), len(inputs), len(raw), len(near_outs), len(outs))
    results = pl.pallas_call(
        partial(staged_kernel, body, counts),
        out_shape=[pltpu.VMEM(item.shape, item.dtype) for item in near_outs]
        + [pltpu.HBM(item.shape, item.dtype) for item in stores],
        in_specs=[VMEM_SPEC] * len(near) + [HBM_SPEC] * (len(inputs) + len(raw)),
        out_specs=[VMEM_SPEC] * len(near_outs) + [HBM_SPEC] * len(stores),
        scratch_shapes=copies + sems + list(scratch),
        compiler_params=pltpu.CompilerParams(vmem_limit_bytes=needed + (6 << 20), **params),
        cost_estimate=pl.CostEstimate(
            flops=flops, bytes_accessed=length * 3_500_000, transcendentals=0
        ),
    )(*map(in_vmem, near), *map(in_hbm, (*inputs, *raw)))
    return list(results)


def greet(place, count, others=()):
    barrier = pltpu.get_barrier_semaphore()
    below, above = {"mp": place - 1}, {"mp": place + 1}

    @pl.when(place > 0)
    def _():
        pl.semaphore_signal(barrier, inc=1, device_id=below, device_id_type=MESH_ID)

    @pl.when(place < count - 1)
    def _():
        pl.semaphore_signal(barrier, inc=1, device_id=above, device_id_type=MESH_ID)

    signal_all(barrier, others)
    inside = jnp.logical_and(place > 0, place < count - 1)

    @pl.when(inside)
    def _():
        pl.semaphore_wait(barrier, 2 + len(others))

    @pl.when(jnp.logical_not(inside))
    def _():
        pl.semaphore_wait(barrier, 1 + len(others))


def views(refs, base=3):
    result = []
    for ref in refs:
        if len(ref.shape) == base:
            result.append(ref)
        else:
            result += [ref.at[slot] for slot in range(ref.shape[0])]
    return result


def line_sum_kernel(count, count_dp, extra, tiled, stage, held, raws, results, scratch):
    refs = list(scratch)

    def pull(number):
        taken = refs[:number]
        del refs[:number]
        return taken

    part_ref, base_ref, tile = held[0], held[1], held[2 + extra :]
    items, outs = views(held[2 : 2 + extra]), views(results[1 : 1 + extra], 2)
    out_ref, tile_out = results[0], results[1 + extra : 1 + extra + tiled]
    blocks, base_rows = raws, base_ref.shape[0]
    wide = results[1 + extra + tiled :]
    converted = len(wide)
    inner, from_away, from_toward, toward_send, away_send, away_recv, toward_recv = pull(7)
    chunks = toward_send.shape[0]
    spread = Spread("dp", count_dp, *pull(3)) if tiled else None
    convert = Convert(count, chunks, blocks[0], wide, *pull(2)) if converted else None
    sums = PieceSums(count_dp, items, outs, refs)
    place = lax.axis_index("mp")
    half = count // 2
    low_side = place < half
    toward = {"mp": jnp.where(low_side, place + 1, place - 1)}
    away = {"mp": jnp.where(low_side, place - 1, place + 1)}
    middle = jnp.logical_or(place == half - 1, place == half)
    outermost = jnp.logical_or(place == 0, place == count - 1)
    rows = part_ref.shape[0] // chunks
    others = [spread.peer(step) for step in range(1, count_dp)] if tiled else sums.peers()
    greet(place, count, others)

    def window(step):
        return pl.ds(pl.multiple_of(step * rows, rows), rows)

    def put(step, total):
        first = lax.rem(step * rows, base_rows)
        out_ref[window(step)] = total + base_ref[pl.ds(pl.multiple_of(first, rows), rows)]

    def push(step, source, inside):
        target = from_toward if inside else from_away
        recv = toward_recv if inside else away_recv
        return remote(
            source.at[window(step)],
            target.at[window(step)],
            toward_send.at[step],
            recv.at[step],
            toward,
        )

    def back(step, source):
        return remote(
            source.at[window(step)],
            from_toward.at[window(step)],
            away_send.at[step],
            toward_recv.at[step],
            away,
        )

    def gather_in(step):
        push(step, part_ref, False).wait_recv()
        inner[window(step)] = part_ref[window(step)] + from_away[window(step)]

    @pl.when(outermost)
    def _():
        def leave(step, carry):
            push(step, part_ref, False).start()
            return carry

        lax.fori_loop(0, chunks, leave, 0)

    stage.wait()
    if tiled:
        spread.held[spread.place] = tile[0][...]
        spread.start()
    if converted:
        convert.begin()
    sums.begin()

    @pl.when(outermost)
    def _():

        def arrive(step, carry):
            push(step, part_ref, True).wait_recv()
            put(step, from_toward[window(step)])
            push(step, part_ref, False).wait_send()
            if converted:
                convert.step(step)
            return carry

        for low, high, phase in sums.moments(chunks):
            lax.fori_loop(low, high, arrive, 0)
            sums.advance(phase)

    lag = 2

    @pl.when(middle)
    def _():
        def finish(step):
            push(step, inner, True).wait_recv()
            push(step, inner, True).wait_send()
            total = inner[window(step)] + from_toward[window(step)]
            inner[window(step)] = total
            back(step, inner).start()
            put(step, total)

        def first(step, carry):
            gather_in(step)
            push(step, inner, True).start()
            if converted:
                convert.step(step)
            return carry

        def both(step, carry):
            first(step, carry)
            finish(step - lag)
            return carry

        def last(step, carry):
            finish(step)
            return carry

        def drain(step, carry):
            back(step, inner).wait_send()
            return carry

        lax.fori_loop(0, lag, first, 0)
        for low, high, phase in sums.moments(chunks):
            lax.fori_loop(max(low, lag), high, both, 0)
            if high == chunks:
                lax.fori_loop(chunks - lag, chunks, last, 0)
            sums.advance(phase)
        lax.fori_loop(0, chunks, drain, 0)

    if count > 4:

        @pl.when(jnp.logical_not(jnp.logical_or(middle, outermost)))
        def _():
            def inwards(step, carry):
                gather_in(step)
                push(step, inner, False).start()
                return carry

            def outwards(step, carry):
                push(step, inner, True).wait_recv()
                back(step, from_toward).start()
                put(step, from_toward[window(step)])
                if converted:
                    convert.step(step)
                return carry

            def drain(step, carry):
                push(step, inner, False).wait_send()
                back(step, from_toward).wait_send()
                return carry

            lax.fori_loop(0, chunks, inwards, 0)
            for low, high, phase in sums.moments(chunks):
                lax.fori_loop(low, high, outwards, 0)
                sums.advance(phase)
            lax.fori_loop(0, chunks, drain, 0)

    sums.finish()
    if tiled:
        spread.take()
        tile_out[0][...] = spread.total()
        spread.finish()


def piece_shapes(items):
    count = lax.axis_size("dp")
    items = [item.reshape(item.shape[:-2] + (count, -1, item.shape[-1])) for item in items]
    shapes, shares = [], []
    for item in items:
        shapes += [item.shape[-2:]] * (item.shape[0] if item.ndim == 4 else 1)
        shares.append(jax.ShapeDtypeStruct(item.shape[:-3] + item.shape[-2:], jnp.float32))
    return items, shapes, shares


def line_sum(part, base, call_id, items=(), tile=None, blocks=None):
    items, shapes, shares = piece_shapes(items)
    count, count_dp = lax.axis_size("mp"), lax.axis_size("dp")
    rows, width = part.shape
    buffer = pltpu.VMEM((rows, width), jnp.float32)
    sems = pltpu.SemaphoreType.DMA((CHUNKS,))
    inputs, raw = [base, *items], []
    outs = list(shares)
    scratch = [buffer] * 3 + [sems] * 4
    if tile is not None:
        inputs.append(tile)
        outs.append(jax.ShapeDtypeStruct(tile.shape, jnp.float32))
        scratch += Spread.scratch(count_dp, tile.shape)
    if blocks is not None:
        blocks, sizes = blocks
        raw.append(blocks)
        outs += [
            jax.ShapeDtypeStruct((size, count * blocks.shape[2]), jnp.bfloat16) for size in sizes
        ]
        scratch += Convert.scratch(blocks.shape[1:])
    scratch += PieceSums.scratch(count_dp, shapes)
    total = jax.ShapeDtypeStruct((rows, width), jnp.float32)
    results = staged(
        partial(line_sum_kernel, count, count_dp, len(items), int(tile is not None)),
        inputs,
        outs,
        scratch,
        4 * rows * width,
        raw,
        call_id,
        55,
        [part],
        [total],
    )
    return results[0], results[-1], results[1:-1]


class LineScatter:
    def __init__(self, count, part, out, buffers, sems):
        self.count, self.part, self.out = count, part, out
        self.up_acc, self.down_acc, self.from_below, self.from_above = buffers
        self.up_send, self.down_send, self.up_recv, self.down_recv = sems
        self.place = lax.axis_index("mp")
        self.steps = self.up_send.shape[1]
        self.block = part.shape[0] // count
        self.rows = self.block // self.steps

    @staticmethod
    def scratch(count, shape, steps):
        sems = pltpu.SemaphoreType.DMA((count, steps))
        return [pltpu.VMEM(shape, jnp.float32)] * 4 + [sems] * 4

    def window(self, owner, step):
        return pl.ds(pl.multiple_of(owner * self.block + step * self.rows, self.rows), self.rows)

    def up(self, owner, step, source):
        where = self.window(owner, step)
        return remote(
            source.at[where],
            self.from_below.at[where],
            self.up_send.at[owner, step],
            self.up_recv.at[owner, step],
            {"mp": self.place + 1},
        )

    def down(self, owner, step, source):
        where = self.window(owner, step)
        return remote(
            source.at[where],
            self.from_above.at[where],
            self.down_send.at[owner, step],
            self.down_recv.at[owner, step],
            {"mp": self.place - 1},
        )

    def up_turn(self, index):
        place, part = self.place, self.part
        owner, step = self.count - 1 - index // self.steps, lax.rem(index, self.steps)

        @pl.when(jnp.logical_and(owner > place, place == 0))
        def _():
            self.up(owner, step, part).start()

        @pl.when(jnp.logical_and(owner > place, place > 0))
        def _():
            self.up(owner, step, part).wait_recv()
            where = self.window(owner, step)
            self.up_acc[where] = part[where] + self.from_below[where]
            self.up(owner, step, self.up_acc).start()

    def down_turn(self, index):
        place, part, count = self.place, self.part, self.count
        owner, step = index // self.steps, lax.rem(index, self.steps)

        @pl.when(jnp.logical_and(owner < place, place == count - 1))
        def _():
            self.down(owner, step, part).start()

        @pl.when(jnp.logical_and(owner < place, place < count - 1))
        def _():
            self.down(owner, step, part).wait_recv()
            where = self.window(owner, step)
            self.down_acc[where] = part[where] + self.from_above[where]
            self.down(owner, step, self.down_acc).start()

    def run(self, pause=None):
        turns, lag = self.count * self.steps, self.steps

        def staggered(first, second):
            def begin(index, carry):
                first(index)
                return carry

            def both(index, carry):
                first(index)
                second(index - lag)
                return carry

            def end(index, carry):
                second(index)
                return carry

            lax.fori_loop(0, lag, begin, 0)
            if pause is not None:
                pause()
            lax.fori_loop(lag, turns, both, 0)
            lax.fori_loop(turns - lag, turns, end, 0)

        @pl.when(self.place < self.count // 2)
        def _():
            staggered(self.up_turn, self.down_turn)

        @pl.when(self.place >= self.count // 2)
        def _():
            staggered(self.down_turn, self.up_turn)

    def settle(self):
        place, rows = self.place, self.rows

        def one(step, carry):
            where = self.window(place, step)
            mine = pl.ds(pl.multiple_of(step * rows, rows), rows)
            self.out[mine] = self.part[where]

            @pl.when(place > 0)
            def _():
                self.up(place, step, self.part).wait_recv()
                self.out[mine] += self.from_below[where]

            @pl.when(place < self.count - 1)
            def _():
                self.down(place, step, self.part).wait_recv()
                self.out[mine] += self.from_above[where]

            return carry

        lax.fori_loop(0, self.steps, one, 0)

    def finish(self):
        place = self.place

        def one(index, carry):
            owner, step = index // self.steps, lax.rem(index, self.steps)

            @pl.when(owner > place)
            def _():
                self.up(owner, step, self.part).wait_send()

            @pl.when(owner < place)
            def _():
                self.down(owner, step, self.part).wait_send()

            return carry

        lax.fori_loop(0, self.count * self.steps, one, 0)


def line_scatter_kernel(count, stage, held, raws, results, scratch):
    own, sem = scratch[8:]
    scatter = LineScatter(count, held[0], results[0], scratch[:4], scratch[4:8])
    rows = own.shape[0]
    load = pltpu.make_async_copy(
        raws[0].at[pl.ds(pl.multiple_of(scatter.place * rows, rows), rows)], own, sem
    )
    load.start()
    greet(scatter.place, count)
    scatter.run()
    scatter.settle()
    load.wait()
    results[0][...] += own[...]
    scatter.finish()


def line_scatter(part, base, call_id):
    rows, width = part.shape
    count = lax.axis_size("mp")
    own = (rows // count, width)
    (result,) = staged(
        partial(line_scatter_kernel, count),
        [],
        [jax.ShapeDtypeStruct(own, jnp.float32)],
        LineScatter.scratch(count, (rows, width), 8)
        + [pltpu.VMEM(own, jnp.float32), pltpu.SemaphoreType.DMA],
        2 * rows * width,
        [base],
        call_id=call_id,
        length=33,
        near=[part],
    )
    return result


def line_gather_kernel(count, count_dp, extra, stage, held, raws, results, scratch):
    own_ref, out_ref = held[0], results[0]
    items, outs = views(held[1:]), views(results[1:], 2)
    up_send, down_send, up_recv, down_recv = scratch[:4]
    sums = PieceSums(count_dp, items, outs, scratch[4:])
    place = lax.axis_index("mp")
    steps = up_send.shape[1]
    block = own_ref.shape[0]
    rows = block // steps
    below, above = {"mp": place - 1}, {"mp": place + 1}
    greet(place, count, sums.peers())
    stage.wait(0)

    def window(owner, step):
        return pl.ds(pl.multiple_of(owner * block + step * rows, rows), rows)

    def up(owner, step):
        part = out_ref.at[window(owner, step)]
        return remote(part, part, up_send.at[owner, step], up_recv.at[owner, step], above)

    def down(owner, step):
        part = out_ref.at[window(owner, step)]
        return remote(part, part, down_send.at[owner, step], down_recv.at[owner, step], below)

    def begin(step, carry):
        out_ref[window(place, step)] = own_ref[pl.ds(pl.multiple_of(step * rows, rows), rows)]

        @pl.when(place < count - 1)
        def _():
            up(place, step).start()

        @pl.when(place > 0)
        def _():
            down(place, step).start()

        return carry

    lax.fori_loop(0, steps, begin, 0)
    stage.wait(*range(1, len(stage.loads)))
    sums.begin()

    def pass_on(index, carry):
        away, step = 1 + index // steps, lax.rem(index, steps)

        @pl.when(place - away >= 0)
        def _():
            up(place - away, step).wait_recv()

        @pl.when(jnp.logical_and(place - away >= 0, place < count - 1))
        def _():
            up(place - away, step).start()

        @pl.when(place + away < count)
        def _():
            down(place + away, step).wait_recv()

        @pl.when(jnp.logical_and(place + away < count, place > 0))
        def _():
            down(place + away, step).start()

        return carry

    for low, high, phase in sums.moments((count - 1) * steps):
        lax.fori_loop(low, high, pass_on, 0)
        sums.advance(phase)

    def drain(index, carry):
        owner, step = index // steps, lax.rem(index, steps)

        @pl.when(jnp.logical_and(owner <= place, place < count - 1))
        def _():
            up(owner, step).wait_send()

        @pl.when(jnp.logical_and(owner >= place, place > 0))
        def _():
            down(owner, step).wait_send()

        return carry

    lax.fori_loop(0, count * steps, drain, 0)
    sums.finish()


def line_gather(own, call_id, items=()):
    rows, width = own.shape
    count, count_dp = lax.axis_size("mp"), lax.axis_size("dp")
    sems = pltpu.SemaphoreType.DMA((count, 8))
    items, shapes, shares = piece_shapes(items)
    results = staged(
        partial(line_gather_kernel, count, count_dp, len(items)),
        [own, *items],
        shares,
        [sems] * 4 + PieceSums.scratch(count_dp, shapes),
        rows * width,
        call_id=call_id,
        length=38,
        near_outs=[jax.ShapeDtypeStruct((rows * count, width), jnp.float32)],
    )
    return results[0], results[-1], results[1:-1]


def dot(left, right, left_dim=1, right_dim=0):
    return lax.dot_general(
        left, right, (((left_dim,), (right_dim,)), ((), ())), preferred_element_type=jnp.float32
    )


def head_mask(width, copies):
    lane = lax.broadcasted_iota(jnp.int32, (1, width), 1)
    return [lane // HEAD_DIM == head for head in range(copies)]


def spread_heads(values):
    masks = head_mask(values.shape[1], values.shape[1] // HEAD_DIM)
    return jnp.concatenate([jnp.where(mask, values, jnp.zeros_like(values)) for mask in masks], 0)


def join_heads(values, heads):
    rows = values.shape[0] // heads
    masks = head_mask(values.shape[1], heads)
    return sum(
        jnp.where(mask, values[head * rows : (head + 1) * rows], 0.0)
        for head, mask in enumerate(masks)
    )


def split_three(values):
    first = values.astype(jnp.bfloat16)
    left = values - first.astype(jnp.float32)
    second = left.astype(jnp.bfloat16)
    third = (left - second.astype(jnp.float32)).astype(jnp.bfloat16)
    return first, second, third


def norm_rows(values):
    centered = values - jnp.mean(values, -1, keepdims=True)
    scale = lax.rsqrt(jnp.mean(centered * centered, -1, keepdims=True) + 1e-05)
    return centered * scale, scale


def norm_rows_back(upstream, gain, normed, scale):
    inner = upstream * gain
    return scale * (
        inner
        - jnp.mean(inner, -1, keepdims=True)
        - normed * jnp.mean(inner * normed, -1, keepdims=True)
    )


def embed(noisy, pixels, place):
    stacked = jnp.concatenate(split_three(noisy), 0)
    return dot(stacked, jnp.concatenate([pixels] * 3, 0), 0, 0) + place


def read_forward_kernel(
    noisy_ref,
    keep_ref,
    place_ref,
    pixels_ref,
    latents_ref,
    wide_gain_ref,
    gain_ref,
    query_weight_ref,
    pair_weight_ref,
    out_weight_ref,
    part_ref,
    pairs_ref,
    output_ref,
    queries_ref,
    normed_ref,
    scale_ref,
    side_ref,
    probs_ref,
):
    heads = query_weight_ref.shape[2] // HEAD_DIM

    @pl.when(pl.program_id(0) == 0)
    def _():
        normed, _ = norm_rows(latents_ref[...].astype(jnp.float32))
        low = (normed * wide_gain_ref[...]).astype(jnp.bfloat16)
        queries = dot(low, query_weight_ref[0]).astype(jnp.bfloat16)
        queries_ref[...] = spread_heads(queries * jnp.bfloat16(HEAD_DIM ** (-0.5)))

    normed, scale = norm_rows(embed(noisy_ref[0], pixels_ref[...], place_ref[...]))
    normed_ref[0] = normed
    scale_ref[0] = scale
    side = (normed * gain_ref[...]).astype(jnp.bfloat16)
    side_ref[0] = side.T
    keys = dot(side, pair_weight_ref[0]).astype(jnp.bfloat16)
    values = dot(side, pair_weight_ref[1]).astype(jnp.bfloat16)
    pairs_ref[0, 0] = keys
    pairs_ref[0, 1] = values
    scores = dot(keys, queries_ref[...], 1, 1)
    scores = jnp.where(keep_ref[0] > 0, scores, -1e30)
    top = jnp.max(scores, 0, keepdims=True)
    grown = jnp.exp(scores - top)
    probs = grown / jnp.sum(grown, 0, keepdims=True)
    probs_ref[0] = probs
    output = join_heads(dot(probs.astype(jnp.bfloat16), values, 0, 0), heads)
    output = output.astype(jnp.bfloat16)
    output_ref[0] = output
    part_ref[...] = dot(output, out_weight_ref[0])


def whole(shape):
    return pl.BlockSpec(shape, lambda b: (0,) * len(shape))


def each(shape):
    return pl.BlockSpec((1,) + shape, lambda b: (b,) + (0,) * len(shape))


def slot_of(shape, slot):
    return pl.BlockSpec(shape, lambda b: (slot,) + (0,) * (len(shape) - 1))


def read_forward(noisy, keep, place, pixels, latents, wide_gain, gain, wide, narrow, wideout):
    images, _, patches = noisy.shape
    count, d_lat = latents.shape
    d_if, local = narrow.shape[1:]
    stacked = local // HEAD_DIM * count
    return pl.pallas_call(
        read_forward_kernel,
        grid=(images,),
        out_shape=[
            pltpu.VMEM((images * count, d_lat), jnp.float32),
            pltpu.HBM((images, 2, patches, local), jnp.bfloat16),
            pltpu.HBM((images, count, local), jnp.bfloat16),
            pltpu.HBM((stacked, local), jnp.bfloat16),
            pltpu.HBM((images, patches, d_if), jnp.float32),
            pltpu.HBM((images, patches, 1), jnp.float32),
            pltpu.HBM((images, d_if, patches), jnp.bfloat16),
            pltpu.HBM((images, patches, stacked), jnp.float32),
        ],
        in_specs=[
            each(noisy.shape[1:]),
            each((patches, 1)),
            whole((patches, d_if)),
            whole(pixels.shape),
            whole(latents.shape),
            whole((1, d_lat)),
            whole((1, d_if)),
            slot_of((1, d_lat, local), 0),
            slot_of((2, d_if, local), 0),
            slot_of((1, local, d_lat), 0),
        ],
        out_specs=[
            pl.BlockSpec((count, d_lat), lambda b: (b, 0)),
            each((2, patches, local)),
            each((count, local)),
            whole((stacked, local)),
            each((patches, d_if)),
            each((patches, 1)),
            each((d_if, patches)),
            each((patches, stacked)),
        ],
        compiler_params=pltpu.CompilerParams(vmem_limit_bytes=52 << 20),
        cost_estimate=pl.CostEstimate(
            flops=10**10, bytes_accessed=30 * 10**6, transcendentals=2 * 10**6
        ),
    )(in_hbm(noisy), in_hbm(keep), in_hbm(place), in_hbm(pixels), in_hbm(latents), in_hbm(wide_gain), in_hbm(gain), in_hbm(wide), in_hbm(narrow), in_hbm(wideout))


def read_backward_kernel(
    noisy_ref,
    latents_ref,
    wide_gain_ref,
    gain_ref,
    query_weight_ref,
    pair_weight_ref,
    out_weight_ref,
    pairs_ref,
    output_ref,
    queries_ref,
    normed_ref,
    scale_ref,
    side_ref,
    probs_ref,
    grad_ref,
    lead_ref,
    wide_grad_ref,
    narrow_grad_ref,
    latents_grad_ref,
    wide_gain_grad_ref,
    gain_grad_ref,
    embed_grad_ref,
    low_ref,
    returned_ref,
):
    step, steps = pl.program_id(0), pl.num_programs(0)
    heads = query_weight_ref.shape[2] // HEAD_DIM

    @pl.when(step == 0)
    def _():
        normed, _ = norm_rows(latents_ref[...].astype(jnp.float32))
        low_ref[...] = (normed * wide_gain_ref[...]).astype(jnp.bfloat16)
        for ref in (
            wide_grad_ref,
            narrow_grad_ref,
            latents_grad_ref,
            gain_grad_ref,
            embed_grad_ref,
            returned_ref,
        ):
            ref[...] = jnp.zeros_like(ref)

    normed, scale, side, probs = normed_ref[0], scale_ref[0], side_ref[0], probs_ref[0]
    keys, values, queries = pairs_ref[0, 0], pairs_ref[0, 1], queries_ref[...]
    branch = grad_ref[...].astype(jnp.bfloat16)
    latents_grad_ref[...] += lead_ref[...] * grad_ref[...]
    wide_grad_ref[1] += dot(branch, output_ref[0], 0, 0)
    upstream = spread_heads(dot(branch, out_weight_ref[0], 1, 1).astype(jnp.bfloat16))
    value_grad = dot(probs.astype(jnp.bfloat16), upstream).astype(jnp.bfloat16)
    prob_grad = dot(values, upstream, 1, 1)
    inner = jnp.sum(prob_grad * probs, 0, keepdims=True)
    score_grad = (probs * (prob_grad - inner)).astype(jnp.bfloat16)
    key_grad = dot(score_grad, queries).astype(jnp.bfloat16)
    query_grad = join_heads(dot(score_grad, keys, 0, 0), heads) * HEAD_DIM ** (-0.5)
    query_grad = query_grad.astype(jnp.bfloat16)
    wide_grad_ref[0] += dot(low_ref[...], query_grad, 0, 0)
    returned_ref[...] += dot(query_grad, query_weight_ref[0], 1, 1)
    narrow_grad_ref[0] += dot(side, key_grad)
    narrow_grad_ref[1] += dot(side, value_grad)
    side_grad = dot(key_grad, pair_weight_ref[0], 1, 1) + dot(value_grad, pair_weight_ref[1], 1, 1)
    gain_grad_ref[...] += jnp.sum(side_grad * normed, 0, keepdims=True)
    back = norm_rows_back(side_grad, gain_ref[...], normed, scale)
    embed_grad_ref[...] += embed_back(noisy_ref[0], back)

    @pl.when(step == steps - 1)
    def _():
        normed, scale = norm_rows(latents_ref[...].astype(jnp.float32))
        returned = returned_ref[...]
        wide_gain_grad_ref[...] = jnp.sum(returned * normed, 0, keepdims=True)
        latents_grad_ref[...] += norm_rows_back(returned, wide_gain_ref[...], normed, scale)


def embed_back(noisy, back):
    first, second, _ = split_three(noisy)
    high = back.astype(jnp.bfloat16)
    low = (back - high.astype(jnp.float32)).astype(jnp.bfloat16)
    rows = noisy.shape[0]
    both = dot(jnp.concatenate([first, second], 0), high)
    return both[:rows] + both[rows:] + dot(first, low)


def read_backward(
    noisy,
    latents,
    wide_gain,
    gain,
    wide,
    narrow,
    wideout,
    pairs,
    output,
    queries,
    normed,
    scale,
    side,
    probs,
    grad,
    lead,
):
    images, rows, patches = noisy.shape
    count, d_lat = latents.shape
    d_if, local = narrow.shape[1:]
    stacked = local // HEAD_DIM * count
    results = [
        (2, d_lat, local),
        (2, d_if, local),
        (count, d_lat),
        (1, d_lat),
        (1, d_if),
        (rows, d_if),
    ]
    return pl.pallas_call(
        read_backward_kernel,
        grid=(images,),
        out_shape=[pltpu.HBM(shape, jnp.float32) for shape in results],
        in_specs=[
            each(noisy.shape[1:]),
            whole(latents.shape),
            whole((1, d_lat)),
            whole((1, d_if)),
            slot_of((1, d_lat, local), 0),
            slot_of((2, d_if, local), 0),
            slot_of((1, local, d_lat), 0),
            each((2, patches, local)),
            each((count, local)),
            whole((stacked, local)),
            each((patches, d_if)),
            each((patches, 1)),
            each((d_if, patches)),
            each((patches, stacked)),
            pl.BlockSpec((count, d_lat), lambda b: (b, 0)),
            whole((1, 1)),
        ],
        out_specs=[whole(shape) for shape in results],
        scratch_shapes=[
            pltpu.VMEM((count, d_lat), jnp.bfloat16),
            pltpu.VMEM((count, d_lat), jnp.float32),
        ],
        compiler_params=pltpu.CompilerParams(vmem_limit_bytes=52 << 20),
        cost_estimate=pl.CostEstimate(
            flops=2 * 10**10, bytes_accessed=30 * 10**6, transcendentals=2 * 10**6
        ),
    )(*map(in_hbm, (noisy, latents, wide_gain, gain, wide, narrow, wideout, pairs, output, queries, normed, scale, side, probs)), in_vmem(grad), in_hbm(lead))


def rows_of(rows, width):
    return pl.BlockSpec((rows, width), lambda b: (b, 0))


def attend_few(keys, values, queries):
    scores = dot(keys, queries, 1, 1)
    top = jnp.max(scores, 0, keepdims=True)
    grown = jnp.exp(scores - top)
    summed = jnp.sum(grown, 0, keepdims=True)
    probs = (grown / summed).astype(jnp.bfloat16)
    return dot(probs, values, 0, 0), top + jnp.log(summed)


def scaled_heads(queries):
    return spread_heads(queries * jnp.bfloat16(HEAD_DIM ** (-0.5)))


def self_forward_kernel(
    latent_ref, gain_ref, q_ref, k_ref, v_ref, out_weight_ref, part_ref, triple_ref, output_ref, total_ref, low_ref
):
    heads = q_ref.shape[2] // HEAD_DIM
    normed, _ = norm_rows(latent_ref[...])
    low = (normed * gain_ref[...]).astype(jnp.bfloat16)
    low_ref[...] = low
    queries, keys, values = (dot(low, ref[0]).astype(jnp.bfloat16) for ref in (q_ref, k_ref, v_ref))
    for index, item in enumerate((queries, keys, values)):
        triple_ref[0, index] = item
    output, total_ref[0] = attend_few(keys, values, scaled_heads(queries))
    output = join_heads(output, heads).astype(jnp.bfloat16)
    output_ref[0] = output
    part_ref[...] = dot(output, out_weight_ref[0])


def self_forward(latent, gain, wide, wideout, images):
    total, d_lat = latent.shape
    count, local = total // images, wide.shape[2]
    stacked = local // HEAD_DIM * count
    return pl.pallas_call(
        self_forward_kernel,
        grid=(images,),
        out_shape=[
            pltpu.VMEM((total, d_lat), jnp.float32),
            pltpu.HBM((images, 3, count, local), jnp.bfloat16),
            pltpu.HBM((images, count, local), jnp.bfloat16),
            pltpu.HBM((images, 1, stacked), jnp.float32),
            pltpu.HBM((total, d_lat), jnp.bfloat16),
        ],
        in_specs=[rows_of(count, d_lat), whole((1, d_lat))]
        + [slot_of((1, d_lat, local), slot) for slot in (1, 2, 3)]
        + [slot_of((1, local, d_lat), 1)],
        out_specs=[
            rows_of(count, d_lat),
            each((3, count, local)),
            each((count, local)),
            each((1, stacked)),
            rows_of(count, d_lat),
        ],
        compiler_params=pltpu.CompilerParams(vmem_limit_bytes=20 << 20),
        cost_estimate=pl.CostEstimate(
            flops=3 * 10**9, bytes_accessed=12 * 10**6, transcendentals=3 * 10**5
        ),
    )(in_vmem(latent), in_hbm(gain), in_hbm(wide), in_hbm(wide), in_hbm(wide), in_hbm(wideout))


def self_backward_kernel(
    grad_ref,
    latent_ref,
    gain_ref,
    q_ref,
    k_ref,
    v_ref,
    out_weight_ref,
    triple_ref,
    output_ref,
    total_ref,
    low_ref,
    part_ref,
    first_ref,
    last_ref,
    gain_grad_ref,
    branches,
    outputs,
    grads,
    lows,
):
    step, steps = pl.program_id(0), pl.num_programs(0)
    heads = q_ref.shape[2] // HEAD_DIM
    count = grad_ref.shape[0]
    mine = pl.ds(pl.multiple_of(step * count, count), count)
    normed, scale = norm_rows(latent_ref[...])
    branch = grad_ref[...].astype(jnp.bfloat16)
    branches[mine] = branch
    outputs[mine] = output_ref[0]
    lows[mine] = low_ref[...]
    upstream = spread_heads(dot(branch, out_weight_ref[0], 1, 1).astype(jnp.bfloat16))
    keys, values = triple_ref[0, 1], triple_ref[0, 2]
    queries = scaled_heads(triple_ref[0, 0])
    probs = jnp.exp(dot(keys, queries, 1, 1) - total_ref[0])
    value_grad = dot(probs.astype(jnp.bfloat16), upstream).astype(jnp.bfloat16)
    prob_grad = dot(values, upstream, 1, 1)
    inner = jnp.sum(prob_grad * probs, 0, keepdims=True)
    score_grad = (probs * (prob_grad - inner)).astype(jnp.bfloat16)
    key_grad = dot(score_grad, queries).astype(jnp.bfloat16)
    query_grad = join_heads(dot(score_grad, keys, 0, 0), heads) * HEAD_DIM ** (-0.5)
    query_grad = query_grad.astype(jnp.bfloat16)
    part = (
        dot(query_grad, q_ref[0], 1, 1)
        + dot(key_grad, k_ref[0], 1, 1)
        + dot(value_grad, v_ref[0], 1, 1)
    )
    for index, item in enumerate((query_grad, key_grad, value_grad)):
        grads[index, mine] = item
    gain_part = jnp.sum(part * normed, 0, keepdims=True)
    gain_grad_ref[...] = gain_part + jnp.where(step == 0, 0.0, gain_grad_ref[...])
    part_ref[...] = norm_rows_back(part, gain_ref[...], normed, scale)

    @pl.when(step == steps - 1)
    def _():
        turned = lows[...].T
        first_ref[0] = dot(turned, grads[0])
        first_ref[1] = dot(turned, grads[1])
        last_ref[0] = dot(turned, grads[2])
        last_ref[1] = dot(branches[...], outputs[...], 0, 0)


def self_backward(grad, latent, gain, wide, wideout, triple, output, total, low):
    rows, d_lat = latent.shape
    images, _, count, local = triple.shape
    stacked = local // HEAD_DIM * count
    weight = pltpu.HBM((2, d_lat, local), jnp.float32)
    return pl.pallas_call(
        self_backward_kernel,
        grid=(images,),
        out_shape=[pltpu.VMEM((rows, d_lat), jnp.float32)]
        + [weight] * 2
        + [pltpu.HBM((1, d_lat), jnp.float32)],
        in_specs=[rows_of(count, d_lat), rows_of(count, d_lat), whole((1, d_lat))]
        + [slot_of((1, d_lat, local), slot) for slot in (1, 2, 3)]
        + [
            slot_of((1, local, d_lat), 1),
            each((3, count, local)),
            each((count, local)),
            each((1, stacked)),
            rows_of(count, d_lat),
        ],
        out_specs=[rows_of(count, d_lat)] + [whole((2, d_lat, local))] * 2 + [whole((1, d_lat))],
        scratch_shapes=[
            pltpu.VMEM((rows, d_lat), jnp.bfloat16),
            pltpu.VMEM((rows, local), jnp.bfloat16),
            pltpu.VMEM((3, rows, local), jnp.bfloat16),
            pltpu.VMEM((rows, d_lat), jnp.bfloat16),
        ],
        compiler_params=pltpu.CompilerParams(vmem_limit_bytes=28 << 20),
        cost_estimate=pl.CostEstimate(
            flops=6 * 10**9, bytes_accessed=16 * 10**6, transcendentals=3 * 10**5
        ),
    )(in_vmem(grad), in_hbm(latent), in_hbm(gain), in_hbm(wide), in_hbm(wide), in_hbm(wide), in_hbm(wideout), in_hbm(triple), in_hbm(output), in_hbm(total), in_hbm(low))


def feed_forward_kernel(
    latent_ref, gain_ref, up_ref, down_ref, part_ref, active_ref, slope_ref, low_ref
):
    @pl.when(pl.program_id(0) == 0)
    def _():
        normed, _ = norm_rows(latent_ref[...])
        low_ref[...] = (normed * gain_ref[...]).astype(jnp.bfloat16)

    hidden = dot(low_ref[...], up_ref[0])
    share = 0.5 * (1.0 + lax.erf(hidden * math.sqrt(0.5)))
    density = jnp.exp(-0.5 * hidden * hidden) * (1.0 / math.sqrt(2.0 * math.pi))
    active = (hidden * share).astype(jnp.bfloat16)
    active_ref[0] = active
    slope_ref[0] = share + hidden * density
    part = dot(active, down_ref[0])

    @pl.when(pl.program_id(0) == 0)
    def _():
        part_ref[...] = part

    @pl.when(pl.program_id(0) > 0)
    def _():
        part_ref[...] += part


def feed_forward(latent, gain, wide, wideout):
    rows, d_lat = latent.shape
    local = wide.shape[2]
    return pl.pallas_call(
        feed_forward_kernel,
        grid=(4,),
        out_shape=[
            pltpu.VMEM((rows, d_lat), jnp.float32),
            pltpu.HBM((4, rows, local), jnp.bfloat16),
            pltpu.HBM((4, rows, local), jnp.float32),
            pltpu.HBM((rows, d_lat), jnp.bfloat16),
        ],
        in_specs=[
            whole((rows, d_lat)),
            whole((1, d_lat)),
            pl.BlockSpec((1, d_lat, local), lambda s: (4 + s, 0, 0)),
            pl.BlockSpec((1, local, d_lat), lambda s: (2 + s, 0, 0)),
        ],
        out_specs=[
            whole((rows, d_lat)),
            each((rows, local)),
            each((rows, local)),
            whole((rows, d_lat)),
        ],
        compiler_params=pltpu.CompilerParams(vmem_limit_bytes=24 << 20),
        cost_estimate=pl.CostEstimate(
            flops=4 * 10**9, bytes_accessed=14 * 10**6, transcendentals=10**6
        ),
    )(in_vmem(latent), in_hbm(gain), in_hbm(wide), in_hbm(wideout))


def feed_backward_kernel(
    grad_ref,
    latent_ref,
    gain_ref,
    up_ref,
    down_ref,
    active_ref,
    slope_ref,
    low_ref,
    part_ref,
    up_first_ref,
    up_last_ref,
    down_grad_ref,
    gain_grad_ref,
    branch,
    branch_turned,
    low_turned,
    total,
):
    step, steps = pl.program_id(0), pl.num_programs(0)

    @pl.when(step == 0)
    def _():
        low = grad_ref[...].astype(jnp.bfloat16)
        branch[...] = low
        branch_turned[...] = low.T
        low_turned[...] = low_ref[...].T
        total[...] = jnp.zeros_like(total)

    active_grad = dot(branch[...], down_ref[0], 1, 1)
    hidden_grad = (active_grad * slope_ref[0]).astype(jnp.bfloat16)
    down_grad_ref[0] = dot(branch_turned[...], active_ref[0])
    total[...] += dot(hidden_grad, up_ref[0], 1, 1)
    up_grad = dot(low_turned[...], hidden_grad)

    @pl.when(step < 2)
    def _():
        up_first_ref[0] = up_grad

    @pl.when(step >= 2)
    def _():
        up_last_ref[0] = up_grad

    @pl.when(step == steps - 1)
    def _():
        normed, scale = norm_rows(latent_ref[...])
        part = total[...]
        gain_grad_ref[...] = jnp.sum(part * normed, 0, keepdims=True)
        part_ref[...] = norm_rows_back(part, gain_ref[...], normed, scale)


def feed_backward(grad, latent, gain, wide, wideout, active, slope, low):
    rows, d_lat = latent.shape
    local = wide.shape[2]
    return pl.pallas_call(
        feed_backward_kernel,
        grid=(4,),
        out_shape=[
            pltpu.VMEM((rows, d_lat), jnp.float32),
            pltpu.HBM((2, d_lat, local), jnp.float32),
            pltpu.HBM((2, d_lat, local), jnp.float32),
            pltpu.HBM((4, d_lat, local), jnp.float32),
            pltpu.HBM((1, d_lat), jnp.float32),
        ],
        in_specs=[
            whole((rows, d_lat)),
            whole((rows, d_lat)),
            whole((1, d_lat)),
            pl.BlockSpec((1, d_lat, local), lambda s: (4 + s, 0, 0)),
            pl.BlockSpec((1, local, d_lat), lambda s: (2 + s, 0, 0)),
            each((rows, local)),
            each((rows, local)),
            whole((rows, d_lat)),
        ],
        out_specs=[
            whole((rows, d_lat)),
            pl.BlockSpec((1, d_lat, local), lambda s: (jnp.minimum(s, 1), 0, 0)),
            pl.BlockSpec((1, d_lat, local), lambda s: (jnp.maximum(s - 2, 0), 0, 0)),
            each((d_lat, local)),
            whole((1, d_lat)),
        ],
        scratch_shapes=[
            pltpu.VMEM((rows, d_lat), jnp.bfloat16),
            pltpu.VMEM((d_lat, rows), jnp.bfloat16),
            pltpu.VMEM((d_lat, rows), jnp.bfloat16),
            pltpu.VMEM((rows, d_lat), jnp.float32),
        ],
        compiler_params=pltpu.CompilerParams(vmem_limit_bytes=36 << 20),
        cost_estimate=pl.CostEstimate(
            flops=9 * 10**9, bytes_accessed=26 * 10**6, transcendentals=0
        ),
    )(in_vmem(grad), in_hbm(latent), in_hbm(gain), in_hbm(wide), in_hbm(wideout), in_hbm(active), in_hbm(slope), in_hbm(low))


def write_kernel(stage, held, raws, results, scratch):
    (
        own_weight_ref,
        weight_total_ref,
        latent_ref,
        noisy_ref,
        noise_ref,
        keep_ref,
        place_ref,
        pixels_ref,
        wide_gain_ref,
        gain_ref,
        key_weight_ref,
        value_weight_ref,
        query_weight_ref,
        out_weight_ref,
    ) = held
    (
        latent_grad_ref,
        key_grad_ref,
        value_grad_ref,
        query_grad_ref,
        out_grad_ref,
        wide_gain_grad_ref,
        gain_grad_ref,
        embed_grad_ref,
        head_grad_ref,
        loss_ref,
    ) = results
    queries, outputs, upstream, query_grads, normed_ref, scale_ref = scratch
    stage.wait(*range(10))
    patches, width = queries.shape
    group = 4 * HEAD_DIM
    groups = width // group
    latents = latent_ref.shape[0]
    rows = 4 * latents
    weight, weight_total = own_weight_ref[:1, :1], weight_total_ref[:1, :1]

    latent_normed, latent_scale = norm_rows(latent_ref[...])
    latent_low = (latent_normed * wide_gain_ref[...]).astype(jnp.bfloat16)
    interface = embed(noisy_ref[...], pixels_ref[0], place_ref[...])
    normed, scale = norm_rows(interface)
    normed_ref[...] = normed
    scale_ref[...] = scale
    outer_low = (normed * gain_ref[1:2]).astype(jnp.bfloat16)
    stage.wait(10, 11)
    keys = dot(latent_low, key_weight_ref[...]).astype(jnp.bfloat16)
    values = dot(latent_low, value_weight_ref[...]).astype(jnp.bfloat16)
    stage.wait(12, 13)
    queries[...] = dot(outer_low, query_weight_ref[...]).astype(jnp.bfloat16)

    def part(values, index):
        return values[:, index * group : (index + 1) * group]

    def by_head(values):
        return values.reshape(4, latents, patches)

    def group_probs(index):
        scores = by_head(dot(scaled_heads(part(keys, index)), part(queries, index), 1, 1))
        grown = jnp.exp(scores - jnp.max(scores, 1, keepdims=True))
        return grown / jnp.sum(grown, 1, keepdims=True)

    for index in range(groups):
        probs = group_probs(index).reshape(rows, patches).astype(jnp.bfloat16)
        output = dot(probs, spread_heads(part(values, index)), 0, 0)
        outputs[:, index * group : (index + 1) * group] = output.astype(jnp.bfloat16)

    outer = interface + dot(outputs[...], out_weight_ref[...], 1, 1)
    final_normed, final_scale = norm_rows(outer)
    final_low = (final_normed * gain_ref[2:3]).astype(jnp.bfloat16)
    head = pixels_ref[1]
    difference = dot(head, final_low, 1, 1) - noise_ref[...]
    masked = weight * keep_ref[...] * difference
    loss_ref[...] = jnp.full(loss_ref.shape, jnp.sum(masked * difference))
    predict_grad = (2.0 * masked / weight_total).astype(jnp.bfloat16)
    head_grad_ref[...] = dot(predict_grad, final_low)
    final_grad = dot(predict_grad, head, 0, 0)
    gain_final = jnp.sum(final_grad * final_normed, 0, keepdims=True)
    outer_grad = norm_rows_back(final_grad, gain_ref[2:3], final_normed, final_scale)
    branch = outer_grad.astype(jnp.bfloat16)
    out_grad_ref[...] = dot(branch, outputs[...], 0, 0)
    stage.store(4)
    upstream[...] = dot(branch, out_weight_ref[...]).astype(jnp.bfloat16)

    key_grads, value_grads = [], []
    for index in range(groups):
        probs = group_probs(index)
        low = probs.reshape(rows, patches).astype(jnp.bfloat16)
        above = part(upstream, index)
        value_grads.append(join_heads(dot(low, above), 4).astype(jnp.bfloat16))
        prob_grad = by_head(dot(spread_heads(part(values, index)), above, 1, 1))
        inner = jnp.sum(prob_grad * probs, 1, keepdims=True)
        score_grad = (probs * (prob_grad - inner)).reshape(rows, patches).astype(jnp.bfloat16)
        key_grad = join_heads(dot(score_grad, part(queries, index)), 4) * HEAD_DIM ** (-0.5)
        key_grads.append(key_grad.astype(jnp.bfloat16))
        query_grad = dot(score_grad, scaled_heads(part(keys, index)), 0, 0)
        query_grads[:, index * group : (index + 1) * group] = query_grad.astype(jnp.bfloat16)
    key_grad, value_grad = (jnp.concatenate(item, 1) for item in (key_grads, value_grads))

    turned = latent_low.T
    key_grad_ref[...] = dot(turned, key_grad)
    value_grad_ref[...] = dot(turned, value_grad)
    stage.store(1, 2)
    latent_part = dot(key_grad, key_weight_ref[...], 1, 1) + dot(
        value_grad, value_weight_ref[...], 1, 1
    )
    wide_gain_grad_ref[...] = jnp.sum(latent_part * latent_normed, 0, keepdims=True)
    latent_grad_ref[...] = norm_rows_back(
        latent_part, wide_gain_ref[...], latent_normed, latent_scale
    )
    normed, scale = normed_ref[...], scale_ref[...]
    outer_low = (normed * gain_ref[1:2]).astype(jnp.bfloat16)
    query_grad_ref[...] = dot(outer_low, query_grads[...], 0, 0)
    stage.store(3)
    outer_part = dot(query_grads[...], query_weight_ref[...], 1, 1)
    gain_outer = jnp.sum(outer_part * normed, 0, keepdims=True)
    gain_grad_ref[...] = jnp.concatenate([gain_outer, gain_final], 0)
    back = outer_grad + norm_rows_back(outer_part, gain_ref[1:2], normed, scale)
    embed_grad_ref[...] = embed_back(noisy_ref[...], back)


def write_stage(
    own_weight, weight_total, latent, noisy, noise, keep, place, pixels, wide_gain, gains, weights
):
    latents, d_lat = latent.shape
    rows, patches = noisy.shape
    d_if = place.shape[1]
    width = weights[0].shape[1]
    results = [
        (latents, d_lat),
        (d_lat, width),
        (d_lat, width),
        (d_if, width),
        (d_if, width),
        (1, d_lat),
        (2, d_if),
        (rows, d_if),
        (rows, d_if),
        (8, 128),
    ]
    wide = pltpu.VMEM((patches, width), jnp.bfloat16)
    return staged(
        write_kernel,
        [
            own_weight,
            weight_total,
            latent,
            noisy,
            noise,
            keep,
            place,
            pixels,
            wide_gain,
            gains,
            *weights,
        ],
        [jax.ShapeDtypeStruct(shape, jnp.float32) for shape in results],
        [wide] * 4
        + [pltpu.VMEM((patches, d_if), jnp.float32), pltpu.VMEM((patches, 1), jnp.float32)],
        15 * 10**9,
        length=27,
    )


def adam_update(master, first, second, gradient, scale):
    clipped = gradient * scale
    moment = adam_beta * first + (1.0 - adam_beta) * clipped
    square = adam_beta * second + (1.0 - adam_beta) * clipped * clipped
    fixed_first = moment / (1.0 - adam_beta**STEP)
    fixed_second = square / (1.0 - adam_beta**STEP)
    updated = master - learning_rate * (
        fixed_first / (jnp.sqrt(fixed_second) + adam_eps) + weight_decay * master
    )
    return (updated, moment, square)


def sum_rows(values):
    return jnp.sum(values.reshape(-1, 8, values.shape[-1]), 0)


def closing_kernel(count, count_dp, sizes, stage, held, raws, results, scratch):
    refs, given = list(scratch), list(held)

    def pull(number, source=None):
        source = refs if source is None else source
        taken = source[:number]
        del source[:number]
        return taken

    number, finished = sizes
    items, small_parts = views(pull(number, given)), pull(10, given)
    loss_tile, weight_tile = pull(2, given)
    done = views(pull(finished, given), 2)
    wide_out, narrow_out, turned_out, last_out, latents_out, rest_out, stats = results
    latents_item, rest_item, columns, column_sems = pull(4)
    number = len(items)
    shares = pull(number + 2)
    each = count_dp.bit_length() + 1
    sums = PieceSums(count_dp, items, shares[:number], pull(number * each))
    tiny = PieceSums(count_dp, [latents_item, rest_item], shares[number:], pull(2 * each))
    (write_share,) = pull(1)
    scatter = LineScatter(count, columns, write_share, pull(4), pull(4))
    small = [Spread("mp", count, *pull(3)) for _ in range(2)]
    over_dp, over_mp = Spread("dp", count_dp, *pull(3)), Spread("mp", count, *pull(3))

    column_loads, low = [], 0
    block, local = columns.shape[0] // count, columns.shape[1]
    for source in raws:
        rows = source.shape[0]
        for owner in range(count):
            column_loads.append(
                pltpu.make_async_copy(
                    source.at[:, pl.ds(owner * local, local)],
                    columns.at[pl.ds(owner * block + low, rows)],
                    column_sems.at[len(column_loads)],
                )
            )
        low += rows
    for load in column_loads:
        load.start()
    barrier = pltpu.get_barrier_semaphore()
    others = [over_dp.peer(step) for step in range(1, count_dp)]
    others += [over_mp.peer(step) for step in range(1, count)]
    signal_all(barrier, others)
    stage.wait()
    (latent_total, *gains, gain_side, gain_pair, side_embed, own_embed, head_grad) = small_parts
    d_if = gain_side.shape[1]
    lanes = d_if // count_dp
    width = latents_item.shape[2]
    rest_item[...] = jnp.zeros_like(rest_item)
    rows = []
    for gain in gains:
        rows += [gain[:, :d_if], gain[:, d_if:]]
    rows += [gain_side[...], gain_pair[...]]
    blocks = [(0, jnp.concatenate(rows, 0)), (16, side_embed[...] + own_embed[...]), (32, head_grad[...])]
    for piece in range(count_dp):
        latents_item[piece] = latent_total[:, piece * width : (piece + 1) * width]
        for first, block in blocks:
            rest_item[piece, pl.ds(first, block.shape[0]), :lanes] = block[
                :, piece * lanes : (piece + 1) * lanes
            ]
    pl.semaphore_wait(barrier, len(others))

    tiny.begin()
    sums.begin()
    for load in column_loads:
        load.wait()
    tiny.advance(1)

    def between():
        sums.advance(1)
        tiny.advance(2)

    scatter.run(between)
    for phase in range(3, tiny.bits + 1):
        tiny.advance(phase)
    for spread, share in zip(small, shares[-2:]):
        spread.held[spread.place] = share[...]
        spread.start()
    for phase in range(2, sums.bits + 1):
        sums.advance(phase)
    scatter.settle()

    self_in_2, self_out, read_query, read_out, read_key, read_value = shares[:6]
    self_in_0, self_in_1 = done[:2]
    up, down = done[2:6], done[6:10]
    lat_rows, if_rows = self_out.shape[0], read_key.shape[0]
    write_key, write_value = (write_share.at[pl.ds(i * lat_rows, lat_rows)] for i in range(2))
    write_query, write_out = (
        write_share.at[pl.ds(2 * lat_rows + i * if_rows, if_rows)] for i in range(2)
    )
    square = 0.0

    def keep(out, gradient, turn=False):
        nonlocal square
        value = gradient[...]
        square = square + sum_rows(value * value)
        out[...] = value.T if turn else value

    wide = [read_query, self_in_0, self_in_1, self_in_2] + up + [write_key, write_value]
    for slot, gradient in enumerate(wide):
        keep(wide_out.at[slot], gradient)
    for slot, gradient in enumerate([read_key, read_value, write_query]):
        keep(narrow_out.at[slot], gradient)
    for slot, gradient in enumerate([read_out, self_out] + down):
        keep(turned_out.at[slot], gradient, True)
    keep(last_out, write_out)
    stage.store(0, 1, 2, 3)
    for spread in small:
        spread.take()
    latents, rest = (spread.total() for spread in small)
    latents_out[...] = latents
    rest_out[...] = rest
    lead = (over_mp.place == 0).astype(jnp.float32)
    local = jnp.sum(square) + lead * (
        jnp.sum(sum_rows(latents * latents)) + jnp.sum(sum_rows(rest * rest))
    )
    lane = lax.broadcasted_iota(jnp.int32, (8, 128), 1)
    value = jnp.where(lane == 0, local, loss_tile[...])
    for spread in (over_dp, over_mp):
        spread.held[spread.place] = value
        spread.start()
        spread.take()
        value = spread.total()
    stats[...] = jnp.where(lane == 0, jnp.sqrt(value), value / weight_tile[...])
    sums.finish()
    tiny.finish()
    scatter.finish()
    for spread in small + [over_dp, over_mp]:
        spread.finish()


def closing(items, small_parts, tiles, done, write_shares, call_id):
    items, shapes, _ = piece_shapes(items)
    count, count_dp = lax.axis_size("mp"), lax.axis_size("dp")
    latents, d_lat = small_parts[0].shape
    lat_rows, local = done[0].shape[1:]
    if_rows = write_shares[2].shape[0]
    extra = [(latents, d_lat // count_dp), (48, 128)]
    block = (sum(item.shape[0] for item in write_shares), local)
    columns = (count * block[0], local)
    outs = [
        (10, lat_rows, local),
        (3, if_rows, local),
        (6, local, lat_rows),
        (if_rows, local),
        *extra,
        (8, 128),
    ]
    shapes = shapes + extra
    scratch = (
        [pltpu.VMEM((count_dp,) + shape, jnp.float32) for shape in extra]
        + [
            pltpu.VMEM(columns, jnp.float32),
            pltpu.SemaphoreType.DMA((count * len(write_shares),)),
        ]
        + [pltpu.VMEM(shape, jnp.float32) for shape in shapes]
        + PieceSums.scratch(count_dp, shapes)
        + [pltpu.VMEM(block, jnp.float32)]
        + LineScatter.scratch(count, columns, 4)
        + Spread.scratch(count, extra[0])
        + Spread.scratch(count, extra[1])
        + Spread.scratch(count_dp, (8, 128))
        + Spread.scratch(count, (8, 128))
    )
    return staged(
        partial(closing_kernel, count, count_dp, (len(items), len(done))),
        [*items, *small_parts, *tiles, *done],
        [jax.ShapeDtypeStruct(shape, jnp.float32) for shape in outs],
        scratch,
        10**7,
        write_shares,
        call_id,
        50,
    )


def clip_scale(norm):
    return clip_level / jnp.maximum(norm, clip_level)


def update_kernel(kinds, *refs):
    number = 3 * (kinds + 1)
    sources, states, refs = refs[: 1 + kinds], refs[1 + kinds :][:number], refs[1 + kinds + number :]
    outs, local, refs = refs[:number], refs[number:][: 1 + kinds], refs[number + 1 + kinds :]
    local_sems, held, (in_sems, out_sems) = refs[0], refs[1 : 1 + number], refs[1 + number :]
    stats, gradients = local[0], local[1:]
    kinds += 1
    firsts = [
        pltpu.make_async_copy(source, target, local_sems.at[index])
        for index, (source, target) in enumerate(zip(sources, local))
    ]
    for first in firsts:
        first.start()
    lane = lax.broadcasted_iota(jnp.int32, (8, 128), 1)
    corner = jnp.logical_and(lane == 0, lax.broadcasted_iota(jnp.int32, (8, 128), 0) == 0)
    loads, copies = [], []
    pieces = []
    for kind, gradient in enumerate(gradients):
        slots = range(gradient.shape[0]) if len(gradient.shape) == 3 else [None]
        pieces += [(kind, slot) for slot in slots]

    def at(ref, slot):
        return ref if slot is None else ref.at[slot]

    for kind, slot in pieces:
        for index in range(3 * kind, 3 * kind + 3):
            source, target = at(states[index], slot), at(held[index], slot)
            loads.append(pltpu.make_async_copy(source, target, in_sems.at[len(loads)]))
            loads[-1].start()
    for load in firsts:
        load.wait()
    scale = jnp.sum(jnp.where(corner, clip_scale(stats[...]), 0.0))
    pixel_loads = [
        pltpu.make_async_copy(states[index], held[index], in_sems.at[len(loads) + index - 18])
        for index in range(18, 21)
    ]
    for load in pixel_loads:
        load.start()
    for order, (kind, slot) in enumerate(pieces):
        for load in loads[3 * order : 3 * order + 3]:
            load.wait()
        refs = [at(held[index], slot) for index in range(3 * kind, 3 * kind + 3)]
        source = at(gradients[kind], slot)
        rows, width = refs[0].shape
        step = math.gcd(rows, max(8, 8192 // width)) if rows % 8 == 0 else rows

        def one(index, carry, refs=refs, source=source, step=step, width=width):
            where = pl.ds(pl.multiple_of(index * step, step), step)
            state = [ref[where] for ref in refs]
            for ref, result in zip(refs, adam_update(*state, source[where, :width], scale)):
                ref[where] = result
            return carry

        lax.fori_loop(0, rows // step, one, 0)
        for index in range(3 * kind, 3 * kind + 3):
            source, target = at(held[index], slot), at(outs[index], slot)
            copies.append(pltpu.make_async_copy(source, target, out_sems.at[len(copies)]))
            copies[-1].start()
    for load in pixel_loads:
        load.wait()
    pixels, rest = held[18:21], gradients[-1]
    for slot in range(2):
        gradient = rest[16 * (slot + 1) : 16 * (slot + 1) + PIX, : pixels[0].shape[2]]
        state = [ref[:, slot, :] for ref in pixels]
        for ref, result in zip(pixels, adam_update(*state, gradient, scale)):
            ref[:, slot, :] = result
    for index in range(18, 21):
        copies.append(pltpu.make_async_copy(held[index], outs[index], out_sems.at[len(copies)]))
        copies[-1].start()
    for copy in copies:
        copy.wait()


def update_states(stats, gradients, states):
    kinds = len(gradients)
    copies = sum(3 * (item.shape[0] if item.ndim == 3 else 1) for item in gradients) + 3
    sems = pltpu.SemaphoreType.DMA((copies,))
    return pl.pallas_call(
        partial(update_kernel, kinds),
        out_shape=[pltpu.HBM(item.shape, item.dtype) for item in states],
        in_specs=[HBM_SPEC] * (1 + kinds + len(states)),
        out_specs=[HBM_SPEC] * len(states),
        scratch_shapes=[pltpu.VMEM(item.shape, jnp.float32) for item in (stats, *gradients)]
        + [pltpu.SemaphoreType.DMA((1 + kinds,))]
        + [pltpu.VMEM(item.shape, jnp.float32) for item in states]
        + [sems] * 2,
        compiler_params=pltpu.CompilerParams(vmem_limit_bytes=24 << 20),
        cost_estimate=pl.CostEstimate(
            flops=2 * 10**7, bytes_accessed=14 * 10**6, transcendentals=0
        ),
    )(*(in_hbm(item) for item in (stats, *gradients, *states)))


def write_apart(
    latent_three,
    own_noisy,
    own_noise,
    own_keep,
    own_weight,
    weight_total,
    place,
    copy_pixels,
    gain,
    gain_rows,
    weights,
    layout,
    timesteps,
):
    write_key_weight, write_value_weight, write_query_weight, write_out_weight = weights
    images, latents, first_image, sharers = layout
    own_images, own_latents, d_lat = latent_three.shape
    write_norm, write_stats = layer_norm(latent_three, gain)
    write_low = write_norm.astype(jnp.bfloat16)

    own_interface = (
        jnp.einsum(
            "bcp,cd->bpd", own_noisy, copy_pixels[0].astype(jnp.float32), precision=precise
        )
        + place
    )

    outer_norm, outer_stats = layer_norm(own_interface, gain_rows[9])
    outer_low = outer_norm.astype(jnp.bfloat16)

    def join(spec, values, weight):
        product = jnp.einsum(spec, values, weight, preferred_element_type=jnp.float32)
        return product.astype(jnp.bfloat16)

    def image_rows(values):
        if sharers == 1:
            return values
        nothing = jnp.where(timesteps[0] > 0, 0.0, -0.0)
        whole = lax.all_gather(values.astype(jnp.float32), "mp", axis=0, tiled=True)
        whole = whole + nothing
        whole = whole.reshape(images, latents, d_lat).astype(jnp.bfloat16)
        return lax.dynamic_slice_in_dim(whole, first_image, own_images, 0)

    write_query = join("bpd,dc->bpc", outer_low, write_query_weight)
    write_key = image_rows(join("bld,dc->blc", write_low, write_key_weight))
    write_value = image_rows(join("bld,dc->blc", write_low, write_value_weight))
    write_out, write_total = attend_forward(write_query, write_key, write_value, None)
    outer = own_interface + jnp.einsum(
        "bpc,dc->bpd", write_out, write_out_weight, preferred_element_type=jnp.float32
    )
    final_norm, final_stats = layer_norm(outer, gain_rows[10])
    final_low = final_norm.astype(jnp.bfloat16)
    predicted = jnp.einsum(
        "bpd,cd->bcp", final_low, copy_pixels[1], preferred_element_type=jnp.float32
    )
    difference = predicted - own_noise
    masked = own_weight[:, None, None] * own_keep[:, None, :] * difference
    loss_local = jnp.sum(masked * difference)
    predict_grad = (2.0 * masked / weight_total).astype(jnp.bfloat16)
    head_grad = jnp.einsum(
        "bcp,bpd->cd", predict_grad, final_low, preferred_element_type=jnp.float32
    )
    final_grad = jnp.einsum(
        "bcp,cd->bpd", predict_grad, copy_pixels[1], preferred_element_type=jnp.float32
    )
    outer_grad, gain_final = norm_back(final_grad, gain_rows[10], final_stats)
    branch_low = outer_grad.astype(jnp.bfloat16)
    narrowout_grad = jnp.einsum(
        "bpd,bpc->dc", branch_low, write_out, preferred_element_type=jnp.float32
    )
    write_upstream = join("bpd,dc->bpc", branch_low, write_out_weight)
    query_grad, key_grad, value_grad = attend_back(
        write_query, write_key, write_value, None, write_total, write_upstream
    )
    write_query_grad = jnp.einsum(
        "bpd,bpc->dc", outer_low, query_grad, preferred_element_type=jnp.float32
    )
    outer_part = jnp.einsum(
        "bpc,dc->bpd", query_grad, write_query_weight, preferred_element_type=jnp.float32
    )

    def row_grad(values):
        if sharers > 1:
            whole = jnp.zeros((images, latents, d_lat), jnp.float32)
            whole = lax.dynamic_update_slice_in_dim(whole, values, first_image, 0)
            values = lax.psum_scatter(
                whole.reshape(images * sharers, own_latents, d_lat),
                "mp",
                scatter_dimension=0,
                tiled=True,
            )
        return values.astype(jnp.bfloat16)

    key_grad, value_grad = row_grad(key_grad), row_grad(value_grad)
    write_key_grad = jnp.einsum(
        "bld,blc->dc", write_low, key_grad, preferred_element_type=jnp.float32
    )
    write_value_grad = jnp.einsum(
        "bld,blc->dc", write_low, value_grad, preferred_element_type=jnp.float32
    )
    write_part = jnp.einsum(
        "blc,dc->bld", key_grad, write_key_weight, preferred_element_type=jnp.float32
    ) + jnp.einsum(
        "blc,dc->bld", value_grad, write_value_weight, preferred_element_type=jnp.float32
    )
    own_grad, gain_write = norm_back(write_part, gain, write_stats)
    outer_back, gain_outer = norm_back(outer_part, gain_rows[9], outer_stats)
    embed_grad = jnp.einsum(
        "bcp,bpd->cd", own_noisy, outer_grad + outer_back, precision=precise
    )
    return (
        own_grad,
        write_key_grad,
        write_value_grad,
        write_query_grad,
        narrowout_grad,
        gain_write,
        gain_outer,
        gain_final,
        embed_grad,
        head_grad,
        loss_local,
    )


def body(
    clean_patches,
    noise_patches,
    timesteps,
    present_mask,
    copy_widein,
    copy_narrowin,
    copy_wideout,
    copy_narrowout,
    copy_latents,
    copy_gains,
    copy_pixels,
    master_widein,
    first_widein,
    second_widein,
    master_narrowin,
    first_narrowin,
    second_narrowin,
    master_wideout,
    first_wideout,
    second_wideout,
    master_narrowout,
    first_narrowout,
    second_narrowout,
    master_latents,
    first_latents,
    second_latents,
    master_gains,
    first_gains,
    second_gains,
    master_pixels,
    first_pixels,
    second_pixels,
):
    images = clean_patches.shape[0]
    patches = clean_patches.shape[2]
    count_mp, count_dp = lax.axis_size("mp"), lax.axis_size("dp")
    mp_index, dp_index = lax.axis_index("mp"), lax.axis_index("dp")
    lead = (mp_index == 0).astype(jnp.float32)
    latents, d_lat = copy_latents.shape
    d_if = copy_gains.shape[1]
    local = copy_widein.shape[2]
    sharers = max(1, count_mp // images)
    own_images = max(1, images // count_mp)
    own_patches, own_latents = patches // sharers, latents // sharers
    first_image = mp_index * own_images // sharers
    share = lax.rem(mp_index, sharers)

    def dp_piece(values, axis):
        size = values.shape[axis] // count_dp
        return lax.dynamic_slice_in_dim(values, dp_index * size, size, axis).astype(jnp.float32)

    key_piece = dp_piece(copy_widein[:, 8], 0)
    value_piece = dp_piece(copy_widein[:, 9], 0)
    query_piece = dp_piece(copy_narrowin[:, 2], 0)
    out_piece = dp_piece(copy_narrowout, 1).T
    gathered = lax.all_gather(
        jnp.concatenate([key_piece, value_piece, query_piece, out_piece], 0), "mp"
    )

    signal = jnp.cos(0.5 * math.pi * (timesteps.astype(jnp.float32) + 0.5) / NSTEPS) ** 2
    noisy = (
        jnp.sqrt(signal)[:, None, None] * clean_patches
        + jnp.sqrt(1.0 - signal)[:, None, None] * noise_patches
    )
    loss_weight = 0.5 + signal
    keep_float = present_mask.astype(jnp.float32)
    weight_here = jnp.sum(loss_weight * PIX * jnp.sum(keep_float, 1))
    gain_rows = copy_gains.astype(jnp.float32)

    def wide_gain(index):
        return gain_rows[2 * index : 2 * index + 2].reshape(-1)

    wide_in = in_hbm(jnp.swapaxes(copy_widein, 0, 1))
    narrow_in = in_hbm(jnp.swapaxes(copy_narrowin, 0, 1))
    wide_out = in_hbm(copy_wideout)
    place = position_table(patches, d_if)
    noisy_rows, pixel_rows, noise_rows = (
        jnp.pad(item, ((0, 0), (0, 16 - PIX), (0, 0)))
        for item in (noisy, copy_pixels, noise_patches)
    )
    read_args = (
        noisy_rows,
        keep_float[:, :, None],
        place,
        pixel_rows[0],
        copy_latents,
        wide_gain(0)[None],
        gain_rows[8:9],
        wide_in,
        narrow_in,
        wide_out,
    )
    read_part, *read_kept = read_forward(*read_args)
    wide_gains = [wide_gain(index)[None] for index in range(1, 4)]
    latent_base = copy_latents.astype(jnp.float32)

    def own_tokens(values, axis):
        values = lax.dynamic_slice_in_dim(values, first_image, own_images, 0)
        return lax.dynamic_slice_in_dim(values, share * own_patches, own_patches, axis)

    own_weight = lax.dynamic_slice_in_dim(loss_weight, first_image, own_images, 0)
    own_scalar = jnp.broadcast_to(own_weight[0], (8, 128))
    own_pieces = [
        own_tokens(noisy_rows, 2),
        own_tokens(noise_rows, 2),
        own_tokens(keep_float, 1),
    ]
    side_gains = gain_rows[8:11]
    here_tile, lead = jnp.full((8, 128), weight_here), lead.reshape(1, 1)
    ready = (own_pieces, own_scalar, wide_gains, side_gains, latent_base, here_tile, lead, pixel_rows)
    gathered, read_part, ready = lax.optimization_barrier((gathered, read_part, ready))
    own_pieces, own_scalar, wide_gains, side_gains, latent_base, here_tile, lead, pixel_rows = ready
    gathered = lax.all_gather(gathered, "dp").reshape(count_dp * count_mp, -1, local)
    latent_near, latent_one, (weight_tile,) = line_sum(
        read_part, latent_base, 2, tile=here_tile
    )
    self_part, *self_kept = self_forward(
        latent_near, wide_gains[0], wide_in, wide_out, images
    )
    latent_near, latent_two, write_weights = line_sum(
        self_part, latent_one, 3, blocks=(gathered, [d_lat, d_lat, d_if, d_if])
    )
    feed_part, *feed_kept = feed_forward(latent_near, wide_gains[1], wide_in, wide_out)
    latent_three = line_scatter(feed_part, latent_two, 4)
    latent_three = latent_three.reshape(own_images, own_latents, d_lat)
    if sharers == 1 and own_images == 1:
        (
            own_grad,
            write_key_grad,
            write_value_grad,
            write_query_grad,
            narrowout_grad,
            gain_write,
            gain_pair,
            own_embed,
            head_grad,
            loss_tile,
        ) = write_stage(
            own_scalar,
            weight_tile,
            latent_three[0],
            own_pieces[0][0],
            own_pieces[1][0],
            own_pieces[2],
            place,
            pixel_rows,
            wide_gains[2],
            side_gains,
            write_weights,
        )
    else:
        (
            own_grad,
            write_key_grad,
            write_value_grad,
            write_query_grad,
            narrowout_grad,
            gain_write,
            gain_outer,
            gain_final,
            own_embed,
            head_grad,
            loss_local,
        ) = write_apart(
            latent_three,
            own_tokens(noisy, 2),
            own_tokens(noise_patches, 2),
            own_tokens(keep_float, 1),
            own_weight,
            weight_tile[0, 0],
            lax.dynamic_slice_in_dim(place, share * own_patches, own_patches, 0),
            copy_pixels,
            wide_gain(3),
            gain_rows,
            write_weights,
            (images, latents, first_image, sharers),
            timesteps,
        )
        gain_write, gain_pair = gain_write[None], jnp.stack([gain_outer, gain_final])
        own_embed, head_grad = (
            jnp.pad(item, ((0, 16 - PIX), (0, 0))) for item in (own_embed, head_grad)
        )
        loss_tile = jnp.full((8, 128), loss_local)
    latent_near, latent_grad, (key_share, query_share) = line_gather(
        own_grad.reshape(-1, d_lat), 5, [write_key_grad, write_query_grad]
    )
    latent_part, up_first, up_last, down_grad, gain_feed = feed_backward(
        latent_near, latent_two, wide_gains[1], wide_in, wide_out, *feed_kept
    )
    latent_near, latent_grad, five_shares = line_sum(
        latent_part, latent_grad, 6, [write_value_grad, narrowout_grad, up_first]
    )
    latent_part, self_first, self_last, gain_self = self_backward(
        latent_near, latent_one, wide_gains[0], wide_in, wide_out, *self_kept
    )
    latent_near, latent_grad, six_shares = line_sum(
        latent_part, latent_grad, 7, [up_last, down_grad, self_first]
    )
    read_wide, read_narrow, latent_total, gain_read, gain_side, side_embed = read_backward(
        read_args[0], *read_args[4:], *read_kept, latent_near, lead
    )
    *gradients, stats = closing(
        [self_last, read_wide, read_narrow],
        [
            latent_total,
            gain_read,
            gain_self,
            gain_feed,
            gain_write,
            gain_side,
            gain_pair,
            side_embed,
            own_embed,
            head_grad,
        ],
        [loss_tile, weight_tile],
        [six_shares[2], five_shares[2], six_shares[0], six_shares[1]],
        [key_share, five_shares[0], query_share, five_shares[1]],
        8,
    )
    states = (
        *(jnp.swapaxes(item, 0, 1) for item in (master_widein, first_widein, second_widein)),
        *(jnp.swapaxes(item, 0, 1) for item in (master_narrowin, first_narrowin, second_narrowin)),
        master_wideout,
        first_wideout,
        second_wideout,
        *(item.T for item in (master_narrowout, first_narrowout, second_narrowout)),
        master_latents,
        first_latents,
        second_latents,
        master_gains,
        first_gains,
        second_gains,
        *(jnp.swapaxes(item, 0, 1) for item in (master_pixels, first_pixels, second_pixels)),
    )
    results = update_states(stats, gradients, states)
    results = [
        jnp.swapaxes(item, 0, 1) if index < 6 or 9 <= index < 12 or index >= 18 else item
        for index, item in enumerate(results)
    ]
    return (stats[0, 1], stats[0, 0], *results)


def solution(mesh):
    in_specs = (
        P("dp", None, None),
        P("dp", None, None),
        P("dp"),
        P("dp", None),
        P(None, None, "mp"),
        P(None, None, "mp"),
        P(None, "mp", None),
        P("mp", None),
        P(),
        P(),
        P(),
        P("dp", None, "mp"),
        P("dp", None, "mp"),
        P("dp", None, "mp"),
        P("dp", None, "mp"),
        P("dp", None, "mp"),
        P("dp", None, "mp"),
        P(None, "mp", "dp"),
        P(None, "mp", "dp"),
        P(None, "mp", "dp"),
        P("mp", "dp"),
        P("mp", "dp"),
        P("mp", "dp"),
        P(None, "dp"),
        P(None, "dp"),
        P(None, "dp"),
        P(None, "dp"),
        P(None, "dp"),
        P(None, "dp"),
        P(None, None, "dp"),
        P(None, None, "dp"),
        P(None, None, "dp"),
    )
    out_specs = (
        P(),
        P(),
        P("dp", None, "mp"),
        P("dp", None, "mp"),
        P("dp", None, "mp"),
        P("dp", None, "mp"),
        P("dp", None, "mp"),
        P("dp", None, "mp"),
        P(None, "mp", "dp"),
        P(None, "mp", "dp"),
        P(None, "mp", "dp"),
        P("mp", "dp"),
        P("mp", "dp"),
        P("mp", "dp"),
        P(None, "dp"),
        P(None, "dp"),
        P(None, "dp"),
        P(None, "dp"),
        P(None, "dp"),
        P(None, "dp"),
        P(None, None, "dp"),
        P(None, None, "dp"),
        P(None, None, "dp"),
    )
    return jax.shard_map(body, mesh=mesh, in_specs=in_specs, out_specs=out_specs, check_vma=False)
```

```python
from functools import partial
import math

import jax
import jax.numpy as jnp
import numpy as np
from jax import lax
from jax.experimental import pallas as pl
from jax.experimental.pallas import tpu as pltpu
from jax.sharding import PartitionSpec as P

HEAD_DIM = 64
PIX = 12
NSTEPS = 1000
STEP = 10


precise = lax.Precision.HIGHEST
clip_level = 0.01
learning_rate = 0.05
weight_decay = 0.1
adam_beta = 0.5
adam_eps = 1e-08


def layer_norm(values, gain):
    centered = values - jnp.mean(values, -1, keepdims=True)
    scale = lax.rsqrt(jnp.mean(centered * centered, -1, keepdims=True) + 1e-05)
    normed = centered * scale
    return (normed * gain, (normed, scale))


def norm_back(upstream, gain, stats):
    normed, scale = stats
    inner = upstream * gain
    values = scale * (
        inner
        - jnp.mean(inner, -1, keepdims=True)
        - normed * jnp.mean(inner * normed, -1, keepdims=True)
    )
    gain_grad = jnp.sum((upstream * normed).reshape(-1, normed.shape[-1]), 0)
    return (values, gain_grad)


def position_table(count, width):
    place = np.arange(count, dtype=np.float64)[:, None]
    angle = place * 10000.0 ** (-2.0 * np.arange(width // 2) / width)
    return jnp.asarray(np.concatenate([np.sin(angle), np.cos(angle)], -1), jnp.float32)


def positions(count, width):
    place = jnp.arange(count, dtype=jnp.float32)[:, None]
    index = jnp.arange(width // 2, dtype=jnp.float32)[None, :]
    angle = place * jnp.exp(-math.log(10000.0) * 2.0 * index / width)
    return jnp.concatenate([jnp.sin(angle), jnp.cos(angle)], -1)


def split_heads(values):
    return values.reshape(values.shape[:-1] + (values.shape[-1] // HEAD_DIM, HEAD_DIM))


def attend_scores(queries, keys, keep_mask):
    scores = jnp.einsum(
        "bqhe,bkhe->bhqk",
        split_heads(queries),
        split_heads(keys),
        preferred_element_type=jnp.float32,
    ) * HEAD_DIM ** (-0.5)
    if keep_mask is not None:
        scores = jnp.where(keep_mask[:, None, None, :] > 0, scores, -1e30)
    return scores


def attend_forward(queries, keys, values, keep_mask):
    scores = attend_scores(queries, keys, keep_mask)
    top = jnp.max(scores, -1, keepdims=True)
    log_total = top + jnp.log(jnp.sum(jnp.exp(scores - top), -1, keepdims=True))
    probs = jnp.exp(scores - log_total).astype(jnp.bfloat16)
    output = jnp.einsum(
        "bhqk,bkhe->bqhe", probs, split_heads(values), preferred_element_type=jnp.float32
    )
    return (output.reshape(queries.shape).astype(jnp.bfloat16), log_total)


def attend_back(queries, keys, values, keep_mask, log_total, upstream):
    scores = attend_scores(queries, keys, keep_mask)
    probs = jnp.exp(scores - log_total)
    value_grad = jnp.einsum(
        "bhqk,bqhe->bkhe",
        probs.astype(jnp.bfloat16),
        split_heads(upstream),
        preferred_element_type=jnp.float32,
    )
    prob_grad = jnp.einsum(
        "bqhe,bkhe->bhqk",
        split_heads(upstream),
        split_heads(values),
        preferred_element_type=jnp.float32,
    )
    score_grad = (probs * (prob_grad - jnp.sum(prob_grad * probs, -1, keepdims=True))).astype(
        jnp.bfloat16
    )
    query_grad = jnp.einsum(
        "bhqk,bkhe->bqhe", score_grad, split_heads(keys), preferred_element_type=jnp.float32
    ) * HEAD_DIM ** (-0.5)
    key_grad = jnp.einsum(
        "bhqk,bqhe->bkhe", score_grad, split_heads(queries), preferred_element_type=jnp.float32
    ) * HEAD_DIM ** (-0.5)
    return (
        query_grad.reshape(queries.shape).astype(jnp.bfloat16),
        key_grad.reshape(keys.shape),
        value_grad.reshape(values.shape),
    )


MESH_ID = pl.DeviceIdType.MESH
HBM_SPEC = pl.BlockSpec(memory_space=pltpu.HBM)
VMEM_SPEC = pl.BlockSpec(memory_space=pltpu.VMEM)
CHUNKS = 32
VMEM_LIMIT = 56 << 20


def in_hbm(values):
    return pltpu.with_memory_space_constraint(values, pltpu.HBM)


def in_vmem(values):
    return pltpu.with_memory_space_constraint(values, pltpu.VMEM)


def remote(source, target, send_sem, recv_sem, device):
    return pltpu.make_async_remote_copy(
        src_ref=source,
        dst_ref=target,
        send_sem=send_sem,
        recv_sem=recv_sem,
        device_id=device,
        device_id_type=MESH_ID,
    )


class PieceSums:
    def __init__(self, count, items, outs, scratch):
        self.count, self.items, self.outs = count, items, outs
        self.bits = count.bit_length() - 1
        self.place = lax.axis_index("dp") if items else None
        self.held = []
        for index in range(len(items)):
            self.held.append(scratch[index * (self.bits + 2) : (index + 1) * (self.bits + 2)])

    @staticmethod
    def scratch(count, shapes):
        bits = count.bit_length() - 1
        result = []
        for rows, width in shapes:
            result.append(pltpu.VMEM((count // 2, rows, width), jnp.float32))
            for phase in range(2, bits + 1):
                result.append(
                    pltpu.VMEM((2 * (count >> phase), rows // 2, width), jnp.float32)
                )
            copies = count // 2 + 2 * sum(count >> phase for phase in range(2, bits + 1))
            result += [pltpu.SemaphoreType.DMA((copies,))] * 2
        return result

    def peers(self):
        return [{"dp": self.place ^ (1 << bit)} for bit in range(self.bits)] if self.items else []

    def order(self, half):
        later = list(range(1, self.bits))
        turn = half * (len(later) // 2)
        return later[turn:] + later[:turn]

    def first_copy(self, index, piece):
        item, held = self.items[index], self.held[index]
        other = 1 - (self.place & 1)
        return remote(
            item.at[2 * piece + other],
            held[0].at[piece],
            held[-2].at[piece],
            held[-1].at[piece],
            {"dp": self.place ^ 1},
        )

    def member(self, half, phase, entry, flip):
        bits = self.order(half)
        settled, now, rest = bits[: phase - 2], bits[phase - 2], bits[phase - 1 :]
        piece = 0
        for bit in settled:
            piece = piece | (self.place & (1 << bit))
        own = self.place & (1 << now)
        piece = piece | ((own ^ (1 << now)) if flip else own)
        for position, bit in enumerate(rest):
            if (entry >> position) & 1:
                piece = piece | (1 << bit)
        return piece >> 1

    def later_copy(self, index, half, phase, entry):
        held = self.held[index]
        rows = self.items[index].shape[1] // 2
        size = self.count >> phase
        sem = self.count // 2 + 2 * sum(self.count >> p for p in range(2, phase)) + half * size + entry
        return remote(
            held[0].at[self.member(half, phase, entry, True), pl.ds(half * rows, rows)],
            held[phase - 1].at[half * size + entry],
            held[-2].at[sem],
            held[-1].at[sem],
            {"dp": self.place ^ (1 << self.order(half)[phase - 2])},
        )

    def entries(self, phase):
        return [
            (index, half, entry)
            for index in range(len(self.items))
            for half in range(2)
            for entry in range(self.count >> phase)
        ]

    def begin(self):
        for index in range(len(self.items)):
            for piece in range(self.count // 2):
                self.first_copy(index, piece).start()

    def send(self, phase):
        for index, half, entry in self.entries(phase):
            self.later_copy(index, half, phase, entry).start()

    def advance(self, phase):
        if not self.items:
            return
        if phase == 1:
            own = self.place & 1
            for index, item in enumerate(self.items):
                total = self.held[index][0]
                for piece in range(self.count // 2):
                    self.first_copy(index, piece).wait_recv()
                    add_rows(total.at[piece], total.at[piece], item.at[2 * piece + own])
        else:
            for index, half, entry in self.entries(phase):
                self.later_copy(index, half, phase, entry).wait_recv()
                held, rows = self.held[index], self.items[index].shape[1] // 2
                where = pl.ds(half * rows, rows)
                came = held[phase - 1].at[half * (self.count >> phase) + entry]
                kept = held[0].at[self.member(half, phase, entry, False), where]
                if phase == self.bits:
                    add_rows(self.outs[index].at[where], kept, came)
                else:
                    add_rows(kept, kept, came)
        if phase < self.bits:
            self.send(phase + 1)

    def finish(self):
        for index in range(len(self.items)):
            for piece in range(self.count // 2):
                self.first_copy(index, piece).wait_send()
        for phase in range(2, self.bits + 1):
            for index, half, entry in self.entries(phase):
                self.later_copy(index, half, phase, entry).wait_send()

    def moments(self, total):
        if not self.items:
            return [(0, total, None)]
        marks, low = [], 0
        for phase in range(1, self.bits + 1):
            share = (1 - 0.5 ** (phase - 1)) / (1 - 0.5 ** (self.bits - 1))
            high = total if phase == self.bits else int(total * (0.22 + 0.78 * share))
            marks.append((low, high, phase))
            low = high
        return marks


def add_rows(target, left, right):
    rows, width = target.shape
    step = math.gcd(rows, max(8, 8192 // width))

    def one(index, carry):
        where = pl.ds(pl.multiple_of(index * step, step), step)
        target[where] = left[where] + right[where]
        return carry

    lax.fori_loop(0, rows // step, one, 0)


class Spread:
    def __init__(self, name, count, held, send_sem, recv_sem):
        self.name, self.count, self.held = name, count, held
        self.send_sem, self.recv_sem = send_sem, recv_sem
        self.place = lax.axis_index(name)

    @staticmethod
    def scratch(count, shape):
        sems = pltpu.SemaphoreType.DMA((count,))
        return [pltpu.VMEM((count,) + shape, jnp.float32), sems, sems]

    def peer(self, step):
        return {self.name: lax.rem(self.place + step, self.count)}

    def copy(self, step, slot):
        return remote(
            self.held.at[slot],
            self.held.at[slot],
            self.send_sem.at[step],
            self.recv_sem.at[slot],
            self.peer(step),
        )

    def each(self, action):
        def one(step, carry):
            action(step)
            return carry

        lax.fori_loop(1, self.count, one, 0)

    def start(self):
        self.each(lambda step: self.copy(step, self.place).start())

    def take(self):
        self.each(lambda step: self.copy(step, lax.rem(self.place + step, self.count)).wait_recv())

    def finish(self):
        self.each(lambda step: self.copy(step, self.place).wait_send())

    def total(self):
        return lax.fori_loop(
            1, self.count, lambda slot, carry: carry + self.held[slot], self.held[0]
        )


class Convert:
    def __init__(self, count_mp, steps, blocks, outs, buffer, sems):
        self.count_mp, self.blocks, self.outs = count_mp, blocks, outs
        self.buffer, self.sems = buffer, sems
        self.number = blocks.shape[0]
        self.each, self.stride = max(1, self.number // steps), max(1, steps // self.number)

    @staticmethod
    def scratch(block):
        return [pltpu.VMEM((3,) + block, jnp.float32), pltpu.SemaphoreType.DMA((3,))]

    def copy(self, index):
        slot = lax.rem(index, 3)
        return pltpu.make_async_copy(
            self.blocks.at[index], self.buffer.at[slot], self.sems.at[slot]
        )

    def begin(self):
        self.copy(0).start()
        self.copy(1).start()

    def one(self, index):
        self.copy(index).wait()

        @pl.when(index + 2 < self.number)
        def _():
            self.copy(index + 2).start()

        block = self.buffer.at[lax.rem(index, 3)]
        local = block.shape[1]
        columns = pl.ds(pl.multiple_of(lax.rem(index, self.count_mp) * local, local), local)
        low = 0
        for out in self.outs:
            rows = out.shape[0] * self.count_mp // self.number
            where = pl.ds(pl.multiple_of(index // self.count_mp * rows, rows), rows)
            out[where, columns] = block[pl.ds(low, rows)].astype(jnp.bfloat16)
            low += rows

    def step(self, index):
        @pl.when(lax.rem(index, self.stride) == 0)
        def _():
            for entry in range(self.each):
                self.one(index // self.stride * self.each + entry)


def signal_all(barrier, others):
    for other in others:
        pl.semaphore_signal(barrier, inc=1, device_id=other, device_id_type=MESH_ID)


class Stage:
    def __init__(self, sources, held, in_sems, results, targets, out_sems):
        self.loads = [
            pltpu.make_async_copy(source, target, in_sems.at[index])
            for index, (source, target) in enumerate(zip(sources, held))
        ]
        self.stores = [
            pltpu.make_async_copy(source, target, out_sems.at[index])
            for index, (source, target) in enumerate(zip(results, targets))
        ]
        self.stored, self.waited = [], []

    def start(self):
        for load in self.loads:
            load.start()

    def wait(self, *indices):
        for index in indices or range(len(self.loads)):
            if index not in self.waited:
                self.loads[index].wait()
                self.waited.append(index)

    def store(self, *indices):
        for index in indices:
            self.stores[index].start()
            self.stored.append(index)

    def finish(self):
        self.store(*(index for index in range(len(self.stores)) if index not in self.stored))
        for store in self.stores:
            store.wait()


def staged_kernel(body, counts, *refs):
    refs = list(refs)

    def pull(number):
        taken = refs[:number]
        del refs[:number]
        return taken

    close, number, raw, close_outs, results = counts
    near, sources, raws = pull(close), pull(number), pull(raw)
    near_outs, targets, echoes = pull(close_outs), pull(results), pull(close_outs)
    held, outs, (in_sems, out_sems) = pull(number), pull(results), pull(2)
    stage = Stage(
        sources, held, in_sems, [*near_outs, *outs], [*echoes, *targets], out_sems
    )
    stage.start()
    body(stage, [*near, *held], raws, [*near_outs, *outs], refs)
    stage.finish()


def staged(
    body, inputs, outs, scratch, flops, raw=(), call_id=None, length=0, near=(), near_outs=()
):
    copies = [pltpu.VMEM(item.shape, item.dtype) for item in (*inputs, *outs)]
    stores = [*outs, *near_outs]
    sems = [pltpu.SemaphoreType.DMA((max(1, len(group)),)) for group in (inputs, stores)]
    needed = sum(
        math.prod(item.shape) * jnp.dtype(item.dtype).itemsize
        for item in copies + list(scratch)
        if getattr(item, "dtype", None) in (jnp.float32, jnp.bfloat16)
    )
    params = {} if call_id is None else {"collective_id": call_id, "has_side_effects": True}
    counts = (len(near), len(inputs), len(raw), len(near_outs), len(outs))
    results = pl.pallas_call(
        partial(staged_kernel, body, counts),
        out_shape=[pltpu.VMEM(item.shape, item.dtype) for item in near_outs]
        + [pltpu.HBM(item.shape, item.dtype) for item in stores],
        in_specs=[VMEM_SPEC] * len(near) + [HBM_SPEC] * (len(inputs) + len(raw)),
        out_specs=[VMEM_SPEC] * len(near_outs) + [HBM_SPEC] * len(stores),
        scratch_shapes=copies + sems + list(scratch),
        compiler_params=pltpu.CompilerParams(vmem_limit_bytes=needed + (6 << 20), **params),
        cost_estimate=pl.CostEstimate(
            flops=flops, bytes_accessed=length * 3_500_000, transcendentals=0
        ),
    )(*map(in_vmem, near), *map(in_hbm, (*inputs, *raw)))
    return list(results)


def greet(place, count, others=()):
    barrier = pltpu.get_barrier_semaphore()
    below, above = {"mp": place - 1}, {"mp": place + 1}

    @pl.when(place > 0)
    def _():
        pl.semaphore_signal(barrier, inc=1, device_id=below, device_id_type=MESH_ID)

    @pl.when(place < count - 1)
    def _():
        pl.semaphore_signal(barrier, inc=1, device_id=above, device_id_type=MESH_ID)

    signal_all(barrier, others)
    inside = jnp.logical_and(place > 0, place < count - 1)

    @pl.when(inside)
    def _():
        pl.semaphore_wait(barrier, 2 + len(others))

    @pl.when(jnp.logical_not(inside))
    def _():
        pl.semaphore_wait(barrier, 1 + len(others))


def views(refs, base=3):
    result = []
    for ref in refs:
        if len(ref.shape) == base:
            result.append(ref)
        else:
            result += [ref.at[slot] for slot in range(ref.shape[0])]
    return result


def line_sum_kernel(count, count_dp, extra, tiled, stage, held, raws, results, scratch):
    refs = list(scratch)

    def pull(number):
        taken = refs[:number]
        del refs[:number]
        return taken

    part_ref, base_ref, tile = held[0], held[1], held[2 + extra :]
    items, outs = views(held[2 : 2 + extra]), views(results[1 : 1 + extra], 2)
    out_ref, tile_out = results[0], results[1 + extra : 1 + extra + tiled]
    base_rows = base_ref.shape[0]
    inner, from_away, from_toward, toward_send, away_send, away_recv, toward_recv = pull(7)
    chunks = toward_send.shape[0]
    spread = Spread("dp", count_dp, *pull(3)) if tiled else None
    turn = pull(1)[0] if tiled else None
    sums = PieceSums(count_dp, items, outs, refs)
    place = lax.axis_index("mp")
    half = count // 2
    low_side = place < half
    toward = {"mp": jnp.where(low_side, place + 1, place - 1)}
    away = {"mp": jnp.where(low_side, place - 1, place + 1)}
    middle = jnp.logical_or(place == half - 1, place == half)
    outermost = jnp.logical_or(place == 0, place == count - 1)
    rows = part_ref.shape[0] // chunks
    others = [spread.peer(step) for step in range(1, count_dp)] if tiled else sums.peers()
    greet(place, count, others)

    def window(step):
        return pl.ds(pl.multiple_of(step * rows, rows), rows)

    def put(step, total):
        first = lax.rem(step * rows, base_rows)
        out_ref[window(step)] = total + base_ref[pl.ds(pl.multiple_of(first, rows), rows)]

    def push(step, source, inside):
        target = from_toward if inside else from_away
        recv = toward_recv if inside else away_recv
        return remote(
            source.at[window(step)],
            target.at[window(step)],
            toward_send.at[step],
            recv.at[step],
            toward,
        )

    def back(step, source):
        return remote(
            source.at[window(step)],
            from_toward.at[window(step)],
            away_send.at[step],
            toward_recv.at[step],
            away,
        )

    def gather_in(step):
        push(step, part_ref, False).wait_recv()
        inner[window(step)] = part_ref[window(step)] + from_away[window(step)]

    odd = lax.rem(lax.axis_index("dp"), 2) == 1
    if tiled:
        stage.wait()
        spread.held[spread.place] = tile[0][...]
        spread.start()

        @pl.when(jnp.logical_and(outermost, odd))
        def _():
            pl.semaphore_wait(turn, 1)

    def pass_turn():
        if tiled:

            @pl.when(jnp.logical_not(odd))
            def _():
                pl.semaphore_signal(
                    turn, inc=1, device_id=spread.peer(1), device_id_type=MESH_ID
                )

    @pl.when(outermost)
    def _():
        def leave(step, carry):
            push(step, part_ref, False).start()
            return carry

        lax.fori_loop(0, chunks, leave, 0)

    stage.wait()
    sums.begin()

    @pl.when(outermost)
    def _():

        def arrive(step, carry):
            push(step, part_ref, True).wait_recv()
            put(step, from_toward[window(step)])
            push(step, part_ref, False).wait_send()
            return carry

        if tiled:
            early = chunks * 3 // 8
            lax.fori_loop(0, early, arrive, 0)
            pass_turn()
            lax.fori_loop(early, chunks, arrive, 0)
        else:
            for low, high, phase in sums.moments(chunks):
                lax.fori_loop(low, high, arrive, 0)
                sums.advance(phase)

    lag = 2

    @pl.when(middle)
    def _():
        def finish(step):
            push(step, inner, True).wait_recv()
            push(step, inner, True).wait_send()
            total = inner[window(step)] + from_toward[window(step)]
            inner[window(step)] = total
            back(step, inner).start()
            put(step, total)

        def first(step, carry):
            gather_in(step)
            push(step, inner, True).start()
            return carry

        def both(step, carry):
            first(step, carry)
            finish(step - lag)
            return carry

        def last(step, carry):
            finish(step)
            return carry

        def drain(step, carry):
            back(step, inner).wait_send()
            return carry

        lax.fori_loop(0, lag, first, 0)
        for low, high, phase in sums.moments(chunks):
            lax.fori_loop(max(low, lag), high, both, 0)
            if high == chunks:
                lax.fori_loop(chunks - lag, chunks, last, 0)
            sums.advance(phase)
        lax.fori_loop(0, chunks, drain, 0)

    if count > 4:

        @pl.when(jnp.logical_not(jnp.logical_or(middle, outermost)))
        def _():
            def inwards(step, carry):
                gather_in(step)
                push(step, inner, False).start()
                return carry

            def outwards(step, carry):
                push(step, inner, True).wait_recv()
                back(step, from_toward).start()
                put(step, from_toward[window(step)])
                return carry

            def drain(step, carry):
                push(step, inner, False).wait_send()
                back(step, from_toward).wait_send()
                return carry

            lax.fori_loop(0, chunks, inwards, 0)
            for low, high, phase in sums.moments(chunks):
                lax.fori_loop(low, high, outwards, 0)
                sums.advance(phase)
            lax.fori_loop(0, chunks, drain, 0)

    sums.finish()
    if tiled:
        spread.take()
        tile_out[0][...] = spread.total()
        spread.finish()


def piece_shapes(items):
    count = lax.axis_size("dp")
    items = [item.reshape(item.shape[:-2] + (count, -1, item.shape[-1])) for item in items]
    shapes, shares = [], []
    for item in items:
        shapes += [item.shape[-2:]] * (item.shape[0] if item.ndim == 4 else 1)
        shares.append(jax.ShapeDtypeStruct(item.shape[:-3] + item.shape[-2:], jnp.float32))
    return items, shapes, shares


def line_sum(part, base, call_id, items=(), tile=None):
    items, shapes, shares = piece_shapes(items)
    count, count_dp = lax.axis_size("mp"), lax.axis_size("dp")
    rows, width = part.shape
    buffer = pltpu.VMEM((rows, width), jnp.float32)
    sems = pltpu.SemaphoreType.DMA((CHUNKS,))
    inputs = [base, *items]
    outs = list(shares)
    scratch = [buffer] * 3 + [sems] * 4
    if tile is not None:
        inputs.append(tile)
        outs.append(jax.ShapeDtypeStruct(tile.shape, jnp.float32))
        scratch += Spread.scratch(count_dp, tile.shape) + [pltpu.SemaphoreType.REGULAR]
    scratch += PieceSums.scratch(count_dp, shapes)
    total = jax.ShapeDtypeStruct((rows, width), jnp.float32)
    results = staged(
        partial(line_sum_kernel, count, count_dp, len(items), int(tile is not None)),
        inputs,
        outs,
        scratch,
        4 * rows * width,
        call_id=call_id,
        length=55,
        near=[part],
        near_outs=[total],
    )
    return results[0], results[-1], results[1:-1]


class LineScatter:
    def __init__(self, count, part, out, buffers, sems):
        self.count, self.part, self.out = count, part, out
        self.up_acc, self.down_acc, self.from_below, self.from_above = buffers
        self.up_send, self.down_send, self.up_recv, self.down_recv = sems
        self.place = lax.axis_index("mp")
        self.steps = self.up_send.shape[1]
        self.block = part.shape[0] // count
        self.rows = self.block // self.steps

    @staticmethod
    def scratch(count, shape, steps):
        sems = pltpu.SemaphoreType.DMA((count, steps))
        return [pltpu.VMEM(shape, jnp.float32)] * 4 + [sems] * 4

    def window(self, owner, step):
        return pl.ds(pl.multiple_of(owner * self.block + step * self.rows, self.rows), self.rows)

    def up(self, owner, step, source):
        where = self.window(owner, step)
        return remote(
            source.at[where],
            self.from_below.at[where],
            self.up_send.at[owner, step],
            self.up_recv.at[owner, step],
            {"mp": self.place + 1},
        )

    def down(self, owner, step, source):
        where = self.window(owner, step)
        return remote(
            source.at[where],
            self.from_above.at[where],
            self.down_send.at[owner, step],
            self.down_recv.at[owner, step],
            {"mp": self.place - 1},
        )

    def up_turn(self, index):
        place, part = self.place, self.part
        owner, step = self.count - 1 - index // self.steps, lax.rem(index, self.steps)

        @pl.when(jnp.logical_and(owner > place, place == 0))
        def _():
            self.up(owner, step, part).start()

        @pl.when(jnp.logical_and(owner > place, place > 0))
        def _():
            self.up(owner, step, part).wait_recv()
            where = self.window(owner, step)
            self.up_acc[where] = part[where] + self.from_below[where]
            self.up(owner, step, self.up_acc).start()

    def down_turn(self, index):
        place, part, count = self.place, self.part, self.count
        owner, step = index // self.steps, lax.rem(index, self.steps)

        @pl.when(jnp.logical_and(owner < place, place == count - 1))
        def _():
            self.down(owner, step, part).start()

        @pl.when(jnp.logical_and(owner < place, place < count - 1))
        def _():
            self.down(owner, step, part).wait_recv()
            where = self.window(owner, step)
            self.down_acc[where] = part[where] + self.from_above[where]
            self.down(owner, step, self.down_acc).start()

    def run(self, pause=None, beside=None):
        turns, lag = self.count * self.steps, self.steps

        def staggered(first, second):
            def begin(index, carry):
                first(index)
                if beside is not None:
                    beside(index)
                return carry

            def both(index, carry):
                first(index)
                second(index - lag)
                if beside is not None:
                    beside(index)
                return carry

            def end(index, carry):
                second(index)
                return carry

            lax.fori_loop(0, lag, begin, 0)
            if pause is not None:
                pause()
            lax.fori_loop(lag, turns, both, 0)
            lax.fori_loop(turns - lag, turns, end, 0)

        @pl.when(self.place < self.count // 2)
        def _():
            staggered(self.up_turn, self.down_turn)

        @pl.when(self.place >= self.count // 2)
        def _():
            staggered(self.down_turn, self.up_turn)

    def settle(self):
        place, rows = self.place, self.rows

        def one(step, carry):
            where = self.window(place, step)
            mine = pl.ds(pl.multiple_of(step * rows, rows), rows)
            self.out[mine] = self.part[where]

            @pl.when(place > 0)
            def _():
                self.up(place, step, self.part).wait_recv()
                self.out[mine] += self.from_below[where]

            @pl.when(place < self.count - 1)
            def _():
                self.down(place, step, self.part).wait_recv()
                self.out[mine] += self.from_above[where]

            return carry

        lax.fori_loop(0, self.steps, one, 0)

    def finish(self):
        place = self.place

        def one(index, carry):
            owner, step = index // self.steps, lax.rem(index, self.steps)

            @pl.when(owner > place)
            def _():
                self.up(owner, step, self.part).wait_send()

            @pl.when(owner < place)
            def _():
                self.down(owner, step, self.part).wait_send()

            return carry

        lax.fori_loop(0, self.count * self.steps, one, 0)


def line_scatter_kernel(count, stage, held, raws, results, scratch):
    own, sem = scratch[8:10]
    base, blocks = raws
    scatter = LineScatter(count, held[0], results[0], scratch[:4], scratch[4:8])
    convert = Convert(
        count, count * scatter.steps, blocks, results[1:], scratch[10], scratch[11]
    )
    rows = own.shape[0]
    load = pltpu.make_async_copy(
        base.at[pl.ds(pl.multiple_of(scatter.place * rows, rows), rows)], own, sem
    )
    load.start()
    convert.begin()
    greet(scatter.place, count)
    scatter.run(None, convert.step)
    stage.store(1, 2, 3, 4)
    scatter.settle()
    load.wait()
    results[0][...] += own[...]
    scatter.finish()


def line_scatter(part, base, blocks, sizes, call_id):
    rows, width = part.shape
    count = lax.axis_size("mp")
    own = (rows // count, width)
    result, *weights = staged(
        partial(line_scatter_kernel, count),
        [],
        [jax.ShapeDtypeStruct(own, jnp.float32)]
        + [jax.ShapeDtypeStruct((size, count * blocks.shape[2]), jnp.bfloat16) for size in sizes],
        LineScatter.scratch(count, (rows, width), 8)
        + [pltpu.VMEM(own, jnp.float32), pltpu.SemaphoreType.DMA]
        + Convert.scratch(blocks.shape[1:]),
        2 * rows * width,
        [base, blocks],
        call_id=call_id,
        length=33,
        near=[part],
    )
    return result, weights


def line_gather_kernel(count, count_dp, extra, stage, held, raws, results, scratch):
    own_ref, out_ref = held[0], results[0]
    items, outs = views(held[1:]), views(results[1:], 2)
    up_send, down_send, up_recv, down_recv = scratch[:4]
    sums = PieceSums(count_dp, items, outs, scratch[4:])
    place = lax.axis_index("mp")
    steps = up_send.shape[1]
    block = own_ref.shape[0]
    rows = block // steps
    below, above = {"mp": place - 1}, {"mp": place + 1}
    greet(place, count, sums.peers())
    stage.wait(0)

    def window(owner, step):
        return pl.ds(pl.multiple_of(owner * block + step * rows, rows), rows)

    def up(owner, step):
        part = out_ref.at[window(owner, step)]
        return remote(part, part, up_send.at[owner, step], up_recv.at[owner, step], above)

    def down(owner, step):
        part = out_ref.at[window(owner, step)]
        return remote(part, part, down_send.at[owner, step], down_recv.at[owner, step], below)

    def begin(step, carry):
        out_ref[window(place, step)] = own_ref[pl.ds(pl.multiple_of(step * rows, rows), rows)]

        @pl.when(place < count - 1)
        def _():
            up(place, step).start()

        @pl.when(place > 0)
        def _():
            down(place, step).start()

        return carry

    lax.fori_loop(0, steps, begin, 0)
    stage.wait(*range(1, len(stage.loads)))
    sums.begin()

    def pass_on(index, carry):
        away, step = 1 + index // steps, lax.rem(index, steps)

        @pl.when(place - away >= 0)
        def _():
            up(place - away, step).wait_recv()

        @pl.when(jnp.logical_and(place - away >= 0, place < count - 1))
        def _():
            up(place - away, step).start()

        @pl.when(place + away < count)
        def _():
            down(place + away, step).wait_recv()

        @pl.when(jnp.logical_and(place + away < count, place > 0))
        def _():
            down(place + away, step).start()

        return carry

    for low, high, phase in sums.moments((count - 1) * steps):
        lax.fori_loop(low, high, pass_on, 0)
        sums.advance(phase)

    def drain(index, carry):
        owner, step = index // steps, lax.rem(index, steps)

        @pl.when(jnp.logical_and(owner <= place, place < count - 1))
        def _():
            up(owner, step).wait_send()

        @pl.when(jnp.logical_and(owner >= place, place > 0))
        def _():
            down(owner, step).wait_send()

        return carry

    lax.fori_loop(0, count * steps, drain, 0)
    sums.finish()


def line_gather(own, call_id, items=()):
    rows, width = own.shape
    count, count_dp = lax.axis_size("mp"), lax.axis_size("dp")
    sems = pltpu.SemaphoreType.DMA((count, 8))
    items, shapes, shares = piece_shapes(items)
    results = staged(
        partial(line_gather_kernel, count, count_dp, len(items)),
        [own, *items],
        shares,
        [sems] * 4 + PieceSums.scratch(count_dp, shapes),
        rows * width,
        call_id=call_id,
        length=38,
        near_outs=[jax.ShapeDtypeStruct((rows * count, width), jnp.float32)],
    )
    return results[0], results[-1], results[1:-1]


def dot(left, right, left_dim=1, right_dim=0):
    return lax.dot_general(
        left, right, (((left_dim,), (right_dim,)), ((), ())), preferred_element_type=jnp.float32
    )


def head_mask(width, copies):
    lane = lax.broadcasted_iota(jnp.int32, (1, width), 1)
    return [lane // HEAD_DIM == head for head in range(copies)]


def spread_heads(values):
    masks = head_mask(values.shape[1], values.shape[1] // HEAD_DIM)
    return jnp.concatenate([jnp.where(mask, values, jnp.zeros_like(values)) for mask in masks], 0)


def join_heads(values, heads):
    rows = values.shape[0] // heads
    masks = head_mask(values.shape[1], heads)
    return sum(
        jnp.where(mask, values[head * rows : (head + 1) * rows], 0.0)
        for head, mask in enumerate(masks)
    )


def split_three(values):
    first = values.astype(jnp.bfloat16)
    left = values - first.astype(jnp.float32)
    second = left.astype(jnp.bfloat16)
    third = (left - second.astype(jnp.float32)).astype(jnp.bfloat16)
    return first, second, third


def norm_rows(values):
    centered = values - jnp.mean(values, -1, keepdims=True)
    scale = lax.rsqrt(jnp.mean(centered * centered, -1, keepdims=True) + 1e-05)
    return centered * scale, scale


def norm_rows_back(upstream, gain, normed, scale):
    inner = upstream * gain
    return scale * (
        inner
        - jnp.mean(inner, -1, keepdims=True)
        - normed * jnp.mean(inner * normed, -1, keepdims=True)
    )


def embed(noisy, pixels, place):
    stacked = jnp.concatenate(split_three(noisy), 0)
    return dot(stacked, jnp.concatenate([pixels] * 3, 0), 0, 0) + place


def read_forward_kernel(
    noisy_ref,
    keep_ref,
    place_ref,
    pixels_ref,
    latents_ref,
    wide_gain_ref,
    gain_ref,
    query_weight_ref,
    pair_weight_ref,
    out_weight_ref,
    part_ref,
    pairs_ref,
    output_ref,
    queries_ref,
    normed_ref,
    scale_ref,
    side_ref,
    probs_ref,
):
    heads = query_weight_ref.shape[2] // HEAD_DIM

    @pl.when(pl.program_id(0) == 0)
    def _():
        normed, _ = norm_rows(latents_ref[...].astype(jnp.float32))
        low = (normed * wide_gain_ref[...]).astype(jnp.bfloat16)
        queries = dot(low, query_weight_ref[0]).astype(jnp.bfloat16)
        queries_ref[...] = spread_heads(queries * jnp.bfloat16(HEAD_DIM ** (-0.5)))

    normed, scale = norm_rows(embed(noisy_ref[0], pixels_ref[...], place_ref[...]))
    normed_ref[0] = normed
    scale_ref[0] = scale
    side = (normed * gain_ref[...]).astype(jnp.bfloat16)
    side_ref[0] = side.T
    keys = dot(side, pair_weight_ref[0]).astype(jnp.bfloat16)
    values = dot(side, pair_weight_ref[1]).astype(jnp.bfloat16)
    pairs_ref[0, 0] = keys
    pairs_ref[0, 1] = values
    scores = dot(keys, queries_ref[...], 1, 1)
    scores = jnp.where(keep_ref[0] > 0, scores, -1e30)
    top = jnp.max(scores, 0, keepdims=True)
    grown = jnp.exp(scores - top)
    probs = grown / jnp.sum(grown, 0, keepdims=True)
    probs_ref[0] = probs
    output = join_heads(dot(probs.astype(jnp.bfloat16), values, 0, 0), heads)
    output = output.astype(jnp.bfloat16)
    output_ref[0] = output
    part_ref[...] = dot(output, out_weight_ref[0])


def whole(shape):
    return pl.BlockSpec(shape, lambda b: (0,) * len(shape))


def each(shape):
    return pl.BlockSpec((1,) + shape, lambda b: (b,) + (0,) * len(shape))


def slot_of(shape, slot):
    return pl.BlockSpec(shape, lambda b: (slot,) + (0,) * (len(shape) - 1))


def read_forward(noisy, keep, place, pixels, latents, wide_gain, gain, wide, narrow, wideout):
    images, _, patches = noisy.shape
    count, d_lat = latents.shape
    d_if, local = narrow.shape[1:]
    stacked = local // HEAD_DIM * count
    return pl.pallas_call(
        read_forward_kernel,
        grid=(images,),
        out_shape=[
            pltpu.VMEM((images * count, d_lat), jnp.float32),
            pltpu.HBM((images, 2, patches, local), jnp.bfloat16),
            pltpu.HBM((images, count, local), jnp.bfloat16),
            pltpu.HBM((stacked, local), jnp.bfloat16),
            pltpu.HBM((images, patches, d_if), jnp.float32),
            pltpu.HBM((images, patches, 1), jnp.float32),
            pltpu.HBM((images, d_if, patches), jnp.bfloat16),
            pltpu.HBM((images, patches, stacked), jnp.float32),
        ],
        in_specs=[
            each(noisy.shape[1:]),
            each((patches, 1)),
            whole((patches, d_if)),
            whole(pixels.shape),
            whole(latents.shape),
            whole((1, d_lat)),
            whole((1, d_if)),
            slot_of((1, d_lat, local), 0),
            slot_of((2, d_if, local), 0),
            slot_of((1, local, d_lat), 0),
        ],
        out_specs=[
            pl.BlockSpec((count, d_lat), lambda b: (b, 0)),
            each((2, patches, local)),
            each((count, local)),
            whole((stacked, local)),
            each((patches, d_if)),
            each((patches, 1)),
            each((d_if, patches)),
            each((patches, stacked)),
        ],
        compiler_params=pltpu.CompilerParams(vmem_limit_bytes=52 << 20),
        cost_estimate=pl.CostEstimate(
            flops=10**10, bytes_accessed=30 * 10**6, transcendentals=2 * 10**6
        ),
    )(in_hbm(noisy), in_hbm(keep), in_hbm(place), in_hbm(pixels), in_hbm(latents), in_hbm(wide_gain), in_hbm(gain), in_hbm(wide), in_hbm(narrow), in_hbm(wideout))


def read_backward_kernel(
    noisy_ref,
    latents_ref,
    wide_gain_ref,
    gain_ref,
    query_weight_ref,
    pair_weight_ref,
    out_weight_ref,
    pairs_ref,
    output_ref,
    queries_ref,
    normed_ref,
    scale_ref,
    side_ref,
    probs_ref,
    grad_ref,
    lead_ref,
    wide_grad_ref,
    narrow_grad_ref,
    latents_grad_ref,
    wide_gain_grad_ref,
    gain_grad_ref,
    embed_grad_ref,
    low_ref,
    returned_ref,
):
    step, steps = pl.program_id(0), pl.num_programs(0)
    heads = query_weight_ref.shape[2] // HEAD_DIM

    @pl.when(step == 0)
    def _():
        normed, _ = norm_rows(latents_ref[...].astype(jnp.float32))
        low_ref[...] = (normed * wide_gain_ref[...]).astype(jnp.bfloat16)
        for ref in (
            wide_grad_ref,
            narrow_grad_ref,
            latents_grad_ref,
            gain_grad_ref,
            embed_grad_ref,
            returned_ref,
        ):
            ref[...] = jnp.zeros_like(ref)

    normed, scale, side, probs = normed_ref[0], scale_ref[0], side_ref[0], probs_ref[0]
    keys, values, queries = pairs_ref[0, 0], pairs_ref[0, 1], queries_ref[...]
    branch = grad_ref[...].astype(jnp.bfloat16)
    latents_grad_ref[...] += lead_ref[...] * grad_ref[...]
    wide_grad_ref[1] += dot(branch, output_ref[0], 0, 0)
    upstream = spread_heads(dot(branch, out_weight_ref[0], 1, 1).astype(jnp.bfloat16))
    value_grad = dot(probs.astype(jnp.bfloat16), upstream).astype(jnp.bfloat16)
    prob_grad = dot(values, upstream, 1, 1)
    inner = jnp.sum(prob_grad * probs, 0, keepdims=True)
    score_grad = (probs * (prob_grad - inner)).astype(jnp.bfloat16)
    key_grad = dot(score_grad, queries).astype(jnp.bfloat16)
    query_grad = join_heads(dot(score_grad, keys, 0, 0), heads) * HEAD_DIM ** (-0.5)
    query_grad = query_grad.astype(jnp.bfloat16)
    wide_grad_ref[0] += dot(low_ref[...], query_grad, 0, 0)
    returned_ref[...] += dot(query_grad, query_weight_ref[0], 1, 1)
    narrow_grad_ref[0] += dot(side, key_grad)
    narrow_grad_ref[1] += dot(side, value_grad)
    side_grad = dot(key_grad, pair_weight_ref[0], 1, 1) + dot(value_grad, pair_weight_ref[1], 1, 1)
    gain_grad_ref[...] += jnp.sum(side_grad * normed, 0, keepdims=True)
    back = norm_rows_back(side_grad, gain_ref[...], normed, scale)
    embed_grad_ref[...] += embed_back(noisy_ref[0], back)

    @pl.when(step == steps - 1)
    def _():
        normed, scale = norm_rows(latents_ref[...].astype(jnp.float32))
        returned = returned_ref[...]
        wide_gain_grad_ref[...] = jnp.sum(returned * normed, 0, keepdims=True)
        latents_grad_ref[...] += norm_rows_back(returned, wide_gain_ref[...], normed, scale)


def embed_back(noisy, back):
    first, second, _ = split_three(noisy)
    high = back.astype(jnp.bfloat16)
    low = (back - high.astype(jnp.float32)).astype(jnp.bfloat16)
    rows = noisy.shape[0]
    both = dot(jnp.concatenate([first, second], 0), high)
    return both[:rows] + both[rows:] + dot(first, low)


def read_backward(
    noisy,
    latents,
    wide_gain,
    gain,
    wide,
    narrow,
    wideout,
    pairs,
    output,
    queries,
    normed,
    scale,
    side,
    probs,
    grad,
    lead,
):
    images, rows, patches = noisy.shape
    count, d_lat = latents.shape
    d_if, local = narrow.shape[1:]
    stacked = local // HEAD_DIM * count
    results = [
        (2, d_lat, local),
        (2, d_if, local),
        (count, d_lat),
        (1, d_lat),
        (1, d_if),
        (rows, d_if),
    ]
    return pl.pallas_call(
        read_backward_kernel,
        grid=(images,),
        out_shape=[pltpu.HBM(shape, jnp.float32) for shape in results],
        in_specs=[
            each(noisy.shape[1:]),
            whole(latents.shape),
            whole((1, d_lat)),
            whole((1, d_if)),
            slot_of((1, d_lat, local), 0),
            slot_of((2, d_if, local), 0),
            slot_of((1, local, d_lat), 0),
            each((2, patches, local)),
            each((count, local)),
            whole((stacked, local)),
            each((patches, d_if)),
            each((patches, 1)),
            each((d_if, patches)),
            each((patches, stacked)),
            pl.BlockSpec((count, d_lat), lambda b: (b, 0)),
            whole((1, 1)),
        ],
        out_specs=[whole(shape) for shape in results],
        scratch_shapes=[
            pltpu.VMEM((count, d_lat), jnp.bfloat16),
            pltpu.VMEM((count, d_lat), jnp.float32),
        ],
        compiler_params=pltpu.CompilerParams(vmem_limit_bytes=52 << 20),
        cost_estimate=pl.CostEstimate(
            flops=2 * 10**10, bytes_accessed=30 * 10**6, transcendentals=2 * 10**6
        ),
    )(*map(in_hbm, (noisy, latents, wide_gain, gain, wide, narrow, wideout, pairs, output, queries, normed, scale, side, probs)), in_vmem(grad), in_hbm(lead))


def rows_of(rows, width):
    return pl.BlockSpec((rows, width), lambda b: (b, 0))


def attend_few(keys, values, queries):
    scores = dot(keys, queries, 1, 1)
    top = jnp.max(scores, 0, keepdims=True)
    grown = jnp.exp(scores - top)
    summed = jnp.sum(grown, 0, keepdims=True)
    probs = (grown / summed).astype(jnp.bfloat16)
    return dot(probs, values, 0, 0), top + jnp.log(summed)


def scaled_heads(queries):
    return spread_heads(queries * jnp.bfloat16(HEAD_DIM ** (-0.5)))


def self_forward_kernel(
    latent_ref, gain_ref, q_ref, k_ref, v_ref, out_weight_ref, part_ref, triple_ref, output_ref, total_ref, low_ref
):
    heads = q_ref.shape[2] // HEAD_DIM
    normed, _ = norm_rows(latent_ref[...])
    low = (normed * gain_ref[...]).astype(jnp.bfloat16)
    low_ref[...] = low
    queries, keys, values = (dot(low, ref[0]).astype(jnp.bfloat16) for ref in (q_ref, k_ref, v_ref))
    for index, item in enumerate((queries, keys, values)):
        triple_ref[0, index] = item
    output, total_ref[0] = attend_few(keys, values, scaled_heads(queries))
    output = join_heads(output, heads).astype(jnp.bfloat16)
    output_ref[0] = output
    part_ref[...] = dot(output, out_weight_ref[0])


def self_forward(latent, gain, wide, wideout, images):
    total, d_lat = latent.shape
    count, local = total // images, wide.shape[2]
    stacked = local // HEAD_DIM * count
    return pl.pallas_call(
        self_forward_kernel,
        grid=(images,),
        out_shape=[
            pltpu.VMEM((total, d_lat), jnp.float32),
            pltpu.HBM((images, 3, count, local), jnp.bfloat16),
            pltpu.HBM((images, count, local), jnp.bfloat16),
            pltpu.HBM((images, 1, stacked), jnp.float32),
            pltpu.HBM((total, d_lat), jnp.bfloat16),
        ],
        in_specs=[rows_of(count, d_lat), whole((1, d_lat))]
        + [slot_of((1, d_lat, local), slot) for slot in (1, 2, 3)]
        + [slot_of((1, local, d_lat), 1)],
        out_specs=[
            rows_of(count, d_lat),
            each((3, count, local)),
            each((count, local)),
            each((1, stacked)),
            rows_of(count, d_lat),
        ],
        compiler_params=pltpu.CompilerParams(vmem_limit_bytes=20 << 20),
        cost_estimate=pl.CostEstimate(
            flops=3 * 10**9, bytes_accessed=12 * 10**6, transcendentals=3 * 10**5
        ),
    )(in_vmem(latent), in_hbm(gain), in_hbm(wide), in_hbm(wide), in_hbm(wide), in_hbm(wideout))


def self_backward_kernel(
    grad_ref,
    latent_ref,
    gain_ref,
    q_ref,
    k_ref,
    v_ref,
    out_weight_ref,
    triple_ref,
    output_ref,
    total_ref,
    low_ref,
    part_ref,
    first_ref,
    last_ref,
    gain_grad_ref,
    branches,
    outputs,
    grads,
    lows,
):
    step, steps = pl.program_id(0), pl.num_programs(0)
    heads = q_ref.shape[2] // HEAD_DIM
    count = grad_ref.shape[0]
    mine = pl.ds(pl.multiple_of(step * count, count), count)
    normed, scale = norm_rows(latent_ref[...])
    branch = grad_ref[...].astype(jnp.bfloat16)
    branches[mine] = branch
    outputs[mine] = output_ref[0]
    lows[mine] = low_ref[...]
    upstream = spread_heads(dot(branch, out_weight_ref[0], 1, 1).astype(jnp.bfloat16))
    keys, values = triple_ref[0, 1], triple_ref[0, 2]
    queries = scaled_heads(triple_ref[0, 0])
    probs = jnp.exp(dot(keys, queries, 1, 1) - total_ref[0])
    value_grad = dot(probs.astype(jnp.bfloat16), upstream).astype(jnp.bfloat16)
    prob_grad = dot(values, upstream, 1, 1)
    inner = jnp.sum(prob_grad * probs, 0, keepdims=True)
    score_grad = (probs * (prob_grad - inner)).astype(jnp.bfloat16)
    key_grad = dot(score_grad, queries).astype(jnp.bfloat16)
    query_grad = join_heads(dot(score_grad, keys, 0, 0), heads) * HEAD_DIM ** (-0.5)
    query_grad = query_grad.astype(jnp.bfloat16)
    part = (
        dot(query_grad, q_ref[0], 1, 1)
        + dot(key_grad, k_ref[0], 1, 1)
        + dot(value_grad, v_ref[0], 1, 1)
    )
    for index, item in enumerate((query_grad, key_grad, value_grad)):
        grads[index, mine] = item
    gain_part = jnp.sum(part * normed, 0, keepdims=True)
    gain_grad_ref[...] = gain_part + jnp.where(step == 0, 0.0, gain_grad_ref[...])
    part_ref[...] = norm_rows_back(part, gain_ref[...], normed, scale)

    @pl.when(step == steps - 1)
    def _():
        turned = lows[...].T
        first_ref[0] = dot(turned, grads[0])
        first_ref[1] = dot(turned, grads[1])
        last_ref[0] = dot(turned, grads[2])
        last_ref[1] = dot(branches[...], outputs[...], 0, 0)


def self_backward(grad, latent, gain, wide, wideout, triple, output, total, low):
    rows, d_lat = latent.shape
    images, _, count, local = triple.shape
    stacked = local // HEAD_DIM * count
    weight = pltpu.HBM((2, d_lat, local), jnp.float32)
    return pl.pallas_call(
        self_backward_kernel,
        grid=(images,),
        out_shape=[pltpu.VMEM((rows, d_lat), jnp.float32)]
        + [weight] * 2
        + [pltpu.HBM((1, d_lat), jnp.float32)],
        in_specs=[rows_of(count, d_lat), rows_of(count, d_lat), whole((1, d_lat))]
        + [slot_of((1, d_lat, local), slot) for slot in (1, 2, 3)]
        + [
            slot_of((1, local, d_lat), 1),
            each((3, count, local)),
            each((count, local)),
            each((1, stacked)),
            rows_of(count, d_lat),
        ],
        out_specs=[rows_of(count, d_lat)] + [whole((2, d_lat, local))] * 2 + [whole((1, d_lat))],
        scratch_shapes=[
            pltpu.VMEM((rows, d_lat), jnp.bfloat16),
            pltpu.VMEM((rows, local), jnp.bfloat16),
            pltpu.VMEM((3, rows, local), jnp.bfloat16),
            pltpu.VMEM((rows, d_lat), jnp.bfloat16),
        ],
        compiler_params=pltpu.CompilerParams(vmem_limit_bytes=28 << 20),
        cost_estimate=pl.CostEstimate(
            flops=6 * 10**9, bytes_accessed=16 * 10**6, transcendentals=3 * 10**5
        ),
    )(in_vmem(grad), in_hbm(latent), in_hbm(gain), in_hbm(wide), in_hbm(wide), in_hbm(wide), in_hbm(wideout), in_hbm(triple), in_hbm(output), in_hbm(total), in_hbm(low))


def feed_forward_kernel(
    latent_ref, gain_ref, up_ref, down_ref, part_ref, active_ref, slope_ref, low_ref
):
    @pl.when(pl.program_id(0) == 0)
    def _():
        normed, _ = norm_rows(latent_ref[...])
        low_ref[...] = (normed * gain_ref[...]).astype(jnp.bfloat16)

    hidden = dot(low_ref[...], up_ref[0])
    share = 0.5 * (1.0 + lax.erf(hidden * math.sqrt(0.5)))
    density = jnp.exp(-0.5 * hidden * hidden) * (1.0 / math.sqrt(2.0 * math.pi))
    active = (hidden * share).astype(jnp.bfloat16)
    active_ref[0] = active
    slope_ref[0] = share + hidden * density
    part = dot(active, down_ref[0])

    @pl.when(pl.program_id(0) == 0)
    def _():
        part_ref[...] = part

    @pl.when(pl.program_id(0) > 0)
    def _():
        part_ref[...] += part


def feed_forward(latent, gain, wide, wideout):
    rows, d_lat = latent.shape
    local = wide.shape[2]
    return pl.pallas_call(
        feed_forward_kernel,
        grid=(4,),
        out_shape=[
            pltpu.VMEM((rows, d_lat), jnp.float32),
            pltpu.HBM((4, rows, local), jnp.bfloat16),
            pltpu.HBM((4, rows, local), jnp.float32),
            pltpu.HBM((rows, d_lat), jnp.bfloat16),
        ],
        in_specs=[
            whole((rows, d_lat)),
            whole((1, d_lat)),
            pl.BlockSpec((1, d_lat, local), lambda s: (4 + s, 0, 0)),
            pl.BlockSpec((1, local, d_lat), lambda s: (2 + s, 0, 0)),
        ],
        out_specs=[
            whole((rows, d_lat)),
            each((rows, local)),
            each((rows, local)),
            whole((rows, d_lat)),
        ],
        compiler_params=pltpu.CompilerParams(vmem_limit_bytes=24 << 20),
        cost_estimate=pl.CostEstimate(
            flops=4 * 10**9, bytes_accessed=14 * 10**6, transcendentals=10**6
        ),
    )(in_vmem(latent), in_hbm(gain), in_hbm(wide), in_hbm(wideout))


def feed_backward_kernel(
    grad_ref,
    latent_ref,
    gain_ref,
    up_ref,
    down_ref,
    active_ref,
    slope_ref,
    low_ref,
    part_ref,
    up_first_ref,
    up_last_ref,
    down_grad_ref,
    gain_grad_ref,
    branch,
    branch_turned,
    low_turned,
    total,
):
    step, steps = pl.program_id(0), pl.num_programs(0)

    @pl.when(step == 0)
    def _():
        low = grad_ref[...].astype(jnp.bfloat16)
        branch[...] = low
        branch_turned[...] = low.T
        low_turned[...] = low_ref[...].T
        total[...] = jnp.zeros_like(total)

    active_grad = dot(branch[...], down_ref[0], 1, 1)
    hidden_grad = (active_grad * slope_ref[0]).astype(jnp.bfloat16)
    down_grad_ref[0] = dot(branch_turned[...], active_ref[0])
    total[...] += dot(hidden_grad, up_ref[0], 1, 1)
    up_grad = dot(low_turned[...], hidden_grad)

    @pl.when(step < 2)
    def _():
        up_first_ref[0] = up_grad

    @pl.when(step >= 2)
    def _():
        up_last_ref[0] = up_grad

    @pl.when(step == steps - 1)
    def _():
        normed, scale = norm_rows(latent_ref[...])
        part = total[...]
        gain_grad_ref[...] = jnp.sum(part * normed, 0, keepdims=True)
        part_ref[...] = norm_rows_back(part, gain_ref[...], normed, scale)


def feed_backward(grad, latent, gain, wide, wideout, active, slope, low):
    rows, d_lat = latent.shape
    local = wide.shape[2]
    return pl.pallas_call(
        feed_backward_kernel,
        grid=(4,),
        out_shape=[
            pltpu.VMEM((rows, d_lat), jnp.float32),
            pltpu.HBM((2, d_lat, local), jnp.float32),
            pltpu.HBM((2, d_lat, local), jnp.float32),
            pltpu.HBM((4, d_lat, local), jnp.float32),
            pltpu.HBM((1, d_lat), jnp.float32),
        ],
        in_specs=[
            whole((rows, d_lat)),
            whole((rows, d_lat)),
            whole((1, d_lat)),
            pl.BlockSpec((1, d_lat, local), lambda s: (4 + s, 0, 0)),
            pl.BlockSpec((1, local, d_lat), lambda s: (2 + s, 0, 0)),
            each((rows, local)),
            each((rows, local)),
            whole((rows, d_lat)),
        ],
        out_specs=[
            whole((rows, d_lat)),
            pl.BlockSpec((1, d_lat, local), lambda s: (jnp.minimum(s, 1), 0, 0)),
            pl.BlockSpec((1, d_lat, local), lambda s: (jnp.maximum(s - 2, 0), 0, 0)),
            each((d_lat, local)),
            whole((1, d_lat)),
        ],
        scratch_shapes=[
            pltpu.VMEM((rows, d_lat), jnp.bfloat16),
            pltpu.VMEM((d_lat, rows), jnp.bfloat16),
            pltpu.VMEM((d_lat, rows), jnp.bfloat16),
            pltpu.VMEM((rows, d_lat), jnp.float32),
        ],
        compiler_params=pltpu.CompilerParams(vmem_limit_bytes=36 << 20),
        cost_estimate=pl.CostEstimate(
            flops=9 * 10**9, bytes_accessed=26 * 10**6, transcendentals=0
        ),
    )(in_vmem(grad), in_hbm(latent), in_hbm(gain), in_hbm(wide), in_hbm(wideout), in_hbm(active), in_hbm(slope), in_hbm(low))


def write_kernel(stage, held, raws, results, scratch):
    (
        own_weight_ref,
        weight_total_ref,
        latent_ref,
        noisy_ref,
        noise_ref,
        keep_ref,
        place_ref,
        pixels_ref,
        wide_gain_ref,
        gain_ref,
        key_weight_ref,
        value_weight_ref,
        query_weight_ref,
        out_weight_ref,
    ) = held
    (
        latent_grad_ref,
        key_grad_ref,
        value_grad_ref,
        query_grad_ref,
        out_grad_ref,
        wide_gain_grad_ref,
        gain_grad_ref,
        embed_grad_ref,
        head_grad_ref,
        loss_ref,
    ) = results
    queries, outputs, upstream, query_grads, normed_ref, scale_ref = scratch
    stage.wait(*range(10))
    patches, width = queries.shape
    group = 4 * HEAD_DIM
    groups = width // group
    latents = latent_ref.shape[0]
    rows = 4 * latents
    weight, weight_total = own_weight_ref[:1, :1], weight_total_ref[:1, :1]

    latent_normed, latent_scale = norm_rows(latent_ref[...])
    latent_low = (latent_normed * wide_gain_ref[...]).astype(jnp.bfloat16)
    interface = embed(noisy_ref[...], pixels_ref[0], place_ref[...])
    normed, scale = norm_rows(interface)
    normed_ref[...] = normed
    scale_ref[...] = scale
    outer_low = (normed * gain_ref[1:2]).astype(jnp.bfloat16)
    stage.wait(10, 11)
    keys = dot(latent_low, key_weight_ref[...]).astype(jnp.bfloat16)
    values = dot(latent_low, value_weight_ref[...]).astype(jnp.bfloat16)
    stage.wait(12, 13)
    queries[...] = dot(outer_low, query_weight_ref[...]).astype(jnp.bfloat16)

    def part(values, index):
        return values[:, index * group : (index + 1) * group]

    def by_head(values):
        return values.reshape(4, latents, patches)

    def group_probs(index):
        scores = by_head(dot(scaled_heads(part(keys, index)), part(queries, index), 1, 1))
        grown = jnp.exp(scores - jnp.max(scores, 1, keepdims=True))
        return grown / jnp.sum(grown, 1, keepdims=True)

    for index in range(groups):
        probs = group_probs(index).reshape(rows, patches).astype(jnp.bfloat16)
        output = dot(probs, spread_heads(part(values, index)), 0, 0)
        outputs[:, index * group : (index + 1) * group] = output.astype(jnp.bfloat16)

    outer = interface + dot(outputs[...], out_weight_ref[...], 1, 1)
    final_normed, final_scale = norm_rows(outer)
    final_low = (final_normed * gain_ref[2:3]).astype(jnp.bfloat16)
    head = pixels_ref[1]
    difference = dot(head, final_low, 1, 1) - noise_ref[...]
    masked = weight * keep_ref[...] * difference
    loss_ref[...] = jnp.full(loss_ref.shape, jnp.sum(masked * difference))
    predict_grad = (2.0 * masked / weight_total).astype(jnp.bfloat16)
    head_grad_ref[...] = dot(predict_grad, final_low)
    final_grad = dot(predict_grad, head, 0, 0)
    gain_final = jnp.sum(final_grad * final_normed, 0, keepdims=True)
    outer_grad = norm_rows_back(final_grad, gain_ref[2:3], final_normed, final_scale)
    branch = outer_grad.astype(jnp.bfloat16)
    out_grad_ref[...] = dot(branch, outputs[...], 0, 0)
    stage.store(4)
    upstream[...] = dot(branch, out_weight_ref[...]).astype(jnp.bfloat16)

    key_grads, value_grads = [], []
    for index in range(groups):
        probs = group_probs(index)
        low = probs.reshape(rows, patches).astype(jnp.bfloat16)
        above = part(upstream, index)
        value_grads.append(join_heads(dot(low, above), 4).astype(jnp.bfloat16))
        prob_grad = by_head(dot(spread_heads(part(values, index)), above, 1, 1))
        inner = jnp.sum(prob_grad * probs, 1, keepdims=True)
        score_grad = (probs * (prob_grad - inner)).reshape(rows, patches).astype(jnp.bfloat16)
        key_grad = join_heads(dot(score_grad, part(queries, index)), 4) * HEAD_DIM ** (-0.5)
        key_grads.append(key_grad.astype(jnp.bfloat16))
        query_grad = dot(score_grad, scaled_heads(part(keys, index)), 0, 0)
        query_grads[:, index * group : (index + 1) * group] = query_grad.astype(jnp.bfloat16)
    key_grad, value_grad = (jnp.concatenate(item, 1) for item in (key_grads, value_grads))

    turned = latent_low.T
    key_grad_ref[...] = dot(turned, key_grad)
    value_grad_ref[...] = dot(turned, value_grad)
    stage.store(1, 2)
    latent_part = dot(key_grad, key_weight_ref[...], 1, 1) + dot(
        value_grad, value_weight_ref[...], 1, 1
    )
    wide_gain_grad_ref[...] = jnp.sum(latent_part * latent_normed, 0, keepdims=True)
    latent_grad_ref[...] = norm_rows_back(
        latent_part, wide_gain_ref[...], latent_normed, latent_scale
    )
    normed, scale = normed_ref[...], scale_ref[...]
    outer_low = (normed * gain_ref[1:2]).astype(jnp.bfloat16)
    query_grad_ref[...] = dot(outer_low, query_grads[...], 0, 0)
    stage.store(3)
    outer_part = dot(query_grads[...], query_weight_ref[...], 1, 1)
    gain_outer = jnp.sum(outer_part * normed, 0, keepdims=True)
    gain_grad_ref[...] = jnp.concatenate([gain_outer, gain_final], 0)
    back = outer_grad + norm_rows_back(outer_part, gain_ref[1:2], normed, scale)
    embed_grad_ref[...] = embed_back(noisy_ref[...], back)


def write_stage(
    own_weight, weight_total, latent, noisy, noise, keep, place, pixels, wide_gain, gains, weights
):
    latents, d_lat = latent.shape
    rows, patches = noisy.shape
    d_if = place.shape[1]
    width = weights[0].shape[1]
    results = [
        (latents, d_lat),
        (d_lat, width),
        (d_lat, width),
        (d_if, width),
        (d_if, width),
        (1, d_lat),
        (2, d_if),
        (rows, d_if),
        (rows, d_if),
        (8, 128),
    ]
    wide = pltpu.VMEM((patches, width), jnp.bfloat16)
    return staged(
        write_kernel,
        [
            own_weight,
            weight_total,
            latent,
            noisy,
            noise,
            keep,
            place,
            pixels,
            wide_gain,
            gains,
            *weights,
        ],
        [jax.ShapeDtypeStruct(shape, jnp.float32) for shape in results],
        [wide] * 4
        + [pltpu.VMEM((patches, d_if), jnp.float32), pltpu.VMEM((patches, 1), jnp.float32)],
        15 * 10**9,
        length=27,
    )


def adam_update(master, first, second, gradient, scale):
    clipped = gradient * scale
    moment = adam_beta * first + (1.0 - adam_beta) * clipped
    square = adam_beta * second + (1.0 - adam_beta) * clipped * clipped
    fixed_first = moment / (1.0 - adam_beta**STEP)
    fixed_second = square / (1.0 - adam_beta**STEP)
    updated = master - learning_rate * (
        fixed_first / (jnp.sqrt(fixed_second) + adam_eps) + weight_decay * master
    )
    return (updated, moment, square)


def sum_rows(values):
    return jnp.sum(values.reshape(-1, 8, values.shape[-1]), 0)


def closing_kernel(count, count_dp, sizes, stage, held, raws, results, scratch):
    refs, given = list(scratch), list(held)

    def pull(number, source=None):
        source = refs if source is None else source
        taken = source[:number]
        del source[:number]
        return taken

    number, finished = sizes
    items, small_parts = views(pull(number, given)), pull(10, given)
    loss_tile, weight_tile = pull(2, given)
    done = views(pull(finished, given), 2)
    wide_out, narrow_out, turned_out, last_out, latents_out, rest_out, stats = results
    latents_item, rest_item, columns, column_sems = pull(4)
    number = len(items)
    shares = pull(number + 2)
    each = count_dp.bit_length() + 1
    sums = PieceSums(count_dp, items, shares[:number], pull(number * each))
    tiny = PieceSums(count_dp, [latents_item, rest_item], shares[number:], pull(2 * each))
    (write_share,) = pull(1)
    scatter = LineScatter(count, columns, write_share, pull(4), pull(4))
    small = [Spread("mp", count, *pull(3)) for _ in range(2)]
    over_dp, over_mp = Spread("dp", count_dp, *pull(3)), Spread("mp", count, *pull(3))

    column_loads, low = [], 0
    block, local = columns.shape[0] // count, columns.shape[1]
    for source in raws:
        rows = source.shape[0]
        for owner in range(count):
            column_loads.append(
                pltpu.make_async_copy(
                    source.at[:, pl.ds(owner * local, local)],
                    columns.at[pl.ds(owner * block + low, rows)],
                    column_sems.at[len(column_loads)],
                )
            )
        low += rows
    for load in column_loads:
        load.start()
    barrier = pltpu.get_barrier_semaphore()
    others = [over_dp.peer(step) for step in range(1, count_dp)]
    others += [over_mp.peer(step) for step in range(1, count)]
    signal_all(barrier, others)
    stage.wait()
    (latent_total, *gains, gain_side, gain_pair, side_embed, own_embed, head_grad) = small_parts
    d_if = gain_side.shape[1]
    lanes = d_if // count_dp
    width = latents_item.shape[2]
    rest_item[...] = jnp.zeros_like(rest_item)
    rows = []
    for gain in gains:
        rows += [gain[:, :d_if], gain[:, d_if:]]
    rows += [gain_side[...], gain_pair[...]]
    blocks = [(0, jnp.concatenate(rows, 0)), (16, side_embed[...] + own_embed[...]), (32, head_grad[...])]
    for piece in range(count_dp):
        latents_item[piece] = latent_total[:, piece * width : (piece + 1) * width]
        for first, block in blocks:
            rest_item[piece, pl.ds(first, block.shape[0]), :lanes] = block[
                :, piece * lanes : (piece + 1) * lanes
            ]
    pl.semaphore_wait(barrier, len(others))

    tiny.begin()
    sums.begin()
    for load in column_loads:
        load.wait()
    tiny.advance(1)

    def between():
        sums.advance(1)
        tiny.advance(2)

    scatter.run(between)
    for phase in range(3, tiny.bits + 1):
        tiny.advance(phase)
    for spread, share in zip(small, shares[-2:]):
        spread.held[spread.place] = share[...]
        spread.start()
    for phase in range(2, sums.bits + 1):
        sums.advance(phase)
    scatter.settle()

    self_in_2, self_out, read_query, read_out, read_key, read_value = shares[:6]
    self_in_0, self_in_1 = done[:2]
    up, down = done[2:6], done[6:10]
    lat_rows, if_rows = self_out.shape[0], read_key.shape[0]
    write_key, write_value = (write_share.at[pl.ds(i * lat_rows, lat_rows)] for i in range(2))
    write_query, write_out = (
        write_share.at[pl.ds(2 * lat_rows + i * if_rows, if_rows)] for i in range(2)
    )
    square = 0.0

    def keep(out, gradient, turn=False):
        nonlocal square
        value = gradient[...]
        square = square + sum_rows(value * value)
        out[...] = value.T if turn else value

    wide = [read_query, self_in_0, self_in_1, self_in_2] + up + [write_key, write_value]
    for slot, gradient in enumerate(wide):
        keep(wide_out.at[slot], gradient)
    for slot, gradient in enumerate([read_key, read_value, write_query]):
        keep(narrow_out.at[slot], gradient)
    for slot, gradient in enumerate([read_out, self_out] + down):
        keep(turned_out.at[slot], gradient, True)
    keep(last_out, write_out)
    stage.store(0, 1, 2, 3)
    for spread in small:
        spread.take()
    latents, rest = (spread.total() for spread in small)
    latents_out[...] = latents
    rest_out[...] = rest
    lead = (over_mp.place == 0).astype(jnp.float32)
    local = jnp.sum(square) + lead * (
        jnp.sum(sum_rows(latents * latents)) + jnp.sum(sum_rows(rest * rest))
    )
    lane = lax.broadcasted_iota(jnp.int32, (8, 128), 1)
    value = jnp.where(lane == 0, local, loss_tile[...])
    for spread in (over_dp, over_mp):
        spread.held[spread.place] = value
        spread.start()
        spread.take()
        value = spread.total()
    stats[...] = jnp.where(lane == 0, jnp.sqrt(value), value / weight_tile[...])
    sums.finish()
    tiny.finish()
    scatter.finish()
    for spread in small + [over_dp, over_mp]:
        spread.finish()


def closing(items, small_parts, tiles, done, write_shares, call_id):
    items, shapes, _ = piece_shapes(items)
    count, count_dp = lax.axis_size("mp"), lax.axis_size("dp")
    latents, d_lat = small_parts[0].shape
    lat_rows, local = done[0].shape[1:]
    if_rows = write_shares[2].shape[0]
    extra = [(latents, d_lat // count_dp), (48, 128)]
    block = (sum(item.shape[0] for item in write_shares), local)
    columns = (count * block[0], local)
    outs = [
        (10, lat_rows, local),
        (3, if_rows, local),
        (6, local, lat_rows),
        (if_rows, local),
        *extra,
        (8, 128),
    ]
    shapes = shapes + extra
    scratch = (
        [pltpu.VMEM((count_dp,) + shape, jnp.float32) for shape in extra]
        + [
            pltpu.VMEM(columns, jnp.float32),
            pltpu.SemaphoreType.DMA((count * len(write_shares),)),
        ]
        + [pltpu.VMEM(shape, jnp.float32) for shape in shapes]
        + PieceSums.scratch(count_dp, shapes)
        + [pltpu.VMEM(block, jnp.float32)]
        + LineScatter.scratch(count, columns, 4)
        + Spread.scratch(count, extra[0])
        + Spread.scratch(count, extra[1])
        + Spread.scratch(count_dp, (8, 128))
        + Spread.scratch(count, (8, 128))
    )
    return staged(
        partial(closing_kernel, count, count_dp, (len(items), len(done))),
        [*items, *small_parts, *tiles, *done],
        [jax.ShapeDtypeStruct(shape, jnp.float32) for shape in outs],
        scratch,
        10**7,
        write_shares,
        call_id,
        50,
    )


def clip_scale(norm):
    return clip_level / jnp.maximum(norm, clip_level)


def update_kernel(kinds, *refs):
    number = 3 * (kinds + 1)
    sources, states, refs = refs[: 1 + kinds], refs[1 + kinds :][:number], refs[1 + kinds + number :]
    outs, local, refs = refs[:number], refs[number:][: 1 + kinds], refs[number + 1 + kinds :]
    local_sems, held, (in_sems, out_sems) = refs[0], refs[1 : 1 + number], refs[1 + number :]
    stats, gradients = local[0], local[1:]
    kinds += 1
    firsts = [
        pltpu.make_async_copy(source, target, local_sems.at[index])
        for index, (source, target) in enumerate(zip(sources, local))
    ]
    for first in firsts:
        first.start()
    lane = lax.broadcasted_iota(jnp.int32, (8, 128), 1)
    corner = jnp.logical_and(lane == 0, lax.broadcasted_iota(jnp.int32, (8, 128), 0) == 0)
    loads, copies = [], []
    pieces = []
    for kind, gradient in enumerate(gradients):
        slots = range(gradient.shape[0]) if len(gradient.shape) == 3 else [None]
        pieces += [(kind, slot) for slot in slots]

    def at(ref, slot):
        return ref if slot is None else ref.at[slot]

    for kind, slot in pieces:
        for index in range(3 * kind, 3 * kind + 3):
            source, target = at(states[index], slot), at(held[index], slot)
            loads.append(pltpu.make_async_copy(source, target, in_sems.at[len(loads)]))
            loads[-1].start()
    for load in firsts:
        load.wait()
    scale = jnp.sum(jnp.where(corner, clip_scale(stats[...]), 0.0))
    pixel_loads = [
        pltpu.make_async_copy(states[index], held[index], in_sems.at[len(loads) + index - 18])
        for index in range(18, 21)
    ]
    for load in pixel_loads:
        load.start()
    for order, (kind, slot) in enumerate(pieces):
        for load in loads[3 * order : 3 * order + 3]:
            load.wait()
        refs = [at(held[index], slot) for index in range(3 * kind, 3 * kind + 3)]
        source = at(gradients[kind], slot)
        rows, width = refs[0].shape
        step = math.gcd(rows, max(8, 8192 // width)) if rows % 8 == 0 else rows

        def one(index, carry, refs=refs, source=source, step=step, width=width):
            where = pl.ds(pl.multiple_of(index * step, step), step)
            state = [ref[where] for ref in refs]
            for ref, result in zip(refs, adam_update(*state, source[where, :width], scale)):
                ref[where] = result
            return carry

        lax.fori_loop(0, rows // step, one, 0)
        for index in range(3 * kind, 3 * kind + 3):
            source, target = at(held[index], slot), at(outs[index], slot)
            copies.append(pltpu.make_async_copy(source, target, out_sems.at[len(copies)]))
            copies[-1].start()
    for load in pixel_loads:
        load.wait()
    pixels, rest = held[18:21], gradients[-1]
    for slot in range(2):
        gradient = rest[16 * (slot + 1) : 16 * (slot + 1) + PIX, : pixels[0].shape[2]]
        state = [ref[:, slot, :] for ref in pixels]
        for ref, result in zip(pixels, adam_update(*state, gradient, scale)):
            ref[:, slot, :] = result
    for index in range(18, 21):
        copies.append(pltpu.make_async_copy(held[index], outs[index], out_sems.at[len(copies)]))
        copies[-1].start()
    for copy in copies:
        copy.wait()


def update_states(stats, gradients, states):
    kinds = len(gradients)
    copies = sum(3 * (item.shape[0] if item.ndim == 3 else 1) for item in gradients) + 3
    sems = pltpu.SemaphoreType.DMA((copies,))
    return pl.pallas_call(
        partial(update_kernel, kinds),
        out_shape=[pltpu.HBM(item.shape, item.dtype) for item in states],
        in_specs=[HBM_SPEC] * (1 + kinds + len(states)),
        out_specs=[HBM_SPEC] * len(states),
        scratch_shapes=[pltpu.VMEM(item.shape, jnp.float32) for item in (stats, *gradients)]
        + [pltpu.SemaphoreType.DMA((1 + kinds,))]
        + [pltpu.VMEM(item.shape, jnp.float32) for item in states]
        + [sems] * 2,
        compiler_params=pltpu.CompilerParams(vmem_limit_bytes=24 << 20),
        cost_estimate=pl.CostEstimate(
            flops=2 * 10**7, bytes_accessed=14 * 10**6, transcendentals=0
        ),
    )(*(in_hbm(item) for item in (stats, *gradients, *states)))


def write_apart(
    latent_three,
    own_noisy,
    own_noise,
    own_keep,
    own_weight,
    weight_total,
    place,
    copy_pixels,
    gain,
    gain_rows,
    weights,
    layout,
    timesteps,
):
    write_key_weight, write_value_weight, write_query_weight, write_out_weight = weights
    images, latents, first_image, sharers = layout
    own_images, own_latents, d_lat = latent_three.shape
    write_norm, write_stats = layer_norm(latent_three, gain)
    write_low = write_norm.astype(jnp.bfloat16)

    own_interface = (
        jnp.einsum(
            "bcp,cd->bpd", own_noisy, copy_pixels[0].astype(jnp.float32), precision=precise
        )
        + place
    )

    outer_norm, outer_stats = layer_norm(own_interface, gain_rows[9])
    outer_low = outer_norm.astype(jnp.bfloat16)

    def join(spec, values, weight):
        product = jnp.einsum(spec, values, weight, preferred_element_type=jnp.float32)
        return product.astype(jnp.bfloat16)

    def image_rows(values):
        if sharers == 1:
            return values
        nothing = jnp.where(timesteps[0] > 0, 0.0, -0.0)
        whole = lax.all_gather(values.astype(jnp.float32), "mp", axis=0, tiled=True)
        whole = whole + nothing
        whole = whole.reshape(images, latents, d_lat).astype(jnp.bfloat16)
        return lax.dynamic_slice_in_dim(whole, first_image, own_images, 0)

    write_query = join("bpd,dc->bpc", outer_low, write_query_weight)
    write_key = image_rows(join("bld,dc->blc", write_low, write_key_weight))
    write_value = image_rows(join("bld,dc->blc", write_low, write_value_weight))
    write_out, write_total = attend_forward(write_query, write_key, write_value, None)
    outer = own_interface + jnp.einsum(
        "bpc,dc->bpd", write_out, write_out_weight, preferred_element_type=jnp.float32
    )
    final_norm, final_stats = layer_norm(outer, gain_rows[10])
    final_low = final_norm.astype(jnp.bfloat16)
    predicted = jnp.einsum(
        "bpd,cd->bcp", final_low, copy_pixels[1], preferred_element_type=jnp.float32
    )
    difference = predicted - own_noise
    masked = own_weight[:, None, None] * own_keep[:, None, :] * difference
    loss_local = jnp.sum(masked * difference)
    predict_grad = (2.0 * masked / weight_total).astype(jnp.bfloat16)
    head_grad = jnp.einsum(
        "bcp,bpd->cd", predict_grad, final_low, preferred_element_type=jnp.float32
    )
    final_grad = jnp.einsum(
        "bcp,cd->bpd", predict_grad, copy_pixels[1], preferred_element_type=jnp.float32
    )
    outer_grad, gain_final = norm_back(final_grad, gain_rows[10], final_stats)
    branch_low = outer_grad.astype(jnp.bfloat16)
    narrowout_grad = jnp.einsum(
        "bpd,bpc->dc", branch_low, write_out, preferred_element_type=jnp.float32
    )
    write_upstream = join("bpd,dc->bpc", branch_low, write_out_weight)
    query_grad, key_grad, value_grad = attend_back(
        write_query, write_key, write_value, None, write_total, write_upstream
    )
    write_query_grad = jnp.einsum(
        "bpd,bpc->dc", outer_low, query_grad, preferred_element_type=jnp.float32
    )
    outer_part = jnp.einsum(
        "bpc,dc->bpd", query_grad, write_query_weight, preferred_element_type=jnp.float32
    )

    def row_grad(values):
        if sharers > 1:
            whole = jnp.zeros((images, latents, d_lat), jnp.float32)
            whole = lax.dynamic_update_slice_in_dim(whole, values, first_image, 0)
            values = lax.psum_scatter(
                whole.reshape(images * sharers, own_latents, d_lat),
                "mp",
                scatter_dimension=0,
                tiled=True,
            )
        return values.astype(jnp.bfloat16)

    key_grad, value_grad = row_grad(key_grad), row_grad(value_grad)
    write_key_grad = jnp.einsum(
        "bld,blc->dc", write_low, key_grad, preferred_element_type=jnp.float32
    )
    write_value_grad = jnp.einsum(
        "bld,blc->dc", write_low, value_grad, preferred_element_type=jnp.float32
    )
    write_part = jnp.einsum(
        "blc,dc->bld", key_grad, write_key_weight, preferred_element_type=jnp.float32
    ) + jnp.einsum(
        "blc,dc->bld", value_grad, write_value_weight, preferred_element_type=jnp.float32
    )
    own_grad, gain_write = norm_back(write_part, gain, write_stats)
    outer_back, gain_outer = norm_back(outer_part, gain_rows[9], outer_stats)
    embed_grad = jnp.einsum(
        "bcp,bpd->cd", own_noisy, outer_grad + outer_back, precision=precise
    )
    return (
        own_grad,
        write_key_grad,
        write_value_grad,
        write_query_grad,
        narrowout_grad,
        gain_write,
        gain_outer,
        gain_final,
        embed_grad,
        head_grad,
        loss_local,
    )


def body(
    clean_patches,
    noise_patches,
    timesteps,
    present_mask,
    copy_widein,
    copy_narrowin,
    copy_wideout,
    copy_narrowout,
    copy_latents,
    copy_gains,
    copy_pixels,
    master_widein,
    first_widein,
    second_widein,
    master_narrowin,
    first_narrowin,
    second_narrowin,
    master_wideout,
    first_wideout,
    second_wideout,
    master_narrowout,
    first_narrowout,
    second_narrowout,
    master_latents,
    first_latents,
    second_latents,
    master_gains,
    first_gains,
    second_gains,
    master_pixels,
    first_pixels,
    second_pixels,
):
    images = clean_patches.shape[0]
    patches = clean_patches.shape[2]
    count_mp, count_dp = lax.axis_size("mp"), lax.axis_size("dp")
    mp_index, dp_index = lax.axis_index("mp"), lax.axis_index("dp")
    lead = (mp_index == 0).astype(jnp.float32)
    latents, d_lat = copy_latents.shape
    d_if = copy_gains.shape[1]
    local = copy_widein.shape[2]
    sharers = max(1, count_mp // images)
    own_images = max(1, images // count_mp)
    own_patches, own_latents = patches // sharers, latents // sharers
    first_image = mp_index * own_images // sharers
    share = lax.rem(mp_index, sharers)

    def dp_piece(values, axis):
        size = values.shape[axis] // count_dp
        return lax.dynamic_slice_in_dim(values, dp_index * size, size, axis).astype(jnp.float32)

    key_piece = dp_piece(copy_widein[:, 8], 0)
    value_piece = dp_piece(copy_widein[:, 9], 0)
    query_piece = dp_piece(copy_narrowin[:, 2], 0)
    out_piece = dp_piece(copy_narrowout, 1).T
    gathered = lax.all_gather(
        jnp.concatenate([key_piece, value_piece, query_piece, out_piece], 0), "mp"
    )

    signal = jnp.cos(0.5 * math.pi * (timesteps.astype(jnp.float32) + 0.5) / NSTEPS) ** 2
    noisy = (
        jnp.sqrt(signal)[:, None, None] * clean_patches
        + jnp.sqrt(1.0 - signal)[:, None, None] * noise_patches
    )
    loss_weight = 0.5 + signal
    keep_float = present_mask.astype(jnp.float32)
    weight_here = jnp.sum(loss_weight * PIX * jnp.sum(keep_float, 1))
    gain_rows = copy_gains.astype(jnp.float32)

    def wide_gain(index):
        return gain_rows[2 * index : 2 * index + 2].reshape(-1)

    wide_in = in_hbm(jnp.swapaxes(copy_widein, 0, 1))
    narrow_in = in_hbm(jnp.swapaxes(copy_narrowin, 0, 1))
    wide_out = in_hbm(copy_wideout)
    place = position_table(patches, d_if)
    noisy_rows, pixel_rows, noise_rows = (
        jnp.pad(item, ((0, 0), (0, 16 - PIX), (0, 0)))
        for item in (noisy, copy_pixels, noise_patches)
    )
    read_args = (
        noisy_rows,
        keep_float[:, :, None],
        place,
        pixel_rows[0],
        copy_latents,
        wide_gain(0)[None],
        gain_rows[8:9],
        wide_in,
        narrow_in,
        wide_out,
    )
    read_part, *read_kept = read_forward(*read_args)
    wide_gains = [wide_gain(index)[None] for index in range(1, 4)]
    latent_base = copy_latents.astype(jnp.float32)

    def own_tokens(values, axis):
        values = lax.dynamic_slice_in_dim(values, first_image, own_images, 0)
        return lax.dynamic_slice_in_dim(values, share * own_patches, own_patches, axis)

    own_weight = lax.dynamic_slice_in_dim(loss_weight, first_image, own_images, 0)
    own_scalar = jnp.broadcast_to(own_weight[0], (8, 128))
    own_pieces = [
        own_tokens(noisy_rows, 2),
        own_tokens(noise_rows, 2),
        own_tokens(keep_float, 1),
    ]
    side_gains = gain_rows[8:11]
    here_tile, lead = jnp.full((8, 128), weight_here), lead.reshape(1, 1)
    ready = (own_pieces, own_scalar, wide_gains, side_gains, latent_base, here_tile, lead, pixel_rows)
    gathered, read_part, ready = lax.optimization_barrier((gathered, read_part, ready))
    own_pieces, own_scalar, wide_gains, side_gains, latent_base, here_tile, lead, pixel_rows = ready
    gathered = lax.all_gather(gathered, "dp").reshape(count_dp * count_mp, -1, local)
    latent_near, latent_one, (weight_tile,) = line_sum(
        read_part, latent_base, 2, tile=here_tile
    )
    self_part, *self_kept = self_forward(
        latent_near, wide_gains[0], wide_in, wide_out, images
    )
    latent_near, latent_two, _ = line_sum(self_part, latent_one, 3)
    feed_part, *feed_kept = feed_forward(latent_near, wide_gains[1], wide_in, wide_out)
    latent_three, write_weights = line_scatter(
        feed_part, latent_two, gathered, [d_lat, d_lat, d_if, d_if], 4
    )
    latent_three = latent_three.reshape(own_images, own_latents, d_lat)
    if sharers == 1 and own_images == 1:
        (
            own_grad,
            write_key_grad,
            write_value_grad,
            write_query_grad,
            narrowout_grad,
            gain_write,
            gain_pair,
            own_embed,
            head_grad,
            loss_tile,
        ) = write_stage(
            own_scalar,
            weight_tile,
            latent_three[0],
            own_pieces[0][0],
            own_pieces[1][0],
            own_pieces[2],
            place,
            pixel_rows,
            wide_gains[2],
            side_gains,
            write_weights,
        )
    else:
        (
            own_grad,
            write_key_grad,
            write_value_grad,
            write_query_grad,
            narrowout_grad,
            gain_write,
            gain_outer,
            gain_final,
            own_embed,
            head_grad,
            loss_local,
        ) = write_apart(
            latent_three,
            own_tokens(noisy, 2),
            own_tokens(noise_patches, 2),
            own_tokens(keep_float, 1),
            own_weight,
            weight_tile[0, 0],
            lax.dynamic_slice_in_dim(place, share * own_patches, own_patches, 0),
            copy_pixels,
            wide_gain(3),
            gain_rows,
            write_weights,
            (images, latents, first_image, sharers),
            timesteps,
        )
        gain_write, gain_pair = gain_write[None], jnp.stack([gain_outer, gain_final])
        own_embed, head_grad = (
            jnp.pad(item, ((0, 16 - PIX), (0, 0))) for item in (own_embed, head_grad)
        )
        loss_tile = jnp.full((8, 128), loss_local)
    latent_near, latent_grad, (key_share, query_share) = line_gather(
        own_grad.reshape(-1, d_lat), 5, [write_key_grad, write_query_grad]
    )
    latent_part, up_first, up_last, down_grad, gain_feed = feed_backward(
        latent_near, latent_two, wide_gains[1], wide_in, wide_out, *feed_kept
    )
    latent_near, latent_grad, five_shares = line_sum(
        latent_part, latent_grad, 6, [write_value_grad, narrowout_grad, up_first]
    )
    latent_part, self_first, self_last, gain_self = self_backward(
        latent_near, latent_one, wide_gains[0], wide_in, wide_out, *self_kept
    )
    latent_near, latent_grad, six_shares = line_sum(
        latent_part, latent_grad, 7, [up_last, down_grad, self_first]
    )
    read_wide, read_narrow, latent_total, gain_read, gain_side, side_embed = read_backward(
        read_args[0], *read_args[4:], *read_kept, latent_near, lead
    )
    *gradients, stats = closing(
        [self_last, read_wide, read_narrow],
        [
            latent_total,
            gain_read,
            gain_self,
            gain_feed,
            gain_write,
            gain_side,
            gain_pair,
            side_embed,
            own_embed,
            head_grad,
        ],
        [loss_tile, weight_tile],
        [six_shares[2], five_shares[2], six_shares[0], six_shares[1]],
        [key_share, five_shares[0], query_share, five_shares[1]],
        8,
    )
    states = (
        *(jnp.swapaxes(item, 0, 1) for item in (master_widein, first_widein, second_widein)),
        *(jnp.swapaxes(item, 0, 1) for item in (master_narrowin, first_narrowin, second_narrowin)),
        master_wideout,
        first_wideout,
        second_wideout,
        *(item.T for item in (master_narrowout, first_narrowout, second_narrowout)),
        master_latents,
        first_latents,
        second_latents,
        master_gains,
        first_gains,
        second_gains,
        *(jnp.swapaxes(item, 0, 1) for item in (master_pixels, first_pixels, second_pixels)),
    )
    results = update_states(stats, gradients, states)
    results = [
        jnp.swapaxes(item, 0, 1) if index < 6 or 9 <= index < 12 or index >= 18 else item
        for index, item in enumerate(results)
    ]
    return (stats[0, 1], stats[0, 0], *results)


def solution(mesh):
    in_specs = (
        P("dp", None, None),
        P("dp", None, None),
        P("dp"),
        P("dp", None),
        P(None, None, "mp"),
        P(None, None, "mp"),
        P(None, "mp", None),
        P("mp", None),
        P(),
        P(),
        P(),
        P("dp", None, "mp"),
        P("dp", None, "mp"),
        P("dp", None, "mp"),
        P("dp", None, "mp"),
        P("dp", None, "mp"),
        P("dp", None, "mp"),
        P(None, "mp", "dp"),
        P(None, "mp", "dp"),
        P(None, "mp", "dp"),
        P("mp", "dp"),
        P("mp", "dp"),
        P("mp", "dp"),
        P(None, "dp"),
        P(None, "dp"),
        P(None, "dp"),
        P(None, "dp"),
        P(None, "dp"),
        P(None, "dp"),
        P(None, None, "dp"),
        P(None, None, "dp"),
        P(None, None, "dp"),
    )
    out_specs = (
        P(),
        P(),
        P("dp", None, "mp"),
        P("dp", None, "mp"),
        P("dp", None, "mp"),
        P("dp", None, "mp"),
        P("dp", None, "mp"),
        P("dp", None, "mp"),
        P(None, "mp", "dp"),
        P(None, "mp", "dp"),
        P(None, "mp", "dp"),
        P("mp", "dp"),
        P("mp", "dp"),
        P("mp", "dp"),
        P(None, "dp"),
        P(None, "dp"),
        P(None, "dp"),
        P(None, "dp"),
        P(None, "dp"),
        P(None, "dp"),
        P(None, None, "dp"),
        P(None, None, "dp"),
        P(None, None, "dp"),
    )
    return jax.shard_map(body, mesh=mesh, in_specs=in_specs, out_specs=out_specs, check_vma=False)
```

```python
from functools import partial
import math

import jax
import jax.numpy as jnp
import numpy as np
from jax import lax
from jax.experimental import pallas as pl
from jax.experimental.pallas import tpu as pltpu
from jax.sharding import PartitionSpec as P

HEAD_DIM = 64
PIX = 12
NSTEPS = 1000
STEP = 10


precise = lax.Precision.HIGHEST
clip_level = 0.01
learning_rate = 0.05
weight_decay = 0.1
adam_beta = 0.5
adam_eps = 1e-08


def layer_norm(values, gain):
    centered = values - jnp.mean(values, -1, keepdims=True)
    scale = lax.rsqrt(jnp.mean(centered * centered, -1, keepdims=True) + 1e-05)
    normed = centered * scale
    return (normed * gain, (normed, scale))


def norm_back(upstream, gain, stats):
    normed, scale = stats
    inner = upstream * gain
    values = scale * (
        inner
        - jnp.mean(inner, -1, keepdims=True)
        - normed * jnp.mean(inner * normed, -1, keepdims=True)
    )
    gain_grad = jnp.sum((upstream * normed).reshape(-1, normed.shape[-1]), 0)
    return (values, gain_grad)


def position_table(count, width):
    place = np.arange(count, dtype=np.float64)[:, None]
    angle = place * 10000.0 ** (-2.0 * np.arange(width // 2) / width)
    return jnp.asarray(np.concatenate([np.sin(angle), np.cos(angle)], -1), jnp.float32)


def positions(count, width):
    place = jnp.arange(count, dtype=jnp.float32)[:, None]
    index = jnp.arange(width // 2, dtype=jnp.float32)[None, :]
    angle = place * jnp.exp(-math.log(10000.0) * 2.0 * index / width)
    return jnp.concatenate([jnp.sin(angle), jnp.cos(angle)], -1)


def split_heads(values):
    return values.reshape(values.shape[:-1] + (values.shape[-1] // HEAD_DIM, HEAD_DIM))


def attend_scores(queries, keys, keep_mask):
    scores = jnp.einsum(
        "bqhe,bkhe->bhqk",
        split_heads(queries),
        split_heads(keys),
        preferred_element_type=jnp.float32,
    ) * HEAD_DIM ** (-0.5)
    if keep_mask is not None:
        scores = jnp.where(keep_mask[:, None, None, :] > 0, scores, -1e30)
    return scores


def attend_forward(queries, keys, values, keep_mask):
    scores = attend_scores(queries, keys, keep_mask)
    top = jnp.max(scores, -1, keepdims=True)
    log_total = top + jnp.log(jnp.sum(jnp.exp(scores - top), -1, keepdims=True))
    probs = jnp.exp(scores - log_total).astype(jnp.bfloat16)
    output = jnp.einsum(
        "bhqk,bkhe->bqhe", probs, split_heads(values), preferred_element_type=jnp.float32
    )
    return (output.reshape(queries.shape).astype(jnp.bfloat16), log_total)


def attend_back(queries, keys, values, keep_mask, log_total, upstream):
    scores = attend_scores(queries, keys, keep_mask)
    probs = jnp.exp(scores - log_total)
    value_grad = jnp.einsum(
        "bhqk,bqhe->bkhe",
        probs.astype(jnp.bfloat16),
        split_heads(upstream),
        preferred_element_type=jnp.float32,
    )
    prob_grad = jnp.einsum(
        "bqhe,bkhe->bhqk",
        split_heads(upstream),
        split_heads(values),
        preferred_element_type=jnp.float32,
    )
    score_grad = (probs * (prob_grad - jnp.sum(prob_grad * probs, -1, keepdims=True))).astype(
        jnp.bfloat16
    )
    query_grad = jnp.einsum(
        "bhqk,bkhe->bqhe", score_grad, split_heads(keys), preferred_element_type=jnp.float32
    ) * HEAD_DIM ** (-0.5)
    key_grad = jnp.einsum(
        "bhqk,bqhe->bkhe", score_grad, split_heads(queries), preferred_element_type=jnp.float32
    ) * HEAD_DIM ** (-0.5)
    return (
        query_grad.reshape(queries.shape).astype(jnp.bfloat16),
        key_grad.reshape(keys.shape),
        value_grad.reshape(values.shape),
    )


MESH_ID = pl.DeviceIdType.MESH
HBM_SPEC = pl.BlockSpec(memory_space=pltpu.HBM)
VMEM_SPEC = pl.BlockSpec(memory_space=pltpu.VMEM)
CHUNKS = 32
VMEM_LIMIT = 56 << 20


def in_hbm(values):
    return pltpu.with_memory_space_constraint(values, pltpu.HBM)


def in_vmem(values):
    return pltpu.with_memory_space_constraint(values, pltpu.VMEM)


def remote(source, target, send_sem, recv_sem, device):
    return pltpu.make_async_remote_copy(
        src_ref=source,
        dst_ref=target,
        send_sem=send_sem,
        recv_sem=recv_sem,
        device_id=device,
        device_id_type=MESH_ID,
    )


class PieceSums:
    def __init__(self, count, items, outs, scratch):
        self.count, self.items, self.outs = count, items, outs
        self.bits = count.bit_length() - 1
        self.place = lax.axis_index("dp") if items else None
        self.held = []
        for index in range(len(items)):
            self.held.append(scratch[index * (self.bits + 2) : (index + 1) * (self.bits + 2)])

    @staticmethod
    def scratch(count, shapes):
        bits = count.bit_length() - 1
        result = []
        for rows, width in shapes:
            result.append(pltpu.VMEM((count // 2, rows, width), jnp.float32))
            for phase in range(2, bits + 1):
                result.append(
                    pltpu.VMEM((2 * (count >> phase), rows // 2, width), jnp.float32)
                )
            copies = count // 2 + 2 * sum(count >> phase for phase in range(2, bits + 1))
            result += [pltpu.SemaphoreType.DMA((copies,))] * 2
        return result

    def peers(self):
        return [{"dp": self.place ^ (1 << bit)} for bit in range(self.bits)] if self.items else []

    def order(self, half):
        later = list(range(1, self.bits))
        turn = half * (len(later) // 2)
        return later[turn:] + later[:turn]

    def first_copy(self, index, piece):
        item, held = self.items[index], self.held[index]
        other = 1 - (self.place & 1)
        return remote(
            item.at[2 * piece + other],
            held[0].at[piece],
            held[-2].at[piece],
            held[-1].at[piece],
            {"dp": self.place ^ 1},
        )

    def member(self, half, phase, entry, flip):
        bits = self.order(half)
        settled, now, rest = bits[: phase - 2], bits[phase - 2], bits[phase - 1 :]
        piece = 0
        for bit in settled:
            piece = piece | (self.place & (1 << bit))
        own = self.place & (1 << now)
        piece = piece | ((own ^ (1 << now)) if flip else own)
        for position, bit in enumerate(rest):
            if (entry >> position) & 1:
                piece = piece | (1 << bit)
        return piece >> 1

    def later_copy(self, index, half, phase, entry):
        held = self.held[index]
        rows = self.items[index].shape[1] // 2
        size = self.count >> phase
        sem = self.count // 2 + 2 * sum(self.count >> p for p in range(2, phase)) + half * size + entry
        return remote(
            held[0].at[self.member(half, phase, entry, True), pl.ds(half * rows, rows)],
            held[phase - 1].at[half * size + entry],
            held[-2].at[sem],
            held[-1].at[sem],
            {"dp": self.place ^ (1 << self.order(half)[phase - 2])},
        )

    def entries(self, phase):
        return [
            (index, half, entry)
            for index in range(len(self.items))
            for half in range(2)
            for entry in range(self.count >> phase)
        ]

    def begin(self):
        for index in range(len(self.items)):
            for piece in range(self.count // 2):
                self.first_copy(index, piece).start()

    def send(self, phase):
        for index, half, entry in self.entries(phase):
            self.later_copy(index, half, phase, entry).start()

    def advance(self, phase):
        if not self.items:
            return
        if phase == 1:
            own = self.place & 1
            for index, item in enumerate(self.items):
                total = self.held[index][0]
                for piece in range(self.count // 2):
                    self.first_copy(index, piece).wait_recv()
                    add_rows(total.at[piece], total.at[piece], item.at[2 * piece + own])
        else:
            for index, half, entry in self.entries(phase):
                self.later_copy(index, half, phase, entry).wait_recv()
                held, rows = self.held[index], self.items[index].shape[1] // 2
                where = pl.ds(half * rows, rows)
                came = held[phase - 1].at[half * (self.count >> phase) + entry]
                kept = held[0].at[self.member(half, phase, entry, False), where]
                if phase == self.bits:
                    add_rows(self.outs[index].at[where], kept, came)
                else:
                    add_rows(kept, kept, came)
        if phase < self.bits:
            self.send(phase + 1)

    def finish(self):
        for index in range(len(self.items)):
            for piece in range(self.count // 2):
                self.first_copy(index, piece).wait_send()
        for phase in range(2, self.bits + 1):
            for index, half, entry in self.entries(phase):
                self.later_copy(index, half, phase, entry).wait_send()

    def moments(self, total):
        if not self.items:
            return [(0, total, None)]
        marks, low = [], 0
        for phase in range(1, self.bits + 1):
            share = (1 - 0.5 ** (phase - 1)) / (1 - 0.5 ** (self.bits - 1))
            high = total if phase == self.bits else int(total * (0.22 + 0.78 * share))
            marks.append((low, high, phase))
            low = high
        return marks


def add_rows(target, left, right):
    rows, width = target.shape
    step = math.gcd(rows, max(8, 8192 // width))

    def one(index, carry):
        where = pl.ds(pl.multiple_of(index * step, step), step)
        target[where] = left[where] + right[where]
        return carry

    lax.fori_loop(0, rows // step, one, 0)


class Spread:
    def __init__(self, name, count, held, send_sem, recv_sem):
        self.name, self.count, self.held = name, count, held
        self.send_sem, self.recv_sem = send_sem, recv_sem
        self.place = lax.axis_index(name)

    @staticmethod
    def scratch(count, shape):
        sems = pltpu.SemaphoreType.DMA((count,))
        return [pltpu.VMEM((count,) + shape, jnp.float32), sems, sems]

    def peer(self, step):
        return {self.name: lax.rem(self.place + step, self.count)}

    def copy(self, step, slot):
        return remote(
            self.held.at[slot],
            self.held.at[slot],
            self.send_sem.at[step],
            self.recv_sem.at[slot],
            self.peer(step),
        )

    def each(self, action):
        def one(step, carry):
            action(step)
            return carry

        lax.fori_loop(1, self.count, one, 0)

    def start(self):
        self.each(lambda step: self.copy(step, self.place).start())

    def take(self):
        self.each(lambda step: self.copy(step, lax.rem(self.place + step, self.count)).wait_recv())

    def finish(self):
        self.each(lambda step: self.copy(step, self.place).wait_send())

    def total(self):
        return lax.fori_loop(
            1, self.count, lambda slot, carry: carry + self.held[slot], self.held[0]
        )


class Convert:
    def __init__(self, count_mp, steps, blocks, outs, buffer, sems):
        self.count_mp, self.blocks, self.outs = count_mp, blocks, outs
        self.buffer, self.sems = buffer, sems
        self.number = blocks.shape[0]
        self.each, self.stride = max(1, self.number // steps), max(1, steps // self.number)

    @staticmethod
    def scratch(block):
        return [pltpu.VMEM((3,) + block, jnp.float32), pltpu.SemaphoreType.DMA((3,))]

    def copy(self, index):
        slot = lax.rem(index, 3)
        return pltpu.make_async_copy(
            self.blocks.at[index], self.buffer.at[slot], self.sems.at[slot]
        )

    def begin(self):
        self.copy(0).start()
        self.copy(1).start()

    def one(self, index):
        self.copy(index).wait()

        @pl.when(index + 2 < self.number)
        def _():
            self.copy(index + 2).start()

        block = self.buffer.at[lax.rem(index, 3)]
        local = block.shape[1]
        columns = pl.ds(pl.multiple_of(lax.rem(index, self.count_mp) * local, local), local)
        low = 0
        for out in self.outs:
            rows = out.shape[0] * self.count_mp // self.number
            where = pl.ds(pl.multiple_of(index // self.count_mp * rows, rows), rows)
            out[where, columns] = block[pl.ds(low, rows)].astype(jnp.bfloat16)
            low += rows

    def step(self, index):
        @pl.when(lax.rem(index, self.stride) == 0)
        def _():
            for entry in range(self.each):
                self.one(index // self.stride * self.each + entry)


def signal_all(barrier, others):
    for other in others:
        pl.semaphore_signal(barrier, inc=1, device_id=other, device_id_type=MESH_ID)


class Stage:
    def __init__(self, sources, held, in_sems, results, targets, out_sems):
        self.loads = [
            pltpu.make_async_copy(source, target, in_sems.at[index])
            for index, (source, target) in enumerate(zip(sources, held))
        ]
        self.stores = [
            pltpu.make_async_copy(source, target, out_sems.at[index])
            for index, (source, target) in enumerate(zip(results, targets))
        ]
        self.stored, self.waited = [], []

    def start(self):
        for load in self.loads:
            load.start()

    def wait(self, *indices):
        for index in indices or range(len(self.loads)):
            if index not in self.waited:
                self.loads[index].wait()
                self.waited.append(index)

    def store(self, *indices):
        for index in indices:
            self.stores[index].start()
            self.stored.append(index)

    def finish(self):
        self.store(*(index for index in range(len(self.stores)) if index not in self.stored))
        for store in self.stores:
            store.wait()


def staged_kernel(body, counts, *refs):
    refs = list(refs)

    def pull(number):
        taken = refs[:number]
        del refs[:number]
        return taken

    close, number, raw, close_outs, results = counts
    near, sources, raws = pull(close), pull(number), pull(raw)
    near_outs, targets, echoes = pull(close_outs), pull(results), pull(close_outs)
    held, outs, (in_sems, out_sems) = pull(number), pull(results), pull(2)
    stage = Stage(
        sources, held, in_sems, [*near_outs, *outs], [*echoes, *targets], out_sems
    )
    stage.start()
    body(stage, [*near, *held], raws, [*near_outs, *outs], refs)
    stage.finish()


def staged(
    body, inputs, outs, scratch, flops, raw=(), call_id=None, length=0, near=(), near_outs=()
):
    copies = [pltpu.VMEM(item.shape, item.dtype) for item in (*inputs, *outs)]
    stores = [*outs, *near_outs]
    sems = [pltpu.SemaphoreType.DMA((max(1, len(group)),)) for group in (inputs, stores)]
    needed = sum(
        math.prod(item.shape) * jnp.dtype(item.dtype).itemsize
        for item in copies + list(scratch)
        if getattr(item, "dtype", None) in (jnp.float32, jnp.bfloat16)
    )
    params = {} if call_id is None else {"collective_id": call_id, "has_side_effects": True}
    counts = (len(near), len(inputs), len(raw), len(near_outs), len(outs))
    results = pl.pallas_call(
        partial(staged_kernel, body, counts),
        out_shape=[pltpu.VMEM(item.shape, item.dtype) for item in near_outs]
        + [pltpu.HBM(item.shape, item.dtype) for item in stores],
        in_specs=[VMEM_SPEC] * len(near) + [HBM_SPEC] * (len(inputs) + len(raw)),
        out_specs=[VMEM_SPEC] * len(near_outs) + [HBM_SPEC] * len(stores),
        scratch_shapes=copies + sems + list(scratch),
        compiler_params=pltpu.CompilerParams(vmem_limit_bytes=needed + (6 << 20), **params),
        cost_estimate=pl.CostEstimate(
            flops=flops, bytes_accessed=length * 3_500_000, transcendentals=0
        ),
    )(*map(in_vmem, near), *map(in_hbm, (*inputs, *raw)))
    return list(results)


def greet(place, count, others=()):
    barrier = pltpu.get_barrier_semaphore()
    below, above = {"mp": place - 1}, {"mp": place + 1}

    @pl.when(place > 0)
    def _():
        pl.semaphore_signal(barrier, inc=1, device_id=below, device_id_type=MESH_ID)

    @pl.when(place < count - 1)
    def _():
        pl.semaphore_signal(barrier, inc=1, device_id=above, device_id_type=MESH_ID)

    signal_all(barrier, others)
    inside = jnp.logical_and(place > 0, place < count - 1)

    @pl.when(inside)
    def _():
        pl.semaphore_wait(barrier, 2 + len(others))

    @pl.when(jnp.logical_not(inside))
    def _():
        pl.semaphore_wait(barrier, 1 + len(others))


def views(refs, base=3):
    result = []
    for ref in refs:
        if len(ref.shape) == base:
            result.append(ref)
        else:
            result += [ref.at[slot] for slot in range(ref.shape[0])]
    return result


def line_sum_kernel(count, count_dp, extra, tiled, stage, held, raws, results, scratch):
    refs = list(scratch)

    def pull(number):
        taken = refs[:number]
        del refs[:number]
        return taken

    part_ref, base_ref, tile = held[0], held[1], held[2 + extra :]
    items, outs = views(held[2 : 2 + extra]), views(results[1 : 1 + extra], 2)
    out_ref, tile_out = results[0], results[1 + extra : 1 + extra + tiled]
    base_rows = base_ref.shape[0]
    inner, from_away, from_toward, toward_send, away_send, away_recv, toward_recv = pull(7)
    chunks = toward_send.shape[0]
    spread = Spread("dp", count_dp, *pull(3)) if tiled else None
    turn = pull(1)[0] if tiled else None
    sums = PieceSums(count_dp, items, outs, refs)
    place = lax.axis_index("mp")
    half = count // 2
    low_side = place < half
    toward = {"mp": jnp.where(low_side, place + 1, place - 1)}
    away = {"mp": jnp.where(low_side, place - 1, place + 1)}
    middle = jnp.logical_or(place == half - 1, place == half)
    outermost = jnp.logical_or(place == 0, place == count - 1)
    rows = part_ref.shape[0] // chunks
    others = [spread.peer(step) for step in range(1, count_dp)] if tiled else sums.peers()
    greet(place, count, others)

    def window(step):
        return pl.ds(pl.multiple_of(step * rows, rows), rows)

    def put(step, total):
        first = lax.rem(step * rows, base_rows)
        out_ref[window(step)] = total + base_ref[pl.ds(pl.multiple_of(first, rows), rows)]

    def push(step, source, inside):
        target = from_toward if inside else from_away
        recv = toward_recv if inside else away_recv
        return remote(
            source.at[window(step)],
            target.at[window(step)],
            toward_send.at[step],
            recv.at[step],
            toward,
        )

    def back(step, source):
        return remote(
            source.at[window(step)],
            from_toward.at[window(step)],
            away_send.at[step],
            toward_recv.at[step],
            away,
        )

    def gather_in(step):
        push(step, part_ref, False).wait_recv()
        inner[window(step)] = part_ref[window(step)] + from_away[window(step)]

    odd = lax.rem(lax.axis_index("dp"), 2) == 1
    if tiled:
        stage.wait()
        spread.held[spread.place] = tile[0][...]
        spread.start()

        @pl.when(jnp.logical_and(outermost, odd))
        def _():
            pl.semaphore_wait(turn, 1)

    def pass_turn():
        if tiled:

            @pl.when(jnp.logical_not(odd))
            def _():
                pl.semaphore_signal(
                    turn, inc=1, device_id=spread.peer(1), device_id_type=MESH_ID
                )

    @pl.when(outermost)
    def _():
        def leave(step, carry):
            push(step, part_ref, False).start()
            return carry

        lax.fori_loop(0, chunks, leave, 0)

    stage.wait()
    sums.begin()

    @pl.when(outermost)
    def _():

        def arrive(step, carry):
            push(step, part_ref, True).wait_recv()
            put(step, from_toward[window(step)])
            push(step, part_ref, False).wait_send()
            return carry

        if tiled:
            early = chunks // 4
            lax.fori_loop(0, early, arrive, 0)
            pass_turn()
            lax.fori_loop(early, chunks, arrive, 0)
        else:
            for low, high, phase in sums.moments(chunks):
                lax.fori_loop(low, high, arrive, 0)
                sums.advance(phase)

    lag = 2

    @pl.when(middle)
    def _():
        def finish(step):
            push(step, inner, True).wait_recv()
            total = inner[window(step)] + from_toward[window(step)]
            from_away[window(step)] = total
            back(step, from_away).start()
            put(step, total)

        def first(step, carry):
            gather_in(step)
            push(step, inner, True).start()
            return carry

        def both(step, carry):
            first(step, carry)
            finish(step - lag)
            return carry

        def last(step, carry):
            finish(step)
            return carry

        def drain(step, carry):
            push(step, inner, True).wait_send()
            back(step, from_away).wait_send()
            return carry

        lax.fori_loop(0, lag, first, 0)
        for low, high, phase in sums.moments(chunks):
            lax.fori_loop(max(low, lag), high, both, 0)
            if high == chunks:
                lax.fori_loop(chunks - lag, chunks, last, 0)
            sums.advance(phase)
        lax.fori_loop(0, chunks, drain, 0)

    if count > 4:

        @pl.when(jnp.logical_not(jnp.logical_or(middle, outermost)))
        def _():
            def inwards(step, carry):
                gather_in(step)
                push(step, inner, False).start()
                return carry

            def outwards(step, carry):
                push(step, inner, True).wait_recv()
                back(step, from_toward).start()
                put(step, from_toward[window(step)])
                return carry

            def drain(step, carry):
                push(step, inner, False).wait_send()
                back(step, from_toward).wait_send()
                return carry

            lax.fori_loop(0, chunks, inwards, 0)
            for low, high, phase in sums.moments(chunks):
                lax.fori_loop(low, high, outwards, 0)
                sums.advance(phase)
            lax.fori_loop(0, chunks, drain, 0)

    sums.finish()
    if tiled:
        spread.take()
        tile_out[0][...] = spread.total()
        spread.finish()


def piece_shapes(items):
    count = lax.axis_size("dp")
    items = [item.reshape(item.shape[:-2] + (count, -1, item.shape[-1])) for item in items]
    shapes, shares = [], []
    for item in items:
        shapes += [item.shape[-2:]] * (item.shape[0] if item.ndim == 4 else 1)
        shares.append(jax.ShapeDtypeStruct(item.shape[:-3] + item.shape[-2:], jnp.float32))
    return items, shapes, shares


def line_sum(part, base, call_id, items=(), tile=None):
    items, shapes, shares = piece_shapes(items)
    count, count_dp = lax.axis_size("mp"), lax.axis_size("dp")
    rows, width = part.shape
    buffer = pltpu.VMEM((rows, width), jnp.float32)
    sems = pltpu.SemaphoreType.DMA((CHUNKS,))
    inputs = [base, *items]
    outs = list(shares)
    scratch = [buffer] * 3 + [sems] * 4
    if tile is not None:
        inputs.append(tile)
        outs.append(jax.ShapeDtypeStruct(tile.shape, jnp.float32))
        scratch += Spread.scratch(count_dp, tile.shape) + [pltpu.SemaphoreType.REGULAR]
    scratch += PieceSums.scratch(count_dp, shapes)
    total = jax.ShapeDtypeStruct((rows, width), jnp.float32)
    results = staged(
        partial(line_sum_kernel, count, count_dp, len(items), int(tile is not None)),
        inputs,
        outs,
        scratch,
        4 * rows * width,
        call_id=call_id,
        length=55,
        near=[part],
        near_outs=[total],
    )
    return results[0], results[-1], results[1:-1]


class LineScatter:
    def __init__(self, count, part, out, buffers, sems):
        self.count, self.part, self.out = count, part, out
        self.up_acc, self.down_acc, self.from_below, self.from_above = buffers
        self.up_send, self.down_send, self.up_recv, self.down_recv = sems
        self.place = lax.axis_index("mp")
        self.steps = self.up_send.shape[1]
        self.block = part.shape[0] // count
        self.rows = self.block // self.steps

    @staticmethod
    def scratch(count, shape, steps):
        sems = pltpu.SemaphoreType.DMA((count, steps))
        return [pltpu.VMEM(shape, jnp.float32)] * 4 + [sems] * 4

    def window(self, owner, step):
        return pl.ds(pl.multiple_of(owner * self.block + step * self.rows, self.rows), self.rows)

    def up(self, owner, step, source):
        where = self.window(owner, step)
        return remote(
            source.at[where],
            self.from_below.at[where],
            self.up_send.at[owner, step],
            self.up_recv.at[owner, step],
            {"mp": self.place + 1},
        )

    def down(self, owner, step, source):
        where = self.window(owner, step)
        return remote(
            source.at[where],
            self.from_above.at[where],
            self.down_send.at[owner, step],
            self.down_recv.at[owner, step],
            {"mp": self.place - 1},
        )

    def up_turn(self, index):
        place, part = self.place, self.part
        owner, step = self.count - 1 - index // self.steps, lax.rem(index, self.steps)

        @pl.when(jnp.logical_and(owner > place, place == 0))
        def _():
            self.up(owner, step, part).start()

        @pl.when(jnp.logical_and(owner > place, place > 0))
        def _():
            self.up(owner, step, part).wait_recv()
            where = self.window(owner, step)
            self.up_acc[where] = part[where] + self.from_below[where]
            self.up(owner, step, self.up_acc).start()

    def down_turn(self, index):
        place, part, count = self.place, self.part, self.count
        owner, step = index // self.steps, lax.rem(index, self.steps)

        @pl.when(jnp.logical_and(owner < place, place == count - 1))
        def _():
            self.down(owner, step, part).start()

        @pl.when(jnp.logical_and(owner < place, place < count - 1))
        def _():
            self.down(owner, step, part).wait_recv()
            where = self.window(owner, step)
            self.down_acc[where] = part[where] + self.from_above[where]
            self.down(owner, step, self.down_acc).start()

    def run(self, pause=None, beside=None):
        turns, lag = self.count * self.steps, self.steps

        def staggered(first, second):
            def begin(index, carry):
                first(index)
                if beside is not None:
                    beside(index)
                return carry

            def both(index, carry):
                first(index)
                second(index - lag)
                if beside is not None:
                    beside(index)
                return carry

            def end(index, carry):
                second(index)
                return carry

            lax.fori_loop(0, lag, begin, 0)
            if pause is not None:
                pause()
            lax.fori_loop(lag, turns, both, 0)
            lax.fori_loop(turns - lag, turns, end, 0)

        @pl.when(self.place < self.count // 2)
        def _():
            staggered(self.up_turn, self.down_turn)

        @pl.when(self.place >= self.count // 2)
        def _():
            staggered(self.down_turn, self.up_turn)

    def settle(self):
        place, rows = self.place, self.rows

        def one(step, carry):
            where = self.window(place, step)
            mine = pl.ds(pl.multiple_of(step * rows, rows), rows)
            self.out[mine] = self.part[where]

            @pl.when(place > 0)
            def _():
                self.up(place, step, self.part).wait_recv()
                self.out[mine] += self.from_below[where]

            @pl.when(place < self.count - 1)
            def _():
                self.down(place, step, self.part).wait_recv()
                self.out[mine] += self.from_above[where]

            return carry

        lax.fori_loop(0, self.steps, one, 0)

    def finish(self):
        place = self.place

        def one(index, carry):
            owner, step = index // self.steps, lax.rem(index, self.steps)

            @pl.when(owner > place)
            def _():
                self.up(owner, step, self.part).wait_send()

            @pl.when(owner < place)
            def _():
                self.down(owner, step, self.part).wait_send()

            return carry

        lax.fori_loop(0, self.count * self.steps, one, 0)


def line_scatter_kernel(count, stage, held, raws, results, scratch):
    own, sem = scratch[8:10]
    base, blocks = raws
    scatter = LineScatter(count, held[0], results[0], scratch[:4], scratch[4:8])
    convert = Convert(
        count, count * scatter.steps, blocks, results[1:], scratch[10], scratch[11]
    )
    rows = own.shape[0]
    load = pltpu.make_async_copy(
        base.at[pl.ds(pl.multiple_of(scatter.place * rows, rows), rows)], own, sem
    )
    load.start()
    convert.begin()
    greet(scatter.place, count)
    scatter.run(None, convert.step)
    stage.store(1, 2, 3, 4)
    scatter.settle()
    load.wait()
    results[0][...] += own[...]
    scatter.finish()


def line_scatter(part, base, blocks, sizes, call_id):
    rows, width = part.shape
    count = lax.axis_size("mp")
    own = (rows // count, width)
    result, *weights = staged(
        partial(line_scatter_kernel, count),
        [],
        [jax.ShapeDtypeStruct(own, jnp.float32)]
        + [jax.ShapeDtypeStruct((size, count * blocks.shape[2]), jnp.bfloat16) for size in sizes],
        LineScatter.scratch(count, (rows, width), 8)
        + [pltpu.VMEM(own, jnp.float32), pltpu.SemaphoreType.DMA]
        + Convert.scratch(blocks.shape[1:]),
        2 * rows * width,
        [base, blocks],
        call_id=call_id,
        length=33,
        near=[part],
    )
    return result, weights


def line_gather_kernel(count, count_dp, extra, stage, held, raws, results, scratch):
    own_ref, out_ref = held[0], results[0]
    items, outs = views(held[1:]), views(results[1:], 2)
    up_send, down_send, up_recv, down_recv = scratch[:4]
    sums = PieceSums(count_dp, items, outs, scratch[4:])
    place = lax.axis_index("mp")
    steps = up_send.shape[1]
    block = own_ref.shape[0]
    rows = block // steps
    below, above = {"mp": place - 1}, {"mp": place + 1}
    greet(place, count, sums.peers())
    stage.wait(0)

    def window(owner, step):
        return pl.ds(pl.multiple_of(owner * block + step * rows, rows), rows)

    def up(owner, step):
        part = out_ref.at[window(owner, step)]
        return remote(part, part, up_send.at[owner, step], up_recv.at[owner, step], above)

    def down(owner, step):
        part = out_ref.at[window(owner, step)]
        return remote(part, part, down_send.at[owner, step], down_recv.at[owner, step], below)

    def begin(step, carry):
        out_ref[window(place, step)] = own_ref[pl.ds(pl.multiple_of(step * rows, rows), rows)]

        @pl.when(place < count - 1)
        def _():
            up(place, step).start()

        @pl.when(place > 0)
        def _():
            down(place, step).start()

        return carry

    lax.fori_loop(0, steps, begin, 0)
    stage.wait(*range(1, len(stage.loads)))
    sums.begin()

    def pass_on(index, carry):
        away, step = 1 + index // steps, lax.rem(index, steps)

        @pl.when(place - away >= 0)
        def _():
            up(place - away, step).wait_recv()

        @pl.when(jnp.logical_and(place - away >= 0, place < count - 1))
        def _():
            up(place - away, step).start()

        @pl.when(place + away < count)
        def _():
            down(place + away, step).wait_recv()

        @pl.when(jnp.logical_and(place + away < count, place > 0))
        def _():
            down(place + away, step).start()

        return carry

    for low, high, phase in sums.moments((count - 1) * steps):
        lax.fori_loop(low, high, pass_on, 0)
        sums.advance(phase)

    def drain(index, carry):
        owner, step = index // steps, lax.rem(index, steps)

        @pl.when(jnp.logical_and(owner <= place, place < count - 1))
        def _():
            up(owner, step).wait_send()

        @pl.when(jnp.logical_and(owner >= place, place > 0))
        def _():
            down(owner, step).wait_send()

        return carry

    lax.fori_loop(0, count * steps, drain, 0)
    sums.finish()


def line_gather(own, call_id, items=()):
    rows, width = own.shape
    count, count_dp = lax.axis_size("mp"), lax.axis_size("dp")
    sems = pltpu.SemaphoreType.DMA((count, 8))
    items, shapes, shares = piece_shapes(items)
    results = staged(
        partial(line_gather_kernel, count, count_dp, len(items)),
        [own, *items],
        shares,
        [sems] * 4 + PieceSums.scratch(count_dp, shapes),
        rows * width,
        call_id=call_id,
        length=38,
        near_outs=[jax.ShapeDtypeStruct((rows * count, width), jnp.float32)],
    )
    return results[0], results[-1], results[1:-1]


def dot(left, right, left_dim=1, right_dim=0):
    return lax.dot_general(
        left, right, (((left_dim,), (right_dim,)), ((), ())), preferred_element_type=jnp.float32
    )


def head_mask(width, copies):
    lane = lax.broadcasted_iota(jnp.int32, (1, width), 1)
    return [lane // HEAD_DIM == head for head in range(copies)]


def spread_heads(values):
    masks = head_mask(values.shape[1], values.shape[1] // HEAD_DIM)
    return jnp.concatenate([jnp.where(mask, values, jnp.zeros_like(values)) for mask in masks], 0)


def join_heads(values, heads):
    rows = values.shape[0] // heads
    masks = head_mask(values.shape[1], heads)
    return sum(
        jnp.where(mask, values[head * rows : (head + 1) * rows], 0.0)
        for head, mask in enumerate(masks)
    )


def split_three(values):
    first = values.astype(jnp.bfloat16)
    left = values - first.astype(jnp.float32)
    second = left.astype(jnp.bfloat16)
    third = (left - second.astype(jnp.float32)).astype(jnp.bfloat16)
    return first, second, third


def norm_rows(values):
    centered = values - jnp.mean(values, -1, keepdims=True)
    scale = lax.rsqrt(jnp.mean(centered * centered, -1, keepdims=True) + 1e-05)
    return centered * scale, scale


def norm_rows_back(upstream, gain, normed, scale):
    inner = upstream * gain
    return scale * (
        inner
        - jnp.mean(inner, -1, keepdims=True)
        - normed * jnp.mean(inner * normed, -1, keepdims=True)
    )


def embed(noisy, pixels, place):
    stacked = jnp.concatenate(split_three(noisy), 0)
    return dot(stacked, jnp.concatenate([pixels] * 3, 0), 0, 0) + place


def read_forward_kernel(
    noisy_ref,
    keep_ref,
    place_ref,
    pixels_ref,
    latents_ref,
    wide_gain_ref,
    gain_ref,
    query_weight_ref,
    pair_weight_ref,
    out_weight_ref,
    part_ref,
    pairs_ref,
    output_ref,
    queries_ref,
    normed_ref,
    scale_ref,
    side_ref,
    probs_ref,
):
    heads = query_weight_ref.shape[2] // HEAD_DIM

    @pl.when(pl.program_id(0) == 0)
    def _():
        normed, _ = norm_rows(latents_ref[...].astype(jnp.float32))
        low = (normed * wide_gain_ref[...]).astype(jnp.bfloat16)
        queries = dot(low, query_weight_ref[0]).astype(jnp.bfloat16)
        queries_ref[...] = spread_heads(queries * jnp.bfloat16(HEAD_DIM ** (-0.5)))

    normed, scale = norm_rows(embed(noisy_ref[0], pixels_ref[...], place_ref[...]))
    normed_ref[0] = normed
    scale_ref[0] = scale
    side = (normed * gain_ref[...]).astype(jnp.bfloat16)
    side_ref[0] = side.T
    keys = dot(side, pair_weight_ref[0]).astype(jnp.bfloat16)
    values = dot(side, pair_weight_ref[1]).astype(jnp.bfloat16)
    pairs_ref[0, 0] = keys
    pairs_ref[0, 1] = values
    scores = dot(keys, queries_ref[...], 1, 1)
    scores = jnp.where(keep_ref[0] > 0, scores, -1e30)
    top = jnp.max(scores, 0, keepdims=True)
    grown = jnp.exp(scores - top)
    probs = grown / jnp.sum(grown, 0, keepdims=True)
    probs_ref[0] = probs
    output = join_heads(dot(probs.astype(jnp.bfloat16), values, 0, 0), heads)
    output = output.astype(jnp.bfloat16)
    output_ref[0] = output
    part_ref[...] = dot(output, out_weight_ref[0])


def whole(shape):
    return pl.BlockSpec(shape, lambda b: (0,) * len(shape))


def each(shape):
    return pl.BlockSpec((1,) + shape, lambda b: (b,) + (0,) * len(shape))


def slot_of(shape, slot):
    return pl.BlockSpec(shape, lambda b: (slot,) + (0,) * (len(shape) - 1))


def read_forward(noisy, keep, place, pixels, latents, wide_gain, gain, wide, narrow, wideout):
    images, _, patches = noisy.shape
    count, d_lat = latents.shape
    d_if, local = narrow.shape[1:]
    stacked = local // HEAD_DIM * count
    return pl.pallas_call(
        read_forward_kernel,
        grid=(images,),
        out_shape=[
            pltpu.VMEM((images * count, d_lat), jnp.float32),
            pltpu.HBM((images, 2, patches, local), jnp.bfloat16),
            pltpu.HBM((images, count, local), jnp.bfloat16),
            pltpu.HBM((stacked, local), jnp.bfloat16),
            pltpu.HBM((images, patches, d_if), jnp.float32),
            pltpu.HBM((images, patches, 1), jnp.float32),
            pltpu.HBM((images, d_if, patches), jnp.bfloat16),
            pltpu.HBM((images, patches, stacked), jnp.float32),
        ],
        in_specs=[
            each(noisy.shape[1:]),
            each((patches, 1)),
            whole((patches, d_if)),
            whole(pixels.shape),
            whole(latents.shape),
            whole((1, d_lat)),
            whole((1, d_if)),
            slot_of((1, d_lat, local), 0),
            slot_of((2, d_if, local), 0),
            slot_of((1, local, d_lat), 0),
        ],
        out_specs=[
            pl.BlockSpec((count, d_lat), lambda b: (b, 0)),
            each((2, patches, local)),
            each((count, local)),
            whole((stacked, local)),
            each((patches, d_if)),
            each((patches, 1)),
            each((d_if, patches)),
            each((patches, stacked)),
        ],
        compiler_params=pltpu.CompilerParams(vmem_limit_bytes=52 << 20),
        cost_estimate=pl.CostEstimate(
            flops=10**10, bytes_accessed=30 * 10**6, transcendentals=2 * 10**6
        ),
    )(in_hbm(noisy), in_hbm(keep), in_hbm(place), in_hbm(pixels), in_hbm(latents), in_hbm(wide_gain), in_hbm(gain), in_hbm(wide), in_hbm(narrow), in_hbm(wideout))


def read_backward_kernel(
    noisy_ref,
    latents_ref,
    wide_gain_ref,
    gain_ref,
    query_weight_ref,
    pair_weight_ref,
    out_weight_ref,
    pairs_ref,
    output_ref,
    queries_ref,
    normed_ref,
    scale_ref,
    side_ref,
    probs_ref,
    grad_ref,
    lead_ref,
    wide_grad_ref,
    narrow_grad_ref,
    latents_grad_ref,
    wide_gain_grad_ref,
    gain_grad_ref,
    embed_grad_ref,
    low_ref,
    returned_ref,
    pair_ref,
):
    step, steps = pl.program_id(0), pl.num_programs(0)
    heads = query_weight_ref.shape[2] // HEAD_DIM

    @pl.when(step == 0)
    def _():
        normed, _ = norm_rows(latents_ref[...].astype(jnp.float32))
        low_ref[...] = (normed * wide_gain_ref[...]).astype(jnp.bfloat16)
        pair_ref[...] = jnp.concatenate([pair_weight_ref[0], pair_weight_ref[1]], 1)
        for ref in (
            wide_grad_ref,
            narrow_grad_ref,
            latents_grad_ref,
            gain_grad_ref,
            embed_grad_ref,
            returned_ref,
        ):
            ref[...] = jnp.zeros_like(ref)

    normed, scale, side, probs = normed_ref[0], scale_ref[0], side_ref[0], probs_ref[0]
    keys, values, queries = pairs_ref[0, 0], pairs_ref[0, 1], queries_ref[...]
    branch = grad_ref[...].astype(jnp.bfloat16)
    latents_grad_ref[...] += lead_ref[...] * grad_ref[...]
    wide_grad_ref[1] += dot(branch, output_ref[0], 0, 0)
    upstream = spread_heads(dot(branch, out_weight_ref[0], 1, 1).astype(jnp.bfloat16))
    value_grad = dot(probs.astype(jnp.bfloat16), upstream).astype(jnp.bfloat16)
    prob_grad = dot(values, upstream, 1, 1)
    inner = jnp.sum(prob_grad * probs, 0, keepdims=True)
    score_grad = (probs * (prob_grad - inner)).astype(jnp.bfloat16)
    key_grad = dot(score_grad, queries).astype(jnp.bfloat16)
    query_grad = join_heads(dot(score_grad, keys, 0, 0), heads) * HEAD_DIM ** (-0.5)
    query_grad = query_grad.astype(jnp.bfloat16)
    wide_grad_ref[0] += dot(low_ref[...], query_grad, 0, 0)
    returned_ref[...] += dot(query_grad, query_weight_ref[0], 1, 1)
    pair_grad = jnp.concatenate([key_grad, value_grad], 1)
    narrow_grad = dot(side, pair_grad)
    narrow_grad_ref[0] += narrow_grad[:, : keys.shape[1]]
    narrow_grad_ref[1] += narrow_grad[:, keys.shape[1] :]
    side_grad = dot(pair_grad, pair_ref[...], 1, 1)
    gain_grad_ref[...] += jnp.sum(side_grad * normed, 0, keepdims=True)
    back = norm_rows_back(side_grad, gain_ref[...], normed, scale)
    embed_grad_ref[...] += embed_back(noisy_ref[0], back)

    @pl.when(step == steps - 1)
    def _():
        normed, scale = norm_rows(latents_ref[...].astype(jnp.float32))
        returned = returned_ref[...]
        wide_gain_grad_ref[...] = jnp.sum(returned * normed, 0, keepdims=True)
        latents_grad_ref[...] += norm_rows_back(returned, wide_gain_ref[...], normed, scale)


def embed_back(noisy, back):
    first, second, _ = split_three(noisy)
    high = back.astype(jnp.bfloat16)
    low = (back - high.astype(jnp.float32)).astype(jnp.bfloat16)
    rows = noisy.shape[0]
    both = dot(jnp.concatenate([first, second], 0), high)
    return both[:rows] + both[rows:] + dot(first, low)


def read_backward(
    noisy,
    latents,
    wide_gain,
    gain,
    wide,
    narrow,
    wideout,
    pairs,
    output,
    queries,
    normed,
    scale,
    side,
    probs,
    grad,
    lead,
):
    images, rows, patches = noisy.shape
    count, d_lat = latents.shape
    d_if, local = narrow.shape[1:]
    stacked = local // HEAD_DIM * count
    results = [
        (2, d_lat, local),
        (2, d_if, local),
        (count, d_lat),
        (1, d_lat),
        (1, d_if),
        (rows, d_if),
    ]
    return pl.pallas_call(
        read_backward_kernel,
        grid=(images,),
        out_shape=[pltpu.HBM(shape, jnp.float32) for shape in results],
        in_specs=[
            each(noisy.shape[1:]),
            whole(latents.shape),
            whole((1, d_lat)),
            whole((1, d_if)),
            slot_of((1, d_lat, local), 0),
            slot_of((2, d_if, local), 0),
            slot_of((1, local, d_lat), 0),
            each((2, patches, local)),
            each((count, local)),
            whole((stacked, local)),
            each((patches, d_if)),
            each((patches, 1)),
            each((d_if, patches)),
            each((patches, stacked)),
            pl.BlockSpec((count, d_lat), lambda b: (b, 0)),
            whole((1, 1)),
        ],
        out_specs=[whole(shape) for shape in results],
        scratch_shapes=[
            pltpu.VMEM((count, d_lat), jnp.bfloat16),
            pltpu.VMEM((count, d_lat), jnp.float32),
            pltpu.VMEM((d_if, 2 * local), jnp.bfloat16),
        ],
        compiler_params=pltpu.CompilerParams(vmem_limit_bytes=52 << 20),
        cost_estimate=pl.CostEstimate(
            flops=2 * 10**10, bytes_accessed=30 * 10**6, transcendentals=2 * 10**6
        ),
    )(*map(in_hbm, (noisy, latents, wide_gain, gain, wide, narrow, wideout, pairs, output, queries, normed, scale, side, probs)), in_vmem(grad), in_hbm(lead))


def rows_of(rows, width):
    return pl.BlockSpec((rows, width), lambda b: (b, 0))


def attend_few(keys, values, queries):
    scores = dot(keys, queries, 1, 1)
    top = jnp.max(scores, 0, keepdims=True)
    grown = jnp.exp(scores - top)
    summed = jnp.sum(grown, 0, keepdims=True)
    probs = (grown / summed).astype(jnp.bfloat16)
    return dot(probs, values, 0, 0), top + jnp.log(summed)


def scaled_heads(queries):
    return spread_heads(queries * jnp.bfloat16(HEAD_DIM ** (-0.5)))


def self_forward_kernel(
    latent_ref, gain_ref, q_ref, k_ref, v_ref, out_weight_ref, part_ref, triple_ref, output_ref, total_ref, low_ref
):
    heads = q_ref.shape[2] // HEAD_DIM
    normed, _ = norm_rows(latent_ref[...])
    low = (normed * gain_ref[...]).astype(jnp.bfloat16)
    low_ref[...] = low
    queries, keys, values = (dot(low, ref[0]).astype(jnp.bfloat16) for ref in (q_ref, k_ref, v_ref))
    for index, item in enumerate((queries, keys, values)):
        triple_ref[0, index] = item
    output, total_ref[0] = attend_few(keys, values, scaled_heads(queries))
    output = join_heads(output, heads).astype(jnp.bfloat16)
    output_ref[0] = output
    part_ref[...] = dot(output, out_weight_ref[0])


def self_forward(latent, gain, wide, wideout, images):
    total, d_lat = latent.shape
    count, local = total // images, wide.shape[2]
    stacked = local // HEAD_DIM * count
    return pl.pallas_call(
        self_forward_kernel,
        grid=(images,),
        out_shape=[
            pltpu.VMEM((total, d_lat), jnp.float32),
            pltpu.HBM((images, 3, count, local), jnp.bfloat16),
            pltpu.HBM((images, count, local), jnp.bfloat16),
            pltpu.HBM((images, 1, stacked), jnp.float32),
            pltpu.HBM((total, d_lat), jnp.bfloat16),
        ],
        in_specs=[rows_of(count, d_lat), whole((1, d_lat))]
        + [slot_of((1, d_lat, local), slot) for slot in (1, 2, 3)]
        + [slot_of((1, local, d_lat), 1)],
        out_specs=[
            rows_of(count, d_lat),
            each((3, count, local)),
            each((count, local)),
            each((1, stacked)),
            rows_of(count, d_lat),
        ],
        compiler_params=pltpu.CompilerParams(vmem_limit_bytes=20 << 20),
        cost_estimate=pl.CostEstimate(
            flops=3 * 10**9, bytes_accessed=12 * 10**6, transcendentals=3 * 10**5
        ),
    )(in_vmem(latent), in_hbm(gain), in_hbm(wide), in_hbm(wide), in_hbm(wide), in_hbm(wideout))


def self_backward_kernel(
    grad_ref,
    latent_ref,
    gain_ref,
    q_ref,
    k_ref,
    v_ref,
    out_weight_ref,
    triple_ref,
    output_ref,
    total_ref,
    low_ref,
    part_ref,
    first_ref,
    last_ref,
    gain_grad_ref,
    branches,
    outputs,
    grads,
    lows,
):
    step, steps = pl.program_id(0), pl.num_programs(0)
    heads = q_ref.shape[2] // HEAD_DIM
    count = grad_ref.shape[0]
    mine = pl.ds(pl.multiple_of(step * count, count), count)
    normed, scale = norm_rows(latent_ref[...])
    branch = grad_ref[...].astype(jnp.bfloat16)
    branches[mine] = branch
    outputs[mine] = output_ref[0]
    lows[mine] = low_ref[...]
    upstream = spread_heads(dot(branch, out_weight_ref[0], 1, 1).astype(jnp.bfloat16))
    keys, values = triple_ref[0, 1], triple_ref[0, 2]
    queries = scaled_heads(triple_ref[0, 0])
    probs = jnp.exp(dot(keys, queries, 1, 1) - total_ref[0])
    value_grad = dot(probs.astype(jnp.bfloat16), upstream).astype(jnp.bfloat16)
    prob_grad = dot(values, upstream, 1, 1)
    inner = jnp.sum(prob_grad * probs, 0, keepdims=True)
    score_grad = (probs * (prob_grad - inner)).astype(jnp.bfloat16)
    key_grad = dot(score_grad, queries).astype(jnp.bfloat16)
    query_grad = join_heads(dot(score_grad, keys, 0, 0), heads) * HEAD_DIM ** (-0.5)
    query_grad = query_grad.astype(jnp.bfloat16)
    part = (
        dot(query_grad, q_ref[0], 1, 1)
        + dot(key_grad, k_ref[0], 1, 1)
        + dot(value_grad, v_ref[0], 1, 1)
    )
    for index, item in enumerate((query_grad, key_grad, value_grad)):
        grads[index, mine] = item
    gain_part = jnp.sum(part * normed, 0, keepdims=True)
    gain_grad_ref[...] = gain_part + jnp.where(step == 0, 0.0, gain_grad_ref[...])
    part_ref[...] = norm_rows_back(part, gain_ref[...], normed, scale)

    @pl.when(step == steps - 1)
    def _():
        turned = lows[...].T
        first_ref[0] = dot(turned, grads[0])
        first_ref[1] = dot(turned, grads[1])
        last_ref[0] = dot(turned, grads[2])
        last_ref[1] = dot(branches[...], outputs[...], 0, 0)


def self_backward(grad, latent, gain, wide, wideout, triple, output, total, low):
    rows, d_lat = latent.shape
    images, _, count, local = triple.shape
    stacked = local // HEAD_DIM * count
    weight = pltpu.HBM((2, d_lat, local), jnp.float32)
    return pl.pallas_call(
        self_backward_kernel,
        grid=(images,),
        out_shape=[pltpu.VMEM((rows, d_lat), jnp.float32)]
        + [weight] * 2
        + [pltpu.HBM((1, d_lat), jnp.float32)],
        in_specs=[rows_of(count, d_lat), rows_of(count, d_lat), whole((1, d_lat))]
        + [slot_of((1, d_lat, local), slot) for slot in (1, 2, 3)]
        + [
            slot_of((1, local, d_lat), 1),
            each((3, count, local)),
            each((count, local)),
            each((1, stacked)),
            rows_of(count, d_lat),
        ],
        out_specs=[rows_of(count, d_lat)] + [whole((2, d_lat, local))] * 2 + [whole((1, d_lat))],
        scratch_shapes=[
            pltpu.VMEM((rows, d_lat), jnp.bfloat16),
            pltpu.VMEM((rows, local), jnp.bfloat16),
            pltpu.VMEM((3, rows, local), jnp.bfloat16),
            pltpu.VMEM((rows, d_lat), jnp.bfloat16),
        ],
        compiler_params=pltpu.CompilerParams(vmem_limit_bytes=28 << 20),
        cost_estimate=pl.CostEstimate(
            flops=6 * 10**9, bytes_accessed=16 * 10**6, transcendentals=3 * 10**5
        ),
    )(in_vmem(grad), in_hbm(latent), in_hbm(gain), in_hbm(wide), in_hbm(wide), in_hbm(wide), in_hbm(wideout), in_hbm(triple), in_hbm(output), in_hbm(total), in_hbm(low))


def feed_forward_kernel(
    latent_ref, gain_ref, up_ref, down_ref, part_ref, active_ref, slope_ref, low_ref
):
    @pl.when(pl.program_id(0) == 0)
    def _():
        normed, _ = norm_rows(latent_ref[...])
        low_ref[...] = (normed * gain_ref[...]).astype(jnp.bfloat16)

    hidden = dot(low_ref[...], up_ref[0])
    share = 0.5 * (1.0 + lax.erf(hidden * math.sqrt(0.5)))
    density = jnp.exp(-0.5 * hidden * hidden) * (1.0 / math.sqrt(2.0 * math.pi))
    active = (hidden * share).astype(jnp.bfloat16)
    active_ref[0] = active
    slope_ref[0] = share + hidden * density
    part = dot(active, down_ref[0])

    @pl.when(pl.program_id(0) == 0)
    def _():
        part_ref[...] = part

    @pl.when(pl.program_id(0) > 0)
    def _():
        part_ref[...] += part


def feed_forward(latent, gain, wide, wideout):
    rows, d_lat = latent.shape
    local = wide.shape[2]
    return pl.pallas_call(
        feed_forward_kernel,
        grid=(4,),
        out_shape=[
            pltpu.VMEM((rows, d_lat), jnp.float32),
            pltpu.HBM((4, rows, local), jnp.bfloat16),
            pltpu.HBM((4, rows, local), jnp.float32),
            pltpu.HBM((rows, d_lat), jnp.bfloat16),
        ],
        in_specs=[
            whole((rows, d_lat)),
            whole((1, d_lat)),
            pl.BlockSpec((1, d_lat, local), lambda s: (4 + s, 0, 0)),
            pl.BlockSpec((1, local, d_lat), lambda s: (2 + s, 0, 0)),
        ],
        out_specs=[
            whole((rows, d_lat)),
            each((rows, local)),
            each((rows, local)),
            whole((rows, d_lat)),
        ],
        compiler_params=pltpu.CompilerParams(vmem_limit_bytes=24 << 20),
        cost_estimate=pl.CostEstimate(
            flops=4 * 10**9, bytes_accessed=14 * 10**6, transcendentals=10**6
        ),
    )(in_vmem(latent), in_hbm(gain), in_hbm(wide), in_hbm(wideout))


def feed_backward_kernel(
    grad_ref,
    latent_ref,
    gain_ref,
    up_ref,
    down_ref,
    active_ref,
    slope_ref,
    low_ref,
    part_ref,
    up_first_ref,
    up_last_ref,
    down_grad_ref,
    gain_grad_ref,
    branch,
    branch_turned,
    low_turned,
    total,
):
    step, steps = pl.program_id(0), pl.num_programs(0)

    @pl.when(step == 0)
    def _():
        low = grad_ref[...].astype(jnp.bfloat16)
        branch[...] = low
        branch_turned[...] = low.T
        low_turned[...] = low_ref[...].T
        total[...] = jnp.zeros_like(total)

    active_grad = dot(branch[...], down_ref[0], 1, 1)
    hidden_grad = (active_grad * slope_ref[0]).astype(jnp.bfloat16)
    down_grad_ref[0] = dot(branch_turned[...], active_ref[0])
    total[...] += dot(hidden_grad, up_ref[0], 1, 1)
    up_grad = dot(low_turned[...], hidden_grad)

    @pl.when(step < 2)
    def _():
        up_first_ref[0] = up_grad

    @pl.when(step >= 2)
    def _():
        up_last_ref[0] = up_grad

    @pl.when(step == steps - 1)
    def _():
        normed, scale = norm_rows(latent_ref[...])
        part = total[...]
        gain_grad_ref[...] = jnp.sum(part * normed, 0, keepdims=True)
        part_ref[...] = norm_rows_back(part, gain_ref[...], normed, scale)


def feed_backward(grad, latent, gain, wide, wideout, active, slope, low):
    rows, d_lat = latent.shape
    local = wide.shape[2]
    return pl.pallas_call(
        feed_backward_kernel,
        grid=(4,),
        out_shape=[
            pltpu.VMEM((rows, d_lat), jnp.float32),
            pltpu.HBM((2, d_lat, local), jnp.float32),
            pltpu.HBM((2, d_lat, local), jnp.float32),
            pltpu.HBM((4, d_lat, local), jnp.float32),
            pltpu.HBM((1, d_lat), jnp.float32),
        ],
        in_specs=[
            whole((rows, d_lat)),
            whole((rows, d_lat)),
            whole((1, d_lat)),
            pl.BlockSpec((1, d_lat, local), lambda s: (4 + s, 0, 0)),
            pl.BlockSpec((1, local, d_lat), lambda s: (2 + s, 0, 0)),
            each((rows, local)),
            each((rows, local)),
            whole((rows, d_lat)),
        ],
        out_specs=[
            whole((rows, d_lat)),
            pl.BlockSpec((1, d_lat, local), lambda s: (jnp.minimum(s, 1), 0, 0)),
            pl.BlockSpec((1, d_lat, local), lambda s: (jnp.maximum(s - 2, 0), 0, 0)),
            each((d_lat, local)),
            whole((1, d_lat)),
        ],
        scratch_shapes=[
            pltpu.VMEM((rows, d_lat), jnp.bfloat16),
            pltpu.VMEM((d_lat, rows), jnp.bfloat16),
            pltpu.VMEM((d_lat, rows), jnp.bfloat16),
            pltpu.VMEM((rows, d_lat), jnp.float32),
        ],
        compiler_params=pltpu.CompilerParams(vmem_limit_bytes=36 << 20),
        cost_estimate=pl.CostEstimate(
            flops=9 * 10**9, bytes_accessed=26 * 10**6, transcendentals=0
        ),
    )(in_vmem(grad), in_hbm(latent), in_hbm(gain), in_hbm(wide), in_hbm(wideout), in_hbm(active), in_hbm(slope), in_hbm(low))


def write_kernel(stage, held, raws, results, scratch):
    (
        own_weight_ref,
        weight_total_ref,
        latent_ref,
        noisy_ref,
        noise_ref,
        keep_ref,
        place_ref,
        pixels_ref,
        wide_gain_ref,
        gain_ref,
        key_weight_ref,
        value_weight_ref,
        query_weight_ref,
        out_weight_ref,
    ) = held
    (
        latent_grad_ref,
        key_grad_ref,
        value_grad_ref,
        query_grad_ref,
        out_grad_ref,
        wide_gain_grad_ref,
        gain_grad_ref,
        embed_grad_ref,
        head_grad_ref,
        loss_ref,
    ) = results
    queries, outputs, upstream, query_grads, normed_ref, scale_ref = scratch
    stage.wait(*range(10))
    patches, width = queries.shape
    group = 4 * HEAD_DIM
    groups = width // group
    latents = latent_ref.shape[0]
    rows = 4 * latents
    weight, weight_total = own_weight_ref[:1, :1], weight_total_ref[:1, :1]

    latent_normed, latent_scale = norm_rows(latent_ref[...])
    latent_low = (latent_normed * wide_gain_ref[...]).astype(jnp.bfloat16)
    interface = embed(noisy_ref[...], pixels_ref[0], place_ref[...])
    normed, scale = norm_rows(interface)
    normed_ref[...] = normed
    scale_ref[...] = scale
    outer_low = (normed * gain_ref[1:2]).astype(jnp.bfloat16)
    stage.wait(10, 11)
    keys = dot(latent_low, key_weight_ref[...]).astype(jnp.bfloat16)
    values = dot(latent_low, value_weight_ref[...]).astype(jnp.bfloat16)
    stage.wait(12, 13)
    queries[...] = dot(outer_low, query_weight_ref[...]).astype(jnp.bfloat16)

    def part(values, index):
        return values[:, index * group : (index + 1) * group]

    def by_head(values):
        return values.reshape(4, latents, patches)

    def probs_of(index):
        later = (key_grad_ref, value_grad_ref)[index * rows // key_grad_ref.shape[0]]
        return later.at[pl.ds(index * rows % key_grad_ref.shape[0], rows)]

    def group_probs(index):
        scores = by_head(dot(scaled_heads(part(keys, index)), part(queries, index), 1, 1))
        grown = jnp.exp(scores - jnp.max(scores, 1, keepdims=True))
        return grown / jnp.sum(grown, 1, keepdims=True)

    for index in range(groups):
        probs = group_probs(index).reshape(rows, patches)
        probs_of(index)[...] = probs
        output = dot(probs.astype(jnp.bfloat16), spread_heads(part(values, index)), 0, 0)
        outputs[:, index * group : (index + 1) * group] = output.astype(jnp.bfloat16)

    outer = interface + dot(outputs[...], out_weight_ref[...], 1, 1)
    final_normed, final_scale = norm_rows(outer)
    final_low = (final_normed * gain_ref[2:3]).astype(jnp.bfloat16)
    head = pixels_ref[1]
    difference = dot(head, final_low, 1, 1) - noise_ref[...]
    masked = weight * keep_ref[...] * difference
    loss_ref[...] = jnp.full(loss_ref.shape, jnp.sum(masked * difference))
    predict_grad = (2.0 * masked / weight_total).astype(jnp.bfloat16)
    head_grad_ref[...] = dot(predict_grad, final_low)
    final_grad = dot(predict_grad, head, 0, 0)
    gain_final = jnp.sum(final_grad * final_normed, 0, keepdims=True)
    outer_grad = norm_rows_back(final_grad, gain_ref[2:3], final_normed, final_scale)
    branch = outer_grad.astype(jnp.bfloat16)
    out_grad_ref[...] = dot(branch, outputs[...], 0, 0)
    stage.store(4)
    upstream[...] = dot(branch, out_weight_ref[...]).astype(jnp.bfloat16)

    key_grads, value_grads = [], []
    for index in range(groups):
        probs = probs_of(index)[...]
        low, probs = probs.astype(jnp.bfloat16), by_head(probs)
        above = part(upstream, index)
        value_grads.append(join_heads(dot(low, above), 4).astype(jnp.bfloat16))
        prob_grad = by_head(dot(spread_heads(part(values, index)), above, 1, 1))
        inner = jnp.sum(prob_grad * probs, 1, keepdims=True)
        score_grad = (probs * (prob_grad - inner)).reshape(rows, patches).astype(jnp.bfloat16)
        key_grad = join_heads(dot(score_grad, part(queries, index)), 4) * HEAD_DIM ** (-0.5)
        key_grads.append(key_grad.astype(jnp.bfloat16))
        query_grad = dot(score_grad, scaled_heads(part(keys, index)), 0, 0)
        query_grads[:, index * group : (index + 1) * group] = query_grad.astype(jnp.bfloat16)
    key_grad, value_grad = (jnp.concatenate(item, 1) for item in (key_grads, value_grads))

    turned = latent_low.T
    key_grad_ref[...] = dot(turned, key_grad)
    value_grad_ref[...] = dot(turned, value_grad)
    stage.store(1, 2)
    latent_part = dot(key_grad, key_weight_ref[...], 1, 1) + dot(
        value_grad, value_weight_ref[...], 1, 1
    )
    wide_gain_grad_ref[...] = jnp.sum(latent_part * latent_normed, 0, keepdims=True)
    latent_grad_ref[...] = norm_rows_back(
        latent_part, wide_gain_ref[...], latent_normed, latent_scale
    )
    normed, scale = normed_ref[...], scale_ref[...]
    outer_low = (normed * gain_ref[1:2]).astype(jnp.bfloat16)
    query_grad_ref[...] = dot(outer_low, query_grads[...], 0, 0)
    stage.store(3)
    outer_part = dot(query_grads[...], query_weight_ref[...], 1, 1)
    gain_outer = jnp.sum(outer_part * normed, 0, keepdims=True)
    gain_grad_ref[...] = jnp.concatenate([gain_outer, gain_final], 0)
    back = outer_grad + norm_rows_back(outer_part, gain_ref[1:2], normed, scale)
    embed_grad_ref[...] = embed_back(noisy_ref[...], back)


def write_stage(
    own_weight, weight_total, latent, noisy, noise, keep, place, pixels, wide_gain, gains, weights
):
    latents, d_lat = latent.shape
    rows, patches = noisy.shape
    d_if = place.shape[1]
    width = weights[0].shape[1]
    results = [
        (latents, d_lat),
        (d_lat, width),
        (d_lat, width),
        (d_if, width),
        (d_if, width),
        (1, d_lat),
        (2, d_if),
        (rows, d_if),
        (rows, d_if),
        (8, 128),
    ]
    wide = pltpu.VMEM((patches, width), jnp.bfloat16)
    return staged(
        write_kernel,
        [
            own_weight,
            weight_total,
            latent,
            noisy,
            noise,
            keep,
            place,
            pixels,
            wide_gain,
            gains,
            *weights,
        ],
        [jax.ShapeDtypeStruct(shape, jnp.float32) for shape in results],
        [wide] * 4
        + [
            pltpu.VMEM((patches, d_if), jnp.float32),
            pltpu.VMEM((patches, 1), jnp.float32),
        ],
        15 * 10**9,
        length=27,
    )


def adam_update(master, first, second, gradient, scale):
    clipped = gradient * scale
    moment = adam_beta * first + (1.0 - adam_beta) * clipped
    square = adam_beta * second + (1.0 - adam_beta) * clipped * clipped
    fixed_first = moment / (1.0 - adam_beta**STEP)
    fixed_second = square / (1.0 - adam_beta**STEP)
    updated = master - learning_rate * (
        fixed_first / (jnp.sqrt(fixed_second) + adam_eps) + weight_decay * master
    )
    return (updated, moment, square)


def sum_rows(values):
    return jnp.sum(values.reshape(-1, 8, values.shape[-1]), 0)


def closing_kernel(count, count_dp, sizes, stage, held, raws, results, scratch):
    refs, given = list(scratch), list(held)

    def pull(number, source=None):
        source = refs if source is None else source
        taken = source[:number]
        del source[:number]
        return taken

    number, finished = sizes
    items, small_parts = views(pull(number, given)), pull(10, given)
    loss_tile, weight_tile = pull(2, given)
    done = views(pull(finished, given), 2)
    wide_out, narrow_out, turned_out, last_out, latents_out, rest_out, stats = results
    latents_item, rest_item, columns, column_sems = pull(4)
    number = len(items)
    shares = pull(number + 2)
    each = count_dp.bit_length() + 1
    sums = PieceSums(count_dp, items, shares[:number], pull(number * each))
    tiny = PieceSums(count_dp, [latents_item, rest_item], shares[number:], pull(2 * each))
    (write_share,) = pull(1)
    scatter = LineScatter(count, columns, write_share, pull(4), pull(4))
    small = [Spread("mp", count, *pull(3)) for _ in range(2)]
    over_dp, over_mp = Spread("dp", count_dp, *pull(3)), Spread("mp", count, *pull(3))

    column_loads, low = [], 0
    block, local = columns.shape[0] // count, columns.shape[1]
    for source in raws:
        rows = source.shape[0]
        for owner in range(count):
            column_loads.append(
                pltpu.make_async_copy(
                    source.at[:, pl.ds(owner * local, local)],
                    columns.at[pl.ds(owner * block + low, rows)],
                    column_sems.at[len(column_loads)],
                )
            )
        low += rows
    for load in column_loads:
        load.start()
    barrier = pltpu.get_barrier_semaphore()
    others = [over_dp.peer(step) for step in range(1, count_dp)]
    others += [over_mp.peer(step) for step in range(1, count)]
    signal_all(barrier, others)
    stage.wait()
    (latent_total, *gains, gain_side, gain_pair, side_embed, own_embed, head_grad) = small_parts
    d_if = gain_side.shape[1]
    lanes = d_if // count_dp
    width = latents_item.shape[2]
    rest_item[...] = jnp.zeros_like(rest_item)
    rows = []
    for gain in gains:
        rows += [gain[:, :d_if], gain[:, d_if:]]
    rows += [gain_side[...], gain_pair[...]]
    blocks = [(0, jnp.concatenate(rows, 0)), (16, side_embed[...] + own_embed[...]), (32, head_grad[...])]
    for piece in range(count_dp):
        latents_item[piece] = latent_total[:, piece * width : (piece + 1) * width]
        for first, block in blocks:
            rest_item[piece, pl.ds(first, block.shape[0]), :lanes] = block[
                :, piece * lanes : (piece + 1) * lanes
            ]
    pl.semaphore_wait(barrier, len(others))

    tiny.begin()
    sums.begin()
    for load in column_loads:
        load.wait()
    tiny.advance(1)

    def between():
        sums.advance(1)
        tiny.advance(2)

    scatter.run(between)
    for phase in range(3, tiny.bits + 1):
        tiny.advance(phase)
    for spread, share in zip(small, shares[-2:]):
        spread.held[spread.place] = share[...]
        spread.start()
    for phase in range(2, sums.bits + 1):
        sums.advance(phase)
    scatter.settle()

    self_in_2, self_out, read_query, read_out, read_key, read_value = shares[:6]
    self_in_0, self_in_1 = done[:2]
    up, down = done[2:6], done[6:10]
    lat_rows, if_rows = self_out.shape[0], read_key.shape[0]
    write_key, write_value = (write_share.at[pl.ds(i * lat_rows, lat_rows)] for i in range(2))
    write_query, write_out = (
        write_share.at[pl.ds(2 * lat_rows + i * if_rows, if_rows)] for i in range(2)
    )
    square = 0.0

    def keep(out, gradient, turn=False):
        nonlocal square
        value = gradient[...]
        square = square + sum_rows(value * value)
        out[...] = value.T if turn else value

    wide = [read_query, self_in_0, self_in_1, self_in_2] + up + [write_key, write_value]
    for slot, gradient in enumerate(wide):
        keep(wide_out.at[slot], gradient)
    for slot, gradient in enumerate([read_key, read_value, write_query]):
        keep(narrow_out.at[slot], gradient)
    for slot, gradient in enumerate([read_out, self_out] + down):
        keep(turned_out.at[slot], gradient, True)
    keep(last_out, write_out)
    stage.store(0, 1, 2, 3)
    for spread in small:
        spread.take()
    latents, rest = (spread.total() for spread in small)
    latents_out[...] = latents
    rest_out[...] = rest
    lead = (over_mp.place == 0).astype(jnp.float32)
    local = jnp.sum(square) + lead * (
        jnp.sum(sum_rows(latents * latents)) + jnp.sum(sum_rows(rest * rest))
    )
    lane = lax.broadcasted_iota(jnp.int32, (8, 128), 1)
    value = jnp.where(lane == 0, local, loss_tile[...])
    for spread in (over_dp, over_mp):
        spread.held[spread.place] = value
        spread.start()
        spread.take()
        value = spread.total()
    stats[...] = jnp.where(lane == 0, jnp.sqrt(value), value / weight_tile[...])
    sums.finish()
    tiny.finish()
    scatter.finish()
    for spread in small + [over_dp, over_mp]:
        spread.finish()


def closing(items, small_parts, tiles, done, write_shares, call_id):
    items, shapes, _ = piece_shapes(items)
    count, count_dp = lax.axis_size("mp"), lax.axis_size("dp")
    latents, d_lat = small_parts[0].shape
    lat_rows, local = done[0].shape[1:]
    if_rows = write_shares[2].shape[0]
    extra = [(latents, d_lat // count_dp), (48, 128)]
    block = (sum(item.shape[0] for item in write_shares), local)
    columns = (count * block[0], local)
    outs = [
        (10, lat_rows, local),
        (3, if_rows, local),
        (6, local, lat_rows),
        (if_rows, local),
        *extra,
        (8, 128),
    ]
    shapes = shapes + extra
    scratch = (
        [pltpu.VMEM((count_dp,) + shape, jnp.float32) for shape in extra]
        + [
            pltpu.VMEM(columns, jnp.float32),
            pltpu.SemaphoreType.DMA((count * len(write_shares),)),
        ]
        + [pltpu.VMEM(shape, jnp.float32) for shape in shapes]
        + PieceSums.scratch(count_dp, shapes)
        + [pltpu.VMEM(block, jnp.float32)]
        + LineScatter.scratch(count, columns, 4)
        + Spread.scratch(count, extra[0])
        + Spread.scratch(count, extra[1])
        + Spread.scratch(count_dp, (8, 128))
        + Spread.scratch(count, (8, 128))
    )
    return staged(
        partial(closing_kernel, count, count_dp, (len(items), len(done))),
        [*items, *small_parts, *tiles, *done],
        [jax.ShapeDtypeStruct(shape, jnp.float32) for shape in outs],
        scratch,
        10**7,
        write_shares,
        call_id,
        50,
    )


def clip_scale(norm):
    return clip_level / jnp.maximum(norm, clip_level)


def update_kernel(kinds, *refs):
    number = 3 * (kinds + 1)
    sources, states, refs = refs[: 1 + kinds], refs[1 + kinds :][:number], refs[1 + kinds + number :]
    outs, local, refs = refs[:number], refs[number:][: 1 + kinds], refs[number + 1 + kinds :]
    local_sems, held, (in_sems, out_sems) = refs[0], refs[1 : 1 + number], refs[1 + number :]
    stats, gradients = local[0], local[1:]
    kinds += 1
    firsts = [
        pltpu.make_async_copy(source, target, local_sems.at[index])
        for index, (source, target) in enumerate(zip(sources, local))
    ]
    for first in firsts:
        first.start()
    lane = lax.broadcasted_iota(jnp.int32, (8, 128), 1)
    corner = jnp.logical_and(lane == 0, lax.broadcasted_iota(jnp.int32, (8, 128), 0) == 0)
    loads, copies = [], []
    pieces = []
    for kind, gradient in enumerate(gradients):
        slots = range(gradient.shape[0]) if len(gradient.shape) == 3 else [None]
        pieces += [(kind, slot) for slot in slots]

    def at(ref, slot):
        return ref if slot is None else ref.at[slot]

    for kind, slot in pieces:
        for index in range(3 * kind, 3 * kind + 3):
            source, target = at(states[index], slot), at(held[index], slot)
            loads.append(pltpu.make_async_copy(source, target, in_sems.at[len(loads)]))
            loads[-1].start()
    for load in firsts:
        load.wait()
    scale = jnp.sum(jnp.where(corner, clip_scale(stats[...]), 0.0))
    pixel_loads = [
        pltpu.make_async_copy(states[index], held[index], in_sems.at[len(loads) + index - 18])
        for index in range(18, 21)
    ]
    for load in pixel_loads:
        load.start()
    for order, (kind, slot) in enumerate(pieces):
        for load in loads[3 * order : 3 * order + 3]:
            load.wait()
        refs = [at(held[index], slot) for index in range(3 * kind, 3 * kind + 3)]
        source = at(gradients[kind], slot)
        rows, width = refs[0].shape
        step = math.gcd(rows, max(8, 8192 // width)) if rows % 8 == 0 else rows

        def one(index, carry, refs=refs, source=source, step=step, width=width):
            where = pl.ds(pl.multiple_of(index * step, step), step)
            state = [ref[where] for ref in refs]
            for ref, result in zip(refs, adam_update(*state, source[where, :width], scale)):
                ref[where] = result
            return carry

        lax.fori_loop(0, rows // step, one, 0)
        for index in range(3 * kind, 3 * kind + 3):
            source, target = at(held[index], slot), at(outs[index], slot)
            copies.append(pltpu.make_async_copy(source, target, out_sems.at[len(copies)]))
            copies[-1].start()
    for load in pixel_loads:
        load.wait()
    pixels, rest = held[18:21], gradients[-1]
    for slot in range(2):
        gradient = rest[16 * (slot + 1) : 16 * (slot + 1) + PIX, : pixels[0].shape[2]]
        state = [ref[:, slot, :] for ref in pixels]
        for ref, result in zip(pixels, adam_update(*state, gradient, scale)):
            ref[:, slot, :] = result
    for index in range(18, 21):
        copies.append(pltpu.make_async_copy(held[index], outs[index], out_sems.at[len(copies)]))
        copies[-1].start()
    for copy in copies:
        copy.wait()


def update_states(stats, gradients, states):
    kinds = len(gradients)
    copies = sum(3 * (item.shape[0] if item.ndim == 3 else 1) for item in gradients) + 3
    sems = pltpu.SemaphoreType.DMA((copies,))
    return pl.pallas_call(
        partial(update_kernel, kinds),
        out_shape=[pltpu.HBM(item.shape, item.dtype) for item in states],
        in_specs=[HBM_SPEC] * (1 + kinds + len(states)),
        out_specs=[HBM_SPEC] * len(states),
        scratch_shapes=[pltpu.VMEM(item.shape, jnp.float32) for item in (stats, *gradients)]
        + [pltpu.SemaphoreType.DMA((1 + kinds,))]
        + [pltpu.VMEM(item.shape, jnp.float32) for item in states]
        + [sems] * 2,
        compiler_params=pltpu.CompilerParams(vmem_limit_bytes=24 << 20),
        cost_estimate=pl.CostEstimate(
            flops=2 * 10**7, bytes_accessed=14 * 10**6, transcendentals=0
        ),
    )(*(in_hbm(item) for item in (stats, *gradients, *states)))


def write_apart(
    latent_three,
    own_noisy,
    own_noise,
    own_keep,
    own_weight,
    weight_total,
    place,
    copy_pixels,
    gain,
    gain_rows,
    weights,
    layout,
    timesteps,
):
    write_key_weight, write_value_weight, write_query_weight, write_out_weight = weights
    images, latents, first_image, sharers = layout
    own_images, own_latents, d_lat = latent_three.shape
    write_norm, write_stats = layer_norm(latent_three, gain)
    write_low = write_norm.astype(jnp.bfloat16)

    own_interface = (
        jnp.einsum(
            "bcp,cd->bpd", own_noisy, copy_pixels[0].astype(jnp.float32), precision=precise
        )
        + place
    )

    outer_norm, outer_stats = layer_norm(own_interface, gain_rows[9])
    outer_low = outer_norm.astype(jnp.bfloat16)

    def join(spec, values, weight):
        product = jnp.einsum(spec, values, weight, preferred_element_type=jnp.float32)
        return product.astype(jnp.bfloat16)

    def image_rows(values):
        if sharers == 1:
            return values
        nothing = jnp.where(timesteps[0] > 0, 0.0, -0.0)
        whole = lax.all_gather(values.astype(jnp.float32), "mp", axis=0, tiled=True)
        whole = whole + nothing
        whole = whole.reshape(images, latents, d_lat).astype(jnp.bfloat16)
        return lax.dynamic_slice_in_dim(whole, first_image, own_images, 0)

    write_query = join("bpd,dc->bpc", outer_low, write_query_weight)
    write_key = image_rows(join("bld,dc->blc", write_low, write_key_weight))
    write_value = image_rows(join("bld,dc->blc", write_low, write_value_weight))
    write_out, write_total = attend_forward(write_query, write_key, write_value, None)
    outer = own_interface + jnp.einsum(
        "bpc,dc->bpd", write_out, write_out_weight, preferred_element_type=jnp.float32
    )
    final_norm, final_stats = layer_norm(outer, gain_rows[10])
    final_low = final_norm.astype(jnp.bfloat16)
    predicted = jnp.einsum(
        "bpd,cd->bcp", final_low, copy_pixels[1], preferred_element_type=jnp.float32
    )
    difference = predicted - own_noise
    masked = own_weight[:, None, None] * own_keep[:, None, :] * difference
    loss_local = jnp.sum(masked * difference)
    predict_grad = (2.0 * masked / weight_total).astype(jnp.bfloat16)
    head_grad = jnp.einsum(
        "bcp,bpd->cd", predict_grad, final_low, preferred_element_type=jnp.float32
    )
    final_grad = jnp.einsum(
        "bcp,cd->bpd", predict_grad, copy_pixels[1], preferred_element_type=jnp.float32
    )
    outer_grad, gain_final = norm_back(final_grad, gain_rows[10], final_stats)
    branch_low = outer_grad.astype(jnp.bfloat16)
    narrowout_grad = jnp.einsum(
        "bpd,bpc->dc", branch_low, write_out, preferred_element_type=jnp.float32
    )
    write_upstream = join("bpd,dc->bpc", branch_low, write_out_weight)
    query_grad, key_grad, value_grad = attend_back(
        write_query, write_key, write_value, None, write_total, write_upstream
    )
    write_query_grad = jnp.einsum(
        "bpd,bpc->dc", outer_low, query_grad, preferred_element_type=jnp.float32
    )
    outer_part = jnp.einsum(
        "bpc,dc->bpd", query_grad, write_query_weight, preferred_element_type=jnp.float32
    )

    def row_grad(values):
        if sharers > 1:
            whole = jnp.zeros((images, latents, d_lat), jnp.float32)
            whole = lax.dynamic_update_slice_in_dim(whole, values, first_image, 0)
            values = lax.psum_scatter(
                whole.reshape(images * sharers, own_latents, d_lat),
                "mp",
                scatter_dimension=0,
                tiled=True,
            )
        return values.astype(jnp.bfloat16)

    key_grad, value_grad = row_grad(key_grad), row_grad(value_grad)
    write_key_grad = jnp.einsum(
        "bld,blc->dc", write_low, key_grad, preferred_element_type=jnp.float32
    )
    write_value_grad = jnp.einsum(
        "bld,blc->dc", write_low, value_grad, preferred_element_type=jnp.float32
    )
    write_part = jnp.einsum(
        "blc,dc->bld", key_grad, write_key_weight, preferred_element_type=jnp.float32
    ) + jnp.einsum(
        "blc,dc->bld", value_grad, write_value_weight, preferred_element_type=jnp.float32
    )
    own_grad, gain_write = norm_back(write_part, gain, write_stats)
    outer_back, gain_outer = norm_back(outer_part, gain_rows[9], outer_stats)
    embed_grad = jnp.einsum(
        "bcp,bpd->cd", own_noisy, outer_grad + outer_back, precision=precise
    )
    return (
        own_grad,
        write_key_grad,
        write_value_grad,
        write_query_grad,
        narrowout_grad,
        gain_write,
        gain_outer,
        gain_final,
        embed_grad,
        head_grad,
        loss_local,
    )


def body(
    clean_patches,
    noise_patches,
    timesteps,
    present_mask,
    copy_widein,
    copy_narrowin,
    copy_wideout,
    copy_narrowout,
    copy_latents,
    copy_gains,
    copy_pixels,
    master_widein,
    first_widein,
    second_widein,
    master_narrowin,
    first_narrowin,
    second_narrowin,
    master_wideout,
    first_wideout,
    second_wideout,
    master_narrowout,
    first_narrowout,
    second_narrowout,
    master_latents,
    first_latents,
    second_latents,
    master_gains,
    first_gains,
    second_gains,
    master_pixels,
    first_pixels,
    second_pixels,
):
    images = clean_patches.shape[0]
    patches = clean_patches.shape[2]
    count_mp, count_dp = lax.axis_size("mp"), lax.axis_size("dp")
    mp_index, dp_index = lax.axis_index("mp"), lax.axis_index("dp")
    lead = (mp_index == 0).astype(jnp.float32)
    latents, d_lat = copy_latents.shape
    d_if = copy_gains.shape[1]
    local = copy_widein.shape[2]
    sharers = max(1, count_mp // images)
    own_images = max(1, images // count_mp)
    own_patches, own_latents = patches // sharers, latents // sharers
    first_image = mp_index * own_images // sharers
    share = lax.rem(mp_index, sharers)

    def dp_piece(values, axis):
        size = values.shape[axis] // count_dp
        return lax.dynamic_slice_in_dim(values, dp_index * size, size, axis).astype(jnp.float32)

    key_piece = dp_piece(copy_widein[:, 8], 0)
    value_piece = dp_piece(copy_widein[:, 9], 0)
    query_piece = dp_piece(copy_narrowin[:, 2], 0)
    out_piece = dp_piece(copy_narrowout, 1).T
    gathered = lax.all_gather(
        jnp.concatenate([key_piece, value_piece, query_piece, out_piece], 0), "mp"
    )

    signal = jnp.cos(0.5 * math.pi * (timesteps.astype(jnp.float32) + 0.5) / NSTEPS) ** 2
    noisy = (
        jnp.sqrt(signal)[:, None, None] * clean_patches
        + jnp.sqrt(1.0 - signal)[:, None, None] * noise_patches
    )
    loss_weight = 0.5 + signal
    keep_float = present_mask.astype(jnp.float32)
    weight_here = jnp.sum(loss_weight * PIX * jnp.sum(keep_float, 1))
    gain_rows = copy_gains.astype(jnp.float32)

    def wide_gain(index):
        return gain_rows[2 * index : 2 * index + 2].reshape(-1)

    wide_in = in_hbm(jnp.swapaxes(copy_widein, 0, 1))
    narrow_in = in_hbm(jnp.swapaxes(copy_narrowin, 0, 1))
    wide_out = in_hbm(copy_wideout)
    place = position_table(patches, d_if)
    noisy_rows, pixel_rows, noise_rows = (
        jnp.pad(item, ((0, 0), (0, 16 - PIX), (0, 0)))
        for item in (noisy, copy_pixels, noise_patches)
    )
    read_args = (
        noisy_rows,
        keep_float[:, :, None],
        place,
        pixel_rows[0],
        copy_latents,
        wide_gain(0)[None],
        gain_rows[8:9],
        wide_in,
        narrow_in,
        wide_out,
    )
    read_part, *read_kept = read_forward(*read_args)
    wide_gains = [wide_gain(index)[None] for index in range(1, 4)]
    latent_base = copy_latents.astype(jnp.float32)

    def own_tokens(values, axis):
        values = lax.dynamic_slice_in_dim(values, first_image, own_images, 0)
        return lax.dynamic_slice_in_dim(values, share * own_patches, own_patches, axis)

    own_weight = lax.dynamic_slice_in_dim(loss_weight, first_image, own_images, 0)
    own_scalar = jnp.broadcast_to(own_weight[0], (8, 128))
    own_pieces = [
        own_tokens(noisy_rows, 2),
        own_tokens(noise_rows, 2),
        own_tokens(keep_float, 1),
    ]
    side_gains = gain_rows[8:11]
    here_tile, lead = jnp.full((8, 128), weight_here), lead.reshape(1, 1)
    ready = (own_pieces, own_scalar, wide_gains, side_gains, latent_base, here_tile, lead, pixel_rows)
    gathered, read_part, ready = lax.optimization_barrier((gathered, read_part, ready))
    own_pieces, own_scalar, wide_gains, side_gains, latent_base, here_tile, lead, pixel_rows = ready
    gathered = lax.all_gather(gathered, "dp").reshape(count_dp * count_mp, -1, local)
    latent_near, latent_one, (weight_tile,) = line_sum(
        read_part, latent_base, 2, tile=here_tile
    )
    self_part, *self_kept = self_forward(
        latent_near, wide_gains[0], wide_in, wide_out, images
    )
    latent_near, latent_two, _ = line_sum(self_part, latent_one, 3)
    feed_part, *feed_kept = feed_forward(latent_near, wide_gains[1], wide_in, wide_out)
    latent_three, write_weights = line_scatter(
        feed_part, latent_two, gathered, [d_lat, d_lat, d_if, d_if], 4
    )
    latent_three = latent_three.reshape(own_images, own_latents, d_lat)
    fits = patches == count_mp * local and d_lat % (4 * latents) == 0
    if sharers == 1 and own_images == 1 and fits:
        (
            own_grad,
            write_key_grad,
            write_value_grad,
            write_query_grad,
            narrowout_grad,
            gain_write,
            gain_pair,
            own_embed,
            head_grad,
            loss_tile,
        ) = write_stage(
            own_scalar,
            weight_tile,
            latent_three[0],
            own_pieces[0][0],
            own_pieces[1][0],
            own_pieces[2],
            place,
            pixel_rows,
            wide_gains[2],
            side_gains,
            write_weights,
        )
    else:
        (
            own_grad,
            write_key_grad,
            write_value_grad,
            write_query_grad,
            narrowout_grad,
            gain_write,
            gain_outer,
            gain_final,
            own_embed,
            head_grad,
            loss_local,
        ) = write_apart(
            latent_three,
            own_tokens(noisy, 2),
            own_tokens(noise_patches, 2),
            own_tokens(keep_float, 1),
            own_weight,
            weight_tile[0, 0],
            lax.dynamic_slice_in_dim(place, share * own_patches, own_patches, 0),
            copy_pixels,
            wide_gain(3),
            gain_rows,
            write_weights,
            (images, latents, first_image, sharers),
            timesteps,
        )
        gain_write, gain_pair = gain_write[None], jnp.stack([gain_outer, gain_final])
        own_embed, head_grad = (
            jnp.pad(item, ((0, 16 - PIX), (0, 0))) for item in (own_embed, head_grad)
        )
        loss_tile = jnp.full((8, 128), loss_local)
    latent_near, latent_grad, (key_share, query_share) = line_gather(
        own_grad.reshape(-1, d_lat), 5, [write_key_grad, write_query_grad]
    )
    latent_part, up_first, up_last, down_grad, gain_feed = feed_backward(
        latent_near, latent_two, wide_gains[1], wide_in, wide_out, *feed_kept
    )
    latent_near, latent_grad, five_shares = line_sum(
        latent_part, latent_grad, 6, [write_value_grad, narrowout_grad, up_first]
    )
    latent_part, self_first, self_last, gain_self = self_backward(
        latent_near, latent_one, wide_gains[0], wide_in, wide_out, *self_kept
    )
    latent_near, latent_grad, six_shares = line_sum(
        latent_part, latent_grad, 7, [up_last, down_grad, self_first]
    )
    read_wide, read_narrow, latent_total, gain_read, gain_side, side_embed = read_backward(
        read_args[0], *read_args[4:], *read_kept, latent_near, lead
    )
    *gradients, stats = closing(
        [self_last, read_wide, read_narrow],
        [
            latent_total,
            gain_read,
            gain_self,
            gain_feed,
            gain_write,
            gain_side,
            gain_pair,
            side_embed,
            own_embed,
            head_grad,
        ],
        [loss_tile, weight_tile],
        [six_shares[2], five_shares[2], six_shares[0], six_shares[1]],
        [key_share, five_shares[0], query_share, five_shares[1]],
        8,
    )
    states = (
        *(jnp.swapaxes(item, 0, 1) for item in (master_widein, first_widein, second_widein)),
        *(jnp.swapaxes(item, 0, 1) for item in (master_narrowin, first_narrowin, second_narrowin)),
        master_wideout,
        first_wideout,
        second_wideout,
        *(item.T for item in (master_narrowout, first_narrowout, second_narrowout)),
        master_latents,
        first_latents,
        second_latents,
        master_gains,
        first_gains,
        second_gains,
        *(jnp.swapaxes(item, 0, 1) for item in (master_pixels, first_pixels, second_pixels)),
    )
    results = update_states(stats, gradients, states)
    results = [
        jnp.swapaxes(item, 0, 1) if index < 6 or 9 <= index < 12 or index >= 18 else item
        for index, item in enumerate(results)
    ]
    return (stats[0, 1], stats[0, 0], *results)


def solution(mesh):
    in_specs = (
        P("dp", None, None),
        P("dp", None, None),
        P("dp"),
        P("dp", None),
        P(None, None, "mp"),
        P(None, None, "mp"),
        P(None, "mp", None),
        P("mp", None),
        P(),
        P(),
        P(),
        P("dp", None, "mp"),
        P("dp", None, "mp"),
        P("dp", None, "mp"),
        P("dp", None, "mp"),
        P("dp", None, "mp"),
        P("dp", None, "mp"),
        P(None, "mp", "dp"),
        P(None, "mp", "dp"),
        P(None, "mp", "dp"),
        P("mp", "dp"),
        P("mp", "dp"),
        P("mp", "dp"),
        P(None, "dp"),
        P(None, "dp"),
        P(None, "dp"),
        P(None, "dp"),
        P(None, "dp"),
        P(None, "dp"),
        P(None, None, "dp"),
        P(None, None, "dp"),
        P(None, None, "dp"),
    )
    out_specs = (
        P(),
        P(),
        P("dp", None, "mp"),
        P("dp", None, "mp"),
        P("dp", None, "mp"),
        P("dp", None, "mp"),
        P("dp", None, "mp"),
        P("dp", None, "mp"),
        P(None, "mp", "dp"),
        P(None, "mp", "dp"),
        P(None, "mp", "dp"),
        P("mp", "dp"),
        P("mp", "dp"),
        P("mp", "dp"),
        P(None, "dp"),
        P(None, "dp"),
        P(None, "dp"),
        P(None, "dp"),
        P(None, "dp"),
        P(None, "dp"),
        P(None, None, "dp"),
        P(None, None, "dp"),
        P(None, None, "dp"),
    )
    return jax.shard_map(body, mesh=mesh, in_specs=in_specs, out_specs=out_specs, check_vma=False)
```

```python
from functools import partial
import math

import jax
import jax.numpy as jnp
import numpy as np
from jax import lax
from jax.experimental import pallas as pl
from jax.experimental.pallas import tpu as pltpu
from jax.sharding import PartitionSpec as P

HEAD_DIM = 64
PIX = 12
NSTEPS = 1000
STEP = 10


precise = lax.Precision.HIGHEST
clip_level = 0.01
learning_rate = 0.05
weight_decay = 0.1
adam_beta = 0.5
adam_eps = 1e-08


def layer_norm(values, gain):
    centered = values - jnp.mean(values, -1, keepdims=True)
    scale = lax.rsqrt(jnp.mean(centered * centered, -1, keepdims=True) + 1e-05)
    normed = centered * scale
    return (normed * gain, (normed, scale))


def norm_back(upstream, gain, stats):
    normed, scale = stats
    inner = upstream * gain
    values = scale * (
        inner
        - jnp.mean(inner, -1, keepdims=True)
        - normed * jnp.mean(inner * normed, -1, keepdims=True)
    )
    gain_grad = jnp.sum((upstream * normed).reshape(-1, normed.shape[-1]), 0)
    return (values, gain_grad)


def position_table(count, width):
    place = np.arange(count, dtype=np.float64)[:, None]
    angle = place * 10000.0 ** (-2.0 * np.arange(width // 2) / width)
    return jnp.asarray(np.concatenate([np.sin(angle), np.cos(angle)], -1), jnp.float32)


def positions(count, width):
    place = jnp.arange(count, dtype=jnp.float32)[:, None]
    index = jnp.arange(width // 2, dtype=jnp.float32)[None, :]
    angle = place * jnp.exp(-math.log(10000.0) * 2.0 * index / width)
    return jnp.concatenate([jnp.sin(angle), jnp.cos(angle)], -1)


def split_heads(values):
    return values.reshape(values.shape[:-1] + (values.shape[-1] // HEAD_DIM, HEAD_DIM))


def attend_scores(queries, keys, keep_mask):
    scores = jnp.einsum(
        "bqhe,bkhe->bhqk",
        split_heads(queries),
        split_heads(keys),
        preferred_element_type=jnp.float32,
    ) * HEAD_DIM ** (-0.5)
    if keep_mask is not None:
        scores = jnp.where(keep_mask[:, None, None, :] > 0, scores, -1e30)
    return scores


def attend_forward(queries, keys, values, keep_mask):
    scores = attend_scores(queries, keys, keep_mask)
    top = jnp.max(scores, -1, keepdims=True)
    log_total = top + jnp.log(jnp.sum(jnp.exp(scores - top), -1, keepdims=True))
    probs = jnp.exp(scores - log_total).astype(jnp.bfloat16)
    output = jnp.einsum(
        "bhqk,bkhe->bqhe", probs, split_heads(values), preferred_element_type=jnp.float32
    )
    return (output.reshape(queries.shape).astype(jnp.bfloat16), log_total)


def attend_back(queries, keys, values, keep_mask, log_total, upstream):
    scores = attend_scores(queries, keys, keep_mask)
    probs = jnp.exp(scores - log_total)
    value_grad = jnp.einsum(
        "bhqk,bqhe->bkhe",
        probs.astype(jnp.bfloat16),
        split_heads(upstream),
        preferred_element_type=jnp.float32,
    )
    prob_grad = jnp.einsum(
        "bqhe,bkhe->bhqk",
        split_heads(upstream),
        split_heads(values),
        preferred_element_type=jnp.float32,
    )
    score_grad = (probs * (prob_grad - jnp.sum(prob_grad * probs, -1, keepdims=True))).astype(
        jnp.bfloat16
    )
    query_grad = jnp.einsum(
        "bhqk,bkhe->bqhe", score_grad, split_heads(keys), preferred_element_type=jnp.float32
    ) * HEAD_DIM ** (-0.5)
    key_grad = jnp.einsum(
        "bhqk,bqhe->bkhe", score_grad, split_heads(queries), preferred_element_type=jnp.float32
    ) * HEAD_DIM ** (-0.5)
    return (
        query_grad.reshape(queries.shape).astype(jnp.bfloat16),
        key_grad.reshape(keys.shape),
        value_grad.reshape(values.shape),
    )


MESH_ID = pl.DeviceIdType.MESH
HBM_SPEC = pl.BlockSpec(memory_space=pltpu.HBM)
VMEM_SPEC = pl.BlockSpec(memory_space=pltpu.VMEM)
CHUNKS = 32
VMEM_LIMIT = 56 << 20


def in_hbm(values):
    return pltpu.with_memory_space_constraint(values, pltpu.HBM)


def in_vmem(values):
    return pltpu.with_memory_space_constraint(values, pltpu.VMEM)


def remote(source, target, send_sem, recv_sem, device):
    return pltpu.make_async_remote_copy(
        src_ref=source,
        dst_ref=target,
        send_sem=send_sem,
        recv_sem=recv_sem,
        device_id=device,
        device_id_type=MESH_ID,
    )


class PieceSums:
    def __init__(self, count, items, outs, scratch):
        self.count, self.items, self.outs = count, items, outs
        self.bits = count.bit_length() - 1
        self.place = lax.axis_index("dp") if items else None
        self.held = []
        for index in range(len(items)):
            self.held.append(scratch[index * (self.bits + 2) : (index + 1) * (self.bits + 2)])

    @staticmethod
    def scratch(count, shapes):
        bits = count.bit_length() - 1
        result = []
        for rows, width in shapes:
            result.append(pltpu.VMEM((count // 2, rows, width), jnp.float32))
            for phase in range(2, bits + 1):
                result.append(
                    pltpu.VMEM((2 * (count >> phase), rows // 2, width), jnp.float32)
                )
            copies = count // 2 + 2 * sum(count >> phase for phase in range(2, bits + 1))
            result += [pltpu.SemaphoreType.DMA((copies,))] * 2
        return result

    def peers(self):
        return [{"dp": self.place ^ (1 << bit)} for bit in range(self.bits)] if self.items else []

    def order(self, half):
        later = list(range(1, self.bits))
        turn = half * (len(later) // 2)
        return later[turn:] + later[:turn]

    def first_copy(self, index, piece):
        item, held = self.items[index], self.held[index]
        other = 1 - (self.place & 1)
        return remote(
            item.at[2 * piece + other],
            held[0].at[piece],
            held[-2].at[piece],
            held[-1].at[piece],
            {"dp": self.place ^ 1},
        )

    def member(self, half, phase, entry, flip):
        bits = self.order(half)
        settled, now, rest = bits[: phase - 2], bits[phase - 2], bits[phase - 1 :]
        piece = 0
        for bit in settled:
            piece = piece | (self.place & (1 << bit))
        own = self.place & (1 << now)
        piece = piece | ((own ^ (1 << now)) if flip else own)
        for position, bit in enumerate(rest):
            if (entry >> position) & 1:
                piece = piece | (1 << bit)
        return piece >> 1

    def later_copy(self, index, half, phase, entry):
        held = self.held[index]
        rows = self.items[index].shape[1] // 2
        size = self.count >> phase
        sem = self.count // 2 + 2 * sum(self.count >> p for p in range(2, phase)) + half * size + entry
        return remote(
            held[0].at[self.member(half, phase, entry, True), pl.ds(half * rows, rows)],
            held[phase - 1].at[half * size + entry],
            held[-2].at[sem],
            held[-1].at[sem],
            {"dp": self.place ^ (1 << self.order(half)[phase - 2])},
        )

    def entries(self, phase):
        return [
            (index, half, entry)
            for index in range(len(self.items))
            for half in range(2)
            for entry in range(self.count >> phase)
        ]

    def begin(self):
        for index in range(len(self.items)):
            for piece in range(self.count // 2):
                self.first_copy(index, piece).start()

    def send(self, phase):
        for index, half, entry in self.entries(phase):
            self.later_copy(index, half, phase, entry).start()

    def advance(self, phase):
        if not self.items:
            return
        if phase == 1:
            own = self.place & 1
            for index, item in enumerate(self.items):
                total = self.held[index][0]
                for piece in range(self.count // 2):
                    self.first_copy(index, piece).wait_recv()
                    add_rows(total.at[piece], total.at[piece], item.at[2 * piece + own])
        else:
            for index, half, entry in self.entries(phase):
                self.later_copy(index, half, phase, entry).wait_recv()
                held, rows = self.held[index], self.items[index].shape[1] // 2
                where = pl.ds(half * rows, rows)
                came = held[phase - 1].at[half * (self.count >> phase) + entry]
                kept = held[0].at[self.member(half, phase, entry, False), where]
                if phase == self.bits:
                    add_rows(self.outs[index].at[where], kept, came)
                else:
                    add_rows(kept, kept, came)
        if phase < self.bits:
            self.send(phase + 1)

    def finish(self):
        for index in range(len(self.items)):
            for piece in range(self.count // 2):
                self.first_copy(index, piece).wait_send()
        for phase in range(2, self.bits + 1):
            for index, half, entry in self.entries(phase):
                self.later_copy(index, half, phase, entry).wait_send()

    def moments(self, total):
        if not self.items:
            return [(0, total, None)]
        marks, low = [], 0
        for phase in range(1, self.bits + 1):
            share = (1 - 0.5 ** (phase - 1)) / (1 - 0.5 ** (self.bits - 1))
            high = total if phase == self.bits else int(total * (0.22 + 0.78 * share))
            marks.append((low, high, phase))
            low = high
        return marks


def add_rows(target, left, right):
    rows, width = target.shape
    step = math.gcd(rows, max(8, 8192 // width))

    def one(index, carry):
        where = pl.ds(pl.multiple_of(index * step, step), step)
        target[where] = left[where] + right[where]
        return carry

    lax.fori_loop(0, rows // step, one, 0)


class Spread:
    def __init__(self, name, count, held, send_sem, recv_sem):
        self.name, self.count, self.held = name, count, held
        self.send_sem, self.recv_sem = send_sem, recv_sem
        self.place = lax.axis_index(name)

    @staticmethod
    def scratch(count, shape):
        sems = pltpu.SemaphoreType.DMA((count,))
        return [pltpu.VMEM((count,) + shape, jnp.float32), sems, sems]

    def peer(self, step):
        return {self.name: lax.rem(self.place + step, self.count)}

    def copy(self, step, slot):
        return remote(
            self.held.at[slot],
            self.held.at[slot],
            self.send_sem.at[step],
            self.recv_sem.at[slot],
            self.peer(step),
        )

    def each(self, action):
        def one(step, carry):
            action(step)
            return carry

        lax.fori_loop(1, self.count, one, 0)

    def start(self):
        self.each(lambda step: self.copy(step, self.place).start())

    def take(self):
        self.each(lambda step: self.copy(step, lax.rem(self.place + step, self.count)).wait_recv())

    def finish(self):
        self.each(lambda step: self.copy(step, self.place).wait_send())

    def total(self):
        return lax.fori_loop(
            1, self.count, lambda slot, carry: carry + self.held[slot], self.held[0]
        )


class Convert:
    def __init__(self, count_mp, steps, blocks, outs, buffer, sems):
        self.count_mp, self.blocks, self.outs = count_mp, blocks, outs
        self.buffer, self.sems = buffer, sems
        self.number = blocks.shape[0]
        self.each, self.stride = max(1, self.number // steps), max(1, steps // self.number)

    @staticmethod
    def scratch(block):
        return [pltpu.VMEM((3,) + block, jnp.float32), pltpu.SemaphoreType.DMA((3,))]

    def copy(self, index):
        slot = lax.rem(index, 3)
        return pltpu.make_async_copy(
            self.blocks.at[index], self.buffer.at[slot], self.sems.at[slot]
        )

    def begin(self):
        self.copy(0).start()
        self.copy(1).start()

    def one(self, index):
        self.copy(index).wait()

        @pl.when(index + 2 < self.number)
        def _():
            self.copy(index + 2).start()

        block = self.buffer.at[lax.rem(index, 3)]
        local = block.shape[1]
        columns = pl.ds(pl.multiple_of(lax.rem(index, self.count_mp) * local, local), local)
        low = 0
        for out in self.outs:
            rows = out.shape[0] * self.count_mp // self.number
            where = pl.ds(pl.multiple_of(index // self.count_mp * rows, rows), rows)
            out[where, columns] = block[pl.ds(low, rows)].astype(jnp.bfloat16)
            low += rows

    def step(self, index):
        @pl.when(lax.rem(index, self.stride) == 0)
        def _():
            for entry in range(self.each):
                self.one(index // self.stride * self.each + entry)


def signal_all(barrier, others):
    for other in others:
        pl.semaphore_signal(barrier, inc=1, device_id=other, device_id_type=MESH_ID)


class Stage:
    def __init__(self, sources, held, in_sems, results, targets, out_sems):
        self.loads = [
            pltpu.make_async_copy(source, target, in_sems.at[index])
            for index, (source, target) in enumerate(zip(sources, held))
        ]
        self.stores = [
            pltpu.make_async_copy(source, target, out_sems.at[index])
            for index, (source, target) in enumerate(zip(results, targets))
        ]
        self.stored, self.waited = [], []

    def start(self):
        for load in self.loads:
            load.start()

    def wait(self, *indices):
        for index in indices or range(len(self.loads)):
            if index not in self.waited:
                self.loads[index].wait()
                self.waited.append(index)

    def store(self, *indices):
        for index in indices:
            self.stores[index].start()
            self.stored.append(index)

    def finish(self):
        self.store(*(index for index in range(len(self.stores)) if index not in self.stored))
        for store in self.stores:
            store.wait()


def staged_kernel(body, counts, *refs):
    refs = list(refs)

    def pull(number):
        taken = refs[:number]
        del refs[:number]
        return taken

    close, number, raw, close_outs, results = counts
    near, sources, raws = pull(close), pull(number), pull(raw)
    near_outs, targets, echoes = pull(close_outs), pull(results), pull(close_outs)
    held, outs, (in_sems, out_sems) = pull(number), pull(results), pull(2)
    stage = Stage(
        sources, held, in_sems, [*near_outs, *outs], [*echoes, *targets], out_sems
    )
    stage.start()
    body(stage, [*near, *held], raws, [*near_outs, *outs], refs)
    stage.finish()


def staged(
    body, inputs, outs, scratch, flops, raw=(), call_id=None, length=0, near=(), near_outs=()
):
    copies = [pltpu.VMEM(item.shape, item.dtype) for item in (*inputs, *outs)]
    stores = [*outs, *near_outs]
    sems = [pltpu.SemaphoreType.DMA((max(1, len(group)),)) for group in (inputs, stores)]
    needed = sum(
        math.prod(item.shape) * jnp.dtype(item.dtype).itemsize
        for item in copies + list(scratch)
        if getattr(item, "dtype", None) in (jnp.float32, jnp.bfloat16)
    )
    params = {} if call_id is None else {"collective_id": call_id, "has_side_effects": True}
    counts = (len(near), len(inputs), len(raw), len(near_outs), len(outs))
    results = pl.pallas_call(
        partial(staged_kernel, body, counts),
        out_shape=[pltpu.VMEM(item.shape, item.dtype) for item in near_outs]
        + [pltpu.HBM(item.shape, item.dtype) for item in stores],
        in_specs=[VMEM_SPEC] * len(near) + [HBM_SPEC] * (len(inputs) + len(raw)),
        out_specs=[VMEM_SPEC] * len(near_outs) + [HBM_SPEC] * len(stores),
        scratch_shapes=copies + sems + list(scratch),
        compiler_params=pltpu.CompilerParams(vmem_limit_bytes=needed + (6 << 20), **params),
        cost_estimate=pl.CostEstimate(
            flops=flops, bytes_accessed=length * 3_500_000, transcendentals=0
        ),
    )(*map(in_vmem, near), *map(in_hbm, (*inputs, *raw)))
    return list(results)


def greet(place, count, others=()):
    barrier = pltpu.get_barrier_semaphore()
    below, above = {"mp": place - 1}, {"mp": place + 1}

    @pl.when(place > 0)
    def _():
        pl.semaphore_signal(barrier, inc=1, device_id=below, device_id_type=MESH_ID)

    @pl.when(place < count - 1)
    def _():
        pl.semaphore_signal(barrier, inc=1, device_id=above, device_id_type=MESH_ID)

    signal_all(barrier, others)
    inside = jnp.logical_and(place > 0, place < count - 1)

    @pl.when(inside)
    def _():
        pl.semaphore_wait(barrier, 2 + len(others))

    @pl.when(jnp.logical_not(inside))
    def _():
        pl.semaphore_wait(barrier, 1 + len(others))


def views(refs, base=3):
    result = []
    for ref in refs:
        if len(ref.shape) == base:
            result.append(ref)
        else:
            result += [ref.at[slot] for slot in range(ref.shape[0])]
    return result


def line_sum_kernel(count, count_dp, extra, tiled, stage, held, raws, results, scratch):
    refs = list(scratch)

    def pull(number):
        taken = refs[:number]
        del refs[:number]
        return taken

    part_ref, base_ref, tile = held[0], held[1], held[2 + extra :]
    items, outs = views(held[2 : 2 + extra]), views(results[1 : 1 + extra], 2)
    out_ref, tile_out = results[0], results[1 + extra : 1 + extra + tiled]
    base_rows = base_ref.shape[0]
    inner, from_away, from_toward, toward_send, away_send, away_recv, toward_recv = pull(7)
    chunks = toward_send.shape[0]
    spread = Spread("dp", count_dp, *pull(3)) if tiled else None
    turn = pull(1)[0] if tiled else None
    sums = PieceSums(count_dp, items, outs, refs)
    place = lax.axis_index("mp")
    half = count // 2
    low_side = place < half
    toward = {"mp": jnp.where(low_side, place + 1, place - 1)}
    away = {"mp": jnp.where(low_side, place - 1, place + 1)}
    middle = jnp.logical_or(place == half - 1, place == half)
    outermost = jnp.logical_or(place == 0, place == count - 1)
    rows = part_ref.shape[0] // chunks
    others = [spread.peer(step) for step in range(1, count_dp)] if tiled else sums.peers()
    greet(place, count, others)

    def window(step):
        return pl.ds(pl.multiple_of(step * rows, rows), rows)

    def put(step, total):
        first = lax.rem(step * rows, base_rows)
        out_ref[window(step)] = total + base_ref[pl.ds(pl.multiple_of(first, rows), rows)]

    def push(step, source, inside):
        target = from_toward if inside else from_away
        recv = toward_recv if inside else away_recv
        return remote(
            source.at[window(step)],
            target.at[window(step)],
            toward_send.at[step],
            recv.at[step],
            toward,
        )

    def back(step, source):
        return remote(
            source.at[window(step)],
            from_toward.at[window(step)],
            away_send.at[step],
            toward_recv.at[step],
            away,
        )

    def gather_in(step):
        push(step, part_ref, False).wait_recv()
        inner[window(step)] = part_ref[window(step)] + from_away[window(step)]

    odd = lax.rem(lax.axis_index("dp"), 2) == 1
    if tiled:
        stage.wait()
        spread.held[spread.place] = tile[0][...]
        spread.start()

        @pl.when(jnp.logical_and(outermost, odd))
        def _():
            pl.semaphore_wait(turn, 1)

    def pass_turn():
        if tiled:

            @pl.when(jnp.logical_not(odd))
            def _():
                pl.semaphore_signal(
                    turn, inc=1, device_id=spread.peer(1), device_id_type=MESH_ID
                )

    @pl.when(outermost)
    def _():
        def leave(step, carry):
            push(step, part_ref, False).start()
            return carry

        lax.fori_loop(0, chunks, leave, 0)

    stage.wait()
    sums.begin()

    @pl.when(outermost)
    def _():

        def arrive(step, carry):
            push(step, part_ref, True).wait_recv()
            put(step, from_toward[window(step)])
            push(step, part_ref, False).wait_send()
            return carry

        if tiled:
            early = chunks * 3 // 8
            lax.fori_loop(0, early, arrive, 0)
            pass_turn()
            lax.fori_loop(early, chunks, arrive, 0)
        else:
            for low, high, phase in sums.moments(chunks):
                lax.fori_loop(low, high, arrive, 0)
                sums.advance(phase)

    lag = 2

    @pl.when(middle)
    def _():
        def finish(step):
            push(step, inner, True).wait_recv()
            push(step, inner, True).wait_send()
            total = inner[window(step)] + from_toward[window(step)]
            inner[window(step)] = total
            back(step, inner).start()
            put(step, total)

        def first(step, carry):
            gather_in(step)
            push(step, inner, True).start()
            return carry

        def both(step, carry):
            first(step, carry)
            finish(step - lag)
            return carry

        def last(step, carry):
            finish(step)
            return carry

        def drain(step, carry):
            back(step, inner).wait_send()
            return carry

        lax.fori_loop(0, lag, first, 0)
        for low, high, phase in sums.moments(chunks):
            lax.fori_loop(max(low, lag), high, both, 0)
            if high == chunks:
                lax.fori_loop(chunks - lag, chunks, last, 0)
            sums.advance(phase)
        lax.fori_loop(0, chunks, drain, 0)

    if count > 4:

        @pl.when(jnp.logical_not(jnp.logical_or(middle, outermost)))
        def _():
            def inwards(step, carry):
                gather_in(step)
                push(step, inner, False).start()
                return carry

            def outwards(step, carry):
                push(step, inner, True).wait_recv()
                back(step, from_toward).start()
                put(step, from_toward[window(step)])
                return carry

            def drain(step, carry):
                push(step, inner, False).wait_send()
                back(step, from_toward).wait_send()
                return carry

            lax.fori_loop(0, chunks, inwards, 0)
            for low, high, phase in sums.moments(chunks):
                lax.fori_loop(low, high, outwards, 0)
                sums.advance(phase)
            lax.fori_loop(0, chunks, drain, 0)

    sums.finish()
    if tiled:
        spread.take()
        tile_out[0][...] = spread.total()
        spread.finish()


def piece_shapes(items):
    count = lax.axis_size("dp")
    items = [item.reshape(item.shape[:-2] + (count, -1, item.shape[-1])) for item in items]
    shapes, shares = [], []
    for item in items:
        shapes += [item.shape[-2:]] * (item.shape[0] if item.ndim == 4 else 1)
        shares.append(jax.ShapeDtypeStruct(item.shape[:-3] + item.shape[-2:], jnp.float32))
    return items, shapes, shares


def line_sum(part, base, call_id, items=(), tile=None):
    items, shapes, shares = piece_shapes(items)
    count, count_dp = lax.axis_size("mp"), lax.axis_size("dp")
    rows, width = part.shape
    buffer = pltpu.VMEM((rows, width), jnp.float32)
    sems = pltpu.SemaphoreType.DMA((CHUNKS,))
    inputs = [base, *items]
    outs = list(shares)
    scratch = [buffer] * 3 + [sems] * 4
    if tile is not None:
        inputs.append(tile)
        outs.append(jax.ShapeDtypeStruct(tile.shape, jnp.float32))
        scratch += Spread.scratch(count_dp, tile.shape) + [pltpu.SemaphoreType.REGULAR]
    scratch += PieceSums.scratch(count_dp, shapes)
    total = jax.ShapeDtypeStruct((rows, width), jnp.float32)
    results = staged(
        partial(line_sum_kernel, count, count_dp, len(items), int(tile is not None)),
        inputs,
        outs,
        scratch,
        4 * rows * width,
        call_id=call_id,
        length=55,
        near=[part],
        near_outs=[total],
    )
    return results[0], results[-1], results[1:-1]


class LineScatter:
    def __init__(self, count, part, out, buffers, sems):
        self.count, self.part, self.out = count, part, out
        self.up_acc, self.down_acc, self.from_below, self.from_above = buffers
        self.up_send, self.down_send, self.up_recv, self.down_recv = sems
        self.place = lax.axis_index("mp")
        self.steps = self.up_send.shape[1]
        self.block = part.shape[0] // count
        self.rows = self.block // self.steps

    @staticmethod
    def scratch(count, shape, steps):
        sems = pltpu.SemaphoreType.DMA((count, steps))
        return [pltpu.VMEM(shape, jnp.float32)] * 4 + [sems] * 4

    def window(self, owner, step):
        return pl.ds(pl.multiple_of(owner * self.block + step * self.rows, self.rows), self.rows)

    def up(self, owner, step, source):
        where = self.window(owner, step)
        return remote(
            source.at[where],
            self.from_below.at[where],
            self.up_send.at[owner, step],
            self.up_recv.at[owner, step],
            {"mp": self.place + 1},
        )

    def down(self, owner, step, source):
        where = self.window(owner, step)
        return remote(
            source.at[where],
            self.from_above.at[where],
            self.down_send.at[owner, step],
            self.down_recv.at[owner, step],
            {"mp": self.place - 1},
        )

    def up_turn(self, index):
        place, part = self.place, self.part
        owner, step = self.count - 1 - index // self.steps, lax.rem(index, self.steps)

        @pl.when(jnp.logical_and(owner > place, place == 0))
        def _():
            self.up(owner, step, part).start()

        @pl.when(jnp.logical_and(owner > place, place > 0))
        def _():
            self.up(owner, step, part).wait_recv()
            where = self.window(owner, step)
            self.up_acc[where] = part[where] + self.from_below[where]
            self.up(owner, step, self.up_acc).start()

    def down_turn(self, index):
        place, part, count = self.place, self.part, self.count
        owner, step = index // self.steps, lax.rem(index, self.steps)

        @pl.when(jnp.logical_and(owner < place, place == count - 1))
        def _():
            self.down(owner, step, part).start()

        @pl.when(jnp.logical_and(owner < place, place < count - 1))
        def _():
            self.down(owner, step, part).wait_recv()
            where = self.window(owner, step)
            self.down_acc[where] = part[where] + self.from_above[where]
            self.down(owner, step, self.down_acc).start()

    def run(self, pauses=(), beside=None):
        turns, lag = self.count * self.steps, self.steps

        def staggered(first, second):
            def begin(index, carry):
                first(index)
                if beside is not None:
                    beside(index)
                return carry

            def both(index, carry):
                first(index)
                second(index - lag)
                if beside is not None:
                    beside(index)
                return carry

            def end(index, carry):
                second(index)
                return carry

            lax.fori_loop(0, lag, begin, 0)
            low = lag
            for share, action in pauses:
                high = lag + int((turns - lag) * share)
                lax.fori_loop(low, high, both, 0)
                action()
                low = high
            lax.fori_loop(low, turns, both, 0)
            lax.fori_loop(turns - lag, turns, end, 0)

        @pl.when(self.place < self.count // 2)
        def _():
            staggered(self.up_turn, self.down_turn)

        @pl.when(self.place >= self.count // 2)
        def _():
            staggered(self.down_turn, self.up_turn)

    def settle(self):
        place, rows = self.place, self.rows

        def one(step, carry):
            where = self.window(place, step)
            mine = pl.ds(pl.multiple_of(step * rows, rows), rows)
            self.out[mine] = self.part[where]

            @pl.when(place > 0)
            def _():
                self.up(place, step, self.part).wait_recv()
                self.out[mine] += self.from_below[where]

            @pl.when(place < self.count - 1)
            def _():
                self.down(place, step, self.part).wait_recv()
                self.out[mine] += self.from_above[where]

            return carry

        lax.fori_loop(0, self.steps, one, 0)

    def finish(self):
        place = self.place

        def one(index, carry):
            owner, step = index // self.steps, lax.rem(index, self.steps)

            @pl.when(owner > place)
            def _():
                self.up(owner, step, self.part).wait_send()

            @pl.when(owner < place)
            def _():
                self.down(owner, step, self.part).wait_send()

            return carry

        lax.fori_loop(0, self.count * self.steps, one, 0)


def line_scatter_kernel(count, stage, held, raws, results, scratch):
    own, sem = scratch[8:10]
    base, blocks = raws
    scatter = LineScatter(count, held[0], results[0], scratch[:4], scratch[4:8])
    convert = Convert(
        count, count * scatter.steps, blocks, results[1:], scratch[10], scratch[11]
    )
    rows = own.shape[0]
    load = pltpu.make_async_copy(
        base.at[pl.ds(pl.multiple_of(scatter.place * rows, rows), rows)], own, sem
    )
    load.start()
    convert.begin()
    greet(scatter.place, count)
    scatter.run((), convert.step)
    stage.store(1, 2, 3, 4)
    scatter.settle()
    load.wait()
    results[0][...] += own[...]
    scatter.finish()


def line_scatter(part, base, blocks, sizes, call_id):
    rows, width = part.shape
    count = lax.axis_size("mp")
    own = (rows // count, width)
    result, *weights = staged(
        partial(line_scatter_kernel, count),
        [],
        [jax.ShapeDtypeStruct(own, jnp.float32)]
        + [jax.ShapeDtypeStruct((size, count * blocks.shape[2]), jnp.bfloat16) for size in sizes],
        LineScatter.scratch(count, (rows, width), 8)
        + [pltpu.VMEM(own, jnp.float32), pltpu.SemaphoreType.DMA]
        + Convert.scratch(blocks.shape[1:]),
        2 * rows * width,
        [base, blocks],
        call_id=call_id,
        length=33,
        near=[part],
    )
    return result, weights


def line_gather_kernel(count, count_dp, extra, stage, held, raws, results, scratch):
    own_ref, out_ref = held[0], results[0]
    items, outs = views(held[1:]), views(results[1:], 2)
    up_send, down_send, up_recv, down_recv = scratch[:4]
    sums = PieceSums(count_dp, items, outs, scratch[4:])
    place = lax.axis_index("mp")
    steps = up_send.shape[1]
    block = own_ref.shape[0]
    rows = block // steps
    below, above = {"mp": place - 1}, {"mp": place + 1}
    greet(place, count, sums.peers())
    stage.wait(0)

    def window(owner, step):
        return pl.ds(pl.multiple_of(owner * block + step * rows, rows), rows)

    def up(owner, step):
        part = out_ref.at[window(owner, step)]
        return remote(part, part, up_send.at[owner, step], up_recv.at[owner, step], above)

    def down(owner, step):
        part = out_ref.at[window(owner, step)]
        return remote(part, part, down_send.at[owner, step], down_recv.at[owner, step], below)

    def begin(step, carry):
        out_ref[window(place, step)] = own_ref[pl.ds(pl.multiple_of(step * rows, rows), rows)]

        @pl.when(place < count - 1)
        def _():
            up(place, step).start()

        @pl.when(place > 0)
        def _():
            down(place, step).start()

        return carry

    lax.fori_loop(0, steps, begin, 0)
    stage.wait(*range(1, len(stage.loads)))
    sums.begin()

    def pass_on(index, carry):
        away, step = 1 + index // steps, lax.rem(index, steps)

        @pl.when(place - away >= 0)
        def _():
            up(place - away, step).wait_recv()

        @pl.when(jnp.logical_and(place - away >= 0, place < count - 1))
        def _():
            up(place - away, step).start()

        @pl.when(place + away < count)
        def _():
            down(place + away, step).wait_recv()

        @pl.when(jnp.logical_and(place + away < count, place > 0))
        def _():
            down(place + away, step).start()

        return carry

    for low, high, phase in sums.moments((count - 1) * steps):
        lax.fori_loop(low, high, pass_on, 0)
        sums.advance(phase)

    def drain(index, carry):
        owner, step = index // steps, lax.rem(index, steps)

        @pl.when(jnp.logical_and(owner <= place, place < count - 1))
        def _():
            up(owner, step).wait_send()

        @pl.when(jnp.logical_and(owner >= place, place > 0))
        def _():
            down(owner, step).wait_send()

        return carry

    lax.fori_loop(0, count * steps, drain, 0)
    sums.finish()


def line_gather(own, call_id, items=()):
    rows, width = own.shape
    count, count_dp = lax.axis_size("mp"), lax.axis_size("dp")
    sems = pltpu.SemaphoreType.DMA((count, 8))
    items, shapes, shares = piece_shapes(items)
    results = staged(
        partial(line_gather_kernel, count, count_dp, len(items)),
        [own, *items],
        shares,
        [sems] * 4 + PieceSums.scratch(count_dp, shapes),
        rows * width,
        call_id=call_id,
        length=38,
        near_outs=[jax.ShapeDtypeStruct((rows * count, width), jnp.float32)],
    )
    return results[0], results[-1], results[1:-1]


def dot(left, right, left_dim=1, right_dim=0):
    return lax.dot_general(
        left, right, (((left_dim,), (right_dim,)), ((), ())), preferred_element_type=jnp.float32
    )


def head_mask(width, copies):
    lane = lax.broadcasted_iota(jnp.int32, (1, width), 1)
    return [lane // HEAD_DIM == head for head in range(copies)]


def spread_heads(values):
    masks = head_mask(values.shape[1], values.shape[1] // HEAD_DIM)
    return jnp.concatenate([jnp.where(mask, values, jnp.zeros_like(values)) for mask in masks], 0)


def join_heads(values, heads):
    rows = values.shape[0] // heads
    masks = head_mask(values.shape[1], heads)
    return sum(
        jnp.where(mask, values[head * rows : (head + 1) * rows], 0.0)
        for head, mask in enumerate(masks)
    )


def split_three(values):
    first = values.astype(jnp.bfloat16)
    left = values - first.astype(jnp.float32)
    second = left.astype(jnp.bfloat16)
    third = (left - second.astype(jnp.float32)).astype(jnp.bfloat16)
    return first, second, third


def norm_rows(values):
    centered = values - jnp.mean(values, -1, keepdims=True)
    scale = lax.rsqrt(jnp.mean(centered * centered, -1, keepdims=True) + 1e-05)
    return centered * scale, scale


def norm_rows_back(upstream, gain, normed, scale):
    inner = upstream * gain
    return scale * (
        inner
        - jnp.mean(inner, -1, keepdims=True)
        - normed * jnp.mean(inner * normed, -1, keepdims=True)
    )


def embed(noisy, pixels, place):
    stacked = jnp.concatenate(split_three(noisy), 0)
    return dot(stacked, jnp.concatenate([pixels] * 3, 0), 0, 0) + place


def read_forward_kernel(
    noisy_ref,
    keep_ref,
    place_ref,
    pixels_ref,
    latents_ref,
    wide_gain_ref,
    gain_ref,
    query_weight_ref,
    pair_weight_ref,
    out_weight_ref,
    part_ref,
    pairs_ref,
    output_ref,
    queries_ref,
    normed_ref,
    scale_ref,
    side_ref,
    probs_ref,
):
    heads = query_weight_ref.shape[2] // HEAD_DIM

    @pl.when(pl.program_id(0) == 0)
    def _():
        normed, _ = norm_rows(latents_ref[...].astype(jnp.float32))
        low = (normed * wide_gain_ref[...]).astype(jnp.bfloat16)
        queries = dot(low, query_weight_ref[0]).astype(jnp.bfloat16)
        queries_ref[...] = spread_heads(queries * jnp.bfloat16(HEAD_DIM ** (-0.5)))

    normed, scale = norm_rows(embed(noisy_ref[0], pixels_ref[...], place_ref[...]))
    normed_ref[0] = normed
    scale_ref[0] = scale
    side = (normed * gain_ref[...]).astype(jnp.bfloat16)
    side_ref[0] = side.T
    keys = dot(side, pair_weight_ref[0]).astype(jnp.bfloat16)
    values = dot(side, pair_weight_ref[1]).astype(jnp.bfloat16)
    pairs_ref[0, 0] = keys
    pairs_ref[0, 1] = values
    scores = dot(keys, queries_ref[...], 1, 1)
    scores = jnp.where(keep_ref[0] > 0, scores, -1e30)
    top = jnp.max(scores, 0, keepdims=True)
    grown = jnp.exp(scores - top)
    probs = grown / jnp.sum(grown, 0, keepdims=True)
    probs_ref[0] = probs
    output = join_heads(dot(probs.astype(jnp.bfloat16), values, 0, 0), heads)
    output = output.astype(jnp.bfloat16)
    output_ref[0] = output
    part_ref[...] = dot(output, out_weight_ref[0])


def whole(shape):
    return pl.BlockSpec(shape, lambda b: (0,) * len(shape))


def each(shape):
    return pl.BlockSpec((1,) + shape, lambda b: (b,) + (0,) * len(shape))


def slot_of(shape, slot):
    return pl.BlockSpec(shape, lambda b: (slot,) + (0,) * (len(shape) - 1))


def read_forward(noisy, keep, place, pixels, latents, wide_gain, gain, wide, narrow, wideout):
    images, _, patches = noisy.shape
    count, d_lat = latents.shape
    d_if, local = narrow.shape[1:]
    stacked = local // HEAD_DIM * count
    return pl.pallas_call(
        read_forward_kernel,
        grid=(images,),
        out_shape=[
            pltpu.VMEM((images * count, d_lat), jnp.float32),
            pltpu.HBM((images, 2, patches, local), jnp.bfloat16),
            pltpu.HBM((images, count, local), jnp.bfloat16),
            pltpu.HBM((stacked, local), jnp.bfloat16),
            pltpu.HBM((images, patches, d_if), jnp.float32),
            pltpu.HBM((images, patches, 1), jnp.float32),
            pltpu.HBM((images, d_if, patches), jnp.bfloat16),
            pltpu.HBM((images, patches, stacked), jnp.float32),
        ],
        in_specs=[
            each(noisy.shape[1:]),
            each((patches, 1)),
            whole((patches, d_if)),
            whole(pixels.shape),
            whole(latents.shape),
            whole((1, d_lat)),
            whole((1, d_if)),
            slot_of((1, d_lat, local), 0),
            slot_of((2, d_if, local), 0),
            slot_of((1, local, d_lat), 0),
        ],
        out_specs=[
            pl.BlockSpec((count, d_lat), lambda b: (b, 0)),
            each((2, patches, local)),
            each((count, local)),
            whole((stacked, local)),
            each((patches, d_if)),
            each((patches, 1)),
            each((d_if, patches)),
            each((patches, stacked)),
        ],
        compiler_params=pltpu.CompilerParams(vmem_limit_bytes=52 << 20),
        cost_estimate=pl.CostEstimate(
            flops=10**10, bytes_accessed=30 * 10**6, transcendentals=2 * 10**6
        ),
    )(in_hbm(noisy), in_hbm(keep), in_hbm(place), in_hbm(pixels), in_hbm(latents), in_hbm(wide_gain), in_hbm(gain), in_hbm(wide), in_hbm(narrow), in_hbm(wideout))


def read_backward_kernel(
    noisy_ref,
    latents_ref,
    wide_gain_ref,
    gain_ref,
    query_weight_ref,
    pair_weight_ref,
    out_weight_ref,
    pairs_ref,
    output_ref,
    queries_ref,
    normed_ref,
    scale_ref,
    side_ref,
    probs_ref,
    grad_ref,
    lead_ref,
    wide_grad_ref,
    narrow_grad_ref,
    latents_grad_ref,
    wide_gain_grad_ref,
    gain_grad_ref,
    embed_grad_ref,
    low_ref,
    returned_ref,
):
    step, steps = pl.program_id(0), pl.num_programs(0)
    heads = query_weight_ref.shape[2] // HEAD_DIM

    @pl.when(step == 0)
    def _():
        normed, _ = norm_rows(latents_ref[...].astype(jnp.float32))
        low_ref[...] = (normed * wide_gain_ref[...]).astype(jnp.bfloat16)
        for ref in (
            wide_grad_ref,
            narrow_grad_ref,
            latents_grad_ref,
            gain_grad_ref,
            embed_grad_ref,
            returned_ref,
        ):
            ref[...] = jnp.zeros_like(ref)

    normed, scale, side, probs = normed_ref[0], scale_ref[0], side_ref[0], probs_ref[0]
    keys, values, queries = pairs_ref[0, 0], pairs_ref[0, 1], queries_ref[...]
    branch = grad_ref[...].astype(jnp.bfloat16)
    latents_grad_ref[...] += lead_ref[...] * grad_ref[...]
    wide_grad_ref[1] += dot(branch, output_ref[0], 0, 0)
    upstream = spread_heads(dot(branch, out_weight_ref[0], 1, 1).astype(jnp.bfloat16))
    value_grad = dot(probs.astype(jnp.bfloat16), upstream).astype(jnp.bfloat16)
    prob_grad = dot(values, upstream, 1, 1)
    inner = jnp.sum(prob_grad * probs, 0, keepdims=True)
    score_grad = (probs * (prob_grad - inner)).astype(jnp.bfloat16)
    key_grad = dot(score_grad, queries).astype(jnp.bfloat16)
    query_grad = join_heads(dot(score_grad, keys, 0, 0), heads) * HEAD_DIM ** (-0.5)
    query_grad = query_grad.astype(jnp.bfloat16)
    wide_grad_ref[0] += dot(low_ref[...], query_grad, 0, 0)
    returned_ref[...] += dot(query_grad, query_weight_ref[0], 1, 1)
    narrow_grad_ref[0] += dot(side, key_grad)
    narrow_grad_ref[1] += dot(side, value_grad)
    side_grad = dot(key_grad, pair_weight_ref[0], 1, 1) + dot(value_grad, pair_weight_ref[1], 1, 1)
    gain_grad_ref[...] += jnp.sum(side_grad * normed, 0, keepdims=True)
    back = norm_rows_back(side_grad, gain_ref[...], normed, scale)
    embed_grad_ref[...] += embed_back(noisy_ref[0], back)

    @pl.when(step == steps - 1)
    def _():
        normed, scale = norm_rows(latents_ref[...].astype(jnp.float32))
        returned = returned_ref[...]
        wide_gain_grad_ref[...] = jnp.sum(returned * normed, 0, keepdims=True)
        latents_grad_ref[...] += norm_rows_back(returned, wide_gain_ref[...], normed, scale)


def embed_back(noisy, back):
    first, second, _ = split_three(noisy)
    high = back.astype(jnp.bfloat16)
    low = (back - high.astype(jnp.float32)).astype(jnp.bfloat16)
    rows = noisy.shape[0]
    both = dot(jnp.concatenate([first, second], 0), high)
    return both[:rows] + both[rows:] + dot(first, low)


def read_backward(
    noisy,
    latents,
    wide_gain,
    gain,
    wide,
    narrow,
    wideout,
    pairs,
    output,
    queries,
    normed,
    scale,
    side,
    probs,
    grad,
    lead,
):
    images, rows, patches = noisy.shape
    count, d_lat = latents.shape
    d_if, local = narrow.shape[1:]
    stacked = local // HEAD_DIM * count
    results = [
        (2, d_lat, local),
        (2, d_if, local),
        (count, d_lat),
        (1, d_lat),
        (1, d_if),
        (rows, d_if),
    ]
    return pl.pallas_call(
        read_backward_kernel,
        grid=(images,),
        out_shape=[pltpu.HBM(shape, jnp.float32) for shape in results],
        in_specs=[
            each(noisy.shape[1:]),
            whole(latents.shape),
            whole((1, d_lat)),
            whole((1, d_if)),
            slot_of((1, d_lat, local), 0),
            slot_of((2, d_if, local), 0),
            slot_of((1, local, d_lat), 0),
            each((2, patches, local)),
            each((count, local)),
            whole((stacked, local)),
            each((patches, d_if)),
            each((patches, 1)),
            each((d_if, patches)),
            each((patches, stacked)),
            pl.BlockSpec((count, d_lat), lambda b: (b, 0)),
            whole((1, 1)),
        ],
        out_specs=[whole(shape) for shape in results],
        scratch_shapes=[
            pltpu.VMEM((count, d_lat), jnp.bfloat16),
            pltpu.VMEM((count, d_lat), jnp.float32),
        ],
        compiler_params=pltpu.CompilerParams(vmem_limit_bytes=52 << 20),
        cost_estimate=pl.CostEstimate(
            flops=2 * 10**10, bytes_accessed=30 * 10**6, transcendentals=2 * 10**6
        ),
    )(*map(in_hbm, (noisy, latents, wide_gain, gain, wide, narrow, wideout, pairs, output, queries, normed, scale, side, probs)), in_vmem(grad), in_hbm(lead))


def rows_of(rows, width):
    return pl.BlockSpec((rows, width), lambda b: (b, 0))


def attend_few(keys, values, queries):
    scores = dot(keys, queries, 1, 1)
    top = jnp.max(scores, 0, keepdims=True)
    grown = jnp.exp(scores - top)
    summed = jnp.sum(grown, 0, keepdims=True)
    probs = (grown / summed).astype(jnp.bfloat16)
    return dot(probs, values, 0, 0), top + jnp.log(summed)


def scaled_heads(queries):
    return spread_heads(queries * jnp.bfloat16(HEAD_DIM ** (-0.5)))


def self_forward_kernel(
    latent_ref, gain_ref, q_ref, k_ref, v_ref, out_weight_ref, part_ref, triple_ref, output_ref, total_ref, low_ref
):
    heads = q_ref.shape[2] // HEAD_DIM
    normed, _ = norm_rows(latent_ref[...])
    low = (normed * gain_ref[...]).astype(jnp.bfloat16)
    low_ref[...] = low
    queries, keys, values = (dot(low, ref[0]).astype(jnp.bfloat16) for ref in (q_ref, k_ref, v_ref))
    for index, item in enumerate((queries, keys, values)):
        triple_ref[0, index] = item
    output, total_ref[0] = attend_few(keys, values, scaled_heads(queries))
    output = join_heads(output, heads).astype(jnp.bfloat16)
    output_ref[0] = output
    part_ref[...] = dot(output, out_weight_ref[0])


def self_forward(latent, gain, wide, wideout, images):
    total, d_lat = latent.shape
    count, local = total // images, wide.shape[2]
    stacked = local // HEAD_DIM * count
    return pl.pallas_call(
        self_forward_kernel,
        grid=(images,),
        out_shape=[
            pltpu.VMEM((total, d_lat), jnp.float32),
            pltpu.HBM((images, 3, count, local), jnp.bfloat16),
            pltpu.HBM((images, count, local), jnp.bfloat16),
            pltpu.HBM((images, 1, stacked), jnp.float32),
            pltpu.HBM((total, d_lat), jnp.bfloat16),
        ],
        in_specs=[rows_of(count, d_lat), whole((1, d_lat))]
        + [slot_of((1, d_lat, local), slot) for slot in (1, 2, 3)]
        + [slot_of((1, local, d_lat), 1)],
        out_specs=[
            rows_of(count, d_lat),
            each((3, count, local)),
            each((count, local)),
            each((1, stacked)),
            rows_of(count, d_lat),
        ],
        compiler_params=pltpu.CompilerParams(vmem_limit_bytes=20 << 20),
        cost_estimate=pl.CostEstimate(
            flops=3 * 10**9, bytes_accessed=12 * 10**6, transcendentals=3 * 10**5
        ),
    )(in_vmem(latent), in_hbm(gain), in_hbm(wide), in_hbm(wide), in_hbm(wide), in_hbm(wideout))


def self_backward_kernel(
    grad_ref,
    latent_ref,
    gain_ref,
    q_ref,
    k_ref,
    v_ref,
    out_weight_ref,
    triple_ref,
    output_ref,
    total_ref,
    low_ref,
    part_ref,
    first_ref,
    last_ref,
    gain_grad_ref,
    branches,
    outputs,
    grads,
    lows,
):
    step, steps = pl.program_id(0), pl.num_programs(0)
    heads = q_ref.shape[2] // HEAD_DIM
    count = grad_ref.shape[0]
    mine = pl.ds(pl.multiple_of(step * count, count), count)
    normed, scale = norm_rows(latent_ref[...])
    branch = grad_ref[...].astype(jnp.bfloat16)
    branches[mine] = branch
    outputs[mine] = output_ref[0]
    lows[mine] = low_ref[...]
    upstream = spread_heads(dot(branch, out_weight_ref[0], 1, 1).astype(jnp.bfloat16))
    keys, values = triple_ref[0, 1], triple_ref[0, 2]
    queries = scaled_heads(triple_ref[0, 0])
    probs = jnp.exp(dot(keys, queries, 1, 1) - total_ref[0])
    value_grad = dot(probs.astype(jnp.bfloat16), upstream).astype(jnp.bfloat16)
    prob_grad = dot(values, upstream, 1, 1)
    inner = jnp.sum(prob_grad * probs, 0, keepdims=True)
    score_grad = (probs * (prob_grad - inner)).astype(jnp.bfloat16)
    key_grad = dot(score_grad, queries).astype(jnp.bfloat16)
    query_grad = join_heads(dot(score_grad, keys, 0, 0), heads) * HEAD_DIM ** (-0.5)
    query_grad = query_grad.astype(jnp.bfloat16)
    part = (
        dot(query_grad, q_ref[0], 1, 1)
        + dot(key_grad, k_ref[0], 1, 1)
        + dot(value_grad, v_ref[0], 1, 1)
    )
    for index, item in enumerate((query_grad, key_grad, value_grad)):
        grads[index, mine] = item
    gain_part = jnp.sum(part * normed, 0, keepdims=True)
    gain_grad_ref[...] = gain_part + jnp.where(step == 0, 0.0, gain_grad_ref[...])
    part_ref[...] = norm_rows_back(part, gain_ref[...], normed, scale)

    @pl.when(step == steps - 1)
    def _():
        turned = lows[...].T
        first_ref[0] = dot(turned, grads[0])
        first_ref[1] = dot(turned, grads[1])
        last_ref[0] = dot(turned, grads[2])
        last_ref[1] = dot(branches[...], outputs[...], 0, 0)


def self_backward(grad, latent, gain, wide, wideout, triple, output, total, low):
    rows, d_lat = latent.shape
    images, _, count, local = triple.shape
    stacked = local // HEAD_DIM * count
    weight = pltpu.HBM((2, d_lat, local), jnp.float32)
    return pl.pallas_call(
        self_backward_kernel,
        grid=(images,),
        out_shape=[pltpu.VMEM((rows, d_lat), jnp.float32)]
        + [weight] * 2
        + [pltpu.HBM((1, d_lat), jnp.float32)],
        in_specs=[rows_of(count, d_lat), rows_of(count, d_lat), whole((1, d_lat))]
        + [slot_of((1, d_lat, local), slot) for slot in (1, 2, 3)]
        + [
            slot_of((1, local, d_lat), 1),
            each((3, count, local)),
            each((count, local)),
            each((1, stacked)),
            rows_of(count, d_lat),
        ],
        out_specs=[rows_of(count, d_lat)] + [whole((2, d_lat, local))] * 2 + [whole((1, d_lat))],
        scratch_shapes=[
            pltpu.VMEM((rows, d_lat), jnp.bfloat16),
            pltpu.VMEM((rows, local), jnp.bfloat16),
            pltpu.VMEM((3, rows, local), jnp.bfloat16),
            pltpu.VMEM((rows, d_lat), jnp.bfloat16),
        ],
        compiler_params=pltpu.CompilerParams(vmem_limit_bytes=28 << 20),
        cost_estimate=pl.CostEstimate(
            flops=6 * 10**9, bytes_accessed=16 * 10**6, transcendentals=3 * 10**5
        ),
    )(in_vmem(grad), in_hbm(latent), in_hbm(gain), in_hbm(wide), in_hbm(wide), in_hbm(wide), in_hbm(wideout), in_hbm(triple), in_hbm(output), in_hbm(total), in_hbm(low))


def feed_forward_kernel(
    latent_ref, gain_ref, up_ref, down_ref, part_ref, active_ref, slope_ref, low_ref
):
    @pl.when(pl.program_id(0) == 0)
    def _():
        normed, _ = norm_rows(latent_ref[...])
        low_ref[...] = (normed * gain_ref[...]).astype(jnp.bfloat16)

    hidden = dot(low_ref[...], up_ref[0])
    share = 0.5 * (1.0 + lax.erf(hidden * math.sqrt(0.5)))
    density = jnp.exp(-0.5 * hidden * hidden) * (1.0 / math.sqrt(2.0 * math.pi))
    active = (hidden * share).astype(jnp.bfloat16)
    active_ref[0] = active
    slope_ref[0] = share + hidden * density
    part = dot(active, down_ref[0])

    @pl.when(pl.program_id(0) == 0)
    def _():
        part_ref[...] = part

    @pl.when(pl.program_id(0) > 0)
    def _():
        part_ref[...] += part


def feed_forward(latent, gain, wide, wideout):
    rows, d_lat = latent.shape
    local = wide.shape[2]
    return pl.pallas_call(
        feed_forward_kernel,
        grid=(4,),
        out_shape=[
            pltpu.VMEM((rows, d_lat), jnp.float32),
            pltpu.HBM((4, rows, local), jnp.bfloat16),
            pltpu.HBM((4, rows, local), jnp.float32),
            pltpu.HBM((rows, d_lat), jnp.bfloat16),
        ],
        in_specs=[
            whole((rows, d_lat)),
            whole((1, d_lat)),
            pl.BlockSpec((1, d_lat, local), lambda s: (4 + s, 0, 0)),
            pl.BlockSpec((1, local, d_lat), lambda s: (2 + s, 0, 0)),
        ],
        out_specs=[
            whole((rows, d_lat)),
            each((rows, local)),
            each((rows, local)),
            whole((rows, d_lat)),
        ],
        compiler_params=pltpu.CompilerParams(vmem_limit_bytes=24 << 20),
        cost_estimate=pl.CostEstimate(
            flops=4 * 10**9, bytes_accessed=14 * 10**6, transcendentals=10**6
        ),
    )(in_vmem(latent), in_hbm(gain), in_hbm(wide), in_hbm(wideout))


def feed_backward_kernel(
    grad_ref,
    latent_ref,
    gain_ref,
    up_ref,
    down_ref,
    active_ref,
    slope_ref,
    low_ref,
    part_ref,
    up_first_ref,
    up_last_ref,
    down_grad_ref,
    gain_grad_ref,
    branch,
    branch_turned,
    low_turned,
    total,
):
    step, steps = pl.program_id(0), pl.num_programs(0)

    @pl.when(step == 0)
    def _():
        low = grad_ref[...].astype(jnp.bfloat16)
        branch[...] = low
        branch_turned[...] = low.T
        low_turned[...] = low_ref[...].T
        total[...] = jnp.zeros_like(total)

    active_grad = dot(branch[...], down_ref[0], 1, 1)
    hidden_grad = (active_grad * slope_ref[0]).astype(jnp.bfloat16)
    down_grad_ref[0] = dot(branch_turned[...], active_ref[0])
    total[...] += dot(hidden_grad, up_ref[0], 1, 1)
    up_grad = dot(low_turned[...], hidden_grad)

    @pl.when(step < 2)
    def _():
        up_first_ref[0] = up_grad

    @pl.when(step >= 2)
    def _():
        up_last_ref[0] = up_grad

    @pl.when(step == steps - 1)
    def _():
        normed, scale = norm_rows(latent_ref[...])
        part = total[...]
        gain_grad_ref[...] = jnp.sum(part * normed, 0, keepdims=True)
        part_ref[...] = norm_rows_back(part, gain_ref[...], normed, scale)


def feed_backward(grad, latent, gain, wide, wideout, active, slope, low):
    rows, d_lat = latent.shape
    local = wide.shape[2]
    return pl.pallas_call(
        feed_backward_kernel,
        grid=(4,),
        out_shape=[
            pltpu.VMEM((rows, d_lat), jnp.float32),
            pltpu.HBM((2, d_lat, local), jnp.float32),
            pltpu.HBM((2, d_lat, local), jnp.float32),
            pltpu.HBM((4, d_lat, local), jnp.float32),
            pltpu.HBM((1, d_lat), jnp.float32),
        ],
        in_specs=[
            whole((rows, d_lat)),
            whole((rows, d_lat)),
            whole((1, d_lat)),
            pl.BlockSpec((1, d_lat, local), lambda s: (4 + s, 0, 0)),
            pl.BlockSpec((1, local, d_lat), lambda s: (2 + s, 0, 0)),
            each((rows, local)),
            each((rows, local)),
            whole((rows, d_lat)),
        ],
        out_specs=[
            whole((rows, d_lat)),
            pl.BlockSpec((1, d_lat, local), lambda s: (jnp.minimum(s, 1), 0, 0)),
            pl.BlockSpec((1, d_lat, local), lambda s: (jnp.maximum(s - 2, 0), 0, 0)),
            each((d_lat, local)),
            whole((1, d_lat)),
        ],
        scratch_shapes=[
            pltpu.VMEM((rows, d_lat), jnp.bfloat16),
            pltpu.VMEM((d_lat, rows), jnp.bfloat16),
            pltpu.VMEM((d_lat, rows), jnp.bfloat16),
            pltpu.VMEM((rows, d_lat), jnp.float32),
        ],
        compiler_params=pltpu.CompilerParams(vmem_limit_bytes=36 << 20),
        cost_estimate=pl.CostEstimate(
            flops=9 * 10**9, bytes_accessed=26 * 10**6, transcendentals=0
        ),
    )(in_vmem(grad), in_hbm(latent), in_hbm(gain), in_hbm(wide), in_hbm(wideout), in_hbm(active), in_hbm(slope), in_hbm(low))


def write_kernel(stage, held, raws, results, scratch):
    (
        own_weight_ref,
        weight_total_ref,
        latent_ref,
        noisy_ref,
        noise_ref,
        keep_ref,
        place_ref,
        pixels_ref,
        wide_gain_ref,
        gain_ref,
        key_weight_ref,
        value_weight_ref,
        query_weight_ref,
        out_weight_ref,
    ) = held
    (
        latent_grad_ref,
        key_grad_ref,
        value_grad_ref,
        query_grad_ref,
        out_grad_ref,
        wide_gain_grad_ref,
        gain_grad_ref,
        embed_grad_ref,
        head_grad_ref,
        loss_ref,
    ) = results
    queries, outputs, upstream, query_grads, normed_ref, scale_ref = scratch
    stage.wait(*range(10))
    patches, width = queries.shape
    group = 4 * HEAD_DIM
    groups = width // group
    latents = latent_ref.shape[0]
    rows = 4 * latents
    weight, weight_total = own_weight_ref[:1, :1], weight_total_ref[:1, :1]

    latent_normed, latent_scale = norm_rows(latent_ref[...])
    latent_low = (latent_normed * wide_gain_ref[...]).astype(jnp.bfloat16)
    interface = embed(noisy_ref[...], pixels_ref[0], place_ref[...])
    normed, scale = norm_rows(interface)
    normed_ref[...] = normed
    scale_ref[...] = scale
    outer_low = (normed * gain_ref[1:2]).astype(jnp.bfloat16)
    stage.wait(10, 11)
    keys = dot(latent_low, key_weight_ref[...]).astype(jnp.bfloat16)
    values = dot(latent_low, value_weight_ref[...]).astype(jnp.bfloat16)
    stage.wait(12, 13)
    queries[...] = dot(outer_low, query_weight_ref[...]).astype(jnp.bfloat16)

    def part(values, index):
        return values[:, index * group : (index + 1) * group]

    def by_head(values):
        return values.reshape(4, latents, patches)

    def group_probs(index):
        scores = by_head(dot(scaled_heads(part(keys, index)), part(queries, index), 1, 1))
        grown = jnp.exp(scores - jnp.max(scores, 1, keepdims=True))
        return grown / jnp.sum(grown, 1, keepdims=True)

    for index in range(groups):
        probs = group_probs(index).reshape(rows, patches).astype(jnp.bfloat16)
        output = dot(probs, spread_heads(part(values, index)), 0, 0)
        outputs[:, index * group : (index + 1) * group] = output.astype(jnp.bfloat16)

    outer = interface + dot(outputs[...], out_weight_ref[...], 1, 1)
    final_normed, final_scale = norm_rows(outer)
    final_low = (final_normed * gain_ref[2:3]).astype(jnp.bfloat16)
    head = pixels_ref[1]
    difference = dot(head, final_low, 1, 1) - noise_ref[...]
    masked = weight * keep_ref[...] * difference
    loss_ref[...] = jnp.full(loss_ref.shape, jnp.sum(masked * difference))
    predict_grad = (2.0 * masked / weight_total).astype(jnp.bfloat16)
    head_grad_ref[...] = dot(predict_grad, final_low)
    final_grad = dot(predict_grad, head, 0, 0)
    gain_final = jnp.sum(final_grad * final_normed, 0, keepdims=True)
    outer_grad = norm_rows_back(final_grad, gain_ref[2:3], final_normed, final_scale)
    branch = outer_grad.astype(jnp.bfloat16)
    out_grad_ref[...] = dot(branch, outputs[...], 0, 0)
    stage.store(4)
    upstream[...] = dot(branch, out_weight_ref[...]).astype(jnp.bfloat16)

    key_grads, value_grads = [], []
    for index in range(groups):
        probs = group_probs(index)
        low = probs.reshape(rows, patches).astype(jnp.bfloat16)
        above = part(upstream, index)
        value_grads.append(join_heads(dot(low, above), 4).astype(jnp.bfloat16))
        prob_grad = by_head(dot(spread_heads(part(values, index)), above, 1, 1))
        inner = jnp.sum(prob_grad * probs, 1, keepdims=True)
        score_grad = (probs * (prob_grad - inner)).reshape(rows, patches).astype(jnp.bfloat16)
        key_grad = join_heads(dot(score_grad, part(queries, index)), 4) * HEAD_DIM ** (-0.5)
        key_grads.append(key_grad.astype(jnp.bfloat16))
        query_grad = dot(score_grad, scaled_heads(part(keys, index)), 0, 0)
        query_grads[:, index * group : (index + 1) * group] = query_grad.astype(jnp.bfloat16)
    key_grad, value_grad = (jnp.concatenate(item, 1) for item in (key_grads, value_grads))

    turned = latent_low.T
    key_grad_ref[...] = dot(turned, key_grad)
    value_grad_ref[...] = dot(turned, value_grad)
    stage.store(1, 2)
    latent_part = dot(key_grad, key_weight_ref[...], 1, 1) + dot(
        value_grad, value_weight_ref[...], 1, 1
    )
    wide_gain_grad_ref[...] = jnp.sum(latent_part * latent_normed, 0, keepdims=True)
    latent_grad_ref[...] = norm_rows_back(
        latent_part, wide_gain_ref[...], latent_normed, latent_scale
    )
    normed, scale = normed_ref[...], scale_ref[...]
    outer_low = (normed * gain_ref[1:2]).astype(jnp.bfloat16)
    query_grad_ref[...] = dot(outer_low, query_grads[...], 0, 0)
    stage.store(3)
    outer_part = dot(query_grads[...], query_weight_ref[...], 1, 1)
    gain_outer = jnp.sum(outer_part * normed, 0, keepdims=True)
    gain_grad_ref[...] = jnp.concatenate([gain_outer, gain_final], 0)
    back = outer_grad + norm_rows_back(outer_part, gain_ref[1:2], normed, scale)
    embed_grad_ref[...] = embed_back(noisy_ref[...], back)


def write_stage(
    own_weight, weight_total, latent, noisy, noise, keep, place, pixels, wide_gain, gains, weights
):
    latents, d_lat = latent.shape
    rows, patches = noisy.shape
    d_if = place.shape[1]
    width = weights[0].shape[1]
    results = [
        (latents, d_lat),
        (d_lat, width),
        (d_lat, width),
        (d_if, width),
        (d_if, width),
        (1, d_lat),
        (2, d_if),
        (rows, d_if),
        (rows, d_if),
        (8, 128),
    ]
    wide = pltpu.VMEM((patches, width), jnp.bfloat16)
    return staged(
        write_kernel,
        [
            own_weight,
            weight_total,
            latent,
            noisy,
            noise,
            keep,
            place,
            pixels,
            wide_gain,
            gains,
            *weights,
        ],
        [jax.ShapeDtypeStruct(shape, jnp.float32) for shape in results],
        [wide] * 4
        + [pltpu.VMEM((patches, d_if), jnp.float32), pltpu.VMEM((patches, 1), jnp.float32)],
        15 * 10**9,
        length=27,
    )


def adam_update(master, first, second, gradient, scale):
    clipped = gradient * scale
    moment = adam_beta * first + (1.0 - adam_beta) * clipped
    square = adam_beta * second + (1.0 - adam_beta) * clipped * clipped
    fixed_first = moment / (1.0 - adam_beta**STEP)
    fixed_second = square / (1.0 - adam_beta**STEP)
    updated = master - learning_rate * (
        fixed_first / (jnp.sqrt(fixed_second) + adam_eps) + weight_decay * master
    )
    return (updated, moment, square)


def sum_rows(values):
    return jnp.sum(values.reshape(-1, 8, values.shape[-1]), 0)


def closing_kernel(count, count_dp, sizes, stage, held, raws, results, scratch):
    refs, given = list(scratch), list(held)

    def pull(number, source=None):
        source = refs if source is None else source
        taken = source[:number]
        del source[:number]
        return taken

    number, finished = sizes
    items, small_parts = views(pull(number, given)), pull(10, given)
    loss_tile, weight_tile = pull(2, given)
    done = views(pull(finished, given), 2)
    wide_out, narrow_out, turned_out, last_out, latents_out, rest_out, stats = results
    latents_item, rest_item, columns, column_sems = pull(4)
    number = len(items)
    shares = pull(number + 2)
    each = count_dp.bit_length() + 1
    sums = PieceSums(count_dp, items, shares[:number], pull(number * each))
    tiny = PieceSums(count_dp, [latents_item, rest_item], shares[number:], pull(2 * each))
    (write_share,) = pull(1)
    scatter = LineScatter(count, columns, write_share, pull(4), pull(4))
    small = [Spread("mp", count, *pull(3)) for _ in range(2)]
    over_dp, over_mp = Spread("dp", count_dp, *pull(3)), Spread("mp", count, *pull(3))

    column_loads, low = [], 0
    block, local = columns.shape[0] // count, columns.shape[1]
    for source in raws:
        rows = source.shape[0]
        for owner in range(count):
            column_loads.append(
                pltpu.make_async_copy(
                    source.at[:, pl.ds(owner * local, local)],
                    columns.at[pl.ds(owner * block + low, rows)],
                    column_sems.at[len(column_loads)],
                )
            )
        low += rows
    for load in column_loads:
        load.start()
    barrier = pltpu.get_barrier_semaphore()
    others = [over_dp.peer(step) for step in range(1, count_dp)]
    others += [over_mp.peer(step) for step in range(1, count)]
    signal_all(barrier, others)
    stage.wait()
    (latent_total, *gains, gain_side, gain_pair, side_embed, own_embed, head_grad) = small_parts
    d_if = gain_side.shape[1]
    lanes = d_if // count_dp
    width = latents_item.shape[2]
    rest_item[...] = jnp.zeros_like(rest_item)
    rows = []
    for gain in gains:
        rows += [gain[:, :d_if], gain[:, d_if:]]
    rows += [gain_side[...], gain_pair[...]]
    blocks = [(0, jnp.concatenate(rows, 0)), (16, side_embed[...] + own_embed[...]), (32, head_grad[...])]
    for piece in range(count_dp):
        latents_item[piece] = latent_total[:, piece * width : (piece + 1) * width]
        for first, block in blocks:
            rest_item[piece, pl.ds(first, block.shape[0]), :lanes] = block[
                :, piece * lanes : (piece + 1) * lanes
            ]
    pl.semaphore_wait(barrier, len(others))

    tiny.begin()
    sums.begin()
    for load in column_loads:
        load.wait()
    tiny.advance(1)

    def early():
        sums.advance(1)
        tiny.advance(2)

    def middle():
        for phase in range(3, tiny.bits + 1):
            tiny.advance(phase)
        for spread, share in zip(small, shares[-2:]):
            spread.held[spread.place] = share[...]
            spread.start()

    scatter.run([(0.0, early), (0.35, middle), (0.75, lambda: sums.advance(2))])
    for phase in range(3, sums.bits + 1):
        sums.advance(phase)
    scatter.settle()

    self_in_2, self_out, read_query, read_out, read_key, read_value = shares[:6]
    self_in_0, self_in_1 = done[:2]
    up, down = done[2:6], done[6:10]
    lat_rows, if_rows = self_out.shape[0], read_key.shape[0]
    write_key, write_value = (write_share.at[pl.ds(i * lat_rows, lat_rows)] for i in range(2))
    write_query, write_out = (
        write_share.at[pl.ds(2 * lat_rows + i * if_rows, if_rows)] for i in range(2)
    )
    square = 0.0

    def keep(out, gradient, turn=False):
        nonlocal square
        value = gradient[...]
        square = square + sum_rows(value * value)
        out[...] = value.T if turn else value

    wide = [read_query, self_in_0, self_in_1, self_in_2] + up + [write_key, write_value]
    for slot, gradient in enumerate(wide):
        keep(wide_out.at[slot], gradient)
    for slot, gradient in enumerate([read_key, read_value, write_query]):
        keep(narrow_out.at[slot], gradient)
    for slot, gradient in enumerate([read_out, self_out] + down):
        keep(turned_out.at[slot], gradient, True)
    keep(last_out, write_out)
    stage.store(0, 1, 2, 3)
    for spread in small:
        spread.take()
    latents, rest = (spread.total() for spread in small)
    latents_out[...] = latents
    rest_out[...] = rest
    lead = (over_mp.place == 0).astype(jnp.float32)
    local = jnp.sum(square) + lead * (
        jnp.sum(sum_rows(latents * latents)) + jnp.sum(sum_rows(rest * rest))
    )
    lane = lax.broadcasted_iota(jnp.int32, (8, 128), 1)
    value = jnp.where(lane == 0, local, loss_tile[...])
    for spread in (over_dp, over_mp):
        spread.held[spread.place] = value
        spread.start()
        spread.take()
        value = spread.total()
    stats[...] = jnp.where(lane == 0, jnp.sqrt(value), value / weight_tile[...])
    sums.finish()
    tiny.finish()
    scatter.finish()
    for spread in small + [over_dp, over_mp]:
        spread.finish()


def closing(items, small_parts, tiles, done, write_shares, call_id):
    items, shapes, _ = piece_shapes(items)
    count, count_dp = lax.axis_size("mp"), lax.axis_size("dp")
    latents, d_lat = small_parts[0].shape
    lat_rows, local = done[0].shape[1:]
    if_rows = write_shares[2].shape[0]
    extra = [(latents, d_lat // count_dp), (48, 128)]
    block = (sum(item.shape[0] for item in write_shares), local)
    columns = (count * block[0], local)
    outs = [
        (10, lat_rows, local),
        (3, if_rows, local),
        (6, local, lat_rows),
        (if_rows, local),
        *extra,
        (8, 128),
    ]
    shapes = shapes + extra
    scratch = (
        [pltpu.VMEM((count_dp,) + shape, jnp.float32) for shape in extra]
        + [
            pltpu.VMEM(columns, jnp.float32),
            pltpu.SemaphoreType.DMA((count * len(write_shares),)),
        ]
        + [pltpu.VMEM(shape, jnp.float32) for shape in shapes]
        + PieceSums.scratch(count_dp, shapes)
        + [pltpu.VMEM(block, jnp.float32)]
        + LineScatter.scratch(count, columns, 4)
        + Spread.scratch(count, extra[0])
        + Spread.scratch(count, extra[1])
        + Spread.scratch(count_dp, (8, 128))
        + Spread.scratch(count, (8, 128))
    )
    return staged(
        partial(closing_kernel, count, count_dp, (len(items), len(done))),
        [*items, *small_parts, *tiles, *done],
        [jax.ShapeDtypeStruct(shape, jnp.float32) for shape in outs],
        scratch,
        10**7,
        write_shares,
        call_id,
        50,
    )


def clip_scale(norm):
    return clip_level / jnp.maximum(norm, clip_level)


def update_kernel(kinds, *refs):
    number = 3 * (kinds + 1)
    sources, states, refs = refs[: 1 + kinds], refs[1 + kinds :][:number], refs[1 + kinds + number :]
    outs, local, refs = refs[:number], refs[number:][: 1 + kinds], refs[number + 1 + kinds :]
    local_sems, held, (in_sems, out_sems) = refs[0], refs[1 : 1 + number], refs[1 + number :]
    stats, gradients = local[0], local[1:]
    kinds += 1
    firsts = [
        pltpu.make_async_copy(source, target, local_sems.at[index])
        for index, (source, target) in enumerate(zip(sources, local))
    ]
    for first in firsts:
        first.start()
    lane = lax.broadcasted_iota(jnp.int32, (8, 128), 1)
    corner = jnp.logical_and(lane == 0, lax.broadcasted_iota(jnp.int32, (8, 128), 0) == 0)
    loads, copies, pieces = [], [], []
    for kind, gradient in enumerate(gradients):
        if len(gradient.shape) == 2:
            pieces.append((kind, None))
        else:
            slots = gradient.shape[0]
            size = 2 if slots % 2 == 0 else slots
            pieces += [(kind, pl.ds(low, size)) for low in range(0, slots, size)]

    def at(ref, group):
        return ref if group is None else ref.at[group]

    def load(order):
        kind, group = pieces[order]
        for index in range(3 * kind, 3 * kind + 3):
            source, target = at(states[index], group), at(held[index], group)
            loads.append(pltpu.make_async_copy(source, target, in_sems.at[len(loads)]))
            loads[-1].start()

    ahead = 4
    for order in range(ahead):
        load(order)
    for copy in firsts:
        copy.wait()
    scale = jnp.sum(jnp.where(corner, clip_scale(stats[...]), 0.0))
    for order, (kind, group) in enumerate(pieces):
        if order + ahead < len(pieces):
            load(order + ahead)
        for copy in loads[3 * order : 3 * order + 3]:
            copy.wait()
        for slot in [None] if group is None else range(group.start, group.start + group.size):
            refs = [
                ref if slot is None else ref.at[slot] for ref in held[3 * kind : 3 * kind + 3]
            ]
            source = gradients[kind] if slot is None else gradients[kind].at[slot]
            rows, width = refs[0].shape
            step = math.gcd(rows, max(8, 8192 // width)) if rows % 8 == 0 else rows

            def one(index, carry, refs=refs, source=source, step=step, width=width):
                where = pl.ds(pl.multiple_of(index * step, step), step)
                state = [ref[where] for ref in refs]
                for ref, result in zip(refs, adam_update(*state, source[where, :width], scale)):
                    ref[where] = result
                return carry

            lax.fori_loop(0, rows // step, one, 0)
        for index in range(3 * kind, 3 * kind + 3):
            source, target = at(held[index], group), at(outs[index], group)
            copies.append(pltpu.make_async_copy(source, target, out_sems.at[len(copies)]))
            copies[-1].start()
    pixel_loads = [
        pltpu.make_async_copy(states[index], held[index], in_sems.at[len(loads) + index - 18])
        for index in range(18, 21)
    ]
    for copy in pixel_loads:
        copy.start()
    for copy in pixel_loads:
        copy.wait()
    pixels, rest = held[18:21], gradients[-1]
    for slot in range(2):
        gradient = rest[16 * (slot + 1) : 16 * (slot + 1) + PIX, : pixels[0].shape[2]]
        state = [ref[:, slot, :] for ref in pixels]
        for ref, result in zip(pixels, adam_update(*state, gradient, scale)):
            ref[:, slot, :] = result
    for index in range(18, 21):
        copies.append(pltpu.make_async_copy(held[index], outs[index], out_sems.at[len(copies)]))
        copies[-1].start()
    for copy in copies:
        copy.wait()


def update_states(stats, gradients, states):
    kinds = len(gradients)
    copies = sum(3 * (item.shape[0] if item.ndim == 3 else 1) for item in gradients) + 3
    sems = pltpu.SemaphoreType.DMA((copies,))
    return pl.pallas_call(
        partial(update_kernel, kinds),
        out_shape=[pltpu.HBM(item.shape, item.dtype) for item in states],
        in_specs=[HBM_SPEC] * (1 + kinds + len(states)),
        out_specs=[HBM_SPEC] * len(states),
        scratch_shapes=[pltpu.VMEM(item.shape, jnp.float32) for item in (stats, *gradients)]
        + [pltpu.SemaphoreType.DMA((1 + kinds,))]
        + [pltpu.VMEM(item.shape, jnp.float32) for item in states]
        + [sems] * 2,
        compiler_params=pltpu.CompilerParams(vmem_limit_bytes=24 << 20),
        cost_estimate=pl.CostEstimate(
            flops=2 * 10**7, bytes_accessed=14 * 10**6, transcendentals=0
        ),
    )(*(in_hbm(item) for item in (stats, *gradients, *states)))


def write_apart(
    latent_three,
    own_noisy,
    own_noise,
    own_keep,
    own_weight,
    weight_total,
    place,
    copy_pixels,
    gain,
    gain_rows,
    weights,
    layout,
    timesteps,
):
    write_key_weight, write_value_weight, write_query_weight, write_out_weight = weights
    images, latents, first_image, sharers = layout
    own_images, own_latents, d_lat = latent_three.shape
    write_norm, write_stats = layer_norm(latent_three, gain)
    write_low = write_norm.astype(jnp.bfloat16)

    own_interface = (
        jnp.einsum(
            "bcp,cd->bpd", own_noisy, copy_pixels[0].astype(jnp.float32), precision=precise
        )
        + place
    )

    outer_norm, outer_stats = layer_norm(own_interface, gain_rows[9])
    outer_low = outer_norm.astype(jnp.bfloat16)

    def join(spec, values, weight):
        product = jnp.einsum(spec, values, weight, preferred_element_type=jnp.float32)
        return product.astype(jnp.bfloat16)

    def image_rows(values):
        if sharers == 1:
            return values
        nothing = jnp.where(timesteps[0] > 0, 0.0, -0.0)
        whole = lax.all_gather(values.astype(jnp.float32), "mp", axis=0, tiled=True)
        whole = whole + nothing
        whole = whole.reshape(images, latents, d_lat).astype(jnp.bfloat16)
        return lax.dynamic_slice_in_dim(whole, first_image, own_images, 0)

    write_query = join("bpd,dc->bpc", outer_low, write_query_weight)
    write_key = image_rows(join("bld,dc->blc", write_low, write_key_weight))
    write_value = image_rows(join("bld,dc->blc", write_low, write_value_weight))
    write_out, write_total = attend_forward(write_query, write_key, write_value, None)
    outer = own_interface + jnp.einsum(
        "bpc,dc->bpd", write_out, write_out_weight, preferred_element_type=jnp.float32
    )
    final_norm, final_stats = layer_norm(outer, gain_rows[10])
    final_low = final_norm.astype(jnp.bfloat16)
    predicted = jnp.einsum(
        "bpd,cd->bcp", final_low, copy_pixels[1], preferred_element_type=jnp.float32
    )
    difference = predicted - own_noise
    masked = own_weight[:, None, None] * own_keep[:, None, :] * difference
    loss_local = jnp.sum(masked * difference)
    predict_grad = (2.0 * masked / weight_total).astype(jnp.bfloat16)
    head_grad = jnp.einsum(
        "bcp,bpd->cd", predict_grad, final_low, preferred_element_type=jnp.float32
    )
    final_grad = jnp.einsum(
        "bcp,cd->bpd", predict_grad, copy_pixels[1], preferred_element_type=jnp.float32
    )
    outer_grad, gain_final = norm_back(final_grad, gain_rows[10], final_stats)
    branch_low = outer_grad.astype(jnp.bfloat16)
    narrowout_grad = jnp.einsum(
        "bpd,bpc->dc", branch_low, write_out, preferred_element_type=jnp.float32
    )
    write_upstream = join("bpd,dc->bpc", branch_low, write_out_weight)
    query_grad, key_grad, value_grad = attend_back(
        write_query, write_key, write_value, None, write_total, write_upstream
    )
    write_query_grad = jnp.einsum(
        "bpd,bpc->dc", outer_low, query_grad, preferred_element_type=jnp.float32
    )
    outer_part = jnp.einsum(
        "bpc,dc->bpd", query_grad, write_query_weight, preferred_element_type=jnp.float32
    )

    def row_grad(values):
        if sharers > 1:
            whole = jnp.zeros((images, latents, d_lat), jnp.float32)
            whole = lax.dynamic_update_slice_in_dim(whole, values, first_image, 0)
            values = lax.psum_scatter(
                whole.reshape(images * sharers, own_latents, d_lat),
                "mp",
                scatter_dimension=0,
                tiled=True,
            )
        return values.astype(jnp.bfloat16)

    key_grad, value_grad = row_grad(key_grad), row_grad(value_grad)
    write_key_grad = jnp.einsum(
        "bld,blc->dc", write_low, key_grad, preferred_element_type=jnp.float32
    )
    write_value_grad = jnp.einsum(
        "bld,blc->dc", write_low, value_grad, preferred_element_type=jnp.float32
    )
    write_part = jnp.einsum(
        "blc,dc->bld", key_grad, write_key_weight, preferred_element_type=jnp.float32
    ) + jnp.einsum(
        "blc,dc->bld", value_grad, write_value_weight, preferred_element_type=jnp.float32
    )
    own_grad, gain_write = norm_back(write_part, gain, write_stats)
    outer_back, gain_outer = norm_back(outer_part, gain_rows[9], outer_stats)
    embed_grad = jnp.einsum(
        "bcp,bpd->cd", own_noisy, outer_grad + outer_back, precision=precise
    )
    return (
        own_grad,
        write_key_grad,
        write_value_grad,
        write_query_grad,
        narrowout_grad,
        gain_write,
        gain_outer,
        gain_final,
        embed_grad,
        head_grad,
        loss_local,
    )


def body(
    clean_patches,
    noise_patches,
    timesteps,
    present_mask,
    copy_widein,
    copy_narrowin,
    copy_wideout,
    copy_narrowout,
    copy_latents,
    copy_gains,
    copy_pixels,
    master_widein,
    first_widein,
    second_widein,
    master_narrowin,
    first_narrowin,
    second_narrowin,
    master_wideout,
    first_wideout,
    second_wideout,
    master_narrowout,
    first_narrowout,
    second_narrowout,
    master_latents,
    first_latents,
    second_latents,
    master_gains,
    first_gains,
    second_gains,
    master_pixels,
    first_pixels,
    second_pixels,
):
    images = clean_patches.shape[0]
    patches = clean_patches.shape[2]
    count_mp, count_dp = lax.axis_size("mp"), lax.axis_size("dp")
    mp_index, dp_index = lax.axis_index("mp"), lax.axis_index("dp")
    lead = (mp_index == 0).astype(jnp.float32)
    latents, d_lat = copy_latents.shape
    d_if = copy_gains.shape[1]
    local = copy_widein.shape[2]
    sharers = max(1, count_mp // images)
    own_images = max(1, images // count_mp)
    own_patches, own_latents = patches // sharers, latents // sharers
    first_image = mp_index * own_images // sharers
    share = lax.rem(mp_index, sharers)

    def dp_piece(values, axis):
        size = values.shape[axis] // count_dp
        return lax.dynamic_slice_in_dim(values, dp_index * size, size, axis).astype(jnp.float32)

    key_piece = dp_piece(copy_widein[:, 8], 0)
    value_piece = dp_piece(copy_widein[:, 9], 0)
    query_piece = dp_piece(copy_narrowin[:, 2], 0)
    out_piece = dp_piece(copy_narrowout, 1).T
    gathered = lax.all_gather(
        jnp.concatenate([key_piece, value_piece, query_piece, out_piece], 0), "mp"
    )

    signal = jnp.cos(0.5 * math.pi * (timesteps.astype(jnp.float32) + 0.5) / NSTEPS) ** 2
    noisy = (
        jnp.sqrt(signal)[:, None, None] * clean_patches
        + jnp.sqrt(1.0 - signal)[:, None, None] * noise_patches
    )
    loss_weight = 0.5 + signal
    keep_float = present_mask.astype(jnp.float32)
    weight_here = jnp.sum(loss_weight * PIX * jnp.sum(keep_float, 1))
    gain_rows = copy_gains.astype(jnp.float32)

    def wide_gain(index):
        return gain_rows[2 * index : 2 * index + 2].reshape(-1)

    wide_in = in_hbm(jnp.swapaxes(copy_widein, 0, 1))
    narrow_in = in_hbm(jnp.swapaxes(copy_narrowin, 0, 1))
    wide_out = in_hbm(copy_wideout)
    place = position_table(patches, d_if)
    noisy_rows, pixel_rows, noise_rows = (
        jnp.pad(item, ((0, 0), (0, 16 - PIX), (0, 0)))
        for item in (noisy, copy_pixels, noise_patches)
    )
    read_args = (
        noisy_rows,
        keep_float[:, :, None],
        place,
        pixel_rows[0],
        copy_latents,
        wide_gain(0)[None],
        gain_rows[8:9],
        wide_in,
        narrow_in,
        wide_out,
    )
    read_part, *read_kept = read_forward(*read_args)
    wide_gains = [wide_gain(index)[None] for index in range(1, 4)]
    latent_base = copy_latents.astype(jnp.float32)

    def own_tokens(values, axis):
        values = lax.dynamic_slice_in_dim(values, first_image, own_images, 0)
        return lax.dynamic_slice_in_dim(values, share * own_patches, own_patches, axis)

    own_weight = lax.dynamic_slice_in_dim(loss_weight, first_image, own_images, 0)
    own_scalar = jnp.broadcast_to(own_weight[0], (8, 128))
    own_pieces = [
        own_tokens(noisy_rows, 2),
        own_tokens(noise_rows, 2),
        own_tokens(keep_float, 1),
    ]
    side_gains = gain_rows[8:11]
    here_tile, lead = jnp.full((8, 128), weight_here), lead.reshape(1, 1)
    ready = (own_pieces, own_scalar, wide_gains, side_gains, latent_base, here_tile, lead, pixel_rows)
    gathered, read_part, ready = lax.optimization_barrier((gathered, read_part, ready))
    own_pieces, own_scalar, wide_gains, side_gains, latent_base, here_tile, lead, pixel_rows = ready
    gathered = lax.all_gather(gathered, "dp").reshape(count_dp * count_mp, -1, local)
    latent_near, latent_one, (weight_tile,) = line_sum(
        read_part, latent_base, 2, tile=here_tile
    )
    self_part, *self_kept = self_forward(
        latent_near, wide_gains[0], wide_in, wide_out, images
    )
    latent_near, latent_two, _ = line_sum(self_part, latent_one, 3)
    feed_part, *feed_kept = feed_forward(latent_near, wide_gains[1], wide_in, wide_out)
    latent_three, write_weights = line_scatter(
        feed_part, latent_two, gathered, [d_lat, d_lat, d_if, d_if], 4
    )
    latent_three = latent_three.reshape(own_images, own_latents, d_lat)
    if sharers == 1 and own_images == 1:
        (
            own_grad,
            write_key_grad,
            write_value_grad,
            write_query_grad,
            narrowout_grad,
            gain_write,
            gain_pair,
            own_embed,
            head_grad,
            loss_tile,
        ) = write_stage(
            own_scalar,
            weight_tile,
            latent_three[0],
            own_pieces[0][0],
            own_pieces[1][0],
            own_pieces[2],
            place,
            pixel_rows,
            wide_gains[2],
            side_gains,
            write_weights,
        )
    else:
        (
            own_grad,
            write_key_grad,
            write_value_grad,
            write_query_grad,
            narrowout_grad,
            gain_write,
            gain_outer,
            gain_final,
            own_embed,
            head_grad,
            loss_local,
        ) = write_apart(
            latent_three,
            own_tokens(noisy, 2),
            own_tokens(noise_patches, 2),
            own_tokens(keep_float, 1),
            own_weight,
            weight_tile[0, 0],
            lax.dynamic_slice_in_dim(place, share * own_patches, own_patches, 0),
            copy_pixels,
            wide_gain(3),
            gain_rows,
            write_weights,
            (images, latents, first_image, sharers),
            timesteps,
        )
        gain_write, gain_pair = gain_write[None], jnp.stack([gain_outer, gain_final])
        own_embed, head_grad = (
            jnp.pad(item, ((0, 16 - PIX), (0, 0))) for item in (own_embed, head_grad)
        )
        loss_tile = jnp.full((8, 128), loss_local)
    latent_near, latent_grad, (key_share, query_share) = line_gather(
        own_grad.reshape(-1, d_lat), 5, [write_key_grad, write_query_grad]
    )
    latent_part, up_first, up_last, down_grad, gain_feed = feed_backward(
        latent_near, latent_two, wide_gains[1], wide_in, wide_out, *feed_kept
    )
    latent_near, latent_grad, five_shares = line_sum(
        latent_part, latent_grad, 6, [write_value_grad, narrowout_grad, up_first]
    )
    latent_part, self_first, self_last, gain_self = self_backward(
        latent_near, latent_one, wide_gains[0], wide_in, wide_out, *self_kept
    )
    latent_near, latent_grad, six_shares = line_sum(
        latent_part, latent_grad, 7, [up_last, down_grad, self_first]
    )
    read_wide, read_narrow, latent_total, gain_read, gain_side, side_embed = read_backward(
        read_args[0], *read_args[4:], *read_kept, latent_near, lead
    )
    *gradients, stats = closing(
        [self_last, read_wide, read_narrow],
        [
            latent_total,
            gain_read,
            gain_self,
            gain_feed,
            gain_write,
            gain_side,
            gain_pair,
            side_embed,
            own_embed,
            head_grad,
        ],
        [loss_tile, weight_tile],
        [six_shares[2], five_shares[2], six_shares[0], six_shares[1]],
        [key_share, five_shares[0], query_share, five_shares[1]],
        8,
    )
    states = (
        *(jnp.swapaxes(item, 0, 1) for item in (master_widein, first_widein, second_widein)),
        *(jnp.swapaxes(item, 0, 1) for item in (master_narrowin, first_narrowin, second_narrowin)),
        master_wideout,
        first_wideout,
        second_wideout,
        *(item.T for item in (master_narrowout, first_narrowout, second_narrowout)),
        master_latents,
        first_latents,
        second_latents,
        master_gains,
        first_gains,
        second_gains,
        *(jnp.swapaxes(item, 0, 1) for item in (master_pixels, first_pixels, second_pixels)),
    )
    results = update_states(stats, gradients, states)
    results = [
        jnp.swapaxes(item, 0, 1) if index < 6 or 9 <= index < 12 or index >= 18 else item
        for index, item in enumerate(results)
    ]
    return (stats[0, 1], stats[0, 0], *results)


def solution(mesh):
    in_specs = (
        P("dp", None, None),
        P("dp", None, None),
        P("dp"),
        P("dp", None),
        P(None, None, "mp"),
        P(None, None, "mp"),
        P(None, "mp", None),
        P("mp", None),
        P(),
        P(),
        P(),
        P("dp", None, "mp"),
        P("dp", None, "mp"),
        P("dp", None, "mp"),
        P("dp", None, "mp"),
        P("dp", None, "mp"),
        P("dp", None, "mp"),
        P(None, "mp", "dp"),
        P(None, "mp", "dp"),
        P(None, "mp", "dp"),
        P("mp", "dp"),
        P("mp", "dp"),
        P("mp", "dp"),
        P(None, "dp"),
        P(None, "dp"),
        P(None, "dp"),
        P(None, "dp"),
        P(None, "dp"),
        P(None, "dp"),
        P(None, None, "dp"),
        P(None, None, "dp"),
        P(None, None, "dp"),
    )
    out_specs = (
        P(),
        P(),
        P("dp", None, "mp"),
        P("dp", None, "mp"),
        P("dp", None, "mp"),
        P("dp", None, "mp"),
        P("dp", None, "mp"),
        P("dp", None, "mp"),
        P(None, "mp", "dp"),
        P(None, "mp", "dp"),
        P(None, "mp", "dp"),
        P("mp", "dp"),
        P("mp", "dp"),
        P("mp", "dp"),
        P(None, "dp"),
        P(None, "dp"),
        P(None, "dp"),
        P(None, "dp"),
        P(None, "dp"),
        P(None, "dp"),
        P(None, None, "dp"),
        P(None, None, "dp"),
        P(None, None, "dp"),
    )
    return jax.shard_map(body, mesh=mesh, in_specs=in_specs, out_specs=out_specs, check_vma=False)
```

```python
from functools import partial
import math

import jax
import jax.numpy as jnp
import numpy as np
from jax import lax
from jax.experimental import pallas as pl
from jax.experimental.pallas import tpu as pltpu
from jax.sharding import PartitionSpec as P

HEAD_DIM = 64
PIX = 12
NSTEPS = 1000
STEP = 10


precise = lax.Precision.HIGHEST
clip_level = 0.01
learning_rate = 0.05
weight_decay = 0.1
adam_beta = 0.5
adam_eps = 1e-08


def layer_norm(values, gain):
    centered = values - jnp.mean(values, -1, keepdims=True)
    scale = lax.rsqrt(jnp.mean(centered * centered, -1, keepdims=True) + 1e-05)
    normed = centered * scale
    return (normed * gain, (normed, scale))


def norm_back(upstream, gain, stats):
    normed, scale = stats
    inner = upstream * gain
    values = scale * (
        inner
        - jnp.mean(inner, -1, keepdims=True)
        - normed * jnp.mean(inner * normed, -1, keepdims=True)
    )
    gain_grad = jnp.sum((upstream * normed).reshape(-1, normed.shape[-1]), 0)
    return (values, gain_grad)


def position_table(count, width):
    place = np.arange(count, dtype=np.float64)[:, None]
    angle = place * 10000.0 ** (-2.0 * np.arange(width // 2) / width)
    return jnp.asarray(np.concatenate([np.sin(angle), np.cos(angle)], -1), jnp.float32)


def positions(count, width):
    place = jnp.arange(count, dtype=jnp.float32)[:, None]
    index = jnp.arange(width // 2, dtype=jnp.float32)[None, :]
    angle = place * jnp.exp(-math.log(10000.0) * 2.0 * index / width)
    return jnp.concatenate([jnp.sin(angle), jnp.cos(angle)], -1)


def split_heads(values):
    return values.reshape(values.shape[:-1] + (values.shape[-1] // HEAD_DIM, HEAD_DIM))


def attend_scores(queries, keys, keep_mask):
    scores = jnp.einsum(
        "bqhe,bkhe->bhqk",
        split_heads(queries),
        split_heads(keys),
        preferred_element_type=jnp.float32,
    ) * HEAD_DIM ** (-0.5)
    if keep_mask is not None:
        scores = jnp.where(keep_mask[:, None, None, :] > 0, scores, -1e30)
    return scores


def attend_forward(queries, keys, values, keep_mask):
    scores = attend_scores(queries, keys, keep_mask)
    top = jnp.max(scores, -1, keepdims=True)
    log_total = top + jnp.log(jnp.sum(jnp.exp(scores - top), -1, keepdims=True))
    probs = jnp.exp(scores - log_total).astype(jnp.bfloat16)
    output = jnp.einsum(
        "bhqk,bkhe->bqhe", probs, split_heads(values), preferred_element_type=jnp.float32
    )
    return (output.reshape(queries.shape).astype(jnp.bfloat16), log_total)


def attend_back(queries, keys, values, keep_mask, log_total, upstream):
    scores = attend_scores(queries, keys, keep_mask)
    probs = jnp.exp(scores - log_total)
    value_grad = jnp.einsum(
        "bhqk,bqhe->bkhe",
        probs.astype(jnp.bfloat16),
        split_heads(upstream),
        preferred_element_type=jnp.float32,
    )
    prob_grad = jnp.einsum(
        "bqhe,bkhe->bhqk",
        split_heads(upstream),
        split_heads(values),
        preferred_element_type=jnp.float32,
    )
    score_grad = (probs * (prob_grad - jnp.sum(prob_grad * probs, -1, keepdims=True))).astype(
        jnp.bfloat16
    )
    query_grad = jnp.einsum(
        "bhqk,bkhe->bqhe", score_grad, split_heads(keys), preferred_element_type=jnp.float32
    ) * HEAD_DIM ** (-0.5)
    key_grad = jnp.einsum(
        "bhqk,bqhe->bkhe", score_grad, split_heads(queries), preferred_element_type=jnp.float32
    ) * HEAD_DIM ** (-0.5)
    return (
        query_grad.reshape(queries.shape).astype(jnp.bfloat16),
        key_grad.reshape(keys.shape),
        value_grad.reshape(values.shape),
    )


MESH_ID = pl.DeviceIdType.MESH
HBM_SPEC = pl.BlockSpec(memory_space=pltpu.HBM)
VMEM_SPEC = pl.BlockSpec(memory_space=pltpu.VMEM)
CHUNKS = 32
VMEM_LIMIT = 56 << 20


def in_hbm(values):
    return pltpu.with_memory_space_constraint(values, pltpu.HBM)


def in_vmem(values):
    return pltpu.with_memory_space_constraint(values, pltpu.VMEM)


def remote(source, target, send_sem, recv_sem, device):
    return pltpu.make_async_remote_copy(
        src_ref=source,
        dst_ref=target,
        send_sem=send_sem,
        recv_sem=recv_sem,
        device_id=device,
        device_id_type=MESH_ID,
    )


class PieceSums:
    def __init__(self, count, items, outs, scratch):
        self.count, self.items, self.outs = count, items, outs
        self.bits = count.bit_length() - 1
        self.place = lax.axis_index("dp") if items else None
        self.held = []
        for index in range(len(items)):
            self.held.append(scratch[index * (self.bits + 2) : (index + 1) * (self.bits + 2)])

    @staticmethod
    def scratch(count, shapes):
        bits = count.bit_length() - 1
        result = []
        for rows, width in shapes:
            result.append(pltpu.VMEM((count // 2, rows, width), jnp.float32))
            for phase in range(2, bits + 1):
                result.append(
                    pltpu.VMEM((2 * (count >> phase), rows // 2, width), jnp.float32)
                )
            copies = count // 2 + 2 * sum(count >> phase for phase in range(2, bits + 1))
            result += [pltpu.SemaphoreType.DMA((copies,))] * 2
        return result

    def peers(self):
        return [{"dp": self.place ^ (1 << bit)} for bit in range(self.bits)] if self.items else []

    def order(self, half):
        later = list(range(1, self.bits))
        turn = half * (len(later) // 2)
        return later[turn:] + later[:turn]

    def first_copy(self, index, piece):
        item, held = self.items[index], self.held[index]
        other = 1 - (self.place & 1)
        return remote(
            item.at[2 * piece + other],
            held[0].at[piece],
            held[-2].at[piece],
            held[-1].at[piece],
            {"dp": self.place ^ 1},
        )

    def member(self, half, phase, entry, flip):
        bits = self.order(half)
        settled, now, rest = bits[: phase - 2], bits[phase - 2], bits[phase - 1 :]
        piece = 0
        for bit in settled:
            piece = piece | (self.place & (1 << bit))
        own = self.place & (1 << now)
        piece = piece | ((own ^ (1 << now)) if flip else own)
        for position, bit in enumerate(rest):
            if (entry >> position) & 1:
                piece = piece | (1 << bit)
        return piece >> 1

    def later_copy(self, index, half, phase, entry):
        held = self.held[index]
        rows = self.items[index].shape[1] // 2
        size = self.count >> phase
        sem = self.count // 2 + 2 * sum(self.count >> p for p in range(2, phase)) + half * size + entry
        return remote(
            held[0].at[self.member(half, phase, entry, True), pl.ds(half * rows, rows)],
            held[phase - 1].at[half * size + entry],
            held[-2].at[sem],
            held[-1].at[sem],
            {"dp": self.place ^ (1 << self.order(half)[phase - 2])},
        )

    def entries(self, phase):
        return [
            (index, half, entry)
            for index in range(len(self.items))
            for half in range(2)
            for entry in range(self.count >> phase)
        ]

    def begin(self):
        for index in range(len(self.items)):
            for piece in range(self.count // 2):
                self.first_copy(index, piece).start()

    def send(self, phase):
        for index, half, entry in self.entries(phase):
            self.later_copy(index, half, phase, entry).start()

    def advance(self, phase):
        if not self.items:
            return
        if phase == 1:
            own = self.place & 1
            for index, item in enumerate(self.items):
                total = self.held[index][0]
                for piece in range(self.count // 2):
                    self.first_copy(index, piece).wait_recv()
                    add_rows(total.at[piece], total.at[piece], item.at[2 * piece + own])
        else:
            for index, half, entry in self.entries(phase):
                self.later_copy(index, half, phase, entry).wait_recv()
                held, rows = self.held[index], self.items[index].shape[1] // 2
                where = pl.ds(half * rows, rows)
                came = held[phase - 1].at[half * (self.count >> phase) + entry]
                kept = held[0].at[self.member(half, phase, entry, False), where]
                if phase == self.bits:
                    add_rows(self.outs[index].at[where], kept, came)
                else:
                    add_rows(kept, kept, came)
        if phase < self.bits:
            self.send(phase + 1)

    def finish(self):
        for index in range(len(self.items)):
            for piece in range(self.count // 2):
                self.first_copy(index, piece).wait_send()
        for phase in range(2, self.bits + 1):
            for index, half, entry in self.entries(phase):
                self.later_copy(index, half, phase, entry).wait_send()

    def moments(self, total):
        if not self.items:
            return [(0, total, None)]
        marks, low = [], 0
        for phase in range(1, self.bits + 1):
            share = (1 - 0.5 ** (phase - 1)) / (1 - 0.5 ** (self.bits - 1))
            high = total if phase == self.bits else int(total * (0.22 + 0.78 * share))
            marks.append((low, high, phase))
            low = high
        return marks


def add_rows(target, left, right):
    rows, width = target.shape
    step = math.gcd(rows, max(8, 8192 // width))

    def one(index, carry):
        where = pl.ds(pl.multiple_of(index * step, step), step)
        target[where] = left[where] + right[where]
        return carry

    lax.fori_loop(0, rows // step, one, 0)


class Spread:
    def __init__(self, name, count, held, send_sem, recv_sem):
        self.name, self.count, self.held = name, count, held
        self.send_sem, self.recv_sem = send_sem, recv_sem
        self.place = lax.axis_index(name)

    @staticmethod
    def scratch(count, shape):
        sems = pltpu.SemaphoreType.DMA((count,))
        return [pltpu.VMEM((count,) + shape, jnp.float32), sems, sems]

    def peer(self, step):
        return {self.name: lax.rem(self.place + step, self.count)}

    def copy(self, step, slot):
        return remote(
            self.held.at[slot],
            self.held.at[slot],
            self.send_sem.at[step],
            self.recv_sem.at[slot],
            self.peer(step),
        )

    def each(self, action):
        def one(step, carry):
            action(step)
            return carry

        lax.fori_loop(1, self.count, one, 0)

    def start(self):
        self.each(lambda step: self.copy(step, self.place).start())

    def take(self):
        self.each(lambda step: self.copy(step, lax.rem(self.place + step, self.count)).wait_recv())

    def finish(self):
        self.each(lambda step: self.copy(step, self.place).wait_send())

    def total(self):
        return lax.fori_loop(
            1, self.count, lambda slot, carry: carry + self.held[slot], self.held[0]
        )


class Convert:
    def __init__(self, count_mp, steps, blocks, outs, buffer, sems):
        self.count_mp, self.blocks, self.outs = count_mp, blocks, outs
        self.buffer, self.sems = buffer, sems
        self.number = blocks.shape[0]
        self.each, self.stride = max(1, self.number // steps), max(1, steps // self.number)

    @staticmethod
    def scratch(block):
        return [pltpu.VMEM((3,) + block, jnp.float32), pltpu.SemaphoreType.DMA((3,))]

    def copy(self, index):
        slot = lax.rem(index, 3)
        return pltpu.make_async_copy(
            self.blocks.at[index], self.buffer.at[slot], self.sems.at[slot]
        )

    def begin(self):
        self.copy(0).start()
        self.copy(1).start()

    def one(self, index):
        self.copy(index).wait()

        @pl.when(index + 2 < self.number)
        def _():
            self.copy(index + 2).start()

        block = self.buffer.at[lax.rem(index, 3)]
        local = block.shape[1]
        columns = pl.ds(pl.multiple_of(lax.rem(index, self.count_mp) * local, local), local)
        low = 0
        for out in self.outs:
            rows = out.shape[0] * self.count_mp // self.number
            where = pl.ds(pl.multiple_of(index // self.count_mp * rows, rows), rows)
            out[where, columns] = block[pl.ds(low, rows)].astype(jnp.bfloat16)
            low += rows

    def step(self, index):
        @pl.when(lax.rem(index, self.stride) == 0)
        def _():
            for entry in range(self.each):
                self.one(index // self.stride * self.each + entry)


def signal_all(barrier, others):
    for other in others:
        pl.semaphore_signal(barrier, inc=1, device_id=other, device_id_type=MESH_ID)


class Stage:
    def __init__(self, sources, held, in_sems, results, targets, out_sems):
        self.loads = [
            pltpu.make_async_copy(source, target, in_sems.at[index])
            for index, (source, target) in enumerate(zip(sources, held))
        ]
        self.stores = [
            pltpu.make_async_copy(source, target, out_sems.at[index])
            for index, (source, target) in enumerate(zip(results, targets))
        ]
        self.stored, self.waited = [], []

    def start(self):
        for load in self.loads:
            load.start()

    def wait(self, *indices):
        for index in indices or range(len(self.loads)):
            if index not in self.waited:
                self.loads[index].wait()
                self.waited.append(index)

    def store(self, *indices):
        for index in indices:
            self.stores[index].start()
            self.stored.append(index)

    def finish(self):
        self.store(*(index for index in range(len(self.stores)) if index not in self.stored))
        for store in self.stores:
            store.wait()


def staged_kernel(body, counts, *refs):
    refs = list(refs)

    def pull(number):
        taken = refs[:number]
        del refs[:number]
        return taken

    close, number, raw, close_outs, results = counts
    near, sources, raws = pull(close), pull(number), pull(raw)
    near_outs, targets, echoes = pull(close_outs), pull(results), pull(close_outs)
    held, outs, (in_sems, out_sems) = pull(number), pull(results), pull(2)
    stage = Stage(
        sources, held, in_sems, [*near_outs, *outs], [*echoes, *targets], out_sems
    )
    stage.start()
    body(stage, [*near, *held], raws, [*near_outs, *outs], refs)
    stage.finish()


def staged(
    body, inputs, outs, scratch, flops, raw=(), call_id=None, length=0, near=(), near_outs=()
):
    copies = [pltpu.VMEM(item.shape, item.dtype) for item in (*inputs, *outs)]
    stores = [*outs, *near_outs]
    sems = [pltpu.SemaphoreType.DMA((max(1, len(group)),)) for group in (inputs, stores)]
    needed = sum(
        math.prod(item.shape) * jnp.dtype(item.dtype).itemsize
        for item in copies + list(scratch)
        if getattr(item, "dtype", None) in (jnp.float32, jnp.bfloat16)
    )
    params = {} if call_id is None else {"collective_id": call_id, "has_side_effects": True}
    counts = (len(near), len(inputs), len(raw), len(near_outs), len(outs))
    results = pl.pallas_call(
        partial(staged_kernel, body, counts),
        out_shape=[pltpu.VMEM(item.shape, item.dtype) for item in near_outs]
        + [pltpu.HBM(item.shape, item.dtype) for item in stores],
        in_specs=[VMEM_SPEC] * len(near) + [HBM_SPEC] * (len(inputs) + len(raw)),
        out_specs=[VMEM_SPEC] * len(near_outs) + [HBM_SPEC] * len(stores),
        scratch_shapes=copies + sems + list(scratch),
        compiler_params=pltpu.CompilerParams(vmem_limit_bytes=needed + (6 << 20), **params),
        cost_estimate=pl.CostEstimate(
            flops=flops, bytes_accessed=length * 3_500_000, transcendentals=0
        ),
    )(*map(in_vmem, near), *map(in_hbm, (*inputs, *raw)))
    return list(results)


def greet(place, count, others=()):
    barrier = pltpu.get_barrier_semaphore()
    below, above = {"mp": place - 1}, {"mp": place + 1}

    @pl.when(place > 0)
    def _():
        pl.semaphore_signal(barrier, inc=1, device_id=below, device_id_type=MESH_ID)

    @pl.when(place < count - 1)
    def _():
        pl.semaphore_signal(barrier, inc=1, device_id=above, device_id_type=MESH_ID)

    signal_all(barrier, others)
    inside = jnp.logical_and(place > 0, place < count - 1)

    @pl.when(inside)
    def _():
        pl.semaphore_wait(barrier, 2 + len(others))

    @pl.when(jnp.logical_not(inside))
    def _():
        pl.semaphore_wait(barrier, 1 + len(others))


def views(refs, base=3):
    result = []
    for ref in refs:
        if len(ref.shape) == base:
            result.append(ref)
        else:
            result += [ref.at[slot] for slot in range(ref.shape[0])]
    return result


def line_sum_kernel(count, count_dp, extra, tiled, stage, held, raws, results, scratch):
    refs = list(scratch)

    def pull(number):
        taken = refs[:number]
        del refs[:number]
        return taken

    part_ref, base_ref, tile = held[0], held[1], held[2 + extra :]
    items, outs = views(held[2 : 2 + extra]), views(results[1 : 1 + extra], 2)
    out_ref, tile_out = results[0], results[1 + extra : 1 + extra + tiled]
    base_rows = base_ref.shape[0]
    inner, from_away, from_toward, toward_send, away_send, away_recv, toward_recv = pull(7)
    chunks = toward_send.shape[0]
    spread = Spread("dp", count_dp, *pull(3)) if tiled else None
    turn = pull(1)[0] if tiled else None
    sums = PieceSums(count_dp, items, outs, refs)
    place = lax.axis_index("mp")
    half = count // 2
    low_side = place < half
    toward = {"mp": jnp.where(low_side, place + 1, place - 1)}
    away = {"mp": jnp.where(low_side, place - 1, place + 1)}
    middle = jnp.logical_or(place == half - 1, place == half)
    outermost = jnp.logical_or(place == 0, place == count - 1)
    rows = part_ref.shape[0] // chunks
    others = [spread.peer(step) for step in range(1, count_dp)] if tiled else sums.peers()
    greet(place, count, others)

    def window(step):
        return pl.ds(pl.multiple_of(step * rows, rows), rows)

    def put(step, total):
        first = lax.rem(step * rows, base_rows)
        out_ref[window(step)] = total + base_ref[pl.ds(pl.multiple_of(first, rows), rows)]

    def push(step, source, inside):
        target = from_toward if inside else from_away
        recv = toward_recv if inside else away_recv
        return remote(
            source.at[window(step)],
            target.at[window(step)],
            toward_send.at[step],
            recv.at[step],
            toward,
        )

    def back(step, source):
        return remote(
            source.at[window(step)],
            from_toward.at[window(step)],
            away_send.at[step],
            toward_recv.at[step],
            away,
        )

    def gather_in(step):
        push(step, part_ref, False).wait_recv()
        inner[window(step)] = part_ref[window(step)] + from_away[window(step)]

    odd = lax.rem(lax.axis_index("dp"), 2) == 1
    if tiled:
        stage.wait()
        spread.held[spread.place] = tile[0][...]
        spread.start()

        @pl.when(jnp.logical_and(outermost, odd))
        def _():
            pl.semaphore_wait(turn, 1)

    def pass_turn():
        if tiled:

            @pl.when(jnp.logical_not(odd))
            def _():
                pl.semaphore_signal(
                    turn, inc=1, device_id=spread.peer(1), device_id_type=MESH_ID
                )

    @pl.when(outermost)
    def _():
        def leave(step, carry):
            push(step, part_ref, False).start()
            return carry

        lax.fori_loop(0, chunks, leave, 0)

    stage.wait()
    sums.begin()

    @pl.when(outermost)
    def _():

        def arrive(step, carry):
            push(step, part_ref, True).wait_recv()
            put(step, from_toward[window(step)])
            push(step, part_ref, False).wait_send()
            return carry

        if tiled:
            early = chunks * 3 // 8
            lax.fori_loop(0, early, arrive, 0)
            pass_turn()
            lax.fori_loop(early, chunks, arrive, 0)
        else:
            for low, high, phase in sums.moments(chunks):
                lax.fori_loop(low, high, arrive, 0)
                sums.advance(phase)

    lag = 2

    @pl.when(middle)
    def _():
        def finish(step):
            push(step, inner, True).wait_recv()
            push(step, inner, True).wait_send()
            total = inner[window(step)] + from_toward[window(step)]
            inner[window(step)] = total
            back(step, inner).start()
            put(step, total)

        def first(step, carry):
            gather_in(step)
            push(step, inner, True).start()
            return carry

        def both(step, carry):
            first(step, carry)
            finish(step - lag)
            return carry

        def last(step, carry):
            finish(step)
            return carry

        def drain(step, carry):
            back(step, inner).wait_send()
            return carry

        lax.fori_loop(0, lag, first, 0)
        for low, high, phase in sums.moments(chunks):
            lax.fori_loop(max(low, lag), high, both, 0)
            if high == chunks:
                lax.fori_loop(chunks - lag, chunks, last, 0)
            sums.advance(phase)
        lax.fori_loop(0, chunks, drain, 0)

    if count > 4:

        @pl.when(jnp.logical_not(jnp.logical_or(middle, outermost)))
        def _():
            def inwards(step, carry):
                gather_in(step)
                push(step, inner, False).start()
                return carry

            def outwards(step, carry):
                push(step, inner, True).wait_recv()
                back(step, from_toward).start()
                put(step, from_toward[window(step)])
                return carry

            def drain(step, carry):
                push(step, inner, False).wait_send()
                back(step, from_toward).wait_send()
                return carry

            lax.fori_loop(0, chunks, inwards, 0)
            for low, high, phase in sums.moments(chunks):
                lax.fori_loop(low, high, outwards, 0)
                sums.advance(phase)
            lax.fori_loop(0, chunks, drain, 0)

    sums.finish()
    if tiled:
        spread.take()
        tile_out[0][...] = spread.total()
        spread.finish()


def piece_shapes(items):
    count = lax.axis_size("dp")
    items = [item.reshape(item.shape[:-2] + (count, -1, item.shape[-1])) for item in items]
    shapes, shares = [], []
    for item in items:
        shapes += [item.shape[-2:]] * (item.shape[0] if item.ndim == 4 else 1)
        shares.append(jax.ShapeDtypeStruct(item.shape[:-3] + item.shape[-2:], jnp.float32))
    return items, shapes, shares


def line_sum(part, base, call_id, items=(), tile=None):
    items, shapes, shares = piece_shapes(items)
    count, count_dp = lax.axis_size("mp"), lax.axis_size("dp")
    rows, width = part.shape
    buffer = pltpu.VMEM((rows, width), jnp.float32)
    sems = pltpu.SemaphoreType.DMA((CHUNKS if items else CHUNKS // 2,))
    inputs = [base, *items]
    outs = list(shares)
    scratch = [buffer] * 3 + [sems] * 4
    if tile is not None:
        inputs.append(tile)
        outs.append(jax.ShapeDtypeStruct(tile.shape, jnp.float32))
        scratch += Spread.scratch(count_dp, tile.shape) + [pltpu.SemaphoreType.REGULAR]
    scratch += PieceSums.scratch(count_dp, shapes)
    total = jax.ShapeDtypeStruct((rows, width), jnp.float32)
    results = staged(
        partial(line_sum_kernel, count, count_dp, len(items), int(tile is not None)),
        inputs,
        outs,
        scratch,
        4 * rows * width,
        call_id=call_id,
        length=55,
        near=[part],
        near_outs=[total],
    )
    return results[0], results[-1], results[1:-1]


class LineScatter:
    def __init__(self, count, part, out, buffers, sems):
        self.count, self.part, self.out = count, part, out
        self.up_acc, self.down_acc, self.from_below, self.from_above = buffers
        self.up_send, self.down_send, self.up_recv, self.down_recv = sems
        self.place = lax.axis_index("mp")
        self.steps = self.up_send.shape[1]
        self.block = part.shape[0] // count
        self.rows = self.block // self.steps

    @staticmethod
    def scratch(count, shape, steps):
        sems = pltpu.SemaphoreType.DMA((count, steps))
        return [pltpu.VMEM(shape, jnp.float32)] * 4 + [sems] * 4

    def window(self, owner, step):
        return pl.ds(pl.multiple_of(owner * self.block + step * self.rows, self.rows), self.rows)

    def up(self, owner, step, source):
        where = self.window(owner, step)
        return remote(
            source.at[where],
            self.from_below.at[where],
            self.up_send.at[owner, step],
            self.up_recv.at[owner, step],
            {"mp": self.place + 1},
        )

    def down(self, owner, step, source):
        where = self.window(owner, step)
        return remote(
            source.at[where],
            self.from_above.at[where],
            self.down_send.at[owner, step],
            self.down_recv.at[owner, step],
            {"mp": self.place - 1},
        )

    def up_turn(self, index):
        place, part = self.place, self.part
        owner, step = self.count - 1 - index // self.steps, lax.rem(index, self.steps)

        @pl.when(jnp.logical_and(owner > place, place == 0))
        def _():
            self.up(owner, step, part).start()

        @pl.when(jnp.logical_and(owner > place, place > 0))
        def _():
            self.up(owner, step, part).wait_recv()
            where = self.window(owner, step)
            self.up_acc[where] = part[where] + self.from_below[where]
            self.up(owner, step, self.up_acc).start()

    def down_turn(self, index):
        place, part, count = self.place, self.part, self.count
        owner, step = index // self.steps, lax.rem(index, self.steps)

        @pl.when(jnp.logical_and(owner < place, place == count - 1))
        def _():
            self.down(owner, step, part).start()

        @pl.when(jnp.logical_and(owner < place, place < count - 1))
        def _():
            self.down(owner, step, part).wait_recv()
            where = self.window(owner, step)
            self.down_acc[where] = part[where] + self.from_above[where]
            self.down(owner, step, self.down_acc).start()

    def run(self, pause=None, beside=None):
        turns, lag = self.count * self.steps, self.steps

        def staggered(first, second):
            def begin(index, carry):
                first(index)
                if beside is not None:
                    beside(index)
                return carry

            def both(index, carry):
                first(index)
                second(index - lag)
                if beside is not None:
                    beside(index)
                return carry

            def end(index, carry):
                second(index)
                return carry

            lax.fori_loop(0, lag, begin, 0)
            if pause is not None:
                pause()
            lax.fori_loop(lag, turns, both, 0)
            lax.fori_loop(turns - lag, turns, end, 0)

        @pl.when(self.place < self.count // 2)
        def _():
            staggered(self.up_turn, self.down_turn)

        @pl.when(self.place >= self.count // 2)
        def _():
            staggered(self.down_turn, self.up_turn)

    def settle(self):
        place, rows = self.place, self.rows

        def one(step, carry):
            where = self.window(place, step)
            mine = pl.ds(pl.multiple_of(step * rows, rows), rows)
            self.out[mine] = self.part[where]

            @pl.when(place > 0)
            def _():
                self.up(place, step, self.part).wait_recv()
                self.out[mine] += self.from_below[where]

            @pl.when(place < self.count - 1)
            def _():
                self.down(place, step, self.part).wait_recv()
                self.out[mine] += self.from_above[where]

            return carry

        lax.fori_loop(0, self.steps, one, 0)

    def finish(self):
        place = self.place

        def one(index, carry):
            owner, step = index // self.steps, lax.rem(index, self.steps)

            @pl.when(owner > place)
            def _():
                self.up(owner, step, self.part).wait_send()

            @pl.when(owner < place)
            def _():
                self.down(owner, step, self.part).wait_send()

            return carry

        lax.fori_loop(0, self.count * self.steps, one, 0)


def line_scatter_kernel(count, stage, held, raws, results, scratch):
    own, sem = scratch[8:10]
    base, blocks = raws
    scatter = LineScatter(count, held[0], results[0], scratch[:4], scratch[4:8])
    convert = Convert(
        count, count * scatter.steps, blocks, results[1:], scratch[10], scratch[11]
    )
    rows = own.shape[0]
    load = pltpu.make_async_copy(
        base.at[pl.ds(pl.multiple_of(scatter.place * rows, rows), rows)], own, sem
    )
    load.start()
    convert.begin()
    greet(scatter.place, count)
    scatter.run(None, convert.step)
    stage.store(1, 2, 3, 4)
    scatter.settle()
    load.wait()
    results[0][...] += own[...]
    scatter.finish()


def line_scatter(part, base, blocks, sizes, call_id):
    rows, width = part.shape
    count = lax.axis_size("mp")
    own = (rows // count, width)
    result, *weights = staged(
        partial(line_scatter_kernel, count),
        [],
        [jax.ShapeDtypeStruct(own, jnp.float32)]
        + [jax.ShapeDtypeStruct((size, count * blocks.shape[2]), jnp.bfloat16) for size in sizes],
        LineScatter.scratch(count, (rows, width), 8)
        + [pltpu.VMEM(own, jnp.float32), pltpu.SemaphoreType.DMA]
        + Convert.scratch(blocks.shape[1:]),
        2 * rows * width,
        [base, blocks],
        call_id=call_id,
        length=33,
        near=[part],
    )
    return result, weights


def line_gather_kernel(count, count_dp, extra, stage, held, raws, results, scratch):
    own_ref, out_ref = held[0], results[0]
    items, outs = views(held[1:]), views(results[1:], 2)
    up_send, down_send, up_recv, down_recv = scratch[:4]
    sums = PieceSums(count_dp, items, outs, scratch[4:])
    place = lax.axis_index("mp")
    steps = up_send.shape[1]
    block = own_ref.shape[0]
    rows = block // steps
    below, above = {"mp": place - 1}, {"mp": place + 1}
    greet(place, count, sums.peers())
    stage.wait(0)

    def window(owner, step):
        return pl.ds(pl.multiple_of(owner * block + step * rows, rows), rows)

    def up(owner, step):
        part = out_ref.at[window(owner, step)]
        return remote(part, part, up_send.at[owner, step], up_recv.at[owner, step], above)

    def down(owner, step):
        part = out_ref.at[window(owner, step)]
        return remote(part, part, down_send.at[owner, step], down_recv.at[owner, step], below)

    def begin(step, carry):
        out_ref[window(place, step)] = own_ref[pl.ds(pl.multiple_of(step * rows, rows), rows)]

        @pl.when(place < count - 1)
        def _():
            up(place, step).start()

        @pl.when(place > 0)
        def _():
            down(place, step).start()

        return carry

    lax.fori_loop(0, steps, begin, 0)
    stage.wait(*range(1, len(stage.loads)))
    sums.begin()

    def pass_on(index, carry):
        away, step = 1 + index // steps, lax.rem(index, steps)

        @pl.when(place - away >= 0)
        def _():
            up(place - away, step).wait_recv()

        @pl.when(jnp.logical_and(place - away >= 0, place < count - 1))
        def _():
            up(place - away, step).start()

        @pl.when(place + away < count)
        def _():
            down(place + away, step).wait_recv()

        @pl.when(jnp.logical_and(place + away < count, place > 0))
        def _():
            down(place + away, step).start()

        return carry

    for low, high, phase in sums.moments((count - 1) * steps):
        lax.fori_loop(low, high, pass_on, 0)
        sums.advance(phase)

    def drain(index, carry):
        owner, step = index // steps, lax.rem(index, steps)

        @pl.when(jnp.logical_and(owner <= place, place < count - 1))
        def _():
            up(owner, step).wait_send()

        @pl.when(jnp.logical_and(owner >= place, place > 0))
        def _():
            down(owner, step).wait_send()

        return carry

    lax.fori_loop(0, count * steps, drain, 0)
    sums.finish()


def line_gather(own, call_id, items=()):
    rows, width = own.shape
    count, count_dp = lax.axis_size("mp"), lax.axis_size("dp")
    sems = pltpu.SemaphoreType.DMA((count, 8))
    items, shapes, shares = piece_shapes(items)
    results = staged(
        partial(line_gather_kernel, count, count_dp, len(items)),
        [own, *items],
        shares,
        [sems] * 4 + PieceSums.scratch(count_dp, shapes),
        rows * width,
        call_id=call_id,
        length=38,
        near_outs=[jax.ShapeDtypeStruct((rows * count, width), jnp.float32)],
    )
    return results[0], results[-1], results[1:-1]


def dot(left, right, left_dim=1, right_dim=0):
    return lax.dot_general(
        left, right, (((left_dim,), (right_dim,)), ((), ())), preferred_element_type=jnp.float32
    )


def head_mask(width, copies):
    lane = lax.broadcasted_iota(jnp.int32, (1, width), 1)
    return [lane // HEAD_DIM == head for head in range(copies)]


def spread_heads(values):
    masks = head_mask(values.shape[1], values.shape[1] // HEAD_DIM)
    return jnp.concatenate([jnp.where(mask, values, jnp.zeros_like(values)) for mask in masks], 0)


def join_heads(values, heads):
    rows = values.shape[0] // heads
    masks = head_mask(values.shape[1], heads)
    return sum(
        jnp.where(mask, values[head * rows : (head + 1) * rows], 0.0)
        for head, mask in enumerate(masks)
    )


def split_three(values):
    first = values.astype(jnp.bfloat16)
    left = values - first.astype(jnp.float32)
    second = left.astype(jnp.bfloat16)
    third = (left - second.astype(jnp.float32)).astype(jnp.bfloat16)
    return first, second, third


def norm_rows(values):
    centered = values - jnp.mean(values, -1, keepdims=True)
    scale = lax.rsqrt(jnp.mean(centered * centered, -1, keepdims=True) + 1e-05)
    return centered * scale, scale


def norm_rows_back(upstream, gain, normed, scale):
    inner = upstream * gain
    return scale * (
        inner
        - jnp.mean(inner, -1, keepdims=True)
        - normed * jnp.mean(inner * normed, -1, keepdims=True)
    )


def embed(noisy, pixels, place):
    stacked = jnp.concatenate(split_three(noisy), 0)
    return dot(stacked, jnp.concatenate([pixels] * 3, 0), 0, 0) + place


def read_forward_kernel(
    noisy_ref,
    keep_ref,
    place_ref,
    pixels_ref,
    latents_ref,
    wide_gain_ref,
    gain_ref,
    query_weight_ref,
    pair_weight_ref,
    out_weight_ref,
    part_ref,
    pairs_ref,
    output_ref,
    queries_ref,
    normed_ref,
    scale_ref,
    side_ref,
    probs_ref,
):
    heads = query_weight_ref.shape[2] // HEAD_DIM

    @pl.when(pl.program_id(0) == 0)
    def _():
        normed, _ = norm_rows(latents_ref[...].astype(jnp.float32))
        low = (normed * wide_gain_ref[...]).astype(jnp.bfloat16)
        queries = dot(low, query_weight_ref[0]).astype(jnp.bfloat16)
        queries_ref[...] = spread_heads(queries * jnp.bfloat16(HEAD_DIM ** (-0.5)))

    normed, scale = norm_rows(embed(noisy_ref[0], pixels_ref[...], place_ref[...]))
    normed_ref[0] = normed
    scale_ref[0] = scale
    side = (normed * gain_ref[...]).astype(jnp.bfloat16)
    side_ref[0] = side.T
    keys = dot(side, pair_weight_ref[0]).astype(jnp.bfloat16)
    values = dot(side, pair_weight_ref[1]).astype(jnp.bfloat16)
    pairs_ref[0, 0] = keys
    pairs_ref[0, 1] = values
    scores = dot(keys, queries_ref[...], 1, 1)
    scores = jnp.where(keep_ref[0] > 0, scores, -1e30)
    top = jnp.max(scores, 0, keepdims=True)
    grown = jnp.exp(scores - top)
    probs = grown / jnp.sum(grown, 0, keepdims=True)
    probs_ref[0] = probs
    output = join_heads(dot(probs.astype(jnp.bfloat16), values, 0, 0), heads)
    output = output.astype(jnp.bfloat16)
    output_ref[0] = output
    part_ref[...] = dot(output, out_weight_ref[0])


def whole(shape):
    return pl.BlockSpec(shape, lambda b: (0,) * len(shape))


def each(shape):
    return pl.BlockSpec((1,) + shape, lambda b: (b,) + (0,) * len(shape))


def slot_of(shape, slot):
    return pl.BlockSpec(shape, lambda b: (slot,) + (0,) * (len(shape) - 1))


def read_forward(noisy, keep, place, pixels, latents, wide_gain, gain, wide, narrow, wideout):
    images, _, patches = noisy.shape
    count, d_lat = latents.shape
    d_if, local = narrow.shape[1:]
    stacked = local // HEAD_DIM * count
    return pl.pallas_call(
        read_forward_kernel,
        grid=(images,),
        out_shape=[
            pltpu.VMEM((images * count, d_lat), jnp.float32),
            pltpu.HBM((images, 2, patches, local), jnp.bfloat16),
            pltpu.HBM((images, count, local), jnp.bfloat16),
            pltpu.HBM((stacked, local), jnp.bfloat16),
            pltpu.HBM((images, patches, d_if), jnp.float32),
            pltpu.HBM((images, patches, 1), jnp.float32),
            pltpu.HBM((images, d_if, patches), jnp.bfloat16),
            pltpu.HBM((images, patches, stacked), jnp.float32),
        ],
        in_specs=[
            each(noisy.shape[1:]),
            each((patches, 1)),
            whole((patches, d_if)),
            whole(pixels.shape),
            whole(latents.shape),
            whole((1, d_lat)),
            whole((1, d_if)),
            slot_of((1, d_lat, local), 0),
            slot_of((2, d_if, local), 0),
            slot_of((1, local, d_lat), 0),
        ],
        out_specs=[
            pl.BlockSpec((count, d_lat), lambda b: (b, 0)),
            each((2, patches, local)),
            each((count, local)),
            whole((stacked, local)),
            each((patches, d_if)),
            each((patches, 1)),
            each((d_if, patches)),
            each((patches, stacked)),
        ],
        compiler_params=pltpu.CompilerParams(vmem_limit_bytes=52 << 20),
        cost_estimate=pl.CostEstimate(
            flops=10**10, bytes_accessed=30 * 10**6, transcendentals=2 * 10**6
        ),
    )(in_hbm(noisy), in_hbm(keep), in_hbm(place), in_hbm(pixels), in_hbm(latents), in_hbm(wide_gain), in_hbm(gain), in_hbm(wide), in_hbm(narrow), in_hbm(wideout))


def read_backward_kernel(
    noisy_ref,
    latents_ref,
    wide_gain_ref,
    gain_ref,
    query_weight_ref,
    pair_weight_ref,
    out_weight_ref,
    pairs_ref,
    output_ref,
    queries_ref,
    normed_ref,
    scale_ref,
    side_ref,
    probs_ref,
    grad_ref,
    lead_ref,
    wide_grad_ref,
    narrow_grad_ref,
    latents_grad_ref,
    wide_gain_grad_ref,
    gain_grad_ref,
    embed_grad_ref,
    low_ref,
    returned_ref,
):
    step, steps = pl.program_id(0), pl.num_programs(0)
    heads = query_weight_ref.shape[2] // HEAD_DIM

    @pl.when(step == 0)
    def _():
        normed, _ = norm_rows(latents_ref[...].astype(jnp.float32))
        low_ref[...] = (normed * wide_gain_ref[...]).astype(jnp.bfloat16)
        for ref in (
            wide_grad_ref,
            narrow_grad_ref,
            latents_grad_ref,
            gain_grad_ref,
            embed_grad_ref,
            returned_ref,
        ):
            ref[...] = jnp.zeros_like(ref)

    normed, scale, side, probs = normed_ref[0], scale_ref[0], side_ref[0], probs_ref[0]
    keys, values, queries = pairs_ref[0, 0], pairs_ref[0, 1], queries_ref[...]
    branch = grad_ref[...].astype(jnp.bfloat16)
    latents_grad_ref[...] += lead_ref[...] * grad_ref[...]
    wide_grad_ref[1] += dot(branch, output_ref[0], 0, 0)
    upstream = spread_heads(dot(branch, out_weight_ref[0], 1, 1).astype(jnp.bfloat16))
    value_grad = dot(probs.astype(jnp.bfloat16), upstream).astype(jnp.bfloat16)
    prob_grad = dot(values, upstream, 1, 1)
    inner = jnp.sum(prob_grad * probs, 0, keepdims=True)
    score_grad = (probs * (prob_grad - inner)).astype(jnp.bfloat16)
    key_grad = dot(score_grad, queries).astype(jnp.bfloat16)
    query_grad = join_heads(dot(score_grad, keys, 0, 0), heads) * HEAD_DIM ** (-0.5)
    query_grad = query_grad.astype(jnp.bfloat16)
    wide_grad_ref[0] += dot(low_ref[...], query_grad, 0, 0)
    returned_ref[...] += dot(query_grad, query_weight_ref[0], 1, 1)
    narrow_grad_ref[0] += dot(side, key_grad)
    narrow_grad_ref[1] += dot(side, value_grad)
    side_grad = dot(key_grad, pair_weight_ref[0], 1, 1) + dot(value_grad, pair_weight_ref[1], 1, 1)
    gain_grad_ref[...] += jnp.sum(side_grad * normed, 0, keepdims=True)
    back = norm_rows_back(side_grad, gain_ref[...], normed, scale)
    embed_grad_ref[...] += embed_back(noisy_ref[0], back)

    @pl.when(step == steps - 1)
    def _():
        normed, scale = norm_rows(latents_ref[...].astype(jnp.float32))
        returned = returned_ref[...]
        wide_gain_grad_ref[...] = jnp.sum(returned * normed, 0, keepdims=True)
        latents_grad_ref[...] += norm_rows_back(returned, wide_gain_ref[...], normed, scale)


def embed_back(noisy, back):
    first, second, _ = split_three(noisy)
    high = back.astype(jnp.bfloat16)
    low = (back - high.astype(jnp.float32)).astype(jnp.bfloat16)
    rows = noisy.shape[0]
    both = dot(jnp.concatenate([first, second], 0), high)
    return both[:rows] + both[rows:] + dot(first, low)


def read_backward(
    noisy,
    latents,
    wide_gain,
    gain,
    wide,
    narrow,
    wideout,
    pairs,
    output,
    queries,
    normed,
    scale,
    side,
    probs,
    grad,
    lead,
):
    images, rows, patches = noisy.shape
    count, d_lat = latents.shape
    d_if, local = narrow.shape[1:]
    stacked = local // HEAD_DIM * count
    results = [
        (2, d_lat, local),
        (2, d_if, local),
        (count, d_lat),
        (1, d_lat),
        (1, d_if),
        (rows, d_if),
    ]
    return pl.pallas_call(
        read_backward_kernel,
        grid=(images,),
        out_shape=[pltpu.HBM(shape, jnp.float32) for shape in results],
        in_specs=[
            each(noisy.shape[1:]),
            whole(latents.shape),
            whole((1, d_lat)),
            whole((1, d_if)),
            slot_of((1, d_lat, local), 0),
            slot_of((2, d_if, local), 0),
            slot_of((1, local, d_lat), 0),
            each((2, patches, local)),
            each((count, local)),
            whole((stacked, local)),
            each((patches, d_if)),
            each((patches, 1)),
            each((d_if, patches)),
            each((patches, stacked)),
            pl.BlockSpec((count, d_lat), lambda b: (b, 0)),
            whole((1, 1)),
        ],
        out_specs=[whole(shape) for shape in results],
        scratch_shapes=[
            pltpu.VMEM((count, d_lat), jnp.bfloat16),
            pltpu.VMEM((count, d_lat), jnp.float32),
        ],
        compiler_params=pltpu.CompilerParams(vmem_limit_bytes=52 << 20),
        cost_estimate=pl.CostEstimate(
            flops=2 * 10**10, bytes_accessed=30 * 10**6, transcendentals=2 * 10**6
        ),
    )(*map(in_hbm, (noisy, latents, wide_gain, gain, wide, narrow, wideout, pairs, output, queries, normed, scale, side, probs)), in_vmem(grad), in_hbm(lead))


def rows_of(rows, width):
    return pl.BlockSpec((rows, width), lambda b: (b, 0))


def attend_few(keys, values, queries):
    scores = dot(keys, queries, 1, 1)
    top = jnp.max(scores, 0, keepdims=True)
    grown = jnp.exp(scores - top)
    summed = jnp.sum(grown, 0, keepdims=True)
    probs = (grown / summed).astype(jnp.bfloat16)
    return dot(probs, values, 0, 0), top + jnp.log(summed)


def scaled_heads(queries):
    return spread_heads(queries * jnp.bfloat16(HEAD_DIM ** (-0.5)))


def self_forward_kernel(
    latent_ref, gain_ref, q_ref, k_ref, v_ref, out_weight_ref, part_ref, triple_ref, output_ref, total_ref, low_ref
):
    heads = q_ref.shape[2] // HEAD_DIM
    normed, _ = norm_rows(latent_ref[...])
    low = (normed * gain_ref[...]).astype(jnp.bfloat16)
    low_ref[...] = low
    queries, keys, values = (dot(low, ref[0]).astype(jnp.bfloat16) for ref in (q_ref, k_ref, v_ref))
    for index, item in enumerate((queries, keys, values)):
        triple_ref[0, index] = item
    output, total_ref[0] = attend_few(keys, values, scaled_heads(queries))
    output = join_heads(output, heads).astype(jnp.bfloat16)
    output_ref[0] = output
    part_ref[...] = dot(output, out_weight_ref[0])


def self_forward(latent, gain, wide, wideout, images):
    total, d_lat = latent.shape
    count, local = total // images, wide.shape[2]
    stacked = local // HEAD_DIM * count
    return pl.pallas_call(
        self_forward_kernel,
        grid=(images,),
        out_shape=[
            pltpu.VMEM((total, d_lat), jnp.float32),
            pltpu.HBM((images, 3, count, local), jnp.bfloat16),
            pltpu.HBM((images, count, local), jnp.bfloat16),
            pltpu.HBM((images, 1, stacked), jnp.float32),
            pltpu.HBM((total, d_lat), jnp.bfloat16),
        ],
        in_specs=[rows_of(count, d_lat), whole((1, d_lat))]
        + [slot_of((1, d_lat, local), slot) for slot in (1, 2, 3)]
        + [slot_of((1, local, d_lat), 1)],
        out_specs=[
            rows_of(count, d_lat),
            each((3, count, local)),
            each((count, local)),
            each((1, stacked)),
            rows_of(count, d_lat),
        ],
        compiler_params=pltpu.CompilerParams(vmem_limit_bytes=20 << 20),
        cost_estimate=pl.CostEstimate(
            flops=3 * 10**9, bytes_accessed=12 * 10**6, transcendentals=3 * 10**5
        ),
    )(in_vmem(latent), in_hbm(gain), in_hbm(wide), in_hbm(wide), in_hbm(wide), in_hbm(wideout))


def self_backward_kernel(
    grad_ref,
    latent_ref,
    gain_ref,
    q_ref,
    k_ref,
    v_ref,
    out_weight_ref,
    triple_ref,
    output_ref,
    total_ref,
    low_ref,
    part_ref,
    first_ref,
    last_ref,
    gain_grad_ref,
    branches,
    outputs,
    grads,
    lows,
):
    step, steps = pl.program_id(0), pl.num_programs(0)
    heads = q_ref.shape[2] // HEAD_DIM
    count = grad_ref.shape[0]
    mine = pl.ds(pl.multiple_of(step * count, count), count)
    normed, scale = norm_rows(latent_ref[...])
    branch = grad_ref[...].astype(jnp.bfloat16)
    branches[mine] = branch
    outputs[mine] = output_ref[0]
    lows[mine] = low_ref[...]
    upstream = spread_heads(dot(branch, out_weight_ref[0], 1, 1).astype(jnp.bfloat16))
    keys, values = triple_ref[0, 1], triple_ref[0, 2]
    queries = scaled_heads(triple_ref[0, 0])
    probs = jnp.exp(dot(keys, queries, 1, 1) - total_ref[0])
    value_grad = dot(probs.astype(jnp.bfloat16), upstream).astype(jnp.bfloat16)
    prob_grad = dot(values, upstream, 1, 1)
    inner = jnp.sum(prob_grad * probs, 0, keepdims=True)
    score_grad = (probs * (prob_grad - inner)).astype(jnp.bfloat16)
    key_grad = dot(score_grad, queries).astype(jnp.bfloat16)
    query_grad = join_heads(dot(score_grad, keys, 0, 0), heads) * HEAD_DIM ** (-0.5)
    query_grad = query_grad.astype(jnp.bfloat16)
    part = (
        dot(query_grad, q_ref[0], 1, 1)
        + dot(key_grad, k_ref[0], 1, 1)
        + dot(value_grad, v_ref[0], 1, 1)
    )
    for index, item in enumerate((query_grad, key_grad, value_grad)):
        grads[index, mine] = item
    gain_part = jnp.sum(part * normed, 0, keepdims=True)
    gain_grad_ref[...] = gain_part + jnp.where(step == 0, 0.0, gain_grad_ref[...])
    part_ref[...] = norm_rows_back(part, gain_ref[...], normed, scale)

    @pl.when(step == steps - 1)
    def _():
        turned = lows[...].T
        first_ref[0] = dot(turned, grads[0])
        first_ref[1] = dot(turned, grads[1])
        last_ref[0] = dot(turned, grads[2])
        last_ref[1] = dot(branches[...], outputs[...], 0, 0)


def self_backward(grad, latent, gain, wide, wideout, triple, output, total, low):
    rows, d_lat = latent.shape
    images, _, count, local = triple.shape
    stacked = local // HEAD_DIM * count
    weight = pltpu.HBM((2, d_lat, local), jnp.float32)
    return pl.pallas_call(
        self_backward_kernel,
        grid=(images,),
        out_shape=[pltpu.VMEM((rows, d_lat), jnp.float32)]
        + [weight] * 2
        + [pltpu.HBM((1, d_lat), jnp.float32)],
        in_specs=[rows_of(count, d_lat), rows_of(count, d_lat), whole((1, d_lat))]
        + [slot_of((1, d_lat, local), slot) for slot in (1, 2, 3)]
        + [
            slot_of((1, local, d_lat), 1),
            each((3, count, local)),
            each((count, local)),
            each((1, stacked)),
            rows_of(count, d_lat),
        ],
        out_specs=[rows_of(count, d_lat)] + [whole((2, d_lat, local))] * 2 + [whole((1, d_lat))],
        scratch_shapes=[
            pltpu.VMEM((rows, d_lat), jnp.bfloat16),
            pltpu.VMEM((rows, local), jnp.bfloat16),
            pltpu.VMEM((3, rows, local), jnp.bfloat16),
            pltpu.VMEM((rows, d_lat), jnp.bfloat16),
        ],
        compiler_params=pltpu.CompilerParams(vmem_limit_bytes=28 << 20),
        cost_estimate=pl.CostEstimate(
            flops=6 * 10**9, bytes_accessed=16 * 10**6, transcendentals=3 * 10**5
        ),
    )(in_vmem(grad), in_hbm(latent), in_hbm(gain), in_hbm(wide), in_hbm(wide), in_hbm(wide), in_hbm(wideout), in_hbm(triple), in_hbm(output), in_hbm(total), in_hbm(low))


def feed_forward_kernel(
    latent_ref, gain_ref, up_ref, down_ref, part_ref, active_ref, slope_ref, low_ref
):
    @pl.when(pl.program_id(0) == 0)
    def _():
        normed, _ = norm_rows(latent_ref[...])
        low_ref[...] = (normed * gain_ref[...]).astype(jnp.bfloat16)

    hidden = dot(low_ref[...], up_ref[0])
    share = 0.5 * (1.0 + lax.erf(hidden * math.sqrt(0.5)))
    density = jnp.exp(-0.5 * hidden * hidden) * (1.0 / math.sqrt(2.0 * math.pi))
    active = (hidden * share).astype(jnp.bfloat16)
    active_ref[0] = active
    slope_ref[0] = share + hidden * density
    part = dot(active, down_ref[0])

    @pl.when(pl.program_id(0) == 0)
    def _():
        part_ref[...] = part

    @pl.when(pl.program_id(0) > 0)
    def _():
        part_ref[...] += part


def feed_forward(latent, gain, wide, wideout):
    rows, d_lat = latent.shape
    local = wide.shape[2]
    return pl.pallas_call(
        feed_forward_kernel,
        grid=(4,),
        out_shape=[
            pltpu.VMEM((rows, d_lat), jnp.float32),
            pltpu.HBM((4, rows, local), jnp.bfloat16),
            pltpu.HBM((4, rows, local), jnp.float32),
            pltpu.HBM((rows, d_lat), jnp.bfloat16),
        ],
        in_specs=[
            whole((rows, d_lat)),
            whole((1, d_lat)),
            pl.BlockSpec((1, d_lat, local), lambda s: (4 + s, 0, 0)),
            pl.BlockSpec((1, local, d_lat), lambda s: (2 + s, 0, 0)),
        ],
        out_specs=[
            whole((rows, d_lat)),
            each((rows, local)),
            each((rows, local)),
            whole((rows, d_lat)),
        ],
        compiler_params=pltpu.CompilerParams(vmem_limit_bytes=24 << 20),
        cost_estimate=pl.CostEstimate(
            flops=4 * 10**9, bytes_accessed=14 * 10**6, transcendentals=10**6
        ),
    )(in_vmem(latent), in_hbm(gain), in_hbm(wide), in_hbm(wideout))


def feed_backward_kernel(
    grad_ref,
    latent_ref,
    gain_ref,
    up_ref,
    down_ref,
    active_ref,
    slope_ref,
    low_ref,
    part_ref,
    up_first_ref,
    up_last_ref,
    down_grad_ref,
    gain_grad_ref,
    branch,
    branch_turned,
    low_turned,
    total,
):
    step, steps = pl.program_id(0), pl.num_programs(0)

    @pl.when(step == 0)
    def _():
        low = grad_ref[...].astype(jnp.bfloat16)
        branch[...] = low
        branch_turned[...] = low.T
        low_turned[...] = low_ref[...].T
        total[...] = jnp.zeros_like(total)

    active_grad = dot(branch[...], down_ref[0], 1, 1)
    hidden_grad = (active_grad * slope_ref[0]).astype(jnp.bfloat16)
    down_grad_ref[0] = dot(branch_turned[...], active_ref[0])
    total[...] += dot(hidden_grad, up_ref[0], 1, 1)
    up_grad = dot(low_turned[...], hidden_grad)

    @pl.when(step < 2)
    def _():
        up_first_ref[0] = up_grad

    @pl.when(step >= 2)
    def _():
        up_last_ref[0] = up_grad

    @pl.when(step == steps - 1)
    def _():
        normed, scale = norm_rows(latent_ref[...])
        part = total[...]
        gain_grad_ref[...] = jnp.sum(part * normed, 0, keepdims=True)
        part_ref[...] = norm_rows_back(part, gain_ref[...], normed, scale)


def feed_backward(grad, latent, gain, wide, wideout, active, slope, low):
    rows, d_lat = latent.shape
    local = wide.shape[2]
    return pl.pallas_call(
        feed_backward_kernel,
        grid=(4,),
        out_shape=[
            pltpu.VMEM((rows, d_lat), jnp.float32),
            pltpu.HBM((2, d_lat, local), jnp.float32),
            pltpu.HBM((2, d_lat, local), jnp.float32),
            pltpu.HBM((4, d_lat, local), jnp.float32),
            pltpu.HBM((1, d_lat), jnp.float32),
        ],
        in_specs=[
            whole((rows, d_lat)),
            whole((rows, d_lat)),
            whole((1, d_lat)),
            pl.BlockSpec((1, d_lat, local), lambda s: (4 + s, 0, 0)),
            pl.BlockSpec((1, local, d_lat), lambda s: (2 + s, 0, 0)),
            each((rows, local)),
            each((rows, local)),
            whole((rows, d_lat)),
        ],
        out_specs=[
            whole((rows, d_lat)),
            pl.BlockSpec((1, d_lat, local), lambda s: (jnp.minimum(s, 1), 0, 0)),
            pl.BlockSpec((1, d_lat, local), lambda s: (jnp.maximum(s - 2, 0), 0, 0)),
            each((d_lat, local)),
            whole((1, d_lat)),
        ],
        scratch_shapes=[
            pltpu.VMEM((rows, d_lat), jnp.bfloat16),
            pltpu.VMEM((d_lat, rows), jnp.bfloat16),
            pltpu.VMEM((d_lat, rows), jnp.bfloat16),
            pltpu.VMEM((rows, d_lat), jnp.float32),
        ],
        compiler_params=pltpu.CompilerParams(vmem_limit_bytes=36 << 20),
        cost_estimate=pl.CostEstimate(
            flops=9 * 10**9, bytes_accessed=26 * 10**6, transcendentals=0
        ),
    )(in_vmem(grad), in_hbm(latent), in_hbm(gain), in_hbm(wide), in_hbm(wideout), in_hbm(active), in_hbm(slope), in_hbm(low))


def write_kernel(stage, held, raws, results, scratch):
    (
        own_weight_ref,
        weight_total_ref,
        latent_ref,
        noisy_ref,
        noise_ref,
        keep_ref,
        place_ref,
        pixels_ref,
        wide_gain_ref,
        gain_ref,
        key_weight_ref,
        value_weight_ref,
        query_weight_ref,
        out_weight_ref,
    ) = held
    (
        latent_grad_ref,
        key_grad_ref,
        value_grad_ref,
        query_grad_ref,
        out_grad_ref,
        wide_gain_grad_ref,
        gain_grad_ref,
        embed_grad_ref,
        head_grad_ref,
        loss_ref,
    ) = results
    queries, outputs, upstream, query_grads, normed_ref, scale_ref = scratch
    stage.wait(*range(10))
    patches, width = queries.shape
    group = 4 * HEAD_DIM
    groups = width // group
    latents = latent_ref.shape[0]
    rows = 4 * latents
    weight, weight_total = own_weight_ref[:1, :1], weight_total_ref[:1, :1]

    latent_normed, latent_scale = norm_rows(latent_ref[...])
    latent_low = (latent_normed * wide_gain_ref[...]).astype(jnp.bfloat16)
    interface = embed(noisy_ref[...], pixels_ref[0], place_ref[...])
    normed, scale = norm_rows(interface)
    normed_ref[...] = normed
    scale_ref[...] = scale
    outer_low = (normed * gain_ref[1:2]).astype(jnp.bfloat16)
    stage.wait(10, 11)
    keys = dot(latent_low, key_weight_ref[...]).astype(jnp.bfloat16)
    values = dot(latent_low, value_weight_ref[...]).astype(jnp.bfloat16)
    stage.wait(12, 13)
    queries[...] = dot(outer_low, query_weight_ref[...]).astype(jnp.bfloat16)

    def part(values, index):
        return values[:, index * group : (index + 1) * group]

    def by_head(values):
        return values.reshape(4, latents, patches)

    def group_probs(index):
        scores = by_head(dot(scaled_heads(part(keys, index)), part(queries, index), 1, 1))
        grown = jnp.exp(scores - jnp.max(scores, 1, keepdims=True))
        return grown / jnp.sum(grown, 1, keepdims=True)

    for index in range(groups):
        probs = group_probs(index).reshape(rows, patches).astype(jnp.bfloat16)
        output = dot(probs, spread_heads(part(values, index)), 0, 0)
        outputs[:, index * group : (index + 1) * group] = output.astype(jnp.bfloat16)

    outer = interface + dot(outputs[...], out_weight_ref[...], 1, 1)
    final_normed, final_scale = norm_rows(outer)
    final_low = (final_normed * gain_ref[2:3]).astype(jnp.bfloat16)
    head = pixels_ref[1]
    difference = dot(head, final_low, 1, 1) - noise_ref[...]
    masked = weight * keep_ref[...] * difference
    loss_ref[...] = jnp.full(loss_ref.shape, jnp.sum(masked * difference))
    predict_grad = (2.0 * masked / weight_total).astype(jnp.bfloat16)
    head_grad_ref[...] = dot(predict_grad, final_low)
    final_grad = dot(predict_grad, head, 0, 0)
    gain_final = jnp.sum(final_grad * final_normed, 0, keepdims=True)
    outer_grad = norm_rows_back(final_grad, gain_ref[2:3], final_normed, final_scale)
    branch = outer_grad.astype(jnp.bfloat16)
    out_grad_ref[...] = dot(branch, outputs[...], 0, 0)
    stage.store(4)
    upstream[...] = dot(branch, out_weight_ref[...]).astype(jnp.bfloat16)

    key_grads, value_grads = [], []
    for index in range(groups):
        probs = group_probs(index)
        low = probs.reshape(rows, patches).astype(jnp.bfloat16)
        above = part(upstream, index)
        value_grads.append(join_heads(dot(low, above), 4).astype(jnp.bfloat16))
        prob_grad = by_head(dot(spread_heads(part(values, index)), above, 1, 1))
        inner = jnp.sum(prob_grad * probs, 1, keepdims=True)
        score_grad = (probs * (prob_grad - inner)).reshape(rows, patches).astype(jnp.bfloat16)
        key_grad = join_heads(dot(score_grad, part(queries, index)), 4) * HEAD_DIM ** (-0.5)
        key_grads.append(key_grad.astype(jnp.bfloat16))
        query_grad = dot(score_grad, scaled_heads(part(keys, index)), 0, 0)
        query_grads[:, index * group : (index + 1) * group] = query_grad.astype(jnp.bfloat16)
    key_grad, value_grad = (jnp.concatenate(item, 1) for item in (key_grads, value_grads))

    turned = latent_low.T
    key_grad_ref[...] = dot(turned, key_grad)
    value_grad_ref[...] = dot(turned, value_grad)
    stage.store(1, 2)
    latent_part = dot(key_grad, key_weight_ref[...], 1, 1) + dot(
        value_grad, value_weight_ref[...], 1, 1
    )
    wide_gain_grad_ref[...] = jnp.sum(latent_part * latent_normed, 0, keepdims=True)
    latent_grad_ref[...] = norm_rows_back(
        latent_part, wide_gain_ref[...], latent_normed, latent_scale
    )
    normed, scale = normed_ref[...], scale_ref[...]
    outer_low = (normed * gain_ref[1:2]).astype(jnp.bfloat16)
    query_grad_ref[...] = dot(outer_low, query_grads[...], 0, 0)
    stage.store(3)
    outer_part = dot(query_grads[...], query_weight_ref[...], 1, 1)
    gain_outer = jnp.sum(outer_part * normed, 0, keepdims=True)
    gain_grad_ref[...] = jnp.concatenate([gain_outer, gain_final], 0)
    back = outer_grad + norm_rows_back(outer_part, gain_ref[1:2], normed, scale)
    embed_grad_ref[...] = embed_back(noisy_ref[...], back)


def write_stage(
    own_weight, weight_total, latent, noisy, noise, keep, place, pixels, wide_gain, gains, weights
):
    latents, d_lat = latent.shape
    rows, patches = noisy.shape
    d_if = place.shape[1]
    width = weights[0].shape[1]
    results = [
        (latents, d_lat),
        (d_lat, width),
        (d_lat, width),
        (d_if, width),
        (d_if, width),
        (1, d_lat),
        (2, d_if),
        (rows, d_if),
        (rows, d_if),
        (8, 128),
    ]
    wide = pltpu.VMEM((patches, width), jnp.bfloat16)
    return staged(
        write_kernel,
        [
            own_weight,
            weight_total,
            latent,
            noisy,
            noise,
            keep,
            place,
            pixels,
            wide_gain,
            gains,
            *weights,
        ],
        [jax.ShapeDtypeStruct(shape, jnp.float32) for shape in results],
        [wide] * 4
        + [pltpu.VMEM((patches, d_if), jnp.float32), pltpu.VMEM((patches, 1), jnp.float32)],
        15 * 10**9,
        length=27,
    )


def adam_update(master, first, second, gradient, scale):
    clipped = gradient * scale
    moment = adam_beta * first + (1.0 - adam_beta) * clipped
    square = adam_beta * second + (1.0 - adam_beta) * clipped * clipped
    fixed_first = moment / (1.0 - adam_beta**STEP)
    fixed_second = square / (1.0 - adam_beta**STEP)
    updated = master - learning_rate * (
        fixed_first / (jnp.sqrt(fixed_second) + adam_eps) + weight_decay * master
    )
    return (updated, moment, square)


def sum_rows(values):
    return jnp.sum(values.reshape(-1, 8, values.shape[-1]), 0)


def closing_kernel(count, count_dp, sizes, stage, held, raws, results, scratch):
    refs, given = list(scratch), list(held)

    def pull(number, source=None):
        source = refs if source is None else source
        taken = source[:number]
        del source[:number]
        return taken

    number, finished = sizes
    items, small_parts = views(pull(number, given)), pull(10, given)
    loss_tile, weight_tile = pull(2, given)
    done = views(pull(finished, given), 2)
    wide_out, narrow_out, turned_out, last_out, latents_out, rest_out, stats = results
    latents_item, rest_item, columns, column_sems = pull(4)
    number = len(items)
    shares = pull(number + 2)
    each = count_dp.bit_length() + 1
    sums = PieceSums(count_dp, items, shares[:number], pull(number * each))
    tiny = PieceSums(count_dp, [latents_item, rest_item], shares[number:], pull(2 * each))
    (write_share,) = pull(1)
    scatter = LineScatter(count, columns, write_share, pull(4), pull(4))
    small = [Spread("mp", count, *pull(3)) for _ in range(2)]
    over_dp, over_mp = Spread("dp", count_dp, *pull(3)), Spread("mp", count, *pull(3))

    column_loads, low = [], 0
    block, local = columns.shape[0] // count, columns.shape[1]
    for source in raws:
        rows = source.shape[0]
        for owner in range(count):
            column_loads.append(
                pltpu.make_async_copy(
                    source.at[:, pl.ds(owner * local, local)],
                    columns.at[pl.ds(owner * block + low, rows)],
                    column_sems.at[len(column_loads)],
                )
            )
        low += rows
    for load in column_loads:
        load.start()
    barrier = pltpu.get_barrier_semaphore()
    others = [over_dp.peer(step) for step in range(1, count_dp)]
    others += [over_mp.peer(step) for step in range(1, count)]
    signal_all(barrier, others)
    stage.wait()
    (latent_total, *gains, gain_side, gain_pair, side_embed, own_embed, head_grad) = small_parts
    d_if = gain_side.shape[1]
    lanes = d_if // count_dp
    width = latents_item.shape[2]
    rest_item[...] = jnp.zeros_like(rest_item)
    rows = []
    for gain in gains:
        rows += [gain[:, :d_if], gain[:, d_if:]]
    rows += [gain_side[...], gain_pair[...]]
    blocks = [(0, jnp.concatenate(rows, 0)), (16, side_embed[...] + own_embed[...]), (32, head_grad[...])]
    for piece in range(count_dp):
        latents_item[piece] = latent_total[:, piece * width : (piece + 1) * width]
        for first, block in blocks:
            rest_item[piece, pl.ds(first, block.shape[0]), :lanes] = block[
                :, piece * lanes : (piece + 1) * lanes
            ]
    pl.semaphore_wait(barrier, len(others))

    tiny.begin()
    sums.begin()
    for load in column_loads:
        load.wait()
    tiny.advance(1)

    def between():
        sums.advance(1)
        tiny.advance(2)

    scatter.run(between)
    for phase in range(3, tiny.bits + 1):
        tiny.advance(phase)
    for spread, share in zip(small, shares[-2:]):
        spread.held[spread.place] = share[...]
        spread.start()
    for phase in range(2, sums.bits + 1):
        sums.advance(phase)
    scatter.settle()

    self_in_2, self_out, read_query, read_out, read_key, read_value = shares[:6]
    self_in_0, self_in_1 = done[:2]
    up, down = done[2:6], done[6:10]
    lat_rows, if_rows = self_out.shape[0], read_key.shape[0]
    write_key, write_value = (write_share.at[pl.ds(i * lat_rows, lat_rows)] for i in range(2))
    write_query, write_out = (
        write_share.at[pl.ds(2 * lat_rows + i * if_rows, if_rows)] for i in range(2)
    )
    square = 0.0

    def keep(out, gradient, turn=False):
        nonlocal square
        value = gradient[...]
        square = square + sum_rows(value * value)
        out[...] = value.T if turn else value

    wide = [read_query, self_in_0, self_in_1, self_in_2] + up + [write_key, write_value]
    for slot, gradient in enumerate(wide):
        keep(wide_out.at[slot], gradient)
    for slot, gradient in enumerate([read_key, read_value, write_query]):
        keep(narrow_out.at[slot], gradient)
    for slot, gradient in enumerate([read_out, self_out] + down):
        keep(turned_out.at[slot], gradient, True)
    keep(last_out, write_out)
    stage.store(0, 1, 2, 3)
    for spread in small:
        spread.take()
    latents, rest = (spread.total() for spread in small)
    latents_out[...] = latents
    rest_out[...] = rest
    lead = (over_mp.place == 0).astype(jnp.float32)
    local = jnp.sum(square) + lead * (
        jnp.sum(sum_rows(latents * latents)) + jnp.sum(sum_rows(rest * rest))
    )
    lane = lax.broadcasted_iota(jnp.int32, (8, 128), 1)
    value = jnp.where(lane == 0, local, loss_tile[...])
    for spread in (over_dp, over_mp):
        spread.held[spread.place] = value
        spread.start()
        spread.take()
        value = spread.total()
    stats[...] = jnp.where(lane == 0, jnp.sqrt(value), value / weight_tile[...])
    sums.finish()
    tiny.finish()
    scatter.finish()
    for spread in small + [over_dp, over_mp]:
        spread.finish()


def closing(items, small_parts, tiles, done, write_shares, call_id):
    items, shapes, _ = piece_shapes(items)
    count, count_dp = lax.axis_size("mp"), lax.axis_size("dp")
    latents, d_lat = small_parts[0].shape
    lat_rows, local = done[0].shape[1:]
    if_rows = write_shares[2].shape[0]
    extra = [(latents, d_lat // count_dp), (48, 128)]
    block = (sum(item.shape[0] for item in write_shares), local)
    columns = (count * block[0], local)
    outs = [
        (10, lat_rows, local),
        (3, if_rows, local),
        (6, local, lat_rows),
        (if_rows, local),
        *extra,
        (8, 128),
    ]
    shapes = shapes + extra
    scratch = (
        [pltpu.VMEM((count_dp,) + shape, jnp.float32) for shape in extra]
        + [
            pltpu.VMEM(columns, jnp.float32),
            pltpu.SemaphoreType.DMA((count * len(write_shares),)),
        ]
        + [pltpu.VMEM(shape, jnp.float32) for shape in shapes]
        + PieceSums.scratch(count_dp, shapes)
        + [pltpu.VMEM(block, jnp.float32)]
        + LineScatter.scratch(count, columns, 4)
        + Spread.scratch(count, extra[0])
        + Spread.scratch(count, extra[1])
        + Spread.scratch(count_dp, (8, 128))
        + Spread.scratch(count, (8, 128))
    )
    return staged(
        partial(closing_kernel, count, count_dp, (len(items), len(done))),
        [*items, *small_parts, *tiles, *done],
        [jax.ShapeDtypeStruct(shape, jnp.float32) for shape in outs],
        scratch,
        10**7,
        write_shares,
        call_id,
        50,
    )


def clip_scale(norm):
    return clip_level / jnp.maximum(norm, clip_level)


def update_kernel(kinds, *refs):
    number = 3 * (kinds + 1)
    sources, states, refs = refs[: 1 + kinds], refs[1 + kinds :][:number], refs[1 + kinds + number :]
    outs, local, refs = refs[:number], refs[number:][: 1 + kinds], refs[number + 1 + kinds :]
    local_sems, held, (in_sems, out_sems) = refs[0], refs[1 : 1 + number], refs[1 + number :]
    stats, gradients = local[0], local[1:]
    kinds += 1
    firsts = [
        pltpu.make_async_copy(source, target, local_sems.at[index])
        for index, (source, target) in enumerate(zip(sources, local))
    ]
    for first in firsts:
        first.start()
    lane = lax.broadcasted_iota(jnp.int32, (8, 128), 1)
    corner = jnp.logical_and(lane == 0, lax.broadcasted_iota(jnp.int32, (8, 128), 0) == 0)
    loads, copies = [], []
    pieces = []
    for kind, gradient in enumerate(gradients):
        slots = range(gradient.shape[0]) if len(gradient.shape) == 3 else [None]
        pieces += [(kind, slot) for slot in slots]

    def at(ref, slot):
        return ref if slot is None else ref.at[slot]

    for kind, slot in pieces:
        for index in range(3 * kind, 3 * kind + 3):
            source, target = at(states[index], slot), at(held[index], slot)
            loads.append(pltpu.make_async_copy(source, target, in_sems.at[len(loads)]))
            loads[-1].start()
    for load in firsts:
        load.wait()
    scale = jnp.sum(jnp.where(corner, clip_scale(stats[...]), 0.0))
    pixel_loads = [
        pltpu.make_async_copy(states[index], held[index], in_sems.at[len(loads) + index - 18])
        for index in range(18, 21)
    ]
    for load in pixel_loads:
        load.start()
    for order, (kind, slot) in enumerate(pieces):
        for load in loads[3 * order : 3 * order + 3]:
            load.wait()
        refs = [at(held[index], slot) for index in range(3 * kind, 3 * kind + 3)]
        source = at(gradients[kind], slot)
        rows, width = refs[0].shape
        step = math.gcd(rows, max(8, 8192 // width)) if rows % 8 == 0 else rows

        def one(index, carry, refs=refs, source=source, step=step, width=width):
            where = pl.ds(pl.multiple_of(index * step, step), step)
            state = [ref[where] for ref in refs]
            for ref, result in zip(refs, adam_update(*state, source[where, :width], scale)):
                ref[where] = result
            return carry

        lax.fori_loop(0, rows // step, one, 0)
        for index in range(3 * kind, 3 * kind + 3):
            source, target = at(held[index], slot), at(outs[index], slot)
            copies.append(pltpu.make_async_copy(source, target, out_sems.at[len(copies)]))
            copies[-1].start()
    for load in pixel_loads:
        load.wait()
    pixels, rest = held[18:21], gradients[-1]
    for slot in range(2):
        gradient = rest[16 * (slot + 1) : 16 * (slot + 1) + PIX, : pixels[0].shape[2]]
        state = [ref[:, slot, :] for ref in pixels]
        for ref, result in zip(pixels, adam_update(*state, gradient, scale)):
            ref[:, slot, :] = result
    for index in range(18, 21):
        copies.append(pltpu.make_async_copy(held[index], outs[index], out_sems.at[len(copies)]))
        copies[-1].start()
    for copy in copies:
        copy.wait()


def update_states(stats, gradients, states):
    kinds = len(gradients)
    copies = sum(3 * (item.shape[0] if item.ndim == 3 else 1) for item in gradients) + 3
    sems = pltpu.SemaphoreType.DMA((copies,))
    return pl.pallas_call(
        partial(update_kernel, kinds),
        out_shape=[pltpu.HBM(item.shape, item.dtype) for item in states],
        in_specs=[HBM_SPEC] * (1 + kinds + len(states)),
        out_specs=[HBM_SPEC] * len(states),
        scratch_shapes=[pltpu.VMEM(item.shape, jnp.float32) for item in (stats, *gradients)]
        + [pltpu.SemaphoreType.DMA((1 + kinds,))]
        + [pltpu.VMEM(item.shape, jnp.float32) for item in states]
        + [sems] * 2,
        compiler_params=pltpu.CompilerParams(vmem_limit_bytes=24 << 20),
        cost_estimate=pl.CostEstimate(
            flops=2 * 10**7, bytes_accessed=14 * 10**6, transcendentals=0
        ),
    )(*(in_hbm(item) for item in (stats, *gradients, *states)))


def write_apart(
    latent_three,
    own_noisy,
    own_noise,
    own_keep,
    own_weight,
    weight_total,
    place,
    copy_pixels,
    gain,
    gain_rows,
    weights,
    layout,
    timesteps,
):
    write_key_weight, write_value_weight, write_query_weight, write_out_weight = weights
    images, latents, first_image, sharers = layout
    own_images, own_latents, d_lat = latent_three.shape
    write_norm, write_stats = layer_norm(latent_three, gain)
    write_low = write_norm.astype(jnp.bfloat16)

    own_interface = (
        jnp.einsum(
            "bcp,cd->bpd", own_noisy, copy_pixels[0].astype(jnp.float32), precision=precise
        )
        + place
    )

    outer_norm, outer_stats = layer_norm(own_interface, gain_rows[9])
    outer_low = outer_norm.astype(jnp.bfloat16)

    def join(spec, values, weight):
        product = jnp.einsum(spec, values, weight, preferred_element_type=jnp.float32)
        return product.astype(jnp.bfloat16)

    def image_rows(values):
        if sharers == 1:
            return values
        nothing = jnp.where(timesteps[0] > 0, 0.0, -0.0)
        whole = lax.all_gather(values.astype(jnp.float32), "mp", axis=0, tiled=True)
        whole = whole + nothing
        whole = whole.reshape(images, latents, d_lat).astype(jnp.bfloat16)
        return lax.dynamic_slice_in_dim(whole, first_image, own_images, 0)

    write_query = join("bpd,dc->bpc", outer_low, write_query_weight)
    write_key = image_rows(join("bld,dc->blc", write_low, write_key_weight))
    write_value = image_rows(join("bld,dc->blc", write_low, write_value_weight))
    write_out, write_total = attend_forward(write_query, write_key, write_value, None)
    outer = own_interface + jnp.einsum(
        "bpc,dc->bpd", write_out, write_out_weight, preferred_element_type=jnp.float32
    )
    final_norm, final_stats = layer_norm(outer, gain_rows[10])
    final_low = final_norm.astype(jnp.bfloat16)
    predicted = jnp.einsum(
        "bpd,cd->bcp", final_low, copy_pixels[1], preferred_element_type=jnp.float32
    )
    difference = predicted - own_noise
    masked = own_weight[:, None, None] * own_keep[:, None, :] * difference
    loss_local = jnp.sum(masked * difference)
    predict_grad = (2.0 * masked / weight_total).astype(jnp.bfloat16)
    head_grad = jnp.einsum(
        "bcp,bpd->cd", predict_grad, final_low, preferred_element_type=jnp.float32
    )
    final_grad = jnp.einsum(
        "bcp,cd->bpd", predict_grad, copy_pixels[1], preferred_element_type=jnp.float32
    )
    outer_grad, gain_final = norm_back(final_grad, gain_rows[10], final_stats)
    branch_low = outer_grad.astype(jnp.bfloat16)
    narrowout_grad = jnp.einsum(
        "bpd,bpc->dc", branch_low, write_out, preferred_element_type=jnp.float32
    )
    write_upstream = join("bpd,dc->bpc", branch_low, write_out_weight)
    query_grad, key_grad, value_grad = attend_back(
        write_query, write_key, write_value, None, write_total, write_upstream
    )
    write_query_grad = jnp.einsum(
        "bpd,bpc->dc", outer_low, query_grad, preferred_element_type=jnp.float32
    )
    outer_part = jnp.einsum(
        "bpc,dc->bpd", query_grad, write_query_weight, preferred_element_type=jnp.float32
    )

    def row_grad(values):
        if sharers > 1:
            whole = jnp.zeros((images, latents, d_lat), jnp.float32)
            whole = lax.dynamic_update_slice_in_dim(whole, values, first_image, 0)
            values = lax.psum_scatter(
                whole.reshape(images * sharers, own_latents, d_lat),
                "mp",
                scatter_dimension=0,
                tiled=True,
            )
        return values.astype(jnp.bfloat16)

    key_grad, value_grad = row_grad(key_grad), row_grad(value_grad)
    write_key_grad = jnp.einsum(
        "bld,blc->dc", write_low, key_grad, preferred_element_type=jnp.float32
    )
    write_value_grad = jnp.einsum(
        "bld,blc->dc", write_low, value_grad, preferred_element_type=jnp.float32
    )
    write_part = jnp.einsum(
        "blc,dc->bld", key_grad, write_key_weight, preferred_element_type=jnp.float32
    ) + jnp.einsum(
        "blc,dc->bld", value_grad, write_value_weight, preferred_element_type=jnp.float32
    )
    own_grad, gain_write = norm_back(write_part, gain, write_stats)
    outer_back, gain_outer = norm_back(outer_part, gain_rows[9], outer_stats)
    embed_grad = jnp.einsum(
        "bcp,bpd->cd", own_noisy, outer_grad + outer_back, precision=precise
    )
    return (
        own_grad,
        write_key_grad,
        write_value_grad,
        write_query_grad,
        narrowout_grad,
        gain_write,
        gain_outer,
        gain_final,
        embed_grad,
        head_grad,
        loss_local,
    )


def body(
    clean_patches,
    noise_patches,
    timesteps,
    present_mask,
    copy_widein,
    copy_narrowin,
    copy_wideout,
    copy_narrowout,
    copy_latents,
    copy_gains,
    copy_pixels,
    master_widein,
    first_widein,
    second_widein,
    master_narrowin,
    first_narrowin,
    second_narrowin,
    master_wideout,
    first_wideout,
    second_wideout,
    master_narrowout,
    first_narrowout,
    second_narrowout,
    master_latents,
    first_latents,
    second_latents,
    master_gains,
    first_gains,
    second_gains,
    master_pixels,
    first_pixels,
    second_pixels,
):
    images = clean_patches.shape[0]
    patches = clean_patches.shape[2]
    count_mp, count_dp = lax.axis_size("mp"), lax.axis_size("dp")
    mp_index, dp_index = lax.axis_index("mp"), lax.axis_index("dp")
    lead = (mp_index == 0).astype(jnp.float32)
    latents, d_lat = copy_latents.shape
    d_if = copy_gains.shape[1]
    local = copy_widein.shape[2]
    sharers = max(1, count_mp // images)
    own_images = max(1, images // count_mp)
    own_patches, own_latents = patches // sharers, latents // sharers
    first_image = mp_index * own_images // sharers
    share = lax.rem(mp_index, sharers)

    def dp_piece(values, axis):
        size = values.shape[axis] // count_dp
        return lax.dynamic_slice_in_dim(values, dp_index * size, size, axis).astype(jnp.float32)

    key_piece = dp_piece(copy_widein[:, 8], 0)
    value_piece = dp_piece(copy_widein[:, 9], 0)
    query_piece = dp_piece(copy_narrowin[:, 2], 0)
    out_piece = dp_piece(copy_narrowout, 1).T
    gathered = lax.all_gather(
        jnp.concatenate([key_piece, value_piece, query_piece, out_piece], 0), "mp"
    )

    signal = jnp.cos(0.5 * math.pi * (timesteps.astype(jnp.float32) + 0.5) / NSTEPS) ** 2
    noisy = (
        jnp.sqrt(signal)[:, None, None] * clean_patches
        + jnp.sqrt(1.0 - signal)[:, None, None] * noise_patches
    )
    loss_weight = 0.5 + signal
    keep_float = present_mask.astype(jnp.float32)
    weight_here = jnp.sum(loss_weight * PIX * jnp.sum(keep_float, 1))
    gain_rows = copy_gains.astype(jnp.float32)

    def wide_gain(index):
        return gain_rows[2 * index : 2 * index + 2].reshape(-1)

    wide_in = in_hbm(jnp.swapaxes(copy_widein, 0, 1))
    narrow_in = in_hbm(jnp.swapaxes(copy_narrowin, 0, 1))
    wide_out = in_hbm(copy_wideout)
    place = position_table(patches, d_if)
    noisy_rows, pixel_rows, noise_rows = (
        jnp.pad(item, ((0, 0), (0, 16 - PIX), (0, 0)))
        for item in (noisy, copy_pixels, noise_patches)
    )
    read_args = (
        noisy_rows,
        keep_float[:, :, None],
        place,
        pixel_rows[0],
        copy_latents,
        wide_gain(0)[None],
        gain_rows[8:9],
        wide_in,
        narrow_in,
        wide_out,
    )
    read_part, *read_kept = read_forward(*read_args)
    wide_gains = [wide_gain(index)[None] for index in range(1, 4)]
    latent_base = copy_latents.astype(jnp.float32)

    def own_tokens(values, axis):
        values = lax.dynamic_slice_in_dim(values, first_image, own_images, 0)
        return lax.dynamic_slice_in_dim(values, share * own_patches, own_patches, axis)

    own_weight = lax.dynamic_slice_in_dim(loss_weight, first_image, own_images, 0)
    own_scalar = jnp.broadcast_to(own_weight[0], (8, 128))
    own_pieces = [
        own_tokens(noisy_rows, 2),
        own_tokens(noise_rows, 2),
        own_tokens(keep_float, 1),
    ]
    side_gains = gain_rows[8:11]
    here_tile, lead = jnp.full((8, 128), weight_here), lead.reshape(1, 1)
    ready = (own_pieces, own_scalar, wide_gains, side_gains, latent_base, here_tile, lead, pixel_rows)
    gathered, read_part, ready = lax.optimization_barrier((gathered, read_part, ready))
    own_pieces, own_scalar, wide_gains, side_gains, latent_base, here_tile, lead, pixel_rows = ready
    gathered = lax.all_gather(gathered, "dp").reshape(count_dp * count_mp, -1, local)
    latent_near, latent_one, (weight_tile,) = line_sum(
        read_part, latent_base, 2, tile=here_tile
    )
    self_part, *self_kept = self_forward(
        latent_near, wide_gains[0], wide_in, wide_out, images
    )
    latent_near, latent_two, _ = line_sum(self_part, latent_one, 3)
    feed_part, *feed_kept = feed_forward(latent_near, wide_gains[1], wide_in, wide_out)
    latent_three, write_weights = line_scatter(
        feed_part, latent_two, gathered, [d_lat, d_lat, d_if, d_if], 4
    )
    latent_three = latent_three.reshape(own_images, own_latents, d_lat)
    if sharers == 1 and own_images == 1:
        (
            own_grad,
            write_key_grad,
            write_value_grad,
            write_query_grad,
            narrowout_grad,
            gain_write,
            gain_pair,
            own_embed,
            head_grad,
            loss_tile,
        ) = write_stage(
            own_scalar,
            weight_tile,
            latent_three[0],
            own_pieces[0][0],
            own_pieces[1][0],
            own_pieces[2],
            place,
            pixel_rows,
            wide_gains[2],
            side_gains,
            write_weights,
        )
    else:
        (
            own_grad,
            write_key_grad,
            write_value_grad,
            write_query_grad,
            narrowout_grad,
            gain_write,
            gain_outer,
            gain_final,
            own_embed,
            head_grad,
            loss_local,
        ) = write_apart(
            latent_three,
            own_tokens(noisy, 2),
            own_tokens(noise_patches, 2),
            own_tokens(keep_float, 1),
            own_weight,
            weight_tile[0, 0],
            lax.dynamic_slice_in_dim(place, share * own_patches, own_patches, 0),
            copy_pixels,
            wide_gain(3),
            gain_rows,
            write_weights,
            (images, latents, first_image, sharers),
            timesteps,
        )
        gain_write, gain_pair = gain_write[None], jnp.stack([gain_outer, gain_final])
        own_embed, head_grad = (
            jnp.pad(item, ((0, 16 - PIX), (0, 0))) for item in (own_embed, head_grad)
        )
        loss_tile = jnp.full((8, 128), loss_local)
    latent_near, latent_grad, (key_share, query_share) = line_gather(
        own_grad.reshape(-1, d_lat), 5, [write_key_grad, write_query_grad]
    )
    latent_part, up_first, up_last, down_grad, gain_feed = feed_backward(
        latent_near, latent_two, wide_gains[1], wide_in, wide_out, *feed_kept
    )
    latent_near, latent_grad, five_shares = line_sum(
        latent_part, latent_grad, 6, [write_value_grad, narrowout_grad, up_first]
    )
    latent_part, self_first, self_last, gain_self = self_backward(
        latent_near, latent_one, wide_gains[0], wide_in, wide_out, *self_kept
    )
    latent_near, latent_grad, six_shares = line_sum(
        latent_part, latent_grad, 7, [up_last, down_grad, self_first]
    )
    read_wide, read_narrow, latent_total, gain_read, gain_side, side_embed = read_backward(
        read_args[0], *read_args[4:], *read_kept, latent_near, lead
    )
    *gradients, stats = closing(
        [self_last, read_wide, read_narrow],
        [
            latent_total,
            gain_read,
            gain_self,
            gain_feed,
            gain_write,
            gain_side,
            gain_pair,
            side_embed,
            own_embed,
            head_grad,
        ],
        [loss_tile, weight_tile],
        [six_shares[2], five_shares[2], six_shares[0], six_shares[1]],
        [key_share, five_shares[0], query_share, five_shares[1]],
        8,
    )
    states = (
        *(jnp.swapaxes(item, 0, 1) for item in (master_widein, first_widein, second_widein)),
        *(jnp.swapaxes(item, 0, 1) for item in (master_narrowin, first_narrowin, second_narrowin)),
        master_wideout,
        first_wideout,
        second_wideout,
        *(item.T for item in (master_narrowout, first_narrowout, second_narrowout)),
        master_latents,
        first_latents,
        second_latents,
        master_gains,
        first_gains,
        second_gains,
        *(jnp.swapaxes(item, 0, 1) for item in (master_pixels, first_pixels, second_pixels)),
    )
    results = update_states(stats, gradients, states)
    results = [
        jnp.swapaxes(item, 0, 1) if index < 6 or 9 <= index < 12 or index >= 18 else item
        for index, item in enumerate(results)
    ]
    return (stats[0, 1], stats[0, 0], *results)


def solution(mesh):
    in_specs = (
        P("dp", None, None),
        P("dp", None, None),
        P("dp"),
        P("dp", None),
        P(None, None, "mp"),
        P(None, None, "mp"),
        P(None, "mp", None),
        P("mp", None),
        P(),
        P(),
        P(),
        P("dp", None, "mp"),
        P("dp", None, "mp"),
        P("dp", None, "mp"),
        P("dp", None, "mp"),
        P("dp", None, "mp"),
        P("dp", None, "mp"),
        P(None, "mp", "dp"),
        P(None, "mp", "dp"),
        P(None, "mp", "dp"),
        P("mp", "dp"),
        P("mp", "dp"),
        P("mp", "dp"),
        P(None, "dp"),
        P(None, "dp"),
        P(None, "dp"),
        P(None, "dp"),
        P(None, "dp"),
        P(None, "dp"),
        P(None, None, "dp"),
        P(None, None, "dp"),
        P(None, None, "dp"),
    )
    out_specs = (
        P(),
        P(),
        P("dp", None, "mp"),
        P("dp", None, "mp"),
        P("dp", None, "mp"),
        P("dp", None, "mp"),
        P("dp", None, "mp"),
        P("dp", None, "mp"),
        P(None, "mp", "dp"),
        P(None, "mp", "dp"),
        P(None, "mp", "dp"),
        P("mp", "dp"),
        P("mp", "dp"),
        P("mp", "dp"),
        P(None, "dp"),
        P(None, "dp"),
        P(None, "dp"),
        P(None, "dp"),
        P(None, "dp"),
        P(None, "dp"),
        P(None, None, "dp"),
        P(None, None, "dp"),
        P(None, None, "dp"),
    )
    return jax.shard_map(body, mesh=mesh, in_specs=in_specs, out_specs=out_specs, check_vma=False)
```
